32 devices in a mesh: fsdp: 8 (over y, x, core), tp: 4 (over z).
Axes of the slice: x: 2, y: 2, z: 4, core: 2. Of those that a mesh axis runs over, the one named last changes fastest.
Arguments:
- block_in: bfloat16 [4096, 2048], P(('fsdp', 'tp')), may hold values from -6 to 6
- out_cotan: bfloat16 [4096, 2048], P(('fsdp', 'tp')), may hold values from -6 to 6
- segment_ids: int32 [4096], P('fsdp'), may hold values from 0 to 63, never falling along the last dimension, each value on 1 to 256 neighbouring positions
- expert_ids: int32 [4096, 6], P('fsdp'), may hold values from 0 to 15, all different within a row; in each aligned block of 128 rows (0 to 127, 128 to 255, ...) at most 64 rows name the same one
- expert_wts: float32 [4096, 6], P('fsdp'), may hold values from 0.5 to 1.5
- attn_gain: bfloat16 [2048], P('fsdp'), may hold values from 0.5 to 1.5
- query_proj: bfloat16 [2048, 3072], P('fsdp', 'tp'), may hold values from -0.125 to 0.125
- latent_proj: bfloat16 [2048, 576], P('fsdp'), may hold values from -0.125 to 0.125
- latent_gain: bfloat16 [512], P('fsdp'), may hold values from 0.5 to 1.5
- latent_up: bfloat16 [512, 4096], P('fsdp', 'tp'), may hold values from -0.25 to 0.25
- out_proj: bfloat16 [2048, 2048], P('tp', 'fsdp'), may hold values from -0.5 to 0.5
- ffn_gain: bfloat16 [2048], P('fsdp'), may hold values from 0.5 to 1.5
- shared_gate: bfloat16 [2048, 2816], P('fsdp', 'tp'), may hold values from -0.125 to 0.125
- shared_up: bfloat16 [2048, 2816], P('fsdp', 'tp'), may hold values from -0.125 to 0.125
- shared_down: bfloat16 [2816, 2048], P('tp', 'fsdp'), may hold values from -0.109375 to 0.109375
- routed_gate: bfloat16 [16, 1408, 2048], P('fsdp', 'tp'), may hold values from -0.125 to 0.125
- routed_up: bfloat16 [16, 1408, 2048], P('fsdp', 'tp'), may hold values from -0.125 to 0.125
- routed_down: bfloat16 [16, 1408, 2048], P('fsdp', 'tp'), may hold values from -0.15625 to 0.15625
Outputs:
- block_out: bfloat16 [4096, 2048], P(('fsdp', 'tp'))
- block_in_grad: float32 [4096, 2048], P(('fsdp', 'tp'))
- attn_gain_grad: float32 [2048], P(('fsdp', 'tp'))
- query_proj_grad: float32 [2048, 3072], P('fsdp', 'tp')
- latent_proj_grad: float32 [2048, 576], P(('fsdp', 'tp'))
- latent_gain_grad: float32 [512], P(('fsdp', 'tp'))
- latent_up_grad: float32 [512, 4096], P('fsdp', 'tp')
- out_proj_grad: float32 [2048, 2048], P('tp', 'fsdp')
- ffn_gain_grad: float32 [2048], P(('fsdp', 'tp'))
- shared_gate_grad: float32 [2048, 2816], P('fsdp', 'tp')
- shared_up_grad: float32 [2048, 2816], P('fsdp', 'tp')
- shared_down_grad: float32 [2816, 2048], P('tp', 'fsdp')
- routed_gate_grad: float32 [16, 1408, 2048], P('fsdp', 'tp')
- routed_up_grad: float32 [16, 1408, 2048], P('fsdp', 'tp')
- routed_down_grad: float32 [16, 1408, 2048], P('fsdp', 'tp')
The draws below stay inside these ranges and needn't reach their ends.
Inputs may be any that keep to these rules, and one draw needn't show every extreme that they name: `expert_ids`: each row names 6 different experts; among the 128 rows of one device no expert is named more than 64 times. `segment_ids`: never falls along the tokens.
All inputs are finite; a program needn't handle non-finite values.
Results may differ from the reference program's by a relative error of at most 0.024.
Values may be sent and summed in bfloat16 or wider, within the bound.
A program may use at most 320 MiB of HBM per device.

```python
import math
import jax
import jax.numpy as jnp
import numpy as np
from jax import lax

D = 2048
H = 16
NOPE = 128
ROPE = 64
DV = 128
LAT = 512
FF = 1408
FS = 2816
TOPK = 6
SEQ = 512
TOK_DEV = 128
TOKENS = 4096
EXPERTS = 16
CAP = 64
N_FSDP = 8
N_TP = 4


def steps_of(rng, dims, split, smallest, largest):
    def one(position, parts):
        heights = jax.random.uniform(jax.random.fold_in(jax.random.fold_in(rng, 6), position), (parts,), jnp.float32, smallest / len(split), largest / len(split))
        return jnp.repeat(jnp.exp(heights), dims[position] // parts).reshape((-1,) + (1,) * (len(dims) - position - 1))

    factor_of = one(*split[0])
    for cut in split[1:]:
        factor_of = factor_of * one(*cut)
    return factor_of


def length_profile(count, total, most, lean):
    loads = [(1 << 20) // math.isqrt(rank ** lean) + 1 for rank in range(2, count + 1)]
    surplus, given = total - most - (count - 1), [1] * (count - 1)
    while surplus > 0:
        candidates = [i for i in range(count - 1) if given[i] < most]
        whole, remaining = sum([loads[i] for i in candidates]), surplus
        for i in candidates:
            addition = min(most - given[i], max(1, remaining * loads[i] // whole), surplus)
            given[i] = given[i] + addition
            surplus = surplus - addition
    return np.array([most] + given)


def uneven(key, count, total, most, slope):
    if count == 2:
        one = jax.random.randint(key, (), max(1, total - most), min(most, total - 1) + 1)
        return jnp.stack([one, total - one])
    tallies = jnp.asarray(length_profile(count, total, most, slope), jnp.int32)
    twos = (count - 1) // 2
    giver, sink = tallies[1:1 + 2 * twos:2], tallies[2:2 + 2 * twos:2]
    slack = jnp.minimum(giver - 1, most - sink)
    shifted = jax.random.randint(jax.random.fold_in(key, 1), (twos,), 0, 1 << 20) % (slack + 1)
    tallies = tallies.at[1:1 + 2 * twos:2].set(giver - shifted).at[2:2 + 2 * twos:2].set(sink + shifted)
    return tallies[jax.random.permutation(jax.random.fold_in(key, 2), count)]


def deal_out(own_key, own, number, rows, count, top, most, slope):
    order = jax.random.permutation(own_key, count)
    crowded, ordinary = shares(count, rows * top, most, slope, True), shares(count, rows * top, most, slope, False)
    places = jnp.arange(count)

    def named(tallies, turn):
        used = int((tallies > 0).sum())
        fixed = max(1, used // 4)
        passed = fixed + (places - fixed + turn * (used - fixed)) % max(1, count - fixed)
        return jnp.zeros((count,), jnp.int32).at[order[jnp.where(places < fixed, places, passed)]].set(jnp.asarray(tallies, jnp.int32))

    tallies = jnp.where(number % 4 == 0, named(crowded, number // 4), named(ordinary, number - number // 4 - 1))
    mixed = jax.random.permutation(jax.random.fold_in(own, 3), count)
    giver, sink = mixed[0:count // 2 * 2:2], mixed[1:count // 2 * 2:2]
    slack = jnp.minimum(tallies[giver] - 1, most - tallies[sink]) // 2
    slack = jnp.where((giver == order[0]) | (sink == order[0]) | (tallies[sink] == 0), 0, jnp.maximum(slack, 0))
    passed = jax.random.randint(jax.random.fold_in(own, 4), (count // 2,), 0, 1 << 20) % (slack + 1)
    tallies = tallies.at[giver].add(-passed).at[sink].add(passed)
    items = jnp.searchsorted(jnp.cumsum(tallies), jnp.arange(rows * top), side="right").astype(jnp.int32)
    table = items.reshape(top, rows).T
    table = table[jax.random.permutation(jax.random.fold_in(own, 1), rows)]
    turn = jax.random.randint(jax.random.fold_in(own, 2), (rows, 1), 0, top)
    return jnp.take_along_axis(table, (jnp.arange(top)[None, :] + turn) % top, axis=1)


def shares(count, total, most, skew, full):
    portions = [(1 << 20) // math.isqrt(rank ** skew) + 1 for rank in range(1, count + 1)]
    largest = most if full else min(most, max(-(-total // count), total * portions[0] // sum(portions)))
    least = 1 if total - largest >= count - 1 else 0
    given, rest = [largest] + [least] * (count - 1), total - largest - least * (count - 1)
    while rest > 0:
        movable = [i for i in range(1, count) if given[i] < largest] or [i for i in range(1, count) if given[i] < most]
        whole, remaining = sum([portions[i] for i in movable]), rest
        for i in movable:
            more = min(most - given[i], max(1, remaining * portions[i] // whole), rest)
            given[i] = given[i] + more
            rest = rest - more
    return np.array(given)


def normal_values(own_key, dims, scale, limit, cuts=(), kind=jnp.bfloat16):
    drawn = scale * jax.random.normal(own_key, dims, jnp.float32)
    if cuts:
        drawn = drawn * steps_of(own_key, dims, cuts, -0.22, 0.18)
    return jnp.clip(drawn, -limit, limit).astype(kind)


def setup_inputs(seed: int = 0) -> dict:
    arg_keys = jax.random.split(jax.random.key(seed), 19)
    block_in = normal_values(arg_keys[0], (TOKENS, D), 1.0, 6.0, ((0, 32),))
    out_cotan = normal_values(arg_keys[1], (TOKENS, D), 1.0, 6.0, ((0, 32),))
    segment_ids = jnp.searchsorted(jnp.cumsum(uneven(arg_keys[2], N_FSDP * 8, TOKENS, SEQ // 2, 2)), jnp.arange(TOKENS), side="right").astype(jnp.int32)
    expert_ids_keys = jax.random.split(jax.random.fold_in(arg_keys[3], 1), TOKENS // TOK_DEV)
    expert_ids_turns = jax.random.permutation(jax.random.fold_in(arg_keys[3], 3), TOKENS // TOK_DEV)
    expert_ids = jax.vmap(lambda own, number: deal_out(jax.random.fold_in(arg_keys[3], 2), own, number, TOK_DEV, EXPERTS, TOPK, CAP, 1))(expert_ids_keys, expert_ids_turns).reshape((TOKENS, TOPK))
    expert_wts = jnp.clip(0.5 + 1.0 * jax.random.uniform(arg_keys[4], (TOKENS, TOPK), jnp.float32) ** steps_of(arg_keys[4], (TOKENS, TOPK), ((0, 8),), -0.2, 0.2), 0.5, 1.5)
    attn_gain = jnp.clip(1.0 + 0.1 * jax.random.normal(arg_keys[5], (D,), jnp.float32), 0.5, 1.5).astype(jnp.bfloat16)
    query_proj = normal_values(arg_keys[6], (D, H * (NOPE + ROPE)), D ** -0.5, 0.125, ((0, 8), (1, 4)))
    latent_proj = normal_values(arg_keys[7], (D, LAT + ROPE), D ** -0.5, 0.125, ((0, 8),))
    latent_gain = jnp.clip(1.0 + 0.1 * jax.random.normal(arg_keys[8], (LAT,), jnp.float32), 0.5, 1.5).astype(jnp.bfloat16)
    latent_up = normal_values(arg_keys[9], (LAT, H * (NOPE + DV)), LAT ** -0.5, 0.25, ((0, 8), (1, 4)))
    out_proj = normal_values(arg_keys[10], (H * DV, D), (H * DV // 16) ** -0.5, 0.5, ((0, 4), (1, 8)))
    ffn_gain = jnp.clip(1.0 + 0.1 * jax.random.normal(arg_keys[11], (D,), jnp.float32), 0.5, 1.5).astype(jnp.bfloat16)
    shared_gate = normal_values(arg_keys[12], (D, FS), D ** -0.5, 0.125, ((0, 8), (1, 4)))
    shared_up = normal_values(arg_keys[13], (D, FS), D ** -0.5, 0.125, ((0, 8), (1, 4)))
    shared_down = normal_values(arg_keys[14], (FS, D), FS ** -0.5, 0.109375, ((0, 4), (1, 8)))
    routed_gate = normal_values(arg_keys[15], (EXPERTS, FF, D), D ** -0.5, 0.125, ((0, 8), (1, 4)))
    routed_up = normal_values(arg_keys[16], (EXPERTS, FF, D), D ** -0.5, 0.125, ((0, 8), (1, 4)))
    routed_down = normal_values(arg_keys[17], (EXPERTS, FF, D), FF ** -0.5, 0.15625, ((0, 8), (1, 4)))
    return {"block_in": block_in, "out_cotan": out_cotan, "segment_ids": segment_ids, "expert_ids": expert_ids, "expert_wts": expert_wts, "attn_gain": attn_gain, "query_proj": query_proj, "latent_proj": latent_proj, "latent_gain": latent_gain, "latent_up": latent_up, "out_proj": out_proj, "ffn_gain": ffn_gain, "shared_gate": shared_gate, "shared_up": shared_up, "shared_down": shared_down, "routed_gate": routed_gate, "routed_up": routed_up, "routed_down": routed_down}


EPSILON = 1e-06
THETA_BASE = 10000.0
MASK_FILL = -1e+30

@jax.custom_vjp
def low(v):
    return lax.optimization_barrier(v.astype(jnp.bfloat16)).astype(jnp.float32)

@jax.custom_vjp
def low_back(v):
    return v

def low_keep(v):
    return (low(v), None)

def low_pass(kept, grad):
    return (grad,)

def back_keep(v):
    return (v, None)

def back_low(kept, grad):
    return (low(grad),)
low.defvjp(low_keep, low_pass)
low_back.defvjp(back_keep, back_low)

def product(pattern, left_side, right_side):
    return jnp.einsum(pattern, left_side, right_side, precision=lax.Precision.HIGHEST)

def norm_rows(values, scaling):
    inverse = lax.rsqrt(lax.optimization_barrier(jnp.mean(values * values, axis=-1, keepdims=True)) + EPSILON)
    return values * inverse * scaling

def rope_tables(positions, width_rope):
    middle = width_rope // 2
    frequency = THETA_BASE ** (-(jnp.arange(middle) * 2).astype(jnp.float32) / width_rope)
    angles = positions.astype(jnp.float32)[:, None] * frequency[None, :]
    return (jnp.cos(angles), jnp.sin(angles))

def rotate(values, cosine, sine_part):
    middle = values.shape[-1] // 2
    first_half = values[..., :middle]
    second_half = values[..., middle:]
    return jnp.concatenate([first_half * cosine - second_half * sine_part, second_half * cosine + first_half * sine_part], axis=-1)

def slot_numbers(expert_row):
    per_block = expert_row.reshape(N_TP, TOK_DEV * TOPK)
    onehot = (per_block[:, :, None] == jnp.arange(EXPERTS, dtype=jnp.int32)[None, None, :]).astype(jnp.int32)
    running = jnp.cumsum(onehot, axis=1)
    slot_rank = lax.optimization_barrier(jnp.sum((running - 1) * onehot, axis=2))
    block_ids = jnp.arange(N_TP, dtype=jnp.int32)[:, None]
    return (per_block * (N_TP * CAP) + block_ids * CAP + slot_rank).reshape(SEQ * TOPK)

def routed_block(normed_ffn, expert_row, weight_row, routed_gate, routed_up, routed_down):
    slot_index = slot_numbers(expert_row)
    owners = (jnp.arange(SEQ * TOPK, dtype=jnp.int32) // TOPK).astype(jnp.int32)
    total_slots = EXPERTS * N_TP * CAP
    slot_owner = jnp.full((total_slots,), SEQ, jnp.int32).at[slot_index].set(owners)
    padded = jnp.concatenate([normed_ffn, jnp.zeros((1, D), jnp.float32)], axis=0)
    inputs = padded[slot_owner].reshape(EXPERTS, N_TP * CAP, D)
    gate_pre = low_back(product('esd,efd->esf', inputs, routed_gate))
    up_pre = low_back(product('esd,efd->esf', inputs, routed_up))
    hidden = low(jax.nn.silu(gate_pre) * up_pre)
    piece_width = FF // N_TP
    expert_out = jnp.zeros((EXPERTS, N_TP * CAP, D), jnp.float32)
    for portion in range(N_TP):
        lower = portion * piece_width
        partial_value = low(low_back(product('esf,efd->esd', hidden[:, :, lower:lower + piece_width], routed_down[:, lower:lower + piece_width, :])))
        expert_out = expert_out + partial_value
    flattened = expert_out.reshape(total_slots, D)
    picked = flattened[slot_index].reshape(SEQ, TOPK, D)
    return lax.optimization_barrier(jnp.sum(weight_row[:, :, None] * picked, axis=1))

def layer(weights, tokens, segment_row, expert_row, weight_row):
    attn_gain, query_proj, latent_proj, latent_gain, latent_up, out_proj, ffn_gain, shared_gate, shared_up, shared_down, routed_gate, routed_up, routed_down = weights
    positions = jnp.arange(SEQ, dtype=jnp.int32)
    cosine, sine_part = rope_tables(positions, ROPE)
    normed = low(norm_rows(tokens, attn_gain))
    queries = low_back(product('td,dc->tc', normed, query_proj)).reshape(SEQ, H, NOPE + ROPE)
    query_nope = low(queries[:, :, :NOPE])
    query_rope = low(rotate(queries[:, :, NOPE:], cosine[:, None, :], sine_part[:, None, :]))
    latent = low_back(product('td,dc->tc', normed, latent_proj))
    compressed = low(norm_rows(latent[:, :LAT], latent_gain))
    key_rope = low(rotate(latent[:, LAT:], cosine, sine_part))
    key_value = low_back(product('tl,lc->tc', compressed, latent_up)).reshape(SEQ, H, NOPE + DV)
    key_nope = low(key_value[:, :, :NOPE])
    values = low(key_value[:, :, NOPE:])
    score_scale = (NOPE + ROPE) ** (-0.5)
    scores = low_back((product('qhd,khd->hqk', query_nope, key_nope) + product('qhd,kd->hqk', query_rope, key_rope)) * score_scale)
    allowed = (positions[None, :] <= positions[:, None]) & (segment_row[None, :] == segment_row[:, None])
    probabilities = low(jax.nn.softmax(jnp.where(allowed[None], scores, MASK_FILL), axis=-1))
    attended = low(low_back(product('hqk,khd->qhd', probabilities, values))).reshape(SEQ, H * DV)
    mixed_rows = tokens + low_back(product('tc,cd->td', attended, out_proj))
    normed_ffn = low(norm_rows(mixed_rows, ffn_gain))
    shared_gate_pre = low_back(product('td,df->tf', normed_ffn, shared_gate))
    shared_up_pre = low_back(product('td,df->tf', normed_ffn, shared_up))
    shared_hidden = low(jax.nn.silu(shared_gate_pre) * shared_up_pre)
    shared_out = low_back(product('tf,fd->td', shared_hidden, shared_down))
    routed_out = routed_block(normed_ffn, expert_row, weight_row, routed_gate, routed_up, routed_down)
    return mixed_rows + shared_out + routed_out

def reference(block_in, out_cotan, segment_ids, expert_ids, expert_wts, attn_gain, query_proj, latent_proj, latent_gain, latent_up, out_proj, ffn_gain, shared_gate, shared_up, shared_down, routed_gate, routed_up, routed_down):
    weights = (attn_gain.astype(jnp.float32), query_proj.astype(jnp.float32), latent_proj.astype(jnp.float32), latent_gain.astype(jnp.float32), latent_up.astype(jnp.float32), out_proj.astype(jnp.float32), ffn_gain.astype(jnp.float32), shared_gate.astype(jnp.float32), shared_up.astype(jnp.float32), shared_down.astype(jnp.float32), routed_gate.astype(jnp.float32), routed_up.astype(jnp.float32), routed_down.astype(jnp.float32))
    segment_rows = segment_ids.reshape(N_FSDP, SEQ)
    expert_rows = expert_ids.reshape(N_FSDP, SEQ, TOPK)
    weight_rows = expert_wts.reshape(N_FSDP, SEQ, TOPK)

    def forward(weight_set, block_all):

        def one_sequence(carry, pieces):
            tokens, segment_row, expert_row, weight_row = pieces
            return (carry, layer(weight_set, tokens, segment_row, expert_row, weight_row))
        unused_carry, outputs = lax.scan(jax.checkpoint(one_sequence), jnp.zeros((), jnp.float32), (block_all.reshape(N_FSDP, SEQ, D), segment_rows, expert_rows, weight_rows))
        return outputs.reshape(TOKENS, D)
    block_sum, pullback = jax.vjp(forward, weights, block_in.astype(jnp.float32))
    weight_grads, block_in_grad = pullback(out_cotan.astype(jnp.float32))
    attn_gain_grad, query_proj_grad, latent_proj_grad, latent_gain_grad, latent_up_grad, out_proj_grad, ffn_gain_grad, shared_gate_grad, shared_up_grad, shared_down_grad, routed_gate_grad, routed_up_grad, routed_down_grad = weight_grads
    return (block_sum.astype(jnp.bfloat16), block_in_grad, attn_gain_grad, query_proj_grad, latent_proj_grad, latent_gain_grad, latent_up_grad, out_proj_grad, ffn_gain_grad, shared_gate_grad, shared_up_grad, shared_down_grad, routed_gate_grad, routed_up_grad, routed_down_grad)
```

```python
import functools

import jax
import jax.numpy as jnp
from jax import lax
from jax.experimental import pallas as pl
from jax.experimental.pallas import tpu as pltpu
from jax.sharding import PartitionSpec as P

H = 16
NOPE = 128
ROPE = 64
DV = 128
LAT = 512
TOPK = 6
SEQ = 512
HALF = 256
QUARTET = 4


EPSILON = 1e-06
THETA_BASE = 10000.0
MASK_FILL = -1e30
NO_SLOT = -1e6

BF = jnp.bfloat16
F32 = jnp.float32


def rope_tables(positions, width_rope):
    middle = width_rope // 2
    frequency = THETA_BASE ** (-(jnp.arange(middle) * 2).astype(jnp.float32) / width_rope)
    angles = positions.astype(jnp.float32)[:, None] * frequency[None, :]
    return (jnp.cos(angles), jnp.sin(angles))


def rotate(values, cosine, sine_part):
    middle = values.shape[-1] // 2
    first_half = values[..., :middle]
    second_half = values[..., middle:]
    return jnp.concatenate(
        [
            first_half * cosine - second_half * sine_part,
            second_half * cosine + first_half * sine_part,
        ],
        axis=-1,
    )


def unrotate(values, cosine, sine_part):
    middle = values.shape[-1] // 2
    first_half = values[..., :middle]
    second_half = values[..., middle:]
    return jnp.concatenate(
        [
            first_half * cosine + second_half * sine_part,
            second_half * cosine - first_half * sine_part,
        ],
        axis=-1,
    )


def norm_parts(values):
    inverse = lax.rsqrt(jnp.mean(values * values, axis=-1, keepdims=True) + EPSILON)
    return (values * inverse, inverse)


def norm_back(upstream, unit_rows, inverse, scaling):
    scaled = upstream * scaling
    gain_grad = jnp.sum(upstream * unit_rows, axis=0)
    input_grad = inverse * (
        scaled - unit_rows * jnp.mean(scaled * unit_rows, axis=-1, keepdims=True)
    )
    return (gain_grad, input_grad)


def silu_back(grad_hidden, gate_pre, up_pre):
    sigmoid = jax.nn.sigmoid(gate_pre)
    gate_grad = grad_hidden * up_pre * (sigmoid * (1.0 + gate_pre * (1.0 - sigmoid)))
    up_grad = grad_hidden * (gate_pre * sigmoid)
    return (gate_grad.astype(jnp.bfloat16), up_grad.astype(jnp.bfloat16))


def is_power(count):
    return count & (count - 1) == 0


def swap(values, axis_name, bit):
    count = lax.axis_size(axis_name)
    return lax.ppermute(values, axis_name, [(i, i ^ bit) for i in range(count)])


def dot_rows(left, right):
    return lax.dot_general(left, right, (((1,), (1,)), ((), ())), preferred_element_type=F32)


def dot_plain(left, right):
    return lax.dot_general(left, right, (((1,), (0,)), ((), ())), preferred_element_type=F32)


def dot_first(left, right):
    return lax.dot_general(left, right, (((0,), (0,)), ((), ())), preferred_element_type=F32)


def select_rows(slot_rows, experts, cap):
    row = lax.broadcasted_iota(jnp.int32, (experts * cap, HALF), 0).astype(F32)
    hit = row == slot_rows[0:1, :]
    for e in range(1, experts):
        hit = hit | (row == slot_rows[e : e + 1, :] + float(e * cap))
    return hit


def select_cols(slot_cols, experts, cap):
    lane = lax.broadcasted_iota(jnp.int32, (HALF, experts * cap), 1).astype(F32)
    hit = lane == slot_cols[:, 0:1]
    for e in range(1, experts):
        hit = hit | (lane == slot_cols[:, e : e + 1] + float(e * cap))
    return hit


def slot_weights(hit, weight_rows, experts, cap):
    pieces = []
    for e in range(experts):
        part = hit[e * cap : (e + 1) * cap, :]
        pieces.append(
            jnp.sum(jnp.where(part, weight_rows[e : e + 1, :], 0.0), axis=1, keepdims=True)
        )
    return jnp.concatenate(pieces, axis=0)


def expert_front_kernel(step, experts, cap, aliased, *refs):
    count = QUARTET
    x_in, dy_in = refs[:count], refs[count : 2 * count]
    gate_up_in, down_in, slot_row_ref, weight_row_ref, slot_col_ref = refs[
        2 * count : 2 * count + 5
    ]
    base = 2 * count + 5 + aliased
    dx_out = refs[base : base + count]
    x_all, d_all, hid_all, dgu_all = refs[base + count : base + count + 4]
    (xb, db, gate_up, down, xs, ds, dxs, dxo, hid, dgu, sem_in, sem_w, sem_out, sem_dx) = refs[
        base + count + 4 :
    ]
    width = xb.shape[2]
    pad = down.shape[1]
    tile = min(1024, width)
    x_copies = [pltpu.make_async_copy(x_in[q], xb.at[q], sem_in.at[q]) for q in range(count)]
    d_copies = [
        pltpu.make_async_copy(dy_in[q], db.at[q], sem_in.at[count + q]) for q in range(count)
    ]
    w_copies = [
        pltpu.make_async_copy(gate_up_in, gate_up, sem_w.at[0]),
        pltpu.make_async_copy(down_in, down, sem_w.at[1]),
    ]
    for q in range(count):
        x_copies[q].start()
        d_copies[q].start()
    for copy in w_copies:
        copy.start()
    for q in range(count):
        x_copies[q].wait()
        d_copies[q].wait()

        hit = select_rows(slot_row_ref[q], experts, cap)
        weights = slot_weights(hit, weight_row_ref[q], experts, cap)
        choose = jnp.where(hit, 1.0, 0.0).astype(BF)

        def spread(n, carry, q=q, choose=choose, weights=weights):
            cols = pl.ds(pl.multiple_of(n * tile, tile), tile)
            rows = dot_plain(choose, xb[q, :, cols])
            grads = dot_plain(choose, db[q, :, cols]) * weights
            for e in range(experts):
                xs[e, q * cap : (q + 1) * cap, cols] = rows[e * cap : (e + 1) * cap].astype(BF)
                ds[e, q * cap : (q + 1) * cap, cols] = grads[e * cap : (e + 1) * cap].astype(BF)
            return carry

        lax.fori_loop(0, width // tile, spread, 0)
    out_copies = [
        pltpu.make_async_copy(xs, x_all.at[step], sem_out.at[0]),
        pltpu.make_async_copy(ds, d_all.at[step], sem_out.at[1]),
        pltpu.make_async_copy(hid, hid_all.at[step], sem_out.at[2]),
        pltpu.make_async_copy(dgu, dgu_all.at[step], sem_out.at[3]),
    ]
    out_copies[0].start()
    out_copies[1].start()
    for copy in w_copies:
        copy.wait()

    def one_expert(e, carry):
        both = dot_rows(xs[e], gate_up[e])
        gate_pre, up_pre = both[:, :pad], both[:, pad:]
        d_hidden = dot_rows(ds[e], down[e])
        sigmoid = jax.nn.sigmoid(gate_pre)
        silu = gate_pre * sigmoid
        hid[e] = (silu * up_pre).astype(BF)
        gate_grad = d_hidden * up_pre * (sigmoid * (1.0 + gate_pre * (1.0 - sigmoid)))
        grads = jnp.concatenate([gate_grad, d_hidden * silu], axis=1).astype(BF)
        dgu[e] = grads

        def back(n, inner):
            cols = pl.ds(pl.multiple_of(n * tile, tile), tile)
            part = dot_plain(dgu[e], gate_up[e, :, cols]).astype(BF)
            for q in range(count):
                dxs[q, pl.ds(pl.multiple_of(e * cap, cap), cap), cols] = part[
                    q * cap : (q + 1) * cap
                ]
            return inner

        lax.fori_loop(0, width // tile, back, 0)
        return carry

    lax.fori_loop(0, experts, one_expert, 0)
    out_copies[2].start()
    out_copies[3].start()
    dx_copies = [pltpu.make_async_copy(dxo.at[q], dx_out[q], sem_dx.at[q]) for q in range(count)]
    for q in range(count):
        choose = jnp.where(select_cols(slot_col_ref[q], experts, cap), 1.0, 0.0).astype(BF)

        def gather(n, carry, q=q, choose=choose):
            cols = pl.ds(pl.multiple_of(n * tile, tile), tile)
            dxo[q, :, cols] = dot_plain(choose, dxs[q, :, cols]).astype(BF)
            return carry

        lax.fori_loop(0, width // tile, gather, 0)
        dx_copies[q].start()
    for copy in out_copies:
        copy.wait()
    for copy in dx_copies:
        copy.wait()


def expert_front(step, steps, x_parts, dy_parts, gate_up, down, tables, kept, cap):
    experts, wide, width = gate_up.shape
    pad = wide // 2
    slots = QUARTET * cap
    slot_row, weight_row, slot_col = (t[step] for t in tables)
    any_spec = pl.BlockSpec(memory_space=pl.ANY)
    vmem_spec = pl.BlockSpec(memory_space=pltpu.VMEM)
    half_shape = jax.ShapeDtypeStruct((HALF, width), BF)
    kept_shapes = [
        jax.ShapeDtypeStruct((steps, experts, slots, columns), BF)
        for columns in (width, width, pad, wide)
    ]
    results = pl.pallas_call(
        functools.partial(expert_front_kernel, step, experts, cap, len(kept)),
        out_shape=[half_shape] * QUARTET + kept_shapes,
        in_specs=[any_spec] * (2 * QUARTET + 2) + [vmem_spec] * 3 + [any_spec] * len(kept),
        out_specs=[any_spec] * (QUARTET + 4),
        input_output_aliases={2 * QUARTET + 5 + i: QUARTET + i for i in range(len(kept))},
        scratch_shapes=[
            pltpu.VMEM((QUARTET, HALF, width), BF),
            pltpu.VMEM((QUARTET, HALF, width), BF),
            pltpu.VMEM((experts, wide, width), BF),
            pltpu.VMEM((experts, pad, width), BF),
            pltpu.VMEM((experts, slots, width), BF),
            pltpu.VMEM((experts, slots, width), BF),
            pltpu.VMEM((QUARTET, experts * cap, width), BF),
            pltpu.VMEM((QUARTET, HALF, width), BF),
            pltpu.VMEM((experts, slots, pad), BF),
            pltpu.VMEM((experts, slots, wide), BF),
            pltpu.SemaphoreType.DMA((2 * QUARTET,)),
            pltpu.SemaphoreType.DMA((2,)),
            pltpu.SemaphoreType.DMA((4,)),
            pltpu.SemaphoreType.DMA((QUARTET,)),
        ],
        compiler_params=pltpu.CompilerParams(vmem_limit_bytes=62 * 1024 * 1024),
        cost_estimate=pl.CostEstimate(
            flops=2 * slots * experts * width * pad * 5
            + 6 * QUARTET * HALF * experts * cap * width,
            bytes_accessed=2 * width * (3 * QUARTET * HALF + experts * 3 * pad + 2 * experts * slots),
            transcendentals=slots * experts * pad,
        ),
        name="expert_front",
    )(*x_parts, *dy_parts, gate_up, down, slot_row, weight_row, slot_col, *kept)
    return list(results[:QUARTET]), list(results[QUARTET:])


def expert_out_kernel(experts, cap, hid, down, slot_row, weight_row, slot_col, out, parts):
    width = down.shape[2]
    tile = min(1024, width)
    for q in range(QUARTET):
        hit = select_rows(slot_row[0, q], experts, cap)
        weights = slot_weights(hit, weight_row[0, q], experts, cap)

        def front(n, carry, q=q, weights=weights):
            cols = pl.ds(pl.multiple_of(n * tile, tile), tile)
            for e in range(experts):
                rows = dot_plain(hid[0, e, q * cap : (q + 1) * cap, :], down[e, :, cols])
                parts[q, e * cap : (e + 1) * cap, cols] = (
                    rows * weights[e * cap : (e + 1) * cap]
                ).astype(BF)
            return carry

        lax.fori_loop(0, width // tile, front, 0)
    for q in range(QUARTET):
        choose = jnp.where(select_cols(slot_col[0, q], experts, cap), 1.0, 0.0).astype(BF)

        def gather(n, carry, q=q, choose=choose):
            cols = pl.ds(pl.multiple_of(n * tile, tile), tile)
            out[0, q, :, cols] = dot_plain(choose, parts[q, :, cols]).astype(BF)
            return carry

        lax.fori_loop(0, width // tile, gather, 0)


def expert_out(hid_all, down, tables, cap):
    steps, experts, slots, pad = hid_all.shape
    width = down.shape[2]
    slot_row, weight_row, slot_col = tables
    return pl.pallas_call(
        functools.partial(expert_out_kernel, experts, cap),
        grid=(steps,),
        out_shape=jax.ShapeDtypeStruct((steps, QUARTET, HALF, width), BF),
        in_specs=[
            pl.BlockSpec((1, experts, slots, pad), lambda i: (i, 0, 0, 0)),
            pl.BlockSpec((experts, pad, width), lambda i: (0, 0, 0)),
            pl.BlockSpec((1,) + slot_row.shape[1:], lambda i: (i, 0, 0, 0)),
            pl.BlockSpec((1,) + weight_row.shape[1:], lambda i: (i, 0, 0, 0)),
            pl.BlockSpec((1,) + slot_col.shape[1:], lambda i: (i, 0, 0, 0)),
        ],
        out_specs=pl.BlockSpec((1, QUARTET, HALF, width), lambda i: (i, 0, 0, 0)),
        scratch_shapes=[pltpu.VMEM((QUARTET, experts * cap, width), BF)],
        compiler_params=pltpu.CompilerParams(vmem_limit_bytes=48 * 1024 * 1024),
        cost_estimate=pl.CostEstimate(
            flops=steps * (2 * slots * experts * width * pad + 2 * QUARTET * HALF * experts * cap * width),
            bytes_accessed=2 * steps * QUARTET * HALF * width + 2 * hid_all.size + 2 * down.size,
            transcendentals=0,
        ),
        name="expert_out",
    )(hid_all, down, slot_row, weight_row, slot_col)


def expert_grads_kernel(dgu, x, hid, d, gate_grad, up_grad, down_grad):
    local = gate_grad.shape[1]
    pad = hid.shape[3]
    width = x.shape[3]
    tile = min(1024, width)

    @pl.when(pl.program_id(1) == 0)
    def _():
        gate_grad[...] = jnp.zeros_like(gate_grad)
        up_grad[...] = jnp.zeros_like(up_grad)
        down_grad[...] = jnp.zeros_like(down_grad)

    def part(n, carry):
        cols = pl.ds(pl.multiple_of(n * tile, tile), tile)
        gate_grad[0, :, cols] += dot_first(dgu[0, 0, :, :pad], x[0, 0, :, cols])[:local]
        up_grad[0, :, cols] += dot_first(dgu[0, 0, :, pad:], x[0, 0, :, cols])[:local]
        down_grad[0, :, cols] += dot_first(hid[0, 0], d[0, 0, :, cols])[:local]
        return carry

    lax.fori_loop(0, width // tile, part, 0)


def expert_grads(kept, local):
    x_all, d_all, hid_all, dgu_all = kept
    steps, experts, slots, width = x_all.shape
    pad = hid_all.shape[3]

    def block(array):
        return pl.BlockSpec((1, 1) + array.shape[2:], lambda e, i: (i, e, 0, 0))

    grad = jax.ShapeDtypeStruct((experts, local, width), F32)
    return pl.pallas_call(
        expert_grads_kernel,
        grid=(experts, steps),
        out_shape=[grad] * 3,
        in_specs=[block(dgu_all), block(x_all), block(hid_all), block(d_all)],
        out_specs=[pl.BlockSpec((1, local, width), lambda e, i: (e, 0, 0))] * 3,
        compiler_params=pltpu.CompilerParams(vmem_limit_bytes=48 * 1024 * 1024),
        cost_estimate=pl.CostEstimate(
            flops=2 * 3 * steps * experts * slots * width * pad,
            bytes_accessed=2 * (x_all.size + d_all.size + hid_all.size + dgu_all.size)
            + 12 * experts * local * width,
            transcendentals=0,
        ),
        name="expert_grads",
    )(dgu_all, x_all, hid_all, d_all)


def plane_units(count):
    if count == 8:
        return [
            [(0, 0), (0, 1), (1, 0), (1, 1)],
            [(2, 0), (4, 1), (3, 0), (5, 1)],
            [(2, 1), (4, 0), (3, 1), (5, 0)],
            [(6, 0), (6, 1), (7, 0), (7, 1)],
        ]
    return [[(2 * i + j // 2, j % 2) for j in range(4)] for i in range(count // 2)]


def plane_gather(rows, count):
    top, bottom = rows[:HALF], rows[HALF:]
    blocks = {}
    if count == 8:
        own = {0: top, 1: bottom}
        for h in (0, 1):
            blocks[0, h] = own[h]
            blocks[1, h] = swap(own[h], "fsdp", 1)
        blocks[2, 0] = swap(top, "fsdp", 2)
        blocks[4, 1] = swap(bottom, "fsdp", 4)
        blocks[2, 1] = swap(bottom, "fsdp", 2)
        blocks[4, 0] = swap(top, "fsdp", 4)
        blocks[6, 0] = swap(blocks[2, 0], "fsdp", 4)
        blocks[6, 1] = swap(blocks[4, 1], "fsdp", 2)
        for r in (2, 4, 6):
            for h in (0, 1):
                blocks[r + 1, h] = swap(blocks[r, h], "fsdp", 1)
        return blocks
    gathered = lax.all_gather(rows, "fsdp", axis=0)
    for r in range(count):
        blocks[r, 0] = gathered[r, :HALF]
        blocks[r, 1] = gathered[r, HALF:]
    return blocks


def plane_scatter(parts, count):
    if count == 8:

        def add(left, right):
            return left.astype(F32) + right.astype(F32)

        chip = {}
        for r in (2, 4, 6, 0):
            for h in (0, 1):
                chip[r, h] = add(parts[r, h], swap(parts[r + 1, h], "fsdp", 1))
        top = add(chip[0, 0], swap(chip[2, 0].astype(BF), "fsdp", 2))
        bottom = add(chip[0, 1], swap(chip[4, 1].astype(BF), "fsdp", 4))
        over_top = add(chip[4, 0], swap(chip[6, 0].astype(BF), "fsdp", 2)).astype(BF)
        over_bottom = add(chip[2, 1], swap(chip[6, 1].astype(BF), "fsdp", 4)).astype(BF)
        top = add(top, swap(over_top, "fsdp", 4))
        bottom = add(bottom, swap(over_bottom, "fsdp", 2))
        return jnp.concatenate([top, bottom], axis=0)
    stacked = jnp.concatenate([parts[r, h] for r in range(count) for h in (0, 1)], axis=0)
    return lax.psum_scatter(stacked, "fsdp", scatter_dimension=0, tiled=True).astype(F32)


def sum_everywhere(values):
    for axis_name in ("fsdp", "tp"):
        count = lax.axis_size(axis_name)
        if is_power(count):
            bit = 1
            while bit < count:
                values = values + swap(values, axis_name, bit)
                bit *= 2
        else:
            values = lax.psum(values, axis_name)
    return values


def expert_tables(expert_ids, expert_wts, local_experts, units, cap):
    fsdp_count = lax.axis_size("fsdp")
    fsdp_rank = lax.axis_index("fsdp")
    expert_count = local_experts * fsdp_count
    names = jnp.arange(expert_count, dtype=jnp.int32)[:, None]
    member = jnp.zeros((expert_count, SEQ), jnp.bool_)
    weight = jnp.zeros((expert_count, SEQ), F32)
    ids_rows, wts_rows = expert_ids.T, expert_wts.T
    for pick in range(TOPK):
        same = ids_rows[pick : pick + 1] == names
        member = member | same
        weight = weight + jnp.where(same, wts_rows[pick : pick + 1], 0.0)
    position = jnp.arange(HALF)
    before = (position[:, None] < position[None, :]).astype(BF)
    rank = jnp.dot(
        member.astype(BF).reshape(expert_count * 2, HALF), before, preferred_element_type=F32
    ).reshape(expert_count, SEQ)
    slot = jnp.where(member, rank, NO_SLOT)
    table = jnp.concatenate([slot, weight], axis=0)
    table = lax.all_gather(table, "fsdp", axis=0).reshape(
        fsdp_count, 2, fsdp_count, local_experts, 2, HALF
    )
    table = lax.dynamic_index_in_dim(table, fsdp_rank, axis=2, keepdims=False)
    relative = jnp.arange(fsdp_count, dtype=jnp.int32)
    order = relative ^ fsdp_rank if fsdp_count == 8 else relative
    table = jnp.take(table, order, axis=0)
    slot_steps, weight_steps = [], []
    for unit in units:
        slot_steps.append(jnp.stack([table[r, 0, :, h] for r, h in unit]))
        weight_steps.append(jnp.stack([table[r, 1, :, h] for r, h in unit]))
    slot_row, weight_row = jnp.stack(slot_steps), jnp.stack(weight_steps)
    return (slot_row, weight_row, jnp.swapaxes(slot_row, 2, 3))


def per_device(
    block_in,
    out_cotan,
    segment_ids,
    expert_ids,
    expert_wts,
    attn_gain,
    query_proj,
    latent_proj,
    latent_gain,
    latent_up,
    out_proj,
    ffn_gain,
    shared_gate,
    shared_up,
    shared_down,
    routed_gate,
    routed_up,
    routed_down,
):
    tp_count = lax.axis_size("tp")
    fsdp_count = lax.axis_size("fsdp")
    tp_rank = lax.axis_index("tp")
    fsdp_rank = lax.axis_index("fsdp")
    tok_rows, model_width = block_in.shape
    local_experts, local_hidden = routed_gate.shape[:2]
    expert_count = local_experts * fsdp_count
    cap_rows = tok_rows * TOPK * 4 // (3 * expert_count)
    cap = cap_rows * (HALF // tok_rows)
    heads_local = H // tp_count
    head_width = NOPE + ROPE
    score_scale = head_width ** (-0.5)
    shard_rows, query_cols = query_proj.shape
    latent_cols = latent_proj.shape[1]
    up_cols = latent_up.shape[1]
    out_rows = out_proj.shape[0]
    units = plane_units(fsdp_count)

    joint = query_cols + latent_cols
    spare = (-joint) % 128
    spare = spare + 128 if spare < 3 else spare
    gains = jnp.concatenate(
        [
            attn_gain[:, None],
            ffn_gain[:, None],
            jnp.pad(latent_gain, (0, shard_rows - latent_gain.shape[0]))[:, None],
            jnp.zeros((shard_rows, spare - 3), BF),
        ],
        axis=1,
    )
    packed = jnp.concatenate(
        [query_proj, latent_proj, gains, latent_up.reshape(shard_rows, -1)], axis=1
    )
    packed_all = lax.all_gather(packed, "fsdp", axis=0, tiled=True)
    joint_weight = packed_all[:, :joint]
    gain_attn = packed_all[:, joint].astype(F32)
    gain_ffn = packed_all[:, joint + 1].astype(F32)
    gain_latent = (
        packed_all[:, joint + 2]
        .reshape(fsdp_count, shard_rows)[:, : latent_gain.shape[0]]
        .reshape(LAT)
        .astype(F32)
    )
    latent_up_weight = packed_all[:, joint + spare :].reshape(LAT, up_cols)
    tokens_all = lax.all_gather(block_in, "tp", axis=0, tiled=True)
    out_down = lax.all_gather(
        jnp.concatenate([out_proj, shared_down], axis=0), "fsdp", axis=1, tiled=True
    )
    out_weight, shared_down_weight = out_down[:out_rows], out_down[out_rows:]
    cotan_all = lax.all_gather(out_cotan, "tp", axis=0, tiled=True)
    shared_weight = lax.all_gather(
        jnp.concatenate([shared_gate, shared_up], axis=1), "fsdp", axis=0, tiled=True
    )
    shared_cols = shared_gate.shape[1]
    tables = expert_tables(expert_ids, expert_wts, local_experts, units, cap)
    hidden_pad = -(-local_hidden // 128) * 128
    lift = ((0, 0), (0, hidden_pad - local_hidden), (0, 0))
    routed_gate_up = jnp.concatenate([jnp.pad(routed_gate, lift), jnp.pad(routed_up, lift)], axis=1)
    routed_down_pad = jnp.pad(routed_down, lift)

    unit_all, inverse_all = norm_parts(tokens_all.astype(F32))
    normed_all = (unit_all * gain_attn).astype(BF)
    joint_rows = jnp.dot(normed_all, joint_weight, preferred_element_type=F32)
    queries = joint_rows[:, :query_cols].reshape(SEQ, heads_local, head_width)
    latent = joint_rows[:, query_cols:]
    unit_lat, inverse_lat = norm_parts(latent[:, :LAT])
    positions = jnp.arange(SEQ, dtype=jnp.int32)
    cosine, sine_part = rope_tables(positions, ROPE)
    compressed_all = (unit_lat * gain_latent).astype(BF)
    key_rope_all = rotate(latent[:, LAT:], cosine, sine_part).astype(BF)
    query_cat = jnp.concatenate(
        [
            queries[:, :, :NOPE],
            rotate(queries[:, :, NOPE:], cosine[:, None, :], sine_part[:, None, :]),
        ],
        axis=2,
    ).astype(BF)
    key_value = (
        jnp.dot(compressed_all, latent_up_weight, preferred_element_type=F32)
        .reshape(SEQ, heads_local, NOPE + DV)
        .astype(BF)
    )
    key_cat = jnp.concatenate(
        [
            key_value[:, :, :NOPE],
            jnp.broadcast_to(key_rope_all[:, None, :], (SEQ, heads_local, ROPE)),
        ],
        axis=2,
    )
    values = key_value[:, :, NOPE:]
    allowed = (positions[None, :] <= positions[:, None]) & (
        segment_ids[None, :] == segment_ids[:, None]
    )
    raw_scores = (
        jnp.einsum("qhd,khd->hqk", query_cat, key_cat, preferred_element_type=F32) * score_scale
    )
    masked = jnp.where(allowed[None], raw_scores, MASK_FILL)
    top_score = jnp.max(masked, axis=2, keepdims=True)
    exponent = jnp.exp(masked - top_score)
    row_total = jnp.sum(exponent, axis=2, keepdims=True)
    probabilities = exponent / row_total
    probs_low = probabilities.astype(BF)
    attended = (
        jnp.einsum("hqk,khd->qhd", probs_low, values, preferred_element_type=F32)
        .reshape(SEQ, heads_local * DV)
        .astype(BF)
    )
    attn_rows = lax.psum_scatter(
        jnp.dot(attended, out_weight, preferred_element_type=F32).astype(BF),
        "tp",
        scatter_dimension=0,
        tiled=True,
    ).astype(F32)
    mixed_rows = block_in.astype(F32) + attn_rows
    unit_two, inverse_two = norm_parts(mixed_rows)
    normed_ffn = (unit_two * gain_ffn).astype(BF)
    normed_ffn_all = lax.all_gather(normed_ffn, "tp", axis=0, tiled=True)

    x_blocks = plane_gather(normed_ffn_all, fsdp_count)
    dy_blocks = plane_gather(cotan_all, fsdp_count)
    kept = []
    dx_parts = {}
    for step, unit in enumerate(units):
        dx_list, kept = expert_front(
            step,
            len(units),
            [x_blocks[key] for key in unit],
            [dy_blocks[key] for key in unit],
            routed_gate_up,
            routed_down_pad,
            tables,
            kept,
            cap,
        )
        for key, part in zip(unit, dx_list):
            dx_parts[key] = part
    d_routed_in = plane_scatter(dx_parts, fsdp_count)
    out_array = expert_out(kept[2], routed_down_pad, tables, cap)
    out_parts = {
        key: out_array[step, q] for step, unit in enumerate(units) for q, key in enumerate(unit)
    }
    routed_rows = plane_scatter(out_parts, fsdp_count)
    routed_gate_grad, routed_up_grad, routed_down_grad = expert_grads(kept, local_hidden)

    shared_pre = jnp.dot(normed_ffn_all, shared_weight, preferred_element_type=F32)
    shared_gate_pre, shared_up_pre = shared_pre[:, :shared_cols], shared_pre[:, shared_cols:]
    shared_hidden = (jax.nn.silu(shared_gate_pre) * shared_up_pre).astype(BF)
    shared_rows = jnp.dot(shared_hidden, shared_down_weight, preferred_element_type=F32)
    shared_down_part = jnp.dot(shared_hidden.T, cotan_all, preferred_element_type=F32)
    d_shared_hidden = jnp.dot(cotan_all, shared_down_weight.T, preferred_element_type=F32)
    d_shared = jnp.concatenate(silu_back(d_shared_hidden, shared_gate_pre, shared_up_pre), axis=1)
    shared_part = jnp.dot(normed_ffn_all.T, d_shared, preferred_element_type=F32)
    d_shared_in = jnp.dot(d_shared, shared_weight.T, preferred_element_type=F32)

    d_normed_ffn = lax.psum_scatter(
        (d_shared_in + d_routed_in).astype(BF), "tp", scatter_dimension=0, tiled=True
    ).astype(F32)
    ffn_rows = lax.psum_scatter(
        (shared_rows + routed_rows).astype(BF), "tp", scatter_dimension=0, tiled=True
    ).astype(F32)
    block_out = (mixed_rows + ffn_rows).astype(BF)
    ffn_gain_part, d_mixed_norm = norm_back(d_normed_ffn, unit_two, inverse_two, gain_ffn)
    d_mixed = out_cotan.astype(F32) + d_mixed_norm
    d_proj_all = lax.all_gather(d_mixed.astype(BF), "tp", axis=0, tiled=True)

    out_part = jnp.dot(attended.T, d_proj_all, preferred_element_type=F32)
    d_attended = (
        jnp.dot(d_proj_all, out_weight.T, preferred_element_type=F32)
        .astype(BF)
        .reshape(SEQ, heads_local, DV)
    )
    prob_grad = jnp.einsum("qhd,khd->hqk", d_attended, values, preferred_element_type=F32)
    score_grad = (
        probabilities
        * (prob_grad - jnp.sum(probabilities * prob_grad, axis=2, keepdims=True))
    ).astype(BF)
    query_grad = (
        jnp.einsum("hqk,khd->qhd", score_grad, key_cat, preferred_element_type=F32) * score_scale
    )
    key_grad = (
        jnp.einsum("hqk,qhd->khd", score_grad, query_cat, preferred_element_type=F32) * score_scale
    )
    value_grad = jnp.einsum("hqk,qhd->khd", probs_low, d_attended, preferred_element_type=F32)
    d_queries = (
        jnp.concatenate(
            [
                query_grad[:, :, :NOPE],
                unrotate(query_grad[:, :, NOPE:], cosine[:, None, :], sine_part[:, None, :]),
            ],
            axis=2,
        )
        .reshape(SEQ, heads_local * head_width)
        .astype(BF)
    )
    d_key_value = (
        jnp.concatenate([key_grad[:, :, :NOPE], value_grad], axis=2)
        .reshape(SEQ, heads_local * (NOPE + DV))
        .astype(BF)
    )
    latent_up_part = jnp.dot(compressed_all.T, d_key_value, preferred_element_type=F32)
    d_compressed = jnp.dot(d_key_value, latent_up_weight.T, preferred_element_type=F32)
    d_key_rope = jnp.sum(key_grad[:, :, NOPE:], axis=1)
    latent_gain_part, d_latent_main = norm_back(d_compressed, unit_lat, inverse_lat, gain_latent)
    d_latent = jnp.concatenate(
        [d_latent_main, unrotate(d_key_rope, cosine, sine_part)], axis=1
    ).astype(BF)
    d_joint = jnp.concatenate([d_queries, d_latent], axis=1)
    joint_part = jnp.dot(normed_all.T, d_joint, preferred_element_type=F32)
    d_normed_part = jnp.dot(d_joint, joint_weight.T, preferred_element_type=F32)
    attn_gain_part = jnp.sum(d_normed_part * unit_all, axis=0)
    d_normed = lax.psum_scatter(
        d_normed_part.astype(BF), "tp", scatter_dimension=0, tiled=True
    ).astype(F32)
    unit_one, inverse_one = norm_parts(block_in.astype(F32))
    _, d_tokens_norm = norm_back(d_normed, unit_one, inverse_one, gain_attn)
    block_in_grad = d_mixed + d_tokens_norm

    def scatter(part, dimension):
        return lax.psum_scatter(
            part.astype(BF), "fsdp", scatter_dimension=dimension, tiled=True
        )

    joint_grad = scatter(joint_part, 0)
    query_proj_grad = joint_grad[:, :query_cols].astype(F32)
    latent_proj_grad = lax.psum_scatter(
        joint_grad[:, query_cols:], "tp", scatter_dimension=0, tiled=True
    ).astype(F32)
    latent_up_grad = scatter(latent_up_part, 0).astype(F32)
    out_proj_grad = scatter(out_part, 1).astype(F32)
    shared_grad = scatter(shared_part, 0).astype(F32)
    shared_gate_grad, shared_up_grad = shared_grad[:, :shared_cols], shared_grad[:, shared_cols:]
    shared_down_grad = scatter(shared_down_part, 1).astype(F32)
    gain_sums = sum_everywhere(
        jnp.concatenate([attn_gain_part, latent_gain_part, ffn_gain_part]).reshape(-1, 128)
    ).reshape(-1)
    device = fsdp_rank * tp_count + tp_rank
    devices = tp_count * fsdp_count

    def own_gain(start, size):
        return lax.dynamic_slice(gain_sums, (start + device * (size // devices),), (size // devices,))

    attn_gain_grad = own_gain(0, model_width)
    latent_gain_grad = own_gain(model_width, LAT)
    ffn_gain_grad = own_gain(model_width + LAT, model_width)
    return (
        block_out,
        block_in_grad,
        attn_gain_grad,
        query_proj_grad,
        latent_proj_grad,
        latent_gain_grad,
        latent_up_grad,
        out_proj_grad,
        ffn_gain_grad,
        shared_gate_grad,
        shared_up_grad,
        shared_down_grad,
        routed_gate_grad,
        routed_up_grad,
        routed_down_grad,
    )


def solution(mesh):
    placed = (
        P(("fsdp", "tp"), None),
        P(("fsdp", "tp"), None),
        P("fsdp"),
        P("fsdp", None),
        P("fsdp", None),
        P("fsdp"),
        P("fsdp", "tp"),
        P("fsdp", None),
        P("fsdp"),
        P("fsdp", "tp"),
        P("tp", "fsdp"),
        P("fsdp"),
        P("fsdp", "tp"),
        P("fsdp", "tp"),
        P("tp", "fsdp"),
        P("fsdp", "tp", None),
        P("fsdp", "tp", None),
        P("fsdp", "tp", None),
    )
    return jax.shard_map(
        per_device,
        mesh=mesh,
        in_specs=placed,
        out_specs=(
            P(("fsdp", "tp"), None),
            P(("fsdp", "tp"), None),
            P(("fsdp", "tp")),
            P("fsdp", "tp"),
            P(("fsdp", "tp"), None),
            P(("fsdp", "tp")),
            P("fsdp", "tp"),
            P("tp", "fsdp"),
            P(("fsdp", "tp")),
            P("fsdp", "tp"),
            P("fsdp", "tp"),
            P("tp", "fsdp"),
            P("fsdp", "tp", None),
            P("fsdp", "tp", None),
            P("fsdp", "tp", None),
        ),
        check_vma=False,
    )
```

```python
import functools

import jax
import jax.numpy as jnp
from jax import lax
from jax.experimental import pallas as pl
from jax.experimental.pallas import tpu as pltpu
from jax.sharding import PartitionSpec as P

H = 16
NOPE = 128
ROPE = 64
DV = 128
LAT = 512
TOPK = 6
SEQ = 512
HALF = 256
QUARTET = 4


EPSILON = 1e-06
THETA_BASE = 10000.0
MASK_FILL = -1e30
NO_SLOT = -1e6

BF = jnp.bfloat16
F32 = jnp.float32


def rope_tables(positions, width_rope):
    middle = width_rope // 2
    frequency = THETA_BASE ** (-(jnp.arange(middle) * 2).astype(jnp.float32) / width_rope)
    angles = positions.astype(jnp.float32)[:, None] * frequency[None, :]
    return (jnp.cos(angles), jnp.sin(angles))


def rotate(values, cosine, sine_part):
    middle = values.shape[-1] // 2
    first_half = values[..., :middle]
    second_half = values[..., middle:]
    return jnp.concatenate(
        [
            first_half * cosine - second_half * sine_part,
            second_half * cosine + first_half * sine_part,
        ],
        axis=-1,
    )


def unrotate(values, cosine, sine_part):
    middle = values.shape[-1] // 2
    first_half = values[..., :middle]
    second_half = values[..., middle:]
    return jnp.concatenate(
        [
            first_half * cosine + second_half * sine_part,
            second_half * cosine - first_half * sine_part,
        ],
        axis=-1,
    )


def norm_parts(values):
    inverse = lax.rsqrt(jnp.mean(values * values, axis=-1, keepdims=True) + EPSILON)
    return (values * inverse, inverse)


def norm_back(upstream, unit_rows, inverse, scaling):
    scaled = upstream * scaling
    gain_grad = jnp.sum(upstream * unit_rows, axis=0)
    input_grad = inverse * (
        scaled - unit_rows * jnp.mean(scaled * unit_rows, axis=-1, keepdims=True)
    )
    return (gain_grad, input_grad)


def silu_back(grad_hidden, gate_pre, up_pre):
    sigmoid = jax.nn.sigmoid(gate_pre)
    gate_grad = grad_hidden * up_pre * (sigmoid * (1.0 + gate_pre * (1.0 - sigmoid)))
    up_grad = grad_hidden * (gate_pre * sigmoid)
    return (gate_grad.astype(jnp.bfloat16), up_grad.astype(jnp.bfloat16))


def is_power(count):
    return count & (count - 1) == 0


def swap(values, axis_name, bit):
    count = lax.axis_size(axis_name)
    return lax.ppermute(values, axis_name, [(i, i ^ bit) for i in range(count)])


def after(values, *earlier):
    return lax.optimization_barrier((values,) + earlier)[0]


def column_gather(rows):
    count = lax.axis_size("tp")
    pieces = [rows]
    for s in range(1, count):
        pieces.append(lax.ppermute(rows, "tp", [((i + s) % count, i) for i in range(count)]))
    return jnp.concatenate(pieces, axis=0)


def column_scatter(values):
    count = lax.axis_size("tp")
    size = values.shape[0] // count
    total = values[:size].astype(F32)
    for s in range(1, count):
        piece = values[s * size : (s + 1) * size].astype(BF)
        total = total + lax.ppermute(
            piece, "tp", [(i, (i + s) % count) for i in range(count)]
        ).astype(F32)
    return total


def dot_rows(left, right):
    return lax.dot_general(left, right, (((1,), (1,)), ((), ())), preferred_element_type=F32)


def dot_plain(left, right):
    return lax.dot_general(left, right, (((1,), (0,)), ((), ())), preferred_element_type=F32)


def dot_first(left, right):
    return lax.dot_general(left, right, (((0,), (0,)), ((), ())), preferred_element_type=F32)


def select_rows(slot_rows, experts, cap):
    row = lax.broadcasted_iota(jnp.int32, (experts * cap, HALF), 0).astype(F32)
    hit = row == slot_rows[0:1, :]
    for e in range(1, experts):
        hit = hit | (row == slot_rows[e : e + 1, :] + float(e * cap))
    return hit


def select_cols(slot_cols, experts, cap):
    lane = lax.broadcasted_iota(jnp.int32, (HALF, experts * cap), 1).astype(F32)
    hit = lane == slot_cols[:, 0:1]
    for e in range(1, experts):
        hit = hit | (lane == slot_cols[:, e : e + 1] + float(e * cap))
    return hit


def slot_weights(hit, weight_rows, experts, cap):
    pieces = []
    for e in range(experts):
        part = hit[e * cap : (e + 1) * cap, :]
        pieces.append(
            jnp.sum(jnp.where(part, weight_rows[e : e + 1, :], 0.0), axis=1, keepdims=True)
        )
    return jnp.concatenate(pieces, axis=0)


def expert_front_kernel(step, experts, cap, aliased, *refs):
    count = QUARTET
    x_in, dy_in = refs[:count], refs[count : 2 * count]
    gate_up_in, down_in, slot_row_ref, weight_row_ref, slot_col_ref = refs[
        2 * count : 2 * count + 5
    ]
    base = 2 * count + 5 + aliased
    dx_out = refs[base : base + 2]
    x_all, d_all, hid_all, dgu_all = refs[base + 2 : base + 6]
    (xb, db, gate_up, down, xs, ds, dxs, dxo, hid, dgu, sem_in, sem_w, sem_out, sem_dx) = refs[
        base + 6 :
    ]
    width = xb.shape[2]
    pad = down.shape[1]
    tile = min(1024, width)
    x_copies = [pltpu.make_async_copy(x_in[q], xb.at[q], sem_in.at[q]) for q in range(count)]
    d_copies = [
        pltpu.make_async_copy(dy_in[q], db.at[q], sem_in.at[count + q]) for q in range(count)
    ]
    w_copies = [
        pltpu.make_async_copy(gate_up_in, gate_up, sem_w.at[0]),
        pltpu.make_async_copy(down_in, down, sem_w.at[1]),
    ]
    for q in range(count):
        x_copies[q].start()
        d_copies[q].start()
    for copy in w_copies:
        copy.start()
    for q in range(count):
        x_copies[q].wait()
        d_copies[q].wait()

        hit = select_rows(slot_row_ref[q], experts, cap)
        weights = slot_weights(hit, weight_row_ref[q], experts, cap)
        choose = jnp.where(hit, 1.0, 0.0).astype(BF)

        def spread(n, carry, q=q, choose=choose, weights=weights):
            cols = pl.ds(pl.multiple_of(n * tile, tile), tile)
            rows = dot_plain(choose, xb[q, :, cols])
            grads = dot_plain(choose, db[q, :, cols]) * weights
            for e in range(experts):
                xs[e, q * cap : (q + 1) * cap, cols] = rows[e * cap : (e + 1) * cap].astype(BF)
                ds[e, q * cap : (q + 1) * cap, cols] = grads[e * cap : (e + 1) * cap].astype(BF)
            return carry

        lax.fori_loop(0, width // tile, spread, 0)
    out_copies = [
        pltpu.make_async_copy(xs, x_all.at[step], sem_out.at[0]),
        pltpu.make_async_copy(ds, d_all.at[step], sem_out.at[1]),
        pltpu.make_async_copy(hid, hid_all.at[step], sem_out.at[2]),
        pltpu.make_async_copy(dgu, dgu_all.at[step], sem_out.at[3]),
    ]
    out_copies[0].start()
    out_copies[1].start()
    for copy in w_copies:
        copy.wait()

    def one_expert(e, carry):
        both = dot_rows(xs[e], gate_up[e])
        gate_pre, up_pre = both[:, :pad], both[:, pad:]
        d_hidden = dot_rows(ds[e], down[e])
        sigmoid = jax.nn.sigmoid(gate_pre)
        silu = gate_pre * sigmoid
        hid[e] = (silu * up_pre).astype(BF)
        gate_grad = d_hidden * up_pre * (sigmoid * (1.0 + gate_pre * (1.0 - sigmoid)))
        grads = jnp.concatenate([gate_grad, d_hidden * silu], axis=1).astype(BF)
        dgu[e] = grads

        def back(n, inner):
            cols = pl.ds(pl.multiple_of(n * tile, tile), tile)
            part = dot_plain(dgu[e], gate_up[e, :, cols]).astype(BF)
            for q in range(count):
                dxs[q, pl.ds(pl.multiple_of(e * cap, cap), cap), cols] = part[
                    q * cap : (q + 1) * cap
                ]
            return inner

        lax.fori_loop(0, width // tile, back, 0)
        return carry

    lax.fori_loop(0, experts, one_expert, 0)
    out_copies[2].start()
    out_copies[3].start()
    dx_copies = [
        pltpu.make_async_copy(dxo.at[q], dx_out[q // 2].at[q % 2], sem_dx.at[q])
        for q in range(count)
    ]
    for q in range(count):
        choose = jnp.where(select_cols(slot_col_ref[q], experts, cap), 1.0, 0.0).astype(BF)

        def gather(n, carry, q=q, choose=choose):
            cols = pl.ds(pl.multiple_of(n * tile, tile), tile)
            dxo[q, :, cols] = dot_plain(choose, dxs[q, :, cols]).astype(BF)
            return carry

        lax.fori_loop(0, width // tile, gather, 0)
        dx_copies[q].start()
    for copy in out_copies:
        copy.wait()
    for copy in dx_copies:
        copy.wait()


def expert_front(step, steps, x_parts, dy_parts, gate_up, down, tables, kept, cap):
    experts, wide, width = gate_up.shape
    pad = wide // 2
    slots = QUARTET * cap
    slot_row, weight_row, slot_col = (t[step] for t in tables)
    any_spec = pl.BlockSpec(memory_space=pl.ANY)
    vmem_spec = pl.BlockSpec(memory_space=pltpu.VMEM)
    pair_shape = jax.ShapeDtypeStruct((2, HALF, width), BF)
    kept_shapes = [
        jax.ShapeDtypeStruct((steps, experts, slots, columns), BF)
        for columns in (width, width, pad, wide)
    ]
    results = pl.pallas_call(
        functools.partial(expert_front_kernel, step, experts, cap, len(kept)),
        out_shape=[pair_shape] * 2 + kept_shapes,
        in_specs=[any_spec] * (2 * QUARTET + 2) + [vmem_spec] * 3 + [any_spec] * len(kept),
        out_specs=[any_spec] * 6,
        input_output_aliases={2 * QUARTET + 5 + i: 2 + i for i in range(len(kept))},
        scratch_shapes=[
            pltpu.VMEM((QUARTET, HALF, width), BF),
            pltpu.VMEM((QUARTET, HALF, width), BF),
            pltpu.VMEM((experts, wide, width), BF),
            pltpu.VMEM((experts, pad, width), BF),
            pltpu.VMEM((experts, slots, width), BF),
            pltpu.VMEM((experts, slots, width), BF),
            pltpu.VMEM((QUARTET, experts * cap, width), BF),
            pltpu.VMEM((QUARTET, HALF, width), BF),
            pltpu.VMEM((experts, slots, pad), BF),
            pltpu.VMEM((experts, slots, wide), BF),
            pltpu.SemaphoreType.DMA((2 * QUARTET,)),
            pltpu.SemaphoreType.DMA((2,)),
            pltpu.SemaphoreType.DMA((4,)),
            pltpu.SemaphoreType.DMA((QUARTET,)),
        ],
        compiler_params=pltpu.CompilerParams(vmem_limit_bytes=62 * 1024 * 1024),
        cost_estimate=pl.CostEstimate(
            flops=2 * slots * experts * width * pad * 5
            + 6 * QUARTET * HALF * experts * cap * width,
            bytes_accessed=2 * width * (3 * QUARTET * HALF + experts * 3 * pad + 2 * experts * slots),
            transcendentals=slots * experts * pad,
        ),
        name="expert_front",
    )(*x_parts, *dy_parts, gate_up, down, slot_row, weight_row, slot_col, *kept)
    return list(results[:2]), list(results[2:])


def expert_out_kernel(experts, cap, hid, down, slot_row, weight_row, slot_col, near, far, parts):
    width = down.shape[2]
    tile = min(1024, width)
    weights = [
        slot_weights(
            select_rows(slot_row[0, q], experts, cap), weight_row[0, q], experts, cap
        )
        for q in range(QUARTET)
    ]
    for e in range(experts):

        def front(n, carry, e=e):
            cols = pl.ds(pl.multiple_of(n * tile, tile), tile)
            rows = dot_plain(hid[0, e], down[e, :, cols])
            for q in range(QUARTET):
                parts[q, e * cap : (e + 1) * cap, cols] = (
                    rows[q * cap : (q + 1) * cap] * weights[q][e * cap : (e + 1) * cap]
                ).astype(BF)
            return carry

        lax.fori_loop(0, width // tile, front, 0)
    for q in range(QUARTET):
        choose = jnp.where(select_cols(slot_col[0, q], experts, cap), 1.0, 0.0).astype(BF)
        out = (near, far)[q // 2]

        def gather(n, carry, q=q, choose=choose, out=out):
            cols = pl.ds(pl.multiple_of(n * tile, tile), tile)
            out[0, q % 2, :, cols] = dot_plain(choose, parts[q, :, cols]).astype(BF)
            return carry

        lax.fori_loop(0, width // tile, gather, 0)


def expert_out(hid_all, down, tables, cap):
    steps, experts, slots, pad = hid_all.shape
    width = down.shape[2]
    slot_row, weight_row, slot_col = tables
    return pl.pallas_call(
        functools.partial(expert_out_kernel, experts, cap),
        grid=(steps,),
        out_shape=[jax.ShapeDtypeStruct((steps, 2, HALF, width), BF)] * 2,
        in_specs=[
            pl.BlockSpec((1, experts, slots, pad), lambda i: (i, 0, 0, 0)),
            pl.BlockSpec((experts, pad, width), lambda i: (0, 0, 0)),
            pl.BlockSpec((1,) + slot_row.shape[1:], lambda i: (i, 0, 0, 0)),
            pl.BlockSpec((1,) + weight_row.shape[1:], lambda i: (i, 0, 0, 0)),
            pl.BlockSpec((1,) + slot_col.shape[1:], lambda i: (i, 0, 0, 0)),
        ],
        out_specs=[pl.BlockSpec((1, 2, HALF, width), lambda i: (i, 0, 0, 0))] * 2,
        scratch_shapes=[pltpu.VMEM((QUARTET, experts * cap, width), BF)],
        compiler_params=pltpu.CompilerParams(vmem_limit_bytes=48 * 1024 * 1024),
        cost_estimate=pl.CostEstimate(
            flops=steps * (2 * slots * experts * width * pad + 2 * QUARTET * HALF * experts * cap * width),
            bytes_accessed=2 * steps * QUARTET * HALF * width + 2 * hid_all.size + 2 * down.size,
            transcendentals=0,
        ),
        name="expert_out",
    )(hid_all, down, slot_row, weight_row, slot_col)


def expert_grads_kernel(dgu, x, hid, d, gate_grad, up_grad, down_grad):
    local = gate_grad.shape[1]
    pad = hid.shape[3]
    width = x.shape[3]
    tile = min(1024, width)

    @pl.when(pl.program_id(1) == 0)
    def _():
        gate_grad[...] = jnp.zeros_like(gate_grad)
        up_grad[...] = jnp.zeros_like(up_grad)
        down_grad[...] = jnp.zeros_like(down_grad)

    def part(n, carry):
        cols = pl.ds(pl.multiple_of(n * tile, tile), tile)
        gate_grad[0, :, cols] += dot_first(dgu[0, 0, :, :pad], x[0, 0, :, cols])[:local]
        up_grad[0, :, cols] += dot_first(dgu[0, 0, :, pad:], x[0, 0, :, cols])[:local]
        down_grad[0, :, cols] += dot_first(hid[0, 0], d[0, 0, :, cols])[:local]
        return carry

    lax.fori_loop(0, width // tile, part, 0)


def expert_grads(kept, local):
    x_all, d_all, hid_all, dgu_all = kept
    steps, experts, slots, width = x_all.shape
    pad = hid_all.shape[3]

    def block(array):
        return pl.BlockSpec((1, 1) + array.shape[2:], lambda e, i: (i, e, 0, 0))

    grad = jax.ShapeDtypeStruct((experts, local, width), F32)
    return pl.pallas_call(
        expert_grads_kernel,
        grid=(experts, steps),
        out_shape=[grad] * 3,
        in_specs=[block(dgu_all), block(x_all), block(hid_all), block(d_all)],
        out_specs=[pl.BlockSpec((1, local, width), lambda e, i: (e, 0, 0))] * 3,
        compiler_params=pltpu.CompilerParams(vmem_limit_bytes=48 * 1024 * 1024),
        cost_estimate=pl.CostEstimate(
            flops=2 * 3 * steps * experts * slots * width * pad,
            bytes_accessed=2 * (x_all.size + d_all.size + hid_all.size + dgu_all.size)
            + 12 * experts * local * width,
            transcendentals=0,
        ),
        name="expert_grads",
    )(dgu_all, x_all, hid_all, d_all)


def plane_units(count):
    if count == 8:
        return [
            [(0, 0), (0, 1), (1, 0), (1, 1)],
            [(2, 0), (4, 1), (3, 0), (5, 1)],
            [(2, 1), (4, 0), (3, 1), (5, 0)],
            [(6, 0), (6, 1), (7, 0), (7, 1)],
        ]
    return [[(2 * i + j // 2, j % 2) for j in range(4)] for i in range(count // 2)]


def partner(block):
    return swap(block, "fsdp", 1)


def plane_gather(rows, count):
    blocks = {}
    if count == 8:
        other = partner(rows)
        for h in (0, 1):
            blocks[0, h] = rows[h * HALF : (h + 1) * HALF]
            blocks[1, h] = other[h * HALF : (h + 1) * HALF]
        blocks[2, 0] = swap(blocks[0, 0], "fsdp", 2)
        blocks[4, 1] = swap(blocks[0, 1], "fsdp", 4)
        blocks[2, 1] = swap(blocks[0, 1], "fsdp", 2)
        blocks[4, 0] = swap(blocks[0, 0], "fsdp", 4)
        blocks[6, 0] = swap(blocks[2, 0], "fsdp", 4)
        blocks[6, 1] = swap(blocks[4, 1], "fsdp", 2)
        for r in (2, 4, 6):
            for h in (0, 1):
                blocks[r + 1, h] = partner(blocks[r, h])
        return blocks
    gathered = lax.all_gather(rows, "fsdp", axis=0)
    for r in range(count):
        blocks[r, 0] = gathered[r, :HALF]
        blocks[r, 1] = gathered[r, HALF:]
    return blocks


def whole_gather_first(rows, count):
    if count == 8:
        return [rows, partner(rows), swap(rows, "fsdp", 2), swap(rows, "fsdp", 4)]
    gathered = lax.all_gather(rows, "fsdp", axis=0)
    return [gathered[r] for r in range(count)]


def whole_gather_rest(first, count):
    blocks = {}
    if count == 8:
        whole = {0: first[0], 1: first[1], 2: first[2], 4: first[3]}
        blocks[6, 0] = swap(whole[2][:HALF], "fsdp", 4)
        blocks[6, 1] = swap(whole[4][HALF:], "fsdp", 2)
        whole[3] = partner(whole[2])
        whole[5] = partner(whole[4])
        for h in (0, 1):
            blocks[7, h] = partner(blocks[6, h])
    else:
        whole = dict(enumerate(first))
    for r, rows in whole.items():
        for h in (0, 1):
            blocks[r, h] = rows[h * HALF : (h + 1) * HALF]
    return blocks


def add_pairs(left, right):
    return left.astype(F32) + right.astype(F32)


def chip_sums(unit, pair):
    theirs = partner(pair[1])
    return {unit[h]: add_pairs(pair[0][h], theirs[h]) for h in (0, 1)}


def plane_scatter(chip):
    top = add_pairs(chip[0, 0], swap(chip[2, 0].astype(BF), "fsdp", 2))
    bottom = add_pairs(chip[0, 1], swap(chip[4, 1].astype(BF), "fsdp", 4))
    over_top = add_pairs(chip[4, 0], swap(chip[6, 0].astype(BF), "fsdp", 2)).astype(BF)
    over_bottom = add_pairs(chip[2, 1], swap(chip[6, 1].astype(BF), "fsdp", 4)).astype(BF)
    top = add_pairs(top, swap(over_top, "fsdp", 4))
    bottom = add_pairs(bottom, swap(over_bottom, "fsdp", 2))
    return jnp.concatenate([top, bottom], axis=0)


def plane_scatter_whole(pairs, units, count):
    parts = {}
    for unit, pair in zip(units, pairs):
        for q, key in enumerate(unit):
            parts[key] = pair[q // 2][q % 2]
    stacked = jnp.concatenate([parts[r, h] for r in range(count) for h in (0, 1)], axis=0)
    return lax.psum_scatter(stacked, "fsdp", scatter_dimension=0, tiled=True).astype(F32)


def sum_everywhere(values):
    for axis_name in ("fsdp", "tp"):
        count = lax.axis_size(axis_name)
        if is_power(count):
            bit = 1
            while bit < count:
                values = values + swap(values, axis_name, bit)
                bit *= 2
        else:
            values = lax.psum(values, axis_name)
    return values


def expert_tables(expert_ids, expert_wts, local_experts, units, cap):
    fsdp_count = lax.axis_size("fsdp")
    fsdp_rank = lax.axis_index("fsdp")
    tp_count = lax.axis_size("tp")
    expert_count = local_experts * fsdp_count
    places = (lax.axis_index("tp") + jnp.arange(tp_count, dtype=jnp.int32)) % tp_count

    def reorder(rows):
        return jnp.take(rows.reshape(tp_count, -1, TOPK), places, axis=0).reshape(SEQ, TOPK)

    expert_ids, expert_wts = reorder(expert_ids), reorder(expert_wts)
    names = jnp.arange(expert_count, dtype=jnp.int32)[:, None]
    member = jnp.zeros((expert_count, SEQ), jnp.bool_)
    weight = jnp.zeros((expert_count, SEQ), F32)
    ids_rows, wts_rows = expert_ids.T, expert_wts.T
    for pick in range(TOPK):
        same = ids_rows[pick : pick + 1] == names
        member = member | same
        weight = weight + jnp.where(same, wts_rows[pick : pick + 1], 0.0)
    position = jnp.arange(HALF)
    before = (position[:, None] < position[None, :]).astype(BF)
    rank = jnp.dot(
        member.astype(BF).reshape(expert_count * 2, HALF), before, preferred_element_type=F32
    ).reshape(expert_count, SEQ)
    slot = jnp.where(member, rank, NO_SLOT)
    table = jnp.concatenate([slot, weight], axis=0)
    if fsdp_count == 8:
        for bit in (1, 2, 4):
            table = jnp.concatenate([table, swap(table, "fsdp", bit)], axis=0)
    else:
        table = lax.all_gather(table, "fsdp", axis=0, tiled=True)
    table = table.reshape(fsdp_count, 2, fsdp_count, local_experts, 2, HALF)
    table = lax.dynamic_index_in_dim(table, fsdp_rank, axis=2, keepdims=False)
    slot_steps, weight_steps = [], []
    for unit in units:
        slot_steps.append(jnp.stack([table[r, 0, :, h] for r, h in unit]))
        weight_steps.append(jnp.stack([table[r, 1, :, h] for r, h in unit]))
    slot_row, weight_row = jnp.stack(slot_steps), jnp.stack(weight_steps)
    return (slot_row, weight_row, jnp.swapaxes(slot_row, 2, 3))


def per_device(
    block_in,
    out_cotan,
    segment_ids,
    expert_ids,
    expert_wts,
    attn_gain,
    query_proj,
    latent_proj,
    latent_gain,
    latent_up,
    out_proj,
    ffn_gain,
    shared_gate,
    shared_up,
    shared_down,
    routed_gate,
    routed_up,
    routed_down,
):
    tp_count = lax.axis_size("tp")
    fsdp_count = lax.axis_size("fsdp")
    tp_rank = lax.axis_index("tp")
    fsdp_rank = lax.axis_index("fsdp")
    tok_rows, model_width = block_in.shape
    local_experts, local_hidden = routed_gate.shape[:2]
    expert_count = local_experts * fsdp_count
    cap_rows = tok_rows * TOPK * 4 // (3 * expert_count)
    cap = cap_rows * (HALF // tok_rows)
    heads_local = H // tp_count
    head_width = NOPE + ROPE
    score_scale = head_width ** (-0.5)
    shard_rows, query_cols = query_proj.shape
    latent_cols = latent_proj.shape[1]
    up_cols = latent_up.shape[1]
    out_rows = out_proj.shape[0]
    units = plane_units(fsdp_count)

    joint = query_cols + latent_cols
    spare = (-joint) % 128
    spare = spare + 128 if spare < 3 else spare
    gains = jnp.concatenate(
        [
            attn_gain[:, None],
            ffn_gain[:, None],
            jnp.pad(latent_gain, (0, shard_rows - latent_gain.shape[0]))[:, None],
            jnp.zeros((shard_rows, spare - 3), BF),
        ],
        axis=1,
    )
    packed = jnp.concatenate(
        [query_proj, latent_proj, gains, latent_up.reshape(shard_rows, -1)], axis=1
    )
    lift_cols = packed.shape[1] - joint - spare
    packed_all = lax.all_gather(packed, "fsdp", axis=0, tiled=True)
    joint_weight = packed_all[:, :joint]
    gain_attn = packed_all[:, joint].astype(F32)
    gain_ffn = packed_all[:, joint + 1].astype(F32)
    gain_latent = (
        packed_all[:, joint + 2]
        .reshape(fsdp_count, shard_rows)[:, : latent_gain.shape[0]]
        .reshape(LAT)
        .astype(F32)
    )
    latent_up_weight = packed_all[:, joint + spare :].reshape(LAT, up_cols)
    tokens_all = column_gather(block_in)
    out_weight = lax.all_gather(after(out_proj, packed_all), "fsdp", axis=1, tiled=True)
    cotan_all = column_gather(after(out_cotan, tokens_all))
    shared_weight = lax.all_gather(
        after(jnp.concatenate([shared_gate, shared_up], axis=1), out_weight),
        "fsdp",
        axis=0,
        tiled=True,
    )
    shared_down_weight = lax.all_gather(
        after(shared_down, shared_weight), "fsdp", axis=1, tiled=True
    )
    shared_cols = shared_gate.shape[1]
    tables = expert_tables(expert_ids, expert_wts, local_experts, units, cap)
    hidden_pad = -(-local_hidden // 128) * 128
    lift = ((0, 0), (0, hidden_pad - local_hidden), (0, 0))
    routed_gate_up = jnp.concatenate([jnp.pad(routed_gate, lift), jnp.pad(routed_up, lift)], axis=1)
    routed_down_pad = jnp.pad(routed_down, lift)

    unit_all, inverse_all = norm_parts(tokens_all.astype(F32))
    normed_all = (unit_all * gain_attn).astype(BF)
    joint_rows = jnp.dot(normed_all, joint_weight, preferred_element_type=F32)
    queries = joint_rows[:, :query_cols].reshape(SEQ, heads_local, head_width)
    latent = joint_rows[:, query_cols:]
    unit_lat, inverse_lat = norm_parts(latent[:, :LAT])
    places = (tp_rank + jnp.arange(tp_count, dtype=jnp.int32)) % tp_count
    positions = (
        places[:, None] * tok_rows + jnp.arange(tok_rows, dtype=jnp.int32)[None, :]
    ).reshape(SEQ)
    segments = jnp.take(segment_ids.reshape(tp_count, tok_rows), places, axis=0).reshape(SEQ)
    cosine, sine_part = rope_tables(positions, ROPE)
    compressed_all = (unit_lat * gain_latent).astype(BF)
    key_rope_all = rotate(latent[:, LAT:], cosine, sine_part).astype(BF)
    query_cat = jnp.concatenate(
        [
            queries[:, :, :NOPE],
            rotate(queries[:, :, NOPE:], cosine[:, None, :], sine_part[:, None, :]),
        ],
        axis=2,
    ).astype(BF)
    key_value = (
        jnp.dot(compressed_all, latent_up_weight, preferred_element_type=F32)
        .reshape(SEQ, heads_local, NOPE + DV)
        .astype(BF)
    )
    key_cat = jnp.concatenate(
        [
            key_value[:, :, :NOPE],
            jnp.broadcast_to(key_rope_all[:, None, :], (SEQ, heads_local, ROPE)),
        ],
        axis=2,
    )
    values = key_value[:, :, NOPE:]
    allowed = (positions[None, :] <= positions[:, None]) & (
        segments[None, :] == segments[:, None]
    )
    raw_scores = (
        jnp.einsum("qhd,khd->hqk", query_cat, key_cat, preferred_element_type=F32) * score_scale
    )
    masked = jnp.where(allowed[None], raw_scores, MASK_FILL)
    top_score = jnp.max(masked, axis=2, keepdims=True)
    exponent = jnp.exp(masked - top_score)
    row_total = jnp.sum(exponent, axis=2, keepdims=True)
    probabilities = exponent / row_total
    probs_low = probabilities.astype(BF)
    attended = (
        jnp.einsum("hqk,khd->qhd", probs_low, values, preferred_element_type=F32)
        .reshape(SEQ, heads_local * DV)
        .astype(BF)
    )
    attended = after(attended, cotan_all)
    dy_first = whole_gather_first(cotan_all, fsdp_count)
    attn_rows = column_scatter(jnp.dot(attended, out_weight, preferred_element_type=F32))
    mixed_rows = block_in.astype(F32) + attn_rows
    unit_two, inverse_two = norm_parts(mixed_rows)
    normed_ffn, dy_first, shared_weight = after(
        ((unit_two * gain_ffn).astype(BF), dy_first, shared_weight)
    )
    normed_ffn_all = column_gather(normed_ffn)

    dy_blocks = whole_gather_rest(dy_first, fsdp_count)
    normed_ffn_all, dy_blocks = after((normed_ffn_all, dy_blocks))
    x_blocks = plane_gather(normed_ffn_all, fsdp_count)
    paired = fsdp_count == 8
    kept = []
    dx_pairs = []
    dx_chip = {}
    for step, unit in enumerate(units):
        x_list = [x_blocks[key] for key in unit]
        if paired and step == 2:
            x_list = after(x_list, dx_pairs[0])
        if paired and step == 3:
            x_list, dx_chip = after((x_list, dx_chip))
        pair, kept = expert_front(
            step,
            len(units),
            x_list,
            [dy_blocks[key] for key in unit],
            routed_gate_up,
            routed_down_pad,
            tables,
            kept,
            cap,
        )
        dx_pairs.append(pair)
        if paired:
            dx_chip.update(chip_sums(unit, pair))
    near, far = expert_out(kept[2], routed_down_pad, tables, cap)
    if paired:
        d_routed_in = plane_scatter(dx_chip)
    else:
        d_routed_in = plane_scatter_whole(dx_pairs, units, fsdp_count)
    routed_gate_grad, routed_up_grad, routed_down_grad = expert_grads(kept, local_hidden)

    shared_pre = jnp.dot(normed_ffn_all, shared_weight, preferred_element_type=F32)
    shared_gate_pre, shared_up_pre = shared_pre[:, :shared_cols], shared_pre[:, shared_cols:]
    shared_hidden = (jax.nn.silu(shared_gate_pre) * shared_up_pre).astype(BF)
    shared_rows = jnp.dot(shared_hidden, shared_down_weight, preferred_element_type=F32)
    shared_down_part = jnp.dot(shared_hidden.T, cotan_all, preferred_element_type=F32)
    d_shared_hidden = jnp.dot(cotan_all, shared_down_weight.T, preferred_element_type=F32)
    d_shared = jnp.concatenate(silu_back(d_shared_hidden, shared_gate_pre, shared_up_pre), axis=1)
    shared_part = jnp.dot(normed_ffn_all.T, d_shared, preferred_element_type=F32)
    d_shared_in = jnp.dot(d_shared, shared_weight.T, preferred_element_type=F32)

    d_ffn_rows, shared_part, shared_down_part, near, far = after(
        (
            d_shared_in + d_routed_in,
            shared_part.astype(BF),
            shared_down_part.astype(BF),
            near,
            far,
        )
    )
    d_normed_ffn = column_scatter(d_ffn_rows)
    out_pairs = [(near[step], far[step]) for step in range(len(units))]
    if paired:
        out_chip = {}
        for unit, pair in zip(units, out_pairs):
            out_chip.update(chip_sums(unit, pair))
        routed_rows = plane_scatter(out_chip)
    else:
        routed_rows = plane_scatter_whole(out_pairs, units, fsdp_count)
    ffn_rows = column_scatter(shared_rows + routed_rows)
    block_out = (mixed_rows + ffn_rows).astype(BF)
    ffn_gain_part, d_mixed_norm = norm_back(d_normed_ffn, unit_two, inverse_two, gain_ffn)
    d_mixed = out_cotan.astype(F32) + d_mixed_norm
    d_proj_all = after(column_gather(d_mixed.astype(BF)), routed_rows)

    out_part = jnp.dot(attended.T, d_proj_all, preferred_element_type=F32)
    d_attended = (
        jnp.dot(d_proj_all, out_weight.T, preferred_element_type=F32)
        .astype(BF)
        .reshape(SEQ, heads_local, DV)
    )
    prob_grad = jnp.einsum("qhd,khd->hqk", d_attended, values, preferred_element_type=F32)
    score_grad = (
        probabilities
        * (prob_grad - jnp.sum(probabilities * prob_grad, axis=2, keepdims=True))
    ).astype(BF)
    query_grad = (
        jnp.einsum("hqk,khd->qhd", score_grad, key_cat, preferred_element_type=F32) * score_scale
    )
    key_grad = (
        jnp.einsum("hqk,qhd->khd", score_grad, query_cat, preferred_element_type=F32) * score_scale
    )
    value_grad = jnp.einsum("hqk,qhd->khd", probs_low, d_attended, preferred_element_type=F32)
    d_queries = (
        jnp.concatenate(
            [
                query_grad[:, :, :NOPE],
                unrotate(query_grad[:, :, NOPE:], cosine[:, None, :], sine_part[:, None, :]),
            ],
            axis=2,
        )
        .reshape(SEQ, heads_local * head_width)
        .astype(BF)
    )
    d_key_value = (
        jnp.concatenate([key_grad[:, :, :NOPE], value_grad], axis=2)
        .reshape(SEQ, heads_local * (NOPE + DV))
        .astype(BF)
    )
    latent_up_part = jnp.dot(compressed_all.T, d_key_value, preferred_element_type=F32)
    d_compressed = jnp.dot(d_key_value, latent_up_weight.T, preferred_element_type=F32)
    d_key_rope = jnp.sum(key_grad[:, :, NOPE:], axis=1)
    latent_gain_part, d_latent_main = norm_back(d_compressed, unit_lat, inverse_lat, gain_latent)
    d_latent = jnp.concatenate(
        [d_latent_main, unrotate(d_key_rope, cosine, sine_part)], axis=1
    ).astype(BF)
    d_joint = jnp.concatenate([d_queries, d_latent], axis=1)
    joint_part = jnp.dot(normed_all.T, d_joint, preferred_element_type=F32)
    d_normed_part = jnp.dot(d_joint, joint_weight.T, preferred_element_type=F32)
    attn_gain_part = jnp.sum(d_normed_part * unit_all, axis=0)
    d_normed = column_scatter(d_normed_part)
    unit_one, inverse_one = norm_parts(block_in.astype(F32))
    _, d_tokens_norm = norm_back(d_normed, unit_one, inverse_one, gain_attn)
    block_in_grad = d_mixed + d_tokens_norm

    def scatter(part, dimension):
        return lax.psum_scatter(
            part.astype(BF), "fsdp", scatter_dimension=dimension, tiled=True
        )

    lift_part = latent_up_part.astype(BF).reshape(model_width, lift_cols)
    joint_grad = scatter(
        jnp.concatenate(
            [
                joint_part.astype(BF),
                jnp.zeros((model_width, (-joint) % 128), BF),
                lift_part,
            ],
            axis=1,
        ),
        0,
    )
    query_proj_grad = joint_grad[:, :query_cols].astype(F32)
    latent_grad = joint_grad[:, query_cols:joint].reshape(tp_count, -1, latent_cols)
    latent_proj_grad = column_scatter(
        jnp.take(latent_grad, places, axis=0).reshape(-1, latent_cols)
    )
    latent_up_grad = (
        joint_grad[:, joint_grad.shape[1] - lift_cols :].reshape(latent_up.shape).astype(F32)
    )
    out_proj_grad = scatter(out_part, 1).astype(F32)
    shared_grad = scatter(shared_part, 0).astype(F32)
    shared_gate_grad, shared_up_grad = shared_grad[:, :shared_cols], shared_grad[:, shared_cols:]
    shared_down_grad = scatter(shared_down_part, 1).astype(F32)
    gain_sums = sum_everywhere(
        jnp.concatenate([attn_gain_part, latent_gain_part, ffn_gain_part]).reshape(-1, 128)
    ).reshape(-1)
    device = fsdp_rank * tp_count + tp_rank
    devices = tp_count * fsdp_count

    def own_gain(start, size):
        return lax.dynamic_slice(gain_sums, (start + device * (size // devices),), (size // devices,))

    attn_gain_grad = own_gain(0, model_width)
    latent_gain_grad = own_gain(model_width, LAT)
    ffn_gain_grad = own_gain(model_width + LAT, model_width)
    return (
        block_out,
        block_in_grad,
        attn_gain_grad,
        query_proj_grad,
        latent_proj_grad,
        latent_gain_grad,
        latent_up_grad,
        out_proj_grad,
        ffn_gain_grad,
        shared_gate_grad,
        shared_up_grad,
        shared_down_grad,
        routed_gate_grad,
        routed_up_grad,
        routed_down_grad,
    )


def solution(mesh):
    placed = (
        P(("fsdp", "tp"), None),
        P(("fsdp", "tp"), None),
        P("fsdp"),
        P("fsdp", None),
        P("fsdp", None),
        P("fsdp"),
        P("fsdp", "tp"),
        P("fsdp", None),
        P("fsdp"),
        P("fsdp", "tp"),
        P("tp", "fsdp"),
        P("fsdp"),
        P("fsdp", "tp"),
        P("fsdp", "tp"),
        P("tp", "fsdp"),
        P("fsdp", "tp", None),
        P("fsdp", "tp", None),
        P("fsdp", "tp", None),
    )
    return jax.shard_map(
        per_device,
        mesh=mesh,
        in_specs=placed,
        out_specs=(
            P(("fsdp", "tp"), None),
            P(("fsdp", "tp"), None),
            P(("fsdp", "tp")),
            P("fsdp", "tp"),
            P(("fsdp", "tp"), None),
            P(("fsdp", "tp")),
            P("fsdp", "tp"),
            P("tp", "fsdp"),
            P(("fsdp", "tp")),
            P("fsdp", "tp"),
            P("fsdp", "tp"),
            P("tp", "fsdp"),
            P("fsdp", "tp", None),
            P("fsdp", "tp", None),
            P("fsdp", "tp", None),
        ),
        check_vma=False,
    )
```

```python
import functools

import jax
import jax.numpy as jnp
from jax import lax
from jax.experimental import pallas as pl
from jax.experimental.pallas import tpu as pltpu
from jax.sharding import PartitionSpec as P

H = 16
NOPE = 128
ROPE = 64
DV = 128
LAT = 512
TOPK = 6
SEQ = 512
HALF = 256
QUARTET = 4
BOX_UNITS = [
    [(0, 0), (0, 1), (1, 0), (1, 1)],
    [(2, 0), (4, 0), (3, 0), (5, 0)],
    [(2, 1), (4, 1), (3, 1), (5, 1)],
    [(6, 0), (6, 1), (7, 0), (7, 1)],
]


EPSILON = 1e-06
THETA_BASE = 10000.0
MASK_FILL = -1e30
NO_SLOT = -1e6

BF = jnp.bfloat16
F32 = jnp.float32


def rope_tables(positions, width_rope):
    middle = width_rope // 2
    frequency = THETA_BASE ** (-(jnp.arange(middle) * 2).astype(jnp.float32) / width_rope)
    angles = positions.astype(jnp.float32)[:, None] * frequency[None, :]
    return (jnp.cos(angles), jnp.sin(angles))


def rotate(values, cosine, sine_part):
    middle = values.shape[-1] // 2
    first_half = values[..., :middle]
    second_half = values[..., middle:]
    return jnp.concatenate(
        [
            first_half * cosine - second_half * sine_part,
            second_half * cosine + first_half * sine_part,
        ],
        axis=-1,
    )


def unrotate(values, cosine, sine_part):
    middle = values.shape[-1] // 2
    first_half = values[..., :middle]
    second_half = values[..., middle:]
    return jnp.concatenate(
        [
            first_half * cosine + second_half * sine_part,
            second_half * cosine - first_half * sine_part,
        ],
        axis=-1,
    )


def norm_parts(values):
    inverse = lax.rsqrt(jnp.mean(values * values, axis=-1, keepdims=True) + EPSILON)
    return (values * inverse, inverse)


def norm_back(upstream, unit_rows, inverse, scaling):
    scaled = upstream * scaling
    gain_grad = jnp.sum(upstream * unit_rows, axis=0)
    input_grad = inverse * (
        scaled - unit_rows * jnp.mean(scaled * unit_rows, axis=-1, keepdims=True)
    )
    return (gain_grad, input_grad)


def silu_back(grad_hidden, gate_pre, up_pre):
    sigmoid = jax.nn.sigmoid(gate_pre)
    gate_grad = grad_hidden * up_pre * (sigmoid * (1.0 + gate_pre * (1.0 - sigmoid)))
    up_grad = grad_hidden * (gate_pre * sigmoid)
    return (gate_grad.astype(jnp.bfloat16), up_grad.astype(jnp.bfloat16))


def is_power(count):
    return count & (count - 1) == 0


def swap(values, axis_name, bit):
    count = lax.axis_size(axis_name)
    return lax.ppermute(values, axis_name, [(i, i ^ bit) for i in range(count)])


def tie(*values):
    return lax.optimization_barrier(values)


def column_gather(rows):
    count = lax.axis_size("tp")
    pieces = [rows]
    for s in range(1, count):
        pieces.append(lax.ppermute(rows, "tp", [((i + s) % count, i) for i in range(count)]))
    return jnp.concatenate(pieces, axis=0)


def column_scatter(values):
    count = lax.axis_size("tp")
    size = values.shape[0] // count
    total = values[:size].astype(F32)
    for s in range(1, count):
        piece = values[s * size : (s + 1) * size].astype(BF)
        total = total + lax.ppermute(
            piece, "tp", [(i, (i + s) % count) for i in range(count)]
        ).astype(F32)
    return total


def dot_rows(left, right):
    return lax.dot_general(left, right, (((1,), (1,)), ((), ())), preferred_element_type=F32)


def dot_plain(left, right):
    return lax.dot_general(left, right, (((1,), (0,)), ((), ())), preferred_element_type=F32)


def dot_first(left, right):
    return lax.dot_general(left, right, (((0,), (0,)), ((), ())), preferred_element_type=F32)


def select_rows(slot_rows, experts, cap):
    row = lax.broadcasted_iota(jnp.int32, (experts * cap, HALF), 0).astype(F32)
    hit = row == slot_rows[0:1, :]
    for e in range(1, experts):
        hit = hit | (row == slot_rows[e : e + 1, :] + float(e * cap))
    return hit


def select_cols(slot_cols, experts, cap):
    lane = lax.broadcasted_iota(jnp.int32, (HALF, experts * cap), 1).astype(F32)
    hit = lane == slot_cols[:, 0:1]
    for e in range(1, experts):
        hit = hit | (lane == slot_cols[:, e : e + 1] + float(e * cap))
    return hit


def slot_weights(hit, weight_rows, experts, cap):
    pieces = []
    for e in range(experts):
        part = hit[e * cap : (e + 1) * cap, :]
        pieces.append(
            jnp.sum(jnp.where(part, weight_rows[e : e + 1, :], 0.0), axis=1, keepdims=True)
        )
    return jnp.concatenate(pieces, axis=0)


def expert_front_kernel(step, experts, cap, aliased, *refs):
    count = QUARTET
    x_in = refs[:count]
    where_ref, dy_in, gate_up_in, down_in, slot_row_ref, weight_row_ref, slot_col_ref = refs[
        count : count + 7
    ]
    base = count + 7 + aliased
    dx_out = refs[base : base + 2]
    x_all, d_all, hid_all, dgu_all = refs[base + 2 : base + 6]
    (xb, db, gate_up, down, xs, ds, dxs, dxo, hid, dgu, sem_in, sem_w, sem_out, sem_dx) = refs[
        base + 6 :
    ]
    width = xb.shape[2]
    pad = down.shape[1]
    tile = min(1024, width)
    x_copies = [pltpu.make_async_copy(x_in[q], xb.at[q], sem_in.at[q]) for q in range(count)]
    d_copies = [
        pltpu.make_async_copy(
            dy_in.at[pl.ds(pl.multiple_of(where_ref[q] * HALF, HALF), HALF)],
            db.at[q],
            sem_in.at[count + q],
        )
        for q in range(count)
    ]
    w_copies = [
        pltpu.make_async_copy(gate_up_in, gate_up, sem_w.at[0]),
        pltpu.make_async_copy(down_in, down, sem_w.at[1]),
    ]
    for q in range(count):
        x_copies[q].start()
        d_copies[q].start()
    for copy in w_copies:
        copy.start()
    for q in range(count):
        x_copies[q].wait()
        d_copies[q].wait()

        hit = select_rows(slot_row_ref[q], experts, cap)
        weights = slot_weights(hit, weight_row_ref[q], experts, cap)
        choose = jnp.where(hit, 1.0, 0.0).astype(BF)

        def spread(n, carry, q=q, choose=choose, weights=weights):
            cols = pl.ds(pl.multiple_of(n * tile, tile), tile)
            rows = dot_plain(choose, xb[q, :, cols])
            grads = dot_plain(choose, db[q, :, cols]) * weights
            for e in range(experts):
                xs[e, q * cap : (q + 1) * cap, cols] = rows[e * cap : (e + 1) * cap].astype(BF)
                ds[e, q * cap : (q + 1) * cap, cols] = grads[e * cap : (e + 1) * cap].astype(BF)
            return carry

        lax.fori_loop(0, width // tile, spread, 0)
    out_copies = [
        pltpu.make_async_copy(xs, x_all.at[step], sem_out.at[0]),
        pltpu.make_async_copy(ds, d_all.at[step], sem_out.at[1]),
        pltpu.make_async_copy(hid, hid_all.at[step], sem_out.at[2]),
        pltpu.make_async_copy(dgu, dgu_all.at[step], sem_out.at[3]),
    ]
    out_copies[0].start()
    out_copies[1].start()
    for copy in w_copies:
        copy.wait()

    def one_expert(e, carry):
        both = dot_rows(xs[e], gate_up[e])
        gate_pre, up_pre = both[:, :pad], both[:, pad:]
        d_hidden = dot_rows(ds[e], down[e])
        sigmoid = jax.nn.sigmoid(gate_pre)
        silu = gate_pre * sigmoid
        hid[e] = (silu * up_pre).astype(BF)
        gate_grad = d_hidden * up_pre * (sigmoid * (1.0 + gate_pre * (1.0 - sigmoid)))
        grads = jnp.concatenate([gate_grad, d_hidden * silu], axis=1).astype(BF)
        dgu[e] = grads

        def back(n, inner):
            cols = pl.ds(pl.multiple_of(n * tile, tile), tile)
            part = dot_plain(dgu[e], gate_up[e, :, cols]).astype(BF)
            for q in range(count):
                dxs[q, pl.ds(pl.multiple_of(e * cap, cap), cap), cols] = part[
                    q * cap : (q + 1) * cap
                ]
            return inner

        lax.fori_loop(0, width // tile, back, 0)
        return carry

    lax.fori_loop(0, experts, one_expert, 0)
    out_copies[2].start()
    out_copies[3].start()
    dx_copies = [
        pltpu.make_async_copy(dxo.at[q], dx_out[q // 2].at[q % 2], sem_dx.at[q])
        for q in range(count)
    ]
    for q in range(count):
        choose = jnp.where(select_cols(slot_col_ref[q], experts, cap), 1.0, 0.0).astype(BF)

        def gather(n, carry, q=q, choose=choose):
            cols = pl.ds(pl.multiple_of(n * tile, tile), tile)
            dxo[q, :, cols] = dot_plain(choose, dxs[q, :, cols]).astype(BF)
            return carry

        lax.fori_loop(0, width // tile, gather, 0)
        dx_copies[q].start()
    for copy in out_copies:
        copy.wait()
    for copy in dx_copies:
        copy.wait()


def expert_front(step, steps, x_parts, where, dy_all, gate_up, down, tables, kept, cap):
    experts, wide, width = gate_up.shape
    pad = wide // 2
    slots = QUARTET * cap
    slot_row, weight_row, slot_col = (t[step] for t in tables)
    any_spec = pl.BlockSpec(memory_space=pl.ANY)
    vmem_spec = pl.BlockSpec(memory_space=pltpu.VMEM)
    pair_shape = jax.ShapeDtypeStruct((2, HALF, width), BF)
    kept_shapes = [
        jax.ShapeDtypeStruct((steps, experts, slots, columns), BF)
        for columns in (width, width, pad, wide)
    ]
    results = pl.pallas_call(
        functools.partial(expert_front_kernel, step, experts, cap, len(kept)),
        out_shape=[pair_shape] * 2 + kept_shapes,
        in_specs=[any_spec] * QUARTET
        + [pl.BlockSpec(memory_space=pltpu.SMEM)]
        + [any_spec] * 3
        + [vmem_spec] * 3
        + [any_spec] * len(kept),
        out_specs=[any_spec] * 6,
        input_output_aliases={QUARTET + 7 + i: 2 + i for i in range(len(kept))},
        scratch_shapes=[
            pltpu.VMEM((QUARTET, HALF, width), BF),
            pltpu.VMEM((QUARTET, HALF, width), BF),
            pltpu.VMEM((experts, wide, width), BF),
            pltpu.VMEM((experts, pad, width), BF),
            pltpu.VMEM((experts, slots, width), BF),
            pltpu.VMEM((experts, slots, width), BF),
            pltpu.VMEM((QUARTET, experts * cap, width), BF),
            pltpu.VMEM((QUARTET, HALF, width), BF),
            pltpu.VMEM((experts, slots, pad), BF),
            pltpu.VMEM((experts, slots, wide), BF),
            pltpu.SemaphoreType.DMA((2 * QUARTET,)),
            pltpu.SemaphoreType.DMA((2,)),
            pltpu.SemaphoreType.DMA((4,)),
            pltpu.SemaphoreType.DMA((QUARTET,)),
        ],
        compiler_params=pltpu.CompilerParams(vmem_limit_bytes=62 * 1024 * 1024),
        cost_estimate=pl.CostEstimate(
            flops=2 * slots * experts * width * pad * 5
            + 6 * QUARTET * HALF * experts * cap * width,
            bytes_accessed=2 * width * (3 * QUARTET * HALF + experts * 3 * pad + 2 * experts * slots),
            transcendentals=slots * experts * pad,
        ),
        name="expert_front",
    )(*x_parts, where, dy_all, gate_up, down, slot_row, weight_row, slot_col, *kept)
    return list(results[:2]), list(results[2:])


def expert_out_kernel(experts, cap, hid, down, slot_row, weight_row, slot_col, near, far, parts):
    width = down.shape[2]
    tile = min(1024, width)
    weights = [
        slot_weights(
            select_rows(slot_row[0, q], experts, cap), weight_row[0, q], experts, cap
        )
        for q in range(QUARTET)
    ]
    for e in range(experts):

        def front(n, carry, e=e):
            cols = pl.ds(pl.multiple_of(n * tile, tile), tile)
            rows = dot_plain(hid[0, e], down[e, :, cols])
            for q in range(QUARTET):
                parts[q, e * cap : (e + 1) * cap, cols] = (
                    rows[q * cap : (q + 1) * cap] * weights[q][e * cap : (e + 1) * cap]
                ).astype(BF)
            return carry

        lax.fori_loop(0, width // tile, front, 0)
    for q in range(QUARTET):
        choose = jnp.where(select_cols(slot_col[0, q], experts, cap), 1.0, 0.0).astype(BF)
        out = (near, far)[q // 2]

        def gather(n, carry, q=q, choose=choose, out=out):
            cols = pl.ds(pl.multiple_of(n * tile, tile), tile)
            out[0, q % 2, :, cols] = dot_plain(choose, parts[q, :, cols]).astype(BF)
            return carry

        lax.fori_loop(0, width // tile, gather, 0)


def expert_out(hid_all, down, tables, cap):
    steps, experts, slots, pad = hid_all.shape
    width = down.shape[2]
    slot_row, weight_row, slot_col = tables
    return pl.pallas_call(
        functools.partial(expert_out_kernel, experts, cap),
        grid=(steps,),
        out_shape=[jax.ShapeDtypeStruct((steps, 2, HALF, width), BF)] * 2,
        in_specs=[
            pl.BlockSpec((1, experts, slots, pad), lambda i: (i, 0, 0, 0)),
            pl.BlockSpec((experts, pad, width), lambda i: (0, 0, 0)),
            pl.BlockSpec((1,) + slot_row.shape[1:], lambda i: (i, 0, 0, 0)),
            pl.BlockSpec((1,) + weight_row.shape[1:], lambda i: (i, 0, 0, 0)),
            pl.BlockSpec((1,) + slot_col.shape[1:], lambda i: (i, 0, 0, 0)),
        ],
        out_specs=[pl.BlockSpec((1, 2, HALF, width), lambda i: (i, 0, 0, 0))] * 2,
        scratch_shapes=[pltpu.VMEM((QUARTET, experts * cap, width), BF)],
        compiler_params=pltpu.CompilerParams(vmem_limit_bytes=48 * 1024 * 1024),
        cost_estimate=pl.CostEstimate(
            flops=steps * (2 * slots * experts * width * pad + 2 * QUARTET * HALF * experts * cap * width),
            bytes_accessed=2 * steps * QUARTET * HALF * width + 2 * hid_all.size + 2 * down.size,
            transcendentals=0,
        ),
        name="expert_out",
    )(hid_all, down, slot_row, weight_row, slot_col)


def expert_grads_kernel(dgu, x, hid, d, gate_grad, up_grad, down_grad):
    local = gate_grad.shape[1]
    pad = hid.shape[3]
    width = x.shape[3]
    tile = min(1024, width)

    @pl.when(pl.program_id(1) == 0)
    def _():
        gate_grad[...] = jnp.zeros_like(gate_grad)
        up_grad[...] = jnp.zeros_like(up_grad)
        down_grad[...] = jnp.zeros_like(down_grad)

    def part(n, carry):
        cols = pl.ds(pl.multiple_of(n * tile, tile), tile)
        gate_grad[0, :, cols] += dot_first(dgu[0, 0, :, :pad], x[0, 0, :, cols])[:local]
        up_grad[0, :, cols] += dot_first(dgu[0, 0, :, pad:], x[0, 0, :, cols])[:local]
        down_grad[0, :, cols] += dot_first(hid[0, 0], d[0, 0, :, cols])[:local]
        return carry

    lax.fori_loop(0, width // tile, part, 0)


def expert_grads(kept, local):
    x_all, d_all, hid_all, dgu_all = kept
    steps, experts, slots, width = x_all.shape
    pad = hid_all.shape[3]

    def block(array):
        return pl.BlockSpec((1, 1) + array.shape[2:], lambda e, i: (i, e, 0, 0))

    grad = jax.ShapeDtypeStruct((experts, local, width), F32)
    return pl.pallas_call(
        expert_grads_kernel,
        grid=(experts, steps),
        out_shape=[grad] * 3,
        in_specs=[block(dgu_all), block(x_all), block(hid_all), block(d_all)],
        out_specs=[pl.BlockSpec((1, local, width), lambda e, i: (e, 0, 0))] * 3,
        compiler_params=pltpu.CompilerParams(vmem_limit_bytes=48 * 1024 * 1024),
        cost_estimate=pl.CostEstimate(
            flops=2 * 3 * steps * experts * slots * width * pad,
            bytes_accessed=2 * (x_all.size + d_all.size + hid_all.size + dgu_all.size)
            + 12 * experts * local * width,
            transcendentals=0,
        ),
        name="expert_grads",
    )(dgu_all, x_all, hid_all, d_all)


def mesh_copy(src, dst, sends, arrivals, number, device):
    return pltpu.make_async_remote_copy(
        src_ref=src,
        dst_ref=dst,
        send_sem=sends.at[number],
        recv_sem=arrivals.at[number],
        device_id=device,
        device_id_type=pl.DeviceIdType.MESH,
    )


def plane_neighbours():
    place, column = lax.axis_index("fsdp"), lax.axis_index("tp")
    core, along, across = place % 2, (place // 2) % 2, place // 4
    return (
        (place + 1 - 2 * core, column),
        (place + 2 - 4 * along, column),
        (place + 4 - 8 * across, column),
    )


def column_neighbours(count):
    place, column = lax.axis_index("fsdp"), lax.axis_index("tp")
    return [(place, (column + s) % count) for s in range(1, count)]


def greet(devices):
    barrier = pltpu.get_barrier_semaphore()
    for device in devices:
        pl.semaphore_signal(
            barrier, inc=1, device_id=device, device_id_type=pl.DeviceIdType.MESH
        )
    pl.semaphore_wait(barrier, len(devices))


class PlaneGather:
    def __init__(self, own, others, size, sends, arrivals, base):
        self.own, self.others, self.size = own, others, size
        self.sends, self.arrivals, self.base = sends, arrivals, base
        self.partner, self.along, self.across = plane_neighbours()

    def copies(self, b):
        half = self.own.shape[1] // 2
        rows = pl.ds(b * self.size, self.size)
        left, right = pl.ds(0, half), pl.ds(half, half)
        other = {r: self.others.at[r - 1] for r in range(1, 8)}
        plan = [
            (self.own.at[rows], other[2].at[rows], self.along),
            (self.own.at[rows], other[4].at[rows], self.across),
            (self.own.at[rows], other[1].at[rows], self.partner),
            (other[2].at[rows, left], other[6].at[rows, left], self.across),
            (other[4].at[rows, right], other[6].at[rows, right], self.along),
            (other[2].at[rows], other[3].at[rows], self.partner),
            (other[4].at[rows], other[5].at[rows], self.partner),
            (other[6].at[rows], other[7].at[rows], self.partner),
        ]
        return [
            mesh_copy(src, dst, self.sends, self.arrivals, self.base + 8 * b + i, device)
            for i, (src, dst, device) in enumerate(plan)
        ]

    def start(self, b):
        for copy in self.copies(b)[:3]:
            copy.start()

    def forward(self, b):
        along, across, _, left, right, third, fifth, _ = self.copies(b)
        along.wait_recv()
        left.start()
        third.start()
        across.wait_recv()
        right.start()
        fifth.start()

    def last(self, b):
        copies = self.copies(b)
        copies[3].wait_recv()
        copies[4].wait_recv()
        copies[7].start()

    def arrived(self, b, numbers):
        copies = self.copies(b)
        for i in numbers:
            copies[i].wait_recv()

    def drain(self, b):
        for copy in self.copies(b):
            copy.wait_send()


def expert_kernel(experts, cap, columns, size, *refs):
    (
        attn_in,
        tokens_in,
        cotan_in,
        gate_up_in,
        down_in,
        gain_ref,
        slot_row_ref,
        weight_row_ref,
        slot_col_ref,
        mixed_out,
        ffn_all,
        dx_out,
        out_all,
        x_all,
        d_all,
        hid_all,
        dgu_all,
        x_others,
        dy_others,
        theirs,
        links,
        attn_v,
        tokens_v,
        arrived_v,
        mixed_v,
        ffn_v,
        xb,
        db,
        gate_up,
        down,
        xs,
        ds,
        dxs,
        others,
        chip,
        hid,
        dgu,
        stage,
        sends,
        arrivals,
        local,
        spill,
    ) = refs
    count = QUARTET
    width = xb.shape[2]
    half_width = width // 2
    pad = down.shape[1]
    tile = min(1024, width)
    blocks = columns
    partner, along, across = plane_neighbours()
    column = column_neighbours(columns)
    number = 0

    def reserve(amount):
        nonlocal number
        number += amount
        return number - amount

    x_gather = PlaneGather(ffn_all, x_others, size, sends, arrivals, reserve(8 * blocks))
    dy_gather = PlaneGather(cotan_in, dy_others, SEQ, sends, arrivals, reserve(8))
    rs_base, ag_base = reserve(columns - 1), reserve(columns - 1)
    pair_base, link_base = reserve(len(BOX_UNITS)), reserve(12)

    greet([partner, along, across] + column)
    sums = [
        mesh_copy(
            attn_in.at[pl.ds(s * size, size)],
            arrived_v.at[s - 1],
            sends,
            arrivals,
            rs_base + s - 1,
            column[s - 1],
        )
        for s in range(1, columns)
    ]
    for copy in sums:
        copy.start()
    first = [
        pltpu.make_async_copy(attn_in.at[pl.ds(0, size)], attn_v, local.at[0]),
        pltpu.make_async_copy(tokens_in, tokens_v, local.at[1]),
    ]
    for copy in first:
        copy.start()
    dy_gather.start(0)
    weights_in = [
        pltpu.make_async_copy(gate_up_in, gate_up, local.at[2]),
        pltpu.make_async_copy(down_in, down, local.at[3]),
    ]
    for copy in weights_in:
        copy.start()
    for copy in first:
        copy.wait()
    total = tokens_v[...].astype(F32) + attn_v[...].astype(F32)
    for s in range(1, columns):
        sums[s - 1].wait_recv()
        total = total + arrived_v[s - 1].astype(F32)
    mixed_v[...] = total
    inverse = lax.rsqrt(jnp.mean(total * total, axis=1, keepdims=True) + EPSILON)
    ffn_v[...] = (total * inverse * gain_ref[...]).astype(BF)
    own_copy = pltpu.make_async_copy(ffn_v, ffn_all.at[pl.ds(0, size)], local.at[0])
    own_copy.start()
    mixed_copy = pltpu.make_async_copy(mixed_v, mixed_out, local.at[1])
    mixed_copy.start()
    own_copy.wait()

    rows_out = [
        mesh_copy(
            ffn_all.at[pl.ds(0, size)],
            ffn_all.at[pl.ds((columns - s) * size, size)],
            sends,
            arrivals,
            ag_base + s - 1,
            column[s - 1],
        )
        for s in range(1, columns)
    ]
    for copy in rows_out:
        copy.start()
    x_gather.start(0)
    dy_gather.forward(0)
    for b in range(1, blocks):
        rows_out[columns - b - 1].wait_recv()
        x_gather.start(b)
        x_gather.forward(b - 1)
    for b in range(blocks):
        x_gather.arrived(b, [2])
    dy_gather.arrived(0, [2])

    def source(own, gathered, r):
        return own if r == 0 else gathered.at[r - 1]

    def load(unit):
        copies = []
        for q, (r, h) in enumerate(unit):
            rows = pl.ds(h * HALF, HALF)
            copies.append(
                pltpu.make_async_copy(
                    source(ffn_all, x_others, r).at[rows], xb.at[q], local.at[4 + q]
                )
            )
            copies.append(
                pltpu.make_async_copy(
                    source(cotan_in, dy_others, r).at[rows], db.at[q], local.at[8 + q]
                )
            )
        return copies

    def choose_cols(step, q):
        return jnp.where(select_cols(slot_col_ref[step, q], experts, cap), 1.0, 0.0).astype(BF)

    def combine(step, target):
        for q in range(count):
            choose = choose_cols(step, q)

            def gather(n, carry, q=q, choose=choose):
                cols = pl.ds(pl.multiple_of(n * tile, tile), tile)
                ref, place = target(q)
                ref[place + (slice(None), cols)] = dot_plain(choose, dxs[q, :, cols]).astype(BF)
                return carry

            lax.fori_loop(0, width // tile, gather, 0)

    def spills(step):
        return [
            pltpu.make_async_copy(xs, x_all.at[step], spill.at[0]),
            pltpu.make_async_copy(ds, d_all.at[step], spill.at[1]),
            pltpu.make_async_copy(hid.at[step], hid_all.at[step], spill.at[2]),
            pltpu.make_async_copy(dgu, dgu_all.at[step], spill.at[3]),
        ]

    def pair_copy(step):
        return mesh_copy(others, theirs.at[step], sends, arrivals, pair_base + step, partner)

    def front(step):
        copies = load(BOX_UNITS[step])
        for copy in copies:
            copy.start()
        if step == 0:
            for copy in weights_in:
                copy.wait()
        if step > 0:
            for copy in spills(step - 1):
                copy.wait()
        for q in range(count):
            copies[2 * q].wait()
            copies[2 * q + 1].wait()
            hit = select_rows(slot_row_ref[step, q], experts, cap)
            weights = slot_weights(hit, weight_row_ref[step, q], experts, cap)
            choose = jnp.where(hit, 1.0, 0.0).astype(BF)

            def spread(n, carry, q=q, choose=choose, weights=weights):
                cols = pl.ds(pl.multiple_of(n * tile, tile), tile)
                rows = dot_plain(choose, xb[q, :, cols])
                grads = dot_plain(choose, db[q, :, cols]) * weights
                for e in range(experts):
                    low, high = e * cap, (e + 1) * cap
                    xs[e, q * cap : (q + 1) * cap, cols] = rows[low:high].astype(BF)
                    ds[e, q * cap : (q + 1) * cap, cols] = grads[low:high].astype(BF)
                return carry

            lax.fori_loop(0, width // tile, spread, 0)
        out_copies = spills(step)
        out_copies[0].start()
        out_copies[1].start()

        def one_expert(e, carry):
            both = dot_rows(xs[e], gate_up[e])
            gate_pre, up_pre = both[:, :pad], both[:, pad:]
            d_hidden = dot_rows(ds[e], down[e])
            sigmoid = jax.nn.sigmoid(gate_pre)
            silu = gate_pre * sigmoid
            hid[step, e] = (silu * up_pre).astype(BF)
            gate_grad = d_hidden * up_pre * (sigmoid * (1.0 + gate_pre * (1.0 - sigmoid)))
            dgu[e] = jnp.concatenate([gate_grad, d_hidden * silu], axis=1).astype(BF)

            def back(n, inner):
                cols = pl.ds(pl.multiple_of(n * tile, tile), tile)
                part = dot_plain(dgu[e], gate_up[e, :, cols]).astype(BF)
                for q in range(count):
                    dxs[q, pl.ds(pl.multiple_of(e * cap, cap), cap), cols] = part[
                        q * cap : (q + 1) * cap
                    ]
                return inner

            lax.fori_loop(0, width // tile, back, 0)
            return carry

        lax.fori_loop(0, experts, one_expert, 0)
        out_copies[2].start()
        out_copies[3].start()
        if step > 0:
            pair_copy(step - 1).wait_send()
        combine(step, lambda q: (chip, (step, q)) if q < 2 else (others, (q - 2,)))
        pair_copy(step).start()

    def add_rows(step, q, cols, landed):
        fetch = pltpu.make_async_copy(landed, stage.at[:, cols], local.at[12])
        fetch.start()
        fetch.wait()

        def some(i, carry):
            rows = pl.ds(pl.multiple_of(i * 32, 32), 32)
            chip[step, q, rows, cols] = (
                chip[step, q, rows, cols].astype(F32) + stage[rows, cols].astype(F32)
            ).astype(BF)
            return carry

        lax.fori_loop(0, HALF // 32, some, 0)

    left, right = pl.ds(0, half_width), pl.ds(half_width, half_width)

    def chip_sum(step):
        pair_copy(step).wait_recv()
        for h in range(2):
            add_rows(step, h, pl.ds(0, width), theirs.at[step, h])

    def chip_place(r, h):
        step = [i for i, unit in enumerate(BOX_UNITS) if (r, h) in unit][0]
        return step, BOX_UNITS[step].index((r, h))

    def chip_rows(r, h):
        return chip.at[chip_place(r, h)]

    def link_copy(stage_number, side, h):
        first_hop, second_hop = (along, across) if side == 0 else (across, along)
        near, far = (2, 4) if side == 0 else (4, 2)
        r = (near, 6, far)[stage_number]
        device = second_hop if stage_number == 2 else first_hop
        i = (stage_number * 2 + side) * 2 + h
        return mesh_copy(
            chip.at[chip_place(r, h) + (pl.ds(0, HALF), (left, right)[side])],
            links.at[i],
            sends,
            arrivals,
            link_base + i,
            device,
        )

    def take_link(stage_number, side, h, r):
        link_copy(stage_number, side, h).wait_recv()
        i = (stage_number * 2 + side) * 2 + h
        add_rows(*chip_place(r, h), (left, right)[side], links.at[i])

    def out_part(step):
        weights = [
            slot_weights(
                select_rows(slot_row_ref[step, q], experts, cap),
                weight_row_ref[step, q],
                experts,
                cap,
            )
            for q in range(count)
        ]
        for e in range(experts):

            def one_tile(n, carry, e=e):
                cols = pl.ds(pl.multiple_of(n * tile, tile), tile)
                rows = dot_plain(hid[step, e], down[e, :, cols])
                for q in range(count):
                    dxs[q, e * cap : (e + 1) * cap, cols] = (
                        rows[q * cap : (q + 1) * cap] * weights[q][e * cap : (e + 1) * cap]
                    ).astype(BF)
                return carry

            lax.fori_loop(0, width // tile, one_tile, 0)
        if step > 0:
            out_copy(step - 1).wait()
        combine(step, lambda q: (db, (q,)))
        out_copy(step).start()

    def out_copy(step):
        return pltpu.make_async_copy(db, out_all.at[step], local.at[13])

    middle = blocks // 2
    front(0)
    x_gather.forward(blocks - 1)
    dy_gather.last(0)
    for b in range(middle):
        x_gather.arrived(b, [5, 6])
    dy_gather.arrived(0, [5, 6])
    front(1)
    for b in range(blocks):
        x_gather.last(b)
    for b in range(middle, blocks):
        x_gather.arrived(b, [5, 6])
    chip_sum(0)
    front(2)
    chip_sum(1)
    for side in range(2):
        link_copy(0, side, 0).start()
    for b in range(blocks):
        x_gather.arrived(b, [7])
    dy_gather.arrived(0, [7])
    front(3)
    chip_sum(2)
    for side in range(2):
        link_copy(0, side, 1).start()
    for copy in spills(3):
        copy.wait()
    out_part(0)
    chip_sum(3)
    for h in range(2):
        for side in range(2):
            link_copy(1, side, h).start()
    out_part(1)
    for h in range(2):
        for side in range(2):
            take_link(1, side, h, (4, 2)[side])
            link_copy(2, side, h).start()
    out_part(2)
    out_part(3)
    for h in range(2):
        for side in range(2):
            take_link(0, side, h, 0)
        for side in range(2):
            take_link(2, side, h, 0)
        done = pltpu.make_async_copy(
            chip_rows(0, h), dx_out.at[pl.ds(h * HALF, HALF)], local.at[14 + h]
        )
        done.start()
    for h in range(2):
        pltpu.make_async_copy(
            chip_rows(0, h), dx_out.at[pl.ds(h * HALF, HALF)], local.at[14 + h]
        ).wait()
    out_copy(3).wait()
    mixed_copy.wait()

    for b in range(blocks):
        x_gather.drain(b)
    dy_gather.drain(0)
    for copy in sums + rows_out:
        copy.wait_send()
    pair_copy(3).wait_send()
    for stage_number in range(3):
        for side in range(2):
            for h in range(2):
                link_copy(stage_number, side, h).wait_send()


def expert_call(attn_part, tokens, cotan_all, gate_up, down, gain, tables, cap):
    columns = lax.axis_size("tp")
    size, width = tokens.shape
    experts, wide, _ = gate_up.shape
    pad = wide // 2
    slots = QUARTET * cap
    steps = len(BOX_UNITS)
    anywhere = pl.BlockSpec(memory_space=pl.ANY)
    held = pl.BlockSpec(memory_space=pltpu.VMEM)

    def array(*dims, kind=BF):
        return jax.ShapeDtypeStruct(dims, kind)

    copies = 8 * columns + 8 + 2 * (columns - 1) + steps + 12
    results = pl.pallas_call(
        functools.partial(expert_kernel, experts, cap, columns, size),
        out_shape=[
            array(size, width, kind=F32),
            array(SEQ, width),
            array(SEQ, width),
            array(steps, QUARTET, HALF, width),
            array(steps, experts, slots, width),
            array(steps, experts, slots, width),
            array(steps, experts, slots, pad),
            array(steps, experts, slots, wide),
            array(7, SEQ, width),
            array(7, SEQ, width),
            array(steps, 2, HALF, width),
            array(12, HALF, width // 2),
        ],
        in_specs=[anywhere] * 5 + [held] * 4,
        out_specs=[anywhere] * 12,
        scratch_shapes=[
            pltpu.VMEM((size, width), BF),
            pltpu.VMEM((size, width), BF),
            pltpu.VMEM((columns - 1, size, width), BF),
            pltpu.VMEM((size, width), F32),
            pltpu.VMEM((size, width), BF),
            pltpu.VMEM((QUARTET, HALF, width), BF),
            pltpu.VMEM((QUARTET, HALF, width), BF),
            pltpu.VMEM((experts, wide, width), BF),
            pltpu.VMEM((experts, pad, width), BF),
            pltpu.VMEM((experts, slots, width), BF),
            pltpu.VMEM((experts, slots, width), BF),
            pltpu.VMEM((QUARTET, experts * cap, width), BF),
            pltpu.VMEM((2, HALF, width), BF),
            pltpu.VMEM((steps, 2, HALF, width), BF),
            pltpu.VMEM((steps, experts, slots, pad), BF),
            pltpu.VMEM((experts, slots, wide), BF),
            pltpu.VMEM((HALF, width), BF),
            pltpu.SemaphoreType.DMA((copies,)),
            pltpu.SemaphoreType.DMA((copies,)),
            pltpu.SemaphoreType.DMA((16,)),
            pltpu.SemaphoreType.DMA((4,)),
        ],
        compiler_params=pltpu.CompilerParams(
            collective_id=1, has_side_effects=True, vmem_limit_bytes=67_043_328
        ),
        cost_estimate=pl.CostEstimate(
            flops=steps
            * (2 * slots * experts * width * pad * 6 + 8 * QUARTET * HALF * experts * cap * width),
            bytes_accessed=60 * SEQ * width,
            transcendentals=0,
        ),
        name="experts",
    )(attn_part, tokens, cotan_all, gate_up, down, gain, *tables)
    return results[:8]


def first_kernel(columns, size, *refs):
    (
        tokens_in,
        packed_in,
        tokens_all,
        packed_all,
        tokens_v,
        packed_v,
        sends,
        arrivals,
        local,
    ) = refs
    partner, along, across = plane_neighbours()
    column = column_neighbours(columns)
    place = lax.axis_index("fsdp")
    rows = packed_in.shape[0]
    top, bottom = pl.ds(0, rows // 2), pl.ds(rows // 2, rows // 2)
    opposite = along[0] + across[0] - place
    greet([partner, along, across] + column)
    plan = [
        (packed_in, packed_all.at[place], along),
        (packed_in, packed_all.at[place], across),
        (packed_in, packed_all.at[place], partner),
        (packed_all.at[along[0], top], packed_all.at[along[0], top], across),
        (packed_all.at[across[0], bottom], packed_all.at[across[0], bottom], along),
        (packed_all.at[along[0]], packed_all.at[along[0]], partner),
        (packed_all.at[across[0]], packed_all.at[across[0]], partner),
        (packed_all.at[opposite], packed_all.at[opposite], partner),
    ]
    copies = [
        mesh_copy(src, dst, sends, arrivals, i, device) for i, (src, dst, device) in enumerate(plan)
    ]
    rows_out = [
        mesh_copy(
            tokens_in,
            tokens_all.at[pl.ds((columns - s) * size, size)],
            sends,
            arrivals,
            7 + s,
            column[s - 1],
        )
        for s in range(1, columns)
    ]
    for copy in copies[:3] + rows_out:
        copy.start()
    here = [
        pltpu.make_async_copy(tokens_in, tokens_v, local.at[0]),
        pltpu.make_async_copy(packed_in, packed_v, local.at[1]),
    ]
    for copy in here:
        copy.start()
    for copy in here:
        copy.wait()
    there = [
        pltpu.make_async_copy(tokens_v, tokens_all.at[pl.ds(0, size)], local.at[0]),
        pltpu.make_async_copy(packed_v, packed_all.at[place], local.at[1]),
    ]
    for copy in there:
        copy.start()
    copies[0].wait_recv()
    copies[3].start()
    copies[5].start()
    copies[1].wait_recv()
    copies[4].start()
    copies[6].start()
    copies[3].wait_recv()
    copies[4].wait_recv()
    copies[7].start()
    for i in (2, 5, 6, 7):
        copies[i].wait_recv()
    for copy in rows_out:
        copy.wait_recv()
    for copy in there:
        copy.wait()
    for copy in copies + rows_out:
        copy.wait_send()


def first_call(tokens, packed):
    columns = lax.axis_size("tp")
    size, width = tokens.shape
    anywhere = pl.BlockSpec(memory_space=pl.ANY)
    copies = 8 + columns - 1
    return pl.pallas_call(
        functools.partial(first_kernel, columns, size),
        out_shape=[
            jax.ShapeDtypeStruct((columns * size, width), BF),
            jax.ShapeDtypeStruct((8,) + packed.shape, BF),
        ],
        in_specs=[anywhere] * 2,
        out_specs=[anywhere] * 2,
        scratch_shapes=[
            pltpu.VMEM((size, width), BF),
            pltpu.VMEM(packed.shape, BF),
            pltpu.SemaphoreType.DMA((copies,)),
            pltpu.SemaphoreType.DMA((copies,)),
            pltpu.SemaphoreType.DMA((2,)),
        ],
        compiler_params=pltpu.CompilerParams(collective_id=2, has_side_effects=True),
        name="first_gather",
    )(tokens, packed)


def plane_units(count):
    if count == 8:
        return BOX_UNITS
    return [[(2 * i + j // 2, j % 2) for j in range(4)] for i in range(count // 2)]


def partner(block):
    return swap(block, "fsdp", 1)


def plane_gather(rows, count):
    gathered = lax.all_gather(rows, "fsdp", axis=0)
    return {
        (r, h): gathered[r, h * HALF : (h + 1) * HALF] for r in range(count) for h in (0, 1)
    }


def add_pairs(left, right):
    return left.astype(F32) + right.astype(F32)


def chip_sums(unit, pair):
    theirs = partner(pair[1])
    return {unit[h]: add_pairs(pair[0][h], theirs[h]) for h in (0, 1)}


def plane_scatter(chip):
    whole = {r: jnp.concatenate([chip[r, 0], chip[r, 1]], axis=0) for r in (0, 2, 4, 6)}
    half = whole[0].shape[1] // 2
    left, right = slice(None, half), slice(half, None)

    def send(rows, bit):
        return swap(rows.astype(BF), "fsdp", bit)

    on_left = add_pairs(whole[4][:, left], send(whole[6][:, left], 2))
    on_right = add_pairs(whole[2][:, right], send(whole[6][:, right], 4))
    first = add_pairs(whole[0][:, left], send(whole[2][:, left], 2))
    second = add_pairs(whole[0][:, right], send(whole[4][:, right], 4))
    first = add_pairs(first, send(on_left, 4))
    second = add_pairs(second, send(on_right, 2))
    return jnp.concatenate([first, second], axis=1)


def plane_scatter_whole(pairs, units, count):
    parts = {}
    for unit, pair in zip(units, pairs):
        for q, key in enumerate(unit):
            parts[key] = pair[q // 2][q % 2]
    stacked = jnp.concatenate([parts[r, h] for r in range(count) for h in (0, 1)], axis=0)
    return lax.psum_scatter(stacked, "fsdp", scatter_dimension=0, tiled=True).astype(F32)


def sum_everywhere(values):
    for axis_name in ("fsdp", "tp"):
        count = lax.axis_size(axis_name)
        if is_power(count):
            bit = 1
            while bit < count:
                values = values + swap(values, axis_name, bit)
                bit *= 2
        else:
            values = lax.psum(values, axis_name)
    return values


def expert_tables(expert_ids, expert_wts, local_experts, units, cap):
    fsdp_count = lax.axis_size("fsdp")
    fsdp_rank = lax.axis_index("fsdp")
    tp_count = lax.axis_size("tp")
    expert_count = local_experts * fsdp_count
    places = (lax.axis_index("tp") + jnp.arange(tp_count, dtype=jnp.int32)) % tp_count

    def reorder(rows):
        return jnp.take(rows.reshape(tp_count, -1, TOPK), places, axis=0).reshape(SEQ, TOPK)

    expert_ids, expert_wts = reorder(expert_ids), reorder(expert_wts)
    names = jnp.arange(expert_count, dtype=jnp.int32)[:, None]
    member = jnp.zeros((expert_count, SEQ), jnp.bool_)
    weight = jnp.zeros((expert_count, SEQ), F32)
    ids_rows, wts_rows = expert_ids.T, expert_wts.T
    for pick in range(TOPK):
        same = ids_rows[pick : pick + 1] == names
        member = member | same
        weight = weight + jnp.where(same, wts_rows[pick : pick + 1], 0.0)
    position = jnp.arange(HALF)
    before = (position[:, None] < position[None, :]).astype(BF)
    rank = jnp.dot(
        member.astype(BF).reshape(expert_count * 2, HALF), before, preferred_element_type=F32
    ).reshape(expert_count, SEQ)
    slot = jnp.where(member, rank, NO_SLOT)
    table = jnp.concatenate([slot, weight], axis=0)
    if fsdp_count == 8:
        for bit in (1, 2, 4):
            table = jnp.concatenate([table, swap(table, "fsdp", bit)], axis=0)
    else:
        table = lax.all_gather(table, "fsdp", axis=0, tiled=True)
    table = table.reshape(fsdp_count, 2, fsdp_count, local_experts, 2, HALF)
    table = lax.dynamic_index_in_dim(table, fsdp_rank, axis=2, keepdims=False)
    slot_steps, weight_steps = [], []
    for unit in units:
        slot_steps.append(jnp.stack([table[r, 0, :, h] for r, h in unit]))
        weight_steps.append(jnp.stack([table[r, 1, :, h] for r, h in unit]))
    slot_row, weight_row = jnp.stack(slot_steps), jnp.stack(weight_steps)
    return (slot_row, weight_row, jnp.swapaxes(slot_row, 2, 3))


def per_device(
    block_in,
    out_cotan,
    segment_ids,
    expert_ids,
    expert_wts,
    attn_gain,
    query_proj,
    latent_proj,
    latent_gain,
    latent_up,
    out_proj,
    ffn_gain,
    shared_gate,
    shared_up,
    shared_down,
    routed_gate,
    routed_up,
    routed_down,
):
    tp_count = lax.axis_size("tp")
    fsdp_count = lax.axis_size("fsdp")
    tp_rank = lax.axis_index("tp")
    fsdp_rank = lax.axis_index("fsdp")
    tok_rows, model_width = block_in.shape
    local_experts, local_hidden = routed_gate.shape[:2]
    expert_count = local_experts * fsdp_count
    cap_rows = tok_rows * TOPK * 4 // (3 * expert_count)
    cap = cap_rows * (HALF // tok_rows)
    heads_local = H // tp_count
    head_width = NOPE + ROPE
    score_scale = head_width ** (-0.5)
    shard_rows, query_cols = query_proj.shape
    latent_cols = latent_proj.shape[1]
    up_cols = latent_up.shape[1]
    out_rows = out_proj.shape[0]
    units = plane_units(fsdp_count)

    joint = query_cols + latent_cols
    spare = (-joint) % 128
    spare = spare + 128 if spare < 3 else spare
    gains = jnp.concatenate(
        [
            attn_gain[:, None],
            ffn_gain[:, None],
            jnp.pad(latent_gain, (0, shard_rows - latent_gain.shape[0]))[:, None],
            jnp.zeros((shard_rows, spare - 3), BF),
        ],
        axis=1,
    )
    packed = jnp.concatenate(
        [query_proj, latent_proj, gains, latent_up.reshape(shard_rows, -1)], axis=1
    )
    lift_cols = packed.shape[1] - joint - spare
    paired = fsdp_count == 8
    if paired:
        tokens_all, packed_all = first_call(block_in, packed)
        packed_all = packed_all.reshape(-1, packed.shape[1])
    else:
        packed_all = lax.all_gather(packed, "fsdp", axis=0, tiled=True)
        tokens_all = column_gather(block_in)
    joint_weight = packed_all[:, :joint]
    gain_attn = packed_all[:, joint].astype(F32)
    gain_ffn = packed_all[:, joint + 1].astype(F32)
    gain_latent = (
        packed_all[:, joint + 2]
        .reshape(fsdp_count, shard_rows)[:, : latent_gain.shape[0]]
        .reshape(LAT)
        .astype(F32)
    )
    latent_up_weight = packed_all[:, joint + spare :].reshape(LAT, up_cols)
    out_weight = lax.all_gather(out_proj, "fsdp", axis=1, tiled=True)
    cotan_own, tokens_all = tie(out_cotan, tokens_all)
    cotan_all = column_gather(cotan_own)
    shared_weight = lax.all_gather(
        jnp.concatenate([shared_gate, shared_up], axis=1), "fsdp", axis=0, tiled=True
    )
    shared_down_weight = lax.all_gather(shared_down, "fsdp", axis=1, tiled=True)
    shared_cols = shared_gate.shape[1]
    tables = expert_tables(expert_ids, expert_wts, local_experts, units, cap)
    hidden_pad = -(-local_hidden // 128) * 128
    lift = ((0, 0), (0, hidden_pad - local_hidden), (0, 0))
    routed_gate_up = jnp.concatenate([jnp.pad(routed_gate, lift), jnp.pad(routed_up, lift)], axis=1)
    routed_down_pad = jnp.pad(routed_down, lift)

    unit_all, inverse_all = norm_parts(tokens_all.astype(F32))
    normed_all = (unit_all * gain_attn).astype(BF)
    joint_rows = jnp.dot(normed_all, joint_weight, preferred_element_type=F32)
    queries = joint_rows[:, :query_cols].reshape(SEQ, heads_local, head_width)
    latent = joint_rows[:, query_cols:]
    unit_lat, inverse_lat = norm_parts(latent[:, :LAT])
    places = (tp_rank + jnp.arange(tp_count, dtype=jnp.int32)) % tp_count
    positions = (
        places[:, None] * tok_rows + jnp.arange(tok_rows, dtype=jnp.int32)[None, :]
    ).reshape(SEQ)
    segments = jnp.take(segment_ids.reshape(tp_count, tok_rows), places, axis=0).reshape(SEQ)
    cosine, sine_part = rope_tables(positions, ROPE)
    compressed_all = (unit_lat * gain_latent).astype(BF)
    key_rope_all = rotate(latent[:, LAT:], cosine, sine_part).astype(BF)
    query_cat = jnp.concatenate(
        [
            queries[:, :, :NOPE],
            rotate(queries[:, :, NOPE:], cosine[:, None, :], sine_part[:, None, :]),
        ],
        axis=2,
    ).astype(BF)
    key_value = (
        jnp.dot(compressed_all, latent_up_weight, preferred_element_type=F32)
        .reshape(SEQ, heads_local, NOPE + DV)
        .astype(BF)
    )
    key_cat = jnp.concatenate(
        [
            key_value[:, :, :NOPE],
            jnp.broadcast_to(key_rope_all[:, None, :], (SEQ, heads_local, ROPE)),
        ],
        axis=2,
    )
    values = key_value[:, :, NOPE:]
    allowed = (positions[None, :] <= positions[:, None]) & (
        segments[None, :] == segments[:, None]
    )
    raw_scores = (
        jnp.einsum("qhd,khd->hqk", query_cat, key_cat, preferred_element_type=F32) * score_scale
    )
    masked = jnp.where(allowed[None], raw_scores, MASK_FILL)
    top_score = jnp.max(masked, axis=2, keepdims=True)
    exponent = jnp.exp(masked - top_score)
    row_total = jnp.sum(exponent, axis=2, keepdims=True)
    probabilities = exponent / row_total
    probs_low = probabilities.astype(BF)
    attended = (
        jnp.einsum("hqk,khd->qhd", probs_low, values, preferred_element_type=F32)
        .reshape(SEQ, heads_local * DV)
        .astype(BF)
    )
    attn_part = jnp.dot(attended, out_weight, preferred_element_type=F32).astype(BF)
    if paired:
        mixed_rows, normed_ffn_all, d_routed_in, out_array, *kept = expert_call(
            attn_part,
            block_in,
            cotan_all,
            routed_gate_up,
            routed_down_pad,
            gain_ffn[None, :],
            tables,
            cap,
        )
        unit_two, inverse_two = norm_parts(mixed_rows)
        d_routed_in = d_routed_in.astype(F32)
        near, far = out_array[:, :2], out_array[:, 2:]
    else:
        mixed_rows = block_in.astype(F32) + column_scatter(attn_part)
        unit_two, inverse_two = norm_parts(mixed_rows)
        normed_ffn_all = column_gather((unit_two * gain_ffn).astype(BF))
        x_blocks = plane_gather(normed_ffn_all, fsdp_count)
        dy_all = lax.all_gather(cotan_all, "fsdp", axis=0, tiled=True)
        kept = []
        dx_pairs = []
        for step, unit in enumerate(units):
            pair, kept = expert_front(
                step,
                len(units),
                [x_blocks[key] for key in unit],
                jnp.array([2 * r + h for r, h in unit], jnp.int32),
                dy_all,
                routed_gate_up,
                routed_down_pad,
                tables,
                kept,
                cap,
            )
            dx_pairs.append(pair)
        near, far = expert_out(kept[2], routed_down_pad, tables, cap)
        d_routed_in = plane_scatter_whole(dx_pairs, units, fsdp_count)
    routed_gate_grad, routed_up_grad, routed_down_grad = expert_grads(kept, local_hidden)

    shared_pre = jnp.dot(normed_ffn_all, shared_weight, preferred_element_type=F32)
    shared_gate_pre, shared_up_pre = shared_pre[:, :shared_cols], shared_pre[:, shared_cols:]
    shared_hidden = (jax.nn.silu(shared_gate_pre) * shared_up_pre).astype(BF)
    shared_rows = jnp.dot(shared_hidden, shared_down_weight, preferred_element_type=F32)
    shared_down_part = jnp.dot(shared_hidden.T, cotan_all, preferred_element_type=F32)
    d_shared_hidden = jnp.dot(cotan_all, shared_down_weight.T, preferred_element_type=F32)
    d_shared = jnp.concatenate(silu_back(d_shared_hidden, shared_gate_pre, shared_up_pre), axis=1)
    shared_part = jnp.dot(normed_ffn_all.T, d_shared, preferred_element_type=F32)
    d_shared_in = jnp.dot(d_shared, shared_weight.T, preferred_element_type=F32)

    d_ffn_rows, shared_part, shared_down_part, near, far = tie(
        d_shared_in + d_routed_in,
        shared_part.astype(BF),
        shared_down_part.astype(BF),
        near,
        far,
    )
    d_normed_ffn = column_scatter(d_ffn_rows)
    out_pairs = [(near[step], far[step]) for step in range(len(units))]
    if paired:
        out_chip = {}
        for unit, pair in zip(units, out_pairs):
            out_chip.update(chip_sums(unit, pair))
        routed_rows = plane_scatter(out_chip)
    else:
        routed_rows = plane_scatter_whole(out_pairs, units, fsdp_count)
    ffn_gain_part, d_mixed_norm = norm_back(d_normed_ffn, unit_two, inverse_two, gain_ffn)
    d_mixed = out_cotan.astype(F32) + d_mixed_norm
    d_proj_all, routed_rows = tie(column_gather(d_mixed.astype(BF)), routed_rows)

    ffn_rows = column_scatter(shared_rows + routed_rows)
    block_out = (mixed_rows + ffn_rows).astype(BF)

    out_part = jnp.dot(attended.T, d_proj_all, preferred_element_type=F32)
    d_attended = (
        jnp.dot(d_proj_all, out_weight.T, preferred_element_type=F32)
        .astype(BF)
        .reshape(SEQ, heads_local, DV)
    )
    prob_grad = jnp.einsum("qhd,khd->hqk", d_attended, values, preferred_element_type=F32)
    score_grad = (
        probabilities
        * (prob_grad - jnp.sum(probabilities * prob_grad, axis=2, keepdims=True))
    ).astype(BF)
    query_grad = (
        jnp.einsum("hqk,khd->qhd", score_grad, key_cat, preferred_element_type=F32) * score_scale
    )
    key_grad = (
        jnp.einsum("hqk,qhd->khd", score_grad, query_cat, preferred_element_type=F32) * score_scale
    )
    value_grad = jnp.einsum("hqk,qhd->khd", probs_low, d_attended, preferred_element_type=F32)
    d_queries = (
        jnp.concatenate(
            [
                query_grad[:, :, :NOPE],
                unrotate(query_grad[:, :, NOPE:], cosine[:, None, :], sine_part[:, None, :]),
            ],
            axis=2,
        )
        .reshape(SEQ, heads_local * head_width)
        .astype(BF)
    )
    d_key_value = (
        jnp.concatenate([key_grad[:, :, :NOPE], value_grad], axis=2)
        .reshape(SEQ, heads_local * (NOPE + DV))
        .astype(BF)
    )
    latent_up_part = jnp.dot(compressed_all.T, d_key_value, preferred_element_type=F32)
    d_compressed = jnp.dot(d_key_value, latent_up_weight.T, preferred_element_type=F32)
    d_key_rope = jnp.sum(key_grad[:, :, NOPE:], axis=1)
    latent_gain_part, d_latent_main = norm_back(d_compressed, unit_lat, inverse_lat, gain_latent)
    d_latent = jnp.concatenate(
        [d_latent_main, unrotate(d_key_rope, cosine, sine_part)], axis=1
    ).astype(BF)
    d_joint = jnp.concatenate([d_queries, d_latent], axis=1)
    joint_part = jnp.dot(normed_all.T, d_joint, preferred_element_type=F32)
    d_normed_part = jnp.dot(d_joint, joint_weight.T, preferred_element_type=F32)
    attn_gain_part = jnp.sum(d_normed_part * unit_all, axis=0)
    d_normed = column_scatter(d_normed_part)
    unit_one, inverse_one = norm_parts(block_in.astype(F32))
    _, d_tokens_norm = norm_back(d_normed, unit_one, inverse_one, gain_attn)
    block_in_grad = d_mixed + d_tokens_norm

    def scatter(part, dimension):
        return lax.psum_scatter(
            part.astype(BF), "fsdp", scatter_dimension=dimension, tiled=True
        )

    shared_down_grad = scatter(shared_down_part, 1)
    shared_part, shared_down_grad = tie(shared_part, shared_down_grad)
    shared_grad = scatter(shared_part, 0)
    out_part, shared_grad = tie(out_part.astype(BF), shared_grad)
    out_proj_grad = scatter(out_part, 1)
    lift_part = latent_up_part.astype(BF).reshape(model_width, lift_cols)
    joint_sum = jnp.concatenate(
        [
            joint_part.astype(BF),
            jnp.zeros((model_width, (-joint) % 128), BF),
            lift_part,
        ],
        axis=1,
    )
    joint_sum, out_proj_grad = tie(joint_sum, out_proj_grad)
    joint_grad = scatter(joint_sum, 0)
    query_proj_grad = joint_grad[:, :query_cols].astype(F32)
    latent_grad = joint_grad[:, query_cols:joint].reshape(tp_count, -1, latent_cols)
    latent_proj_grad = column_scatter(
        jnp.take(latent_grad, places, axis=0).reshape(-1, latent_cols)
    )
    latent_up_grad = (
        joint_grad[:, joint_grad.shape[1] - lift_cols :].reshape(latent_up.shape).astype(F32)
    )
    out_proj_grad = out_proj_grad.astype(F32)
    shared_grad = shared_grad.astype(F32)
    shared_gate_grad, shared_up_grad = shared_grad[:, :shared_cols], shared_grad[:, shared_cols:]
    shared_down_grad = shared_down_grad.astype(F32)
    gain_sums = sum_everywhere(
        jnp.concatenate([attn_gain_part, latent_gain_part, ffn_gain_part]).reshape(-1, 128)
    ).reshape(-1)
    device = fsdp_rank * tp_count + tp_rank
    devices = tp_count * fsdp_count

    def own_gain(start, size):
        return lax.dynamic_slice(gain_sums, (start + device * (size // devices),), (size // devices,))

    attn_gain_grad = own_gain(0, model_width)
    latent_gain_grad = own_gain(model_width, LAT)
    ffn_gain_grad = own_gain(model_width + LAT, model_width)
    return (
        block_out,
        block_in_grad,
        attn_gain_grad,
        query_proj_grad,
        latent_proj_grad,
        latent_gain_grad,
        latent_up_grad,
        out_proj_grad,
        ffn_gain_grad,
        shared_gate_grad,
        shared_up_grad,
        shared_down_grad,
        routed_gate_grad,
        routed_up_grad,
        routed_down_grad,
    )


def solution(mesh):
    placed = (
        P(("fsdp", "tp"), None),
        P(("fsdp", "tp"), None),
        P("fsdp"),
        P("fsdp", None),
        P("fsdp", None),
        P("fsdp"),
        P("fsdp", "tp"),
        P("fsdp", None),
        P("fsdp"),
        P("fsdp", "tp"),
        P("tp", "fsdp"),
        P("fsdp"),
        P("fsdp", "tp"),
        P("fsdp", "tp"),
        P("tp", "fsdp"),
        P("fsdp", "tp", None),
        P("fsdp", "tp", None),
        P("fsdp", "tp", None),
    )
    return jax.shard_map(
        per_device,
        mesh=mesh,
        in_specs=placed,
        out_specs=(
            P(("fsdp", "tp"), None),
            P(("fsdp", "tp"), None),
            P(("fsdp", "tp")),
            P("fsdp", "tp"),
            P(("fsdp", "tp"), None),
            P(("fsdp", "tp")),
            P("fsdp", "tp"),
            P("tp", "fsdp"),
            P(("fsdp", "tp")),
            P("fsdp", "tp"),
            P("fsdp", "tp"),
            P("tp", "fsdp"),
            P("fsdp", "tp", None),
            P("fsdp", "tp", None),
            P("fsdp", "tp", None),
        ),
        check_vma=False,
    )
```

```python
import functools

import jax
import jax.numpy as jnp
from jax import lax
from jax.experimental import pallas as pl
from jax.experimental.pallas import tpu as pltpu
from jax.sharding import PartitionSpec as P

H = 16
NOPE = 128
ROPE = 64
DV = 128
LAT = 512
TOPK = 6
SEQ = 512
HALF = 256
QUARTET = 4
BOX_UNITS = [
    [(0, 0), (0, 1), (1, 0), (1, 1)],
    [(2, 0), (4, 0), (3, 0), (5, 0)],
    [(2, 1), (4, 1), (3, 1), (5, 1)],
    [(6, 0), (6, 1), (7, 0), (7, 1)],
]


EPSILON = 1e-06
THETA_BASE = 10000.0
MASK_FILL = -1e30
NO_SLOT = -1e6

BF = jnp.bfloat16
F32 = jnp.float32


def rope_tables(positions, width_rope):
    middle = width_rope // 2
    frequency = THETA_BASE ** (-(jnp.arange(middle) * 2).astype(jnp.float32) / width_rope)
    angles = positions.astype(jnp.float32)[:, None] * frequency[None, :]
    return (jnp.cos(angles), jnp.sin(angles))


def rotate(values, cosine, sine_part):
    middle = values.shape[-1] // 2
    first_half = values[..., :middle]
    second_half = values[..., middle:]
    return jnp.concatenate(
        [
            first_half * cosine - second_half * sine_part,
            second_half * cosine + first_half * sine_part,
        ],
        axis=-1,
    )


def unrotate(values, cosine, sine_part):
    middle = values.shape[-1] // 2
    first_half = values[..., :middle]
    second_half = values[..., middle:]
    return jnp.concatenate(
        [
            first_half * cosine + second_half * sine_part,
            second_half * cosine - first_half * sine_part,
        ],
        axis=-1,
    )


def norm_parts(values):
    inverse = lax.rsqrt(jnp.mean(values * values, axis=-1, keepdims=True) + EPSILON)
    return (values * inverse, inverse)


def norm_back(upstream, unit_rows, inverse, scaling):
    scaled = upstream * scaling
    gain_grad = jnp.sum(upstream * unit_rows, axis=0)
    input_grad = inverse * (
        scaled - unit_rows * jnp.mean(scaled * unit_rows, axis=-1, keepdims=True)
    )
    return (gain_grad, input_grad)


def silu_back(grad_hidden, gate_pre, up_pre):
    sigmoid = jax.nn.sigmoid(gate_pre)
    gate_grad = grad_hidden * up_pre * (sigmoid * (1.0 + gate_pre * (1.0 - sigmoid)))
    up_grad = grad_hidden * (gate_pre * sigmoid)
    return (gate_grad.astype(jnp.bfloat16), up_grad.astype(jnp.bfloat16))


def is_power(count):
    return count & (count - 1) == 0


def swap(values, axis_name, bit):
    count = lax.axis_size(axis_name)
    return lax.ppermute(values, axis_name, [(i, i ^ bit) for i in range(count)])


def tie(*values):
    return lax.optimization_barrier(values)


def column_gather(rows):
    count = lax.axis_size("tp")
    pieces = [rows]
    for s in range(1, count):
        pieces.append(lax.ppermute(rows, "tp", [((i + s) % count, i) for i in range(count)]))
    return jnp.concatenate(pieces, axis=0)


def column_scatter(values):
    count = lax.axis_size("tp")
    size = values.shape[0] // count
    total = values[:size].astype(F32)
    for s in range(1, count):
        piece = values[s * size : (s + 1) * size].astype(BF)
        total = total + lax.ppermute(
            piece, "tp", [(i, (i + s) % count) for i in range(count)]
        ).astype(F32)
    return total


def dot_rows(left, right):
    return lax.dot_general(left, right, (((1,), (1,)), ((), ())), preferred_element_type=F32)


def dot_plain(left, right):
    return lax.dot_general(left, right, (((1,), (0,)), ((), ())), preferred_element_type=F32)


def dot_first(left, right):
    return lax.dot_general(left, right, (((0,), (0,)), ((), ())), preferred_element_type=F32)


def select_rows(slot_rows, experts, cap):
    row = lax.broadcasted_iota(jnp.int32, (experts * cap, HALF), 0).astype(F32)
    hit = row == slot_rows[0:1, :]
    for e in range(1, experts):
        hit = hit | (row == slot_rows[e : e + 1, :] + float(e * cap))
    return hit


def select_cols(slot_cols, experts, cap):
    lane = lax.broadcasted_iota(jnp.int32, (HALF, experts * cap), 1).astype(F32)
    hit = lane == slot_cols[:, 0:1]
    for e in range(1, experts):
        hit = hit | (lane == slot_cols[:, e : e + 1] + float(e * cap))
    return hit


def slot_weights(hit, weight_rows, experts, cap):
    pieces = []
    for e in range(experts):
        part = hit[e * cap : (e + 1) * cap, :]
        pieces.append(
            jnp.sum(jnp.where(part, weight_rows[e : e + 1, :], 0.0), axis=1, keepdims=True)
        )
    return jnp.concatenate(pieces, axis=0)


def expert_front_kernel(step, experts, cap, aliased, *refs):
    count = QUARTET
    x_in = refs[:count]
    where_ref, dy_in, gate_up_in, down_in, slot_row_ref, weight_row_ref, slot_col_ref = refs[
        count : count + 7
    ]
    base = count + 7 + aliased
    dx_out = refs[base : base + 2]
    x_all, d_all, hid_all, dgu_all = refs[base + 2 : base + 6]
    (xb, db, gate_up, down, xs, ds, dxs, dxo, hid, dgu, sem_in, sem_w, sem_out, sem_dx) = refs[
        base + 6 :
    ]
    width = xb.shape[2]
    pad = down.shape[1]
    tile = min(1024, width)
    x_copies = [pltpu.make_async_copy(x_in[q], xb.at[q], sem_in.at[q]) for q in range(count)]
    d_copies = [
        pltpu.make_async_copy(
            dy_in.at[pl.ds(pl.multiple_of(where_ref[q] * HALF, HALF), HALF)],
            db.at[q],
            sem_in.at[count + q],
        )
        for q in range(count)
    ]
    w_copies = [
        pltpu.make_async_copy(gate_up_in, gate_up, sem_w.at[0]),
        pltpu.make_async_copy(down_in, down, sem_w.at[1]),
    ]
    for q in range(count):
        x_copies[q].start()
        d_copies[q].start()
    for copy in w_copies:
        copy.start()
    for q in range(count):
        x_copies[q].wait()
        d_copies[q].wait()

        hit = select_rows(slot_row_ref[q], experts, cap)
        weights = slot_weights(hit, weight_row_ref[q], experts, cap)
        choose = jnp.where(hit, 1.0, 0.0).astype(BF)

        def spread(n, carry, q=q, choose=choose, weights=weights):
            cols = pl.ds(pl.multiple_of(n * tile, tile), tile)
            rows = dot_plain(choose, xb[q, :, cols])
            grads = dot_plain(choose, db[q, :, cols]) * weights
            for e in range(experts):
                xs[e, q * cap : (q + 1) * cap, cols] = rows[e * cap : (e + 1) * cap].astype(BF)
                ds[e, q * cap : (q + 1) * cap, cols] = grads[e * cap : (e + 1) * cap].astype(BF)
            return carry

        lax.fori_loop(0, width // tile, spread, 0)
    out_copies = [
        pltpu.make_async_copy(xs, x_all.at[step], sem_out.at[0]),
        pltpu.make_async_copy(ds, d_all.at[step], sem_out.at[1]),
        pltpu.make_async_copy(hid, hid_all.at[step], sem_out.at[2]),
        pltpu.make_async_copy(dgu, dgu_all.at[step], sem_out.at[3]),
    ]
    out_copies[0].start()
    out_copies[1].start()
    for copy in w_copies:
        copy.wait()

    def one_expert(e, carry):
        both = dot_rows(xs[e], gate_up[e])
        gate_pre, up_pre = both[:, :pad], both[:, pad:]
        d_hidden = dot_rows(ds[e], down[e])
        sigmoid = jax.nn.sigmoid(gate_pre)
        silu = gate_pre * sigmoid
        hid[e] = (silu * up_pre).astype(BF)
        gate_grad = d_hidden * up_pre * (sigmoid * (1.0 + gate_pre * (1.0 - sigmoid)))
        grads = jnp.concatenate([gate_grad, d_hidden * silu], axis=1).astype(BF)
        dgu[e] = grads

        def back(n, inner):
            cols = pl.ds(pl.multiple_of(n * tile, tile), tile)
            part = dot_plain(dgu[e], gate_up[e, :, cols]).astype(BF)
            for q in range(count):
                dxs[q, pl.ds(pl.multiple_of(e * cap, cap), cap), cols] = part[
                    q * cap : (q + 1) * cap
                ]
            return inner

        lax.fori_loop(0, width // tile, back, 0)
        return carry

    lax.fori_loop(0, experts, one_expert, 0)
    out_copies[2].start()
    out_copies[3].start()
    dx_copies = [
        pltpu.make_async_copy(dxo.at[q], dx_out[q // 2].at[q % 2], sem_dx.at[q])
        for q in range(count)
    ]
    for q in range(count):
        choose = jnp.where(select_cols(slot_col_ref[q], experts, cap), 1.0, 0.0).astype(BF)

        def gather(n, carry, q=q, choose=choose):
            cols = pl.ds(pl.multiple_of(n * tile, tile), tile)
            dxo[q, :, cols] = dot_plain(choose, dxs[q, :, cols]).astype(BF)
            return carry

        lax.fori_loop(0, width // tile, gather, 0)
        dx_copies[q].start()
    for copy in out_copies:
        copy.wait()
    for copy in dx_copies:
        copy.wait()


def expert_front(step, steps, x_parts, where, dy_all, gate_up, down, tables, kept, cap):
    experts, wide, width = gate_up.shape
    pad = wide // 2
    slots = QUARTET * cap
    slot_row, weight_row, slot_col = (t[step] for t in tables)
    any_spec = pl.BlockSpec(memory_space=pl.ANY)
    vmem_spec = pl.BlockSpec(memory_space=pltpu.VMEM)
    pair_shape = jax.ShapeDtypeStruct((2, HALF, width), BF)
    kept_shapes = [
        jax.ShapeDtypeStruct((steps, experts, slots, columns), BF)
        for columns in (width, width, pad, wide)
    ]
    results = pl.pallas_call(
        functools.partial(expert_front_kernel, step, experts, cap, len(kept)),
        out_shape=[pair_shape] * 2 + kept_shapes,
        in_specs=[any_spec] * QUARTET
        + [pl.BlockSpec(memory_space=pltpu.SMEM)]
        + [any_spec] * 3
        + [vmem_spec] * 3
        + [any_spec] * len(kept),
        out_specs=[any_spec] * 6,
        input_output_aliases={QUARTET + 7 + i: 2 + i for i in range(len(kept))},
        scratch_shapes=[
            pltpu.VMEM((QUARTET, HALF, width), BF),
            pltpu.VMEM((QUARTET, HALF, width), BF),
            pltpu.VMEM((experts, wide, width), BF),
            pltpu.VMEM((experts, pad, width), BF),
            pltpu.VMEM((experts, slots, width), BF),
            pltpu.VMEM((experts, slots, width), BF),
            pltpu.VMEM((QUARTET, experts * cap, width), BF),
            pltpu.VMEM((QUARTET, HALF, width), BF),
            pltpu.VMEM((experts, slots, pad), BF),
            pltpu.VMEM((experts, slots, wide), BF),
            pltpu.SemaphoreType.DMA((2 * QUARTET,)),
            pltpu.SemaphoreType.DMA((2,)),
            pltpu.SemaphoreType.DMA((4,)),
            pltpu.SemaphoreType.DMA((QUARTET,)),
        ],
        compiler_params=pltpu.CompilerParams(vmem_limit_bytes=62 * 1024 * 1024),
        cost_estimate=pl.CostEstimate(
            flops=2 * slots * experts * width * pad * 5
            + 6 * QUARTET * HALF * experts * cap * width,
            bytes_accessed=2 * width * (3 * QUARTET * HALF + experts * 3 * pad + 2 * experts * slots),
            transcendentals=slots * experts * pad,
        ),
        name="expert_front",
    )(*x_parts, where, dy_all, gate_up, down, slot_row, weight_row, slot_col, *kept)
    return list(results[:2]), list(results[2:])


def expert_out_kernel(experts, cap, hid, down, slot_row, weight_row, slot_col, near, far, parts):
    width = down.shape[2]
    tile = min(1024, width)
    weights = [
        slot_weights(
            select_rows(slot_row[0, q], experts, cap), weight_row[0, q], experts, cap
        )
        for q in range(QUARTET)
    ]
    for e in range(experts):

        def front(n, carry, e=e):
            cols = pl.ds(pl.multiple_of(n * tile, tile), tile)
            rows = dot_plain(hid[0, e], down[e, :, cols])
            for q in range(QUARTET):
                parts[q, e * cap : (e + 1) * cap, cols] = (
                    rows[q * cap : (q + 1) * cap] * weights[q][e * cap : (e + 1) * cap]
                ).astype(BF)
            return carry

        lax.fori_loop(0, width // tile, front, 0)
    for q in range(QUARTET):
        choose = jnp.where(select_cols(slot_col[0, q], experts, cap), 1.0, 0.0).astype(BF)
        out = (near, far)[q // 2]

        def gather(n, carry, q=q, choose=choose, out=out):
            cols = pl.ds(pl.multiple_of(n * tile, tile), tile)
            out[0, q % 2, :, cols] = dot_plain(choose, parts[q, :, cols]).astype(BF)
            return carry

        lax.fori_loop(0, width // tile, gather, 0)


def expert_out(hid_all, down, tables, cap):
    steps, experts, slots, pad = hid_all.shape
    width = down.shape[2]
    slot_row, weight_row, slot_col = tables
    return pl.pallas_call(
        functools.partial(expert_out_kernel, experts, cap),
        grid=(steps,),
        out_shape=[jax.ShapeDtypeStruct((steps, 2, HALF, width), BF)] * 2,
        in_specs=[
            pl.BlockSpec((1, experts, slots, pad), lambda i: (i, 0, 0, 0)),
            pl.BlockSpec((experts, pad, width), lambda i: (0, 0, 0)),
            pl.BlockSpec((1,) + slot_row.shape[1:], lambda i: (i, 0, 0, 0)),
            pl.BlockSpec((1,) + weight_row.shape[1:], lambda i: (i, 0, 0, 0)),
            pl.BlockSpec((1,) + slot_col.shape[1:], lambda i: (i, 0, 0, 0)),
        ],
        out_specs=[pl.BlockSpec((1, 2, HALF, width), lambda i: (i, 0, 0, 0))] * 2,
        scratch_shapes=[pltpu.VMEM((QUARTET, experts * cap, width), BF)],
        compiler_params=pltpu.CompilerParams(vmem_limit_bytes=48 * 1024 * 1024),
        cost_estimate=pl.CostEstimate(
            flops=steps * (2 * slots * experts * width * pad + 2 * QUARTET * HALF * experts * cap * width),
            bytes_accessed=2 * steps * QUARTET * HALF * width + 2 * hid_all.size + 2 * down.size,
            transcendentals=0,
        ),
        name="expert_out",
    )(hid_all, down, slot_row, weight_row, slot_col)


def expert_grads_kernel(dgu, x, hid, d, gate_grad, up_grad, down_grad):
    local = gate_grad.shape[1]
    pad = hid.shape[3]
    width = x.shape[3]
    tile = min(1024, width)

    @pl.when(pl.program_id(1) == 0)
    def _():
        gate_grad[...] = jnp.zeros_like(gate_grad)
        up_grad[...] = jnp.zeros_like(up_grad)
        down_grad[...] = jnp.zeros_like(down_grad)

    def part(n, carry):
        cols = pl.ds(pl.multiple_of(n * tile, tile), tile)
        gate_grad[0, :, cols] += dot_first(dgu[0, 0, :, :pad], x[0, 0, :, cols])[:local]
        up_grad[0, :, cols] += dot_first(dgu[0, 0, :, pad:], x[0, 0, :, cols])[:local]
        down_grad[0, :, cols] += dot_first(hid[0, 0], d[0, 0, :, cols])[:local]
        return carry

    lax.fori_loop(0, width // tile, part, 0)


def expert_grads(kept, local):
    x_all, d_all, hid_all, dgu_all = kept
    steps, experts, slots, width = x_all.shape
    pad = hid_all.shape[3]

    def block(array):
        return pl.BlockSpec((1, 1) + array.shape[2:], lambda e, i: (i, e, 0, 0))

    grad = jax.ShapeDtypeStruct((experts, local, width), F32)
    return pl.pallas_call(
        expert_grads_kernel,
        grid=(experts, steps),
        out_shape=[grad] * 3,
        in_specs=[block(dgu_all), block(x_all), block(hid_all), block(d_all)],
        out_specs=[pl.BlockSpec((1, local, width), lambda e, i: (e, 0, 0))] * 3,
        compiler_params=pltpu.CompilerParams(vmem_limit_bytes=48 * 1024 * 1024),
        cost_estimate=pl.CostEstimate(
            flops=2 * 3 * steps * experts * slots * width * pad,
            bytes_accessed=2 * (x_all.size + d_all.size + hid_all.size + dgu_all.size)
            + 12 * experts * local * width,
            transcendentals=0,
        ),
        name="expert_grads",
    )(dgu_all, x_all, hid_all, d_all)


def mesh_copy(src, dst, sends, arrivals, number, device):
    return pltpu.make_async_remote_copy(
        src_ref=src,
        dst_ref=dst,
        send_sem=sends.at[number],
        recv_sem=arrivals.at[number],
        device_id=device,
        device_id_type=pl.DeviceIdType.MESH,
    )


def plane_neighbours():
    place, column = lax.axis_index("fsdp"), lax.axis_index("tp")
    core, along, across = place % 2, (place // 2) % 2, place // 4
    return (
        (place + 1 - 2 * core, column),
        (place + 2 - 4 * along, column),
        (place + 4 - 8 * across, column),
    )


def column_neighbours(count):
    place, column = lax.axis_index("fsdp"), lax.axis_index("tp")
    return [(place, (column + s) % count) for s in range(1, count)]


def greet(devices):
    barrier = pltpu.get_barrier_semaphore()
    for device in devices:
        pl.semaphore_signal(
            barrier, inc=1, device_id=device, device_id_type=pl.DeviceIdType.MESH
        )
    pl.semaphore_wait(barrier, len(devices))


class PlaneGather:
    def __init__(self, own, others, size, sends, arrivals, base):
        self.own, self.others, self.size = own, others, size
        self.sends, self.arrivals, self.base = sends, arrivals, base
        self.partner, self.along, self.across = plane_neighbours()

    def copies(self, b):
        half = self.own.shape[1] // 2
        rows = pl.ds(b * self.size, self.size)
        left, right = pl.ds(0, half), pl.ds(half, half)
        other = {r: self.others.at[r - 1] for r in range(1, 8)}
        plan = [
            (self.own.at[rows], other[2].at[rows], self.along),
            (self.own.at[rows], other[4].at[rows], self.across),
            (self.own.at[rows], other[1].at[rows], self.partner),
            (other[2].at[rows, left], other[6].at[rows, left], self.across),
            (other[4].at[rows, right], other[6].at[rows, right], self.along),
            (other[2].at[rows], other[3].at[rows], self.partner),
            (other[4].at[rows], other[5].at[rows], self.partner),
            (other[6].at[rows], other[7].at[rows], self.partner),
        ]
        return [
            mesh_copy(src, dst, self.sends, self.arrivals, self.base + 8 * b + i, device)
            for i, (src, dst, device) in enumerate(plan)
        ]

    def start(self, b):
        for copy in self.copies(b)[:3]:
            copy.start()

    def forward(self, b):
        along, across, _, left, right, third, fifth, _ = self.copies(b)
        along.wait_recv()
        left.start()
        third.start()
        across.wait_recv()
        right.start()
        fifth.start()

    def last(self, b):
        copies = self.copies(b)
        copies[3].wait_recv()
        copies[4].wait_recv()
        copies[7].start()

    def arrived(self, b, numbers):
        copies = self.copies(b)
        for i in numbers:
            copies[i].wait_recv()

    def drain(self, b):
        for copy in self.copies(b):
            copy.wait_send()


def expert_kernel(experts, cap, columns, size, *refs):
    (
        attn_in,
        tokens_in,
        cotan_in,
        gate_up_in,
        down_in,
        gain_ref,
        slot_row_ref,
        weight_row_ref,
        slot_col_ref,
        mixed_out,
        ffn_all,
        dx_out,
        out_all,
        x_all,
        d_all,
        hid_all,
        dgu_all,
        x_others,
        dy_others,
        theirs,
        links,
        attn_v,
        tokens_v,
        arrived_v,
        mixed_v,
        ffn_v,
        xb,
        db,
        gate_up,
        down,
        xs,
        ds,
        dxs,
        others,
        chip,
        hid,
        dgu,
        stage,
        sends,
        arrivals,
        local,
        spill,
    ) = refs
    count = QUARTET
    width = xb.shape[2]
    half_width = width // 2
    pad = down.shape[1]
    tile = min(1024, width)
    blocks = columns
    partner, along, across = plane_neighbours()
    column = column_neighbours(columns)
    number = 0

    def reserve(amount):
        nonlocal number
        number += amount
        return number - amount

    x_gather = PlaneGather(ffn_all, x_others, size, sends, arrivals, reserve(8 * blocks))
    dy_gather = PlaneGather(cotan_in, dy_others, SEQ, sends, arrivals, reserve(8))
    rs_base, ag_base = reserve(columns - 1), reserve(columns - 1)
    pair_base, link_base = reserve(len(BOX_UNITS)), reserve(12)

    greet([partner, along, across] + column)
    sums = [
        mesh_copy(
            attn_in.at[pl.ds(s * size, size)],
            arrived_v.at[s - 1],
            sends,
            arrivals,
            rs_base + s - 1,
            column[s - 1],
        )
        for s in range(1, columns)
    ]
    for copy in sums:
        copy.start()
    first = [
        pltpu.make_async_copy(attn_in.at[pl.ds(0, size)], attn_v, local.at[0]),
        pltpu.make_async_copy(tokens_in, tokens_v, local.at[1]),
    ]
    for copy in first:
        copy.start()
    dy_gather.start(0)
    weights_in = [
        pltpu.make_async_copy(gate_up_in, gate_up, local.at[2]),
        pltpu.make_async_copy(down_in, down, local.at[3]),
    ]
    for copy in weights_in:
        copy.start()
    for copy in first:
        copy.wait()
    total = tokens_v[...].astype(F32) + attn_v[...].astype(F32)
    for s in range(1, columns):
        sums[s - 1].wait_recv()
        total = total + arrived_v[s - 1].astype(F32)
    mixed_v[...] = total
    inverse = lax.rsqrt(jnp.mean(total * total, axis=1, keepdims=True) + EPSILON)
    ffn_v[...] = (total * inverse * gain_ref[...]).astype(BF)
    own_copy = pltpu.make_async_copy(ffn_v, ffn_all.at[pl.ds(0, size)], local.at[0])
    own_copy.start()
    mixed_copy = pltpu.make_async_copy(mixed_v, mixed_out, local.at[1])
    mixed_copy.start()
    own_copy.wait()

    rows_out = [
        mesh_copy(
            ffn_all.at[pl.ds(0, size)],
            ffn_all.at[pl.ds((columns - s) * size, size)],
            sends,
            arrivals,
            ag_base + s - 1,
            column[s - 1],
        )
        for s in range(1, columns)
    ]
    for copy in rows_out:
        copy.start()
    x_gather.start(0)
    dy_gather.forward(0)
    for b in range(1, blocks):
        rows_out[columns - b - 1].wait_recv()
        x_gather.start(b)
        x_gather.forward(b - 1)
    for b in range(blocks):
        x_gather.arrived(b, [2])
    dy_gather.arrived(0, [2])

    def source(own, gathered, r):
        return own if r == 0 else gathered.at[r - 1]

    def load(unit):
        copies = []
        for q, (r, h) in enumerate(unit):
            rows = pl.ds(h * HALF, HALF)
            copies.append(
                pltpu.make_async_copy(
                    source(ffn_all, x_others, r).at[rows], xb.at[q], local.at[4 + q]
                )
            )
            copies.append(
                pltpu.make_async_copy(
                    source(cotan_in, dy_others, r).at[rows], db.at[q], local.at[8 + q]
                )
            )
        return copies

    def choose_cols(step, q):
        return jnp.where(select_cols(slot_col_ref[step, q], experts, cap), 1.0, 0.0).astype(BF)

    def combine(step, target):
        for q in range(count):
            choose = choose_cols(step, q)

            def gather(n, carry, q=q, choose=choose):
                cols = pl.ds(pl.multiple_of(n * tile, tile), tile)
                ref, place = target(q)
                ref[place + (slice(None), cols)] = dot_plain(choose, dxs[q, :, cols]).astype(BF)
                return carry

            lax.fori_loop(0, width // tile, gather, 0)

    def spills(step):
        return [
            pltpu.make_async_copy(xs, x_all.at[step], spill.at[0]),
            pltpu.make_async_copy(ds, d_all.at[step], spill.at[1]),
            pltpu.make_async_copy(hid.at[step], hid_all.at[step], spill.at[2]),
            pltpu.make_async_copy(dgu, dgu_all.at[step], spill.at[3]),
        ]

    def pair_copy(step):
        return mesh_copy(others, theirs.at[step], sends, arrivals, pair_base + step, partner)

    def front(step):
        copies = load(BOX_UNITS[step])
        for copy in copies:
            copy.start()
        if step == 0:
            for copy in weights_in:
                copy.wait()
        if step > 0:
            for copy in spills(step - 1):
                copy.wait()
        for q in range(count):
            copies[2 * q].wait()
            copies[2 * q + 1].wait()
            hit = select_rows(slot_row_ref[step, q], experts, cap)
            weights = slot_weights(hit, weight_row_ref[step, q], experts, cap)
            choose = jnp.where(hit, 1.0, 0.0).astype(BF)

            def spread(n, carry, q=q, choose=choose, weights=weights):
                cols = pl.ds(pl.multiple_of(n * tile, tile), tile)
                rows = dot_plain(choose, xb[q, :, cols])
                grads = dot_plain(choose, db[q, :, cols]) * weights
                for e in range(experts):
                    low, high = e * cap, (e + 1) * cap
                    xs[e, q * cap : (q + 1) * cap, cols] = rows[low:high].astype(BF)
                    ds[e, q * cap : (q + 1) * cap, cols] = grads[low:high].astype(BF)
                return carry

            lax.fori_loop(0, width // tile, spread, 0)
        out_copies = spills(step)
        out_copies[0].start()
        out_copies[1].start()

        def one_expert(e, carry):
            both = dot_rows(xs[e], gate_up[e])
            gate_pre, up_pre = both[:, :pad], both[:, pad:]
            d_hidden = dot_rows(ds[e], down[e])
            sigmoid = jax.nn.sigmoid(gate_pre)
            silu = gate_pre * sigmoid
            hid[step, e] = (silu * up_pre).astype(BF)
            gate_grad = d_hidden * up_pre * (sigmoid * (1.0 + gate_pre * (1.0 - sigmoid)))
            dgu[e] = jnp.concatenate([gate_grad, d_hidden * silu], axis=1).astype(BF)

            def back(n, inner):
                cols = pl.ds(pl.multiple_of(n * tile, tile), tile)
                part = dot_plain(dgu[e], gate_up[e, :, cols]).astype(BF)
                for q in range(count):
                    dxs[q, pl.ds(pl.multiple_of(e * cap, cap), cap), cols] = part[
                        q * cap : (q + 1) * cap
                    ]
                return inner

            lax.fori_loop(0, width // tile, back, 0)
            return carry

        lax.fori_loop(0, experts, one_expert, 0)
        out_copies[2].start()
        out_copies[3].start()
        if step > 0:
            pair_copy(step - 1).wait_send()
        combine(step, lambda q: (chip, (step, q)) if q < 2 else (others, (q - 2,)))
        pair_copy(step).start()

    def add_rows(step, q, cols, landed):
        fetch = pltpu.make_async_copy(landed, stage.at[:, cols], local.at[12])
        fetch.start()
        fetch.wait()

        def some(i, carry):
            rows = pl.ds(pl.multiple_of(i * 32, 32), 32)
            chip[step, q, rows, cols] = (
                chip[step, q, rows, cols].astype(F32) + stage[rows, cols].astype(F32)
            ).astype(BF)
            return carry

        lax.fori_loop(0, HALF // 32, some, 0)

    left, right = pl.ds(0, half_width), pl.ds(half_width, half_width)

    def chip_sum(step):
        pair_copy(step).wait_recv()
        for h in range(2):
            add_rows(step, h, pl.ds(0, width), theirs.at[step, h])

    def chip_place(r, h):
        step = [i for i, unit in enumerate(BOX_UNITS) if (r, h) in unit][0]
        return step, BOX_UNITS[step].index((r, h))

    def chip_rows(r, h):
        return chip.at[chip_place(r, h)]

    def link_copy(stage_number, side, h):
        first_hop, second_hop = (along, across) if side == 0 else (across, along)
        near, far = (2, 4) if side == 0 else (4, 2)
        r = (near, 6, far)[stage_number]
        device = second_hop if stage_number == 2 else first_hop
        i = (stage_number * 2 + side) * 2 + h
        return mesh_copy(
            chip.at[chip_place(r, h) + (pl.ds(0, HALF), (left, right)[side])],
            links.at[i],
            sends,
            arrivals,
            link_base + i,
            device,
        )

    def take_link(stage_number, side, h, r):
        link_copy(stage_number, side, h).wait_recv()
        i = (stage_number * 2 + side) * 2 + h
        add_rows(*chip_place(r, h), (left, right)[side], links.at[i])

    def out_part(step):
        weights = [
            slot_weights(
                select_rows(slot_row_ref[step, q], experts, cap),
                weight_row_ref[step, q],
                experts,
                cap,
            )
            for q in range(count)
        ]
        for e in range(experts):

            def one_tile(n, carry, e=e):
                cols = pl.ds(pl.multiple_of(n * tile, tile), tile)
                rows = dot_plain(hid[step, e], down[e, :, cols])
                for q in range(count):
                    dxs[q, e * cap : (e + 1) * cap, cols] = (
                        rows[q * cap : (q + 1) * cap] * weights[q][e * cap : (e + 1) * cap]
                    ).astype(BF)
                return carry

            lax.fori_loop(0, width // tile, one_tile, 0)
        if step > 0:
            out_copy(step - 1).wait()
        combine(step, lambda q: (db, (q,)))
        out_copy(step).start()

    def out_copy(step):
        return pltpu.make_async_copy(db, out_all.at[step], local.at[13])

    middle = blocks // 2
    front(0)
    x_gather.forward(blocks - 1)
    dy_gather.last(0)
    for b in range(middle):
        x_gather.arrived(b, [5, 6])
    dy_gather.arrived(0, [5, 6])
    front(1)
    for b in range(blocks):
        x_gather.last(b)
    for b in range(middle, blocks):
        x_gather.arrived(b, [5, 6])
    chip_sum(0)
    front(2)
    chip_sum(1)
    for side in range(2):
        link_copy(0, side, 0).start()
    for b in range(blocks):
        x_gather.arrived(b, [7])
    dy_gather.arrived(0, [7])
    front(3)
    chip_sum(2)
    for side in range(2):
        link_copy(0, side, 1).start()
    for copy in spills(3):
        copy.wait()
    out_part(0)
    chip_sum(3)
    for h in range(2):
        for side in range(2):
            link_copy(1, side, h).start()
    out_part(1)
    for h in range(2):
        for side in range(2):
            take_link(1, side, h, (4, 2)[side])
            link_copy(2, side, h).start()
    out_part(2)
    out_part(3)
    for h in range(2):
        for side in range(2):
            take_link(0, side, h, 0)
        for side in range(2):
            take_link(2, side, h, 0)
        done = pltpu.make_async_copy(
            chip_rows(0, h), dx_out.at[pl.ds(h * HALF, HALF)], local.at[14 + h]
        )
        done.start()
    for h in range(2):
        pltpu.make_async_copy(
            chip_rows(0, h), dx_out.at[pl.ds(h * HALF, HALF)], local.at[14 + h]
        ).wait()
    out_copy(3).wait()
    mixed_copy.wait()

    for b in range(blocks):
        x_gather.drain(b)
    dy_gather.drain(0)
    for copy in sums + rows_out:
        copy.wait_send()
    pair_copy(3).wait_send()
    for stage_number in range(3):
        for side in range(2):
            for h in range(2):
                link_copy(stage_number, side, h).wait_send()


def expert_call(attn_part, tokens, cotan_all, gate_up, down, gain, tables, cap):
    columns = lax.axis_size("tp")
    size, width = tokens.shape
    experts, wide, _ = gate_up.shape
    pad = wide // 2
    slots = QUARTET * cap
    steps = len(BOX_UNITS)
    anywhere = pl.BlockSpec(memory_space=pl.ANY)
    held = pl.BlockSpec(memory_space=pltpu.VMEM)

    def array(*dims, kind=BF):
        return jax.ShapeDtypeStruct(dims, kind)

    copies = 8 * columns + 8 + 2 * (columns - 1) + steps + 12
    results = pl.pallas_call(
        functools.partial(expert_kernel, experts, cap, columns, size),
        out_shape=[
            array(size, width, kind=F32),
            array(SEQ, width),
            array(SEQ, width),
            array(steps, QUARTET, HALF, width),
            array(steps, experts, slots, width),
            array(steps, experts, slots, width),
            array(steps, experts, slots, pad),
            array(steps, experts, slots, wide),
            array(7, SEQ, width),
            array(7, SEQ, width),
            array(steps, 2, HALF, width),
            array(12, HALF, width // 2),
        ],
        in_specs=[anywhere] * 5 + [held] * 4,
        out_specs=[anywhere] * 12,
        scratch_shapes=[
            pltpu.VMEM((size, width), BF),
            pltpu.VMEM((size, width), BF),
            pltpu.VMEM((columns - 1, size, width), BF),
            pltpu.VMEM((size, width), F32),
            pltpu.VMEM((size, width), BF),
            pltpu.VMEM((QUARTET, HALF, width), BF),
            pltpu.VMEM((QUARTET, HALF, width), BF),
            pltpu.VMEM((experts, wide, width), BF),
            pltpu.VMEM((experts, pad, width), BF),
            pltpu.VMEM((experts, slots, width), BF),
            pltpu.VMEM((experts, slots, width), BF),
            pltpu.VMEM((QUARTET, experts * cap, width), BF),
            pltpu.VMEM((2, HALF, width), BF),
            pltpu.VMEM((steps, 2, HALF, width), BF),
            pltpu.VMEM((steps, experts, slots, pad), BF),
            pltpu.VMEM((experts, slots, wide), BF),
            pltpu.VMEM((HALF, width), BF),
            pltpu.SemaphoreType.DMA((copies,)),
            pltpu.SemaphoreType.DMA((copies,)),
            pltpu.SemaphoreType.DMA((16,)),
            pltpu.SemaphoreType.DMA((4,)),
        ],
        compiler_params=pltpu.CompilerParams(
            collective_id=1, has_side_effects=True, vmem_limit_bytes=67_043_328
        ),
        cost_estimate=pl.CostEstimate(
            flops=steps
            * (2 * slots * experts * width * pad * 6 + 8 * QUARTET * HALF * experts * cap * width),
            bytes_accessed=60 * SEQ * width,
            transcendentals=0,
        ),
        name="experts",
    )(attn_part, tokens, cotan_all, gate_up, down, gain, *tables)
    return results[:8]


def first_kernel(columns, size, *refs):
    (
        tokens_in,
        packed_in,
        tokens_all,
        packed_all,
        tokens_v,
        packed_v,
        sends,
        arrivals,
        local,
    ) = refs
    partner, along, across = plane_neighbours()
    column = column_neighbours(columns)
    place = lax.axis_index("fsdp")
    rows = packed_in.shape[0]
    top, bottom = pl.ds(0, rows // 2), pl.ds(rows // 2, rows // 2)
    opposite = along[0] + across[0] - place
    greet([partner, along, across] + column)
    plan = [
        (packed_in, packed_all.at[place], along),
        (packed_in, packed_all.at[place], across),
        (packed_in, packed_all.at[place], partner),
        (packed_all.at[along[0], top], packed_all.at[along[0], top], across),
        (packed_all.at[across[0], bottom], packed_all.at[across[0], bottom], along),
        (packed_all.at[along[0]], packed_all.at[along[0]], partner),
        (packed_all.at[across[0]], packed_all.at[across[0]], partner),
        (packed_all.at[opposite], packed_all.at[opposite], partner),
    ]
    copies = [
        mesh_copy(src, dst, sends, arrivals, i, device) for i, (src, dst, device) in enumerate(plan)
    ]
    rows_out = [
        mesh_copy(
            tokens_in,
            tokens_all.at[pl.ds((columns - s) * size, size)],
            sends,
            arrivals,
            7 + s,
            column[s - 1],
        )
        for s in range(1, columns)
    ]
    for copy in copies[:3] + rows_out:
        copy.start()
    here = [
        pltpu.make_async_copy(tokens_in, tokens_v, local.at[0]),
        pltpu.make_async_copy(packed_in, packed_v, local.at[1]),
    ]
    for copy in here:
        copy.start()
    for copy in here:
        copy.wait()
    there = [
        pltpu.make_async_copy(tokens_v, tokens_all.at[pl.ds(0, size)], local.at[0]),
        pltpu.make_async_copy(packed_v, packed_all.at[place], local.at[1]),
    ]
    for copy in there:
        copy.start()
    copies[0].wait_recv()
    copies[3].start()
    copies[5].start()
    copies[1].wait_recv()
    copies[4].start()
    copies[6].start()
    copies[3].wait_recv()
    copies[4].wait_recv()
    copies[7].start()
    for i in (2, 5, 6, 7):
        copies[i].wait_recv()
    for copy in rows_out:
        copy.wait_recv()
    for copy in there:
        copy.wait()
    for copy in copies + rows_out:
        copy.wait_send()


def first_call(tokens, packed):
    columns = lax.axis_size("tp")
    size, width = tokens.shape
    anywhere = pl.BlockSpec(memory_space=pl.ANY)
    copies = 8 + columns - 1
    return pl.pallas_call(
        functools.partial(first_kernel, columns, size),
        out_shape=[
            jax.ShapeDtypeStruct((columns * size, width), BF),
            jax.ShapeDtypeStruct((8,) + packed.shape, BF),
        ],
        in_specs=[anywhere] * 2,
        out_specs=[anywhere] * 2,
        scratch_shapes=[
            pltpu.VMEM((size, width), BF),
            pltpu.VMEM(packed.shape, BF),
            pltpu.SemaphoreType.DMA((copies,)),
            pltpu.SemaphoreType.DMA((copies,)),
            pltpu.SemaphoreType.DMA((2,)),
        ],
        compiler_params=pltpu.CompilerParams(collective_id=2, has_side_effects=True),
        name="first_gather",
    )(tokens, packed)


class PlaneSum:
    def __init__(self, source, chip, theirs, links, stage, sends, arrivals, base, local):
        self.source, self.chip, self.theirs, self.links = source, chip, theirs, links
        self.stage, self.sends, self.arrivals, self.base = stage, sends, arrivals, base
        self.local = local
        self.parts, self.rows = chip.shape[1], chip.shape[2]
        self.partner, self.along, self.across = plane_neighbours()

    def pair(self, i, h):
        return mesh_copy(
            self.source(2 * i + 1, h),
            self.theirs.at[i, h],
            self.sends,
            self.arrivals,
            self.base + i * self.parts + h,
            self.partner,
        )

    def mine(self, i, h):
        return pltpu.make_async_copy(
            self.source(2 * i, h), self.chip.at[i, h], self.local.at[1 + i * self.parts + h]
        )

    def begin(self):
        for i in (3, 1, 2, 0):
            for h in range(self.parts):
                self.pair(i, h).start()
                self.mine(i, h).start()

    def add(self, i, h, start, size, landed):
        fetch = pltpu.make_async_copy(
            landed, self.stage.at[pl.ds(start, size)], self.local.at[0]
        )
        fetch.start()
        fetch.wait()
        some = min(32, size)

        def one(n, carry):
            rows = pl.ds(pl.multiple_of(start + n * some, some), some)
            self.chip[i, h, rows, :] = (
                self.chip[i, h, rows, :].astype(F32) + self.stage[rows, :].astype(F32)
            ).astype(BF)
            return carry

        lax.fori_loop(0, size // some, one, 0)

    def on_chip(self, i):
        for h in range(self.parts):
            self.mine(i, h).wait()
            self.pair(i, h).wait_recv()
            self.add(i, h, 0, self.rows, self.theirs.at[i, h])

    def link(self, stage_number, side, h):
        first_hop, second_hop = (
            (self.along, self.across) if side == 0 else (self.across, self.along)
        )
        near, far = (1, 2) if side == 0 else (2, 1)
        i = (near, 3, far)[stage_number]
        place = (stage_number * 2 + side) * self.parts + h
        rows = pl.ds(side * (self.rows // 2), self.rows // 2)
        return mesh_copy(
            self.chip.at[i, h, rows],
            self.links.at[place],
            self.sends,
            self.arrivals,
            self.base + 4 * self.parts + place,
            second_hop if stage_number == 2 else first_hop,
        )

    def take(self, stage_number, side, h, i):
        self.link(stage_number, side, h).wait_recv()
        place = (stage_number * 2 + side) * self.parts + h
        self.add(i, h, side * (self.rows // 2), self.rows // 2, self.links.at[place])

    def send_first(self):
        self.on_chip(3)
        self.send(1)
        self.on_chip(1)
        self.on_chip(2)
        self.send(0)
        self.on_chip(0)

    def send(self, stage_number):
        for h in range(self.parts):
            for side in range(2):
                self.link(stage_number, side, h).start()

    def send_second(self):
        for h in range(self.parts):
            for side in range(2):
                self.take(1, side, h, (2, 1)[side])
                self.link(2, side, h).start()

    def finish(self):
        for stage_number in (0, 2):
            for h in range(self.parts):
                for side in range(2):
                    self.take(stage_number, side, h, 0)

    def drain(self):
        for h in range(self.parts):
            for i in range(4):
                self.pair(i, h).wait_send()
            for stage_number in range(3):
                for side in range(2):
                    self.link(stage_number, side, h).wait_send()


def plane_sum_sizes(parts):
    return 10 * parts, 1 + 4 * parts


def plane_sum_space(parts, rows, width):
    landing = [
        jax.ShapeDtypeStruct((4, parts, rows, width), BF),
        jax.ShapeDtypeStruct((6 * parts, rows // 2, width), BF),
    ]
    scratch = [pltpu.VMEM((4, parts, rows, width), BF), pltpu.VMEM((rows, width), BF)]
    return landing, scratch


def middle_kernel(columns, size, experts, steps, local_hidden, *refs):
    (
        d_ffn_in,
        mixed_in,
        cotan_in,
        gain_ref,
        out_all,
        x_all,
        d_all,
        hid_all,
        dgu_all,
        d_mixed_out,
        d_proj_all,
        gain_out,
        routed_out,
        gate_grad,
        up_grad,
        down_grad,
        theirs,
        links,
        chip,
        stage,
        own_v,
        arrived_v,
        mixed_v,
        cotan_v,
        proj_v,
        xk,
        dk,
        hk,
        gk,
        totals,
        sends,
        arrivals,
        local,
        sum_local,
        work,
        written,
    ) = refs
    partner, along, across = plane_neighbours()
    column = column_neighbours(columns)
    greet([partner, along, across] + column)
    plane = PlaneSum(
        lambda r, h: out_all.at[
            [(s, unit.index((r, h))) for s, unit in enumerate(BOX_UNITS) if (r, h) in unit][0]
        ],
        chip,
        theirs,
        links,
        stage,
        sends,
        arrivals,
        0,
        sum_local,
    )
    base = plane_sum_sizes(2)[0]
    sums = [
        mesh_copy(
            d_ffn_in.at[pl.ds(s * size, size)],
            arrived_v.at[s - 1],
            sends,
            arrivals,
            base + s - 1,
            column[s - 1],
        )
        for s in range(1, columns)
    ]
    rows_out = [
        mesh_copy(
            d_proj_all.at[pl.ds(0, size)],
            d_proj_all.at[pl.ds((columns - s) * size, size)],
            sends,
            arrivals,
            base + columns - 1 + s - 1,
            column[s - 1],
        )
        for s in range(1, columns)
    ]
    for copy in sums:
        copy.start()
    first = [
        pltpu.make_async_copy(d_ffn_in.at[pl.ds(0, size)], own_v, local.at[0]),
        pltpu.make_async_copy(mixed_in, mixed_v, local.at[1]),
        pltpu.make_async_copy(cotan_in, cotan_v, local.at[2]),
    ]
    for copy in first:
        copy.start()
    plane.begin()

    width = xk.shape[2]
    pad = hk.shape[2]
    tile = min(1024, width)
    jobs = [(e, step) for e in range(experts) for step in range(steps)]

    def fetch(k):
        e, step = jobs[k]
        slot = k % 2
        return [
            pltpu.make_async_copy(x_all.at[step, e], xk.at[slot], work.at[slot, 0]),
            pltpu.make_async_copy(d_all.at[step, e], dk.at[slot], work.at[slot, 1]),
            pltpu.make_async_copy(hid_all.at[step, e], hk.at[slot], work.at[slot, 2]),
            pltpu.make_async_copy(dgu_all.at[step, e], gk.at[slot], work.at[slot, 3]),
        ]

    def write(e):
        return [
            pltpu.make_async_copy(
                totals.at[e % 2, i, pl.ds(0, local_hidden)], grad.at[e], written.at[e % 2, i]
            )
            for i, grad in enumerate((gate_grad, up_grad, down_grad))
        ]

    def job(k):
        e, step = jobs[k]
        slot, place = k % 2, e % 2
        if k + 1 < len(jobs):
            for copy in fetch(k + 1):
                copy.start()
        for copy in fetch(k):
            copy.wait()
        if step == 0 and e > 1:
            for copy in write(e - 2):
                copy.wait()

        def one(n, carry):
            cols = pl.ds(pl.multiple_of(n * tile, tile), tile)
            found = [
                dot_first(gk[slot, :, :pad], xk[slot, :, cols]),
                dot_first(gk[slot, :, pad:], xk[slot, :, cols]),
                dot_first(hk[slot], dk[slot, :, cols]),
            ]
            for i, value in enumerate(found):
                if step == 0:
                    totals[place, i, :, cols] = value
                else:
                    totals[place, i, :, cols] += value
            return carry

        lax.fori_loop(0, width // tile, one, 0)
        if step == steps - 1:
            for copy in write(e):
                copy.start()

    for copy in fetch(0):
        copy.start()
    early = len(jobs) // 2
    late = 3 * len(jobs) // 4
    for k in range(early):
        job(k)
    plane.send_first()
    for k in range(early, late):
        job(k)

    for copy in first:
        copy.wait()
    total = own_v[...].astype(F32)
    for s in range(1, columns):
        sums[s - 1].wait_recv()
        total = total + arrived_v[s - 1].astype(F32)
    mixed = mixed_v[...]
    inverse = lax.rsqrt(jnp.mean(mixed * mixed, axis=1, keepdims=True) + EPSILON)
    unit = mixed * inverse
    scaled = total * gain_ref[...]
    gain_out[...] = jnp.sum(total * unit, axis=0, keepdims=True)
    back = inverse * (scaled - unit * jnp.mean(scaled * unit, axis=1, keepdims=True))
    d_mixed = cotan_v[...].astype(F32) + back
    mixed_v[...] = d_mixed
    proj_v[...] = d_mixed.astype(BF)
    own_copy = pltpu.make_async_copy(proj_v, d_proj_all.at[pl.ds(0, size)], local.at[0])
    own_copy.start()
    mixed_copy = pltpu.make_async_copy(mixed_v, d_mixed_out, local.at[1])
    mixed_copy.start()
    own_copy.wait()
    for copy in rows_out:
        copy.start()
    for k in range(late, len(jobs)):
        job(k)
    plane.send_second()
    plane.finish()
    done = [
        pltpu.make_async_copy(
            chip.at[0, h], routed_out.at[pl.ds(h * HALF, HALF)], sum_local.at[1 + h]
        )
        for h in range(2)
    ]
    for copy in done:
        copy.start()
    for copy in rows_out:
        copy.wait_recv()
    for copy in done + [mixed_copy]:
        copy.wait()
    for e in range(max(0, experts - 2), experts):
        for copy in write(e):
            copy.wait()
    plane.drain()
    for copy in sums + rows_out:
        copy.wait_send()


def middle_call(d_ffn, mixed, cotan, gain, out_all, kept, local_hidden):
    columns = lax.axis_size("tp")
    size, width = cotan.shape
    x_all, d_all, hid_all, dgu_all = kept
    steps, experts, slots, pad = hid_all.shape
    anywhere = pl.BlockSpec(memory_space=pl.ANY)
    held = pl.BlockSpec(memory_space=pltpu.VMEM)
    landing, scratch = plane_sum_space(2, HALF, width)
    remote, near = plane_sum_sizes(2)
    remote = remote + 2 * (columns - 1)
    grad = jax.ShapeDtypeStruct((experts, local_hidden, width), F32)
    results = pl.pallas_call(
        functools.partial(middle_kernel, columns, size, experts, steps, local_hidden),
        out_shape=[
            jax.ShapeDtypeStruct((size, width), F32),
            jax.ShapeDtypeStruct((SEQ, width), BF),
            jax.ShapeDtypeStruct((1, width), F32),
            jax.ShapeDtypeStruct((SEQ, width), BF),
            grad,
            grad,
            grad,
        ]
        + landing,
        in_specs=[anywhere] * 3 + [held] + [anywhere] * 5,
        out_specs=[anywhere] * 2 + [held] + [anywhere] * 6,
        scratch_shapes=scratch
        + [
            pltpu.VMEM((size, width), BF),
            pltpu.VMEM((columns - 1, size, width), BF),
            pltpu.VMEM((size, width), F32),
            pltpu.VMEM((size, width), BF),
            pltpu.VMEM((size, width), BF),
            pltpu.VMEM((2, slots, width), BF),
            pltpu.VMEM((2, slots, width), BF),
            pltpu.VMEM((2, slots, pad), BF),
            pltpu.VMEM((2, slots, 2 * pad), BF),
            pltpu.VMEM((2, 3, pad, width), F32),
            pltpu.SemaphoreType.DMA((remote,)),
            pltpu.SemaphoreType.DMA((remote,)),
            pltpu.SemaphoreType.DMA((3,)),
            pltpu.SemaphoreType.DMA((near,)),
            pltpu.SemaphoreType.DMA((2, 4)),
            pltpu.SemaphoreType.DMA((2, 3)),
        ],
        compiler_params=pltpu.CompilerParams(
            collective_id=3, has_side_effects=True, vmem_limit_bytes=67_043_328
        ),
        cost_estimate=pl.CostEstimate(
            flops=2 * 3 * steps * experts * slots * width * pad,
            bytes_accessed=40 * SEQ * width,
            transcendentals=0,
        ),
        name="middle",
    )(d_ffn, mixed, cotan, gain, out_all, x_all, d_all, hid_all, dgu_all)
    return results[:7]


def last_kernel(columns, size, latent_start, latent_width, *refs):
    (
        d_normed_in,
        tokens_in,
        d_mixed_in,
        gain_ref,
        joint_in,
        up_in,
        out_in,
        sums_in,
        grad_out,
        joint_out,
        up_out,
        out_out,
        latent_out,
        sums_out,
        joint_theirs,
        joint_links,
        up_theirs,
        up_links,
        out_theirs,
        out_links,
        joint_chip,
        joint_stage,
        up_chip,
        up_stage,
        out_chip,
        out_stage,
        own_v,
        arrived_v,
        tokens_v,
        mixed_v,
        running,
        sums_v,
        latent_v,
        sends,
        arrivals,
        local,
        joint_local,
        up_local,
        out_local,
    ) = refs
    partner, along, across = plane_neighbours()
    column = column_neighbours(columns)
    place, row = lax.axis_index("fsdp"), lax.axis_index("tp")
    core, right, above = place % 2, (place // 2) % 2, place // 4

    def absolute(r):
        return (
            (above + r // 4) % 2 * 4 + (right + r // 2 % 2) % 2 * 2 + (core + r % 2) % 2
        )

    greet([partner, along, across] + column)
    each = plane_sum_sizes(1)[0]
    joint_rows, up_rows = joint_chip.shape[2], up_chip.shape[2]
    out_cols = out_chip.shape[3]

    def by_rows(ref, count):
        return lambda r, h: ref.at[pl.ds(pl.multiple_of(absolute(r) * count, count), count)]

    joint = PlaneSum(
        by_rows(joint_in, joint_rows),
        joint_chip,
        joint_theirs,
        joint_links,
        joint_stage,
        sends,
        arrivals,
        0,
        joint_local,
    )
    up = PlaneSum(
        by_rows(up_in, up_rows),
        up_chip,
        up_theirs,
        up_links,
        up_stage,
        sends,
        arrivals,
        each,
        up_local,
    )
    out = PlaneSum(
        lambda r, h: out_in.at[
            :, pl.ds(pl.multiple_of(absolute(r) * out_cols, out_cols), out_cols)
        ],
        out_chip,
        out_theirs,
        out_links,
        out_stage,
        sends,
        arrivals,
        2 * each,
        out_local,
    )
    base = 3 * each
    sums = [
        mesh_copy(
            d_normed_in.at[pl.ds(s * size, size)],
            arrived_v.at[s - 1],
            sends,
            arrivals,
            base + s - 1,
            column[s - 1],
        )
        for s in range(1, columns)
    ]
    base = base + columns - 1
    for copy in sums:
        copy.start()
    first = [
        pltpu.make_async_copy(d_normed_in.at[pl.ds(0, size)], own_v, local.at[0]),
        pltpu.make_async_copy(tokens_in, tokens_v, local.at[1]),
        pltpu.make_async_copy(d_mixed_in, mixed_v, local.at[2]),
        pltpu.make_async_copy(sums_in, running.at[0], local.at[3]),
    ]
    for copy in first:
        copy.start()
    for part in (out, joint, up):
        part.begin()
    first[3].wait()

    def small(i, device):
        return mesh_copy(running.at[i], sums_v.at[i], sends, arrivals, base + i, device)

    hops = [small(i, device) for i, device in enumerate((partner, along, across))]
    for i, copy in enumerate(hops):
        copy.start()
        copy.wait_recv()
        running[i + 1] = running[i] + sums_v[i]
    gains = [
        mesh_copy(running.at[3], sums_v.at[2 + s], sends, arrivals, base + 2 + s, column[s - 1])
        for s in range(1, columns)
    ]
    base = base + 2 + columns
    for copy in gains:
        copy.start()
    for part in (out, joint, up):
        part.send_first()
    for part in (out, joint, up):
        part.send_second()
    for part in (out, joint, up):
        part.finish()

    pieces = joint_rows // columns
    across_columns = [
        mesh_copy(
            joint_chip.at[
                0,
                0,
                pl.ds(pl.multiple_of((row + s) % columns * pieces, pieces), pieces),
                pl.ds(latent_start, latent_width),
            ],
            latent_v.at[s - 1],
            sends,
            arrivals,
            base + s - 1,
            column[s - 1],
        )
        for s in range(1, columns)
    ]
    for copy in across_columns:
        copy.start()
    done = [
        pltpu.make_async_copy(joint_chip.at[0, 0], joint_out, joint_local.at[1]),
        pltpu.make_async_copy(up_chip.at[0, 0], up_out, up_local.at[1]),
        pltpu.make_async_copy(out_chip.at[0, 0], out_out, out_local.at[1]),
    ]
    for copy in done:
        copy.start()

    for copy in first[:3]:
        copy.wait()
    total = own_v[...].astype(F32)
    for s in range(1, columns):
        sums[s - 1].wait_recv()
        total = total + arrived_v[s - 1].astype(F32)
    tokens = tokens_v[...].astype(F32)
    inverse = lax.rsqrt(jnp.mean(tokens * tokens, axis=1, keepdims=True) + EPSILON)
    unit = tokens * inverse
    scaled = total * gain_ref[...]
    mixed_v[...] = mixed_v[...] + inverse * (
        scaled - unit * jnp.mean(scaled * unit, axis=1, keepdims=True)
    )
    grad_copy = pltpu.make_async_copy(mixed_v, grad_out, local.at[0])
    grad_copy.start()
    gathered = running[3]
    for s in range(1, columns):
        gains[s - 1].wait_recv()
        gathered = gathered + sums_v[2 + s]
    sums_out[...] = gathered
    latent = joint_chip[
        0,
        0,
        pl.ds(pl.multiple_of(row * pieces, pieces), pieces),
        pl.ds(latent_start, latent_width),
    ].astype(F32)
    for s in range(1, columns):
        across_columns[s - 1].wait_recv()
        latent = latent + latent_v[s - 1].astype(F32)
    latent_out[...] = latent
    for copy in done + [grad_copy]:
        copy.wait()
    for part in (out, joint, up):
        part.drain()
    for copy in sums + hops + gains + across_columns:
        copy.wait_send()


def last_call(d_normed, tokens, d_mixed, gain, joint, up, out, sums, latent_start, latent_width):
    columns = lax.axis_size("tp")
    size, width = tokens.shape
    anywhere = pl.BlockSpec(memory_space=pl.ANY)
    held = pl.BlockSpec(memory_space=pltpu.VMEM)
    shapes = [
        (joint.shape[0] // 8, joint.shape[1]),
        (up.shape[0] // 8, up.shape[1]),
        (out.shape[0], out.shape[1] // 8),
    ]
    landing, scratch = [], []
    for rows, cols in shapes:
        one = plane_sum_space(1, rows, cols)
        landing, scratch = landing + one[0], scratch + one[1]
    remote, near = plane_sum_sizes(1)
    remote = 3 * remote + 3 * (columns - 1) + 3
    pieces = shapes[0][0] // columns
    return pl.pallas_call(
        functools.partial(last_kernel, columns, size, latent_start, latent_width),
        out_shape=[jax.ShapeDtypeStruct((size, width), F32)]
        + [jax.ShapeDtypeStruct(shape, BF) for shape in shapes]
        + [
            jax.ShapeDtypeStruct((pieces, latent_width), F32),
            jax.ShapeDtypeStruct(sums.shape, F32),
        ]
        + landing,
        in_specs=[anywhere] * 3 + [held] + [anywhere] * 4,
        out_specs=[anywhere] * 4 + [held] * 2 + [anywhere] * 6,
        scratch_shapes=scratch
        + [
            pltpu.VMEM((size, width), BF),
            pltpu.VMEM((columns - 1, size, width), BF),
            pltpu.VMEM((size, width), BF),
            pltpu.VMEM((size, width), F32),
            pltpu.VMEM((4,) + sums.shape, F32),
            pltpu.VMEM((2 + columns,) + sums.shape, F32),
            pltpu.VMEM((columns - 1, pieces, latent_width), BF),
            pltpu.SemaphoreType.DMA((remote,)),
            pltpu.SemaphoreType.DMA((remote,)),
            pltpu.SemaphoreType.DMA((4,)),
            pltpu.SemaphoreType.DMA((near,)),
            pltpu.SemaphoreType.DMA((near,)),
            pltpu.SemaphoreType.DMA((near,)),
        ],
        compiler_params=pltpu.CompilerParams(
            collective_id=4, has_side_effects=True, vmem_limit_bytes=48 * 1024 * 1024
        ),
        name="last_sums",
    )(d_normed, tokens, d_mixed, gain, joint, up, out, sums)[:6]


def plane_units(count):
    if count == 8:
        return BOX_UNITS
    return [[(2 * i + j // 2, j % 2) for j in range(4)] for i in range(count // 2)]


def plane_gather(rows, count):
    gathered = lax.all_gather(rows, "fsdp", axis=0)
    return {
        (r, h): gathered[r, h * HALF : (h + 1) * HALF] for r in range(count) for h in (0, 1)
    }


def plane_scatter_whole(pairs, units, count):
    parts = {}
    for unit, pair in zip(units, pairs):
        for q, key in enumerate(unit):
            parts[key] = pair[q // 2][q % 2]
    stacked = jnp.concatenate([parts[r, h] for r in range(count) for h in (0, 1)], axis=0)
    return lax.psum_scatter(stacked, "fsdp", scatter_dimension=0, tiled=True).astype(F32)


def sum_everywhere(values):
    for axis_name in ("fsdp", "tp"):
        count = lax.axis_size(axis_name)
        if is_power(count):
            bit = 1
            while bit < count:
                values = values + swap(values, axis_name, bit)
                bit *= 2
        else:
            values = lax.psum(values, axis_name)
    return values


def expert_tables(expert_ids, expert_wts, local_experts, units, cap):
    fsdp_count = lax.axis_size("fsdp")
    fsdp_rank = lax.axis_index("fsdp")
    tp_count = lax.axis_size("tp")
    expert_count = local_experts * fsdp_count
    places = (lax.axis_index("tp") + jnp.arange(tp_count, dtype=jnp.int32)) % tp_count

    def reorder(rows):
        return jnp.take(rows.reshape(tp_count, -1, TOPK), places, axis=0).reshape(SEQ, TOPK)

    expert_ids, expert_wts = reorder(expert_ids), reorder(expert_wts)
    names = jnp.arange(expert_count, dtype=jnp.int32)[:, None]
    member = jnp.zeros((expert_count, SEQ), jnp.bool_)
    weight = jnp.zeros((expert_count, SEQ), F32)
    ids_rows, wts_rows = expert_ids.T, expert_wts.T
    for pick in range(TOPK):
        same = ids_rows[pick : pick + 1] == names
        member = member | same
        weight = weight + jnp.where(same, wts_rows[pick : pick + 1], 0.0)
    position = jnp.arange(HALF)
    before = (position[:, None] < position[None, :]).astype(BF)
    rank = jnp.dot(
        member.astype(BF).reshape(expert_count * 2, HALF), before, preferred_element_type=F32
    ).reshape(expert_count, SEQ)
    slot = jnp.where(member, rank, NO_SLOT)
    table = jnp.concatenate([slot, weight], axis=0)
    if fsdp_count == 8:
        for bit in (1, 2, 4):
            table = jnp.concatenate([table, swap(table, "fsdp", bit)], axis=0)
    else:
        table = lax.all_gather(table, "fsdp", axis=0, tiled=True)
    table = table.reshape(fsdp_count, 2, fsdp_count, local_experts, 2, HALF)
    table = lax.dynamic_index_in_dim(table, fsdp_rank, axis=2, keepdims=False)
    slot_steps, weight_steps = [], []
    for unit in units:
        slot_steps.append(jnp.stack([table[r, 0, :, h] for r, h in unit]))
        weight_steps.append(jnp.stack([table[r, 1, :, h] for r, h in unit]))
    slot_row, weight_row = jnp.stack(slot_steps), jnp.stack(weight_steps)
    return (slot_row, weight_row, jnp.swapaxes(slot_row, 2, 3))


def per_device(
    block_in,
    out_cotan,
    segment_ids,
    expert_ids,
    expert_wts,
    attn_gain,
    query_proj,
    latent_proj,
    latent_gain,
    latent_up,
    out_proj,
    ffn_gain,
    shared_gate,
    shared_up,
    shared_down,
    routed_gate,
    routed_up,
    routed_down,
):
    tp_count = lax.axis_size("tp")
    fsdp_count = lax.axis_size("fsdp")
    tp_rank = lax.axis_index("tp")
    fsdp_rank = lax.axis_index("fsdp")
    tok_rows, model_width = block_in.shape
    local_experts, local_hidden = routed_gate.shape[:2]
    expert_count = local_experts * fsdp_count
    cap_rows = tok_rows * TOPK * 4 // (3 * expert_count)
    cap = cap_rows * (HALF // tok_rows)
    heads_local = H // tp_count
    head_width = NOPE + ROPE
    score_scale = head_width ** (-0.5)
    shard_rows, query_cols = query_proj.shape
    latent_cols = latent_proj.shape[1]
    up_cols = latent_up.shape[1]
    out_rows = out_proj.shape[0]
    units = plane_units(fsdp_count)

    joint = query_cols + latent_cols
    spare = (-joint) % 128
    spare = spare + 128 if spare < 3 else spare
    gains = jnp.concatenate(
        [
            attn_gain[:, None],
            ffn_gain[:, None],
            jnp.pad(latent_gain, (0, shard_rows - latent_gain.shape[0]))[:, None],
            jnp.zeros((shard_rows, spare - 3), BF),
        ],
        axis=1,
    )
    packed = jnp.concatenate(
        [query_proj, latent_proj, gains, latent_up.reshape(shard_rows, -1)], axis=1
    )
    lift_cols = packed.shape[1] - joint - spare
    paired = fsdp_count == 8
    if paired:
        tokens_all, packed_all = first_call(block_in, packed)
        packed_all = packed_all.reshape(-1, packed.shape[1])
    else:
        packed_all = lax.all_gather(packed, "fsdp", axis=0, tiled=True)
        tokens_all = column_gather(block_in)
    joint_weight = packed_all[:, :joint]
    gain_attn = packed_all[:, joint].astype(F32)
    gain_ffn = packed_all[:, joint + 1].astype(F32)
    gain_latent = (
        packed_all[:, joint + 2]
        .reshape(fsdp_count, shard_rows)[:, : latent_gain.shape[0]]
        .reshape(LAT)
        .astype(F32)
    )
    latent_up_weight = packed_all[:, joint + spare :].reshape(LAT, up_cols)
    out_weight = lax.all_gather(out_proj, "fsdp", axis=1, tiled=True)
    cotan_own, tokens_all = tie(out_cotan, tokens_all)
    cotan_all = column_gather(cotan_own)
    shared_weight = lax.all_gather(
        jnp.concatenate([shared_gate, shared_up], axis=1), "fsdp", axis=0, tiled=True
    )
    shared_down_weight = lax.all_gather(shared_down, "fsdp", axis=1, tiled=True)
    shared_cols = shared_gate.shape[1]
    tables = expert_tables(expert_ids, expert_wts, local_experts, units, cap)
    hidden_pad = -(-local_hidden // 128) * 128
    lift = ((0, 0), (0, hidden_pad - local_hidden), (0, 0))
    routed_gate_up = jnp.concatenate([jnp.pad(routed_gate, lift), jnp.pad(routed_up, lift)], axis=1)
    routed_down_pad = jnp.pad(routed_down, lift)

    unit_all, inverse_all = norm_parts(tokens_all.astype(F32))
    normed_all = (unit_all * gain_attn).astype(BF)
    joint_rows = jnp.dot(normed_all, joint_weight, preferred_element_type=F32)
    queries = joint_rows[:, :query_cols].reshape(SEQ, heads_local, head_width)
    latent = joint_rows[:, query_cols:]
    unit_lat, inverse_lat = norm_parts(latent[:, :LAT])
    places = (tp_rank + jnp.arange(tp_count, dtype=jnp.int32)) % tp_count
    positions = (
        places[:, None] * tok_rows + jnp.arange(tok_rows, dtype=jnp.int32)[None, :]
    ).reshape(SEQ)
    segments = jnp.take(segment_ids.reshape(tp_count, tok_rows), places, axis=0).reshape(SEQ)
    cosine, sine_part = rope_tables(positions, ROPE)
    compressed_all = (unit_lat * gain_latent).astype(BF)
    key_rope_all = rotate(latent[:, LAT:], cosine, sine_part).astype(BF)
    query_cat = jnp.concatenate(
        [
            queries[:, :, :NOPE],
            rotate(queries[:, :, NOPE:], cosine[:, None, :], sine_part[:, None, :]),
        ],
        axis=2,
    ).astype(BF)
    key_value = (
        jnp.dot(compressed_all, latent_up_weight, preferred_element_type=F32)
        .reshape(SEQ, heads_local, NOPE + DV)
        .astype(BF)
    )
    key_cat = jnp.concatenate(
        [
            key_value[:, :, :NOPE],
            jnp.broadcast_to(key_rope_all[:, None, :], (SEQ, heads_local, ROPE)),
        ],
        axis=2,
    )
    values = key_value[:, :, NOPE:]
    allowed = (positions[None, :] <= positions[:, None]) & (
        segments[None, :] == segments[:, None]
    )
    raw_scores = (
        jnp.einsum("qhd,khd->hqk", query_cat, key_cat, preferred_element_type=F32) * score_scale
    )
    masked = jnp.where(allowed[None], raw_scores, MASK_FILL)
    top_score = jnp.max(masked, axis=2, keepdims=True)
    exponent = jnp.exp(masked - top_score)
    row_total = jnp.sum(exponent, axis=2, keepdims=True)
    probabilities = exponent / row_total
    probs_low = probabilities.astype(BF)
    attended = (
        jnp.einsum("hqk,khd->qhd", probs_low, values, preferred_element_type=F32)
        .reshape(SEQ, heads_local * DV)
        .astype(BF)
    )
    attn_part = jnp.dot(attended, out_weight, preferred_element_type=F32).astype(BF)
    if paired:
        mixed_rows, normed_ffn_all, d_routed_in, out_array, *kept = expert_call(
            attn_part,
            block_in,
            cotan_all,
            routed_gate_up,
            routed_down_pad,
            gain_ffn[None, :],
            tables,
            cap,
        )
        unit_two, inverse_two = norm_parts(mixed_rows)
        d_routed_in = d_routed_in.astype(F32)
    else:
        mixed_rows = block_in.astype(F32) + column_scatter(attn_part)
        unit_two, inverse_two = norm_parts(mixed_rows)
        normed_ffn_all = column_gather((unit_two * gain_ffn).astype(BF))
        x_blocks = plane_gather(normed_ffn_all, fsdp_count)
        dy_all = lax.all_gather(cotan_all, "fsdp", axis=0, tiled=True)
        kept = []
        dx_pairs = []
        for step, unit in enumerate(units):
            pair, kept = expert_front(
                step,
                len(units),
                [x_blocks[key] for key in unit],
                jnp.array([2 * r + h for r, h in unit], jnp.int32),
                dy_all,
                routed_gate_up,
                routed_down_pad,
                tables,
                kept,
                cap,
            )
            dx_pairs.append(pair)
        near, far = expert_out(kept[2], routed_down_pad, tables, cap)
        d_routed_in = plane_scatter_whole(dx_pairs, units, fsdp_count)
    if not paired:
        routed_gate_grad, routed_up_grad, routed_down_grad = expert_grads(kept, local_hidden)

    shared_pre = jnp.dot(normed_ffn_all, shared_weight, preferred_element_type=F32)
    shared_gate_pre, shared_up_pre = shared_pre[:, :shared_cols], shared_pre[:, shared_cols:]
    shared_hidden = (jax.nn.silu(shared_gate_pre) * shared_up_pre).astype(BF)
    shared_rows = jnp.dot(shared_hidden, shared_down_weight, preferred_element_type=F32)
    shared_down_part = jnp.dot(shared_hidden.T, cotan_all, preferred_element_type=F32)
    d_shared_hidden = jnp.dot(cotan_all, shared_down_weight.T, preferred_element_type=F32)
    d_shared = jnp.concatenate(silu_back(d_shared_hidden, shared_gate_pre, shared_up_pre), axis=1)
    shared_part = jnp.dot(normed_ffn_all.T, d_shared, preferred_element_type=F32)
    d_shared_in = jnp.dot(d_shared, shared_weight.T, preferred_element_type=F32)

    if paired:
        d_ffn_rows, shared_part, shared_down_part = tie(
            (d_shared_in + d_routed_in).astype(BF),
            shared_part.astype(BF),
            shared_down_part.astype(BF),
        )
        (
            d_mixed,
            d_proj_all,
            ffn_gain_part,
            routed_rows,
            routed_gate_grad,
            routed_up_grad,
            routed_down_grad,
        ) = middle_call(
            d_ffn_rows, mixed_rows, out_cotan, gain_ffn[None, :], out_array, kept, local_hidden
        )
        ffn_gain_part = ffn_gain_part[0]
        routed_rows = routed_rows.astype(F32)
    else:
        d_normed_ffn = column_scatter(d_shared_in + d_routed_in)
        out_pairs = [(near[step], far[step]) for step in range(len(units))]
        routed_rows = plane_scatter_whole(out_pairs, units, fsdp_count)
        ffn_gain_part, d_mixed_norm = norm_back(d_normed_ffn, unit_two, inverse_two, gain_ffn)
        d_mixed = out_cotan.astype(F32) + d_mixed_norm
        d_proj_all = column_gather(d_mixed.astype(BF))
    ffn_rows = column_scatter(shared_rows + routed_rows)
    block_out = (mixed_rows + ffn_rows).astype(BF)

    out_part = jnp.dot(attended.T, d_proj_all, preferred_element_type=F32)
    d_attended = (
        jnp.dot(d_proj_all, out_weight.T, preferred_element_type=F32)
        .astype(BF)
        .reshape(SEQ, heads_local, DV)
    )
    prob_grad = jnp.einsum("qhd,khd->hqk", d_attended, values, preferred_element_type=F32)
    score_grad = (
        probabilities
        * (prob_grad - jnp.sum(probabilities * prob_grad, axis=2, keepdims=True))
    ).astype(BF)
    query_grad = (
        jnp.einsum("hqk,khd->qhd", score_grad, key_cat, preferred_element_type=F32) * score_scale
    )
    key_grad = (
        jnp.einsum("hqk,qhd->khd", score_grad, query_cat, preferred_element_type=F32) * score_scale
    )
    value_grad = jnp.einsum("hqk,qhd->khd", probs_low, d_attended, preferred_element_type=F32)
    d_queries = (
        jnp.concatenate(
            [
                query_grad[:, :, :NOPE],
                unrotate(query_grad[:, :, NOPE:], cosine[:, None, :], sine_part[:, None, :]),
            ],
            axis=2,
        )
        .reshape(SEQ, heads_local * head_width)
        .astype(BF)
    )
    d_key_value = (
        jnp.concatenate([key_grad[:, :, :NOPE], value_grad], axis=2)
        .reshape(SEQ, heads_local * (NOPE + DV))
        .astype(BF)
    )
    latent_up_part = jnp.dot(compressed_all.T, d_key_value, preferred_element_type=F32)
    d_compressed = jnp.dot(d_key_value, latent_up_weight.T, preferred_element_type=F32)
    d_key_rope = jnp.sum(key_grad[:, :, NOPE:], axis=1)
    latent_gain_part, d_latent_main = norm_back(d_compressed, unit_lat, inverse_lat, gain_latent)
    d_latent = jnp.concatenate(
        [d_latent_main, unrotate(d_key_rope, cosine, sine_part)], axis=1
    ).astype(BF)
    d_joint = jnp.concatenate([d_queries, d_latent], axis=1)
    joint_part = jnp.dot(normed_all.T, d_joint, preferred_element_type=F32)
    d_normed_part = jnp.dot(d_joint, joint_weight.T, preferred_element_type=F32)
    attn_gain_part = jnp.sum(d_normed_part * unit_all, axis=0)

    def scatter(part, dimension):
        return lax.psum_scatter(part.astype(BF), "fsdp", scatter_dimension=dimension, tiled=True)

    gain_parts = jnp.concatenate([attn_gain_part, latent_gain_part, ffn_gain_part]).reshape(
        -1, 128
    )
    joint_part = jnp.pad(joint_part.astype(BF), ((0, 0), (0, (-joint) % 128)))
    shared_down_grad = scatter(shared_down_part, 1)
    shared_grad = scatter(shared_part, 0)
    if paired:
        latent_width = joint_part.shape[1] - query_cols
        (
            block_in_grad,
            joint_grad,
            latent_up_grad,
            out_proj_grad,
            latent_proj_grad,
            gain_sums,
        ) = last_call(
            d_normed_part.astype(BF),
            block_in,
            d_mixed,
            gain_attn[None, :],
            joint_part,
            latent_up_part.astype(BF),
            out_part.astype(BF),
            gain_parts,
            query_cols,
            latent_width,
        )
        latent_proj_grad = latent_proj_grad[:, :latent_cols]
    else:
        d_normed = column_scatter(d_normed_part)
        unit_one, inverse_one = norm_parts(block_in.astype(F32))
        _, d_tokens_norm = norm_back(d_normed, unit_one, inverse_one, gain_attn)
        block_in_grad = d_mixed + d_tokens_norm
        out_proj_grad = scatter(out_part, 1)
        latent_up_grad = scatter(latent_up_part, 0)
        joint_grad = scatter(joint_part, 0)
        latent_grad = joint_grad[:, query_cols:joint].reshape(tp_count, -1, latent_cols)
        latent_proj_grad = column_scatter(
            jnp.take(latent_grad, places, axis=0).reshape(-1, latent_cols)
        )
        gain_sums = sum_everywhere(gain_parts)
    gain_sums = gain_sums.reshape(-1)
    query_proj_grad = joint_grad[:, :query_cols].astype(F32)
    latent_up_grad = latent_up_grad.astype(F32)
    out_proj_grad = out_proj_grad.astype(F32)
    shared_grad = shared_grad.astype(F32)
    shared_gate_grad, shared_up_grad = shared_grad[:, :shared_cols], shared_grad[:, shared_cols:]
    shared_down_grad = shared_down_grad.astype(F32)
    device = fsdp_rank * tp_count + tp_rank
    devices = tp_count * fsdp_count

    def own_gain(start, size):
        return lax.dynamic_slice(gain_sums, (start + device * (size // devices),), (size // devices,))

    attn_gain_grad = own_gain(0, model_width)
    latent_gain_grad = own_gain(model_width, LAT)
    ffn_gain_grad = own_gain(model_width + LAT, model_width)
    return (
        block_out,
        block_in_grad,
        attn_gain_grad,
        query_proj_grad,
        latent_proj_grad,
        latent_gain_grad,
        latent_up_grad,
        out_proj_grad,
        ffn_gain_grad,
        shared_gate_grad,
        shared_up_grad,
        shared_down_grad,
        routed_gate_grad,
        routed_up_grad,
        routed_down_grad,
    )


def solution(mesh):
    placed = (
        P(("fsdp", "tp"), None),
        P(("fsdp", "tp"), None),
        P("fsdp"),
        P("fsdp", None),
        P("fsdp", None),
        P("fsdp"),
        P("fsdp", "tp"),
        P("fsdp", None),
        P("fsdp"),
        P("fsdp", "tp"),
        P("tp", "fsdp"),
        P("fsdp"),
        P("fsdp", "tp"),
        P("fsdp", "tp"),
        P("tp", "fsdp"),
        P("fsdp", "tp", None),
        P("fsdp", "tp", None),
        P("fsdp", "tp", None),
    )
    return jax.shard_map(
        per_device,
        mesh=mesh,
        in_specs=placed,
        out_specs=(
            P(("fsdp", "tp"), None),
            P(("fsdp", "tp"), None),
            P(("fsdp", "tp")),
            P("fsdp", "tp"),
            P(("fsdp", "tp"), None),
            P(("fsdp", "tp")),
            P("fsdp", "tp"),
            P("tp", "fsdp"),
            P(("fsdp", "tp")),
            P("fsdp", "tp"),
            P("fsdp", "tp"),
            P("tp", "fsdp"),
            P("fsdp", "tp", None),
            P("fsdp", "tp", None),
            P("fsdp", "tp", None),
        ),
        check_vma=False,
    )
```

```python
import functools

import jax
import jax.numpy as jnp
from jax import lax
from jax.experimental import pallas as pl
from jax.experimental.pallas import tpu as pltpu
from jax.sharding import PartitionSpec as P

H = 16
NOPE = 128
ROPE = 64
DV = 128
LAT = 512
TOPK = 6
SEQ = 512
HALF = 256
QUARTET = 4
RAW_ROWS = 8


EPSILON = 1e-06
THETA_BASE = 10000.0
MASK_FILL = -1e30
NO_SLOT = -1e6

BF = jnp.bfloat16
F32 = jnp.float32


def rope_tables(positions, width_rope):
    middle = width_rope // 2
    frequency = THETA_BASE ** (-(jnp.arange(middle) * 2).astype(jnp.float32) / width_rope)
    angles = positions.astype(jnp.float32)[:, None] * frequency[None, :]
    return (jnp.cos(angles), jnp.sin(angles))


def rotate(values, cosine, sine_part):
    middle = values.shape[-1] // 2
    first_half = values[..., :middle]
    second_half = values[..., middle:]
    return jnp.concatenate(
        [
            first_half * cosine - second_half * sine_part,
            second_half * cosine + first_half * sine_part,
        ],
        axis=-1,
    )


def unrotate(values, cosine, sine_part):
    middle = values.shape[-1] // 2
    first_half = values[..., :middle]
    second_half = values[..., middle:]
    return jnp.concatenate(
        [
            first_half * cosine + second_half * sine_part,
            second_half * cosine - first_half * sine_part,
        ],
        axis=-1,
    )


def norm_parts(values):
    inverse = lax.rsqrt(jnp.mean(values * values, axis=-1, keepdims=True) + EPSILON)
    return (values * inverse, inverse)


def norm_back(upstream, unit_rows, inverse, scaling):
    scaled = upstream * scaling
    gain_grad = jnp.sum(upstream * unit_rows, axis=0)
    input_grad = inverse * (
        scaled - unit_rows * jnp.mean(scaled * unit_rows, axis=-1, keepdims=True)
    )
    return (gain_grad, input_grad)


def silu_back(grad_hidden, gate_pre, up_pre):
    sigmoid = jax.nn.sigmoid(gate_pre)
    gate_grad = grad_hidden * up_pre * (sigmoid * (1.0 + gate_pre * (1.0 - sigmoid)))
    up_grad = grad_hidden * (gate_pre * sigmoid)
    return (gate_grad.astype(jnp.bfloat16), up_grad.astype(jnp.bfloat16))


def is_power(count):
    return count & (count - 1) == 0


def swap(values, axis_name, bit):
    count = lax.axis_size(axis_name)
    return lax.ppermute(values, axis_name, [(i, i ^ bit) for i in range(count)])


def tie(*values):
    return lax.optimization_barrier(values)


def column_gather(rows):
    return lax.all_gather(rows, "tp", axis=0, tiled=True)


def column_scatter(values):
    return lax.psum_scatter(values.astype(BF), "tp", scatter_dimension=0, tiled=True).astype(F32)


def dot_rows(left, right):
    return lax.dot_general(left, right, (((1,), (1,)), ((), ())), preferred_element_type=F32)


def dot_plain(left, right):
    return lax.dot_general(left, right, (((1,), (0,)), ((), ())), preferred_element_type=F32)


def dot_first(left, right):
    return lax.dot_general(left, right, (((0,), (0,)), ((), ())), preferred_element_type=F32)


def select_rows(slot_rows, experts, cap):
    row = lax.broadcasted_iota(jnp.int32, (experts * cap, HALF), 0).astype(F32)
    hit = row == slot_rows[0:1, :]
    for e in range(1, experts):
        hit = hit | (row == slot_rows[e : e + 1, :] + float(e * cap))
    return hit


def select_cols(slot_cols, experts, cap):
    lane = lax.broadcasted_iota(jnp.int32, (HALF, experts * cap), 1).astype(F32)
    hit = lane == slot_cols[:, 0:1]
    for e in range(1, experts):
        hit = hit | (lane == slot_cols[:, e : e + 1] + float(e * cap))
    return hit


def slot_weights(hit, weight_rows, experts, cap):
    pieces = []
    for e in range(experts):
        part = hit[e * cap : (e + 1) * cap, :]
        pieces.append(
            jnp.sum(jnp.where(part, weight_rows[e : e + 1, :], 0.0), axis=1, keepdims=True)
        )
    return jnp.concatenate(pieces, axis=0)


def expert_front_kernel(step, experts, cap, aliased, *refs):
    count = QUARTET
    x_in = refs[:count]
    where_ref, dy_in, gate_up_in, down_in, slot_row_ref, weight_row_ref, slot_col_ref = refs[
        count : count + 7
    ]
    base = count + 7 + aliased
    dx_out = refs[base : base + 2]
    x_all, d_all, hid_all, dgu_all = refs[base + 2 : base + 6]
    (xb, db, gate_up, down, xs, ds, dxs, dxo, hid, dgu, sem_in, sem_w, sem_out, sem_dx) = refs[
        base + 6 :
    ]
    width = xb.shape[2]
    pad = down.shape[1]
    tile = min(1024, width)
    x_copies = [pltpu.make_async_copy(x_in[q], xb.at[q], sem_in.at[q]) for q in range(count)]
    d_copies = [
        pltpu.make_async_copy(
            dy_in.at[pl.ds(pl.multiple_of(where_ref[q] * HALF, HALF), HALF)],
            db.at[q],
            sem_in.at[count + q],
        )
        for q in range(count)
    ]
    w_copies = [
        pltpu.make_async_copy(gate_up_in, gate_up, sem_w.at[0]),
        pltpu.make_async_copy(down_in, down, sem_w.at[1]),
    ]
    for q in range(count):
        x_copies[q].start()
        d_copies[q].start()
    for copy in w_copies:
        copy.start()
    for q in range(count):
        x_copies[q].wait()
        d_copies[q].wait()

        hit = select_rows(slot_row_ref[q], experts, cap)
        weights = slot_weights(hit, weight_row_ref[q], experts, cap)
        choose = jnp.where(hit, 1.0, 0.0).astype(BF)

        def spread(n, carry, q=q, choose=choose, weights=weights):
            cols = pl.ds(pl.multiple_of(n * tile, tile), tile)
            rows = dot_plain(choose, xb[q, :, cols])
            grads = dot_plain(choose, db[q, :, cols]) * weights
            for e in range(experts):
                xs[e, q * cap : (q + 1) * cap, cols] = rows[e * cap : (e + 1) * cap].astype(BF)
                ds[e, q * cap : (q + 1) * cap, cols] = grads[e * cap : (e + 1) * cap].astype(BF)
            return carry

        lax.fori_loop(0, width // tile, spread, 0)
    out_copies = [
        pltpu.make_async_copy(xs, x_all.at[step], sem_out.at[0]),
        pltpu.make_async_copy(ds, d_all.at[step], sem_out.at[1]),
        pltpu.make_async_copy(hid, hid_all.at[step], sem_out.at[2]),
        pltpu.make_async_copy(dgu, dgu_all.at[step], sem_out.at[3]),
    ]
    out_copies[0].start()
    out_copies[1].start()
    for copy in w_copies:
        copy.wait()

    def one_expert(e, carry):
        both = dot_rows(xs[e], gate_up[e])
        gate_pre, up_pre = both[:, :pad], both[:, pad:]
        d_hidden = dot_rows(ds[e], down[e])
        sigmoid = jax.nn.sigmoid(gate_pre)
        silu = gate_pre * sigmoid
        hid[e] = (silu * up_pre).astype(BF)
        gate_grad = d_hidden * up_pre * (sigmoid * (1.0 + gate_pre * (1.0 - sigmoid)))
        grads = jnp.concatenate([gate_grad, d_hidden * silu], axis=1).astype(BF)
        dgu[e] = grads

        def back(n, inner):
            cols = pl.ds(pl.multiple_of(n * tile, tile), tile)
            part = dot_plain(dgu[e], gate_up[e, :, cols]).astype(BF)
            for q in range(count):
                dxs[q, pl.ds(pl.multiple_of(e * cap, cap), cap), cols] = part[
                    q * cap : (q + 1) * cap
                ]
            return inner

        lax.fori_loop(0, width // tile, back, 0)
        return carry

    lax.fori_loop(0, experts, one_expert, 0)
    out_copies[2].start()
    out_copies[3].start()
    dx_copies = [
        pltpu.make_async_copy(dxo.at[q], dx_out[q // 2].at[q % 2], sem_dx.at[q])
        for q in range(count)
    ]
    for q in range(count):
        choose = jnp.where(select_cols(slot_col_ref[q], experts, cap), 1.0, 0.0).astype(BF)

        def gather(n, carry, q=q, choose=choose):
            cols = pl.ds(pl.multiple_of(n * tile, tile), tile)
            dxo[q, :, cols] = dot_plain(choose, dxs[q, :, cols]).astype(BF)
            return carry

        lax.fori_loop(0, width // tile, gather, 0)
        dx_copies[q].start()
    for copy in out_copies:
        copy.wait()
    for copy in dx_copies:
        copy.wait()


def expert_front(step, steps, x_parts, where, dy_all, gate_up, down, tables, kept, cap):
    experts, wide, width = gate_up.shape
    pad = wide // 2
    slots = QUARTET * cap
    slot_row, weight_row, slot_col = (t[step] for t in tables)
    any_spec = pl.BlockSpec(memory_space=pl.ANY)
    vmem_spec = pl.BlockSpec(memory_space=pltpu.VMEM)
    pair_shape = jax.ShapeDtypeStruct((2, HALF, width), BF)
    kept_shapes = [
        jax.ShapeDtypeStruct((steps, experts, slots, columns), BF)
        for columns in (width, width, pad, wide)
    ]
    results = pl.pallas_call(
        functools.partial(expert_front_kernel, step, experts, cap, len(kept)),
        out_shape=[pair_shape] * 2 + kept_shapes,
        in_specs=[any_spec] * QUARTET
        + [pl.BlockSpec(memory_space=pltpu.SMEM)]
        + [any_spec] * 3
        + [vmem_spec] * 3
        + [any_spec] * len(kept),
        out_specs=[any_spec] * 6,
        input_output_aliases={QUARTET + 7 + i: 2 + i for i in range(len(kept))},
        scratch_shapes=[
            pltpu.VMEM((QUARTET, HALF, width), BF),
            pltpu.VMEM((QUARTET, HALF, width), BF),
            pltpu.VMEM((experts, wide, width), BF),
            pltpu.VMEM((experts, pad, width), BF),
            pltpu.VMEM((experts, slots, width), BF),
            pltpu.VMEM((experts, slots, width), BF),
            pltpu.VMEM((QUARTET, experts * cap, width), BF),
            pltpu.VMEM((QUARTET, HALF, width), BF),
            pltpu.VMEM((experts, slots, pad), BF),
            pltpu.VMEM((experts, slots, wide), BF),
            pltpu.SemaphoreType.DMA((2 * QUARTET,)),
            pltpu.SemaphoreType.DMA((2,)),
            pltpu.SemaphoreType.DMA((4,)),
            pltpu.SemaphoreType.DMA((QUARTET,)),
        ],
        compiler_params=pltpu.CompilerParams(vmem_limit_bytes=62 * 1024 * 1024),
        cost_estimate=pl.CostEstimate(
            flops=2 * slots * experts * width * pad * 5
            + 6 * QUARTET * HALF * experts * cap * width,
            bytes_accessed=2 * width * (3 * QUARTET * HALF + experts * 3 * pad + 2 * experts * slots),
            transcendentals=slots * experts * pad,
        ),
        name="expert_front",
    )(*x_parts, where, dy_all, gate_up, down, slot_row, weight_row, slot_col, *kept)
    return list(results[:2]), list(results[2:])


def expert_out_kernel(experts, cap, hid, down, slot_row, weight_row, slot_col, near, far, parts):
    width = down.shape[2]
    tile = min(1024, width)
    weights = [
        slot_weights(
            select_rows(slot_row[0, q], experts, cap), weight_row[0, q], experts, cap
        )
        for q in range(QUARTET)
    ]
    for e in range(experts):

        def front(n, carry, e=e):
            cols = pl.ds(pl.multiple_of(n * tile, tile), tile)
            rows = dot_plain(hid[0, e], down[e, :, cols])
            for q in range(QUARTET):
                parts[q, e * cap : (e + 1) * cap, cols] = (
                    rows[q * cap : (q + 1) * cap] * weights[q][e * cap : (e + 1) * cap]
                ).astype(BF)
            return carry

        lax.fori_loop(0, width // tile, front, 0)
    for q in range(QUARTET):
        choose = jnp.where(select_cols(slot_col[0, q], experts, cap), 1.0, 0.0).astype(BF)
        out = (near, far)[q // 2]

        def gather(n, carry, q=q, choose=choose, out=out):
            cols = pl.ds(pl.multiple_of(n * tile, tile), tile)
            out[0, q % 2, :, cols] = dot_plain(choose, parts[q, :, cols]).astype(BF)
            return carry

        lax.fori_loop(0, width // tile, gather, 0)


def expert_out(hid_all, down, tables, cap):
    steps, experts, slots, pad = hid_all.shape
    width = down.shape[2]
    slot_row, weight_row, slot_col = tables
    return pl.pallas_call(
        functools.partial(expert_out_kernel, experts, cap),
        grid=(steps,),
        out_shape=[jax.ShapeDtypeStruct((steps, 2, HALF, width), BF)] * 2,
        in_specs=[
            pl.BlockSpec((1, experts, slots, pad), lambda i: (i, 0, 0, 0)),
            pl.BlockSpec((experts, pad, width), lambda i: (0, 0, 0)),
            pl.BlockSpec((1,) + slot_row.shape[1:], lambda i: (i, 0, 0, 0)),
            pl.BlockSpec((1,) + weight_row.shape[1:], lambda i: (i, 0, 0, 0)),
            pl.BlockSpec((1,) + slot_col.shape[1:], lambda i: (i, 0, 0, 0)),
        ],
        out_specs=[pl.BlockSpec((1, 2, HALF, width), lambda i: (i, 0, 0, 0))] * 2,
        scratch_shapes=[pltpu.VMEM((QUARTET, experts * cap, width), BF)],
        compiler_params=pltpu.CompilerParams(vmem_limit_bytes=48 * 1024 * 1024),
        cost_estimate=pl.CostEstimate(
            flops=steps * (2 * slots * experts * width * pad + 2 * QUARTET * HALF * experts * cap * width),
            bytes_accessed=2 * steps * QUARTET * HALF * width + 2 * hid_all.size + 2 * down.size,
            transcendentals=0,
        ),
        name="expert_out",
    )(hid_all, down, slot_row, weight_row, slot_col)


def expert_grads_kernel(dgu, x, hid, d, gate_grad, up_grad, down_grad):
    local = gate_grad.shape[1]
    pad = hid.shape[3]
    width = x.shape[3]
    tile = min(1024, width)

    @pl.when(pl.program_id(1) == 0)
    def _():
        gate_grad[...] = jnp.zeros_like(gate_grad)
        up_grad[...] = jnp.zeros_like(up_grad)
        down_grad[...] = jnp.zeros_like(down_grad)

    def part(n, carry):
        cols = pl.ds(pl.multiple_of(n * tile, tile), tile)
        gate_grad[0, :, cols] += dot_first(dgu[0, 0, :, :pad], x[0, 0, :, cols])[:local]
        up_grad[0, :, cols] += dot_first(dgu[0, 0, :, pad:], x[0, 0, :, cols])[:local]
        down_grad[0, :, cols] += dot_first(hid[0, 0], d[0, 0, :, cols])[:local]
        return carry

    lax.fori_loop(0, width // tile, part, 0)


def expert_grads(kept, local):
    x_all, d_all, hid_all, dgu_all = kept
    steps, experts, slots, width = x_all.shape
    pad = hid_all.shape[3]

    def block(array):
        return pl.BlockSpec((1, 1) + array.shape[2:], lambda e, i: (i, e, 0, 0))

    grad = jax.ShapeDtypeStruct((experts, local, width), F32)
    return pl.pallas_call(
        expert_grads_kernel,
        grid=(experts, steps),
        out_shape=[grad] * 3,
        in_specs=[block(dgu_all), block(x_all), block(hid_all), block(d_all)],
        out_specs=[pl.BlockSpec((1, local, width), lambda e, i: (e, 0, 0))] * 3,
        compiler_params=pltpu.CompilerParams(vmem_limit_bytes=48 * 1024 * 1024),
        cost_estimate=pl.CostEstimate(
            flops=2 * 3 * steps * experts * slots * width * pad,
            bytes_accessed=2 * (x_all.size + d_all.size + hid_all.size + dgu_all.size)
            + 12 * experts * local * width,
            transcendentals=0,
        ),
        name="expert_grads",
    )(dgu_all, x_all, hid_all, d_all)


def mesh_copy(src, dst, sends, arrivals, number, device):
    return pltpu.make_async_remote_copy(
        src_ref=src,
        dst_ref=dst,
        send_sem=sends.at[number],
        recv_sem=arrivals.at[number],
        device_id=device,
        device_id_type=pl.DeviceIdType.MESH,
    )


def plane_neighbours():
    place, column = lax.axis_index("fsdp"), lax.axis_index("tp")
    core, along, across = place % 2, (place // 2) % 2, place // 4
    return (
        (place + 1 - 2 * core, column),
        (place + 2 - 4 * along, column),
        (place + 4 - 8 * across, column),
    )


def column_neighbours(count):
    place, column = lax.axis_index("fsdp"), lax.axis_index("tp")
    return [(place, (column + s) % count) for s in range(1, count)]


def greet(devices):
    barrier = pltpu.get_barrier_semaphore()
    for device in devices:
        pl.semaphore_signal(
            barrier, inc=1, device_id=device, device_id_type=pl.DeviceIdType.MESH
        )
    pl.semaphore_wait(barrier, len(devices))


class PlaneGather:
    def __init__(self, own, others, rows_of, sends, arrivals, base):
        self.own, self.others, self.rows_of = own, others, rows_of
        self.sends, self.arrivals, self.base = sends, arrivals, base
        self.partner, self.along, self.across = plane_neighbours()

    def copies(self, b):
        half = self.own.shape[1] // 2
        rows = self.rows_of(b)
        left, right = pl.ds(0, half), pl.ds(half, half)
        other = {r: self.others.at[r - 1] for r in range(1, 8)}
        plan = [
            (self.own.at[rows], other[2].at[rows], self.along),
            (self.own.at[rows], other[4].at[rows], self.across),
            (self.own.at[rows], other[1].at[rows], self.partner),
            (other[2].at[rows, left], other[6].at[rows, left], self.across),
            (other[4].at[rows, right], other[6].at[rows, right], self.along),
            (other[2].at[rows], other[3].at[rows], self.partner),
            (other[4].at[rows], other[5].at[rows], self.partner),
            (other[6].at[rows], other[7].at[rows], self.partner),
        ]
        return [
            mesh_copy(src, dst, self.sends, self.arrivals, self.base + 8 * b + i, device)
            for i, (src, dst, device) in enumerate(plan)
        ]

    def start(self, b):
        for copy in self.copies(b)[:3]:
            copy.start()

    def forward(self, b):
        along, across, _, left, right, third, fifth, _ = self.copies(b)
        along.wait_recv()
        left.start()
        third.start()
        across.wait_recv()
        right.start()
        fifth.start()

    def last(self, b):
        copies = self.copies(b)
        copies[3].wait_recv()
        copies[4].wait_recv()
        copies[7].start()

    def arrived(self, b, numbers):
        copies = self.copies(b)
        for i in numbers:
            copies[i].wait_recv()

    def drain(self, b):
        for copy in self.copies(b):
            copy.wait_send()


def block_rows(columns, size):
    row = lax.axis_index("tp")
    return lambda s: pl.ds(pl.multiple_of((row + s) % columns * size, size), size)


def expert_kernel(cap, columns, size, *refs):
    (
        attn_in,
        tokens_in,
        cotan_in,
        gate_in,
        up_in,
        down_in,
        gain_ref,
        raw_ref,
        mixed_out,
        ffn_all,
        dx_out,
        out_all,
        x_all,
        d_all,
        hid_all,
        dgu_all,
        x_others,
        dy_others,
        theirs,
        links,
        attn_v,
        tokens_v,
        arrived_v,
        mixed_v,
        ffn_v,
        xb,
        db,
        gate_up,
        down,
        xs,
        ds,
        dxs,
        others,
        chip,
        stage,
        hid,
        dgu,
        slot_table,
        weight_table,
        sends,
        arrivals,
        local,
        loads,
        sum_local,
        spill,
    ) = refs
    count = QUARTET
    experts, local_hidden = gate_in.shape[:2]
    width = xb.shape[2]
    pad = down.shape[1]
    tile = min(1024, width)
    wide = 2 * cap
    rows_of = block_rows(columns, size)
    partner, along, across = plane_neighbours()
    column = column_neighbours(columns)
    number = 0

    def reserve(amount):
        nonlocal number
        number += amount
        return number - amount

    x_gather = PlaneGather(ffn_all, x_others, rows_of, sends, arrivals, reserve(8 * columns))
    dy_gather = PlaneGather(
        cotan_in, dy_others, lambda b: pl.ds(0, SEQ), sends, arrivals, reserve(8)
    )
    rs_base, ag_base = reserve(columns - 1), reserve(columns - 1)
    plane = PlaneSum(
        lambda r, h: others.at[r // 2],
        chip,
        theirs,
        links,
        stage,
        sends,
        arrivals,
        reserve(plane_sum_sizes(columns)[0]),
        sum_local,
    )

    greet([partner, along, across] + column)
    sums = [
        mesh_copy(
            attn_in.at[rows_of(s)],
            arrived_v.at[s - 1],
            sends,
            arrivals,
            rs_base + s - 1,
            column[s - 1],
        )
        for s in range(1, columns)
    ]
    for copy in sums:
        copy.start()
    first = [
        pltpu.make_async_copy(attn_in.at[rows_of(0)], attn_v, local.at[0]),
        pltpu.make_async_copy(tokens_in, tokens_v, local.at[1]),
    ]
    for copy in first:
        copy.start()
    dy_gather.start(0)
    if pad > local_hidden:
        rest = pad - local_hidden
        for e in range(experts):
            for ref, start in ((gate_up, local_hidden), (gate_up, pad + local_hidden), (down, local_hidden)):
                ref[e, start : start + rest, :] = jnp.zeros((rest, width), BF)
    weights_in = []
    for e in range(experts):
        weights_in += [
            pltpu.make_async_copy(
                gate_in.at[e], gate_up.at[e, pl.ds(0, local_hidden)], local.at[2 + 3 * e]
            ),
            pltpu.make_async_copy(
                up_in.at[e], gate_up.at[e, pl.ds(pad, local_hidden)], local.at[3 + 3 * e]
            ),
            pltpu.make_async_copy(
                down_in.at[e], down.at[e, pl.ds(0, local_hidden)], local.at[4 + 3 * e]
            ),
        ]
    for copy in weights_in:
        copy.start()

    earlier = lax.broadcasted_iota(jnp.int32, (size, size), 0)
    later = lax.broadcasted_iota(jnp.int32, (size, size), 1)
    before = jnp.where(earlier < later, 1.0, 0.0).astype(BF)
    own_first = (lax.axis_index("fsdp") * experts).astype(F32)
    for r in range(8):
        for e in range(experts):
            member = jnp.zeros((1, SEQ), F32)
            weight = jnp.zeros((1, SEQ), F32)
            for pick in range(TOPK):
                same = raw_ref[r, pick : pick + 1, :] == own_first + float(e)
                member = jnp.where(same, 1.0, member)
                weight = weight + jnp.where(
                    same, raw_ref[r, RAW_ROWS + pick : RAW_ROWS + pick + 1, :], 0.0
                )
            slot_table[r * experts + e : r * experts + e + 1, :] = member
            weight_table[r * experts + e : r * experts + e + 1, :] = weight
    second = lax.broadcasted_iota(jnp.int32, (8 * experts, size), 0) // experts % 2
    shift = second.astype(F32) * float(cap)
    for b in range(columns):
        cols = pl.ds(b * size, size)
        member = slot_table[:, cols]
        rank = dot_plain(member.astype(BF), before)
        slot_table[:, cols] = jnp.where(member > 0.5, rank + shift, NO_SLOT)

    for copy in first:
        copy.wait()
    total = tokens_v[...].astype(F32) + attn_v[...].astype(F32)
    for s in range(1, columns):
        sums[s - 1].wait_recv()
        total = total + arrived_v[s - 1].astype(F32)
    mixed_v[...] = total
    inverse = lax.rsqrt(jnp.mean(total * total, axis=1, keepdims=True) + EPSILON)
    ffn_v[...] = (total * inverse * gain_ref[...]).astype(BF)
    own_copy = pltpu.make_async_copy(ffn_v, ffn_all.at[rows_of(0)], local.at[0])
    own_copy.start()
    mixed_copy = pltpu.make_async_copy(mixed_v, mixed_out, local.at[1])
    mixed_copy.start()
    own_copy.wait()

    rows_out = [
        mesh_copy(
            ffn_all.at[rows_of(0)],
            ffn_all.at[rows_of(0)],
            sends,
            arrivals,
            ag_base + s - 1,
            column[s - 1],
        )
        for s in range(1, columns)
    ]
    for copy in rows_out:
        copy.start()

    def enter(b):
        if b > 0:
            rows_out[columns - b - 1].wait_recv()
        x_gather.start(b)

    def ready(b):
        x_gather.arrived(b, [2, 5, 6, 7])

    def source(own, gathered, r):
        return own if r == 0 else gathered.at[r - 1]

    def load(b):
        copies = []
        for r in range(8):
            place = pl.ds(r % 2 * size, size)
            for k, (own, gathered, target) in enumerate(
                ((ffn_all, x_others, xb), (cotan_in, dy_others, db))
            ):
                copies.append(
                    pltpu.make_async_copy(
                        source(own, gathered, r).at[rows_of(b)],
                        target.at[r // 2, place],
                        loads.at[2 * r + k],
                    )
                )
        return copies

    def slots_of(table, b, q):
        place = pl.ds(pl.multiple_of((lax.axis_index("tp") + b) % columns * size, size), size)
        rows = []
        for e in range(experts):
            low, high = 2 * q * experts + e, (2 * q + 1) * experts + e
            rows.append(
                jnp.concatenate([table[low : low + 1, place], table[high : high + 1, place]], axis=1)
            )
        return jnp.concatenate(rows, axis=0)

    def combine(b, keep):
        for q in range(count):
            entries = slots_of(slot_table, b, q)
            entries = jnp.concatenate(
                [entries, jnp.full((8 - experts, HALF), NO_SLOT, F32)], axis=0
            )
            hit = select_cols(entries.T, experts, wide)
            choose = jnp.where(hit, 1.0, 0.0).astype(BF)

            def gather(n, carry, q=q, choose=choose):
                cols = pl.ds(pl.multiple_of(n * tile, tile), tile)
                keep(q, cols, dot_plain(choose, dxs[q, :, cols]).astype(BF))
                return carry

            lax.fori_loop(0, width // tile, gather, 0)

    def spills(b):
        return [
            pltpu.make_async_copy(xs, x_all.at[b], spill.at[0]),
            pltpu.make_async_copy(ds, d_all.at[b], spill.at[1]),
            pltpu.make_async_copy(hid.at[b], hid_all.at[b], spill.at[2]),
            pltpu.make_async_copy(dgu, dgu_all.at[b], spill.at[3]),
        ]

    def front(b):
        copies = load(b)
        for copy in copies:
            copy.start()
        if b == 0:
            for copy in weights_in:
                copy.wait()
        if b > 0:
            for copy in spills(b - 1):
                copy.wait()
        for q in range(count):
            for copy in copies[4 * q : 4 * q + 4]:
                copy.wait()
            hit = select_rows(slots_of(slot_table, b, q), experts, wide)
            weights = slot_weights(hit, slots_of(weight_table, b, q), experts, wide)
            choose = jnp.where(hit, 1.0, 0.0).astype(BF)

            def spread(n, carry, q=q, choose=choose, weights=weights):
                cols = pl.ds(pl.multiple_of(n * tile, tile), tile)
                rows = dot_plain(choose, xb[q, :, cols])
                grads = dot_plain(choose, db[q, :, cols]) * weights
                for e in range(experts):
                    low, high = e * wide, (e + 1) * wide
                    xs[e, q * wide : (q + 1) * wide, cols] = rows[low:high].astype(BF)
                    ds[e, q * wide : (q + 1) * wide, cols] = grads[low:high].astype(BF)
                return carry

            lax.fori_loop(0, width // tile, spread, 0)
        out_copies = spills(b)
        out_copies[0].start()
        out_copies[1].start()

        def one_expert(e, carry):
            both = dot_rows(xs[e], gate_up[e])
            gate_pre, up_pre = both[:, :pad], both[:, pad:]
            d_hidden = dot_rows(ds[e], down[e])
            sigmoid = jax.nn.sigmoid(gate_pre)
            silu = gate_pre * sigmoid
            hid[b, e] = (silu * up_pre).astype(BF)
            gate_grad = d_hidden * up_pre * (sigmoid * (1.0 + gate_pre * (1.0 - sigmoid)))
            dgu[e] = jnp.concatenate([gate_grad, d_hidden * silu], axis=1).astype(BF)

            def back(n, inner):
                cols = pl.ds(pl.multiple_of(n * tile, tile), tile)
                part = dot_plain(dgu[e], gate_up[e, :, cols]).astype(BF)
                for q in range(count):
                    dxs[q, pl.ds(pl.multiple_of(e * wide, wide), wide), cols] = part[
                        q * wide : (q + 1) * wide
                    ]
                return inner

            lax.fori_loop(0, width // tile, back, 0)
            return carry

        lax.fori_loop(0, experts, one_expert, 0)
        out_copies[2].start()
        out_copies[3].start()
        if b > 0:
            for i in range(4):
                plane.pair(i, b - 1).wait_send()

        def keep(q, cols, value):
            chip[q, b, :, cols] = value[:size]
            others[q, :, cols] = value[size:]

        combine(b, keep)
        for i in range(4):
            plane.pair(i, b).start()

    def out_part(b):
        weights = [
            slot_weights(
                select_rows(slots_of(slot_table, b, q), experts, wide),
                slots_of(weight_table, b, q),
                experts,
                wide,
            )
            for q in range(count)
        ]
        for e in range(experts):

            def one_tile(n, carry, e=e):
                cols = pl.ds(pl.multiple_of(n * tile, tile), tile)
                rows = dot_plain(hid[b, e], down[e, :, cols])
                for q in range(count):
                    dxs[q, e * wide : (e + 1) * wide, cols] = (
                        rows[q * wide : (q + 1) * wide] * weights[q][e * wide : (e + 1) * wide]
                    ).astype(BF)
                return carry

            lax.fori_loop(0, width // tile, one_tile, 0)
        if b > 0:
            out_copy(b - 1).wait()

        def keep(q, cols, value):
            db[q, :, cols] = value

        combine(b, keep)
        out_copy(b).start()

    def out_copy(b):
        return pltpu.make_async_copy(db, out_all.at[b], local.at[0])

    def send_sums(b):
        plane.on_chip(3, [b], False)
        plane.send(1, [b])
        plane.on_chip(1, [b], False)
        plane.on_chip(2, [b], False)
        plane.send(0, [b])
        plane.on_chip(0, [b], False)

    final = columns - 1
    enter(0)
    dy_gather.forward(0)
    enter(1)
    x_gather.forward(0)
    enter(2)
    x_gather.forward(1)
    x_gather.last(0)
    dy_gather.last(0)
    ready(0)
    dy_gather.arrived(0, [2, 5, 6, 7])
    front(0)
    for b in range(3, columns):
        enter(b)
    x_gather.forward(2)
    x_gather.last(1)
    ready(1)
    front(1)
    for b in range(2, columns):
        if b > 2:
            x_gather.forward(b)
        x_gather.last(b)
        ready(b)
        send_sums(b - 2)
        if b > 2:
            plane.send_second([b - 3])
        front(b)
    send_sums(final - 1)
    plane.send_second([final - 2])
    for copy in spills(final):
        copy.wait()
    out_part(0)
    send_sums(final)
    plane.send_second([final - 1])
    out_part(1)
    plane.send_second([final])
    for b in range(2, columns):
        out_part(b)
    plane.finish(range(columns))
    done = [
        pltpu.make_async_copy(chip.at[0, b], dx_out.at[rows_of(b)], loads.at[b])
        for b in range(columns)
    ]
    for copy in done:
        copy.start()
    for copy in done:
        copy.wait()
    out_copy(final).wait()
    mixed_copy.wait()

    for b in range(columns):
        x_gather.drain(b)
    dy_gather.drain(0)
    for copy in sums + rows_out:
        copy.wait_send()
    plane.drain(final)


def expert_call(attn_part, tokens, cotan_all, gate, up, down, gain, raw, cap):
    columns = lax.axis_size("tp")
    size, width = tokens.shape
    experts, local_hidden, _ = gate.shape
    pad = -(-local_hidden // 128) * 128
    slots = 8 * cap
    anywhere = pl.BlockSpec(memory_space=pl.ANY)
    held = pl.BlockSpec(memory_space=pltpu.VMEM)

    def array(*dims, kind=BF):
        return jax.ShapeDtypeStruct(dims, kind)

    landing, scratch = plane_sum_space(columns, size, width)
    remote, near = plane_sum_sizes(columns)
    remote = remote + 8 * columns + 8 + 2 * (columns - 1)
    results = pl.pallas_call(
        functools.partial(expert_kernel, cap, columns, size),
        out_shape=[
            array(size, width, kind=F32),
            array(SEQ, width),
            array(SEQ, width),
            array(columns, QUARTET, HALF, width),
            array(columns, experts, slots, width),
            array(columns, experts, slots, width),
            array(columns, experts, slots, pad),
            array(columns, experts, slots, 2 * pad),
            array(7, SEQ, width),
            array(7, SEQ, width),
        ]
        + landing,
        in_specs=[anywhere] * 6 + [held] * 2,
        out_specs=[anywhere] * 12,
        scratch_shapes=[
            pltpu.VMEM((size, width), BF),
            pltpu.VMEM((size, width), BF),
            pltpu.VMEM((columns - 1, size, width), BF),
            pltpu.VMEM((size, width), F32),
            pltpu.VMEM((size, width), BF),
            pltpu.VMEM((QUARTET, HALF, width), BF),
            pltpu.VMEM((QUARTET, HALF, width), BF),
            pltpu.VMEM((experts, 2 * pad, width), BF),
            pltpu.VMEM((experts, pad, width), BF),
            pltpu.VMEM((experts, slots, width), BF),
            pltpu.VMEM((experts, slots, width), BF),
            pltpu.VMEM((QUARTET, 2 * experts * cap, width), BF),
            pltpu.VMEM((4, size, width), BF),
        ]
        + scratch
        + [
            pltpu.VMEM((columns, experts, slots, pad), BF),
            pltpu.VMEM((experts, slots, 2 * pad), BF),
            pltpu.VMEM((8 * experts, SEQ), F32),
            pltpu.VMEM((8 * experts, SEQ), F32),
            pltpu.SemaphoreType.DMA((remote,)),
            pltpu.SemaphoreType.DMA((remote,)),
            pltpu.SemaphoreType.DMA((2 + 3 * experts,)),
            pltpu.SemaphoreType.DMA((16,)),
            pltpu.SemaphoreType.DMA((near,)),
            pltpu.SemaphoreType.DMA((4,)),
        ],
        compiler_params=pltpu.CompilerParams(
            collective_id=1, has_side_effects=True, vmem_limit_bytes=67_043_328
        ),
        cost_estimate=pl.CostEstimate(
            flops=16 * SEQ * experts * cap * width * 8,
            bytes_accessed=60 * SEQ * width,
            transcendentals=0,
        ),
        name="experts",
    )(attn_part, tokens, cotan_all, gate, up, down, gain, raw)
    return results[:8]


def first_kernel(columns, size, kinds, *refs):
    amount = len(kinds)
    tokens_in, own_in = refs[0], refs[1 : 1 + amount]
    tokens_all, alls = refs[1 + amount], refs[2 + amount : 2 + 2 * amount]
    tokens_v, held = refs[2 + 2 * amount], refs[3 + 2 * amount : 3 + 3 * amount]
    sends, arrivals, local = refs[3 + 3 * amount :]
    partner, along, across = plane_neighbours()
    column = column_neighbours(columns)
    rows_of = block_rows(columns, size)
    place = lax.axis_index("fsdp")
    devices = {
        0: place,
        1: partner[0],
        2: along[0],
        4: across[0],
        6: along[0] + across[0] - place,
    }
    greet([partner, along, across] + column)
    rows_out = [
        mesh_copy(
            tokens_in,
            tokens_all.at[rows_of(0)],
            sends,
            arrivals,
            8 * amount + s - 1,
            column[s - 1],
        )
        for s in range(1, columns)
    ]
    for copy in rows_out:
        copy.start()
    plans = []
    for k, kind in enumerate(kinds):
        own, everything = own_in[k], alls[k]
        rows, cols = own.shape
        top, bottom = pl.ds(0, rows // 2), pl.ds(rows // 2, rows // 2)
        whole = pl.ds(0, rows)

        def spot(r, hop, part, kind=kind, everything=everything, cols=cols):
            if kind == "relative":
                return everything.at[r ^ hop, part]
            if kind == "rows":
                return everything.at[devices[r], part]
            start = pl.multiple_of(devices[r] * cols, cols)
            return everything.at[part, pl.ds(start, cols)]

        plan = [
            (own, spot(0, 2, whole), along),
            (own, spot(0, 4, whole), across),
            (own, spot(0, 1, whole), partner),
            (spot(2, 0, top), spot(2, 4, top), across),
            (spot(4, 0, bottom), spot(4, 2, bottom), along),
            (spot(2, 0, whole), spot(2, 1, whole), partner),
            (spot(4, 0, whole), spot(4, 1, whole), partner),
            (spot(6, 0, whole), spot(6, 1, whole), partner),
        ]
        plans.append(
            [
                mesh_copy(src, dst, sends, arrivals, 8 * k + i, device)
                for i, (src, dst, device) in enumerate(plan)
            ]
        )
    for copies in plans:
        for copy in copies[:3]:
            copy.start()
    here = [pltpu.make_async_copy(tokens_in, tokens_v, local.at[0])]
    there = [pltpu.make_async_copy(tokens_v, tokens_all.at[rows_of(0)], local.at[0])]
    for k, kind in enumerate(kinds):
        rows, cols = own_in[k].shape
        if kind == "relative":
            spot_here = alls[k].at[0]
        elif kind == "rows":
            spot_here = alls[k].at[place]
        else:
            spot_here = alls[k].at[:, pl.ds(pl.multiple_of(place * cols, cols), cols)]
        here.append(pltpu.make_async_copy(own_in[k], held[k], local.at[1 + k]))
        there.append(pltpu.make_async_copy(held[k], spot_here, local.at[1 + k]))
    for copy in here:
        copy.start()
    for copy in here:
        copy.wait()
    for copy in there:
        copy.start()
    for copies in plans:
        copies[0].wait_recv()
        copies[3].start()
        copies[5].start()
        copies[1].wait_recv()
        copies[4].start()
        copies[6].start()
    for copies in plans:
        copies[3].wait_recv()
        copies[4].wait_recv()
        copies[7].start()
    for copies in plans:
        for i in (2, 5, 6, 7):
            copies[i].wait_recv()
    for copy in rows_out:
        copy.wait_recv()
    for copy in there:
        copy.wait()
    for copies in plans + [rows_out]:
        for copy in copies:
            copy.wait_send()


def first_call(tokens, owns, kinds):
    columns = lax.axis_size("tp")
    size, width = tokens.shape
    anywhere = pl.BlockSpec(memory_space=pl.ANY)
    copies = 8 * len(owns) + columns - 1

    def gathered(own, kind):
        rows, cols = own.shape
        return (rows, 8 * cols) if kind == "columns" else (8, rows, cols)

    return pl.pallas_call(
        functools.partial(first_kernel, columns, size, kinds),
        out_shape=[jax.ShapeDtypeStruct((columns * size, width), BF)]
        + [jax.ShapeDtypeStruct(gathered(own, kind), own.dtype) for own, kind in zip(owns, kinds)],
        in_specs=[anywhere] * (1 + len(owns)),
        out_specs=[anywhere] * (1 + len(owns)),
        scratch_shapes=[pltpu.VMEM((size, width), BF)]
        + [pltpu.VMEM(own.shape, own.dtype) for own in owns]
        + [
            pltpu.SemaphoreType.DMA((copies,)),
            pltpu.SemaphoreType.DMA((copies,)),
            pltpu.SemaphoreType.DMA((1 + len(owns),)),
        ],
        compiler_params=pltpu.CompilerParams(collective_id=2, has_side_effects=True),
        name="first_gather",
    )(tokens, *owns)


class PlaneSum:
    def __init__(self, source, chip, theirs, links, stage, sends, arrivals, base, local):
        self.source, self.chip, self.theirs, self.links = source, chip, theirs, links
        self.stage, self.sends, self.arrivals, self.base = stage, sends, arrivals, base
        self.local = local
        self.parts, self.rows = chip.shape[1], chip.shape[2]
        self.partner, self.along, self.across = plane_neighbours()

    def pair(self, i, h):
        return mesh_copy(
            self.source(2 * i + 1, h),
            self.theirs.at[i, h],
            self.sends,
            self.arrivals,
            self.base + i * self.parts + h,
            self.partner,
        )

    def mine(self, i, h):
        return pltpu.make_async_copy(
            self.source(2 * i, h), self.chip.at[i, h], self.local.at[1 + i * self.parts + h]
        )

    def begin(self):
        for i in (3, 1, 2, 0):
            for h in range(self.parts):
                self.pair(i, h).start()
                self.mine(i, h).start()

    def add(self, i, h, start, size, landed):
        fetch = pltpu.make_async_copy(
            landed, self.stage.at[pl.ds(start, size)], self.local.at[0]
        )
        fetch.start()
        fetch.wait()
        some = min(32, size)

        def one(n, carry):
            rows = pl.ds(pl.multiple_of(start + n * some, some), some)
            self.chip[i, h, rows, :] = (
                self.chip[i, h, rows, :].astype(F32) + self.stage[rows, :].astype(F32)
            ).astype(BF)
            return carry

        lax.fori_loop(0, size // some, one, 0)

    def on_chip(self, i, parts=None, fetched=True):
        for h in range(self.parts) if parts is None else parts:
            if fetched:
                self.mine(i, h).wait()
            self.pair(i, h).wait_recv()
            self.add(i, h, 0, self.rows, self.theirs.at[i, h])

    def link(self, stage_number, side, h):
        first_hop, second_hop = (
            (self.along, self.across) if side == 0 else (self.across, self.along)
        )
        near, far = (1, 2) if side == 0 else (2, 1)
        i = (near, 3, far)[stage_number]
        place = (stage_number * 2 + side) * self.parts + h
        rows = pl.ds(side * (self.rows // 2), self.rows // 2)
        return mesh_copy(
            self.chip.at[i, h, rows],
            self.links.at[place],
            self.sends,
            self.arrivals,
            self.base + 4 * self.parts + place,
            second_hop if stage_number == 2 else first_hop,
        )

    def take(self, stage_number, side, h, i):
        self.link(stage_number, side, h).wait_recv()
        place = (stage_number * 2 + side) * self.parts + h
        self.add(i, h, side * (self.rows // 2), self.rows // 2, self.links.at[place])

    def send_first(self):
        self.on_chip(3)
        self.send(1)
        self.on_chip(1)
        self.on_chip(2)
        self.send(0)
        self.on_chip(0)

    def send(self, stage_number, parts=None):
        for h in range(self.parts) if parts is None else parts:
            for side in range(2):
                self.link(stage_number, side, h).start()

    def send_second(self, parts=None):
        for h in range(self.parts) if parts is None else parts:
            for side in range(2):
                self.take(1, side, h, (2, 1)[side])
                self.link(2, side, h).start()

    def finish(self, parts=None):
        for h in range(self.parts) if parts is None else parts:
            for stage_number in (0, 2):
                for side in range(2):
                    self.take(stage_number, side, h, 0)

    def drain(self, first_part=0):
        for h in range(self.parts):
            for i in range(4):
                if h >= first_part:
                    self.pair(i, h).wait_send()
            for stage_number in range(3):
                for side in range(2):
                    self.link(stage_number, side, h).wait_send()


def plane_sum_sizes(parts):
    return 10 * parts, 1 + 4 * parts


def plane_sum_space(parts, rows, width):
    landing = [
        jax.ShapeDtypeStruct((4, parts, rows, width), BF),
        jax.ShapeDtypeStruct((6 * parts, rows // 2, width), BF),
    ]
    scratch = [pltpu.VMEM((4, parts, rows, width), BF), pltpu.VMEM((rows, width), BF)]
    return landing, scratch


def middle_kernel(columns, size, experts, steps, local_hidden, *refs):
    (
        d_ffn_in,
        mixed_in,
        cotan_in,
        gain_ref,
        out_all,
        x_all,
        d_all,
        hid_all,
        dgu_all,
        d_mixed_out,
        d_proj_all,
        gain_out,
        routed_out,
        gate_grad,
        up_grad,
        down_grad,
        theirs,
        links,
        chip,
        stage,
        own_v,
        arrived_v,
        mixed_v,
        cotan_v,
        proj_v,
        xk,
        dk,
        hk,
        gk,
        totals,
        sends,
        arrivals,
        local,
        sum_local,
        work,
        written,
    ) = refs
    partner, along, across = plane_neighbours()
    column = column_neighbours(columns)
    greet([partner, along, across] + column)
    plane = PlaneSum(
        lambda r, h: out_all.at[h, r // 2, pl.ds(r % 2 * size, size)],
        chip,
        theirs,
        links,
        stage,
        sends,
        arrivals,
        0,
        sum_local,
    )
    base = plane_sum_sizes(columns)[0]
    rows_of = block_rows(columns, size)
    sums = [
        mesh_copy(
            d_ffn_in.at[rows_of(s)],
            arrived_v.at[s - 1],
            sends,
            arrivals,
            base + s - 1,
            column[s - 1],
        )
        for s in range(1, columns)
    ]
    rows_out = [
        mesh_copy(
            d_proj_all.at[rows_of(0)],
            d_proj_all.at[rows_of(0)],
            sends,
            arrivals,
            base + columns - 1 + s - 1,
            column[s - 1],
        )
        for s in range(1, columns)
    ]
    for copy in sums:
        copy.start()
    first = [
        pltpu.make_async_copy(d_ffn_in.at[rows_of(0)], own_v, local.at[0]),
        pltpu.make_async_copy(mixed_in, mixed_v, local.at[1]),
        pltpu.make_async_copy(cotan_in, cotan_v, local.at[2]),
    ]
    for copy in first:
        copy.start()
    plane.begin()

    width = xk.shape[2]
    pad = hk.shape[2]
    tile = min(1024, width)
    jobs = [(e, step) for e in range(experts) for step in range(steps)]

    def fetch(k):
        e, step = jobs[k]
        slot = k % 2
        return [
            pltpu.make_async_copy(x_all.at[step, e], xk.at[slot], work.at[slot, 0]),
            pltpu.make_async_copy(d_all.at[step, e], dk.at[slot], work.at[slot, 1]),
            pltpu.make_async_copy(hid_all.at[step, e], hk.at[slot], work.at[slot, 2]),
            pltpu.make_async_copy(dgu_all.at[step, e], gk.at[slot], work.at[slot, 3]),
        ]

    def write(e):
        return [
            pltpu.make_async_copy(
                totals.at[e % 2, i, pl.ds(0, local_hidden)], grad.at[e], written.at[e % 2, i]
            )
            for i, grad in enumerate((gate_grad, up_grad, down_grad))
        ]

    def job(k):
        e, step = jobs[k]
        slot, place = k % 2, e % 2
        if k + 1 < len(jobs):
            for copy in fetch(k + 1):
                copy.start()
        for copy in fetch(k):
            copy.wait()
        if step == 0 and e > 1:
            for copy in write(e - 2):
                copy.wait()

        def one(n, carry):
            cols = pl.ds(pl.multiple_of(n * tile, tile), tile)
            found = [
                dot_first(gk[slot, :, :pad], xk[slot, :, cols]),
                dot_first(gk[slot, :, pad:], xk[slot, :, cols]),
                dot_first(hk[slot], dk[slot, :, cols]),
            ]
            for i, value in enumerate(found):
                if step == 0:
                    totals[place, i, :, cols] = value
                else:
                    totals[place, i, :, cols] += value
            return carry

        lax.fori_loop(0, width // tile, one, 0)
        if step == steps - 1:
            for copy in write(e):
                copy.start()

    for copy in fetch(0):
        copy.start()
    early = len(jobs) // 2
    late = 3 * len(jobs) // 4
    for k in range(early):
        job(k)
    plane.send_first()
    for k in range(early, late):
        job(k)

    for copy in first:
        copy.wait()
    total = own_v[...].astype(F32)
    for s in range(1, columns):
        sums[s - 1].wait_recv()
        total = total + arrived_v[s - 1].astype(F32)
    mixed = mixed_v[...]
    inverse = lax.rsqrt(jnp.mean(mixed * mixed, axis=1, keepdims=True) + EPSILON)
    unit = mixed * inverse
    scaled = total * gain_ref[...]
    gain_out[...] = jnp.sum(total * unit, axis=0, keepdims=True)
    back = inverse * (scaled - unit * jnp.mean(scaled * unit, axis=1, keepdims=True))
    d_mixed = cotan_v[...].astype(F32) + back
    mixed_v[...] = d_mixed
    proj_v[...] = d_mixed.astype(BF)
    own_copy = pltpu.make_async_copy(proj_v, d_proj_all.at[rows_of(0)], local.at[0])
    own_copy.start()
    mixed_copy = pltpu.make_async_copy(mixed_v, d_mixed_out, local.at[1])
    mixed_copy.start()
    own_copy.wait()
    for copy in rows_out:
        copy.start()
    for k in range(late, len(jobs)):
        job(k)
    plane.send_second()
    plane.finish()
    done = [
        pltpu.make_async_copy(chip.at[0, h], routed_out.at[rows_of(h)], sum_local.at[1 + h])
        for h in range(columns)
    ]
    for copy in done:
        copy.start()
    for copy in rows_out:
        copy.wait_recv()
    for copy in done + [mixed_copy]:
        copy.wait()
    for e in range(max(0, experts - 2), experts):
        for copy in write(e):
            copy.wait()
    plane.drain()
    for copy in sums + rows_out:
        copy.wait_send()


def middle_call(d_ffn, mixed, cotan, gain, out_all, kept, local_hidden):
    columns = lax.axis_size("tp")
    size, width = cotan.shape
    x_all, d_all, hid_all, dgu_all = kept
    steps, experts, slots, pad = hid_all.shape
    anywhere = pl.BlockSpec(memory_space=pl.ANY)
    held = pl.BlockSpec(memory_space=pltpu.VMEM)
    landing, scratch = plane_sum_space(columns, size, width)
    remote, near = plane_sum_sizes(columns)
    remote = remote + 2 * (columns - 1)
    grad = jax.ShapeDtypeStruct((experts, local_hidden, width), F32)
    results = pl.pallas_call(
        functools.partial(middle_kernel, columns, size, experts, steps, local_hidden),
        out_shape=[
            jax.ShapeDtypeStruct((size, width), F32),
            jax.ShapeDtypeStruct((SEQ, width), BF),
            jax.ShapeDtypeStruct((1, width), F32),
            jax.ShapeDtypeStruct((SEQ, width), BF),
            grad,
            grad,
            grad,
        ]
        + landing,
        in_specs=[anywhere] * 3 + [held] + [anywhere] * 5,
        out_specs=[anywhere] * 2 + [held] + [anywhere] * 6,
        scratch_shapes=scratch
        + [
            pltpu.VMEM((size, width), BF),
            pltpu.VMEM((columns - 1, size, width), BF),
            pltpu.VMEM((size, width), F32),
            pltpu.VMEM((size, width), BF),
            pltpu.VMEM((size, width), BF),
            pltpu.VMEM((2, slots, width), BF),
            pltpu.VMEM((2, slots, width), BF),
            pltpu.VMEM((2, slots, pad), BF),
            pltpu.VMEM((2, slots, 2 * pad), BF),
            pltpu.VMEM((2, 3, pad, width), F32),
            pltpu.SemaphoreType.DMA((remote,)),
            pltpu.SemaphoreType.DMA((remote,)),
            pltpu.SemaphoreType.DMA((3,)),
            pltpu.SemaphoreType.DMA((near,)),
            pltpu.SemaphoreType.DMA((2, 4)),
            pltpu.SemaphoreType.DMA((2, 3)),
        ],
        compiler_params=pltpu.CompilerParams(
            collective_id=3, has_side_effects=True, vmem_limit_bytes=67_043_328
        ),
        cost_estimate=pl.CostEstimate(
            flops=2 * 3 * steps * experts * slots * width * pad,
            bytes_accessed=40 * SEQ * width,
            transcendentals=0,
        ),
        name="middle",
    )(d_ffn, mixed, cotan, gain, out_all, x_all, d_all, hid_all, dgu_all)
    return results[:7]


def last_kernel(columns, size, latent_start, latent_width, *refs):
    (
        d_normed_in,
        tokens_in,
        d_mixed_in,
        gain_ref,
        joint_in,
        up_in,
        out_in,
        sums_in,
        grad_out,
        joint_out,
        up_out,
        out_out,
        latent_out,
        sums_out,
        joint_theirs,
        joint_links,
        up_theirs,
        up_links,
        out_theirs,
        out_links,
        joint_chip,
        joint_stage,
        up_chip,
        up_stage,
        out_chip,
        out_stage,
        own_v,
        arrived_v,
        tokens_v,
        mixed_v,
        running,
        sums_v,
        latent_v,
        sends,
        arrivals,
        local,
        joint_local,
        up_local,
        out_local,
    ) = refs
    partner, along, across = plane_neighbours()
    column = column_neighbours(columns)
    place, row = lax.axis_index("fsdp"), lax.axis_index("tp")
    core, right, above = place % 2, (place // 2) % 2, place // 4

    def absolute(r):
        return (
            (above + r // 4) % 2 * 4 + (right + r // 2 % 2) % 2 * 2 + (core + r % 2) % 2
        )

    greet([partner, along, across] + column)
    each = plane_sum_sizes(1)[0]
    joint_rows, up_rows = joint_chip.shape[2], up_chip.shape[2]
    out_cols = out_chip.shape[3]

    def by_rows(ref, count):
        return lambda r, h: ref.at[pl.ds(pl.multiple_of(absolute(r) * count, count), count)]

    joint = PlaneSum(
        by_rows(joint_in, joint_rows),
        joint_chip,
        joint_theirs,
        joint_links,
        joint_stage,
        sends,
        arrivals,
        0,
        joint_local,
    )
    up = PlaneSum(
        by_rows(up_in, up_rows),
        up_chip,
        up_theirs,
        up_links,
        up_stage,
        sends,
        arrivals,
        each,
        up_local,
    )
    out = PlaneSum(
        lambda r, h: out_in.at[
            :, pl.ds(pl.multiple_of(absolute(r) * out_cols, out_cols), out_cols)
        ],
        out_chip,
        out_theirs,
        out_links,
        out_stage,
        sends,
        arrivals,
        2 * each,
        out_local,
    )
    base = 3 * each
    rows_of = block_rows(columns, size)
    sums = [
        mesh_copy(
            d_normed_in.at[rows_of(s)],
            arrived_v.at[s - 1],
            sends,
            arrivals,
            base + s - 1,
            column[s - 1],
        )
        for s in range(1, columns)
    ]
    base = base + columns - 1
    for copy in sums:
        copy.start()
    first = [
        pltpu.make_async_copy(d_normed_in.at[rows_of(0)], own_v, local.at[0]),
        pltpu.make_async_copy(tokens_in, tokens_v, local.at[1]),
        pltpu.make_async_copy(d_mixed_in, mixed_v, local.at[2]),
        pltpu.make_async_copy(sums_in, running.at[0], local.at[3]),
    ]
    for copy in first:
        copy.start()
    for part in (out, joint, up):
        part.begin()
    first[3].wait()

    def small(i, device):
        return mesh_copy(running.at[i], sums_v.at[i], sends, arrivals, base + i, device)

    hops = [small(i, device) for i, device in enumerate((partner, along, across))]
    for i, copy in enumerate(hops):
        copy.start()
        copy.wait_recv()
        running[i + 1] = running[i] + sums_v[i]
    gains = [
        mesh_copy(running.at[3], sums_v.at[2 + s], sends, arrivals, base + 2 + s, column[s - 1])
        for s in range(1, columns)
    ]
    base = base + 2 + columns
    for copy in gains:
        copy.start()
    for part in (out, joint, up):
        part.send_first()
    for part in (out, joint, up):
        part.send_second()
    for part in (out, joint, up):
        part.finish()

    pieces = joint_rows // columns
    across_columns = [
        mesh_copy(
            joint_chip.at[
                0,
                0,
                pl.ds(pl.multiple_of((row + s) % columns * pieces, pieces), pieces),
                pl.ds(latent_start, latent_width),
            ],
            latent_v.at[s - 1],
            sends,
            arrivals,
            base + s - 1,
            column[s - 1],
        )
        for s in range(1, columns)
    ]
    for copy in across_columns:
        copy.start()
    done = [
        pltpu.make_async_copy(joint_chip.at[0, 0], joint_out, joint_local.at[1]),
        pltpu.make_async_copy(up_chip.at[0, 0], up_out, up_local.at[1]),
        pltpu.make_async_copy(out_chip.at[0, 0], out_out, out_local.at[1]),
    ]
    for copy in done:
        copy.start()

    for copy in first[:3]:
        copy.wait()
    total = own_v[...].astype(F32)
    for s in range(1, columns):
        sums[s - 1].wait_recv()
        total = total + arrived_v[s - 1].astype(F32)
    tokens = tokens_v[...].astype(F32)
    inverse = lax.rsqrt(jnp.mean(tokens * tokens, axis=1, keepdims=True) + EPSILON)
    unit = tokens * inverse
    scaled = total * gain_ref[...]
    mixed_v[...] = mixed_v[...] + inverse * (
        scaled - unit * jnp.mean(scaled * unit, axis=1, keepdims=True)
    )
    grad_copy = pltpu.make_async_copy(mixed_v, grad_out, local.at[0])
    grad_copy.start()
    gathered = running[3]
    for s in range(1, columns):
        gains[s - 1].wait_recv()
        gathered = gathered + sums_v[2 + s]
    sums_out[...] = gathered
    latent = joint_chip[
        0,
        0,
        pl.ds(pl.multiple_of(row * pieces, pieces), pieces),
        pl.ds(latent_start, latent_width),
    ].astype(F32)
    for s in range(1, columns):
        across_columns[s - 1].wait_recv()
        latent = latent + latent_v[s - 1].astype(F32)
    latent_out[...] = latent
    for copy in done + [grad_copy]:
        copy.wait()
    for part in (out, joint, up):
        part.drain()
    for copy in sums + hops + gains + across_columns:
        copy.wait_send()


def last_call(d_normed, tokens, d_mixed, gain, joint, up, out, sums, latent_start, latent_width):
    columns = lax.axis_size("tp")
    size, width = tokens.shape
    anywhere = pl.BlockSpec(memory_space=pl.ANY)
    held = pl.BlockSpec(memory_space=pltpu.VMEM)
    shapes = [
        (joint.shape[0] // 8, joint.shape[1]),
        (up.shape[0] // 8, up.shape[1]),
        (out.shape[0], out.shape[1] // 8),
    ]
    landing, scratch = [], []
    for rows, cols in shapes:
        one = plane_sum_space(1, rows, cols)
        landing, scratch = landing + one[0], scratch + one[1]
    remote, near = plane_sum_sizes(1)
    remote = 3 * remote + 3 * (columns - 1) + 3
    pieces = shapes[0][0] // columns
    return pl.pallas_call(
        functools.partial(last_kernel, columns, size, latent_start, latent_width),
        out_shape=[jax.ShapeDtypeStruct((size, width), F32)]
        + [jax.ShapeDtypeStruct(shape, BF) for shape in shapes]
        + [
            jax.ShapeDtypeStruct((pieces, latent_width), F32),
            jax.ShapeDtypeStruct(sums.shape, F32),
        ]
        + landing,
        in_specs=[anywhere] * 3 + [held] + [anywhere] * 4,
        out_specs=[anywhere] * 4 + [held] * 2 + [anywhere] * 6,
        scratch_shapes=scratch
        + [
            pltpu.VMEM((size, width), BF),
            pltpu.VMEM((columns - 1, size, width), BF),
            pltpu.VMEM((size, width), BF),
            pltpu.VMEM((size, width), F32),
            pltpu.VMEM((4,) + sums.shape, F32),
            pltpu.VMEM((2 + columns,) + sums.shape, F32),
            pltpu.VMEM((columns - 1, pieces, latent_width), BF),
            pltpu.SemaphoreType.DMA((remote,)),
            pltpu.SemaphoreType.DMA((remote,)),
            pltpu.SemaphoreType.DMA((4,)),
            pltpu.SemaphoreType.DMA((near,)),
            pltpu.SemaphoreType.DMA((near,)),
            pltpu.SemaphoreType.DMA((near,)),
        ],
        compiler_params=pltpu.CompilerParams(
            collective_id=4, has_side_effects=True, vmem_limit_bytes=48 * 1024 * 1024
        ),
        name="last_sums",
    )(d_normed, tokens, d_mixed, gain, joint, up, out, sums)[:6]


def plane_units(count):
    return [[(2 * i + j // 2, j % 2) for j in range(4)] for i in range(count // 2)]


def plane_gather(rows, count):
    gathered = lax.all_gather(rows, "fsdp", axis=0)
    return {
        (r, h): gathered[r, h * HALF : (h + 1) * HALF] for r in range(count) for h in (0, 1)
    }


def plane_scatter_whole(pairs, units, count):
    parts = {}
    for unit, pair in zip(units, pairs):
        for q, key in enumerate(unit):
            parts[key] = pair[q // 2][q % 2]
    stacked = jnp.concatenate([parts[r, h] for r in range(count) for h in (0, 1)], axis=0)
    return lax.psum_scatter(stacked, "fsdp", scatter_dimension=0, tiled=True).astype(F32)


def sum_everywhere(values):
    for axis_name in ("fsdp", "tp"):
        count = lax.axis_size(axis_name)
        if is_power(count):
            bit = 1
            while bit < count:
                values = values + swap(values, axis_name, bit)
                bit *= 2
        else:
            values = lax.psum(values, axis_name)
    return values


def expert_tables(expert_ids, expert_wts, local_experts, units, cap):
    fsdp_count = lax.axis_size("fsdp")
    fsdp_rank = lax.axis_index("fsdp")
    expert_count = local_experts * fsdp_count
    names = jnp.arange(expert_count, dtype=jnp.int32)[:, None]
    member = jnp.zeros((expert_count, SEQ), jnp.bool_)
    weight = jnp.zeros((expert_count, SEQ), F32)
    ids_rows, wts_rows = expert_ids.T, expert_wts.T
    for pick in range(TOPK):
        same = ids_rows[pick : pick + 1] == names
        member = member | same
        weight = weight + jnp.where(same, wts_rows[pick : pick + 1], 0.0)
    position = jnp.arange(HALF)
    before = (position[:, None] < position[None, :]).astype(BF)
    rank = jnp.dot(
        member.astype(BF).reshape(expert_count * 2, HALF), before, preferred_element_type=F32
    ).reshape(expert_count, SEQ)
    slot = jnp.where(member, rank, NO_SLOT)
    table = jnp.concatenate([slot, weight], axis=0)
    table = lax.all_gather(table, "fsdp", axis=0, tiled=True)
    table = table.reshape(fsdp_count, 2, fsdp_count, local_experts, 2, HALF)
    table = lax.dynamic_index_in_dim(table, fsdp_rank, axis=2, keepdims=False)
    slot_steps, weight_steps = [], []
    for unit in units:
        slot_steps.append(jnp.stack([table[r, 0, :, h] for r, h in unit]))
        weight_steps.append(jnp.stack([table[r, 1, :, h] for r, h in unit]))
    slot_row, weight_row = jnp.stack(slot_steps), jnp.stack(weight_steps)
    return (slot_row, weight_row, jnp.swapaxes(slot_row, 2, 3))


def per_device(
    block_in,
    out_cotan,
    segment_ids,
    expert_ids,
    expert_wts,
    attn_gain,
    query_proj,
    latent_proj,
    latent_gain,
    latent_up,
    out_proj,
    ffn_gain,
    shared_gate,
    shared_up,
    shared_down,
    routed_gate,
    routed_up,
    routed_down,
):
    tp_count = lax.axis_size("tp")
    fsdp_count = lax.axis_size("fsdp")
    tp_rank = lax.axis_index("tp")
    fsdp_rank = lax.axis_index("fsdp")
    tok_rows, model_width = block_in.shape
    local_experts, local_hidden = routed_gate.shape[:2]
    expert_count = local_experts * fsdp_count
    cap_rows = tok_rows * TOPK * 4 // (3 * expert_count)
    cap = cap_rows * (HALF // tok_rows)
    paired = fsdp_count == 8 and tok_rows * 2 == HALF
    heads_local = H // tp_count
    head_width = NOPE + ROPE
    score_scale = head_width ** (-0.5)
    shard_rows, query_cols = query_proj.shape
    latent_cols = latent_proj.shape[1]
    up_cols = latent_up.shape[1]
    out_rows = out_proj.shape[0]

    joint = query_cols + latent_cols
    spare = (-joint) % 128
    spare = spare + 128 if spare < 3 else spare
    gains = jnp.concatenate(
        [
            attn_gain[:, None],
            ffn_gain[:, None],
            jnp.pad(latent_gain, (0, shard_rows - latent_gain.shape[0]))[:, None],
            jnp.zeros((shard_rows, spare - 3), BF),
        ],
        axis=1,
    )
    packed = jnp.concatenate([query_proj, latent_proj, gains], axis=1)
    shared_weight = lax.all_gather(
        jnp.concatenate([shared_gate, shared_up], axis=1), "fsdp", axis=0, tiled=True
    )
    if paired:
        low, high = (0, RAW_ROWS - TOPK), (0, 0)
        raw = jnp.concatenate(
            [jnp.pad(expert_ids.T.astype(F32), (low, high)), jnp.pad(expert_wts.T, (low, high))]
        )
        tokens_all, packed_all, latent_up_weight, out_weight, raw = first_call(
            block_in,
            [packed, latent_up, out_proj, raw],
            ("rows", "rows", "columns", "relative"),
        )
        packed_all = packed_all.reshape(-1, packed.shape[1])
        latent_up_weight = latent_up_weight.reshape(LAT, up_cols)
    else:
        packed_all = lax.all_gather(packed, "fsdp", axis=0, tiled=True)
        latent_up_weight = lax.all_gather(latent_up, "fsdp", axis=0, tiled=True)
        out_weight = lax.all_gather(out_proj, "fsdp", axis=1, tiled=True)
        tokens_all = column_gather(block_in)
    cotan_own, tokens_all = tie(out_cotan, tokens_all)
    cotan_all = column_gather(cotan_own)
    shared_down_weight = lax.all_gather(shared_down, "fsdp", axis=1, tiled=True)
    gain_attn = packed_all[:, joint].astype(F32)
    gain_ffn = packed_all[:, joint + 1].astype(F32)
    gain_latent = (
        packed_all[:, joint + 2]
        .reshape(fsdp_count, shard_rows)[:, : latent_gain.shape[0]]
        .reshape(LAT)
        .astype(F32)
    )
    shared_cols = shared_gate.shape[1]

    unit_all, inverse_all = norm_parts(tokens_all.astype(F32))
    normed_all = (unit_all * gain_attn).astype(BF)
    joint_rows = jnp.dot(normed_all, packed_all, preferred_element_type=F32)
    queries = joint_rows[:, :query_cols].reshape(SEQ, heads_local, head_width)
    latent = joint_rows[:, query_cols:joint]
    unit_lat, inverse_lat = norm_parts(latent[:, :LAT])
    positions = jnp.arange(SEQ, dtype=jnp.int32)
    cosine, sine_part = rope_tables(positions, ROPE)
    compressed_all = (unit_lat * gain_latent).astype(BF)
    key_rope_all = rotate(latent[:, LAT:], cosine, sine_part).astype(BF)
    query_cat = jnp.concatenate(
        [
            queries[:, :, :NOPE],
            rotate(queries[:, :, NOPE:], cosine[:, None, :], sine_part[:, None, :]),
        ],
        axis=2,
    ).astype(BF)
    key_value = (
        jnp.dot(compressed_all, latent_up_weight, preferred_element_type=F32)
        .reshape(SEQ, heads_local, NOPE + DV)
        .astype(BF)
    )
    key_cat = jnp.concatenate(
        [
            key_value[:, :, :NOPE],
            jnp.broadcast_to(key_rope_all[:, None, :], (SEQ, heads_local, ROPE)),
        ],
        axis=2,
    )
    values = key_value[:, :, NOPE:]
    allowed = (positions[None, :] <= positions[:, None]) & (
        segment_ids[None, :] == segment_ids[:, None]
    )
    raw_scores = (
        jnp.einsum("qhd,khd->hqk", query_cat, key_cat, preferred_element_type=F32) * score_scale
    )
    masked = jnp.where(allowed[None], raw_scores, MASK_FILL)
    top_score = jnp.max(masked, axis=2, keepdims=True)
    exponent = jnp.exp(masked - top_score)
    row_total = jnp.sum(exponent, axis=2, keepdims=True)
    probabilities = exponent / row_total
    probs_low = probabilities.astype(BF)
    attended = (
        jnp.einsum("hqk,khd->qhd", probs_low, values, preferred_element_type=F32)
        .reshape(SEQ, heads_local * DV)
        .astype(BF)
    )
    attn_part = jnp.dot(attended, out_weight, preferred_element_type=F32).astype(BF)
    if paired:
        mixed_rows, normed_ffn_all, d_routed_in, out_array, *kept = expert_call(
            attn_part,
            block_in,
            cotan_all,
            routed_gate,
            routed_up,
            routed_down,
            gain_ffn[None, :],
            raw,
            cap_rows,
        )
        unit_two, inverse_two = norm_parts(mixed_rows)
        d_routed_in = d_routed_in.astype(F32)
    else:
        units = plane_units(fsdp_count)
        tables = expert_tables(expert_ids, expert_wts, local_experts, units, cap)
        hidden_pad = -(-local_hidden // 128) * 128
        lift = ((0, 0), (0, hidden_pad - local_hidden), (0, 0))
        routed_gate_up = jnp.concatenate(
            [jnp.pad(routed_gate, lift), jnp.pad(routed_up, lift)], axis=1
        )
        routed_down_pad = jnp.pad(routed_down, lift)
        mixed_rows = block_in.astype(F32) + column_scatter(attn_part)
        unit_two, inverse_two = norm_parts(mixed_rows)
        normed_ffn_all = column_gather((unit_two * gain_ffn).astype(BF))
        x_blocks = plane_gather(normed_ffn_all, fsdp_count)
        dy_all = lax.all_gather(cotan_all, "fsdp", axis=0, tiled=True)
        kept = []
        dx_pairs = []
        for step, unit in enumerate(units):
            pair, kept = expert_front(
                step,
                len(units),
                [x_blocks[key] for key in unit],
                jnp.array([2 * r + h for r, h in unit], jnp.int32),
                dy_all,
                routed_gate_up,
                routed_down_pad,
                tables,
                kept,
                cap,
            )
            dx_pairs.append(pair)
        near, far = expert_out(kept[2], routed_down_pad, tables, cap)
        d_routed_in = plane_scatter_whole(dx_pairs, units, fsdp_count)
    if not paired:
        routed_gate_grad, routed_up_grad, routed_down_grad = expert_grads(kept, local_hidden)

    shared_pre = jnp.dot(normed_ffn_all, shared_weight, preferred_element_type=F32)
    shared_gate_pre, shared_up_pre = shared_pre[:, :shared_cols], shared_pre[:, shared_cols:]
    shared_hidden = (jax.nn.silu(shared_gate_pre) * shared_up_pre).astype(BF)
    shared_rows = jnp.dot(shared_hidden, shared_down_weight, preferred_element_type=F32)
    shared_down_part = jnp.dot(shared_hidden.T, cotan_all, preferred_element_type=F32)
    d_shared_hidden = jnp.dot(cotan_all, shared_down_weight.T, preferred_element_type=F32)
    d_shared = jnp.concatenate(silu_back(d_shared_hidden, shared_gate_pre, shared_up_pre), axis=1)
    shared_part = jnp.dot(normed_ffn_all.T, d_shared, preferred_element_type=F32)
    d_shared_in = jnp.dot(d_shared, shared_weight.T, preferred_element_type=F32)

    if paired:
        d_ffn_rows, shared_part, shared_down_part = tie(
            (d_shared_in + d_routed_in).astype(BF),
            shared_part.astype(BF),
            shared_down_part.astype(BF),
        )
        (
            d_mixed,
            d_proj_all,
            ffn_gain_part,
            routed_rows,
            routed_gate_grad,
            routed_up_grad,
            routed_down_grad,
        ) = middle_call(
            d_ffn_rows, mixed_rows, out_cotan, gain_ffn[None, :], out_array, kept, local_hidden
        )
        ffn_gain_part = ffn_gain_part[0]
        routed_rows = routed_rows.astype(F32)
    else:
        d_normed_ffn = column_scatter(d_shared_in + d_routed_in)
        out_pairs = [(near[step], far[step]) for step in range(len(units))]
        routed_rows = plane_scatter_whole(out_pairs, units, fsdp_count)
        ffn_gain_part, d_mixed_norm = norm_back(d_normed_ffn, unit_two, inverse_two, gain_ffn)
        d_mixed = out_cotan.astype(F32) + d_mixed_norm
        d_proj_all = column_gather(d_mixed.astype(BF))
    ffn_rows = column_scatter(shared_rows + routed_rows)
    block_out = (mixed_rows + ffn_rows).astype(BF)

    out_part = jnp.dot(attended.T, d_proj_all, preferred_element_type=F32)
    d_attended = (
        jnp.dot(d_proj_all, out_weight.T, preferred_element_type=F32)
        .astype(BF)
        .reshape(SEQ, heads_local, DV)
    )
    prob_grad = jnp.einsum("qhd,khd->hqk", d_attended, values, preferred_element_type=F32)
    score_grad = (
        probabilities
        * (prob_grad - jnp.sum(probabilities * prob_grad, axis=2, keepdims=True))
    ).astype(BF)
    query_grad = (
        jnp.einsum("hqk,khd->qhd", score_grad, key_cat, preferred_element_type=F32) * score_scale
    )
    key_grad = (
        jnp.einsum("hqk,qhd->khd", score_grad, query_cat, preferred_element_type=F32) * score_scale
    )
    value_grad = jnp.einsum("hqk,qhd->khd", probs_low, d_attended, preferred_element_type=F32)
    d_queries = (
        jnp.concatenate(
            [
                query_grad[:, :, :NOPE],
                unrotate(query_grad[:, :, NOPE:], cosine[:, None, :], sine_part[:, None, :]),
            ],
            axis=2,
        )
        .reshape(SEQ, heads_local * head_width)
        .astype(BF)
    )
    d_key_value = (
        jnp.concatenate([key_grad[:, :, :NOPE], value_grad], axis=2)
        .reshape(SEQ, heads_local * (NOPE + DV))
        .astype(BF)
    )
    latent_up_part = jnp.dot(compressed_all.T, d_key_value, preferred_element_type=F32)
    d_compressed = jnp.dot(d_key_value, latent_up_weight.T, preferred_element_type=F32)
    d_key_rope = jnp.sum(key_grad[:, :, NOPE:], axis=1)
    latent_gain_part, d_latent_main = norm_back(d_compressed, unit_lat, inverse_lat, gain_latent)
    d_latent = jnp.concatenate(
        [d_latent_main, unrotate(d_key_rope, cosine, sine_part)], axis=1
    ).astype(BF)
    d_joint = jnp.concatenate([d_queries, d_latent, jnp.zeros((SEQ, spare), BF)], axis=1)
    joint_part = jnp.dot(normed_all.T, d_joint, preferred_element_type=F32)
    d_normed_part = jnp.dot(d_joint, packed_all.T, preferred_element_type=F32)
    attn_gain_part = jnp.sum(d_normed_part * unit_all, axis=0)

    def scatter(part, dimension):
        return lax.psum_scatter(part.astype(BF), "fsdp", scatter_dimension=dimension, tiled=True)

    gain_parts = jnp.concatenate([attn_gain_part, latent_gain_part, ffn_gain_part]).reshape(
        -1, 128
    )
    joint_part = joint_part.astype(BF)
    shared_down_grad = scatter(shared_down_part, 1)
    shared_grad = scatter(shared_part, 0)
    if paired:
        latent_width = joint_part.shape[1] - query_cols
        (
            block_in_grad,
            joint_grad,
            latent_up_grad,
            out_proj_grad,
            latent_proj_grad,
            gain_sums,
        ) = last_call(
            d_normed_part.astype(BF),
            block_in,
            d_mixed,
            gain_attn[None, :],
            joint_part,
            latent_up_part.astype(BF),
            out_part.astype(BF),
            gain_parts,
            query_cols,
            latent_width,
        )
        latent_proj_grad = latent_proj_grad[:, :latent_cols]
    else:
        d_normed = column_scatter(d_normed_part)
        unit_one, inverse_one = norm_parts(block_in.astype(F32))
        _, d_tokens_norm = norm_back(d_normed, unit_one, inverse_one, gain_attn)
        block_in_grad = d_mixed + d_tokens_norm
        out_proj_grad = scatter(out_part, 1)
        latent_up_grad = scatter(latent_up_part, 0)
        joint_grad = scatter(joint_part, 0)
        latent_proj_grad = column_scatter(joint_grad[:, query_cols:joint])
        gain_sums = sum_everywhere(gain_parts)
    gain_sums = gain_sums.reshape(-1)
    query_proj_grad = joint_grad[:, :query_cols].astype(F32)
    latent_up_grad = latent_up_grad.astype(F32)
    out_proj_grad = out_proj_grad.astype(F32)
    shared_grad = shared_grad.astype(F32)
    shared_gate_grad, shared_up_grad = shared_grad[:, :shared_cols], shared_grad[:, shared_cols:]
    shared_down_grad = shared_down_grad.astype(F32)
    device = fsdp_rank * tp_count + tp_rank
    devices = tp_count * fsdp_count

    def own_gain(start, size):
        return lax.dynamic_slice(gain_sums, (start + device * (size // devices),), (size // devices,))

    attn_gain_grad = own_gain(0, model_width)
    latent_gain_grad = own_gain(model_width, LAT)
    ffn_gain_grad = own_gain(model_width + LAT, model_width)
    return (
        block_out,
        block_in_grad,
        attn_gain_grad,
        query_proj_grad,
        latent_proj_grad,
        latent_gain_grad,
        latent_up_grad,
        out_proj_grad,
        ffn_gain_grad,
        shared_gate_grad,
        shared_up_grad,
        shared_down_grad,
        routed_gate_grad,
        routed_up_grad,
        routed_down_grad,
    )


def solution(mesh):
    placed = (
        P(("fsdp", "tp"), None),
        P(("fsdp", "tp"), None),
        P("fsdp"),
        P("fsdp", None),
        P("fsdp", None),
        P("fsdp"),
        P("fsdp", "tp"),
        P("fsdp", None),
        P("fsdp"),
        P("fsdp", "tp"),
        P("tp", "fsdp"),
        P("fsdp"),
        P("fsdp", "tp"),
        P("fsdp", "tp"),
        P("tp", "fsdp"),
        P("fsdp", "tp", None),
        P("fsdp", "tp", None),
        P("fsdp", "tp", None),
    )
    return jax.shard_map(
        per_device,
        mesh=mesh,
        in_specs=placed,
        out_specs=(
            P(("fsdp", "tp"), None),
            P(("fsdp", "tp"), None),
            P(("fsdp", "tp")),
            P("fsdp", "tp"),
            P(("fsdp", "tp"), None),
            P(("fsdp", "tp")),
            P("fsdp", "tp"),
            P("tp", "fsdp"),
            P(("fsdp", "tp")),
            P("fsdp", "tp"),
            P("fsdp", "tp"),
            P("tp", "fsdp"),
            P("fsdp", "tp", None),
            P("fsdp", "tp", None),
            P("fsdp", "tp", None),
        ),
        check_vma=False,
    )
```

```python
import functools

import jax
import jax.numpy as jnp
from jax import lax
from jax.experimental import pallas as pl
from jax.experimental.pallas import tpu as pltpu
from jax.sharding import PartitionSpec as P

H = 16
NOPE = 128
ROPE = 64
DV = 128
LAT = 512
TOPK = 6
SEQ = 512
HALF = 256
QUARTET = 4
RAW_ROWS = 8


EPSILON = 1e-06
THETA_BASE = 10000.0
MASK_FILL = -1e30
NO_SLOT = -1e6

BF = jnp.bfloat16
F32 = jnp.float32


def rope_tables(positions, width_rope):
    middle = width_rope // 2
    frequency = THETA_BASE ** (-(jnp.arange(middle) * 2).astype(jnp.float32) / width_rope)
    angles = positions.astype(jnp.float32)[:, None] * frequency[None, :]
    return (jnp.cos(angles), jnp.sin(angles))


def rotate(values, cosine, sine_part):
    middle = values.shape[-1] // 2
    first_half = values[..., :middle]
    second_half = values[..., middle:]
    return jnp.concatenate(
        [
            first_half * cosine - second_half * sine_part,
            second_half * cosine + first_half * sine_part,
        ],
        axis=-1,
    )


def unrotate(values, cosine, sine_part):
    middle = values.shape[-1] // 2
    first_half = values[..., :middle]
    second_half = values[..., middle:]
    return jnp.concatenate(
        [
            first_half * cosine + second_half * sine_part,
            second_half * cosine - first_half * sine_part,
        ],
        axis=-1,
    )


def norm_parts(values):
    inverse = lax.rsqrt(jnp.mean(values * values, axis=-1, keepdims=True) + EPSILON)
    return (values * inverse, inverse)


def norm_back(upstream, unit_rows, inverse, scaling):
    scaled = upstream * scaling
    gain_grad = jnp.sum(upstream * unit_rows, axis=0)
    input_grad = inverse * (
        scaled - unit_rows * jnp.mean(scaled * unit_rows, axis=-1, keepdims=True)
    )
    return (gain_grad, input_grad)


def silu_back(grad_hidden, gate_pre, up_pre):
    sigmoid = jax.nn.sigmoid(gate_pre)
    gate_grad = grad_hidden * up_pre * (sigmoid * (1.0 + gate_pre * (1.0 - sigmoid)))
    up_grad = grad_hidden * (gate_pre * sigmoid)
    return (gate_grad.astype(jnp.bfloat16), up_grad.astype(jnp.bfloat16))


def is_power(count):
    return count & (count - 1) == 0


def swap(values, axis_name, bit):
    count = lax.axis_size(axis_name)
    return lax.ppermute(values, axis_name, [(i, i ^ bit) for i in range(count)])


def tie(*values):
    return lax.optimization_barrier(values)


def column_gather(rows):
    return lax.all_gather(rows, "tp", axis=0, tiled=True)


def column_scatter(values):
    return lax.psum_scatter(values.astype(BF), "tp", scatter_dimension=0, tiled=True).astype(F32)


def dot_rows(left, right):
    return lax.dot_general(left, right, (((1,), (1,)), ((), ())), preferred_element_type=F32)


def dot_plain(left, right):
    return lax.dot_general(left, right, (((1,), (0,)), ((), ())), preferred_element_type=F32)


def dot_first(left, right):
    return lax.dot_general(left, right, (((0,), (0,)), ((), ())), preferred_element_type=F32)


def select_rows(slot_rows, experts, cap):
    row = lax.broadcasted_iota(jnp.int32, (experts * cap, HALF), 0).astype(F32)
    hit = row == slot_rows[0:1, :]
    for e in range(1, experts):
        hit = hit | (row == slot_rows[e : e + 1, :] + float(e * cap))
    return hit


def select_cols(slot_cols, experts, cap):
    lane = lax.broadcasted_iota(jnp.int32, (HALF, experts * cap), 1).astype(F32)
    hit = lane == slot_cols[:, 0:1]
    for e in range(1, experts):
        hit = hit | (lane == slot_cols[:, e : e + 1] + float(e * cap))
    return hit


def slot_weights(hit, weight_rows, experts, cap):
    pieces = []
    for e in range(experts):
        part = hit[e * cap : (e + 1) * cap, :]
        pieces.append(
            jnp.sum(jnp.where(part, weight_rows[e : e + 1, :], 0.0), axis=1, keepdims=True)
        )
    return jnp.concatenate(pieces, axis=0)


def expert_front_kernel(step, experts, cap, aliased, *refs):
    count = QUARTET
    x_in = refs[:count]
    where_ref, dy_in, gate_up_in, down_in, slot_row_ref, weight_row_ref, slot_col_ref = refs[
        count : count + 7
    ]
    base = count + 7 + aliased
    dx_out = refs[base : base + 2]
    x_all, d_all, hid_all, dgu_all = refs[base + 2 : base + 6]
    (xb, db, gate_up, down, xs, ds, dxs, dxo, hid, dgu, sem_in, sem_w, sem_out, sem_dx) = refs[
        base + 6 :
    ]
    width = xb.shape[2]
    pad = down.shape[1]
    tile = min(1024, width)
    x_copies = [pltpu.make_async_copy(x_in[q], xb.at[q], sem_in.at[q]) for q in range(count)]
    d_copies = [
        pltpu.make_async_copy(
            dy_in.at[pl.ds(pl.multiple_of(where_ref[q] * HALF, HALF), HALF)],
            db.at[q],
            sem_in.at[count + q],
        )
        for q in range(count)
    ]
    w_copies = [
        pltpu.make_async_copy(gate_up_in, gate_up, sem_w.at[0]),
        pltpu.make_async_copy(down_in, down, sem_w.at[1]),
    ]
    for q in range(count):
        x_copies[q].start()
        d_copies[q].start()
    for copy in w_copies:
        copy.start()
    for q in range(count):
        x_copies[q].wait()
        d_copies[q].wait()

        hit = select_rows(slot_row_ref[q], experts, cap)
        weights = slot_weights(hit, weight_row_ref[q], experts, cap)
        choose = jnp.where(hit, 1.0, 0.0).astype(BF)

        def spread(n, carry, q=q, choose=choose, weights=weights):
            cols = pl.ds(pl.multiple_of(n * tile, tile), tile)
            rows = dot_plain(choose, xb[q, :, cols])
            grads = dot_plain(choose, db[q, :, cols]) * weights
            for e in range(experts):
                xs[e, q * cap : (q + 1) * cap, cols] = rows[e * cap : (e + 1) * cap].astype(BF)
                ds[e, q * cap : (q + 1) * cap, cols] = grads[e * cap : (e + 1) * cap].astype(BF)
            return carry

        lax.fori_loop(0, width // tile, spread, 0)
    out_copies = [
        pltpu.make_async_copy(xs, x_all.at[step], sem_out.at[0]),
        pltpu.make_async_copy(ds, d_all.at[step], sem_out.at[1]),
        pltpu.make_async_copy(hid, hid_all.at[step], sem_out.at[2]),
        pltpu.make_async_copy(dgu, dgu_all.at[step], sem_out.at[3]),
    ]
    out_copies[0].start()
    out_copies[1].start()
    for copy in w_copies:
        copy.wait()

    def one_expert(e, carry):
        both = dot_rows(xs[e], gate_up[e])
        gate_pre, up_pre = both[:, :pad], both[:, pad:]
        d_hidden = dot_rows(ds[e], down[e])
        sigmoid = jax.nn.sigmoid(gate_pre)
        silu = gate_pre * sigmoid
        hid[e] = (silu * up_pre).astype(BF)
        gate_grad = d_hidden * up_pre * (sigmoid * (1.0 + gate_pre * (1.0 - sigmoid)))
        grads = jnp.concatenate([gate_grad, d_hidden * silu], axis=1).astype(BF)
        dgu[e] = grads

        def back(n, inner):
            cols = pl.ds(pl.multiple_of(n * tile, tile), tile)
            part = dot_plain(dgu[e], gate_up[e, :, cols]).astype(BF)
            for q in range(count):
                dxs[q, pl.ds(pl.multiple_of(e * cap, cap), cap), cols] = part[
                    q * cap : (q + 1) * cap
                ]
            return inner

        lax.fori_loop(0, width // tile, back, 0)
        return carry

    lax.fori_loop(0, experts, one_expert, 0)
    out_copies[2].start()
    out_copies[3].start()
    dx_copies = [
        pltpu.make_async_copy(dxo.at[q], dx_out[q // 2].at[q % 2], sem_dx.at[q])
        for q in range(count)
    ]
    for q in range(count):
        choose = jnp.where(select_cols(slot_col_ref[q], experts, cap), 1.0, 0.0).astype(BF)

        def gather(n, carry, q=q, choose=choose):
            cols = pl.ds(pl.multiple_of(n * tile, tile), tile)
            dxo[q, :, cols] = dot_plain(choose, dxs[q, :, cols]).astype(BF)
            return carry

        lax.fori_loop(0, width // tile, gather, 0)
        dx_copies[q].start()
    for copy in out_copies:
        copy.wait()
    for copy in dx_copies:
        copy.wait()


def expert_front(step, steps, x_parts, where, dy_all, gate_up, down, tables, kept, cap):
    experts, wide, width = gate_up.shape
    pad = wide // 2
    slots = QUARTET * cap
    slot_row, weight_row, slot_col = (t[step] for t in tables)
    any_spec = pl.BlockSpec(memory_space=pl.ANY)
    vmem_spec = pl.BlockSpec(memory_space=pltpu.VMEM)
    pair_shape = jax.ShapeDtypeStruct((2, HALF, width), BF)
    kept_shapes = [
        jax.ShapeDtypeStruct((steps, experts, slots, columns), BF)
        for columns in (width, width, pad, wide)
    ]
    results = pl.pallas_call(
        functools.partial(expert_front_kernel, step, experts, cap, len(kept)),
        out_shape=[pair_shape] * 2 + kept_shapes,
        in_specs=[any_spec] * QUARTET
        + [pl.BlockSpec(memory_space=pltpu.SMEM)]
        + [any_spec] * 3
        + [vmem_spec] * 3
        + [any_spec] * len(kept),
        out_specs=[any_spec] * 6,
        input_output_aliases={QUARTET + 7 + i: 2 + i for i in range(len(kept))},
        scratch_shapes=[
            pltpu.VMEM((QUARTET, HALF, width), BF),
            pltpu.VMEM((QUARTET, HALF, width), BF),
            pltpu.VMEM((experts, wide, width), BF),
            pltpu.VMEM((experts, pad, width), BF),
            pltpu.VMEM((experts, slots, width), BF),
            pltpu.VMEM((experts, slots, width), BF),
            pltpu.VMEM((QUARTET, experts * cap, width), BF),
            pltpu.VMEM((QUARTET, HALF, width), BF),
            pltpu.VMEM((experts, slots, pad), BF),
            pltpu.VMEM((experts, slots, wide), BF),
            pltpu.SemaphoreType.DMA((2 * QUARTET,)),
            pltpu.SemaphoreType.DMA((2,)),
            pltpu.SemaphoreType.DMA((4,)),
            pltpu.SemaphoreType.DMA((QUARTET,)),
        ],
        compiler_params=pltpu.CompilerParams(vmem_limit_bytes=62 * 1024 * 1024),
        cost_estimate=pl.CostEstimate(
            flops=2 * slots * experts * width * pad * 5
            + 6 * QUARTET * HALF * experts * cap * width,
            bytes_accessed=2 * width * (3 * QUARTET * HALF + experts * 3 * pad + 2 * experts * slots),
            transcendentals=slots * experts * pad,
        ),
        name="expert_front",
    )(*x_parts, where, dy_all, gate_up, down, slot_row, weight_row, slot_col, *kept)
    return list(results[:2]), list(results[2:])


def expert_out_kernel(experts, cap, hid, down, slot_row, weight_row, slot_col, near, far, parts):
    width = down.shape[2]
    tile = min(1024, width)
    weights = [
        slot_weights(
            select_rows(slot_row[0, q], experts, cap), weight_row[0, q], experts, cap
        )
        for q in range(QUARTET)
    ]
    for e in range(experts):

        def front(n, carry, e=e):
            cols = pl.ds(pl.multiple_of(n * tile, tile), tile)
            rows = dot_plain(hid[0, e], down[e, :, cols])
            for q in range(QUARTET):
                parts[q, e * cap : (e + 1) * cap, cols] = (
                    rows[q * cap : (q + 1) * cap] * weights[q][e * cap : (e + 1) * cap]
                ).astype(BF)
            return carry

        lax.fori_loop(0, width // tile, front, 0)
    for q in range(QUARTET):
        choose = jnp.where(select_cols(slot_col[0, q], experts, cap), 1.0, 0.0).astype(BF)
        out = (near, far)[q // 2]

        def gather(n, carry, q=q, choose=choose, out=out):
            cols = pl.ds(pl.multiple_of(n * tile, tile), tile)
            out[0, q % 2, :, cols] = dot_plain(choose, parts[q, :, cols]).astype(BF)
            return carry

        lax.fori_loop(0, width // tile, gather, 0)


def expert_out(hid_all, down, tables, cap):
    steps, experts, slots, pad = hid_all.shape
    width = down.shape[2]
    slot_row, weight_row, slot_col = tables
    return pl.pallas_call(
        functools.partial(expert_out_kernel, experts, cap),
        grid=(steps,),
        out_shape=[jax.ShapeDtypeStruct((steps, 2, HALF, width), BF)] * 2,
        in_specs=[
            pl.BlockSpec((1, experts, slots, pad), lambda i: (i, 0, 0, 0)),
            pl.BlockSpec((experts, pad, width), lambda i: (0, 0, 0)),
            pl.BlockSpec((1,) + slot_row.shape[1:], lambda i: (i, 0, 0, 0)),
            pl.BlockSpec((1,) + weight_row.shape[1:], lambda i: (i, 0, 0, 0)),
            pl.BlockSpec((1,) + slot_col.shape[1:], lambda i: (i, 0, 0, 0)),
        ],
        out_specs=[pl.BlockSpec((1, 2, HALF, width), lambda i: (i, 0, 0, 0))] * 2,
        scratch_shapes=[pltpu.VMEM((QUARTET, experts * cap, width), BF)],
        compiler_params=pltpu.CompilerParams(vmem_limit_bytes=48 * 1024 * 1024),
        cost_estimate=pl.CostEstimate(
            flops=steps * (2 * slots * experts * width * pad + 2 * QUARTET * HALF * experts * cap * width),
            bytes_accessed=2 * steps * QUARTET * HALF * width + 2 * hid_all.size + 2 * down.size,
            transcendentals=0,
        ),
        name="expert_out",
    )(hid_all, down, slot_row, weight_row, slot_col)


def expert_grads_kernel(dgu, x, hid, d, gate_grad, up_grad, down_grad):
    local = gate_grad.shape[1]
    pad = hid.shape[3]
    width = x.shape[3]
    tile = min(1024, width)

    @pl.when(pl.program_id(1) == 0)
    def _():
        gate_grad[...] = jnp.zeros_like(gate_grad)
        up_grad[...] = jnp.zeros_like(up_grad)
        down_grad[...] = jnp.zeros_like(down_grad)

    def part(n, carry):
        cols = pl.ds(pl.multiple_of(n * tile, tile), tile)
        gate_grad[0, :, cols] += dot_first(dgu[0, 0, :, :pad], x[0, 0, :, cols])[:local]
        up_grad[0, :, cols] += dot_first(dgu[0, 0, :, pad:], x[0, 0, :, cols])[:local]
        down_grad[0, :, cols] += dot_first(hid[0, 0], d[0, 0, :, cols])[:local]
        return carry

    lax.fori_loop(0, width // tile, part, 0)


def expert_grads(kept, local):
    x_all, d_all, hid_all, dgu_all = kept
    steps, experts, slots, width = x_all.shape
    pad = hid_all.shape[3]

    def block(array):
        return pl.BlockSpec((1, 1) + array.shape[2:], lambda e, i: (i, e, 0, 0))

    grad = jax.ShapeDtypeStruct((experts, local, width), F32)
    return pl.pallas_call(
        expert_grads_kernel,
        grid=(experts, steps),
        out_shape=[grad] * 3,
        in_specs=[block(dgu_all), block(x_all), block(hid_all), block(d_all)],
        out_specs=[pl.BlockSpec((1, local, width), lambda e, i: (e, 0, 0))] * 3,
        compiler_params=pltpu.CompilerParams(vmem_limit_bytes=48 * 1024 * 1024),
        cost_estimate=pl.CostEstimate(
            flops=2 * 3 * steps * experts * slots * width * pad,
            bytes_accessed=2 * (x_all.size + d_all.size + hid_all.size + dgu_all.size)
            + 12 * experts * local * width,
            transcendentals=0,
        ),
        name="expert_grads",
    )(dgu_all, x_all, hid_all, d_all)


def mesh_copy(src, dst, sends, arrivals, number, device):
    return pltpu.make_async_remote_copy(
        src_ref=src,
        dst_ref=dst,
        send_sem=sends.at[number],
        recv_sem=arrivals.at[number],
        device_id=device,
        device_id_type=pl.DeviceIdType.MESH,
    )


def plane_neighbours():
    place, column = lax.axis_index("fsdp"), lax.axis_index("tp")
    core, along, across = place % 2, (place // 2) % 2, place // 4
    return (
        (place + 1 - 2 * core, column),
        (place + 2 - 4 * along, column),
        (place + 4 - 8 * across, column),
    )


def column_neighbours(count):
    place, column = lax.axis_index("fsdp"), lax.axis_index("tp")
    return [(place, (column + s) % count) for s in range(1, count)]


def greet(devices):
    barrier = pltpu.get_barrier_semaphore()
    for device in devices:
        pl.semaphore_signal(
            barrier, inc=1, device_id=device, device_id_type=pl.DeviceIdType.MESH
        )
    pl.semaphore_wait(barrier, len(devices))


class ColumnGather:
    def __init__(self, blocks, rows_of, sends, arrivals, base):
        self.blocks, self.rows_of = blocks, rows_of
        self.sends, self.arrivals, self.base = sends, arrivals, base
        self.row = lax.axis_index("tp")
        self.column = column_neighbours(4)

    def direct(self, s):
        place = self.blocks.at[self.rows_of(0)]
        return mesh_copy(
            place, place, self.sends, self.arrivals, self.base + s - 1, self.column[s - 1]
        )

    def start(self):
        @pl.when(self.row < 3)
        def _():
            self.direct(1).start()

        @pl.when(self.row > 0)
        def _():
            self.direct(3).start()

        self.direct(2).start()

    def wait(self, b):
        self.direct(4 - b).wait_recv()
        if b == 2:

            @pl.when(self.row == 1)
            def _():
                self.relay(3).start()

            @pl.when(self.row == 2)
            def _():
                self.relay(1).start()

    def relay(self, s):
        place = self.blocks.at[self.rows_of(2)]
        return pltpu.make_async_remote_copy(
            src_ref=place,
            dst_ref=place,
            send_sem=self.sends.at[self.base + 3],
            recv_sem=self.arrivals.at[self.base + 3 - s],
            device_id=self.column[s - 1],
            device_id_type=pl.DeviceIdType.MESH,
        )

    def drain(self):
        @pl.when(self.row < 3)
        def _():
            self.direct(1).wait_send()

        @pl.when(self.row > 0)
        def _():
            self.direct(3).wait_send()

        self.direct(2).wait_send()

        @pl.when(self.row == 1)
        def _():
            self.relay(3).wait_send()

        @pl.when(self.row == 2)
        def _():
            self.relay(1).wait_send()


class ColumnSum:
    def __init__(self, parts, rows_of, landed, relayed, sends, arrivals, base):
        self.parts, self.rows_of, self.landed, self.relayed = parts, rows_of, landed, relayed
        self.sends, self.arrivals, self.base = sends, arrivals, base
        self.row = lax.axis_index("tp")
        self.column = column_neighbours(4)

    def direct(self, s):
        return mesh_copy(
            self.parts.at[self.rows_of(s)],
            self.landed.at[s - 1],
            self.sends,
            self.arrivals,
            self.base + s - 1,
            self.column[s - 1],
        )

    def first_leg(self, s):
        return mesh_copy(
            self.parts.at[self.rows_of(4 - s)],
            self.relayed.at[0],
            self.sends,
            self.arrivals,
            self.base + 3,
            self.column[s - 1],
        )

    def own_part(self, local):
        return pltpu.make_async_copy(self.parts.at[self.rows_of(2)], self.relayed.at[1], local)

    def second_leg(self):
        return mesh_copy(
            self.relayed.at[1],
            self.landed.at[1],
            self.sends,
            self.arrivals,
            self.base + 1,
            self.column[1],
        )

    def start(self, local):
        @pl.when(self.row == 0)
        def _():
            self.first_leg(1).start()

        @pl.when(self.row == 3)
        def _():
            self.first_leg(3).start()

        @pl.when((self.row == 1) | (self.row == 2))
        def _():
            self.own_part(local).start()

        @pl.when(self.row < 3)
        def _():
            self.direct(1).start()

        @pl.when(self.row > 0)
        def _():
            self.direct(3).start()

        @pl.when((self.row == 0) | (self.row == 3))
        def _():
            self.direct(2).start()

    def middle(self, local):
        @pl.when((self.row == 1) | (self.row == 2))
        def _():
            self.own_part(local).wait()
            self.first_leg(1).wait_recv()

            def some(i, carry):
                rows = pl.ds(pl.multiple_of(i * 32, 32), 32)
                self.relayed[1, rows, :] = (
                    self.relayed[0, rows, :].astype(F32) + self.relayed[1, rows, :].astype(F32)
                ).astype(BF)
                return carry

            lax.fori_loop(0, self.relayed.shape[1] // 32, some, 0)
            self.second_leg().start()

    def clear(self):
        @pl.when(self.row == 0)
        def _():
            self.landed[0] = jnp.zeros(self.landed.shape[1:], BF)

        @pl.when(self.row == 3)
        def _():
            self.landed[2] = jnp.zeros(self.landed.shape[1:], BF)

    def total(self, own):
        @pl.when(self.row > 0)
        def _():
            self.direct(1).wait_recv()

        @pl.when(self.row < 3)
        def _():
            self.direct(3).wait_recv()

        self.direct(2).wait_recv()
        total = own.astype(F32)
        for s in range(3):
            total = total + self.landed[s].astype(F32)
        return total

    def drain(self):
        @pl.when(self.row == 0)
        def _():
            self.first_leg(1).wait_send()

        @pl.when(self.row == 3)
        def _():
            self.first_leg(3).wait_send()

        @pl.when(self.row < 3)
        def _():
            self.direct(1).wait_send()

        @pl.when(self.row > 0)
        def _():
            self.direct(3).wait_send()

        self.direct(2).wait_send()


class PlaneGather:
    def __init__(self, own, others, rows_of, sends, arrivals, base):
        self.own, self.others, self.rows_of = own, others, rows_of
        self.sends, self.arrivals, self.base = sends, arrivals, base
        self.partner, self.along, self.across = plane_neighbours()

    def copies(self, b):
        half = self.own.shape[1] // 2
        rows = self.rows_of(b)
        left, right = pl.ds(0, half), pl.ds(half, half)
        other = {r: self.others.at[r - 1] for r in range(1, 8)}
        plan = [
            (self.own.at[rows], other[2].at[rows], self.along),
            (self.own.at[rows], other[4].at[rows], self.across),
            (self.own.at[rows], other[1].at[rows], self.partner),
            (other[2].at[rows, left], other[6].at[rows, left], self.across),
            (other[4].at[rows, right], other[6].at[rows, right], self.along),
            (other[2].at[rows], other[3].at[rows], self.partner),
            (other[4].at[rows], other[5].at[rows], self.partner),
            (other[6].at[rows], other[7].at[rows], self.partner),
        ]
        return [
            mesh_copy(src, dst, self.sends, self.arrivals, self.base + 8 * b + i, device)
            for i, (src, dst, device) in enumerate(plan)
        ]

    def start(self, b):
        for copy in self.copies(b)[:3]:
            copy.start()

    def forward(self, b):
        along, across, _, left, right, third, fifth, _ = self.copies(b)
        along.wait_recv()
        left.start()
        third.start()
        across.wait_recv()
        right.start()
        fifth.start()

    def last(self, b):
        copies = self.copies(b)
        copies[3].wait_recv()
        copies[4].wait_recv()
        copies[7].start()

    def arrived(self, b, numbers):
        copies = self.copies(b)
        for i in numbers:
            copies[i].wait_recv()

    def drain(self, b):
        for copy in self.copies(b):
            copy.wait_send()


def block_rows(columns, size):
    row = lax.axis_index("tp")
    return lambda s: pl.ds(pl.multiple_of((row + s) % columns * size, size), size)


def expert_kernel(cap, columns, size, *refs):
    (
        attn_in,
        tokens_in,
        cotan_in,
        gate_in,
        up_in,
        down_in,
        gain_ref,
        raw_ref,
        mixed_out,
        ffn_all,
        dx_out,
        out_all,
        x_all,
        d_all,
        hid_all,
        dgu_all,
        x_others,
        dy_others,
        theirs,
        links,
        attn_v,
        tokens_v,
        arrived_v,
        relayed_v,
        mixed_v,
        ffn_v,
        xb,
        db,
        gate_up,
        down,
        xs,
        ds,
        dxs,
        others,
        chip,
        stage,
        hid,
        dgu,
        slot_table,
        weight_table,
        sends,
        arrivals,
        local,
        loads,
        sum_local,
        spill,
    ) = refs
    count = QUARTET
    previous, following = {2: 0, 1: 2, 3: 1}, {0: 2, 2: 1, 1: 3}
    experts, local_hidden = gate_in.shape[:2]
    width = xb.shape[2]
    pad = down.shape[1]
    tile = min(1024, width)
    wide = 2 * cap
    rows_of = block_rows(columns, size)
    partner, along, across = plane_neighbours()
    column = column_neighbours(columns)
    number = 0

    def reserve(amount):
        nonlocal number
        number += amount
        return number - amount

    x_gather = PlaneGather(ffn_all, x_others, rows_of, sends, arrivals, reserve(8 * columns))
    dy_gather = PlaneGather(
        cotan_in, dy_others, lambda b: pl.ds(0, SEQ), sends, arrivals, reserve(8)
    )
    gather = ColumnGather(ffn_all, rows_of, sends, arrivals, reserve(4))
    summed = ColumnSum(attn_in, rows_of, arrived_v, relayed_v, sends, arrivals, reserve(4))
    plane = PlaneSum(
        lambda r, h: others.at[r // 2],
        chip,
        theirs,
        links,
        stage,
        sends,
        arrivals,
        reserve(plane_sum_sizes(columns)[0]),
        sum_local,
    )

    greet([partner, along, across] + column)
    summed.start(local.at[2])
    first = [
        pltpu.make_async_copy(attn_in.at[rows_of(0)], attn_v, local.at[0]),
        pltpu.make_async_copy(tokens_in, tokens_v, local.at[1]),
    ]
    for copy in first:
        copy.start()
    dy_gather.start(0)
    if pad > local_hidden:
        rest = pad - local_hidden
        for e in range(experts):
            for ref, start in ((gate_up, local_hidden), (gate_up, pad + local_hidden), (down, local_hidden)):
                ref[e, start : start + rest, :] = jnp.zeros((rest, width), BF)
    weights_in = []
    for e in range(experts):
        weights_in += [
            pltpu.make_async_copy(
                gate_in.at[e], gate_up.at[e, pl.ds(0, local_hidden)], local.at[3 + 3 * e]
            ),
            pltpu.make_async_copy(
                up_in.at[e], gate_up.at[e, pl.ds(pad, local_hidden)], local.at[4 + 3 * e]
            ),
            pltpu.make_async_copy(
                down_in.at[e], down.at[e, pl.ds(0, local_hidden)], local.at[5 + 3 * e]
            ),
        ]
    for copy in weights_in:
        copy.start()

    summed.clear()
    summed.middle(local.at[2])

    earlier = lax.broadcasted_iota(jnp.int32, (size, size), 0)
    later = lax.broadcasted_iota(jnp.int32, (size, size), 1)
    before = jnp.where(earlier < later, 1.0, 0.0).astype(BF)
    own_first = (lax.axis_index("fsdp") * experts).astype(F32)
    for r in range(8):
        for e in range(experts):
            member = jnp.zeros((1, SEQ), F32)
            weight = jnp.zeros((1, SEQ), F32)
            for pick in range(TOPK):
                same = raw_ref[r, pick : pick + 1, :] == own_first + float(e)
                member = jnp.where(same, 1.0, member)
                weight = weight + jnp.where(
                    same, raw_ref[r, RAW_ROWS + pick : RAW_ROWS + pick + 1, :], 0.0
                )
            slot_table[r * experts + e : r * experts + e + 1, :] = member
            weight_table[r * experts + e : r * experts + e + 1, :] = weight
    second = lax.broadcasted_iota(jnp.int32, (8 * experts, size), 0) // experts % 2
    shift = second.astype(F32) * float(cap)
    for b in range(columns):
        cols = pl.ds(b * size, size)
        member = slot_table[:, cols]
        rank = dot_plain(member.astype(BF), before)
        slot_table[:, cols] = jnp.where(member > 0.5, rank + shift, NO_SLOT)

    for copy in first:
        copy.wait()
    total = summed.total(attn_v[...]) + tokens_v[...].astype(F32)
    mixed_v[...] = total
    inverse = lax.rsqrt(jnp.mean(total * total, axis=1, keepdims=True) + EPSILON)
    ffn_v[...] = (total * inverse * gain_ref[...]).astype(BF)
    own_copy = pltpu.make_async_copy(ffn_v, ffn_all.at[rows_of(0)], local.at[0])
    own_copy.start()
    mixed_copy = pltpu.make_async_copy(mixed_v, mixed_out, local.at[1])
    mixed_copy.start()
    own_copy.wait()

    gather.start()

    def enter(b):
        if b > 0:
            gather.wait(b)
        x_gather.start(b)

    def ready(b):
        x_gather.arrived(b, [2, 5, 6, 7])

    def source(own, gathered, r):
        return own if r == 0 else gathered.at[r - 1]

    def load(b, k):
        own, gathered, target = ((ffn_all, x_others, xb), (cotan_in, dy_others, db))[k]
        return [
            pltpu.make_async_copy(
                source(own, gathered, r).at[rows_of(b)],
                target.at[r // 2, pl.ds(r % 2 * size, size)],
                loads.at[8 * k + r],
            )
            for r in range(8)
        ]

    def slots_of(table, b, q):
        place = pl.ds(pl.multiple_of((lax.axis_index("tp") + b) % columns * size, size), size)
        rows = []
        for e in range(experts):
            low, high = 2 * q * experts + e, (2 * q + 1) * experts + e
            rows.append(
                jnp.concatenate([table[low : low + 1, place], table[high : high + 1, place]], axis=1)
            )
        return jnp.concatenate(rows, axis=0)

    def combine(b, keep):
        for q in range(count):
            entries = slots_of(slot_table, b, q)
            entries = jnp.concatenate(
                [entries, jnp.full((8 - experts, HALF), NO_SLOT, F32)], axis=0
            )
            hit = select_cols(entries.T, experts, wide)
            choose = jnp.where(hit, 1.0, 0.0).astype(BF)

            def gather(n, carry, q=q, choose=choose):
                cols = pl.ds(pl.multiple_of(n * tile, tile), tile)
                keep(q, cols, dot_plain(choose, dxs[q, :, cols]).astype(BF))
                return carry

            lax.fori_loop(0, width // tile, gather, 0)

    def spills(b):
        return [
            pltpu.make_async_copy(xs, x_all.at[b], spill.at[0]),
            pltpu.make_async_copy(ds, d_all.at[b], spill.at[1]),
            pltpu.make_async_copy(hid.at[b], hid_all.at[b], spill.at[2]),
            pltpu.make_async_copy(dgu, dgu_all.at[b], spill.at[3]),
        ]

    def front(b):
        x_load, dy_load = load(b, 0), load(b, 1)
        for copy in x_load + (dy_load if b == 0 else []):
            copy.start()
        if b == 0:
            for copy in weights_in:
                copy.wait()
        if b > 0:
            for copy in spills(previous[b]):
                copy.wait()
        for q in range(count):
            for copy in x_load[2 * q : 2 * q + 2] + dy_load[2 * q : 2 * q + 2]:
                copy.wait()
            hit = select_rows(slots_of(slot_table, b, q), experts, wide)
            weights = slot_weights(hit, slots_of(weight_table, b, q), experts, wide)
            choose = jnp.where(hit, 1.0, 0.0).astype(BF)

            def spread(n, carry, q=q, choose=choose, weights=weights):
                cols = pl.ds(pl.multiple_of(n * tile, tile), tile)
                rows = dot_plain(choose, xb[q, :, cols])
                grads = dot_plain(choose, db[q, :, cols]) * weights
                for e in range(experts):
                    low, high = e * wide, (e + 1) * wide
                    xs[e, q * wide : (q + 1) * wide, cols] = rows[low:high].astype(BF)
                    ds[e, q * wide : (q + 1) * wide, cols] = grads[low:high].astype(BF)
                return carry

            lax.fori_loop(0, width // tile, spread, 0)
        if b in following:
            for copy in load(following[b], 1):
                copy.start()
        out_copies = spills(b)
        out_copies[0].start()
        out_copies[1].start()

        def one_expert(e, carry):
            both = dot_rows(xs[e], gate_up[e])
            gate_pre, up_pre = both[:, :pad], both[:, pad:]
            d_hidden = dot_rows(ds[e], down[e])
            sigmoid = jax.nn.sigmoid(gate_pre)
            silu = gate_pre * sigmoid
            hid[b, e] = (silu * up_pre).astype(BF)
            gate_grad = d_hidden * up_pre * (sigmoid * (1.0 + gate_pre * (1.0 - sigmoid)))
            dgu[e] = jnp.concatenate([gate_grad, d_hidden * silu], axis=1).astype(BF)

            def back(n, inner):
                cols = pl.ds(pl.multiple_of(n * tile, tile), tile)
                part = dot_plain(dgu[e], gate_up[e, :, cols]).astype(BF)
                for q in range(count):
                    dxs[q, pl.ds(pl.multiple_of(e * wide, wide), wide), cols] = part[
                        q * wide : (q + 1) * wide
                    ]
                return inner

            lax.fori_loop(0, width // tile, back, 0)
            return carry

        lax.fori_loop(0, experts, one_expert, 0)
        out_copies[2].start()
        out_copies[3].start()
        if b > 0:
            for i in range(4):
                plane.pair(i, previous[b]).wait_send()

        def keep(q, cols, value):
            chip[q, b, :, cols] = value[:size]
            others[q, :, cols] = value[size:]

        combine(b, keep)
        for i in range(4):
            plane.pair(i, b).start()

    def out_part(b):
        weights = [
            slot_weights(
                select_rows(slots_of(slot_table, b, q), experts, wide),
                slots_of(weight_table, b, q),
                experts,
                wide,
            )
            for q in range(count)
        ]
        for e in range(experts):

            def one_tile(n, carry, e=e):
                cols = pl.ds(pl.multiple_of(n * tile, tile), tile)
                rows = dot_plain(hid[b, e], down[e, :, cols])
                for q in range(count):
                    dxs[q, e * wide : (e + 1) * wide, cols] = (
                        rows[q * wide : (q + 1) * wide] * weights[q][e * wide : (e + 1) * wide]
                    ).astype(BF)
                return carry

            lax.fori_loop(0, width // tile, one_tile, 0)
        if b > 0:
            out_copy(b - 1).wait()

        def keep(q, cols, value):
            db[q, :, cols] = value

        combine(b, keep)
        out_copy(b).start()

    def out_copy(b):
        return pltpu.make_async_copy(db, out_all.at[b], local.at[0])

    final = columns - 1
    enter(0)
    dy_gather.forward(0)
    enter(2)
    x_gather.forward(0)
    enter(1)
    x_gather.last(0)
    dy_gather.last(0)
    ready(0)
    dy_gather.arrived(0, [2, 5, 6, 7])
    front(0)
    x_gather.forward(2)
    enter(3)
    x_gather.forward(1)
    x_gather.last(2)
    ready(2)
    x_gather.last(1)
    front(2)
    x_gather.forward(3)
    ready(1)
    plane.send_first([0], False)
    front(1)
    x_gather.last(3)
    ready(3)
    plane.send_first([2], False)
    plane.send_second([0])
    front(3)
    plane.send_first([1], False)
    plane.send_second([2])
    for copy in spills(3):
        copy.wait()
    out_part(0)
    plane.send_first([3], False)
    plane.send_second([1])
    done = {}

    def close(b):
        plane.finish([b])
        done[b] = pltpu.make_async_copy(chip.at[0, b], dx_out.at[rows_of(b)], loads.at[b])
        done[b].start()

    out_part(1)
    plane.send_second([3])
    close(0)
    out_part(2)
    close(2)
    out_part(3)
    close(1)
    close(3)
    for b in range(columns):
        done[b].wait()
    out_copy(final).wait()
    mixed_copy.wait()

    for b in range(columns):
        x_gather.drain(b)
    dy_gather.drain(0)
    gather.drain()
    summed.drain()
    plane.drain(final)


def expert_call(attn_part, tokens, cotan_all, gate, up, down, gain, raw, cap):
    columns = lax.axis_size("tp")
    size, width = tokens.shape
    experts, local_hidden, _ = gate.shape
    pad = -(-local_hidden // 128) * 128
    slots = 8 * cap
    anywhere = pl.BlockSpec(memory_space=pl.ANY)
    held = pl.BlockSpec(memory_space=pltpu.VMEM)

    def array(*dims, kind=BF):
        return jax.ShapeDtypeStruct(dims, kind)

    landing, scratch = plane_sum_space(columns, size, width)
    remote, near = plane_sum_sizes(columns)
    remote = remote + 8 * columns + 8 + 8
    results = pl.pallas_call(
        functools.partial(expert_kernel, cap, columns, size),
        out_shape=[
            array(size, width, kind=F32),
            array(SEQ, width),
            array(SEQ, width),
            array(columns, QUARTET, HALF, width),
            array(columns, experts, slots, width),
            array(columns, experts, slots, width),
            array(columns, experts, slots, pad),
            array(columns, experts, slots, 2 * pad),
            array(7, SEQ, width),
            array(7, SEQ, width),
        ]
        + landing,
        in_specs=[anywhere] * 6 + [held] * 2,
        out_specs=[anywhere] * 12,
        scratch_shapes=[
            pltpu.VMEM((size, width), BF),
            pltpu.VMEM((size, width), BF),
            pltpu.VMEM((columns - 1, size, width), BF),
            pltpu.VMEM((2, size, width), BF),
            pltpu.VMEM((size, width), F32),
            pltpu.VMEM((size, width), BF),
            pltpu.VMEM((QUARTET, HALF, width), BF),
            pltpu.VMEM((QUARTET, HALF, width), BF),
            pltpu.VMEM((experts, 2 * pad, width), BF),
            pltpu.VMEM((experts, pad, width), BF),
            pltpu.VMEM((experts, slots, width), BF),
            pltpu.VMEM((experts, slots, width), BF),
            pltpu.VMEM((QUARTET, 2 * experts * cap, width), BF),
            pltpu.VMEM((4, size, width), BF),
        ]
        + scratch
        + [
            pltpu.VMEM((columns, experts, slots, pad), BF),
            pltpu.VMEM((experts, slots, 2 * pad), BF),
            pltpu.VMEM((8 * experts, SEQ), F32),
            pltpu.VMEM((8 * experts, SEQ), F32),
            pltpu.SemaphoreType.DMA((remote,)),
            pltpu.SemaphoreType.DMA((remote,)),
            pltpu.SemaphoreType.DMA((3 + 3 * experts,)),
            pltpu.SemaphoreType.DMA((16,)),
            pltpu.SemaphoreType.DMA((near,)),
            pltpu.SemaphoreType.DMA((4,)),
        ],
        compiler_params=pltpu.CompilerParams(
            collective_id=1, has_side_effects=True, vmem_limit_bytes=67_043_328
        ),
        cost_estimate=pl.CostEstimate(
            flops=16 * SEQ * experts * cap * width * 8,
            bytes_accessed=60 * SEQ * width,
            transcendentals=0,
        ),
        name="experts",
    )(attn_part, tokens, cotan_all, gate, up, down, gain, raw)
    return results[:8]


def first_kernel(columns, size, kinds, *refs):
    amount = len(kinds)
    tokens_in, own_in = refs[0], refs[1 : 1 + amount]
    tokens_all, alls = refs[1 + amount], refs[2 + amount : 2 + 2 * amount]
    tokens_v, held = refs[2 + 2 * amount], refs[3 + 2 * amount : 3 + 3 * amount]
    sends, arrivals, local = refs[3 + 3 * amount :]
    partner, along, across = plane_neighbours()
    column = column_neighbours(columns)
    rows_of = block_rows(columns, size)
    place = lax.axis_index("fsdp")
    devices = {
        0: place,
        1: partner[0],
        2: along[0],
        4: across[0],
        6: along[0] + across[0] - place,
    }
    greet([partner, along, across] + column)
    here = [pltpu.make_async_copy(tokens_in, tokens_v, local.at[0])]
    there = [pltpu.make_async_copy(tokens_v, tokens_all.at[rows_of(0)], local.at[0])]
    here[0].start()
    here[0].wait()
    there[0].start()
    there[0].wait()
    gather = ColumnGather(tokens_all, rows_of, sends, arrivals, 8 * amount)
    gather.start()
    plans = []
    for k, kind in enumerate(kinds):
        own, everything = own_in[k], alls[k]
        rows, cols = own.shape
        top, bottom = pl.ds(0, rows // 2), pl.ds(rows // 2, rows // 2)
        whole = pl.ds(0, rows)

        def spot(r, hop, part, kind=kind, everything=everything, cols=cols):
            if kind == "relative":
                return everything.at[r ^ hop, part]
            if kind == "rows":
                return everything.at[devices[r], part]
            start = pl.multiple_of(devices[r] * cols, cols)
            return everything.at[part, pl.ds(start, cols)]

        plan = [
            (own, spot(0, 2, whole), along),
            (own, spot(0, 4, whole), across),
            (own, spot(0, 1, whole), partner),
            (spot(2, 0, top), spot(2, 4, top), across),
            (spot(4, 0, bottom), spot(4, 2, bottom), along),
            (spot(2, 0, whole), spot(2, 1, whole), partner),
            (spot(4, 0, whole), spot(4, 1, whole), partner),
            (spot(6, 0, whole), spot(6, 1, whole), partner),
        ]
        plans.append(
            [
                mesh_copy(src, dst, sends, arrivals, 8 * k + i, device)
                for i, (src, dst, device) in enumerate(plan)
            ]
        )
    for copies in plans:
        for copy in copies[:3]:
            copy.start()
    here, there = [], []
    for k, kind in enumerate(kinds):
        rows, cols = own_in[k].shape
        if kind == "relative":
            spot_here = alls[k].at[0]
        elif kind == "rows":
            spot_here = alls[k].at[place]
        else:
            spot_here = alls[k].at[:, pl.ds(pl.multiple_of(place * cols, cols), cols)]
        here.append(pltpu.make_async_copy(own_in[k], held[k], local.at[1 + k]))
        there.append(pltpu.make_async_copy(held[k], spot_here, local.at[1 + k]))
    for copy in here:
        copy.start()
    for copy in here:
        copy.wait()
    for copy in there:
        copy.start()
    for copies in plans:
        copies[0].wait_recv()
        copies[3].start()
        copies[5].start()
        copies[1].wait_recv()
        copies[4].start()
        copies[6].start()
    gather.wait(2)
    for copies in plans:
        copies[3].wait_recv()
        copies[4].wait_recv()
        copies[7].start()
    for copies in plans:
        for i in (2, 5, 6, 7):
            copies[i].wait_recv()
    gather.wait(1)
    gather.wait(3)
    for copy in there:
        copy.wait()
    gather.drain()
    for copies in plans:
        for copy in copies:
            copy.wait_send()


def first_call(tokens, owns, kinds):
    columns = lax.axis_size("tp")
    size, width = tokens.shape
    anywhere = pl.BlockSpec(memory_space=pl.ANY)
    copies = 8 * len(owns) + 4

    def gathered(own, kind):
        rows, cols = own.shape
        return (rows, 8 * cols) if kind == "columns" else (8, rows, cols)

    return pl.pallas_call(
        functools.partial(first_kernel, columns, size, kinds),
        out_shape=[jax.ShapeDtypeStruct((columns * size, width), BF)]
        + [jax.ShapeDtypeStruct(gathered(own, kind), own.dtype) for own, kind in zip(owns, kinds)],
        in_specs=[anywhere] * (1 + len(owns)),
        out_specs=[anywhere] * (1 + len(owns)),
        scratch_shapes=[pltpu.VMEM((size, width), BF)]
        + [pltpu.VMEM(own.shape, own.dtype) for own in owns]
        + [
            pltpu.SemaphoreType.DMA((copies,)),
            pltpu.SemaphoreType.DMA((copies,)),
            pltpu.SemaphoreType.DMA((1 + len(owns),)),
        ],
        compiler_params=pltpu.CompilerParams(collective_id=2, has_side_effects=True),
        name="first_gather",
    )(tokens, *owns)


class PlaneSum:
    def __init__(self, source, chip, theirs, links, stage, sends, arrivals, base, local):
        self.source, self.chip, self.theirs, self.links = source, chip, theirs, links
        self.stage, self.sends, self.arrivals, self.base = stage, sends, arrivals, base
        self.local = local
        self.parts, self.rows = chip.shape[1], chip.shape[2]
        self.partner, self.along, self.across = plane_neighbours()

    def pair(self, i, h):
        return mesh_copy(
            self.source(2 * i + 1, h),
            self.theirs.at[i, h],
            self.sends,
            self.arrivals,
            self.base + i * self.parts + h,
            self.partner,
        )

    def mine(self, i, h):
        return pltpu.make_async_copy(
            self.source(2 * i, h), self.chip.at[i, h], self.local.at[4 + i * self.parts + h]
        )

    def begin(self):
        for i in (3, 1, 2, 0):
            for h in range(self.parts):
                self.pair(i, h).start()
                self.mine(i, h).start()

    def fetch(self, landed, slot):
        size = landed.shape[0]
        return pltpu.make_async_copy(
            landed, self.stage.at[slot, pl.ds(0, size)], self.local.at[slot]
        )

    def add(self, i, h, start, size, slot):
        some = min(32, size)

        def one(n, carry):
            rows = pl.ds(pl.multiple_of(start + n * some, some), some)
            from_rows = pl.ds(pl.multiple_of(n * some, some), some)
            self.chip[i, h, rows, :] = (
                self.chip[i, h, rows, :].astype(F32) + self.stage[slot, from_rows, :].astype(F32)
            ).astype(BF)
            return carry

        lax.fori_loop(0, size // some, one, 0)

    def send_first(self, parts=None, fetched=True):
        for h in range(self.parts) if parts is None else parts:
            for i in (3, 1, 2, 0):
                self.pair(i, h).wait_recv()
                self.fetch(self.theirs.at[i, h], i).start()
            for i in (3, 1, 2, 0):
                if fetched:
                    self.mine(i, h).wait()
                self.fetch(self.theirs.at[i, h], i).wait()
                self.add(i, h, 0, self.rows, i)
                if i == 3:
                    self.send(1, [h])
                if i == 2:
                    self.send(0, [h])

    def link(self, stage_number, side, h):
        first_hop, second_hop = (
            (self.along, self.across) if side == 0 else (self.across, self.along)
        )
        near, far = (1, 2) if side == 0 else (2, 1)
        i = (near, 3, far)[stage_number]
        place = (stage_number * 2 + side) * self.parts + h
        rows = pl.ds(side * (self.rows // 2), self.rows // 2)
        return mesh_copy(
            self.chip.at[i, h, rows],
            self.links.at[place],
            self.sends,
            self.arrivals,
            self.base + 4 * self.parts + place,
            second_hop if stage_number == 2 else first_hop,
        )

    def landed(self, stage_number, side, h):
        return self.links.at[(stage_number * 2 + side) * self.parts + h]

    def send(self, stage_number, parts=None):
        for h in range(self.parts) if parts is None else parts:
            for side in range(2):
                self.link(stage_number, side, h).start()

    def send_second(self, parts=None):
        half = self.rows // 2
        for h in range(self.parts) if parts is None else parts:
            for side in range(2):
                self.link(1, side, h).wait_recv()
                self.fetch(self.landed(1, side, h), side).start()
            for side in range(2):
                self.fetch(self.landed(1, side, h), side).wait()
                self.add((2, 1)[side], h, side * half, half, side)
                self.link(2, side, h).start()

    def finish(self, parts=None):
        half = self.rows // 2
        for h in range(self.parts) if parts is None else parts:
            for stage_number in (0, 2):
                for side in range(2):
                    self.link(stage_number, side, h).wait_recv()
                    self.fetch(self.landed(stage_number, side, h), stage_number + side).start()
            for stage_number in (0, 2):
                for side in range(2):
                    slot = stage_number + side
                    self.fetch(self.landed(stage_number, side, h), slot).wait()
                    self.add(0, h, side * half, half, slot)

    def drain(self, first_part=0):
        for h in range(self.parts):
            for i in range(4):
                if h >= first_part:
                    self.pair(i, h).wait_send()
            for stage_number in range(3):
                for side in range(2):
                    self.link(stage_number, side, h).wait_send()


def plane_sum_sizes(parts):
    return 10 * parts, 4 + 4 * parts


def plane_sum_space(parts, rows, width):
    landing = [
        jax.ShapeDtypeStruct((4, parts, rows, width), BF),
        jax.ShapeDtypeStruct((6 * parts, rows // 2, width), BF),
    ]
    scratch = [pltpu.VMEM((4, parts, rows, width), BF), pltpu.VMEM((4, rows, width), BF)]
    return landing, scratch


def middle_kernel(columns, size, experts, steps, local_hidden, *refs):
    (
        d_ffn_in,
        mixed_in,
        cotan_in,
        gain_ref,
        out_all,
        x_all,
        d_all,
        hid_all,
        dgu_all,
        d_mixed_out,
        d_proj_all,
        gain_out,
        routed_out,
        gate_grad,
        up_grad,
        down_grad,
        theirs,
        links,
        chip,
        stage,
        own_v,
        arrived_v,
        relayed_v,
        mixed_v,
        cotan_v,
        proj_v,
        xk,
        dk,
        hk,
        gk,
        totals,
        sends,
        arrivals,
        local,
        sum_local,
        work,
        written,
    ) = refs
    partner, along, across = plane_neighbours()
    column = column_neighbours(columns)
    greet([partner, along, across] + column)
    plane = PlaneSum(
        lambda r, h: out_all.at[h, r // 2, pl.ds(r % 2 * size, size)],
        chip,
        theirs,
        links,
        stage,
        sends,
        arrivals,
        0,
        sum_local,
    )
    base = plane_sum_sizes(columns)[0]
    rows_of = block_rows(columns, size)
    summed = ColumnSum(d_ffn_in, rows_of, arrived_v, relayed_v, sends, arrivals, base)
    gather = ColumnGather(d_proj_all, rows_of, sends, arrivals, base + 4)
    summed.start(local.at[3])
    first = [
        pltpu.make_async_copy(d_ffn_in.at[rows_of(0)], own_v, local.at[0]),
        pltpu.make_async_copy(mixed_in, mixed_v, local.at[1]),
        pltpu.make_async_copy(cotan_in, cotan_v, local.at[2]),
    ]
    for copy in first:
        copy.start()
    plane.begin()
    summed.clear()

    width = xk.shape[2]
    pad = hk.shape[2]
    tile = min(1024, width)
    jobs = [(e, step) for e in range(experts) for step in range(steps)]

    def fetch(k):
        e, step = jobs[k]
        slot = k % 2
        return [
            pltpu.make_async_copy(x_all.at[step, e], xk.at[slot], work.at[slot, 0]),
            pltpu.make_async_copy(d_all.at[step, e], dk.at[slot], work.at[slot, 1]),
            pltpu.make_async_copy(hid_all.at[step, e], hk.at[slot], work.at[slot, 2]),
            pltpu.make_async_copy(dgu_all.at[step, e], gk.at[slot], work.at[slot, 3]),
        ]

    def write(e):
        return [
            pltpu.make_async_copy(
                totals.at[e % 2, i, pl.ds(0, local_hidden)], grad.at[e], written.at[e % 2, i]
            )
            for i, grad in enumerate((gate_grad, up_grad, down_grad))
        ]

    def job(k):
        e, step = jobs[k]
        slot, place = k % 2, e % 2
        if k + 1 < len(jobs):
            for copy in fetch(k + 1):
                copy.start()
        for copy in fetch(k):
            copy.wait()
        if step == 0 and e > 1:
            for copy in write(e - 2):
                copy.wait()

        def one(n, carry):
            cols = pl.ds(pl.multiple_of(n * tile, tile), tile)
            found = [
                dot_first(gk[slot, :, :pad], xk[slot, :, cols]),
                dot_first(gk[slot, :, pad:], xk[slot, :, cols]),
                dot_first(hk[slot], dk[slot, :, cols]),
            ]
            for i, value in enumerate(found):
                if step == 0:
                    totals[place, i, :, cols] = value
                else:
                    totals[place, i, :, cols] += value
            return carry

        lax.fori_loop(0, width // tile, one, 0)
        if step == steps - 1:
            for copy in write(e):
                copy.start()

    for copy in fetch(0):
        copy.start()
    for k in range(2):
        job(k)
    summed.middle(local.at[3])
    early = len(jobs) // 2
    late = 3 * len(jobs) // 4
    for k in range(2, early):
        job(k)
    plane.send_first()
    for k in range(early, late):
        job(k)

    for copy in first:
        copy.wait()
    total = summed.total(own_v[...])
    mixed = mixed_v[...]
    inverse = lax.rsqrt(jnp.mean(mixed * mixed, axis=1, keepdims=True) + EPSILON)
    unit = mixed * inverse
    scaled = total * gain_ref[...]
    gain_out[...] = jnp.sum(total * unit, axis=0, keepdims=True)
    back = inverse * (scaled - unit * jnp.mean(scaled * unit, axis=1, keepdims=True))
    d_mixed = cotan_v[...].astype(F32) + back
    mixed_v[...] = d_mixed
    proj_v[...] = d_mixed.astype(BF)
    own_copy = pltpu.make_async_copy(proj_v, d_proj_all.at[rows_of(0)], local.at[0])
    own_copy.start()
    mixed_copy = pltpu.make_async_copy(mixed_v, d_mixed_out, local.at[1])
    mixed_copy.start()
    own_copy.wait()
    gather.start()
    for k in range(late, len(jobs)):
        job(k)
    plane.send_second()
    gather.wait(2)
    plane.finish()
    done = [
        pltpu.make_async_copy(chip.at[0, h], routed_out.at[rows_of(h)], sum_local.at[4 + h])
        for h in range(columns)
    ]
    for copy in done:
        copy.start()
    gather.wait(1)
    gather.wait(3)
    for copy in done + [mixed_copy]:
        copy.wait()
    for e in range(max(0, experts - 2), experts):
        for copy in write(e):
            copy.wait()
    plane.drain()
    gather.drain()
    summed.drain()


def middle_call(d_ffn, mixed, cotan, gain, out_all, kept, local_hidden):
    columns = lax.axis_size("tp")
    size, width = cotan.shape
    x_all, d_all, hid_all, dgu_all = kept
    steps, experts, slots, pad = hid_all.shape
    anywhere = pl.BlockSpec(memory_space=pl.ANY)
    held = pl.BlockSpec(memory_space=pltpu.VMEM)
    landing, scratch = plane_sum_space(columns, size, width)
    remote, near = plane_sum_sizes(columns)
    remote = remote + 8
    grad = jax.ShapeDtypeStruct((experts, local_hidden, width), F32)
    results = pl.pallas_call(
        functools.partial(middle_kernel, columns, size, experts, steps, local_hidden),
        out_shape=[
            jax.ShapeDtypeStruct((size, width), F32),
            jax.ShapeDtypeStruct((SEQ, width), BF),
            jax.ShapeDtypeStruct((1, width), F32),
            jax.ShapeDtypeStruct((SEQ, width), BF),
            grad,
            grad,
            grad,
        ]
        + landing,
        in_specs=[anywhere] * 3 + [held] + [anywhere] * 5,
        out_specs=[anywhere] * 2 + [held] + [anywhere] * 6,
        scratch_shapes=scratch
        + [
            pltpu.VMEM((size, width), BF),
            pltpu.VMEM((columns - 1, size, width), BF),
            pltpu.VMEM((2, size, width), BF),
            pltpu.VMEM((size, width), F32),
            pltpu.VMEM((size, width), BF),
            pltpu.VMEM((size, width), BF),
            pltpu.VMEM((2, slots, width), BF),
            pltpu.VMEM((2, slots, width), BF),
            pltpu.VMEM((2, slots, pad), BF),
            pltpu.VMEM((2, slots, 2 * pad), BF),
            pltpu.VMEM((2, 3, pad, width), F32),
            pltpu.SemaphoreType.DMA((remote,)),
            pltpu.SemaphoreType.DMA((remote,)),
            pltpu.SemaphoreType.DMA((4,)),
            pltpu.SemaphoreType.DMA((near,)),
            pltpu.SemaphoreType.DMA((2, 4)),
            pltpu.SemaphoreType.DMA((2, 3)),
        ],
        compiler_params=pltpu.CompilerParams(
            collective_id=3, has_side_effects=True, vmem_limit_bytes=67_043_328
        ),
        cost_estimate=pl.CostEstimate(
            flops=2 * 3 * steps * experts * slots * width * pad,
            bytes_accessed=40 * SEQ * width,
            transcendentals=0,
        ),
        name="middle",
    )(d_ffn, mixed, cotan, gain, out_all, x_all, d_all, hid_all, dgu_all)
    return results[:7]


def last_kernel(columns, size, latent_start, latent_width, *refs):
    (
        d_normed_in,
        tokens_in,
        d_mixed_in,
        gain_ref,
        joint_in,
        up_in,
        out_in,
        sums_in,
        grad_out,
        joint_out,
        up_out,
        out_out,
        latent_out,
        sums_out,
        joint_theirs,
        joint_links,
        up_theirs,
        up_links,
        out_theirs,
        out_links,
        joint_chip,
        joint_stage,
        up_chip,
        up_stage,
        out_chip,
        out_stage,
        own_v,
        arrived_v,
        relayed_v,
        tokens_v,
        mixed_v,
        running,
        sums_v,
        latent_v,
        sends,
        arrivals,
        local,
        joint_local,
        up_local,
        out_local,
    ) = refs
    partner, along, across = plane_neighbours()
    column = column_neighbours(columns)
    place, row = lax.axis_index("fsdp"), lax.axis_index("tp")
    core, right, above = place % 2, (place // 2) % 2, place // 4

    def absolute(r):
        return (
            (above + r // 4) % 2 * 4 + (right + r // 2 % 2) % 2 * 2 + (core + r % 2) % 2
        )

    greet([partner, along, across] + column)
    each = plane_sum_sizes(1)[0]
    joint_rows, up_rows = joint_chip.shape[2], up_chip.shape[2]
    out_cols = out_chip.shape[3]

    def by_rows(ref, count):
        return lambda r, h: ref.at[pl.ds(pl.multiple_of(absolute(r) * count, count), count)]

    joint = PlaneSum(
        by_rows(joint_in, joint_rows),
        joint_chip,
        joint_theirs,
        joint_links,
        joint_stage,
        sends,
        arrivals,
        0,
        joint_local,
    )
    up = PlaneSum(
        by_rows(up_in, up_rows),
        up_chip,
        up_theirs,
        up_links,
        up_stage,
        sends,
        arrivals,
        each,
        up_local,
    )
    out = PlaneSum(
        lambda r, h: out_in.at[
            :, pl.ds(pl.multiple_of(absolute(r) * out_cols, out_cols), out_cols)
        ],
        out_chip,
        out_theirs,
        out_links,
        out_stage,
        sends,
        arrivals,
        2 * each,
        out_local,
    )
    base = 3 * each
    rows_of = block_rows(columns, size)
    summed = ColumnSum(d_normed_in, rows_of, arrived_v, relayed_v, sends, arrivals, base)
    base = base + 4
    summed.start(local.at[4])
    first = [
        pltpu.make_async_copy(d_normed_in.at[rows_of(0)], own_v, local.at[0]),
        pltpu.make_async_copy(tokens_in, tokens_v, local.at[1]),
        pltpu.make_async_copy(d_mixed_in, mixed_v, local.at[2]),
        pltpu.make_async_copy(sums_in, running.at[0], local.at[3]),
    ]
    for copy in first:
        copy.start()
    for part in (out, joint, up):
        part.begin()
    summed.clear()
    first[3].wait()

    def small(i, device):
        return mesh_copy(running.at[i], sums_v.at[i], sends, arrivals, base + i, device)

    hops = [small(i, device) for i, device in enumerate((partner, along, across))]
    for i, copy in enumerate(hops):
        copy.start()
        copy.wait_recv()
        running[i + 1] = running[i] + sums_v[i]
    gains = [
        mesh_copy(running.at[3], sums_v.at[2 + s], sends, arrivals, base + 2 + s, column[s - 1])
        for s in range(1, columns)
    ]
    base = base + 2 + columns
    for copy in gains:
        copy.start()
    summed.middle(local.at[4])
    for part in (out, joint, up):
        part.send_first()
    for part in (out, joint, up):
        part.send_second()
    for part in (out, joint, up):
        part.finish()

    pieces = joint_rows // columns
    across_columns = [
        mesh_copy(
            joint_chip.at[
                0,
                0,
                pl.ds(pl.multiple_of((row + s) % columns * pieces, pieces), pieces),
                pl.ds(latent_start, latent_width),
            ],
            latent_v.at[s - 1],
            sends,
            arrivals,
            base + s - 1,
            column[s - 1],
        )
        for s in range(1, columns)
    ]
    for copy in across_columns:
        copy.start()
    done = [
        pltpu.make_async_copy(joint_chip.at[0, 0], joint_out, joint_local.at[4]),
        pltpu.make_async_copy(up_chip.at[0, 0], up_out, up_local.at[4]),
        pltpu.make_async_copy(out_chip.at[0, 0], out_out, out_local.at[4]),
    ]
    for copy in done:
        copy.start()

    for copy in first[:3]:
        copy.wait()
    total = summed.total(own_v[...])
    tokens = tokens_v[...].astype(F32)
    inverse = lax.rsqrt(jnp.mean(tokens * tokens, axis=1, keepdims=True) + EPSILON)
    unit = tokens * inverse
    scaled = total * gain_ref[...]
    mixed_v[...] = mixed_v[...] + inverse * (
        scaled - unit * jnp.mean(scaled * unit, axis=1, keepdims=True)
    )
    grad_copy = pltpu.make_async_copy(mixed_v, grad_out, local.at[0])
    grad_copy.start()
    gathered = running[3]
    for s in range(1, columns):
        gains[s - 1].wait_recv()
        gathered = gathered + sums_v[2 + s]
    sums_out[...] = gathered
    latent = joint_chip[
        0,
        0,
        pl.ds(pl.multiple_of(row * pieces, pieces), pieces),
        pl.ds(latent_start, latent_width),
    ].astype(F32)
    for s in range(1, columns):
        across_columns[s - 1].wait_recv()
        latent = latent + latent_v[s - 1].astype(F32)
    latent_out[...] = latent
    for copy in done + [grad_copy]:
        copy.wait()
    for part in (out, joint, up):
        part.drain()
    summed.drain()
    for copy in hops + gains + across_columns:
        copy.wait_send()


def last_call(d_normed, tokens, d_mixed, gain, joint, up, out, sums, latent_start, latent_width):
    columns = lax.axis_size("tp")
    size, width = tokens.shape
    anywhere = pl.BlockSpec(memory_space=pl.ANY)
    held = pl.BlockSpec(memory_space=pltpu.VMEM)
    shapes = [
        (joint.shape[0] // 8, joint.shape[1]),
        (up.shape[0] // 8, up.shape[1]),
        (out.shape[0], out.shape[1] // 8),
    ]
    landing, scratch = [], []
    for rows, cols in shapes:
        one = plane_sum_space(1, rows, cols)
        landing, scratch = landing + one[0], scratch + one[1]
    remote, near = plane_sum_sizes(1)
    remote = 3 * remote + 2 * (columns - 1) + 7
    pieces = shapes[0][0] // columns
    return pl.pallas_call(
        functools.partial(last_kernel, columns, size, latent_start, latent_width),
        out_shape=[jax.ShapeDtypeStruct((size, width), F32)]
        + [jax.ShapeDtypeStruct(shape, BF) for shape in shapes]
        + [
            jax.ShapeDtypeStruct((pieces, latent_width), F32),
            jax.ShapeDtypeStruct(sums.shape, F32),
        ]
        + landing,
        in_specs=[anywhere] * 3 + [held] + [anywhere] * 4,
        out_specs=[anywhere] * 4 + [held] * 2 + [anywhere] * 6,
        scratch_shapes=scratch
        + [
            pltpu.VMEM((size, width), BF),
            pltpu.VMEM((columns - 1, size, width), BF),
            pltpu.VMEM((2, size, width), BF),
            pltpu.VMEM((size, width), BF),
            pltpu.VMEM((size, width), F32),
            pltpu.VMEM((4,) + sums.shape, F32),
            pltpu.VMEM((2 + columns,) + sums.shape, F32),
            pltpu.VMEM((columns - 1, pieces, latent_width), BF),
            pltpu.SemaphoreType.DMA((remote,)),
            pltpu.SemaphoreType.DMA((remote,)),
            pltpu.SemaphoreType.DMA((5,)),
            pltpu.SemaphoreType.DMA((near,)),
            pltpu.SemaphoreType.DMA((near,)),
            pltpu.SemaphoreType.DMA((near,)),
        ],
        compiler_params=pltpu.CompilerParams(
            collective_id=4, has_side_effects=True, vmem_limit_bytes=48 * 1024 * 1024
        ),
        name="last_sums",
    )(d_normed, tokens, d_mixed, gain, joint, up, out, sums)[:6]


def plane_units(count):
    return [[(2 * i + j // 2, j % 2) for j in range(4)] for i in range(count // 2)]


def plane_gather(rows, count):
    gathered = lax.all_gather(rows, "fsdp", axis=0)
    return {
        (r, h): gathered[r, h * HALF : (h + 1) * HALF] for r in range(count) for h in (0, 1)
    }


def plane_scatter_whole(pairs, units, count):
    parts = {}
    for unit, pair in zip(units, pairs):
        for q, key in enumerate(unit):
            parts[key] = pair[q // 2][q % 2]
    stacked = jnp.concatenate([parts[r, h] for r in range(count) for h in (0, 1)], axis=0)
    return lax.psum_scatter(stacked, "fsdp", scatter_dimension=0, tiled=True).astype(F32)


def sum_everywhere(values):
    for axis_name in ("fsdp", "tp"):
        count = lax.axis_size(axis_name)
        if is_power(count):
            bit = 1
            while bit < count:
                values = values + swap(values, axis_name, bit)
                bit *= 2
        else:
            values = lax.psum(values, axis_name)
    return values


def expert_tables(expert_ids, expert_wts, local_experts, units, cap):
    fsdp_count = lax.axis_size("fsdp")
    fsdp_rank = lax.axis_index("fsdp")
    expert_count = local_experts * fsdp_count
    names = jnp.arange(expert_count, dtype=jnp.int32)[:, None]
    member = jnp.zeros((expert_count, SEQ), jnp.bool_)
    weight = jnp.zeros((expert_count, SEQ), F32)
    ids_rows, wts_rows = expert_ids.T, expert_wts.T
    for pick in range(TOPK):
        same = ids_rows[pick : pick + 1] == names
        member = member | same
        weight = weight + jnp.where(same, wts_rows[pick : pick + 1], 0.0)
    position = jnp.arange(HALF)
    before = (position[:, None] < position[None, :]).astype(BF)
    rank = jnp.dot(
        member.astype(BF).reshape(expert_count * 2, HALF), before, preferred_element_type=F32
    ).reshape(expert_count, SEQ)
    slot = jnp.where(member, rank, NO_SLOT)
    table = jnp.concatenate([slot, weight], axis=0)
    table = lax.all_gather(table, "fsdp", axis=0, tiled=True)
    table = table.reshape(fsdp_count, 2, fsdp_count, local_experts, 2, HALF)
    table = lax.dynamic_index_in_dim(table, fsdp_rank, axis=2, keepdims=False)
    slot_steps, weight_steps = [], []
    for unit in units:
        slot_steps.append(jnp.stack([table[r, 0, :, h] for r, h in unit]))
        weight_steps.append(jnp.stack([table[r, 1, :, h] for r, h in unit]))
    slot_row, weight_row = jnp.stack(slot_steps), jnp.stack(weight_steps)
    return (slot_row, weight_row, jnp.swapaxes(slot_row, 2, 3))


def per_device(
    block_in,
    out_cotan,
    segment_ids,
    expert_ids,
    expert_wts,
    attn_gain,
    query_proj,
    latent_proj,
    latent_gain,
    latent_up,
    out_proj,
    ffn_gain,
    shared_gate,
    shared_up,
    shared_down,
    routed_gate,
    routed_up,
    routed_down,
):
    tp_count = lax.axis_size("tp")
    fsdp_count = lax.axis_size("fsdp")
    tp_rank = lax.axis_index("tp")
    fsdp_rank = lax.axis_index("fsdp")
    tok_rows, model_width = block_in.shape
    local_experts, local_hidden = routed_gate.shape[:2]
    expert_count = local_experts * fsdp_count
    cap_rows = tok_rows * TOPK * 4 // (3 * expert_count)
    cap = cap_rows * (HALF // tok_rows)
    paired = fsdp_count == 8 and tp_count == 4 and tok_rows * 2 == HALF
    heads_local = H // tp_count
    head_width = NOPE + ROPE
    score_scale = head_width ** (-0.5)
    shard_rows, query_cols = query_proj.shape
    latent_cols = latent_proj.shape[1]
    up_cols = latent_up.shape[1]
    out_rows = out_proj.shape[0]

    joint = query_cols + latent_cols
    spare = (-joint) % 128
    spare = spare + 128 if spare < 3 else spare
    gains = jnp.concatenate(
        [
            attn_gain[:, None],
            ffn_gain[:, None],
            jnp.pad(latent_gain, (0, shard_rows - latent_gain.shape[0]))[:, None],
            jnp.zeros((shard_rows, spare - 3), BF),
        ],
        axis=1,
    )
    packed = jnp.concatenate([query_proj, latent_proj, gains], axis=1)
    shared_weight = lax.all_gather(
        jnp.concatenate([shared_gate, shared_up], axis=1), "fsdp", axis=0, tiled=True
    )
    if paired:
        low, high = (0, RAW_ROWS - TOPK), (0, 0)
        raw = jnp.concatenate(
            [jnp.pad(expert_ids.T.astype(F32), (low, high)), jnp.pad(expert_wts.T, (low, high))]
        )
        tokens_all, packed_all, latent_up_weight, out_weight, raw = first_call(
            block_in,
            [packed, latent_up, out_proj, raw],
            ("rows", "rows", "columns", "relative"),
        )
        packed_all = packed_all.reshape(-1, packed.shape[1])
        latent_up_weight = latent_up_weight.reshape(LAT, up_cols)
    else:
        packed_all = lax.all_gather(packed, "fsdp", axis=0, tiled=True)
        latent_up_weight = lax.all_gather(latent_up, "fsdp", axis=0, tiled=True)
        out_weight = lax.all_gather(out_proj, "fsdp", axis=1, tiled=True)
        tokens_all = column_gather(block_in)
    cotan_own, tokens_all, shared_weight = tie(out_cotan, tokens_all, shared_weight)
    cotan_all = column_gather(cotan_own)
    shared_down_weight = lax.all_gather(shared_down, "fsdp", axis=1, tiled=True)
    gain_attn = packed_all[:, joint].astype(F32)
    gain_ffn = packed_all[:, joint + 1].astype(F32)
    gain_latent = (
        packed_all[:, joint + 2]
        .reshape(fsdp_count, shard_rows)[:, : latent_gain.shape[0]]
        .reshape(LAT)
        .astype(F32)
    )
    shared_cols = shared_gate.shape[1]

    def scatter(part, dimension):
        return lax.psum_scatter(part.astype(BF), "fsdp", scatter_dimension=dimension, tiled=True)

    unit_all, inverse_all = norm_parts(tokens_all.astype(F32))
    normed_all = (unit_all * gain_attn).astype(BF)
    joint_rows = jnp.dot(normed_all, packed_all, preferred_element_type=F32)
    queries = joint_rows[:, :query_cols].reshape(SEQ, heads_local, head_width)
    latent = joint_rows[:, query_cols:joint]
    unit_lat, inverse_lat = norm_parts(latent[:, :LAT])
    positions = jnp.arange(SEQ, dtype=jnp.int32)
    cosine, sine_part = rope_tables(positions, ROPE)
    compressed_all = (unit_lat * gain_latent).astype(BF)
    key_rope_all = rotate(latent[:, LAT:], cosine, sine_part).astype(BF)
    query_cat = jnp.concatenate(
        [
            queries[:, :, :NOPE],
            rotate(queries[:, :, NOPE:], cosine[:, None, :], sine_part[:, None, :]),
        ],
        axis=2,
    ).astype(BF)
    key_value = (
        jnp.dot(compressed_all, latent_up_weight, preferred_element_type=F32)
        .reshape(SEQ, heads_local, NOPE + DV)
        .astype(BF)
    )
    key_cat = jnp.concatenate(
        [
            key_value[:, :, :NOPE],
            jnp.broadcast_to(key_rope_all[:, None, :], (SEQ, heads_local, ROPE)),
        ],
        axis=2,
    )
    values = key_value[:, :, NOPE:]
    allowed = (positions[None, :] <= positions[:, None]) & (
        segment_ids[None, :] == segment_ids[:, None]
    )
    raw_scores = (
        jnp.einsum("qhd,khd->hqk", query_cat, key_cat, preferred_element_type=F32) * score_scale
    )
    masked = jnp.where(allowed[None], raw_scores, MASK_FILL)
    top_score = jnp.max(masked, axis=2, keepdims=True)
    exponent = jnp.exp(masked - top_score)
    row_total = jnp.sum(exponent, axis=2, keepdims=True)
    probabilities = exponent / row_total
    probs_low = probabilities.astype(BF)
    attended = (
        jnp.einsum("hqk,khd->qhd", probs_low, values, preferred_element_type=F32)
        .reshape(SEQ, heads_local * DV)
        .astype(BF)
    )
    attn_part = jnp.dot(attended, out_weight, preferred_element_type=F32).astype(BF)
    if paired:
        mixed_rows, normed_ffn_all, d_routed_in, out_array, *kept = expert_call(
            attn_part,
            block_in,
            cotan_all,
            routed_gate,
            routed_up,
            routed_down,
            gain_ffn[None, :],
            raw,
            cap_rows,
        )
        unit_two, inverse_two = norm_parts(mixed_rows)
        d_routed_in = d_routed_in.astype(F32)
    else:
        units = plane_units(fsdp_count)
        tables = expert_tables(expert_ids, expert_wts, local_experts, units, cap)
        hidden_pad = -(-local_hidden // 128) * 128
        lift = ((0, 0), (0, hidden_pad - local_hidden), (0, 0))
        routed_gate_up = jnp.concatenate(
            [jnp.pad(routed_gate, lift), jnp.pad(routed_up, lift)], axis=1
        )
        routed_down_pad = jnp.pad(routed_down, lift)
        mixed_rows = block_in.astype(F32) + column_scatter(attn_part)
        unit_two, inverse_two = norm_parts(mixed_rows)
        normed_ffn_all = column_gather((unit_two * gain_ffn).astype(BF))
        x_blocks = plane_gather(normed_ffn_all, fsdp_count)
        dy_all = lax.all_gather(cotan_all, "fsdp", axis=0, tiled=True)
        kept = []
        dx_pairs = []
        for step, unit in enumerate(units):
            pair, kept = expert_front(
                step,
                len(units),
                [x_blocks[key] for key in unit],
                jnp.array([2 * r + h for r, h in unit], jnp.int32),
                dy_all,
                routed_gate_up,
                routed_down_pad,
                tables,
                kept,
                cap,
            )
            dx_pairs.append(pair)
        near, far = expert_out(kept[2], routed_down_pad, tables, cap)
        d_routed_in = plane_scatter_whole(dx_pairs, units, fsdp_count)
    if not paired:
        routed_gate_grad, routed_up_grad, routed_down_grad = expert_grads(kept, local_hidden)

    shared_pre = jnp.dot(normed_ffn_all, shared_weight, preferred_element_type=F32)
    shared_gate_pre, shared_up_pre = shared_pre[:, :shared_cols], shared_pre[:, shared_cols:]
    shared_hidden = (jax.nn.silu(shared_gate_pre) * shared_up_pre).astype(BF)
    shared_rows = jnp.dot(shared_hidden, shared_down_weight, preferred_element_type=F32)
    shared_down_part = jnp.dot(shared_hidden.T, cotan_all, preferred_element_type=F32)
    d_shared_hidden = jnp.dot(cotan_all, shared_down_weight.T, preferred_element_type=F32)
    d_shared = jnp.concatenate(silu_back(d_shared_hidden, shared_gate_pre, shared_up_pre), axis=1)
    shared_part = jnp.dot(normed_ffn_all.T, d_shared, preferred_element_type=F32)
    d_shared_in = jnp.dot(d_shared, shared_weight.T, preferred_element_type=F32)

    if paired:
        d_ffn_rows, shared_part, shared_down_part = tie(
            (d_shared_in + d_routed_in).astype(BF),
            shared_part.astype(BF),
            shared_down_part.astype(BF),
        )
        (
            d_mixed,
            d_proj_all,
            ffn_gain_part,
            routed_rows,
            routed_gate_grad,
            routed_up_grad,
            routed_down_grad,
        ) = middle_call(
            d_ffn_rows, mixed_rows, out_cotan, gain_ffn[None, :], out_array, kept, local_hidden
        )
        ffn_gain_part = ffn_gain_part[0]
        routed_rows = routed_rows.astype(F32)
    else:
        d_normed_ffn = column_scatter(d_shared_in + d_routed_in)
        out_pairs = [(near[step], far[step]) for step in range(len(units))]
        routed_rows = plane_scatter_whole(out_pairs, units, fsdp_count)
        ffn_gain_part, d_mixed_norm = norm_back(d_normed_ffn, unit_two, inverse_two, gain_ffn)
        d_mixed = out_cotan.astype(F32) + d_mixed_norm
        d_proj_all = column_gather(d_mixed.astype(BF))
    shared_grad = scatter(shared_part, 0)
    d_proj_all, shared_grad = tie(d_proj_all, shared_grad)
    ffn_rows = column_scatter(shared_rows + routed_rows)
    block_out = (mixed_rows + ffn_rows).astype(BF)

    out_part = jnp.dot(attended.T, d_proj_all, preferred_element_type=F32)
    d_attended = (
        jnp.dot(d_proj_all, out_weight.T, preferred_element_type=F32)
        .astype(BF)
        .reshape(SEQ, heads_local, DV)
    )
    prob_grad = jnp.einsum("qhd,khd->hqk", d_attended, values, preferred_element_type=F32)
    score_grad = (
        probabilities
        * (prob_grad - jnp.sum(probabilities * prob_grad, axis=2, keepdims=True))
    ).astype(BF)
    query_grad = (
        jnp.einsum("hqk,khd->qhd", score_grad, key_cat, preferred_element_type=F32) * score_scale
    )
    key_grad = (
        jnp.einsum("hqk,qhd->khd", score_grad, query_cat, preferred_element_type=F32) * score_scale
    )
    value_grad = jnp.einsum("hqk,qhd->khd", probs_low, d_attended, preferred_element_type=F32)
    d_queries = (
        jnp.concatenate(
            [
                query_grad[:, :, :NOPE],
                unrotate(query_grad[:, :, NOPE:], cosine[:, None, :], sine_part[:, None, :]),
            ],
            axis=2,
        )
        .reshape(SEQ, heads_local * head_width)
        .astype(BF)
    )
    d_key_value = (
        jnp.concatenate([key_grad[:, :, :NOPE], value_grad], axis=2)
        .reshape(SEQ, heads_local * (NOPE + DV))
        .astype(BF)
    )
    latent_up_part = jnp.dot(compressed_all.T, d_key_value, preferred_element_type=F32)
    d_compressed = jnp.dot(d_key_value, latent_up_weight.T, preferred_element_type=F32)
    d_key_rope = jnp.sum(key_grad[:, :, NOPE:], axis=1)
    latent_gain_part, d_latent_main = norm_back(d_compressed, unit_lat, inverse_lat, gain_latent)
    d_latent = jnp.concatenate(
        [d_latent_main, unrotate(d_key_rope, cosine, sine_part)], axis=1
    ).astype(BF)
    d_joint = jnp.concatenate([d_queries, d_latent, jnp.zeros((SEQ, spare), BF)], axis=1)
    joint_part = jnp.dot(normed_all.T, d_joint, preferred_element_type=F32)
    d_normed_part = jnp.dot(d_joint, packed_all.T, preferred_element_type=F32)
    attn_gain_part = jnp.sum(d_normed_part * unit_all, axis=0)

    gain_parts = jnp.concatenate([attn_gain_part, latent_gain_part, ffn_gain_part]).reshape(
        -1, 128
    )
    joint_part = joint_part.astype(BF)
    shared_down_grad = scatter(shared_down_part, 1)
    if paired:
        latent_width = joint_part.shape[1] - query_cols
        (
            block_in_grad,
            joint_grad,
            latent_up_grad,
            out_proj_grad,
            latent_proj_grad,
            gain_sums,
        ) = last_call(
            d_normed_part.astype(BF),
            block_in,
            d_mixed,
            gain_attn[None, :],
            joint_part,
            latent_up_part.astype(BF),
            out_part.astype(BF),
            gain_parts,
            query_cols,
            latent_width,
        )
        latent_proj_grad = latent_proj_grad[:, :latent_cols]
    else:
        d_normed = column_scatter(d_normed_part)
        unit_one, inverse_one = norm_parts(block_in.astype(F32))
        _, d_tokens_norm = norm_back(d_normed, unit_one, inverse_one, gain_attn)
        block_in_grad = d_mixed + d_tokens_norm
        out_proj_grad = scatter(out_part, 1)
        latent_up_grad = scatter(latent_up_part, 0)
        joint_grad = scatter(joint_part, 0)
        latent_proj_grad = column_scatter(joint_grad[:, query_cols:joint])
        gain_sums = sum_everywhere(gain_parts)
    gain_sums = gain_sums.reshape(-1)
    query_proj_grad = joint_grad[:, :query_cols].astype(F32)
    latent_up_grad = latent_up_grad.astype(F32)
    out_proj_grad = out_proj_grad.astype(F32)
    shared_grad = shared_grad.astype(F32)
    shared_gate_grad, shared_up_grad = shared_grad[:, :shared_cols], shared_grad[:, shared_cols:]
    shared_down_grad = shared_down_grad.astype(F32)
    device = fsdp_rank * tp_count + tp_rank
    devices = tp_count * fsdp_count

    def own_gain(start, size):
        return lax.dynamic_slice(gain_sums, (start + device * (size // devices),), (size // devices,))

    attn_gain_grad = own_gain(0, model_width)
    latent_gain_grad = own_gain(model_width, LAT)
    ffn_gain_grad = own_gain(model_width + LAT, model_width)
    return (
        block_out,
        block_in_grad,
        attn_gain_grad,
        query_proj_grad,
        latent_proj_grad,
        latent_gain_grad,
        latent_up_grad,
        out_proj_grad,
        ffn_gain_grad,
        shared_gate_grad,
        shared_up_grad,
        shared_down_grad,
        routed_gate_grad,
        routed_up_grad,
        routed_down_grad,
    )


def solution(mesh):
    placed = (
        P(("fsdp", "tp"), None),
        P(("fsdp", "tp"), None),
        P("fsdp"),
        P("fsdp", None),
        P("fsdp", None),
        P("fsdp"),
        P("fsdp", "tp"),
        P("fsdp", None),
        P("fsdp"),
        P("fsdp", "tp"),
        P("tp", "fsdp"),
        P("fsdp"),
        P("fsdp", "tp"),
        P("fsdp", "tp"),
        P("tp", "fsdp"),
        P("fsdp", "tp", None),
        P("fsdp", "tp", None),
        P("fsdp", "tp", None),
    )
    return jax.shard_map(
        per_device,
        mesh=mesh,
        in_specs=placed,
        out_specs=(
            P(("fsdp", "tp"), None),
            P(("fsdp", "tp"), None),
            P(("fsdp", "tp")),
            P("fsdp", "tp"),
            P(("fsdp", "tp"), None),
            P(("fsdp", "tp")),
            P("fsdp", "tp"),
            P("tp", "fsdp"),
            P(("fsdp", "tp")),
            P("fsdp", "tp"),
            P("fsdp", "tp"),
            P("tp", "fsdp"),
            P("fsdp", "tp", None),
            P("fsdp", "tp", None),
            P("fsdp", "tp", None),
        ),
        check_vma=False,
    )
```

```python
import functools

import jax
import jax.numpy as jnp
from jax import lax
from jax.experimental import pallas as pl
from jax.experimental.pallas import tpu as pltpu
from jax.sharding import PartitionSpec as P

H = 16
NOPE = 128
ROPE = 64
DV = 128
LAT = 512
TOPK = 6
SEQ = 512
HALF = 256
QUARTET = 4
RAW_ROWS = 8


EPSILON = 1e-06
THETA_BASE = 10000.0
MASK_FILL = -1e30
NO_SLOT = -1e6

BF = jnp.bfloat16
F32 = jnp.float32


def rope_tables(positions, width_rope):
    middle = width_rope // 2
    frequency = THETA_BASE ** (-(jnp.arange(middle) * 2).astype(jnp.float32) / width_rope)
    angles = positions.astype(jnp.float32)[:, None] * frequency[None, :]
    return (jnp.cos(angles), jnp.sin(angles))


def rotate(values, cosine, sine_part):
    middle = values.shape[-1] // 2
    first_half = values[..., :middle]
    second_half = values[..., middle:]
    return jnp.concatenate(
        [
            first_half * cosine - second_half * sine_part,
            second_half * cosine + first_half * sine_part,
        ],
        axis=-1,
    )


def unrotate(values, cosine, sine_part):
    middle = values.shape[-1] // 2
    first_half = values[..., :middle]
    second_half = values[..., middle:]
    return jnp.concatenate(
        [
            first_half * cosine + second_half * sine_part,
            second_half * cosine - first_half * sine_part,
        ],
        axis=-1,
    )


def norm_parts(values):
    inverse = lax.rsqrt(jnp.mean(values * values, axis=-1, keepdims=True) + EPSILON)
    return (values * inverse, inverse)


def norm_back(upstream, unit_rows, inverse, scaling):
    scaled = upstream * scaling
    gain_grad = jnp.sum(upstream * unit_rows, axis=0)
    input_grad = inverse * (
        scaled - unit_rows * jnp.mean(scaled * unit_rows, axis=-1, keepdims=True)
    )
    return (gain_grad, input_grad)


def silu_back(grad_hidden, gate_pre, up_pre):
    sigmoid = jax.nn.sigmoid(gate_pre)
    gate_grad = grad_hidden * up_pre * (sigmoid * (1.0 + gate_pre * (1.0 - sigmoid)))
    up_grad = grad_hidden * (gate_pre * sigmoid)
    return (gate_grad.astype(jnp.bfloat16), up_grad.astype(jnp.bfloat16))


def is_power(count):
    return count & (count - 1) == 0


def swap(values, axis_name, bit):
    count = lax.axis_size(axis_name)
    return lax.ppermute(values, axis_name, [(i, i ^ bit) for i in range(count)])


def tie(*values):
    return lax.optimization_barrier(values)


def column_gather(rows):
    return lax.all_gather(rows, "tp", axis=0, tiled=True)


def column_scatter(values):
    return lax.psum_scatter(values.astype(BF), "tp", scatter_dimension=0, tiled=True).astype(F32)


def dot_rows(left, right):
    return lax.dot_general(left, right, (((1,), (1,)), ((), ())), preferred_element_type=F32)


def dot_plain(left, right):
    return lax.dot_general(left, right, (((1,), (0,)), ((), ())), preferred_element_type=F32)


def dot_first(left, right):
    return lax.dot_general(left, right, (((0,), (0,)), ((), ())), preferred_element_type=F32)


def select_rows(slot_rows, experts, cap):
    row = lax.broadcasted_iota(jnp.int32, (experts * cap, HALF), 0).astype(F32)
    hit = row == slot_rows[0:1, :]
    for e in range(1, experts):
        hit = hit | (row == slot_rows[e : e + 1, :] + float(e * cap))
    return hit


def select_cols(slot_cols, experts, cap):
    lane = lax.broadcasted_iota(jnp.int32, (HALF, experts * cap), 1).astype(F32)
    hit = lane == slot_cols[:, 0:1]
    for e in range(1, experts):
        hit = hit | (lane == slot_cols[:, e : e + 1] + float(e * cap))
    return hit


def slot_weights(hit, weight_rows, experts, cap):
    pieces = []
    for e in range(experts):
        part = hit[e * cap : (e + 1) * cap, :]
        pieces.append(
            jnp.sum(jnp.where(part, weight_rows[e : e + 1, :], 0.0), axis=1, keepdims=True)
        )
    return jnp.concatenate(pieces, axis=0)


def expert_front_kernel(step, experts, cap, aliased, *refs):
    count = QUARTET
    x_in = refs[:count]
    where_ref, dy_in, gate_up_in, down_in, slot_row_ref, weight_row_ref, slot_col_ref = refs[
        count : count + 7
    ]
    base = count + 7 + aliased
    dx_out = refs[base : base + 2]
    x_all, d_all, hid_all, dgu_all = refs[base + 2 : base + 6]
    (xb, db, gate_up, down, xs, ds, dxs, dxo, hid, dgu, sem_in, sem_w, sem_out, sem_dx) = refs[
        base + 6 :
    ]
    width = xb.shape[2]
    pad = down.shape[1]
    tile = min(1024, width)
    x_copies = [pltpu.make_async_copy(x_in[q], xb.at[q], sem_in.at[q]) for q in range(count)]
    d_copies = [
        pltpu.make_async_copy(
            dy_in.at[pl.ds(pl.multiple_of(where_ref[q] * HALF, HALF), HALF)],
            db.at[q],
            sem_in.at[count + q],
        )
        for q in range(count)
    ]
    w_copies = [
        pltpu.make_async_copy(gate_up_in, gate_up, sem_w.at[0]),
        pltpu.make_async_copy(down_in, down, sem_w.at[1]),
    ]
    for q in range(count):
        x_copies[q].start()
        d_copies[q].start()
    for copy in w_copies:
        copy.start()
    for q in range(count):
        x_copies[q].wait()
        d_copies[q].wait()

        hit = select_rows(slot_row_ref[q], experts, cap)
        weights = slot_weights(hit, weight_row_ref[q], experts, cap)
        choose = jnp.where(hit, 1.0, 0.0).astype(BF)

        def spread(n, carry, q=q, choose=choose, weights=weights):
            cols = pl.ds(pl.multiple_of(n * tile, tile), tile)
            rows = dot_plain(choose, xb[q, :, cols])
            grads = dot_plain(choose, db[q, :, cols]) * weights
            for e in range(experts):
                xs[e, q * cap : (q + 1) * cap, cols] = rows[e * cap : (e + 1) * cap].astype(BF)
                ds[e, q * cap : (q + 1) * cap, cols] = grads[e * cap : (e + 1) * cap].astype(BF)
            return carry

        lax.fori_loop(0, width // tile, spread, 0)
    out_copies = [
        pltpu.make_async_copy(xs, x_all.at[step], sem_out.at[0]),
        pltpu.make_async_copy(ds, d_all.at[step], sem_out.at[1]),
        pltpu.make_async_copy(hid, hid_all.at[step], sem_out.at[2]),
        pltpu.make_async_copy(dgu, dgu_all.at[step], sem_out.at[3]),
    ]
    out_copies[0].start()
    out_copies[1].start()
    for copy in w_copies:
        copy.wait()

    def one_expert(e, carry):
        both = dot_rows(xs[e], gate_up[e])
        gate_pre, up_pre = both[:, :pad], both[:, pad:]
        d_hidden = dot_rows(ds[e], down[e])
        sigmoid = jax.nn.sigmoid(gate_pre)
        silu = gate_pre * sigmoid
        hid[e] = (silu * up_pre).astype(BF)
        gate_grad = d_hidden * up_pre * (sigmoid * (1.0 + gate_pre * (1.0 - sigmoid)))
        grads = jnp.concatenate([gate_grad, d_hidden * silu], axis=1).astype(BF)
        dgu[e] = grads

        def back(n, inner):
            cols = pl.ds(pl.multiple_of(n * tile, tile), tile)
            part = dot_plain(dgu[e], gate_up[e, :, cols]).astype(BF)
            for q in range(count):
                dxs[q, pl.ds(pl.multiple_of(e * cap, cap), cap), cols] = part[
                    q * cap : (q + 1) * cap
                ]
            return inner

        lax.fori_loop(0, width // tile, back, 0)
        return carry

    lax.fori_loop(0, experts, one_expert, 0)
    out_copies[2].start()
    out_copies[3].start()
    dx_copies = [
        pltpu.make_async_copy(dxo.at[q], dx_out[q // 2].at[q % 2], sem_dx.at[q])
        for q in range(count)
    ]
    for q in range(count):
        choose = jnp.where(select_cols(slot_col_ref[q], experts, cap), 1.0, 0.0).astype(BF)

        def gather(n, carry, q=q, choose=choose):
            cols = pl.ds(pl.multiple_of(n * tile, tile), tile)
            dxo[q, :, cols] = dot_plain(choose, dxs[q, :, cols]).astype(BF)
            return carry

        lax.fori_loop(0, width // tile, gather, 0)
        dx_copies[q].start()
    for copy in out_copies:
        copy.wait()
    for copy in dx_copies:
        copy.wait()


def expert_front(step, steps, x_parts, where, dy_all, gate_up, down, tables, kept, cap):
    experts, wide, width = gate_up.shape
    pad = wide // 2
    slots = QUARTET * cap
    slot_row, weight_row, slot_col = (t[step] for t in tables)
    any_spec = pl.BlockSpec(memory_space=pl.ANY)
    vmem_spec = pl.BlockSpec(memory_space=pltpu.VMEM)
    pair_shape = jax.ShapeDtypeStruct((2, HALF, width), BF)
    kept_shapes = [
        jax.ShapeDtypeStruct((steps, experts, slots, columns), BF)
        for columns in (width, width, pad, wide)
    ]
    results = pl.pallas_call(
        functools.partial(expert_front_kernel, step, experts, cap, len(kept)),
        out_shape=[pair_shape] * 2 + kept_shapes,
        in_specs=[any_spec] * QUARTET
        + [pl.BlockSpec(memory_space=pltpu.SMEM)]
        + [any_spec] * 3
        + [vmem_spec] * 3
        + [any_spec] * len(kept),
        out_specs=[any_spec] * 6,
        input_output_aliases={QUARTET + 7 + i: 2 + i for i in range(len(kept))},
        scratch_shapes=[
            pltpu.VMEM((QUARTET, HALF, width), BF),
            pltpu.VMEM((QUARTET, HALF, width), BF),
            pltpu.VMEM((experts, wide, width), BF),
            pltpu.VMEM((experts, pad, width), BF),
            pltpu.VMEM((experts, slots, width), BF),
            pltpu.VMEM((experts, slots, width), BF),
            pltpu.VMEM((QUARTET, experts * cap, width), BF),
            pltpu.VMEM((QUARTET, HALF, width), BF),
            pltpu.VMEM((experts, slots, pad), BF),
            pltpu.VMEM((experts, slots, wide), BF),
            pltpu.SemaphoreType.DMA((2 * QUARTET,)),
            pltpu.SemaphoreType.DMA((2,)),
            pltpu.SemaphoreType.DMA((4,)),
            pltpu.SemaphoreType.DMA((QUARTET,)),
        ],
        compiler_params=pltpu.CompilerParams(vmem_limit_bytes=62 * 1024 * 1024),
        cost_estimate=pl.CostEstimate(
            flops=2 * slots * experts * width * pad * 5
            + 6 * QUARTET * HALF * experts * cap * width,
            bytes_accessed=2 * width * (3 * QUARTET * HALF + experts * 3 * pad + 2 * experts * slots),
            transcendentals=slots * experts * pad,
        ),
        name="expert_front",
    )(*x_parts, where, dy_all, gate_up, down, slot_row, weight_row, slot_col, *kept)
    return list(results[:2]), list(results[2:])


def expert_out_kernel(experts, cap, hid, down, slot_row, weight_row, slot_col, near, far, parts):
    width = down.shape[2]
    tile = min(1024, width)
    weights = [
        slot_weights(
            select_rows(slot_row[0, q], experts, cap), weight_row[0, q], experts, cap
        )
        for q in range(QUARTET)
    ]
    for e in range(experts):

        def front(n, carry, e=e):
            cols = pl.ds(pl.multiple_of(n * tile, tile), tile)
            rows = dot_plain(hid[0, e], down[e, :, cols])
            for q in range(QUARTET):
                parts[q, e * cap : (e + 1) * cap, cols] = (
                    rows[q * cap : (q + 1) * cap] * weights[q][e * cap : (e + 1) * cap]
                ).astype(BF)
            return carry

        lax.fori_loop(0, width // tile, front, 0)
    for q in range(QUARTET):
        choose = jnp.where(select_cols(slot_col[0, q], experts, cap), 1.0, 0.0).astype(BF)
        out = (near, far)[q // 2]

        def gather(n, carry, q=q, choose=choose, out=out):
            cols = pl.ds(pl.multiple_of(n * tile, tile), tile)
            out[0, q % 2, :, cols] = dot_plain(choose, parts[q, :, cols]).astype(BF)
            return carry

        lax.fori_loop(0, width // tile, gather, 0)


def expert_out(hid_all, down, tables, cap):
    steps, experts, slots, pad = hid_all.shape
    width = down.shape[2]
    slot_row, weight_row, slot_col = tables
    return pl.pallas_call(
        functools.partial(expert_out_kernel, experts, cap),
        grid=(steps,),
        out_shape=[jax.ShapeDtypeStruct((steps, 2, HALF, width), BF)] * 2,
        in_specs=[
            pl.BlockSpec((1, experts, slots, pad), lambda i: (i, 0, 0, 0)),
            pl.BlockSpec((experts, pad, width), lambda i: (0, 0, 0)),
            pl.BlockSpec((1,) + slot_row.shape[1:], lambda i: (i, 0, 0, 0)),
            pl.BlockSpec((1,) + weight_row.shape[1:], lambda i: (i, 0, 0, 0)),
            pl.BlockSpec((1,) + slot_col.shape[1:], lambda i: (i, 0, 0, 0)),
        ],
        out_specs=[pl.BlockSpec((1, 2, HALF, width), lambda i: (i, 0, 0, 0))] * 2,
        scratch_shapes=[pltpu.VMEM((QUARTET, experts * cap, width), BF)],
        compiler_params=pltpu.CompilerParams(vmem_limit_bytes=48 * 1024 * 1024),
        cost_estimate=pl.CostEstimate(
            flops=steps * (2 * slots * experts * width * pad + 2 * QUARTET * HALF * experts * cap * width),
            bytes_accessed=2 * steps * QUARTET * HALF * width + 2 * hid_all.size + 2 * down.size,
            transcendentals=0,
        ),
        name="expert_out",
    )(hid_all, down, slot_row, weight_row, slot_col)


def expert_grads_kernel(dgu, x, hid, d, gate_grad, up_grad, down_grad):
    local = gate_grad.shape[1]
    pad = hid.shape[3]
    width = x.shape[3]
    tile = min(1024, width)

    @pl.when(pl.program_id(1) == 0)
    def _():
        gate_grad[...] = jnp.zeros_like(gate_grad)
        up_grad[...] = jnp.zeros_like(up_grad)
        down_grad[...] = jnp.zeros_like(down_grad)

    def part(n, carry):
        cols = pl.ds(pl.multiple_of(n * tile, tile), tile)
        gate_grad[0, :, cols] += dot_first(dgu[0, 0, :, :pad], x[0, 0, :, cols])[:local]
        up_grad[0, :, cols] += dot_first(dgu[0, 0, :, pad:], x[0, 0, :, cols])[:local]
        down_grad[0, :, cols] += dot_first(hid[0, 0], d[0, 0, :, cols])[:local]
        return carry

    lax.fori_loop(0, width // tile, part, 0)


def expert_grads(kept, local):
    x_all, d_all, hid_all, dgu_all = kept
    steps, experts, slots, width = x_all.shape
    pad = hid_all.shape[3]

    def block(array):
        return pl.BlockSpec((1, 1) + array.shape[2:], lambda e, i: (i, e, 0, 0))

    grad = jax.ShapeDtypeStruct((experts, local, width), F32)
    return pl.pallas_call(
        expert_grads_kernel,
        grid=(experts, steps),
        out_shape=[grad] * 3,
        in_specs=[block(dgu_all), block(x_all), block(hid_all), block(d_all)],
        out_specs=[pl.BlockSpec((1, local, width), lambda e, i: (e, 0, 0))] * 3,
        compiler_params=pltpu.CompilerParams(vmem_limit_bytes=48 * 1024 * 1024),
        cost_estimate=pl.CostEstimate(
            flops=2 * 3 * steps * experts * slots * width * pad,
            bytes_accessed=2 * (x_all.size + d_all.size + hid_all.size + dgu_all.size)
            + 12 * experts * local * width,
            transcendentals=0,
        ),
        name="expert_grads",
    )(dgu_all, x_all, hid_all, d_all)


def mesh_copy(src, dst, sends, arrivals, number, device):
    return pltpu.make_async_remote_copy(
        src_ref=src,
        dst_ref=dst,
        send_sem=sends.at[number],
        recv_sem=arrivals.at[number],
        device_id=device,
        device_id_type=pl.DeviceIdType.MESH,
    )


def plane_neighbours():
    place, column = lax.axis_index("fsdp"), lax.axis_index("tp")
    core, along, across = place % 2, (place // 2) % 2, place // 4
    return (
        (place + 1 - 2 * core, column),
        (place + 2 - 4 * along, column),
        (place + 4 - 8 * across, column),
    )


def column_neighbours(count):
    place, column = lax.axis_index("fsdp"), lax.axis_index("tp")
    return [(place, (column + s) % count) for s in range(1, count)]


def greet(devices):
    barrier = pltpu.get_barrier_semaphore()
    for device in devices:
        pl.semaphore_signal(
            barrier, inc=1, device_id=device, device_id_type=pl.DeviceIdType.MESH
        )
    pl.semaphore_wait(barrier, len(devices))


class ColumnGather:
    def __init__(self, blocks, rows_of, sends, arrivals, base):
        self.blocks, self.rows_of = blocks, rows_of
        self.sends, self.arrivals, self.base = sends, arrivals, base
        self.row = lax.axis_index("tp")
        self.column = column_neighbours(4)

    def direct(self, s):
        place = self.blocks.at[self.rows_of(0)]
        return mesh_copy(
            place, place, self.sends, self.arrivals, self.base + s - 1, self.column[s - 1]
        )

    def start(self):
        @pl.when(self.row < 3)
        def _():
            self.direct(1).start()

        @pl.when(self.row > 0)
        def _():
            self.direct(3).start()

        self.direct(2).start()

    def wait(self, b):
        self.direct(4 - b).wait_recv()
        if b == 2:

            @pl.when(self.row == 1)
            def _():
                self.relay(3).start()

            @pl.when(self.row == 2)
            def _():
                self.relay(1).start()

    def relay(self, s):
        place = self.blocks.at[self.rows_of(2)]
        return pltpu.make_async_remote_copy(
            src_ref=place,
            dst_ref=place,
            send_sem=self.sends.at[self.base + 3],
            recv_sem=self.arrivals.at[self.base + 3 - s],
            device_id=self.column[s - 1],
            device_id_type=pl.DeviceIdType.MESH,
        )

    def drain(self):
        @pl.when(self.row < 3)
        def _():
            self.direct(1).wait_send()

        @pl.when(self.row > 0)
        def _():
            self.direct(3).wait_send()

        self.direct(2).wait_send()

        @pl.when(self.row == 1)
        def _():
            self.relay(3).wait_send()

        @pl.when(self.row == 2)
        def _():
            self.relay(1).wait_send()


class ColumnSum:
    def __init__(self, parts, rows_of, landed, relayed, sends, arrivals, base):
        self.parts, self.rows_of, self.landed, self.relayed = parts, rows_of, landed, relayed
        self.sends, self.arrivals, self.base = sends, arrivals, base
        self.row = lax.axis_index("tp")
        self.column = column_neighbours(4)

    def direct(self, s):
        return mesh_copy(
            self.parts.at[self.rows_of(s)],
            self.landed.at[s - 1],
            self.sends,
            self.arrivals,
            self.base + s - 1,
            self.column[s - 1],
        )

    def first_leg(self, s):
        return mesh_copy(
            self.parts.at[self.rows_of(4 - s)],
            self.relayed.at[0],
            self.sends,
            self.arrivals,
            self.base + 3,
            self.column[s - 1],
        )

    def own_part(self, local):
        return pltpu.make_async_copy(self.parts.at[self.rows_of(2)], self.relayed.at[1], local)

    def second_leg(self):
        return mesh_copy(
            self.relayed.at[1],
            self.landed.at[1],
            self.sends,
            self.arrivals,
            self.base + 1,
            self.column[1],
        )

    def start(self, local):
        @pl.when(self.row == 0)
        def _():
            self.first_leg(1).start()

        @pl.when(self.row == 3)
        def _():
            self.first_leg(3).start()

        @pl.when((self.row == 1) | (self.row == 2))
        def _():
            self.own_part(local).start()

        @pl.when(self.row < 3)
        def _():
            self.direct(1).start()

        @pl.when(self.row > 0)
        def _():
            self.direct(3).start()

        @pl.when((self.row == 0) | (self.row == 3))
        def _():
            self.direct(2).start()

    def middle(self, local):
        @pl.when((self.row == 1) | (self.row == 2))
        def _():
            self.own_part(local).wait()
            self.first_leg(1).wait_recv()

            def some(i, carry):
                rows = pl.ds(pl.multiple_of(i * 32, 32), 32)
                self.relayed[1, rows, :] = (
                    self.relayed[0, rows, :].astype(F32) + self.relayed[1, rows, :].astype(F32)
                ).astype(BF)
                return carry

            lax.fori_loop(0, self.relayed.shape[1] // 32, some, 0)
            self.second_leg().start()

    def clear(self):
        @pl.when(self.row == 0)
        def _():
            self.landed[0] = jnp.zeros(self.landed.shape[1:], BF)

        @pl.when(self.row == 3)
        def _():
            self.landed[2] = jnp.zeros(self.landed.shape[1:], BF)

    def total(self, own):
        @pl.when(self.row > 0)
        def _():
            self.direct(1).wait_recv()

        @pl.when(self.row < 3)
        def _():
            self.direct(3).wait_recv()

        self.direct(2).wait_recv()
        total = own.astype(F32)
        for s in range(3):
            total = total + self.landed[s].astype(F32)
        return total

    def drain(self):
        @pl.when(self.row == 0)
        def _():
            self.first_leg(1).wait_send()

        @pl.when(self.row == 3)
        def _():
            self.first_leg(3).wait_send()

        @pl.when(self.row < 3)
        def _():
            self.direct(1).wait_send()

        @pl.when(self.row > 0)
        def _():
            self.direct(3).wait_send()

        self.direct(2).wait_send()


class PlaneGather:
    def __init__(self, own, others, rows_of, sends, arrivals, base):
        self.own, self.others, self.rows_of = own, others, rows_of
        self.sends, self.arrivals, self.base = sends, arrivals, base
        self.partner, self.along, self.across = plane_neighbours()

    def copies(self, b):
        half = self.own.shape[1] // 2
        rows = self.rows_of(b)
        left, right = pl.ds(0, half), pl.ds(half, half)
        other = {r: self.others.at[r - 1] for r in range(1, 8)}
        plan = [
            (self.own.at[rows], other[2].at[rows], self.along),
            (self.own.at[rows], other[4].at[rows], self.across),
            (self.own.at[rows], other[1].at[rows], self.partner),
            (other[2].at[rows, left], other[6].at[rows, left], self.across),
            (other[4].at[rows, right], other[6].at[rows, right], self.along),
            (other[2].at[rows], other[3].at[rows], self.partner),
            (other[4].at[rows], other[5].at[rows], self.partner),
            (other[6].at[rows], other[7].at[rows], self.partner),
        ]
        return [
            mesh_copy(src, dst, self.sends, self.arrivals, self.base + 8 * b + i, device)
            for i, (src, dst, device) in enumerate(plan)
        ]

    def start(self, b):
        for copy in self.copies(b)[:3]:
            copy.start()

    def forward(self, b):
        along, across, _, left, right, third, fifth, _ = self.copies(b)
        along.wait_recv()
        left.start()
        third.start()
        across.wait_recv()
        right.start()
        fifth.start()

    def last(self, b):
        copies = self.copies(b)
        copies[3].wait_recv()
        copies[4].wait_recv()
        copies[7].start()

    def arrived(self, b, numbers):
        copies = self.copies(b)
        for i in numbers:
            copies[i].wait_recv()

    def drain(self, b):
        for copy in self.copies(b):
            copy.wait_send()


def block_rows(columns, size):
    row = lax.axis_index("tp")
    return lambda s: pl.ds(pl.multiple_of((row + s) % columns * size, size), size)


def slots_of(table, experts, columns, size, b, q):
    place = pl.ds(pl.multiple_of((lax.axis_index("tp") + b) % columns * size, size), size)
    rows = []
    for e in range(experts):
        low, high = 2 * q * experts + e, (2 * q + 1) * experts + e
        rows.append(
            jnp.concatenate([table[low : low + 1, place], table[high : high + 1, place]], axis=1)
        )
    return jnp.concatenate(rows, axis=0)


def token_sums(table, experts, columns, size, wide, b, slots, keep):
    width = slots.shape[2]
    tile = min(1024, width)
    for q in range(QUARTET):
        entries = slots_of(table, experts, columns, size, b, q)
        entries = jnp.concatenate(
            [entries, jnp.full((8 - experts, HALF), NO_SLOT, F32)], axis=0
        )
        choose = jnp.where(select_cols(entries.T, experts, wide), 1.0, 0.0).astype(BF)

        def gather(n, carry, q=q, choose=choose):
            cols = pl.ds(pl.multiple_of(n * tile, tile), tile)
            keep(q, cols, dot_plain(choose, slots[q, :, cols]).astype(BF))
            return carry

        lax.fori_loop(0, width // tile, gather, 0)


def expert_kernel(cap, columns, size, *refs):
    (
        attn_in,
        tokens_in,
        cotan_in,
        gate_in,
        up_in,
        down_in,
        gain_ref,
        raw_ref,
        mixed_out,
        ffn_all,
        dx_out,
        slots_out,
        weights_out,
        x_all,
        d_all,
        hid_all,
        dgu_all,
        x_others,
        dy_others,
        theirs,
        links,
        attn_v,
        tokens_v,
        arrived_v,
        relayed_v,
        mixed_v,
        ffn_v,
        xb,
        db,
        gate_up,
        down,
        xs,
        ds,
        dxs,
        others,
        chip,
        stage,
        hid,
        dgu,
        slot_table,
        weight_table,
        sends,
        arrivals,
        local,
        loads,
        sum_local,
        spill,
    ) = refs
    count = QUARTET
    previous = {2: 0, 1: 2, 3: 1}
    experts, local_hidden = gate_in.shape[:2]
    width = xb.shape[2]
    pad = down.shape[1]
    tile = min(1024, width)
    wide = 2 * cap
    rows_of = block_rows(columns, size)
    partner, along, across = plane_neighbours()
    column = column_neighbours(columns)
    number = 0

    def reserve(amount):
        nonlocal number
        number += amount
        return number - amount

    x_gather = PlaneGather(ffn_all, x_others, rows_of, sends, arrivals, reserve(8 * columns))
    dy_gather = PlaneGather(cotan_in, dy_others, rows_of, sends, arrivals, reserve(8 * columns))
    gather = ColumnGather(ffn_all, rows_of, sends, arrivals, reserve(4))
    summed = ColumnSum(attn_in, rows_of, arrived_v, relayed_v, sends, arrivals, reserve(4))
    plane = PlaneSum(
        lambda r, h: others.at[r // 2],
        chip,
        theirs,
        links,
        stage,
        sends,
        arrivals,
        reserve(plane_sum_sizes(columns)[0]),
        sum_local,
    )

    greet([partner, along, across] + column)
    summed.start(local.at[2])
    first = [
        pltpu.make_async_copy(attn_in.at[rows_of(0)], attn_v, local.at[0]),
        pltpu.make_async_copy(tokens_in, tokens_v, local.at[1]),
    ]
    for copy in first:
        copy.start()
    order = (0, 2, 1, 3)
    for b in order:
        dy_gather.start(b)
    if pad > local_hidden:
        rest = pad - local_hidden
        for e in range(experts):
            for ref, start in ((gate_up, local_hidden), (gate_up, pad + local_hidden), (down, local_hidden)):
                ref[e, start : start + rest, :] = jnp.zeros((rest, width), BF)
    weights_in = []
    for e in range(experts):
        weights_in += [
            pltpu.make_async_copy(
                gate_in.at[e], gate_up.at[e, pl.ds(0, local_hidden)], local.at[3 + 3 * e]
            ),
            pltpu.make_async_copy(
                up_in.at[e], gate_up.at[e, pl.ds(pad, local_hidden)], local.at[4 + 3 * e]
            ),
            pltpu.make_async_copy(
                down_in.at[e], down.at[e, pl.ds(0, local_hidden)], local.at[5 + 3 * e]
            ),
        ]
    for copy in weights_in:
        copy.start()

    summed.clear()
    summed.middle(local.at[2])

    earlier = lax.broadcasted_iota(jnp.int32, (size, size), 0)
    later = lax.broadcasted_iota(jnp.int32, (size, size), 1)
    before = jnp.where(earlier < later, 1.0, 0.0).astype(BF)
    own_first = (lax.axis_index("fsdp") * experts).astype(F32)
    for r in range(8):
        for e in range(experts):
            member = jnp.zeros((1, SEQ), F32)
            weight = jnp.zeros((1, SEQ), F32)
            for pick in range(TOPK):
                same = raw_ref[r, pick : pick + 1, :] == own_first + float(e)
                member = jnp.where(same, 1.0, member)
                weight = weight + jnp.where(
                    same, raw_ref[r, RAW_ROWS + pick : RAW_ROWS + pick + 1, :], 0.0
                )
            slot_table[r * experts + e : r * experts + e + 1, :] = member
            weight_table[r * experts + e : r * experts + e + 1, :] = weight
    second = lax.broadcasted_iota(jnp.int32, (8 * experts, size), 0) // experts % 2
    shift = second.astype(F32) * float(cap)
    for b in range(columns):
        cols = pl.ds(b * size, size)
        member = slot_table[:, cols]
        rank = dot_plain(member.astype(BF), before)
        slot_table[:, cols] = jnp.where(member > 0.5, rank + shift, NO_SLOT)
    slots_out[...] = slot_table[...]
    weights_out[...] = weight_table[...]

    for copy in first:
        copy.wait()
    total = summed.total(attn_v[...]) + tokens_v[...].astype(F32)
    mixed_v[...] = total
    inverse = lax.rsqrt(jnp.mean(total * total, axis=1, keepdims=True) + EPSILON)
    ffn_v[...] = (total * inverse * gain_ref[...]).astype(BF)
    own_copy = pltpu.make_async_copy(ffn_v, ffn_all.at[rows_of(0)], local.at[0])
    own_copy.start()
    mixed_copy = pltpu.make_async_copy(mixed_v, mixed_out, local.at[1])
    mixed_copy.start()
    own_copy.wait()

    gather.start()

    def enter(b):
        if b > 0:
            gather.wait(b)
        x_gather.start(b)

    def ready(b):
        x_gather.last(b)
        dy_gather.last(b)
        x_gather.arrived(b, [2, 5, 6, 7])
        dy_gather.arrived(b, [2, 5, 6, 7])

    def source(own, gathered, r):
        return own if r == 0 else gathered.at[r - 1]

    def load(b, k):
        own, gathered, target = ((ffn_all, x_others, xb), (cotan_in, dy_others, db))[k]
        return [
            pltpu.make_async_copy(
                source(own, gathered, r).at[rows_of(b)],
                target.at[r // 2, pl.ds(r % 2 * size, size)],
                loads.at[8 * k + r],
            )
            for r in range(8)
        ]

    def combine(b, keep):
        token_sums(slot_table, experts, columns, size, wide, b, dxs, keep)

    def spills(b):
        return [
            pltpu.make_async_copy(xs, x_all.at[b], spill.at[0]),
            pltpu.make_async_copy(ds, d_all.at[b], spill.at[1]),
            pltpu.make_async_copy(hid.at[b], hid_all.at[b], spill.at[2]),
            pltpu.make_async_copy(dgu, dgu_all.at[b], spill.at[3]),
        ]

    def front(b):
        x_load, dy_load = load(b, 0), load(b, 1)
        for copy in x_load + dy_load:
            copy.start()
        if b == 0:
            for copy in weights_in:
                copy.wait()
        if b > 0:
            for copy in spills(previous[b]):
                copy.wait()
        for q in range(count):
            for copy in x_load[2 * q : 2 * q + 2] + dy_load[2 * q : 2 * q + 2]:
                copy.wait()
            hit = select_rows(slots_of(slot_table, experts, columns, size, b, q), experts, wide)
            weights = slot_weights(hit, slots_of(weight_table, experts, columns, size, b, q), experts, wide)
            choose = jnp.where(hit, 1.0, 0.0).astype(BF)

            def spread(n, carry, q=q, choose=choose, weights=weights):
                cols = pl.ds(pl.multiple_of(n * tile, tile), tile)
                rows = dot_plain(choose, xb[q, :, cols])
                grads = dot_plain(choose, db[q, :, cols]) * weights
                for e in range(experts):
                    low, high = e * wide, (e + 1) * wide
                    xs[e, q * wide : (q + 1) * wide, cols] = rows[low:high].astype(BF)
                    ds[e, q * wide : (q + 1) * wide, cols] = grads[low:high].astype(BF)
                return carry

            lax.fori_loop(0, width // tile, spread, 0)
        out_copies = spills(b)
        out_copies[0].start()
        out_copies[1].start()

        def one_expert(e, carry):
            both = dot_rows(xs[e], gate_up[e])
            gate_pre, up_pre = both[:, :pad], both[:, pad:]
            d_hidden = dot_rows(ds[e], down[e])
            sigmoid = jax.nn.sigmoid(gate_pre)
            silu = gate_pre * sigmoid
            hid[b, e] = (silu * up_pre).astype(BF)
            gate_grad = d_hidden * up_pre * (sigmoid * (1.0 + gate_pre * (1.0 - sigmoid)))
            dgu[e] = jnp.concatenate([gate_grad, d_hidden * silu], axis=1).astype(BF)

            def back(n, inner):
                cols = pl.ds(pl.multiple_of(n * tile, tile), tile)
                part = dot_plain(dgu[e], gate_up[e, :, cols]).astype(BF)
                for q in range(count):
                    dxs[q, pl.ds(pl.multiple_of(e * wide, wide), wide), cols] = part[
                        q * wide : (q + 1) * wide
                    ]
                return inner

            lax.fori_loop(0, width // tile, back, 0)
            return carry

        lax.fori_loop(0, experts, one_expert, 0)
        out_copies[2].start()
        out_copies[3].start()
        if b > 0:
            for i in range(4):
                plane.pair(i, previous[b]).wait_send()

        def keep(q, cols, value):
            chip[q, b, :, cols] = value[:size]
            others[q, :, cols] = value[size:]

        combine(b, keep)
        for i in range(4):
            plane.pair(i, b).start()

    dy_gather.forward(0)
    enter(0)
    x_gather.forward(0)
    dy_gather.forward(2)
    enter(2)
    dy_gather.forward(1)
    enter(1)
    x_gather.forward(2)
    ready(0)
    front(0)
    dy_gather.forward(3)
    enter(3)
    x_gather.forward(1)
    ready(2)
    front(2)
    x_gather.forward(3)
    plane.send_first([0], False)
    ready(1)
    front(1)
    plane.send_first([2], False)
    plane.send_second([0])
    ready(3)
    front(3)
    plane.send_first([1], False)
    plane.send_second([2])
    done = {}

    def close(b):
        plane.finish([b])
        done[b] = pltpu.make_async_copy(chip.at[0, b], dx_out.at[rows_of(b)], loads.at[b])
        done[b].start()

    plane.send_first([3], False)
    close(0)
    plane.send_second([1])
    close(2)
    plane.send_second([3])
    close(1)
    close(3)
    for copy in spills(3):
        copy.wait()
    for b in range(columns):
        done[b].wait()
    mixed_copy.wait()

    for b in range(columns):
        x_gather.drain(b)
        dy_gather.drain(b)
    gather.drain()
    summed.drain()
    plane.drain(3)


def expert_call(attn_part, tokens, cotan_all, gate, up, down, gain, raw, cap):
    columns = lax.axis_size("tp")
    size, width = tokens.shape
    experts, local_hidden, _ = gate.shape
    pad = -(-local_hidden // 128) * 128
    slots = 8 * cap
    anywhere = pl.BlockSpec(memory_space=pl.ANY)
    held = pl.BlockSpec(memory_space=pltpu.VMEM)

    def array(*dims, kind=BF):
        return jax.ShapeDtypeStruct(dims, kind)

    landing, scratch = plane_sum_space(columns, size, width)
    remote, near = plane_sum_sizes(columns)
    remote = remote + 16 * columns + 8
    results = pl.pallas_call(
        functools.partial(expert_kernel, cap, columns, size),
        out_shape=[
            array(size, width, kind=F32),
            array(SEQ, width),
            array(SEQ, width),
            array(8 * experts, SEQ, kind=F32),
            array(8 * experts, SEQ, kind=F32),
            array(columns, experts, slots, width),
            array(columns, experts, slots, width),
            array(columns, experts, slots, pad),
            array(columns, experts, slots, 2 * pad),
            array(7, SEQ, width),
            array(7, SEQ, width),
        ]
        + landing,
        in_specs=[anywhere] * 6 + [held] * 2,
        out_specs=[anywhere] * 3 + [held] * 2 + [anywhere] * 8,
        scratch_shapes=[
            pltpu.VMEM((size, width), BF),
            pltpu.VMEM((size, width), BF),
            pltpu.VMEM((columns - 1, size, width), BF),
            pltpu.VMEM((2, size, width), BF),
            pltpu.VMEM((size, width), F32),
            pltpu.VMEM((size, width), BF),
            pltpu.VMEM((QUARTET, HALF, width), BF),
            pltpu.VMEM((QUARTET, HALF, width), BF),
            pltpu.VMEM((experts, 2 * pad, width), BF),
            pltpu.VMEM((experts, pad, width), BF),
            pltpu.VMEM((experts, slots, width), BF),
            pltpu.VMEM((experts, slots, width), BF),
            pltpu.VMEM((QUARTET, 2 * experts * cap, width), BF),
            pltpu.VMEM((4, size, width), BF),
        ]
        + scratch
        + [
            pltpu.VMEM((columns, experts, slots, pad), BF),
            pltpu.VMEM((experts, slots, 2 * pad), BF),
            pltpu.VMEM((8 * experts, SEQ), F32),
            pltpu.VMEM((8 * experts, SEQ), F32),
            pltpu.SemaphoreType.DMA((remote,)),
            pltpu.SemaphoreType.DMA((remote,)),
            pltpu.SemaphoreType.DMA((3 + 3 * experts,)),
            pltpu.SemaphoreType.DMA((16,)),
            pltpu.SemaphoreType.DMA((near,)),
            pltpu.SemaphoreType.DMA((4,)),
        ],
        compiler_params=pltpu.CompilerParams(
            collective_id=1, has_side_effects=True, vmem_limit_bytes=67_043_328
        ),
        cost_estimate=pl.CostEstimate(
            flops=16 * SEQ * experts * cap * width * 8,
            bytes_accessed=800 * SEQ * width,
            transcendentals=0,
        ),
        name="experts",
    )(attn_part, tokens, cotan_all, gate, up, down, gain, raw)
    return results[:9]


def first_kernel(columns, size, kinds, *refs):
    amount = len(kinds)
    rows_in, own_in = refs[:2], refs[2 : 2 + amount]
    rows_all, alls = refs[2 + amount : 4 + amount], refs[4 + amount : 4 + 2 * amount]
    rows_v, held = refs[4 + 2 * amount : 6 + 2 * amount], refs[6 + 2 * amount : 6 + 3 * amount]
    sends, arrivals, local = refs[6 + 3 * amount :]
    partner, along, across = plane_neighbours()
    column = column_neighbours(columns)
    rows_of = block_rows(columns, size)
    place = lax.axis_index("fsdp")
    devices = {
        0: place,
        1: partner[0],
        2: along[0],
        4: across[0],
        6: along[0] + across[0] - place,
    }
    greet([partner, along, across] + column)
    gathers = []
    for n in range(2):
        inward = pltpu.make_async_copy(rows_in[n], rows_v[n], local.at[n])
        inward.start()
        inward.wait()
        place_here = rows_all[n].at[rows_of(0)]
        outward = pltpu.make_async_copy(rows_v[n], place_here, local.at[n])
        outward.start()
        outward.wait()
        gathers.append(ColumnGather(rows_all[n], rows_of, sends, arrivals, 8 * amount + 4 * n))
        gathers[n].start()
    plans = []
    for k, kind in enumerate(kinds):
        own, everything = own_in[k], alls[k]
        rows, cols = own.shape
        top, bottom = pl.ds(0, rows // 2), pl.ds(rows // 2, rows // 2)
        whole = pl.ds(0, rows)

        def spot(r, hop, part, kind=kind, everything=everything, cols=cols):
            if kind == "relative":
                return everything.at[r ^ hop, part]
            if kind == "rows":
                return everything.at[devices[r], part]
            start = pl.multiple_of(devices[r] * cols, cols)
            return everything.at[part, pl.ds(start, cols)]

        plan = [
            (own, spot(0, 2, whole), along),
            (own, spot(0, 4, whole), across),
            (own, spot(0, 1, whole), partner),
            (spot(2, 0, top), spot(2, 4, top), across),
            (spot(4, 0, bottom), spot(4, 2, bottom), along),
            (spot(2, 0, whole), spot(2, 1, whole), partner),
            (spot(4, 0, whole), spot(4, 1, whole), partner),
            (spot(6, 0, whole), spot(6, 1, whole), partner),
        ]
        plans.append(
            [
                mesh_copy(src, dst, sends, arrivals, 8 * k + i, device)
                for i, (src, dst, device) in enumerate(plan)
            ]
        )
    for copies in plans:
        for copy in copies[:3]:
            copy.start()
    here, there = [], []
    for k, kind in enumerate(kinds):
        rows, cols = own_in[k].shape
        if kind == "relative":
            spot_here = alls[k].at[0]
        elif kind == "rows":
            spot_here = alls[k].at[place]
        else:
            spot_here = alls[k].at[:, pl.ds(pl.multiple_of(place * cols, cols), cols)]
        here.append(pltpu.make_async_copy(own_in[k], held[k], local.at[2 + k]))
        there.append(pltpu.make_async_copy(held[k], spot_here, local.at[2 + k]))
    for copy in here:
        copy.start()
    for copy in here:
        copy.wait()
    for copy in there:
        copy.start()
    for copies in plans:
        copies[0].wait_recv()
        copies[3].start()
        copies[5].start()
        copies[1].wait_recv()
        copies[4].start()
        copies[6].start()
    gathers[0].wait(2)
    for copies in plans:
        copies[3].wait_recv()
        copies[4].wait_recv()
        copies[7].start()
    for copies in plans:
        for i in (2, 5, 6, 7):
            copies[i].wait_recv()
    gathers[1].wait(2)
    for gather in gathers:
        gather.wait(1)
        gather.wait(3)
    for copy in there:
        copy.wait()
    for gather in gathers:
        gather.drain()
    for copies in plans:
        for copy in copies:
            copy.wait_send()


def first_call(tokens, cotan, owns, kinds):
    columns = lax.axis_size("tp")
    size, width = tokens.shape
    anywhere = pl.BlockSpec(memory_space=pl.ANY)
    copies = 8 * len(owns) + 8

    def gathered(own, kind):
        rows, cols = own.shape
        return (rows, 8 * cols) if kind == "columns" else (8, rows, cols)

    return pl.pallas_call(
        functools.partial(first_kernel, columns, size, kinds),
        out_shape=[jax.ShapeDtypeStruct((columns * size, width), BF)] * 2
        + [jax.ShapeDtypeStruct(gathered(own, kind), own.dtype) for own, kind in zip(owns, kinds)],
        in_specs=[anywhere] * (2 + len(owns)),
        out_specs=[anywhere] * (2 + len(owns)),
        scratch_shapes=[pltpu.VMEM((size, width), BF)] * 2
        + [pltpu.VMEM(own.shape, own.dtype) for own in owns]
        + [
            pltpu.SemaphoreType.DMA((copies,)),
            pltpu.SemaphoreType.DMA((copies,)),
            pltpu.SemaphoreType.DMA((2 + len(owns),)),
        ],
        compiler_params=pltpu.CompilerParams(collective_id=2, has_side_effects=True),
        cost_estimate=pl.CostEstimate(
            flops=0, bytes_accessed=240 * SEQ * width, transcendentals=0
        ),
        name="first_gather",
    )(tokens, cotan, *owns)


class PlaneSum:
    def __init__(self, source, chip, theirs, links, stage, sends, arrivals, base, local):
        self.source, self.chip, self.theirs, self.links = source, chip, theirs, links
        self.stage, self.sends, self.arrivals, self.base = stage, sends, arrivals, base
        self.local = local
        self.parts, self.rows = chip.shape[1], chip.shape[2]
        self.partner, self.along, self.across = plane_neighbours()

    def pair(self, i, h):
        return mesh_copy(
            self.source(2 * i + 1, h),
            self.theirs.at[i, h],
            self.sends,
            self.arrivals,
            self.base + i * self.parts + h,
            self.partner,
        )

    def mine(self, i, h):
        return pltpu.make_async_copy(
            self.source(2 * i, h), self.chip.at[i, h], self.local.at[4 + i * self.parts + h]
        )

    def begin(self):
        for i in (3, 1, 2, 0):
            for h in range(self.parts):
                self.pair(i, h).start()
                self.mine(i, h).start()

    def fetch(self, landed, slot):
        size = landed.shape[0]
        return pltpu.make_async_copy(
            landed, self.stage.at[slot, pl.ds(0, size)], self.local.at[slot]
        )

    def add(self, i, h, start, size, slot):
        some = min(32, size)

        def one(n, carry):
            rows = pl.ds(pl.multiple_of(start + n * some, some), some)
            from_rows = pl.ds(pl.multiple_of(n * some, some), some)
            self.chip[i, h, rows, :] = (
                self.chip[i, h, rows, :].astype(F32) + self.stage[slot, from_rows, :].astype(F32)
            ).astype(BF)
            return carry

        lax.fori_loop(0, size // some, one, 0)

    def send_first(self, parts=None, fetched=True):
        for h in range(self.parts) if parts is None else parts:
            for i in (3, 1, 2, 0):
                self.pair(i, h).wait_recv()
                self.fetch(self.theirs.at[i, h], i).start()
            for i in (3, 1, 2, 0):
                if fetched:
                    self.mine(i, h).wait()
                self.fetch(self.theirs.at[i, h], i).wait()
                self.add(i, h, 0, self.rows, i)
                if i == 3:
                    self.send(1, [h])
                if i == 2:
                    self.send(0, [h])

    def link(self, stage_number, side, h):
        first_hop, second_hop = (
            (self.along, self.across) if side == 0 else (self.across, self.along)
        )
        near, far = (1, 2) if side == 0 else (2, 1)
        i = (near, 3, far)[stage_number]
        place = (stage_number * 2 + side) * self.parts + h
        rows = pl.ds(side * (self.rows // 2), self.rows // 2)
        return mesh_copy(
            self.chip.at[i, h, rows],
            self.links.at[place],
            self.sends,
            self.arrivals,
            self.base + 4 * self.parts + place,
            second_hop if stage_number == 2 else first_hop,
        )

    def landed(self, stage_number, side, h):
        return self.links.at[(stage_number * 2 + side) * self.parts + h]

    def send(self, stage_number, parts=None):
        for h in range(self.parts) if parts is None else parts:
            for side in range(2):
                self.link(stage_number, side, h).start()

    def send_second(self, parts=None):
        half = self.rows // 2
        for h in range(self.parts) if parts is None else parts:
            for side in range(2):
                self.link(1, side, h).wait_recv()
                self.fetch(self.landed(1, side, h), side).start()
            for side in range(2):
                self.fetch(self.landed(1, side, h), side).wait()
                self.add((2, 1)[side], h, side * half, half, side)
                self.link(2, side, h).start()

    def finish(self, parts=None):
        half = self.rows // 2
        for h in range(self.parts) if parts is None else parts:
            for stage_number in (0, 2):
                for side in range(2):
                    self.link(stage_number, side, h).wait_recv()
                    self.fetch(self.landed(stage_number, side, h), stage_number + side).start()
            for stage_number in (0, 2):
                for side in range(2):
                    slot = stage_number + side
                    self.fetch(self.landed(stage_number, side, h), slot).wait()
                    self.add(0, h, side * half, half, slot)

    def drain(self, first_part=0):
        for h in range(self.parts):
            for i in range(4):
                if h >= first_part:
                    self.pair(i, h).wait_send()
            for stage_number in range(3):
                for side in range(2):
                    self.link(stage_number, side, h).wait_send()


def plane_sum_sizes(parts):
    return 10 * parts, 4 + 4 * parts


def plane_sum_space(parts, rows, width):
    landing = [
        jax.ShapeDtypeStruct((4, parts, rows, width), BF),
        jax.ShapeDtypeStruct((6 * parts, rows // 2, width), BF),
    ]
    scratch = [pltpu.VMEM((4, parts, rows, width), BF), pltpu.VMEM((4, rows, width), BF)]
    return landing, scratch


def middle_kernel(cap, columns, size, experts, steps, local_hidden, *refs):
    (
        d_ffn_in,
        mixed_in,
        cotan_in,
        gain_ref,
        slot_table,
        weight_table,
        down_in,
        x_all,
        d_all,
        hid_all,
        dgu_all,
        d_mixed_out,
        d_proj_all,
        gain_out,
        routed_out,
        gate_grad,
        up_grad,
        down_grad,
        theirs,
        links,
        chip,
        stage,
        own_v,
        arrived_v,
        relayed_v,
        mixed_v,
        cotan_v,
        proj_v,
        xk,
        dk,
        hk,
        gk,
        totals,
        hid,
        down,
        parts,
        others,
        sends,
        arrivals,
        local,
        sum_local,
        work,
        written,
    ) = refs
    partner, along, across = plane_neighbours()
    column = column_neighbours(columns)
    greet([partner, along, across] + column)
    plane = PlaneSum(
        lambda r, h: others.at[h % 2, r // 2],
        chip,
        theirs,
        links,
        stage,
        sends,
        arrivals,
        0,
        sum_local,
    )
    base = plane_sum_sizes(columns)[0]
    rows_of = block_rows(columns, size)
    summed = ColumnSum(d_ffn_in, rows_of, arrived_v, relayed_v, sends, arrivals, base)
    gather = ColumnGather(d_proj_all, rows_of, sends, arrivals, base + 4)
    summed.start(local.at[3])
    first = [
        pltpu.make_async_copy(d_ffn_in.at[rows_of(0)], own_v, local.at[0]),
        pltpu.make_async_copy(mixed_in, mixed_v, local.at[1]),
        pltpu.make_async_copy(cotan_in, cotan_v, local.at[2]),
    ]
    for copy in first:
        copy.start()
    width = xk.shape[2]
    pad = hk.shape[2]
    tile = min(1024, width)
    hidden_in = [pltpu.make_async_copy(hid_all.at[b], hid.at[b], local.at[4 + b]) for b in range(columns)]
    down_copies = [
        pltpu.make_async_copy(
            down_in.at[e], down.at[e, pl.ds(0, local_hidden)], local.at[4 + columns + e]
        )
        for e in range(experts)
    ]
    for copy in down_copies + hidden_in:
        copy.start()
    summed.clear()
    rest = down.shape[1] - local_hidden
    if rest > 0:
        for e in range(experts):
            down[e, local_hidden:, :] = jnp.zeros((rest, down.shape[2]), BF)
    for copy in down_copies:
        copy.wait()
    wide = 2 * cap

    def out_part(b):
        hidden_in[b].wait()
        weights = [
            slot_weights(
                select_rows(slots_of(slot_table, experts, columns, size, b, q), experts, wide),
                slots_of(weight_table, experts, columns, size, b, q),
                experts,
                wide,
            )
            for q in range(QUARTET)
        ]
        for e in range(experts):

            def one_tile(n, carry, e=e):
                cols = pl.ds(pl.multiple_of(n * tile, tile), tile)
                rows = dot_plain(hid[b, e], down[e, :, cols])
                for q in range(QUARTET):
                    parts[q, e * wide : (e + 1) * wide, cols] = (
                        rows[q * wide : (q + 1) * wide] * weights[q][e * wide : (e + 1) * wide]
                    ).astype(BF)
                return carry

            lax.fori_loop(0, width // tile, one_tile, 0)
        if b > 1:
            for i in range(4):
                plane.pair(i, b - 2).wait_send()

        def keep(q, cols, value):
            chip[q, b, :, cols] = value[:size]
            others[b % 2, q, :, cols] = value[size:]

        token_sums(slot_table, experts, columns, size, wide, b, parts, keep)
        for i in range(4):
            plane.pair(i, b).start()

    jobs = [(e, step) for e in range(experts) for step in range(steps)]

    def fetch(k):
        e, step = jobs[k]
        slot = k % 2
        return [
            pltpu.make_async_copy(x_all.at[step, e], xk.at[slot], work.at[slot, 0]),
            pltpu.make_async_copy(d_all.at[step, e], dk.at[slot], work.at[slot, 1]),
            pltpu.make_async_copy(hid_all.at[step, e], hk.at[slot], work.at[slot, 2]),
            pltpu.make_async_copy(dgu_all.at[step, e], gk.at[slot], work.at[slot, 3]),
        ]

    def write(e):
        return [
            pltpu.make_async_copy(
                totals.at[e % 2, i, pl.ds(0, local_hidden)], grad.at[e], written.at[e % 2, i]
            )
            for i, grad in enumerate((gate_grad, up_grad, down_grad))
        ]

    def job(k):
        e, step = jobs[k]
        slot, place = k % 2, e % 2
        if k + 1 < len(jobs):
            for copy in fetch(k + 1):
                copy.start()
        for copy in fetch(k):
            copy.wait()
        if step == 0 and e > 1:
            for copy in write(e - 2):
                copy.wait()

        def one(n, carry):
            cols = pl.ds(pl.multiple_of(n * tile, tile), tile)
            found = [
                dot_first(gk[slot, :, :pad], xk[slot, :, cols]),
                dot_first(gk[slot, :, pad:], xk[slot, :, cols]),
                dot_first(hk[slot], dk[slot, :, cols]),
            ]
            for i, value in enumerate(found):
                if step == 0:
                    totals[place, i, :, cols] = value
                else:
                    totals[place, i, :, cols] += value
            return carry

        lax.fori_loop(0, width // tile, one, 0)
        if step == steps - 1:
            for copy in write(e):
                copy.start()

    out_part(0)
    out_part(1)
    summed.middle(local.at[3])
    plane.send_first([0], False)
    out_part(2)
    plane.send_first([1], False)
    for copy in fetch(0):
        copy.start()
    out_part(3)
    plane.send_first([2], False)
    job(0)
    plane.send_first([3], False)

    for copy in first:
        copy.wait()
    total = summed.total(own_v[...])
    mixed = mixed_v[...]
    inverse = lax.rsqrt(jnp.mean(mixed * mixed, axis=1, keepdims=True) + EPSILON)
    unit = mixed * inverse
    scaled = total * gain_ref[...]
    gain_out[...] = jnp.sum(total * unit, axis=0, keepdims=True)
    back = inverse * (scaled - unit * jnp.mean(scaled * unit, axis=1, keepdims=True))
    d_mixed = cotan_v[...].astype(F32) + back
    mixed_v[...] = d_mixed
    proj_v[...] = d_mixed.astype(BF)
    own_copy = pltpu.make_async_copy(proj_v, d_proj_all.at[rows_of(0)], local.at[0])
    own_copy.start()
    mixed_copy = pltpu.make_async_copy(mixed_v, d_mixed_out, local.at[1])
    mixed_copy.start()
    own_copy.wait()
    gather.start()
    for b in range(columns):
        if b + 1 < len(jobs):
            job(b + 1)
        plane.send_second([b])
        if b == 1:
            gather.wait(2)
    for b in range(columns):
        if columns + 1 + b < len(jobs):
            job(columns + 1 + b)
        if b < columns - 1:
            plane.finish([b])
    for k in range(2 * columns + 1, len(jobs)):
        job(k)
    plane.finish([columns - 1])
    done = [
        pltpu.make_async_copy(chip.at[0, h], routed_out.at[rows_of(h)], sum_local.at[4 + h])
        for h in range(columns)
    ]
    for copy in done:
        copy.start()
    gather.wait(1)
    gather.wait(3)
    for copy in done + [mixed_copy]:
        copy.wait()
    for e in range(max(0, experts - 2), experts):
        for copy in write(e):
            copy.wait()
    plane.drain(2)
    gather.drain()
    summed.drain()


def middle_call(d_ffn, mixed, cotan, gain, tables, down, kept, cap):
    columns = lax.axis_size("tp")
    size, width = cotan.shape
    x_all, d_all, hid_all, dgu_all = kept
    steps, experts, slots, pad = hid_all.shape
    local_hidden = down.shape[1]
    anywhere = pl.BlockSpec(memory_space=pl.ANY)
    held = pl.BlockSpec(memory_space=pltpu.VMEM)
    landing, scratch = plane_sum_space(columns, size, width)
    remote, near = plane_sum_sizes(columns)
    remote = remote + 8
    grad = jax.ShapeDtypeStruct((experts, local_hidden, width), F32)
    results = pl.pallas_call(
        functools.partial(middle_kernel, cap, columns, size, experts, steps, local_hidden),
        out_shape=[
            jax.ShapeDtypeStruct((size, width), F32),
            jax.ShapeDtypeStruct((SEQ, width), BF),
            jax.ShapeDtypeStruct((1, width), F32),
            jax.ShapeDtypeStruct((SEQ, width), BF),
            grad,
            grad,
            grad,
        ]
        + landing,
        in_specs=[anywhere] * 3 + [held] * 3 + [anywhere] * 5,
        out_specs=[anywhere] * 2 + [held] + [anywhere] * 6,
        scratch_shapes=scratch
        + [
            pltpu.VMEM((size, width), BF),
            pltpu.VMEM((columns - 1, size, width), BF),
            pltpu.VMEM((2, size, width), BF),
            pltpu.VMEM((size, width), F32),
            pltpu.VMEM((size, width), BF),
            pltpu.VMEM((size, width), BF),
            pltpu.VMEM((2, slots, width), BF),
            pltpu.VMEM((2, slots, width), BF),
            pltpu.VMEM((2, slots, pad), BF),
            pltpu.VMEM((2, slots, 2 * pad), BF),
            pltpu.VMEM((2, 3, pad, width), F32),
            pltpu.VMEM((steps, experts, slots, pad), BF),
            pltpu.VMEM((experts, pad, width), BF),
            pltpu.VMEM((QUARTET, 2 * experts * cap, width), BF),
            pltpu.VMEM((2, 4, size, width), BF),
            pltpu.SemaphoreType.DMA((remote,)),
            pltpu.SemaphoreType.DMA((remote,)),
            pltpu.SemaphoreType.DMA((4 + columns + experts,)),
            pltpu.SemaphoreType.DMA((near,)),
            pltpu.SemaphoreType.DMA((2, 4)),
            pltpu.SemaphoreType.DMA((2, 3)),
        ],
        compiler_params=pltpu.CompilerParams(
            collective_id=3, has_side_effects=True, vmem_limit_bytes=67_043_328
        ),
        cost_estimate=pl.CostEstimate(
            flops=2 * 3 * steps * experts * slots * width * pad,
            bytes_accessed=300 * SEQ * width,
            transcendentals=0,
        ),
        name="middle",
    )(d_ffn, mixed, cotan, gain, *tables, down, x_all, d_all, hid_all, dgu_all)
    return results[:7]


def last_kernel(columns, size, latent_start, latent_width, *refs):
    (
        d_normed_in,
        tokens_in,
        d_mixed_in,
        gain_ref,
        joint_in,
        up_in,
        out_in,
        sums_in,
        grad_out,
        joint_out,
        up_out,
        out_out,
        latent_out,
        sums_out,
        joint_theirs,
        joint_links,
        up_theirs,
        up_links,
        out_theirs,
        out_links,
        joint_chip,
        joint_stage,
        up_chip,
        up_stage,
        out_chip,
        out_stage,
        own_v,
        arrived_v,
        relayed_v,
        tokens_v,
        mixed_v,
        running,
        sums_v,
        latent_v,
        sends,
        arrivals,
        local,
        joint_local,
        up_local,
        out_local,
    ) = refs
    partner, along, across = plane_neighbours()
    column = column_neighbours(columns)
    place, row = lax.axis_index("fsdp"), lax.axis_index("tp")
    core, right, above = place % 2, (place // 2) % 2, place // 4

    def absolute(r):
        return (
            (above + r // 4) % 2 * 4 + (right + r // 2 % 2) % 2 * 2 + (core + r % 2) % 2
        )

    greet([partner, along, across] + column)
    each = plane_sum_sizes(1)[0]
    joint_rows, up_rows = joint_chip.shape[2], up_chip.shape[2]
    out_cols = out_chip.shape[3]

    def by_rows(ref, count):
        return lambda r, h: ref.at[pl.ds(pl.multiple_of(absolute(r) * count, count), count)]

    joint = PlaneSum(
        by_rows(joint_in, joint_rows),
        joint_chip,
        joint_theirs,
        joint_links,
        joint_stage,
        sends,
        arrivals,
        0,
        joint_local,
    )
    up = PlaneSum(
        by_rows(up_in, up_rows),
        up_chip,
        up_theirs,
        up_links,
        up_stage,
        sends,
        arrivals,
        each,
        up_local,
    )
    out = PlaneSum(
        lambda r, h: out_in.at[
            :, pl.ds(pl.multiple_of(absolute(r) * out_cols, out_cols), out_cols)
        ],
        out_chip,
        out_theirs,
        out_links,
        out_stage,
        sends,
        arrivals,
        2 * each,
        out_local,
    )
    base = 3 * each
    rows_of = block_rows(columns, size)
    summed = ColumnSum(d_normed_in, rows_of, arrived_v, relayed_v, sends, arrivals, base)
    base = base + 4
    summed.start(local.at[4])
    first = [
        pltpu.make_async_copy(d_normed_in.at[rows_of(0)], own_v, local.at[0]),
        pltpu.make_async_copy(tokens_in, tokens_v, local.at[1]),
        pltpu.make_async_copy(d_mixed_in, mixed_v, local.at[2]),
        pltpu.make_async_copy(sums_in, running.at[0], local.at[3]),
    ]
    for copy in first:
        copy.start()
    for part in (out, joint, up):
        part.begin()
    summed.clear()
    first[3].wait()

    def small(i, device):
        return mesh_copy(running.at[i], sums_v.at[i], sends, arrivals, base + i, device)

    hops = [small(i, device) for i, device in enumerate((partner, along, across))]
    for i, copy in enumerate(hops):
        copy.start()
        copy.wait_recv()
        running[i + 1] = running[i] + sums_v[i]
    gains = [
        mesh_copy(running.at[3], sums_v.at[2 + s], sends, arrivals, base + 2 + s, column[s - 1])
        for s in range(1, columns)
    ]
    base = base + 2 + columns
    for copy in gains:
        copy.start()
    summed.middle(local.at[4])
    for part in (out, joint, up):
        part.send_first()
    for part in (out, joint, up):
        part.send_second()
    for part in (out, joint, up):
        part.finish()

    pieces = joint_rows // columns
    across_columns = [
        mesh_copy(
            joint_chip.at[
                0,
                0,
                pl.ds(pl.multiple_of((row + s) % columns * pieces, pieces), pieces),
                pl.ds(latent_start, latent_width),
            ],
            latent_v.at[s - 1],
            sends,
            arrivals,
            base + s - 1,
            column[s - 1],
        )
        for s in range(1, columns)
    ]
    for copy in across_columns:
        copy.start()
    done = [
        pltpu.make_async_copy(joint_chip.at[0, 0], joint_out, joint_local.at[4]),
        pltpu.make_async_copy(up_chip.at[0, 0], up_out, up_local.at[4]),
        pltpu.make_async_copy(out_chip.at[0, 0], out_out, out_local.at[4]),
    ]
    for copy in done:
        copy.start()

    for copy in first[:3]:
        copy.wait()
    total = summed.total(own_v[...])
    tokens = tokens_v[...].astype(F32)
    inverse = lax.rsqrt(jnp.mean(tokens * tokens, axis=1, keepdims=True) + EPSILON)
    unit = tokens * inverse
    scaled = total * gain_ref[...]
    mixed_v[...] = mixed_v[...] + inverse * (
        scaled - unit * jnp.mean(scaled * unit, axis=1, keepdims=True)
    )
    grad_copy = pltpu.make_async_copy(mixed_v, grad_out, local.at[0])
    grad_copy.start()
    gathered = running[3]
    for s in range(1, columns):
        gains[s - 1].wait_recv()
        gathered = gathered + sums_v[2 + s]
    sums_out[...] = gathered
    latent = joint_chip[
        0,
        0,
        pl.ds(pl.multiple_of(row * pieces, pieces), pieces),
        pl.ds(latent_start, latent_width),
    ].astype(F32)
    for s in range(1, columns):
        across_columns[s - 1].wait_recv()
        latent = latent + latent_v[s - 1].astype(F32)
    latent_out[...] = latent
    for copy in done + [grad_copy]:
        copy.wait()
    for part in (out, joint, up):
        part.drain()
    summed.drain()
    for copy in hops + gains + across_columns:
        copy.wait_send()


def last_call(d_normed, tokens, d_mixed, gain, joint, up, out, sums, latent_start, latent_width):
    columns = lax.axis_size("tp")
    size, width = tokens.shape
    anywhere = pl.BlockSpec(memory_space=pl.ANY)
    held = pl.BlockSpec(memory_space=pltpu.VMEM)
    shapes = [
        (joint.shape[0] // 8, joint.shape[1]),
        (up.shape[0] // 8, up.shape[1]),
        (out.shape[0], out.shape[1] // 8),
    ]
    landing, scratch = [], []
    for rows, cols in shapes:
        one = plane_sum_space(1, rows, cols)
        landing, scratch = landing + one[0], scratch + one[1]
    remote, near = plane_sum_sizes(1)
    remote = 3 * remote + 2 * (columns - 1) + 7
    pieces = shapes[0][0] // columns
    return pl.pallas_call(
        functools.partial(last_kernel, columns, size, latent_start, latent_width),
        out_shape=[jax.ShapeDtypeStruct((size, width), F32)]
        + [jax.ShapeDtypeStruct(shape, BF) for shape in shapes]
        + [
            jax.ShapeDtypeStruct((pieces, latent_width), F32),
            jax.ShapeDtypeStruct(sums.shape, F32),
        ]
        + landing,
        in_specs=[anywhere] * 3 + [held] + [anywhere] * 4,
        out_specs=[anywhere] * 4 + [held] * 2 + [anywhere] * 6,
        scratch_shapes=scratch
        + [
            pltpu.VMEM((size, width), BF),
            pltpu.VMEM((columns - 1, size, width), BF),
            pltpu.VMEM((2, size, width), BF),
            pltpu.VMEM((size, width), BF),
            pltpu.VMEM((size, width), F32),
            pltpu.VMEM((4,) + sums.shape, F32),
            pltpu.VMEM((2 + columns,) + sums.shape, F32),
            pltpu.VMEM((columns - 1, pieces, latent_width), BF),
            pltpu.SemaphoreType.DMA((remote,)),
            pltpu.SemaphoreType.DMA((remote,)),
            pltpu.SemaphoreType.DMA((5,)),
            pltpu.SemaphoreType.DMA((near,)),
            pltpu.SemaphoreType.DMA((near,)),
            pltpu.SemaphoreType.DMA((near,)),
        ],
        compiler_params=pltpu.CompilerParams(
            collective_id=4, has_side_effects=True, vmem_limit_bytes=48 * 1024 * 1024
        ),
        cost_estimate=pl.CostEstimate(
            flops=0, bytes_accessed=180 * SEQ * width, transcendentals=0
        ),
        name="last_sums",
    )(d_normed, tokens, d_mixed, gain, joint, up, out, sums)[:6]


def plane_units(count):
    return [[(2 * i + j // 2, j % 2) for j in range(4)] for i in range(count // 2)]


def plane_gather(rows, count):
    gathered = lax.all_gather(rows, "fsdp", axis=0)
    return {
        (r, h): gathered[r, h * HALF : (h + 1) * HALF] for r in range(count) for h in (0, 1)
    }


def plane_scatter_whole(pairs, units, count):
    parts = {}
    for unit, pair in zip(units, pairs):
        for q, key in enumerate(unit):
            parts[key] = pair[q // 2][q % 2]
    stacked = jnp.concatenate([parts[r, h] for r in range(count) for h in (0, 1)], axis=0)
    return lax.psum_scatter(stacked, "fsdp", scatter_dimension=0, tiled=True).astype(F32)


def sum_everywhere(values):
    for axis_name in ("fsdp", "tp"):
        count = lax.axis_size(axis_name)
        if is_power(count):
            bit = 1
            while bit < count:
                values = values + swap(values, axis_name, bit)
                bit *= 2
        else:
            values = lax.psum(values, axis_name)
    return values


def expert_tables(expert_ids, expert_wts, local_experts, units, cap):
    fsdp_count = lax.axis_size("fsdp")
    fsdp_rank = lax.axis_index("fsdp")
    expert_count = local_experts * fsdp_count
    names = jnp.arange(expert_count, dtype=jnp.int32)[:, None]
    member = jnp.zeros((expert_count, SEQ), jnp.bool_)
    weight = jnp.zeros((expert_count, SEQ), F32)
    ids_rows, wts_rows = expert_ids.T, expert_wts.T
    for pick in range(TOPK):
        same = ids_rows[pick : pick + 1] == names
        member = member | same
        weight = weight + jnp.where(same, wts_rows[pick : pick + 1], 0.0)
    position = jnp.arange(HALF)
    before = (position[:, None] < position[None, :]).astype(BF)
    rank = jnp.dot(
        member.astype(BF).reshape(expert_count * 2, HALF), before, preferred_element_type=F32
    ).reshape(expert_count, SEQ)
    slot = jnp.where(member, rank, NO_SLOT)
    table = jnp.concatenate([slot, weight], axis=0)
    table = lax.all_gather(table, "fsdp", axis=0, tiled=True)
    table = table.reshape(fsdp_count, 2, fsdp_count, local_experts, 2, HALF)
    table = lax.dynamic_index_in_dim(table, fsdp_rank, axis=2, keepdims=False)
    slot_steps, weight_steps = [], []
    for unit in units:
        slot_steps.append(jnp.stack([table[r, 0, :, h] for r, h in unit]))
        weight_steps.append(jnp.stack([table[r, 1, :, h] for r, h in unit]))
    slot_row, weight_row = jnp.stack(slot_steps), jnp.stack(weight_steps)
    return (slot_row, weight_row, jnp.swapaxes(slot_row, 2, 3))


def per_device(
    block_in,
    out_cotan,
    segment_ids,
    expert_ids,
    expert_wts,
    attn_gain,
    query_proj,
    latent_proj,
    latent_gain,
    latent_up,
    out_proj,
    ffn_gain,
    shared_gate,
    shared_up,
    shared_down,
    routed_gate,
    routed_up,
    routed_down,
):
    tp_count = lax.axis_size("tp")
    fsdp_count = lax.axis_size("fsdp")
    tp_rank = lax.axis_index("tp")
    fsdp_rank = lax.axis_index("fsdp")
    tok_rows, model_width = block_in.shape
    local_experts, local_hidden = routed_gate.shape[:2]
    expert_count = local_experts * fsdp_count
    cap_rows = tok_rows * TOPK * 4 // (3 * expert_count)
    cap = cap_rows * (HALF // tok_rows)
    paired = fsdp_count == 8 and tp_count == 4 and tok_rows * 2 == HALF
    heads_local = H // tp_count
    head_width = NOPE + ROPE
    score_scale = head_width ** (-0.5)
    shard_rows, query_cols = query_proj.shape
    latent_cols = latent_proj.shape[1]
    up_cols = latent_up.shape[1]
    out_rows = out_proj.shape[0]

    joint = query_cols + latent_cols
    spare = (-joint) % 128
    spare = spare + 128 if spare < 3 else spare
    gains = jnp.concatenate(
        [
            attn_gain[:, None],
            ffn_gain[:, None],
            jnp.pad(latent_gain, (0, shard_rows - latent_gain.shape[0]))[:, None],
            jnp.zeros((shard_rows, spare - 3), BF),
        ],
        axis=1,
    )
    packed = jnp.concatenate([query_proj, latent_proj, gains], axis=1)
    if paired:
        low, high = (0, RAW_ROWS - TOPK), (0, 0)
        raw = jnp.concatenate(
            [jnp.pad(expert_ids.T.astype(F32), (low, high)), jnp.pad(expert_wts.T, (low, high))]
        )
        (
            tokens_all,
            cotan_all,
            packed_all,
            latent_up_weight,
            out_weight,
            raw,
            shared_weight,
            shared_down_weight,
        ) = first_call(
            block_in,
            out_cotan,
            [
                packed,
                latent_up,
                out_proj,
                raw,
                jnp.concatenate([shared_gate, shared_up], axis=1),
                shared_down,
            ],
            ("rows", "rows", "columns", "relative", "rows", "columns"),
        )
        shared_weight = shared_weight.reshape(model_width, -1)
        packed_all = packed_all.reshape(-1, packed.shape[1])
        latent_up_weight = latent_up_weight.reshape(LAT, up_cols)
    else:
        packed_all = lax.all_gather(packed, "fsdp", axis=0, tiled=True)
        latent_up_weight = lax.all_gather(latent_up, "fsdp", axis=0, tiled=True)
        out_weight = lax.all_gather(out_proj, "fsdp", axis=1, tiled=True)
        tokens_all = column_gather(block_in)
        cotan_all = column_gather(out_cotan)
        shared_weight = lax.all_gather(
            jnp.concatenate([shared_gate, shared_up], axis=1), "fsdp", axis=0, tiled=True
        )
        shared_down_weight = lax.all_gather(shared_down, "fsdp", axis=1, tiled=True)
    gain_attn = packed_all[:, joint].astype(F32)
    gain_ffn = packed_all[:, joint + 1].astype(F32)
    gain_latent = (
        packed_all[:, joint + 2]
        .reshape(fsdp_count, shard_rows)[:, : latent_gain.shape[0]]
        .reshape(LAT)
        .astype(F32)
    )
    shared_cols = shared_gate.shape[1]

    def scatter(part, dimension):
        return lax.psum_scatter(part.astype(BF), "fsdp", scatter_dimension=dimension, tiled=True)

    unit_all, inverse_all = norm_parts(tokens_all.astype(F32))
    normed_all = (unit_all * gain_attn).astype(BF)
    joint_rows = jnp.dot(normed_all, packed_all, preferred_element_type=F32)
    queries = joint_rows[:, :query_cols].reshape(SEQ, heads_local, head_width)
    latent = joint_rows[:, query_cols:joint]
    unit_lat, inverse_lat = norm_parts(latent[:, :LAT])
    positions = jnp.arange(SEQ, dtype=jnp.int32)
    cosine, sine_part = rope_tables(positions, ROPE)
    compressed_all = (unit_lat * gain_latent).astype(BF)
    key_rope_all = rotate(latent[:, LAT:], cosine, sine_part).astype(BF)
    query_cat = jnp.concatenate(
        [
            queries[:, :, :NOPE],
            rotate(queries[:, :, NOPE:], cosine[:, None, :], sine_part[:, None, :]),
        ],
        axis=2,
    ).astype(BF)
    key_value = (
        jnp.dot(compressed_all, latent_up_weight, preferred_element_type=F32)
        .reshape(SEQ, heads_local, NOPE + DV)
        .astype(BF)
    )
    key_cat = jnp.concatenate(
        [
            key_value[:, :, :NOPE],
            jnp.broadcast_to(key_rope_all[:, None, :], (SEQ, heads_local, ROPE)),
        ],
        axis=2,
    )
    values = key_value[:, :, NOPE:]
    allowed = (positions[None, :] <= positions[:, None]) & (
        segment_ids[None, :] == segment_ids[:, None]
    )
    raw_scores = (
        jnp.einsum("qhd,khd->hqk", query_cat, key_cat, preferred_element_type=F32) * score_scale
    )
    masked = jnp.where(allowed[None], raw_scores, MASK_FILL)
    top_score = jnp.max(masked, axis=2, keepdims=True)
    exponent = jnp.exp(masked - top_score)
    row_total = jnp.sum(exponent, axis=2, keepdims=True)
    probabilities = exponent / row_total
    probs_low = probabilities.astype(BF)
    attended = (
        jnp.einsum("hqk,khd->qhd", probs_low, values, preferred_element_type=F32)
        .reshape(SEQ, heads_local * DV)
        .astype(BF)
    )
    attn_part = jnp.dot(attended, out_weight, preferred_element_type=F32).astype(BF)
    if paired:
        mixed_rows, normed_ffn_all, d_routed_in, *kept = expert_call(
            attn_part,
            block_in,
            cotan_all,
            routed_gate,
            routed_up,
            routed_down,
            gain_ffn[None, :],
            raw,
            cap_rows,
        )
        unit_two, inverse_two = norm_parts(mixed_rows)
        d_routed_in = d_routed_in.astype(F32)
    else:
        units = plane_units(fsdp_count)
        tables = expert_tables(expert_ids, expert_wts, local_experts, units, cap)
        hidden_pad = -(-local_hidden // 128) * 128
        lift = ((0, 0), (0, hidden_pad - local_hidden), (0, 0))
        routed_gate_up = jnp.concatenate(
            [jnp.pad(routed_gate, lift), jnp.pad(routed_up, lift)], axis=1
        )
        routed_down_pad = jnp.pad(routed_down, lift)
        mixed_rows = block_in.astype(F32) + column_scatter(attn_part)
        unit_two, inverse_two = norm_parts(mixed_rows)
        normed_ffn_all = column_gather((unit_two * gain_ffn).astype(BF))
        x_blocks = plane_gather(normed_ffn_all, fsdp_count)
        dy_all = lax.all_gather(cotan_all, "fsdp", axis=0, tiled=True)
        kept = []
        dx_pairs = []
        for step, unit in enumerate(units):
            pair, kept = expert_front(
                step,
                len(units),
                [x_blocks[key] for key in unit],
                jnp.array([2 * r + h for r, h in unit], jnp.int32),
                dy_all,
                routed_gate_up,
                routed_down_pad,
                tables,
                kept,
                cap,
            )
            dx_pairs.append(pair)
        near, far = expert_out(kept[2], routed_down_pad, tables, cap)
        d_routed_in = plane_scatter_whole(dx_pairs, units, fsdp_count)
    if not paired:
        routed_gate_grad, routed_up_grad, routed_down_grad = expert_grads(kept, local_hidden)

    shared_pre = jnp.dot(normed_ffn_all, shared_weight, preferred_element_type=F32)
    shared_gate_pre, shared_up_pre = shared_pre[:, :shared_cols], shared_pre[:, shared_cols:]
    shared_hidden = (jax.nn.silu(shared_gate_pre) * shared_up_pre).astype(BF)
    shared_rows = jnp.dot(shared_hidden, shared_down_weight, preferred_element_type=F32)
    shared_down_part = jnp.dot(shared_hidden.T, cotan_all, preferred_element_type=F32)
    d_shared_hidden = jnp.dot(cotan_all, shared_down_weight.T, preferred_element_type=F32)
    d_shared = jnp.concatenate(silu_back(d_shared_hidden, shared_gate_pre, shared_up_pre), axis=1)
    shared_part = jnp.dot(normed_ffn_all.T, d_shared, preferred_element_type=F32)
    d_shared_in = jnp.dot(d_shared, shared_weight.T, preferred_element_type=F32)

    if paired:
        d_ffn_rows, shared_part, shared_down_part = tie(
            (d_shared_in + d_routed_in).astype(BF),
            shared_part.astype(BF),
            shared_down_part.astype(BF),
        )
        (
            d_mixed,
            d_proj_all,
            ffn_gain_part,
            routed_rows,
            routed_gate_grad,
            routed_up_grad,
            routed_down_grad,
        ) = middle_call(
            d_ffn_rows,
            mixed_rows,
            out_cotan,
            gain_ffn[None, :],
            kept[:2],
            routed_down,
            kept[2:],
            cap_rows,
        )
        ffn_gain_part = ffn_gain_part[0]
        routed_rows = routed_rows.astype(F32)
    else:
        d_normed_ffn = column_scatter(d_shared_in + d_routed_in)
        out_pairs = [(near[step], far[step]) for step in range(len(units))]
        routed_rows = plane_scatter_whole(out_pairs, units, fsdp_count)
        ffn_gain_part, d_mixed_norm = norm_back(d_normed_ffn, unit_two, inverse_two, gain_ffn)
        d_mixed = out_cotan.astype(F32) + d_mixed_norm
        d_proj_all = column_gather(d_mixed.astype(BF))
    shared_grad = scatter(shared_part, 0)
    down_own, ffn_rows, shared_grad = tie(
        shared_down_part.astype(BF), (shared_rows + routed_rows).astype(BF), shared_grad
    )
    shared_down_grad = scatter(down_own, 1)
    ffn_rows = column_scatter(ffn_rows)
    block_out = (mixed_rows + ffn_rows).astype(BF)

    out_part = jnp.dot(attended.T, d_proj_all, preferred_element_type=F32)
    d_attended = (
        jnp.dot(d_proj_all, out_weight.T, preferred_element_type=F32)
        .astype(BF)
        .reshape(SEQ, heads_local, DV)
    )
    prob_grad = jnp.einsum("qhd,khd->hqk", d_attended, values, preferred_element_type=F32)
    score_grad = (
        probabilities
        * (prob_grad - jnp.sum(probabilities * prob_grad, axis=2, keepdims=True))
    ).astype(BF)
    query_grad = (
        jnp.einsum("hqk,khd->qhd", score_grad, key_cat, preferred_element_type=F32) * score_scale
    )
    key_grad = (
        jnp.einsum("hqk,qhd->khd", score_grad, query_cat, preferred_element_type=F32) * score_scale
    )
    value_grad = jnp.einsum("hqk,qhd->khd", probs_low, d_attended, preferred_element_type=F32)
    d_queries = (
        jnp.concatenate(
            [
                query_grad[:, :, :NOPE],
                unrotate(query_grad[:, :, NOPE:], cosine[:, None, :], sine_part[:, None, :]),
            ],
            axis=2,
        )
        .reshape(SEQ, heads_local * head_width)
        .astype(BF)
    )
    d_key_value = (
        jnp.concatenate([key_grad[:, :, :NOPE], value_grad], axis=2)
        .reshape(SEQ, heads_local * (NOPE + DV))
        .astype(BF)
    )
    latent_up_part = jnp.dot(compressed_all.T, d_key_value, preferred_element_type=F32)
    d_compressed = jnp.dot(d_key_value, latent_up_weight.T, preferred_element_type=F32)
    d_key_rope = jnp.sum(key_grad[:, :, NOPE:], axis=1)
    latent_gain_part, d_latent_main = norm_back(d_compressed, unit_lat, inverse_lat, gain_latent)
    d_latent = jnp.concatenate(
        [d_latent_main, unrotate(d_key_rope, cosine, sine_part)], axis=1
    ).astype(BF)
    d_joint = jnp.concatenate([d_queries, d_latent, jnp.zeros((SEQ, spare), BF)], axis=1)
    joint_part = jnp.dot(normed_all.T, d_joint, preferred_element_type=F32)
    d_normed_part = jnp.dot(d_joint, packed_all.T, preferred_element_type=F32)
    attn_gain_part = jnp.sum(d_normed_part * unit_all, axis=0)

    gain_parts = jnp.concatenate([attn_gain_part, latent_gain_part, ffn_gain_part]).reshape(
        -1, 128
    )
    joint_part = joint_part.astype(BF)
    if paired:
        latent_width = joint_part.shape[1] - query_cols
        (
            block_in_grad,
            joint_grad,
            latent_up_grad,
            out_proj_grad,
            latent_proj_grad,
            gain_sums,
        ) = last_call(
            d_normed_part.astype(BF),
            block_in,
            d_mixed,
            gain_attn[None, :],
            joint_part,
            latent_up_part.astype(BF),
            out_part.astype(BF),
            gain_parts,
            query_cols,
            latent_width,
        )
        latent_proj_grad = latent_proj_grad[:, :latent_cols]
    else:
        d_normed = column_scatter(d_normed_part)
        unit_one, inverse_one = norm_parts(block_in.astype(F32))
        _, d_tokens_norm = norm_back(d_normed, unit_one, inverse_one, gain_attn)
        block_in_grad = d_mixed + d_tokens_norm
        out_proj_grad = scatter(out_part, 1)
        latent_up_grad = scatter(latent_up_part, 0)
        joint_grad = scatter(joint_part, 0)
        latent_proj_grad = column_scatter(joint_grad[:, query_cols:joint])
        gain_sums = sum_everywhere(gain_parts)
    gain_sums = gain_sums.reshape(-1)
    query_proj_grad = joint_grad[:, :query_cols].astype(F32)
    latent_up_grad = latent_up_grad.astype(F32)
    out_proj_grad = out_proj_grad.astype(F32)
    shared_grad = shared_grad.astype(F32)
    shared_gate_grad, shared_up_grad = shared_grad[:, :shared_cols], shared_grad[:, shared_cols:]
    shared_down_grad = shared_down_grad.astype(F32)
    device = fsdp_rank * tp_count + tp_rank
    devices = tp_count * fsdp_count

    def own_gain(start, size):
        return lax.dynamic_slice(gain_sums, (start + device * (size // devices),), (size // devices,))

    attn_gain_grad = own_gain(0, model_width)
    latent_gain_grad = own_gain(model_width, LAT)
    ffn_gain_grad = own_gain(model_width + LAT, model_width)
    return (
        block_out,
        block_in_grad,
        attn_gain_grad,
        query_proj_grad,
        latent_proj_grad,
        latent_gain_grad,
        latent_up_grad,
        out_proj_grad,
        ffn_gain_grad,
        shared_gate_grad,
        shared_up_grad,
        shared_down_grad,
        routed_gate_grad,
        routed_up_grad,
        routed_down_grad,
    )


def solution(mesh):
    placed = (
        P(("fsdp", "tp"), None),
        P(("fsdp", "tp"), None),
        P("fsdp"),
        P("fsdp", None),
        P("fsdp", None),
        P("fsdp"),
        P("fsdp", "tp"),
        P("fsdp", None),
        P("fsdp"),
        P("fsdp", "tp"),
        P("tp", "fsdp"),
        P("fsdp"),
        P("fsdp", "tp"),
        P("fsdp", "tp"),
        P("tp", "fsdp"),
        P("fsdp", "tp", None),
        P("fsdp", "tp", None),
        P("fsdp", "tp", None),
    )
    return jax.shard_map(
        per_device,
        mesh=mesh,
        in_specs=placed,
        out_specs=(
            P(("fsdp", "tp"), None),
            P(("fsdp", "tp"), None),
            P(("fsdp", "tp")),
            P("fsdp", "tp"),
            P(("fsdp", "tp"), None),
            P(("fsdp", "tp")),
            P("fsdp", "tp"),
            P("tp", "fsdp"),
            P(("fsdp", "tp")),
            P("fsdp", "tp"),
            P("fsdp", "tp"),
            P("tp", "fsdp"),
            P("fsdp", "tp", None),
            P("fsdp", "tp", None),
            P("fsdp", "tp", None),
        ),
        check_vma=False,
    )
```

```python
import functools

import jax
import jax.numpy as jnp
from jax import lax
from jax.experimental import pallas as pl
from jax.experimental.pallas import tpu as pltpu
from jax.sharding import PartitionSpec as P

H = 16
NOPE = 128
ROPE = 64
DV = 128
LAT = 512
TOPK = 6
SEQ = 512
HALF = 256
QUARTET = 4
RAW_ROWS = 8


EPSILON = 1e-06
THETA_BASE = 10000.0
MASK_FILL = -1e30
NO_SLOT = -1e6

BF = jnp.bfloat16
F32 = jnp.float32


def rope_tables(positions, width_rope):
    middle = width_rope // 2
    frequency = THETA_BASE ** (-(jnp.arange(middle) * 2).astype(jnp.float32) / width_rope)
    angles = positions.astype(jnp.float32)[:, None] * frequency[None, :]
    return (jnp.cos(angles), jnp.sin(angles))


def rotate(values, cosine, sine_part):
    middle = values.shape[-1] // 2
    first_half = values[..., :middle]
    second_half = values[..., middle:]
    return jnp.concatenate(
        [
            first_half * cosine - second_half * sine_part,
            second_half * cosine + first_half * sine_part,
        ],
        axis=-1,
    )


def unrotate(values, cosine, sine_part):
    middle = values.shape[-1] // 2
    first_half = values[..., :middle]
    second_half = values[..., middle:]
    return jnp.concatenate(
        [
            first_half * cosine + second_half * sine_part,
            second_half * cosine - first_half * sine_part,
        ],
        axis=-1,
    )


def norm_parts(values):
    inverse = lax.rsqrt(jnp.mean(values * values, axis=-1, keepdims=True) + EPSILON)
    return (values * inverse, inverse)


def norm_back(upstream, unit_rows, inverse, scaling):
    scaled = upstream * scaling
    gain_grad = jnp.sum(upstream * unit_rows, axis=0)
    input_grad = inverse * (
        scaled - unit_rows * jnp.mean(scaled * unit_rows, axis=-1, keepdims=True)
    )
    return (gain_grad, input_grad)


def silu_back(grad_hidden, gate_pre, up_pre):
    sigmoid = jax.nn.sigmoid(gate_pre)
    gate_grad = grad_hidden * up_pre * (sigmoid * (1.0 + gate_pre * (1.0 - sigmoid)))
    up_grad = grad_hidden * (gate_pre * sigmoid)
    return (gate_grad.astype(jnp.bfloat16), up_grad.astype(jnp.bfloat16))


def is_power(count):
    return count & (count - 1) == 0


def swap(values, axis_name, bit):
    count = lax.axis_size(axis_name)
    return lax.ppermute(values, axis_name, [(i, i ^ bit) for i in range(count)])


def tie(*values):
    return lax.optimization_barrier(values)


def column_gather(rows):
    return lax.all_gather(rows, "tp", axis=0, tiled=True)


def column_scatter(values):
    return lax.psum_scatter(values.astype(BF), "tp", scatter_dimension=0, tiled=True).astype(F32)


def dot_rows(left, right):
    return lax.dot_general(left, right, (((1,), (1,)), ((), ())), preferred_element_type=F32)


def dot_plain(left, right):
    return lax.dot_general(left, right, (((1,), (0,)), ((), ())), preferred_element_type=F32)


def dot_first(left, right):
    return lax.dot_general(left, right, (((0,), (0,)), ((), ())), preferred_element_type=F32)


def select_rows(slot_rows, experts, cap):
    row = lax.broadcasted_iota(jnp.int32, (experts * cap, HALF), 0).astype(F32)
    hit = row == slot_rows[0:1, :]
    for e in range(1, experts):
        hit = hit | (row == slot_rows[e : e + 1, :] + float(e * cap))
    return hit


def select_cols(slot_cols, experts, cap):
    lane = lax.broadcasted_iota(jnp.int32, (HALF, experts * cap), 1).astype(F32)
    hit = lane == slot_cols[:, 0:1]
    for e in range(1, experts):
        hit = hit | (lane == slot_cols[:, e : e + 1] + float(e * cap))
    return hit


def slot_weights(hit, weight_rows, experts, cap):
    pieces = []
    for e in range(experts):
        part = hit[e * cap : (e + 1) * cap, :]
        pieces.append(
            jnp.sum(jnp.where(part, weight_rows[e : e + 1, :], 0.0), axis=1, keepdims=True)
        )
    return jnp.concatenate(pieces, axis=0)


def expert_front_kernel(step, experts, cap, aliased, *refs):
    count = QUARTET
    x_in = refs[:count]
    where_ref, dy_in, gate_up_in, down_in, slot_row_ref, weight_row_ref, slot_col_ref = refs[
        count : count + 7
    ]
    base = count + 7 + aliased
    dx_out = refs[base : base + 2]
    x_all, d_all, hid_all, dgu_all = refs[base + 2 : base + 6]
    (xb, db, gate_up, down, xs, ds, dxs, dxo, hid, dgu, sem_in, sem_w, sem_out, sem_dx) = refs[
        base + 6 :
    ]
    width = xb.shape[2]
    pad = down.shape[1]
    tile = min(1024, width)
    x_copies = [pltpu.make_async_copy(x_in[q], xb.at[q], sem_in.at[q]) for q in range(count)]
    d_copies = [
        pltpu.make_async_copy(
            dy_in.at[pl.ds(pl.multiple_of(where_ref[q] * HALF, HALF), HALF)],
            db.at[q],
            sem_in.at[count + q],
        )
        for q in range(count)
    ]
    w_copies = [
        pltpu.make_async_copy(gate_up_in, gate_up, sem_w.at[0]),
        pltpu.make_async_copy(down_in, down, sem_w.at[1]),
    ]
    for q in range(count):
        x_copies[q].start()
        d_copies[q].start()
    for copy in w_copies:
        copy.start()
    for q in range(count):
        x_copies[q].wait()
        d_copies[q].wait()

        hit = select_rows(slot_row_ref[q], experts, cap)
        weights = slot_weights(hit, weight_row_ref[q], experts, cap)
        choose = jnp.where(hit, 1.0, 0.0).astype(BF)

        def spread(n, carry, q=q, choose=choose, weights=weights):
            cols = pl.ds(pl.multiple_of(n * tile, tile), tile)
            rows = dot_plain(choose, xb[q, :, cols])
            grads = dot_plain(choose, db[q, :, cols]) * weights
            for e in range(experts):
                xs[e, q * cap : (q + 1) * cap, cols] = rows[e * cap : (e + 1) * cap].astype(BF)
                ds[e, q * cap : (q + 1) * cap, cols] = grads[e * cap : (e + 1) * cap].astype(BF)
            return carry

        lax.fori_loop(0, width // tile, spread, 0)
    out_copies = [
        pltpu.make_async_copy(xs, x_all.at[step], sem_out.at[0]),
        pltpu.make_async_copy(ds, d_all.at[step], sem_out.at[1]),
        pltpu.make_async_copy(hid, hid_all.at[step], sem_out.at[2]),
        pltpu.make_async_copy(dgu, dgu_all.at[step], sem_out.at[3]),
    ]
    out_copies[0].start()
    out_copies[1].start()
    for copy in w_copies:
        copy.wait()

    def one_expert(e, carry):
        both = dot_rows(xs[e], gate_up[e])
        gate_pre, up_pre = both[:, :pad], both[:, pad:]
        d_hidden = dot_rows(ds[e], down[e])
        sigmoid = jax.nn.sigmoid(gate_pre)
        silu = gate_pre * sigmoid
        hid[e] = (silu * up_pre).astype(BF)
        gate_grad = d_hidden * up_pre * (sigmoid * (1.0 + gate_pre * (1.0 - sigmoid)))
        grads = jnp.concatenate([gate_grad, d_hidden * silu], axis=1).astype(BF)
        dgu[e] = grads

        def back(n, inner):
            cols = pl.ds(pl.multiple_of(n * tile, tile), tile)
            part = dot_plain(dgu[e], gate_up[e, :, cols]).astype(BF)
            for q in range(count):
                dxs[q, pl.ds(pl.multiple_of(e * cap, cap), cap), cols] = part[
                    q * cap : (q + 1) * cap
                ]
            return inner

        lax.fori_loop(0, width // tile, back, 0)
        return carry

    lax.fori_loop(0, experts, one_expert, 0)
    out_copies[2].start()
    out_copies[3].start()
    dx_copies = [
        pltpu.make_async_copy(dxo.at[q], dx_out[q // 2].at[q % 2], sem_dx.at[q])
        for q in range(count)
    ]
    for q in range(count):
        choose = jnp.where(select_cols(slot_col_ref[q], experts, cap), 1.0, 0.0).astype(BF)

        def gather(n, carry, q=q, choose=choose):
            cols = pl.ds(pl.multiple_of(n * tile, tile), tile)
            dxo[q, :, cols] = dot_plain(choose, dxs[q, :, cols]).astype(BF)
            return carry

        lax.fori_loop(0, width // tile, gather, 0)
        dx_copies[q].start()
    for copy in out_copies:
        copy.wait()
    for copy in dx_copies:
        copy.wait()


def expert_front(step, steps, x_parts, where, dy_all, gate_up, down, tables, kept, cap):
    experts, wide, width = gate_up.shape
    pad = wide // 2
    slots = QUARTET * cap
    slot_row, weight_row, slot_col = (t[step] for t in tables)
    any_spec = pl.BlockSpec(memory_space=pl.ANY)
    vmem_spec = pl.BlockSpec(memory_space=pltpu.VMEM)
    pair_shape = jax.ShapeDtypeStruct((2, HALF, width), BF)
    kept_shapes = [
        jax.ShapeDtypeStruct((steps, experts, slots, columns), BF)
        for columns in (width, width, pad, wide)
    ]
    results = pl.pallas_call(
        functools.partial(expert_front_kernel, step, experts, cap, len(kept)),
        out_shape=[pair_shape] * 2 + kept_shapes,
        in_specs=[any_spec] * QUARTET
        + [pl.BlockSpec(memory_space=pltpu.SMEM)]
        + [any_spec] * 3
        + [vmem_spec] * 3
        + [any_spec] * len(kept),
        out_specs=[any_spec] * 6,
        input_output_aliases={QUARTET + 7 + i: 2 + i for i in range(len(kept))},
        scratch_shapes=[
            pltpu.VMEM((QUARTET, HALF, width), BF),
            pltpu.VMEM((QUARTET, HALF, width), BF),
            pltpu.VMEM((experts, wide, width), BF),
            pltpu.VMEM((experts, pad, width), BF),
            pltpu.VMEM((experts, slots, width), BF),
            pltpu.VMEM((experts, slots, width), BF),
            pltpu.VMEM((QUARTET, experts * cap, width), BF),
            pltpu.VMEM((QUARTET, HALF, width), BF),
            pltpu.VMEM((experts, slots, pad), BF),
            pltpu.VMEM((experts, slots, wide), BF),
            pltpu.SemaphoreType.DMA((2 * QUARTET,)),
            pltpu.SemaphoreType.DMA((2,)),
            pltpu.SemaphoreType.DMA((4,)),
            pltpu.SemaphoreType.DMA((QUARTET,)),
        ],
        compiler_params=pltpu.CompilerParams(vmem_limit_bytes=62 * 1024 * 1024),
        cost_estimate=pl.CostEstimate(
            flops=2 * slots * experts * width * pad * 5
            + 6 * QUARTET * HALF * experts * cap * width,
            bytes_accessed=2 * width * (3 * QUARTET * HALF + experts * 3 * pad + 2 * experts * slots),
            transcendentals=slots * experts * pad,
        ),
        name="expert_front",
    )(*x_parts, where, dy_all, gate_up, down, slot_row, weight_row, slot_col, *kept)
    return list(results[:2]), list(results[2:])


def expert_out_kernel(experts, cap, hid, down, slot_row, weight_row, slot_col, near, far, parts):
    width = down.shape[2]
    tile = min(1024, width)
    weights = [
        slot_weights(
            select_rows(slot_row[0, q], experts, cap), weight_row[0, q], experts, cap
        )
        for q in range(QUARTET)
    ]
    for e in range(experts):

        def front(n, carry, e=e):
            cols = pl.ds(pl.multiple_of(n * tile, tile), tile)
            rows = dot_plain(hid[0, e], down[e, :, cols])
            for q in range(QUARTET):
                parts[q, e * cap : (e + 1) * cap, cols] = (
                    rows[q * cap : (q + 1) * cap] * weights[q][e * cap : (e + 1) * cap]
                ).astype(BF)
            return carry

        lax.fori_loop(0, width // tile, front, 0)
    for q in range(QUARTET):
        choose = jnp.where(select_cols(slot_col[0, q], experts, cap), 1.0, 0.0).astype(BF)
        out = (near, far)[q // 2]

        def gather(n, carry, q=q, choose=choose, out=out):
            cols = pl.ds(pl.multiple_of(n * tile, tile), tile)
            out[0, q % 2, :, cols] = dot_plain(choose, parts[q, :, cols]).astype(BF)
            return carry

        lax.fori_loop(0, width // tile, gather, 0)


def expert_out(hid_all, down, tables, cap):
    steps, experts, slots, pad = hid_all.shape
    width = down.shape[2]
    slot_row, weight_row, slot_col = tables
    return pl.pallas_call(
        functools.partial(expert_out_kernel, experts, cap),
        grid=(steps,),
        out_shape=[jax.ShapeDtypeStruct((steps, 2, HALF, width), BF)] * 2,
        in_specs=[
            pl.BlockSpec((1, experts, slots, pad), lambda i: (i, 0, 0, 0)),
            pl.BlockSpec((experts, pad, width), lambda i: (0, 0, 0)),
            pl.BlockSpec((1,) + slot_row.shape[1:], lambda i: (i, 0, 0, 0)),
            pl.BlockSpec((1,) + weight_row.shape[1:], lambda i: (i, 0, 0, 0)),
            pl.BlockSpec((1,) + slot_col.shape[1:], lambda i: (i, 0, 0, 0)),
        ],
        out_specs=[pl.BlockSpec((1, 2, HALF, width), lambda i: (i, 0, 0, 0))] * 2,
        scratch_shapes=[pltpu.VMEM((QUARTET, experts * cap, width), BF)],
        compiler_params=pltpu.CompilerParams(vmem_limit_bytes=48 * 1024 * 1024),
        cost_estimate=pl.CostEstimate(
            flops=steps * (2 * slots * experts * width * pad + 2 * QUARTET * HALF * experts * cap * width),
            bytes_accessed=2 * steps * QUARTET * HALF * width + 2 * hid_all.size + 2 * down.size,
            transcendentals=0,
        ),
        name="expert_out",
    )(hid_all, down, slot_row, weight_row, slot_col)


def expert_grads_kernel(dgu, x, hid, d, gate_grad, up_grad, down_grad):
    local = gate_grad.shape[1]
    pad = hid.shape[3]
    width = x.shape[3]
    tile = min(1024, width)

    @pl.when(pl.program_id(1) == 0)
    def _():
        gate_grad[...] = jnp.zeros_like(gate_grad)
        up_grad[...] = jnp.zeros_like(up_grad)
        down_grad[...] = jnp.zeros_like(down_grad)

    def part(n, carry):
        cols = pl.ds(pl.multiple_of(n * tile, tile), tile)
        gate_grad[0, :, cols] += dot_first(dgu[0, 0, :, :pad], x[0, 0, :, cols])[:local]
        up_grad[0, :, cols] += dot_first(dgu[0, 0, :, pad:], x[0, 0, :, cols])[:local]
        down_grad[0, :, cols] += dot_first(hid[0, 0], d[0, 0, :, cols])[:local]
        return carry

    lax.fori_loop(0, width // tile, part, 0)


def expert_grads(kept, local):
    x_all, d_all, hid_all, dgu_all = kept
    steps, experts, slots, width = x_all.shape
    pad = hid_all.shape[3]

    def block(array):
        return pl.BlockSpec((1, 1) + array.shape[2:], lambda e, i: (i, e, 0, 0))

    grad = jax.ShapeDtypeStruct((experts, local, width), F32)
    return pl.pallas_call(
        expert_grads_kernel,
        grid=(experts, steps),
        out_shape=[grad] * 3,
        in_specs=[block(dgu_all), block(x_all), block(hid_all), block(d_all)],
        out_specs=[pl.BlockSpec((1, local, width), lambda e, i: (e, 0, 0))] * 3,
        compiler_params=pltpu.CompilerParams(vmem_limit_bytes=48 * 1024 * 1024),
        cost_estimate=pl.CostEstimate(
            flops=2 * 3 * steps * experts * slots * width * pad,
            bytes_accessed=2 * (x_all.size + d_all.size + hid_all.size + dgu_all.size)
            + 12 * experts * local * width,
            transcendentals=0,
        ),
        name="expert_grads",
    )(dgu_all, x_all, hid_all, d_all)


def mesh_copy(src, dst, sends, arrivals, number, device):
    return pltpu.make_async_remote_copy(
        src_ref=src,
        dst_ref=dst,
        send_sem=sends.at[number],
        recv_sem=arrivals.at[number],
        device_id=device,
        device_id_type=pl.DeviceIdType.MESH,
    )


def plane_neighbours():
    place, column = lax.axis_index("fsdp"), lax.axis_index("tp")
    core, along, across = place % 2, (place // 2) % 2, place // 4
    return (
        (place + 1 - 2 * core, column),
        (place + 2 - 4 * along, column),
        (place + 4 - 8 * across, column),
    )


def column_neighbours(count):
    place, column = lax.axis_index("fsdp"), lax.axis_index("tp")
    return [(place, (column + s) % count) for s in range(1, count)]


def greet(devices):
    barrier = pltpu.get_barrier_semaphore()
    for device in devices:
        pl.semaphore_signal(
            barrier, inc=1, device_id=device, device_id_type=pl.DeviceIdType.MESH
        )
    pl.semaphore_wait(barrier, len(devices))


class ColumnGather:
    def __init__(self, blocks, rows_of, sends, arrivals, base):
        self.blocks, self.rows_of = blocks, rows_of
        self.sends, self.arrivals, self.base = sends, arrivals, base
        self.row = lax.axis_index("tp")
        self.column = column_neighbours(4)

    def direct(self, s):
        place = self.blocks.at[self.rows_of(0)]
        return mesh_copy(
            place, place, self.sends, self.arrivals, self.base + s - 1, self.column[s - 1]
        )

    def start(self):
        @pl.when(self.row < 3)
        def _():
            self.direct(1).start()

        @pl.when(self.row > 0)
        def _():
            self.direct(3).start()

        self.direct(2).start()

    def wait(self, b):
        self.direct(4 - b).wait_recv()
        if b == 2:

            @pl.when(self.row == 1)
            def _():
                self.relay(3).start()

            @pl.when(self.row == 2)
            def _():
                self.relay(1).start()

    def relay(self, s):
        place = self.blocks.at[self.rows_of(2)]
        return pltpu.make_async_remote_copy(
            src_ref=place,
            dst_ref=place,
            send_sem=self.sends.at[self.base + 3],
            recv_sem=self.arrivals.at[self.base + 3 - s],
            device_id=self.column[s - 1],
            device_id_type=pl.DeviceIdType.MESH,
        )

    def drain(self):
        @pl.when(self.row < 3)
        def _():
            self.direct(1).wait_send()

        @pl.when(self.row > 0)
        def _():
            self.direct(3).wait_send()

        self.direct(2).wait_send()

        @pl.when(self.row == 1)
        def _():
            self.relay(3).wait_send()

        @pl.when(self.row == 2)
        def _():
            self.relay(1).wait_send()


class ColumnSum:
    def __init__(self, parts, rows_of, landed, relayed, sends, arrivals, base):
        self.parts, self.rows_of, self.landed, self.relayed = parts, rows_of, landed, relayed
        self.sends, self.arrivals, self.base = sends, arrivals, base
        self.row = lax.axis_index("tp")
        self.column = column_neighbours(4)

    def direct(self, s):
        return mesh_copy(
            self.parts.at[self.rows_of(s)],
            self.landed.at[s - 1],
            self.sends,
            self.arrivals,
            self.base + s - 1,
            self.column[s - 1],
        )

    def first_leg(self, s):
        return mesh_copy(
            self.parts.at[self.rows_of(4 - s)],
            self.relayed.at[0],
            self.sends,
            self.arrivals,
            self.base + 3,
            self.column[s - 1],
        )

    def own_part(self, local):
        return pltpu.make_async_copy(self.parts.at[self.rows_of(2)], self.relayed.at[1], local)

    def second_leg(self):
        return mesh_copy(
            self.relayed.at[1],
            self.landed.at[1],
            self.sends,
            self.arrivals,
            self.base + 1,
            self.column[1],
        )

    def start(self, local):
        @pl.when(self.row == 0)
        def _():
            self.first_leg(1).start()

        @pl.when(self.row == 3)
        def _():
            self.first_leg(3).start()

        @pl.when((self.row == 1) | (self.row == 2))
        def _():
            self.own_part(local).start()

        @pl.when(self.row < 3)
        def _():
            self.direct(1).start()

        @pl.when(self.row > 0)
        def _():
            self.direct(3).start()

        @pl.when((self.row == 0) | (self.row == 3))
        def _():
            self.direct(2).start()

    def middle(self, local):
        @pl.when((self.row == 1) | (self.row == 2))
        def _():
            self.own_part(local).wait()
            self.first_leg(1).wait_recv()

            def some(i, carry):
                rows = pl.ds(pl.multiple_of(i * 32, 32), 32)
                self.relayed[1, rows, :] = (
                    self.relayed[0, rows, :].astype(F32) + self.relayed[1, rows, :].astype(F32)
                ).astype(BF)
                return carry

            lax.fori_loop(0, self.relayed.shape[1] // 32, some, 0)
            self.second_leg().start()

    def clear(self):
        @pl.when(self.row == 0)
        def _():
            self.landed[0] = jnp.zeros(self.landed.shape[1:], BF)

        @pl.when(self.row == 3)
        def _():
            self.landed[2] = jnp.zeros(self.landed.shape[1:], BF)

    def total(self, own):
        @pl.when(self.row > 0)
        def _():
            self.direct(1).wait_recv()

        @pl.when(self.row < 3)
        def _():
            self.direct(3).wait_recv()

        self.direct(2).wait_recv()
        total = own.astype(F32)
        for s in range(3):
            total = total + self.landed[s].astype(F32)
        return total

    def drain(self):
        @pl.when(self.row == 0)
        def _():
            self.first_leg(1).wait_send()

        @pl.when(self.row == 3)
        def _():
            self.first_leg(3).wait_send()

        @pl.when(self.row < 3)
        def _():
            self.direct(1).wait_send()

        @pl.when(self.row > 0)
        def _():
            self.direct(3).wait_send()

        self.direct(2).wait_send()


class PlaneGather:
    def __init__(self, own, others, rows_of, sends, arrivals, base):
        self.own, self.others, self.rows_of = own, others, rows_of
        self.sends, self.arrivals, self.base = sends, arrivals, base
        self.partner, self.along, self.across = plane_neighbours()

    def copies(self, b):
        half = self.own.shape[1] // 2
        rows = self.rows_of(b)
        left, right = pl.ds(0, half), pl.ds(half, half)
        other = {r: self.others.at[r - 1] for r in range(1, 8)}
        plan = [
            (self.own.at[rows], other[2].at[rows], self.along),
            (self.own.at[rows], other[4].at[rows], self.across),
            (self.own.at[rows], other[1].at[rows], self.partner),
            (other[2].at[rows, left], other[6].at[rows, left], self.across),
            (other[4].at[rows, right], other[6].at[rows, right], self.along),
            (other[2].at[rows], other[3].at[rows], self.partner),
            (other[4].at[rows], other[5].at[rows], self.partner),
            (other[6].at[rows], other[7].at[rows], self.partner),
        ]
        return [
            mesh_copy(src, dst, self.sends, self.arrivals, self.base + 8 * b + i, device)
            for i, (src, dst, device) in enumerate(plan)
        ]

    def start(self, b):
        for copy in self.copies(b)[:3]:
            copy.start()

    def forward(self, b):
        along, across, _, left, right, third, fifth, _ = self.copies(b)
        along.wait_recv()
        left.start()
        third.start()
        across.wait_recv()
        right.start()
        fifth.start()

    def last(self, b):
        copies = self.copies(b)
        copies[3].wait_recv()
        copies[4].wait_recv()
        copies[7].start()

    def arrived(self, b, numbers):
        copies = self.copies(b)
        for i in numbers:
            copies[i].wait_recv()

    def drain(self, b):
        for copy in self.copies(b):
            copy.wait_send()


def block_rows(columns, size):
    row = lax.axis_index("tp")
    return lambda s: pl.ds(pl.multiple_of((row + s) % columns * size, size), size)


def slots_of(table, experts, columns, size, b, q):
    place = pl.ds(pl.multiple_of((lax.axis_index("tp") + b) % columns * size, size), size)
    rows = []
    for e in range(experts):
        low, high = 2 * q * experts + e, (2 * q + 1) * experts + e
        rows.append(
            jnp.concatenate([table[low : low + 1, place], table[high : high + 1, place]], axis=1)
        )
    return jnp.concatenate(rows, axis=0)


def token_sums(table, experts, columns, size, wide, b, slots, keep):
    width = slots.shape[2]
    tile = min(1024, width)
    for q in range(QUARTET):
        entries = slots_of(table, experts, columns, size, b, q)
        entries = jnp.concatenate(
            [entries, jnp.full((8 - experts, HALF), NO_SLOT, F32)], axis=0
        )
        choose = jnp.where(select_cols(entries.T, experts, wide), 1.0, 0.0).astype(BF)

        def gather(n, carry, q=q, choose=choose):
            cols = pl.ds(pl.multiple_of(n * tile, tile), tile)
            keep(q, cols, dot_plain(choose, slots[q, :, cols]).astype(BF))
            return carry

        lax.fori_loop(0, width // tile, gather, 0)


def plane_place(r):
    place = lax.axis_index("fsdp")
    core, along, across = place % 2, (place // 2) % 2, place // 4
    return (across + r // 4) % 2 * 4 + (along + r // 2 % 2) % 2 * 2 + (core + r % 2) % 2


def expert_kernel(cap, columns, size, *refs):
    (
        attn_in,
        tokens_in,
        cotan_in,
        cotan_left,
        gate_in,
        up_in,
        down_in,
        gain_ref,
        raw_ref,
        mixed_out,
        ffn_all,
        dx_out,
        slots_out,
        weights_out,
        x_all,
        d_all,
        hid_all,
        dgu_all,
        x_others,
        dy_others,
        theirs,
        links,
        attn_v,
        tokens_v,
        arrived_v,
        relayed_v,
        mixed_v,
        ffn_v,
        xb,
        db,
        gate_up,
        down,
        xs,
        ds,
        dxs,
        others,
        chip,
        stage,
        hid,
        dgu,
        slot_table,
        weight_table,
        sends,
        arrivals,
        local,
        loads,
        sum_local,
        spill,
    ) = refs
    count = QUARTET
    previous = {2: 0, 1: 2, 3: 1}
    experts, local_hidden = gate_in.shape[:2]
    width = xb.shape[2]
    pad = down.shape[1]
    tile = min(1024, width)
    wide = 2 * cap
    rows_of = block_rows(columns, size)
    partner, along, across = plane_neighbours()
    column = column_neighbours(columns)
    number = 0

    def reserve(amount):
        nonlocal number
        number += amount
        return number - amount

    x_gather = PlaneGather(ffn_all, x_others, rows_of, sends, arrivals, reserve(8 * columns))
    dy_gather = PlaneGather(cotan_in, dy_others, rows_of, sends, arrivals, reserve(8 * columns))
    gather = ColumnGather(ffn_all, rows_of, sends, arrivals, reserve(4))
    summed = ColumnSum(attn_in, rows_of, arrived_v, relayed_v, sends, arrivals, reserve(4))
    plane = PlaneSum(
        lambda r, h: others.at[r // 2],
        chip,
        theirs,
        links,
        stage,
        sends,
        arrivals,
        reserve(plane_sum_sizes(columns)[0]),
        sum_local,
    )

    greet([partner, along, across] + column)
    summed.start(local.at[2])
    first = [
        pltpu.make_async_copy(attn_in.at[rows_of(0)], attn_v, local.at[0]),
        pltpu.make_async_copy(tokens_in, tokens_v, local.at[1]),
    ]
    for copy in first:
        copy.start()
    order = (0, 2, 1, 3)
    for b in order:
        dy_gather.start(b)
    if pad > local_hidden:
        rest = pad - local_hidden
        for e in range(experts):
            for ref, start in ((gate_up, local_hidden), (gate_up, pad + local_hidden), (down, local_hidden)):
                ref[e, start : start + rest, :] = jnp.zeros((rest, width), BF)
    weights_in = []
    for e in range(experts):
        weights_in += [
            pltpu.make_async_copy(
                gate_in.at[e], gate_up.at[e, pl.ds(0, local_hidden)], local.at[3 + 3 * e]
            ),
            pltpu.make_async_copy(
                up_in.at[e], gate_up.at[e, pl.ds(pad, local_hidden)], local.at[4 + 3 * e]
            ),
            pltpu.make_async_copy(
                down_in.at[e], down.at[e, pl.ds(0, local_hidden)], local.at[5 + 3 * e]
            ),
        ]
    for copy in weights_in:
        copy.start()

    summed.clear()
    summed.middle(local.at[2])

    earlier = lax.broadcasted_iota(jnp.int32, (size, size), 0)
    later = lax.broadcasted_iota(jnp.int32, (size, size), 1)
    before = jnp.where(earlier < later, 1.0, 0.0).astype(BF)
    own_first = (lax.axis_index("fsdp") * experts).astype(F32)
    for r in range(8):
        for e in range(experts):
            member = jnp.zeros((1, SEQ), F32)
            weight = jnp.zeros((1, SEQ), F32)
            for pick in range(TOPK):
                same = raw_ref[r, pick : pick + 1, :] == own_first + float(e)
                member = jnp.where(same, 1.0, member)
                weight = weight + jnp.where(
                    same, raw_ref[r, RAW_ROWS + pick : RAW_ROWS + pick + 1, :], 0.0
                )
            slot_table[r * experts + e : r * experts + e + 1, :] = member
            weight_table[r * experts + e : r * experts + e + 1, :] = weight
    second = lax.broadcasted_iota(jnp.int32, (8 * experts, size), 0) // experts % 2
    shift = second.astype(F32) * float(cap)
    for b in range(columns):
        cols = pl.ds(b * size, size)
        member = slot_table[:, cols]
        rank = dot_plain(member.astype(BF), before)
        slot_table[:, cols] = jnp.where(member > 0.5, rank + shift, NO_SLOT)
    slots_out[...] = slot_table[...]
    weights_out[...] = weight_table[...]

    for copy in first:
        copy.wait()
    total = summed.total(attn_v[...]) + tokens_v[...].astype(F32)
    mixed_v[...] = total
    inverse = lax.rsqrt(jnp.mean(total * total, axis=1, keepdims=True) + EPSILON)
    ffn_v[...] = (total * inverse * gain_ref[...]).astype(BF)
    own_copy = pltpu.make_async_copy(ffn_v, ffn_all.at[rows_of(0)], local.at[0])
    own_copy.start()
    mixed_copy = pltpu.make_async_copy(mixed_v, mixed_out, local.at[1])
    mixed_copy.start()
    own_copy.wait()

    gather.start()

    def enter(b):
        if b > 0:
            gather.wait(b)
        x_gather.start(b)

    def ready(b):
        x_gather.last(b)
        dy_gather.last(b)
        x_gather.arrived(b, [2, 5, 6, 7])
        dy_gather.arrived(b, [2, 5, 6, 7])

    def source(own, gathered, r):
        return own if r == 0 else gathered.at[r - 1]

    half = width // 2
    left, right = pl.ds(0, half), pl.ds(half, half)

    def load(b, k):
        copies = []
        for r in range(8):
            place = pl.ds(r % 2 * size, size)
            if k == 0:
                plan = [(source(ffn_all, x_others, r).at[rows_of(b)], xb.at[r // 2, place])]
            else:
                start = plane_place(r) * SEQ + (lax.axis_index("tp") + b) % columns * size
                plan = [
                    (source(cotan_in, dy_others, r).at[rows_of(b)], db.at[r // 2, place, right]),
                    (
                        cotan_left.at[pl.ds(pl.multiple_of(start, size), size)],
                        db.at[r // 2, place, left],
                    ),
                ]
            for n, (src, dst) in enumerate(plan):
                copies.append(pltpu.make_async_copy(src, dst, loads.at[8 * (k + n) + r]))
        return copies

    def combine(b, keep):
        token_sums(slot_table, experts, columns, size, wide, b, dxs, keep)

    def spills(b):
        return [
            pltpu.make_async_copy(xs, x_all.at[b], spill.at[0]),
            pltpu.make_async_copy(ds, d_all.at[b], spill.at[1]),
            pltpu.make_async_copy(hid.at[b], hid_all.at[b], spill.at[2]),
            pltpu.make_async_copy(dgu, dgu_all.at[b], spill.at[3]),
        ]

    def front(b):
        x_load, dy_load = load(b, 0), load(b, 1)
        for copy in x_load + dy_load:
            copy.start()
        if b == 0:
            for copy in weights_in:
                copy.wait()
        if b > 0:
            for copy in spills(previous[b]):
                copy.wait()
        for q in range(count):
            for copy in x_load[2 * q : 2 * q + 2] + dy_load[4 * q : 4 * q + 4]:
                copy.wait()
            hit = select_rows(slots_of(slot_table, experts, columns, size, b, q), experts, wide)
            weights = slot_weights(hit, slots_of(weight_table, experts, columns, size, b, q), experts, wide)
            choose = jnp.where(hit, 1.0, 0.0).astype(BF)

            def spread(n, carry, q=q, choose=choose, weights=weights):
                cols = pl.ds(pl.multiple_of(n * tile, tile), tile)
                rows = dot_plain(choose, xb[q, :, cols])
                grads = dot_plain(choose, db[q, :, cols]) * weights
                for e in range(experts):
                    low, high = e * wide, (e + 1) * wide
                    xs[e, q * wide : (q + 1) * wide, cols] = rows[low:high].astype(BF)
                    ds[e, q * wide : (q + 1) * wide, cols] = grads[low:high].astype(BF)
                return carry

            lax.fori_loop(0, width // tile, spread, 0)
        out_copies = spills(b)
        out_copies[0].start()
        out_copies[1].start()

        def one_expert(e, carry):
            both = dot_rows(xs[e], gate_up[e])
            gate_pre, up_pre = both[:, :pad], both[:, pad:]
            d_hidden = dot_rows(ds[e], down[e])
            sigmoid = jax.nn.sigmoid(gate_pre)
            silu = gate_pre * sigmoid
            hid[b, e] = (silu * up_pre).astype(BF)
            gate_grad = d_hidden * up_pre * (sigmoid * (1.0 + gate_pre * (1.0 - sigmoid)))
            dgu[e] = jnp.concatenate([gate_grad, d_hidden * silu], axis=1).astype(BF)

            def back(n, inner):
                cols = pl.ds(pl.multiple_of(n * tile, tile), tile)
                part = dot_plain(dgu[e], gate_up[e, :, cols]).astype(BF)
                for q in range(count):
                    dxs[q, pl.ds(pl.multiple_of(e * wide, wide), wide), cols] = part[
                        q * wide : (q + 1) * wide
                    ]
                return inner

            lax.fori_loop(0, width // tile, back, 0)
            return carry

        lax.fori_loop(0, experts, one_expert, 0)
        out_copies[2].start()
        out_copies[3].start()
        if b > 0:
            for i in range(4):
                plane.pair(i, previous[b]).wait_send()

        def keep(q, cols, value):
            chip[q, b, :, cols] = value[:size]
            others[q, :, cols] = value[size:]

        combine(b, keep)
        for i in range(4):
            plane.pair(i, b).start()

    dy_gather.forward(0)
    enter(0)
    x_gather.forward(0)
    dy_gather.forward(2)
    enter(2)
    dy_gather.forward(1)
    enter(1)
    x_gather.forward(2)
    ready(0)
    front(0)
    dy_gather.forward(3)
    enter(3)
    x_gather.forward(1)
    ready(2)
    front(2)
    x_gather.forward(3)
    plane.send_first([0], False)
    ready(1)
    front(1)
    plane.send_first([2], False)
    plane.send_second([0])
    ready(3)
    front(3)
    plane.send_first([1], False)
    plane.send_second([2])
    done = {}

    def close(b):
        plane.finish([b])
        done[b] = pltpu.make_async_copy(chip.at[0, b], dx_out.at[rows_of(b)], loads.at[b])
        done[b].start()

    plane.send_first([3], False)
    close(0)
    plane.send_second([1])
    close(2)
    plane.send_second([3])
    close(1)
    close(3)
    for copy in spills(3):
        copy.wait()
    for b in range(columns):
        done[b].wait()
    mixed_copy.wait()

    for b in range(columns):
        x_gather.drain(b)
        dy_gather.drain(b)
    gather.drain()
    summed.drain()
    plane.drain(3)


def expert_call(attn_part, tokens, cotan_right, cotan_left, gate, up, down, gain, raw, cap):
    columns = lax.axis_size("tp")
    size, width = tokens.shape
    experts, local_hidden, _ = gate.shape
    pad = -(-local_hidden // 128) * 128
    slots = 8 * cap
    anywhere = pl.BlockSpec(memory_space=pl.ANY)
    held = pl.BlockSpec(memory_space=pltpu.VMEM)

    def array(*dims, kind=BF):
        return jax.ShapeDtypeStruct(dims, kind)

    landing, scratch = plane_sum_space(columns, size, width)
    remote, near = plane_sum_sizes(columns)
    remote = remote + 16 * columns + 8
    results = pl.pallas_call(
        functools.partial(expert_kernel, cap, columns, size),
        out_shape=[
            array(size, width, kind=F32),
            array(SEQ, width),
            array(SEQ, width),
            array(8 * experts, SEQ, kind=F32),
            array(8 * experts, SEQ, kind=F32),
            array(columns, experts, slots, width),
            array(columns, experts, slots, width),
            array(columns, experts, slots, pad),
            array(columns, experts, slots, 2 * pad),
            array(7, SEQ, width),
            array(7, SEQ, width // 2),
        ]
        + landing,
        in_specs=[anywhere] * 7 + [held] * 2,
        out_specs=[anywhere] * 3 + [held] * 2 + [anywhere] * 8,
        scratch_shapes=[
            pltpu.VMEM((size, width), BF),
            pltpu.VMEM((size, width), BF),
            pltpu.VMEM((columns - 1, size, width), BF),
            pltpu.VMEM((2, size, width), BF),
            pltpu.VMEM((size, width), F32),
            pltpu.VMEM((size, width), BF),
            pltpu.VMEM((QUARTET, HALF, width), BF),
            pltpu.VMEM((QUARTET, HALF, width), BF),
            pltpu.VMEM((experts, 2 * pad, width), BF),
            pltpu.VMEM((experts, pad, width), BF),
            pltpu.VMEM((experts, slots, width), BF),
            pltpu.VMEM((experts, slots, width), BF),
            pltpu.VMEM((QUARTET, 2 * experts * cap, width), BF),
            pltpu.VMEM((4, size, width), BF),
        ]
        + scratch
        + [
            pltpu.VMEM((columns, experts, slots, pad), BF),
            pltpu.VMEM((experts, slots, 2 * pad), BF),
            pltpu.VMEM((8 * experts, SEQ), F32),
            pltpu.VMEM((8 * experts, SEQ), F32),
            pltpu.SemaphoreType.DMA((remote,)),
            pltpu.SemaphoreType.DMA((remote,)),
            pltpu.SemaphoreType.DMA((3 + 3 * experts,)),
            pltpu.SemaphoreType.DMA((24,)),
            pltpu.SemaphoreType.DMA((near,)),
            pltpu.SemaphoreType.DMA((4,)),
        ],
        compiler_params=pltpu.CompilerParams(
            collective_id=1, has_side_effects=True, vmem_limit_bytes=67_043_328
        ),
        cost_estimate=pl.CostEstimate(
            flops=16 * SEQ * experts * cap * width * 8,
            bytes_accessed=800 * SEQ * width,
            transcendentals=0,
        ),
        name="experts",
    )(attn_part, tokens, cotan_right, cotan_left, gate, up, down, gain, raw)
    return results[:9]


def first_kernel(columns, size, kinds, *refs):
    amount = len(kinds)
    rows_in, own_in = refs[:2], refs[2 : 2 + amount]
    rows_all, alls = refs[2 + amount : 4 + amount], refs[4 + amount : 4 + 2 * amount]
    rows_v, held = refs[4 + 2 * amount : 6 + 2 * amount], refs[6 + 2 * amount : 6 + 3 * amount]
    sends, arrivals, local = refs[6 + 3 * amount :]
    partner, along, across = plane_neighbours()
    column = column_neighbours(columns)
    rows_of = block_rows(columns, size)
    place = lax.axis_index("fsdp")
    devices = {
        0: place,
        1: partner[0],
        2: along[0],
        4: across[0],
        6: along[0] + across[0] - place,
    }
    greet([partner, along, across] + column)
    gathers = []
    for n in range(2):
        inward = pltpu.make_async_copy(rows_in[n], rows_v[n], local.at[n])
        inward.start()
        inward.wait()
        place_here = rows_all[n].at[rows_of(0)]
        outward = pltpu.make_async_copy(rows_v[n], place_here, local.at[n])
        outward.start()
        outward.wait()
        gathers.append(ColumnGather(rows_all[n], rows_of, sends, arrivals, 8 * amount + 4 * n))
        gathers[n].start()
    plans = []
    for k, kind in enumerate(kinds):
        own, everything = own_in[k], alls[k]
        rows, cols = own.shape
        top, bottom = pl.ds(0, rows // 2), pl.ds(rows // 2, rows // 2)
        whole = pl.ds(0, rows)

        def spot(r, hop, part, kind=kind, everything=everything, cols=cols):
            if kind == "relative":
                return everything.at[r ^ hop, part]
            if kind == "rows":
                return everything.at[devices[r], part]
            start = pl.multiple_of(devices[r] * cols, cols)
            return everything.at[part, pl.ds(start, cols)]

        plan = [
            (own, spot(0, 2, whole), along),
            (own, spot(0, 4, whole), across),
            (own, spot(0, 1, whole), partner),
            (spot(2, 0, top), spot(2, 4, top), across),
            (spot(4, 0, bottom), spot(4, 2, bottom), along),
            (spot(2, 0, whole), spot(2, 1, whole), partner),
            (spot(4, 0, whole), spot(4, 1, whole), partner),
            (spot(6, 0, whole), spot(6, 1, whole), partner),
        ]
        plans.append(
            [
                mesh_copy(src, dst, sends, arrivals, 8 * k + i, device)
                for i, (src, dst, device) in enumerate(plan)
            ]
        )
    for copies in plans:
        for copy in copies[:3]:
            copy.start()
    here, there = [], []
    for k, kind in enumerate(kinds):
        rows, cols = own_in[k].shape
        if kind == "relative":
            spot_here = alls[k].at[0]
        elif kind == "rows":
            spot_here = alls[k].at[place]
        else:
            spot_here = alls[k].at[:, pl.ds(pl.multiple_of(place * cols, cols), cols)]
        here.append(pltpu.make_async_copy(own_in[k], held[k], local.at[2 + k]))
        there.append(pltpu.make_async_copy(held[k], spot_here, local.at[2 + k]))
    for copy in here:
        copy.start()
    for copy in here:
        copy.wait()
    for copy in there:
        copy.start()
    for copies in plans:
        copies[0].wait_recv()
        copies[3].start()
        copies[5].start()
        copies[1].wait_recv()
        copies[4].start()
        copies[6].start()
    gathers[0].wait(2)
    for copies in plans:
        copies[3].wait_recv()
        copies[4].wait_recv()
        copies[7].start()
    for copies in plans:
        for i in (2, 5, 6, 7):
            copies[i].wait_recv()
    gathers[1].wait(2)
    for gather in gathers:
        gather.wait(1)
        gather.wait(3)
    for copy in there:
        copy.wait()
    for gather in gathers:
        gather.drain()
    for copies in plans:
        for copy in copies:
            copy.wait_send()


def first_call(tokens, cotan, owns, kinds):
    columns = lax.axis_size("tp")
    size, width = tokens.shape
    anywhere = pl.BlockSpec(memory_space=pl.ANY)
    copies = 8 * len(owns) + 8

    def gathered(own, kind):
        rows, cols = own.shape
        return (rows, 8 * cols) if kind == "columns" else (8, rows, cols)

    return pl.pallas_call(
        functools.partial(first_kernel, columns, size, kinds),
        out_shape=[jax.ShapeDtypeStruct((columns * size, rows.shape[1]), BF) for rows in (tokens, cotan)]
        + [jax.ShapeDtypeStruct(gathered(own, kind), own.dtype) for own, kind in zip(owns, kinds)],
        in_specs=[anywhere] * (2 + len(owns)),
        out_specs=[anywhere] * (2 + len(owns)),
        scratch_shapes=[pltpu.VMEM(rows.shape, BF) for rows in (tokens, cotan)]
        + [pltpu.VMEM(own.shape, own.dtype) for own in owns]
        + [
            pltpu.SemaphoreType.DMA((copies,)),
            pltpu.SemaphoreType.DMA((copies,)),
            pltpu.SemaphoreType.DMA((2 + len(owns),)),
        ],
        compiler_params=pltpu.CompilerParams(collective_id=2, has_side_effects=True),
        cost_estimate=pl.CostEstimate(
            flops=0, bytes_accessed=240 * SEQ * width, transcendentals=0
        ),
        name="first_gather",
    )(tokens, cotan, *owns)


class PlaneSum:
    def __init__(self, source, chip, theirs, links, stage, sends, arrivals, base, local):
        self.source, self.chip, self.theirs, self.links = source, chip, theirs, links
        self.stage, self.sends, self.arrivals, self.base = stage, sends, arrivals, base
        self.local = local
        self.parts, self.rows = chip.shape[1], chip.shape[2]
        self.partner, self.along, self.across = plane_neighbours()

    def pair(self, i, h):
        return mesh_copy(
            self.source(2 * i + 1, h),
            self.theirs.at[i, h],
            self.sends,
            self.arrivals,
            self.base + i * self.parts + h,
            self.partner,
        )

    def mine(self, i, h):
        return pltpu.make_async_copy(
            self.source(2 * i, h), self.chip.at[i, h], self.local.at[4 + i * self.parts + h]
        )

    def begin(self):
        for i in (3, 1, 2, 0):
            for h in range(self.parts):
                self.pair(i, h).start()
                self.mine(i, h).start()

    def fetch(self, landed, slot):
        size = landed.shape[0]
        return pltpu.make_async_copy(
            landed, self.stage.at[slot, pl.ds(0, size)], self.local.at[slot]
        )

    def add(self, i, h, start, size, slot):
        some = min(32, size)

        def one(n, carry):
            rows = pl.ds(pl.multiple_of(start + n * some, some), some)
            from_rows = pl.ds(pl.multiple_of(n * some, some), some)
            self.chip[i, h, rows, :] = (
                self.chip[i, h, rows, :].astype(F32) + self.stage[slot, from_rows, :].astype(F32)
            ).astype(BF)
            return carry

        lax.fori_loop(0, size // some, one, 0)

    def send_first(self, parts=None, fetched=True):
        for h in range(self.parts) if parts is None else parts:
            for i in (3, 1, 2, 0):
                self.pair(i, h).wait_recv()
                self.fetch(self.theirs.at[i, h], i).start()
            for i in (3, 1, 2, 0):
                if fetched:
                    self.mine(i, h).wait()
                self.fetch(self.theirs.at[i, h], i).wait()
                self.add(i, h, 0, self.rows, i)
                if i == 3:
                    self.send(1, [h])
                if i == 2:
                    self.send(0, [h])

    def link(self, stage_number, side, h):
        first_hop, second_hop = (
            (self.along, self.across) if side == 0 else (self.across, self.along)
        )
        near, far = (1, 2) if side == 0 else (2, 1)
        i = (near, 3, far)[stage_number]
        place = (stage_number * 2 + side) * self.parts + h
        rows = pl.ds(side * (self.rows // 2), self.rows // 2)
        return mesh_copy(
            self.chip.at[i, h, rows],
            self.links.at[place],
            self.sends,
            self.arrivals,
            self.base + 4 * self.parts + place,
            second_hop if stage_number == 2 else first_hop,
        )

    def landed(self, stage_number, side, h):
        return self.links.at[(stage_number * 2 + side) * self.parts + h]

    def send(self, stage_number, parts=None):
        for h in range(self.parts) if parts is None else parts:
            for side in range(2):
                self.link(stage_number, side, h).start()

    def send_second(self, parts=None):
        half = self.rows // 2
        for h in range(self.parts) if parts is None else parts:
            for side in range(2):
                self.link(1, side, h).wait_recv()
                self.fetch(self.landed(1, side, h), side).start()
            for side in range(2):
                self.fetch(self.landed(1, side, h), side).wait()
                self.add((2, 1)[side], h, side * half, half, side)
                self.link(2, side, h).start()

    def finish(self, parts=None):
        half = self.rows // 2
        for h in range(self.parts) if parts is None else parts:
            for stage_number in (0, 2):
                for side in range(2):
                    self.link(stage_number, side, h).wait_recv()
                    self.fetch(self.landed(stage_number, side, h), stage_number + side).start()
            for stage_number in (0, 2):
                for side in range(2):
                    slot = stage_number + side
                    self.fetch(self.landed(stage_number, side, h), slot).wait()
                    self.add(0, h, side * half, half, slot)

    def drain(self, first_part=0):
        for h in range(self.parts):
            for i in range(4):
                if h >= first_part:
                    self.pair(i, h).wait_send()
            for stage_number in range(3):
                for side in range(2):
                    self.link(stage_number, side, h).wait_send()


def plane_sum_sizes(parts):
    return 10 * parts, 4 + 4 * parts


def plane_sum_space(parts, rows, width):
    landing = [
        jax.ShapeDtypeStruct((4, parts, rows, width), BF),
        jax.ShapeDtypeStruct((6 * parts, rows // 2, width), BF),
    ]
    scratch = [pltpu.VMEM((4, parts, rows, width), BF), pltpu.VMEM((4, rows, width), BF)]
    return landing, scratch


def middle_kernel(cap, columns, size, experts, steps, local_hidden, *refs):
    (
        d_ffn_in,
        mixed_in,
        cotan_in,
        gain_ref,
        slot_table,
        weight_table,
        down_in,
        x_all,
        d_all,
        hid_all,
        dgu_all,
        d_mixed_out,
        d_proj_all,
        gain_out,
        routed_out,
        gate_grad,
        up_grad,
        down_grad,
        theirs,
        links,
        chip,
        stage,
        own_v,
        arrived_v,
        relayed_v,
        mixed_v,
        cotan_v,
        proj_v,
        xk,
        dk,
        hk,
        gk,
        totals,
        hid,
        down,
        parts,
        others,
        sends,
        arrivals,
        local,
        sum_local,
        work,
        written,
    ) = refs
    partner, along, across = plane_neighbours()
    column = column_neighbours(columns)
    greet([partner, along, across] + column)
    plane = PlaneSum(
        lambda r, h: others.at[h % 2, r // 2],
        chip,
        theirs,
        links,
        stage,
        sends,
        arrivals,
        0,
        sum_local,
    )
    base = plane_sum_sizes(columns)[0]
    rows_of = block_rows(columns, size)
    summed = ColumnSum(d_ffn_in, rows_of, arrived_v, relayed_v, sends, arrivals, base)
    gather = ColumnGather(d_proj_all, rows_of, sends, arrivals, base + 4)
    summed.start(local.at[3])
    first = [
        pltpu.make_async_copy(d_ffn_in.at[rows_of(0)], own_v, local.at[0]),
        pltpu.make_async_copy(mixed_in, mixed_v, local.at[1]),
        pltpu.make_async_copy(cotan_in, cotan_v, local.at[2]),
    ]
    for copy in first:
        copy.start()
    width = xk.shape[2]
    pad = hk.shape[2]
    tile = min(1024, width)
    hidden_in = [pltpu.make_async_copy(hid_all.at[b], hid.at[b], local.at[4 + b]) for b in range(columns)]
    down_copies = [
        pltpu.make_async_copy(
            down_in.at[e], down.at[e, pl.ds(0, local_hidden)], local.at[4 + columns + e]
        )
        for e in range(experts)
    ]
    for copy in down_copies + hidden_in:
        copy.start()
    summed.clear()
    rest = down.shape[1] - local_hidden
    if rest > 0:
        for e in range(experts):
            down[e, local_hidden:, :] = jnp.zeros((rest, down.shape[2]), BF)
    for copy in down_copies:
        copy.wait()
    wide = 2 * cap

    def out_part(b):
        hidden_in[b].wait()
        weights = [
            slot_weights(
                select_rows(slots_of(slot_table, experts, columns, size, b, q), experts, wide),
                slots_of(weight_table, experts, columns, size, b, q),
                experts,
                wide,
            )
            for q in range(QUARTET)
        ]
        for e in range(experts):

            def one_tile(n, carry, e=e):
                cols = pl.ds(pl.multiple_of(n * tile, tile), tile)
                rows = dot_plain(hid[b, e], down[e, :, cols])
                for q in range(QUARTET):
                    parts[q, e * wide : (e + 1) * wide, cols] = (
                        rows[q * wide : (q + 1) * wide] * weights[q][e * wide : (e + 1) * wide]
                    ).astype(BF)
                return carry

            lax.fori_loop(0, width // tile, one_tile, 0)
        if b > 1:
            for i in range(4):
                plane.pair(i, b - 2).wait_send()

        def keep(q, cols, value):
            chip[q, b, :, cols] = value[:size]
            others[b % 2, q, :, cols] = value[size:]

        token_sums(slot_table, experts, columns, size, wide, b, parts, keep)
        for i in range(4):
            plane.pair(i, b).start()

    jobs = [(e, step) for e in range(experts) for step in range(steps)]

    def fetch(k):
        e, step = jobs[k]
        slot = k % 2
        return [
            pltpu.make_async_copy(x_all.at[step, e], xk.at[slot], work.at[slot, 0]),
            pltpu.make_async_copy(d_all.at[step, e], dk.at[slot], work.at[slot, 1]),
            pltpu.make_async_copy(hid_all.at[step, e], hk.at[slot], work.at[slot, 2]),
            pltpu.make_async_copy(dgu_all.at[step, e], gk.at[slot], work.at[slot, 3]),
        ]

    def write(e):
        return [
            pltpu.make_async_copy(
                totals.at[e % 2, i, pl.ds(0, local_hidden)], grad.at[e], written.at[e % 2, i]
            )
            for i, grad in enumerate((gate_grad, up_grad, down_grad))
        ]

    def job(k):
        e, step = jobs[k]
        slot, place = k % 2, e % 2
        if k + 1 < len(jobs):
            for copy in fetch(k + 1):
                copy.start()
        for copy in fetch(k):
            copy.wait()
        if step == 0 and e > 1:
            for copy in write(e - 2):
                copy.wait()

        def one(n, carry):
            cols = pl.ds(pl.multiple_of(n * tile, tile), tile)
            found = [
                dot_first(gk[slot, :, :pad], xk[slot, :, cols]),
                dot_first(gk[slot, :, pad:], xk[slot, :, cols]),
                dot_first(hk[slot], dk[slot, :, cols]),
            ]
            for i, value in enumerate(found):
                if step == 0:
                    totals[place, i, :, cols] = value
                else:
                    totals[place, i, :, cols] += value
            return carry

        lax.fori_loop(0, width // tile, one, 0)
        if step == steps - 1:
            for copy in write(e):
                copy.start()

    out_part(0)
    out_part(1)
    summed.middle(local.at[3])
    plane.send_first([0], False)
    out_part(2)
    plane.send_first([1], False)
    for copy in fetch(0):
        copy.start()
    out_part(3)
    plane.send_first([2], False)
    job(0)
    plane.send_first([3], False)

    for copy in first:
        copy.wait()
    total = summed.total(own_v[...])
    mixed = mixed_v[...]
    inverse = lax.rsqrt(jnp.mean(mixed * mixed, axis=1, keepdims=True) + EPSILON)
    unit = mixed * inverse
    scaled = total * gain_ref[...]
    gain_out[...] = jnp.sum(total * unit, axis=0, keepdims=True)
    back = inverse * (scaled - unit * jnp.mean(scaled * unit, axis=1, keepdims=True))
    d_mixed = cotan_v[...].astype(F32) + back
    mixed_v[...] = d_mixed
    proj_v[...] = d_mixed.astype(BF)
    own_copy = pltpu.make_async_copy(proj_v, d_proj_all.at[rows_of(0)], local.at[0])
    own_copy.start()
    mixed_copy = pltpu.make_async_copy(mixed_v, d_mixed_out, local.at[1])
    mixed_copy.start()
    own_copy.wait()
    gather.start()
    for b in range(columns):
        if b + 1 < len(jobs):
            job(b + 1)
        plane.send_second([b])
        if b == 1:
            gather.wait(2)
    for b in range(columns):
        if columns + 1 + b < len(jobs):
            job(columns + 1 + b)
        if b < columns - 1:
            plane.finish([b])
    for k in range(2 * columns + 1, len(jobs)):
        job(k)
    plane.finish([columns - 1])
    done = [
        pltpu.make_async_copy(chip.at[0, h], routed_out.at[rows_of(h)], sum_local.at[4 + h])
        for h in range(columns)
    ]
    for copy in done:
        copy.start()
    gather.wait(1)
    gather.wait(3)
    for copy in done + [mixed_copy]:
        copy.wait()
    for e in range(max(0, experts - 2), experts):
        for copy in write(e):
            copy.wait()
    plane.drain(2)
    gather.drain()
    summed.drain()


def middle_call(d_ffn, mixed, cotan, gain, tables, down, kept, cap):
    columns = lax.axis_size("tp")
    size, width = cotan.shape
    x_all, d_all, hid_all, dgu_all = kept
    steps, experts, slots, pad = hid_all.shape
    local_hidden = down.shape[1]
    anywhere = pl.BlockSpec(memory_space=pl.ANY)
    held = pl.BlockSpec(memory_space=pltpu.VMEM)
    landing, scratch = plane_sum_space(columns, size, width)
    remote, near = plane_sum_sizes(columns)
    remote = remote + 8
    grad = jax.ShapeDtypeStruct((experts, local_hidden, width), F32)
    results = pl.pallas_call(
        functools.partial(middle_kernel, cap, columns, size, experts, steps, local_hidden),
        out_shape=[
            jax.ShapeDtypeStruct((size, width), F32),
            jax.ShapeDtypeStruct((SEQ, width), BF),
            jax.ShapeDtypeStruct((1, width), F32),
            jax.ShapeDtypeStruct((SEQ, width), BF),
            grad,
            grad,
            grad,
        ]
        + landing,
        in_specs=[anywhere] * 3 + [held] * 3 + [anywhere] * 5,
        out_specs=[anywhere] * 2 + [held] + [anywhere] * 6,
        scratch_shapes=scratch
        + [
            pltpu.VMEM((size, width), BF),
            pltpu.VMEM((columns - 1, size, width), BF),
            pltpu.VMEM((2, size, width), BF),
            pltpu.VMEM((size, width), F32),
            pltpu.VMEM((size, width), BF),
            pltpu.VMEM((size, width), BF),
            pltpu.VMEM((2, slots, width), BF),
            pltpu.VMEM((2, slots, width), BF),
            pltpu.VMEM((2, slots, pad), BF),
            pltpu.VMEM((2, slots, 2 * pad), BF),
            pltpu.VMEM((2, 3, pad, width), F32),
            pltpu.VMEM((steps, experts, slots, pad), BF),
            pltpu.VMEM((experts, pad, width), BF),
            pltpu.VMEM((QUARTET, 2 * experts * cap, width), BF),
            pltpu.VMEM((2, 4, size, width), BF),
            pltpu.SemaphoreType.DMA((remote,)),
            pltpu.SemaphoreType.DMA((remote,)),
            pltpu.SemaphoreType.DMA((4 + columns + experts,)),
            pltpu.SemaphoreType.DMA((near,)),
            pltpu.SemaphoreType.DMA((2, 4)),
            pltpu.SemaphoreType.DMA((2, 3)),
        ],
        compiler_params=pltpu.CompilerParams(
            collective_id=3, has_side_effects=True, vmem_limit_bytes=67_043_328
        ),
        cost_estimate=pl.CostEstimate(
            flops=2 * 3 * steps * experts * slots * width * pad,
            bytes_accessed=300 * SEQ * width,
            transcendentals=0,
        ),
        name="middle",
    )(d_ffn, mixed, cotan, gain, *tables, down, x_all, d_all, hid_all, dgu_all)
    return results[:7]


def last_kernel(columns, size, latent_start, latent_width, *refs):
    (
        d_normed_in,
        tokens_in,
        d_mixed_in,
        gain_ref,
        joint_in,
        up_in,
        out_in,
        sums_in,
        grad_out,
        joint_out,
        up_out,
        out_out,
        latent_out,
        sums_out,
        joint_theirs,
        joint_links,
        up_theirs,
        up_links,
        out_theirs,
        out_links,
        joint_chip,
        joint_stage,
        up_chip,
        up_stage,
        out_chip,
        out_stage,
        own_v,
        arrived_v,
        relayed_v,
        tokens_v,
        mixed_v,
        running,
        sums_v,
        latent_v,
        sends,
        arrivals,
        local,
        joint_local,
        up_local,
        out_local,
    ) = refs
    partner, along, across = plane_neighbours()
    column = column_neighbours(columns)
    row = lax.axis_index("tp")
    greet([partner, along, across] + column)
    each = plane_sum_sizes(1)[0]
    joint_rows, up_rows = joint_chip.shape[2], up_chip.shape[2]
    out_cols = out_chip.shape[3]

    def by_rows(ref, count):
        return lambda r, h: ref.at[pl.ds(pl.multiple_of(plane_place(r) * count, count), count)]

    joint = PlaneSum(
        by_rows(joint_in, joint_rows),
        joint_chip,
        joint_theirs,
        joint_links,
        joint_stage,
        sends,
        arrivals,
        0,
        joint_local,
    )
    up = PlaneSum(
        by_rows(up_in, up_rows),
        up_chip,
        up_theirs,
        up_links,
        up_stage,
        sends,
        arrivals,
        each,
        up_local,
    )
    out = PlaneSum(
        lambda r, h: out_in.at[
            :, pl.ds(pl.multiple_of(plane_place(r) * out_cols, out_cols), out_cols)
        ],
        out_chip,
        out_theirs,
        out_links,
        out_stage,
        sends,
        arrivals,
        2 * each,
        out_local,
    )
    base = 3 * each
    rows_of = block_rows(columns, size)
    summed = ColumnSum(d_normed_in, rows_of, arrived_v, relayed_v, sends, arrivals, base)
    base = base + 4
    summed.start(local.at[4])
    first = [
        pltpu.make_async_copy(d_normed_in.at[rows_of(0)], own_v, local.at[0]),
        pltpu.make_async_copy(tokens_in, tokens_v, local.at[1]),
        pltpu.make_async_copy(d_mixed_in, mixed_v, local.at[2]),
        pltpu.make_async_copy(sums_in, running.at[0], local.at[3]),
    ]
    for copy in first:
        copy.start()
    for part in (out, joint, up):
        part.begin()
    summed.clear()
    first[3].wait()

    def small(i, device):
        return mesh_copy(running.at[i], sums_v.at[i], sends, arrivals, base + i, device)

    hops = [small(i, device) for i, device in enumerate((partner, along, across))]
    for i, copy in enumerate(hops):
        copy.start()
        copy.wait_recv()
        running[i + 1] = running[i] + sums_v[i]
    gains = [
        mesh_copy(running.at[3], sums_v.at[2 + s], sends, arrivals, base + 2 + s, column[s - 1])
        for s in range(1, columns)
    ]
    base = base + 2 + columns
    for copy in gains:
        copy.start()
    summed.middle(local.at[4])
    for part in (out, joint, up):
        part.send_first()
    for part in (out, joint, up):
        part.send_second()
    for part in (out, joint, up):
        part.finish()

    pieces = joint_rows // columns
    across_columns = [
        mesh_copy(
            joint_chip.at[
                0,
                0,
                pl.ds(pl.multiple_of((row + s) % columns * pieces, pieces), pieces),
                pl.ds(latent_start, latent_width),
            ],
            latent_v.at[s - 1],
            sends,
            arrivals,
            base + s - 1,
            column[s - 1],
        )
        for s in range(1, columns)
    ]
    for copy in across_columns:
        copy.start()
    done = [
        pltpu.make_async_copy(joint_chip.at[0, 0], joint_out, joint_local.at[4]),
        pltpu.make_async_copy(up_chip.at[0, 0], up_out, up_local.at[4]),
        pltpu.make_async_copy(out_chip.at[0, 0], out_out, out_local.at[4]),
    ]
    for copy in done:
        copy.start()

    for copy in first[:3]:
        copy.wait()
    total = summed.total(own_v[...])
    tokens = tokens_v[...].astype(F32)
    inverse = lax.rsqrt(jnp.mean(tokens * tokens, axis=1, keepdims=True) + EPSILON)
    unit = tokens * inverse
    scaled = total * gain_ref[...]
    mixed_v[...] = mixed_v[...] + inverse * (
        scaled - unit * jnp.mean(scaled * unit, axis=1, keepdims=True)
    )
    grad_copy = pltpu.make_async_copy(mixed_v, grad_out, local.at[0])
    grad_copy.start()
    gathered = running[3]
    for s in range(1, columns):
        gains[s - 1].wait_recv()
        gathered = gathered + sums_v[2 + s]
    sums_out[...] = gathered
    latent = joint_chip[
        0,
        0,
        pl.ds(pl.multiple_of(row * pieces, pieces), pieces),
        pl.ds(latent_start, latent_width),
    ].astype(F32)
    for s in range(1, columns):
        across_columns[s - 1].wait_recv()
        latent = latent + latent_v[s - 1].astype(F32)
    latent_out[...] = latent
    for copy in done + [grad_copy]:
        copy.wait()
    for part in (out, joint, up):
        part.drain()
    summed.drain()
    for copy in hops + gains + across_columns:
        copy.wait_send()


def last_call(d_normed, tokens, d_mixed, gain, joint, up, out, sums, latent_start, latent_width):
    columns = lax.axis_size("tp")
    size, width = tokens.shape
    anywhere = pl.BlockSpec(memory_space=pl.ANY)
    held = pl.BlockSpec(memory_space=pltpu.VMEM)
    shapes = [
        (joint.shape[0] // 8, joint.shape[1]),
        (up.shape[0] // 8, up.shape[1]),
        (out.shape[0], out.shape[1] // 8),
    ]
    landing, scratch = [], []
    for rows, cols in shapes:
        one = plane_sum_space(1, rows, cols)
        landing, scratch = landing + one[0], scratch + one[1]
    remote, near = plane_sum_sizes(1)
    remote = 3 * remote + 2 * (columns - 1) + 7
    pieces = shapes[0][0] // columns
    return pl.pallas_call(
        functools.partial(last_kernel, columns, size, latent_start, latent_width),
        out_shape=[jax.ShapeDtypeStruct((size, width), F32)]
        + [jax.ShapeDtypeStruct(shape, BF) for shape in shapes]
        + [
            jax.ShapeDtypeStruct((pieces, latent_width), F32),
            jax.ShapeDtypeStruct(sums.shape, F32),
        ]
        + landing,
        in_specs=[anywhere] * 3 + [held] + [anywhere] * 4,
        out_specs=[anywhere] * 4 + [held] * 2 + [anywhere] * 6,
        scratch_shapes=scratch
        + [
            pltpu.VMEM((size, width), BF),
            pltpu.VMEM((columns - 1, size, width), BF),
            pltpu.VMEM((2, size, width), BF),
            pltpu.VMEM((size, width), BF),
            pltpu.VMEM((size, width), F32),
            pltpu.VMEM((4,) + sums.shape, F32),
            pltpu.VMEM((2 + columns,) + sums.shape, F32),
            pltpu.VMEM((columns - 1, pieces, latent_width), BF),
            pltpu.SemaphoreType.DMA((remote,)),
            pltpu.SemaphoreType.DMA((remote,)),
            pltpu.SemaphoreType.DMA((5,)),
            pltpu.SemaphoreType.DMA((near,)),
            pltpu.SemaphoreType.DMA((near,)),
            pltpu.SemaphoreType.DMA((near,)),
        ],
        compiler_params=pltpu.CompilerParams(
            collective_id=4, has_side_effects=True, vmem_limit_bytes=48 * 1024 * 1024
        ),
        cost_estimate=pl.CostEstimate(
            flops=0, bytes_accessed=180 * SEQ * width, transcendentals=0
        ),
        name="last_sums",
    )(d_normed, tokens, d_mixed, gain, joint, up, out, sums)[:6]


def plane_units(count):
    return [[(2 * i + j // 2, j % 2) for j in range(4)] for i in range(count // 2)]


def plane_gather(rows, count):
    gathered = lax.all_gather(rows, "fsdp", axis=0)
    return {
        (r, h): gathered[r, h * HALF : (h + 1) * HALF] for r in range(count) for h in (0, 1)
    }


def plane_scatter_whole(pairs, units, count):
    parts = {}
    for unit, pair in zip(units, pairs):
        for q, key in enumerate(unit):
            parts[key] = pair[q // 2][q % 2]
    stacked = jnp.concatenate([parts[r, h] for r in range(count) for h in (0, 1)], axis=0)
    return lax.psum_scatter(stacked, "fsdp", scatter_dimension=0, tiled=True).astype(F32)


def sum_everywhere(values):
    for axis_name in ("fsdp", "tp"):
        count = lax.axis_size(axis_name)
        if is_power(count):
            bit = 1
            while bit < count:
                values = values + swap(values, axis_name, bit)
                bit *= 2
        else:
            values = lax.psum(values, axis_name)
    return values


def expert_tables(expert_ids, expert_wts, local_experts, units, cap):
    fsdp_count = lax.axis_size("fsdp")
    fsdp_rank = lax.axis_index("fsdp")
    expert_count = local_experts * fsdp_count
    names = jnp.arange(expert_count, dtype=jnp.int32)[:, None]
    member = jnp.zeros((expert_count, SEQ), jnp.bool_)
    weight = jnp.zeros((expert_count, SEQ), F32)
    ids_rows, wts_rows = expert_ids.T, expert_wts.T
    for pick in range(TOPK):
        same = ids_rows[pick : pick + 1] == names
        member = member | same
        weight = weight + jnp.where(same, wts_rows[pick : pick + 1], 0.0)
    position = jnp.arange(HALF)
    before = (position[:, None] < position[None, :]).astype(BF)
    rank = jnp.dot(
        member.astype(BF).reshape(expert_count * 2, HALF), before, preferred_element_type=F32
    ).reshape(expert_count, SEQ)
    slot = jnp.where(member, rank, NO_SLOT)
    table = jnp.concatenate([slot, weight], axis=0)
    table = lax.all_gather(table, "fsdp", axis=0, tiled=True)
    table = table.reshape(fsdp_count, 2, fsdp_count, local_experts, 2, HALF)
    table = lax.dynamic_index_in_dim(table, fsdp_rank, axis=2, keepdims=False)
    slot_steps, weight_steps = [], []
    for unit in units:
        slot_steps.append(jnp.stack([table[r, 0, :, h] for r, h in unit]))
        weight_steps.append(jnp.stack([table[r, 1, :, h] for r, h in unit]))
    slot_row, weight_row = jnp.stack(slot_steps), jnp.stack(weight_steps)
    return (slot_row, weight_row, jnp.swapaxes(slot_row, 2, 3))


def per_device(
    block_in,
    out_cotan,
    segment_ids,
    expert_ids,
    expert_wts,
    attn_gain,
    query_proj,
    latent_proj,
    latent_gain,
    latent_up,
    out_proj,
    ffn_gain,
    shared_gate,
    shared_up,
    shared_down,
    routed_gate,
    routed_up,
    routed_down,
):
    tp_count = lax.axis_size("tp")
    fsdp_count = lax.axis_size("fsdp")
    tp_rank = lax.axis_index("tp")
    fsdp_rank = lax.axis_index("fsdp")
    tok_rows, model_width = block_in.shape
    local_experts, local_hidden = routed_gate.shape[:2]
    expert_count = local_experts * fsdp_count
    cap_rows = tok_rows * TOPK * 4 // (3 * expert_count)
    cap = cap_rows * (HALF // tok_rows)
    paired = fsdp_count == 8 and tp_count == 4 and tok_rows * 2 == HALF
    heads_local = H // tp_count
    head_width = NOPE + ROPE
    score_scale = head_width ** (-0.5)
    shard_rows, query_cols = query_proj.shape
    latent_cols = latent_proj.shape[1]
    up_cols = latent_up.shape[1]
    out_rows = out_proj.shape[0]

    joint = query_cols + latent_cols
    spare = (-joint) % 128
    spare = spare + 128 if spare < 3 else spare
    gains = jnp.concatenate(
        [
            attn_gain[:, None],
            ffn_gain[:, None],
            jnp.pad(latent_gain, (0, shard_rows - latent_gain.shape[0]))[:, None],
            jnp.zeros((shard_rows, spare - 3), BF),
        ],
        axis=1,
    )
    packed = jnp.concatenate([query_proj, latent_proj, gains], axis=1)
    if paired:
        low, high = (0, RAW_ROWS - TOPK), (0, 0)
        raw = jnp.concatenate(
            [jnp.pad(expert_ids.T.astype(F32), (low, high)), jnp.pad(expert_wts.T, (low, high))]
        )
        half = model_width // 2
        cotan_left = lax.all_gather(out_cotan[:, :half], ("fsdp", "tp"), axis=0, tiled=True)
        tokens_all, cotan_right, packed_all, latent_up_weight, out_weight, raw = first_call(
            block_in,
            out_cotan[:, half:],
            [packed, latent_up, out_proj, raw],
            ("rows", "rows", "columns", "relative"),
        )
        shared_own, down_own, cotan_right = tie(
            jnp.concatenate([shared_gate, shared_up], axis=1), shared_down, cotan_right
        )
        own_left = lax.dynamic_slice_in_dim(cotan_left, fsdp_rank * SEQ, SEQ, axis=0)
        cotan_all = jnp.concatenate([own_left, cotan_right], axis=1)
        packed_all = packed_all.reshape(-1, packed.shape[1])
        latent_up_weight = latent_up_weight.reshape(LAT, up_cols)
    else:
        packed_all = lax.all_gather(packed, "fsdp", axis=0, tiled=True)
        latent_up_weight = lax.all_gather(latent_up, "fsdp", axis=0, tiled=True)
        out_weight = lax.all_gather(out_proj, "fsdp", axis=1, tiled=True)
        tokens_all = column_gather(block_in)
        cotan_all = column_gather(out_cotan)
        shared_own, down_own = jnp.concatenate([shared_gate, shared_up], axis=1), shared_down
    shared_weight = lax.all_gather(shared_own, "fsdp", axis=0, tiled=True)
    shared_down_weight = lax.all_gather(down_own, "fsdp", axis=1, tiled=True)
    gain_attn = packed_all[:, joint].astype(F32)
    gain_ffn = packed_all[:, joint + 1].astype(F32)
    gain_latent = (
        packed_all[:, joint + 2]
        .reshape(fsdp_count, shard_rows)[:, : latent_gain.shape[0]]
        .reshape(LAT)
        .astype(F32)
    )
    shared_cols = shared_gate.shape[1]

    def scatter(part, dimension):
        return lax.psum_scatter(part.astype(BF), "fsdp", scatter_dimension=dimension, tiled=True)

    unit_all, inverse_all = norm_parts(tokens_all.astype(F32))
    normed_all = (unit_all * gain_attn).astype(BF)
    joint_rows = jnp.dot(normed_all, packed_all, preferred_element_type=F32)
    queries = joint_rows[:, :query_cols].reshape(SEQ, heads_local, head_width)
    latent = joint_rows[:, query_cols:joint]
    unit_lat, inverse_lat = norm_parts(latent[:, :LAT])
    positions = jnp.arange(SEQ, dtype=jnp.int32)
    cosine, sine_part = rope_tables(positions, ROPE)
    compressed_all = (unit_lat * gain_latent).astype(BF)
    key_rope_all = rotate(latent[:, LAT:], cosine, sine_part).astype(BF)
    query_cat = jnp.concatenate(
        [
            queries[:, :, :NOPE],
            rotate(queries[:, :, NOPE:], cosine[:, None, :], sine_part[:, None, :]),
        ],
        axis=2,
    ).astype(BF)
    key_value = (
        jnp.dot(compressed_all, latent_up_weight, preferred_element_type=F32)
        .reshape(SEQ, heads_local, NOPE + DV)
        .astype(BF)
    )
    key_cat = jnp.concatenate(
        [
            key_value[:, :, :NOPE],
            jnp.broadcast_to(key_rope_all[:, None, :], (SEQ, heads_local, ROPE)),
        ],
        axis=2,
    )
    values = key_value[:, :, NOPE:]
    allowed = (positions[None, :] <= positions[:, None]) & (
        segment_ids[None, :] == segment_ids[:, None]
    )
    raw_scores = (
        jnp.einsum("qhd,khd->hqk", query_cat, key_cat, preferred_element_type=F32) * score_scale
    )
    masked = jnp.where(allowed[None], raw_scores, MASK_FILL)
    top_score = jnp.max(masked, axis=2, keepdims=True)
    exponent = jnp.exp(masked - top_score)
    row_total = jnp.sum(exponent, axis=2, keepdims=True)
    probabilities = exponent / row_total
    probs_low = probabilities.astype(BF)
    attended = (
        jnp.einsum("hqk,khd->qhd", probs_low, values, preferred_element_type=F32)
        .reshape(SEQ, heads_local * DV)
        .astype(BF)
    )
    attn_part = jnp.dot(attended, out_weight, preferred_element_type=F32).astype(BF)
    if paired:
        mixed_rows, normed_ffn_all, d_routed_in, *kept = expert_call(
            attn_part,
            block_in,
            cotan_right,
            cotan_left,
            routed_gate,
            routed_up,
            routed_down,
            gain_ffn[None, :],
            raw,
            cap_rows,
        )
        unit_two, inverse_two = norm_parts(mixed_rows)
        d_routed_in = d_routed_in.astype(F32)
    else:
        units = plane_units(fsdp_count)
        tables = expert_tables(expert_ids, expert_wts, local_experts, units, cap)
        hidden_pad = -(-local_hidden // 128) * 128
        lift = ((0, 0), (0, hidden_pad - local_hidden), (0, 0))
        routed_gate_up = jnp.concatenate(
            [jnp.pad(routed_gate, lift), jnp.pad(routed_up, lift)], axis=1
        )
        routed_down_pad = jnp.pad(routed_down, lift)
        mixed_rows = block_in.astype(F32) + column_scatter(attn_part)
        unit_two, inverse_two = norm_parts(mixed_rows)
        normed_ffn_all = column_gather((unit_two * gain_ffn).astype(BF))
        x_blocks = plane_gather(normed_ffn_all, fsdp_count)
        dy_all = lax.all_gather(cotan_all, "fsdp", axis=0, tiled=True)
        kept = []
        dx_pairs = []
        for step, unit in enumerate(units):
            pair, kept = expert_front(
                step,
                len(units),
                [x_blocks[key] for key in unit],
                jnp.array([2 * r + h for r, h in unit], jnp.int32),
                dy_all,
                routed_gate_up,
                routed_down_pad,
                tables,
                kept,
                cap,
            )
            dx_pairs.append(pair)
        near, far = expert_out(kept[2], routed_down_pad, tables, cap)
        d_routed_in = plane_scatter_whole(dx_pairs, units, fsdp_count)
    if not paired:
        routed_gate_grad, routed_up_grad, routed_down_grad = expert_grads(kept, local_hidden)

    shared_pre = jnp.dot(normed_ffn_all, shared_weight, preferred_element_type=F32)
    shared_gate_pre, shared_up_pre = shared_pre[:, :shared_cols], shared_pre[:, shared_cols:]
    shared_hidden = (jax.nn.silu(shared_gate_pre) * shared_up_pre).astype(BF)
    shared_rows = jnp.dot(shared_hidden, shared_down_weight, preferred_element_type=F32)
    shared_down_part = jnp.dot(shared_hidden.T, cotan_all, preferred_element_type=F32)
    d_shared_hidden = jnp.dot(cotan_all, shared_down_weight.T, preferred_element_type=F32)
    d_shared = jnp.concatenate(silu_back(d_shared_hidden, shared_gate_pre, shared_up_pre), axis=1)
    shared_part = jnp.dot(normed_ffn_all.T, d_shared, preferred_element_type=F32)
    d_shared_in = jnp.dot(d_shared, shared_weight.T, preferred_element_type=F32)

    if paired:
        d_ffn_rows, shared_part, shared_down_part = tie(
            (d_shared_in + d_routed_in).astype(BF),
            shared_part.astype(BF),
            shared_down_part.astype(BF),
        )
        (
            d_mixed,
            d_proj_all,
            ffn_gain_part,
            routed_rows,
            routed_gate_grad,
            routed_up_grad,
            routed_down_grad,
        ) = middle_call(
            d_ffn_rows,
            mixed_rows,
            out_cotan,
            gain_ffn[None, :],
            kept[:2],
            routed_down,
            kept[2:],
            cap_rows,
        )
        ffn_gain_part = ffn_gain_part[0]
        routed_rows = routed_rows.astype(F32)
    else:
        d_normed_ffn = column_scatter(d_shared_in + d_routed_in)
        out_pairs = [(near[step], far[step]) for step in range(len(units))]
        routed_rows = plane_scatter_whole(out_pairs, units, fsdp_count)
        ffn_gain_part, d_mixed_norm = norm_back(d_normed_ffn, unit_two, inverse_two, gain_ffn)
        d_mixed = out_cotan.astype(F32) + d_mixed_norm
        d_proj_all = column_gather(d_mixed.astype(BF))
    shared_grad = scatter(shared_part, 0)
    down_own, ffn_rows, shared_grad = tie(
        shared_down_part.astype(BF), (shared_rows + routed_rows).astype(BF), shared_grad
    )
    shared_down_grad = scatter(down_own, 1)
    ffn_rows = column_scatter(ffn_rows)
    block_out = (mixed_rows + ffn_rows).astype(BF)

    out_part = jnp.dot(attended.T, d_proj_all, preferred_element_type=F32)
    d_attended = (
        jnp.dot(d_proj_all, out_weight.T, preferred_element_type=F32)
        .astype(BF)
        .reshape(SEQ, heads_local, DV)
    )
    prob_grad = jnp.einsum("qhd,khd->hqk", d_attended, values, preferred_element_type=F32)
    score_grad = (
        probabilities
        * (prob_grad - jnp.sum(probabilities * prob_grad, axis=2, keepdims=True))
    ).astype(BF)
    query_grad = (
        jnp.einsum("hqk,khd->qhd", score_grad, key_cat, preferred_element_type=F32) * score_scale
    )
    key_grad = (
        jnp.einsum("hqk,qhd->khd", score_grad, query_cat, preferred_element_type=F32) * score_scale
    )
    value_grad = jnp.einsum("hqk,qhd->khd", probs_low, d_attended, preferred_element_type=F32)
    d_queries = (
        jnp.concatenate(
            [
                query_grad[:, :, :NOPE],
                unrotate(query_grad[:, :, NOPE:], cosine[:, None, :], sine_part[:, None, :]),
            ],
            axis=2,
        )
        .reshape(SEQ, heads_local * head_width)
        .astype(BF)
    )
    d_key_value = (
        jnp.concatenate([key_grad[:, :, :NOPE], value_grad], axis=2)
        .reshape(SEQ, heads_local * (NOPE + DV))
        .astype(BF)
    )
    latent_up_part = jnp.dot(compressed_all.T, d_key_value, preferred_element_type=F32)
    d_compressed = jnp.dot(d_key_value, latent_up_weight.T, preferred_element_type=F32)
    d_key_rope = jnp.sum(key_grad[:, :, NOPE:], axis=1)
    latent_gain_part, d_latent_main = norm_back(d_compressed, unit_lat, inverse_lat, gain_latent)
    d_latent = jnp.concatenate(
        [d_latent_main, unrotate(d_key_rope, cosine, sine_part)], axis=1
    ).astype(BF)
    d_joint = jnp.concatenate([d_queries, d_latent, jnp.zeros((SEQ, spare), BF)], axis=1)
    joint_part = jnp.dot(normed_all.T, d_joint, preferred_element_type=F32)
    d_normed_part = jnp.dot(d_joint, packed_all.T, preferred_element_type=F32)
    attn_gain_part = jnp.sum(d_normed_part * unit_all, axis=0)

    gain_parts = jnp.concatenate([attn_gain_part, latent_gain_part, ffn_gain_part]).reshape(
        -1, 128
    )
    joint_part = joint_part.astype(BF)
    if paired:
        latent_width = joint_part.shape[1] - query_cols
        (
            block_in_grad,
            joint_grad,
            latent_up_grad,
            out_proj_grad,
            latent_proj_grad,
            gain_sums,
        ) = last_call(
            d_normed_part.astype(BF),
            block_in,
            d_mixed,
            gain_attn[None, :],
            joint_part,
            latent_up_part.astype(BF),
            out_part.astype(BF),
            gain_parts,
            query_cols,
            latent_width,
        )
        latent_proj_grad = latent_proj_grad[:, :latent_cols]
    else:
        d_normed = column_scatter(d_normed_part)
        unit_one, inverse_one = norm_parts(block_in.astype(F32))
        _, d_tokens_norm = norm_back(d_normed, unit_one, inverse_one, gain_attn)
        block_in_grad = d_mixed + d_tokens_norm
        out_proj_grad = scatter(out_part, 1)
        latent_up_grad = scatter(latent_up_part, 0)
        joint_grad = scatter(joint_part, 0)
        latent_proj_grad = column_scatter(joint_grad[:, query_cols:joint])
        gain_sums = sum_everywhere(gain_parts)
    gain_sums = gain_sums.reshape(-1)
    query_proj_grad = joint_grad[:, :query_cols].astype(F32)
    latent_up_grad = latent_up_grad.astype(F32)
    out_proj_grad = out_proj_grad.astype(F32)
    shared_grad = shared_grad.astype(F32)
    shared_gate_grad, shared_up_grad = shared_grad[:, :shared_cols], shared_grad[:, shared_cols:]
    shared_down_grad = shared_down_grad.astype(F32)
    device = fsdp_rank * tp_count + tp_rank
    devices = tp_count * fsdp_count

    def own_gain(start, size):
        return lax.dynamic_slice(gain_sums, (start + device * (size // devices),), (size // devices,))

    attn_gain_grad = own_gain(0, model_width)
    latent_gain_grad = own_gain(model_width, LAT)
    ffn_gain_grad = own_gain(model_width + LAT, model_width)
    return (
        block_out,
        block_in_grad,
        attn_gain_grad,
        query_proj_grad,
        latent_proj_grad,
        latent_gain_grad,
        latent_up_grad,
        out_proj_grad,
        ffn_gain_grad,
        shared_gate_grad,
        shared_up_grad,
        shared_down_grad,
        routed_gate_grad,
        routed_up_grad,
        routed_down_grad,
    )


def solution(mesh):
    placed = (
        P(("fsdp", "tp"), None),
        P(("fsdp", "tp"), None),
        P("fsdp"),
        P("fsdp", None),
        P("fsdp", None),
        P("fsdp"),
        P("fsdp", "tp"),
        P("fsdp", None),
        P("fsdp"),
        P("fsdp", "tp"),
        P("tp", "fsdp"),
        P("fsdp"),
        P("fsdp", "tp"),
        P("fsdp", "tp"),
        P("tp", "fsdp"),
        P("fsdp", "tp", None),
        P("fsdp", "tp", None),
        P("fsdp", "tp", None),
    )
    return jax.shard_map(
        per_device,
        mesh=mesh,
        in_specs=placed,
        out_specs=(
            P(("fsdp", "tp"), None),
            P(("fsdp", "tp"), None),
            P(("fsdp", "tp")),
            P("fsdp", "tp"),
            P(("fsdp", "tp"), None),
            P(("fsdp", "tp")),
            P("fsdp", "tp"),
            P("tp", "fsdp"),
            P(("fsdp", "tp")),
            P("fsdp", "tp"),
            P("fsdp", "tp"),
            P("tp", "fsdp"),
            P("fsdp", "tp", None),
            P("fsdp", "tp", None),
            P("fsdp", "tp", None),
        ),
        check_vma=False,
    )
```

```python
import functools

import jax
import jax.numpy as jnp
from jax import lax
from jax.experimental import pallas as pl
from jax.experimental.pallas import tpu as pltpu
from jax.sharding import PartitionSpec as P

H = 16
NOPE = 128
ROPE = 64
DV = 128
LAT = 512
TOPK = 6
SEQ = 512
HALF = 256
QUARTET = 4
RAW_ROWS = 8


EPSILON = 1e-06
THETA_BASE = 10000.0
MASK_FILL = -1e30
NO_SLOT = -1e6

BF = jnp.bfloat16
F32 = jnp.float32


def rope_tables(positions, width_rope):
    middle = width_rope // 2
    frequency = THETA_BASE ** (-(jnp.arange(middle) * 2).astype(jnp.float32) / width_rope)
    angles = positions.astype(jnp.float32)[:, None] * frequency[None, :]
    return (jnp.cos(angles), jnp.sin(angles))


def rotate(values, cosine, sine_part):
    middle = values.shape[-1] // 2
    first_half = values[..., :middle]
    second_half = values[..., middle:]
    return jnp.concatenate(
        [
            first_half * cosine - second_half * sine_part,
            second_half * cosine + first_half * sine_part,
        ],
        axis=-1,
    )


def unrotate(values, cosine, sine_part):
    middle = values.shape[-1] // 2
    first_half = values[..., :middle]
    second_half = values[..., middle:]
    return jnp.concatenate(
        [
            first_half * cosine + second_half * sine_part,
            second_half * cosine - first_half * sine_part,
        ],
        axis=-1,
    )


def norm_parts(values):
    inverse = lax.rsqrt(jnp.mean(values * values, axis=-1, keepdims=True) + EPSILON)
    return (values * inverse, inverse)


def norm_back(upstream, unit_rows, inverse, scaling):
    scaled = upstream * scaling
    gain_grad = jnp.sum(upstream * unit_rows, axis=0)
    input_grad = inverse * (
        scaled - unit_rows * jnp.mean(scaled * unit_rows, axis=-1, keepdims=True)
    )
    return (gain_grad, input_grad)


def silu_back(grad_hidden, gate_pre, up_pre):
    sigmoid = jax.nn.sigmoid(gate_pre)
    gate_grad = grad_hidden * up_pre * (sigmoid * (1.0 + gate_pre * (1.0 - sigmoid)))
    up_grad = grad_hidden * (gate_pre * sigmoid)
    return (gate_grad.astype(jnp.bfloat16), up_grad.astype(jnp.bfloat16))


def is_power(count):
    return count & (count - 1) == 0


def swap(values, axis_name, bit):
    count = lax.axis_size(axis_name)
    return lax.ppermute(values, axis_name, [(i, i ^ bit) for i in range(count)])


def tie(*values):
    return lax.optimization_barrier(values)


def column_gather(rows):
    return lax.all_gather(rows, "tp", axis=0, tiled=True)


def column_scatter(values):
    return lax.psum_scatter(values.astype(BF), "tp", scatter_dimension=0, tiled=True).astype(F32)


def dot_rows(left, right):
    return lax.dot_general(left, right, (((1,), (1,)), ((), ())), preferred_element_type=F32)


def dot_plain(left, right):
    return lax.dot_general(left, right, (((1,), (0,)), ((), ())), preferred_element_type=F32)


def dot_first(left, right):
    return lax.dot_general(left, right, (((0,), (0,)), ((), ())), preferred_element_type=F32)


def select_rows(slot_rows, experts, cap):
    row = lax.broadcasted_iota(jnp.int32, (experts * cap, HALF), 0).astype(F32)
    hit = row == slot_rows[0:1, :]
    for e in range(1, experts):
        hit = hit | (row == slot_rows[e : e + 1, :] + float(e * cap))
    return hit


def select_cols(slot_cols, experts, cap):
    lane = lax.broadcasted_iota(jnp.int32, (HALF, experts * cap), 1).astype(F32)
    hit = lane == slot_cols[:, 0:1]
    for e in range(1, experts):
        hit = hit | (lane == slot_cols[:, e : e + 1] + float(e * cap))
    return hit


def slot_weights(hit, weight_rows, experts, cap):
    pieces = []
    for e in range(experts):
        part = hit[e * cap : (e + 1) * cap, :]
        pieces.append(
            jnp.sum(jnp.where(part, weight_rows[e : e + 1, :], 0.0), axis=1, keepdims=True)
        )
    return jnp.concatenate(pieces, axis=0)


def expert_front_kernel(step, experts, cap, aliased, *refs):
    count = QUARTET
    x_in = refs[:count]
    where_ref, dy_in, gate_up_in, down_in, slot_row_ref, weight_row_ref, slot_col_ref = refs[
        count : count + 7
    ]
    base = count + 7 + aliased
    dx_out = refs[base : base + 2]
    x_all, d_all, hid_all, dgu_all = refs[base + 2 : base + 6]
    (xb, db, gate_up, down, xs, ds, dxs, dxo, hid, dgu, sem_in, sem_w, sem_out, sem_dx) = refs[
        base + 6 :
    ]
    width = xb.shape[2]
    pad = down.shape[1]
    tile = min(1024, width)
    x_copies = [pltpu.make_async_copy(x_in[q], xb.at[q], sem_in.at[q]) for q in range(count)]
    d_copies = [
        pltpu.make_async_copy(
            dy_in.at[pl.ds(pl.multiple_of(where_ref[q] * HALF, HALF), HALF)],
            db.at[q],
            sem_in.at[count + q],
        )
        for q in range(count)
    ]
    w_copies = [
        pltpu.make_async_copy(gate_up_in, gate_up, sem_w.at[0]),
        pltpu.make_async_copy(down_in, down, sem_w.at[1]),
    ]
    for q in range(count):
        x_copies[q].start()
        d_copies[q].start()
    for copy in w_copies:
        copy.start()
    for q in range(count):
        x_copies[q].wait()
        d_copies[q].wait()

        hit = select_rows(slot_row_ref[q], experts, cap)
        weights = slot_weights(hit, weight_row_ref[q], experts, cap)
        choose = jnp.where(hit, 1.0, 0.0).astype(BF)

        def spread(n, carry, q=q, choose=choose, weights=weights):
            cols = pl.ds(pl.multiple_of(n * tile, tile), tile)
            rows = dot_plain(choose, xb[q, :, cols])
            grads = dot_plain(choose, db[q, :, cols]) * weights
            for e in range(experts):
                xs[e, q * cap : (q + 1) * cap, cols] = rows[e * cap : (e + 1) * cap].astype(BF)
                ds[e, q * cap : (q + 1) * cap, cols] = grads[e * cap : (e + 1) * cap].astype(BF)
            return carry

        lax.fori_loop(0, width // tile, spread, 0)
    out_copies = [
        pltpu.make_async_copy(xs, x_all.at[step], sem_out.at[0]),
        pltpu.make_async_copy(ds, d_all.at[step], sem_out.at[1]),
        pltpu.make_async_copy(hid, hid_all.at[step], sem_out.at[2]),
        pltpu.make_async_copy(dgu, dgu_all.at[step], sem_out.at[3]),
    ]
    out_copies[0].start()
    out_copies[1].start()
    for copy in w_copies:
        copy.wait()

    def one_expert(e, carry):
        both = dot_rows(xs[e], gate_up[e])
        gate_pre, up_pre = both[:, :pad], both[:, pad:]
        d_hidden = dot_rows(ds[e], down[e])
        sigmoid = jax.nn.sigmoid(gate_pre)
        silu = gate_pre * sigmoid
        hid[e] = (silu * up_pre).astype(BF)
        gate_grad = d_hidden * up_pre * (sigmoid * (1.0 + gate_pre * (1.0 - sigmoid)))
        grads = jnp.concatenate([gate_grad, d_hidden * silu], axis=1).astype(BF)
        dgu[e] = grads

        def back(n, inner):
            cols = pl.ds(pl.multiple_of(n * tile, tile), tile)
            part = dot_plain(dgu[e], gate_up[e, :, cols]).astype(BF)
            for q in range(count):
                dxs[q, pl.ds(pl.multiple_of(e * cap, cap), cap), cols] = part[
                    q * cap : (q + 1) * cap
                ]
            return inner

        lax.fori_loop(0, width // tile, back, 0)
        return carry

    lax.fori_loop(0, experts, one_expert, 0)
    out_copies[2].start()
    out_copies[3].start()
    dx_copies = [
        pltpu.make_async_copy(dxo.at[q], dx_out[q // 2].at[q % 2], sem_dx.at[q])
        for q in range(count)
    ]
    for q in range(count):
        choose = jnp.where(select_cols(slot_col_ref[q], experts, cap), 1.0, 0.0).astype(BF)

        def gather(n, carry, q=q, choose=choose):
            cols = pl.ds(pl.multiple_of(n * tile, tile), tile)
            dxo[q, :, cols] = dot_plain(choose, dxs[q, :, cols]).astype(BF)
            return carry

        lax.fori_loop(0, width // tile, gather, 0)
        dx_copies[q].start()
    for copy in out_copies:
        copy.wait()
    for copy in dx_copies:
        copy.wait()


def expert_front(step, steps, x_parts, where, dy_all, gate_up, down, tables, kept, cap):
    experts, wide, width = gate_up.shape
    pad = wide // 2
    slots = QUARTET * cap
    slot_row, weight_row, slot_col = (t[step] for t in tables)
    any_spec = pl.BlockSpec(memory_space=pl.ANY)
    vmem_spec = pl.BlockSpec(memory_space=pltpu.VMEM)
    pair_shape = jax.ShapeDtypeStruct((2, HALF, width), BF)
    kept_shapes = [
        jax.ShapeDtypeStruct((steps, experts, slots, columns), BF)
        for columns in (width, width, pad, wide)
    ]
    results = pl.pallas_call(
        functools.partial(expert_front_kernel, step, experts, cap, len(kept)),
        out_shape=[pair_shape] * 2 + kept_shapes,
        in_specs=[any_spec] * QUARTET
        + [pl.BlockSpec(memory_space=pltpu.SMEM)]
        + [any_spec] * 3
        + [vmem_spec] * 3
        + [any_spec] * len(kept),
        out_specs=[any_spec] * 6,
        input_output_aliases={QUARTET + 7 + i: 2 + i for i in range(len(kept))},
        scratch_shapes=[
            pltpu.VMEM((QUARTET, HALF, width), BF),
            pltpu.VMEM((QUARTET, HALF, width), BF),
            pltpu.VMEM((experts, wide, width), BF),
            pltpu.VMEM((experts, pad, width), BF),
            pltpu.VMEM((experts, slots, width), BF),
            pltpu.VMEM((experts, slots, width), BF),
            pltpu.VMEM((QUARTET, experts * cap, width), BF),
            pltpu.VMEM((QUARTET, HALF, width), BF),
            pltpu.VMEM((experts, slots, pad), BF),
            pltpu.VMEM((experts, slots, wide), BF),
            pltpu.SemaphoreType.DMA((2 * QUARTET,)),
            pltpu.SemaphoreType.DMA((2,)),
            pltpu.SemaphoreType.DMA((4,)),
            pltpu.SemaphoreType.DMA((QUARTET,)),
        ],
        compiler_params=pltpu.CompilerParams(vmem_limit_bytes=62 * 1024 * 1024),
        cost_estimate=pl.CostEstimate(
            flops=2 * slots * experts * width * pad * 5
            + 6 * QUARTET * HALF * experts * cap * width,
            bytes_accessed=2 * width * (3 * QUARTET * HALF + experts * 3 * pad + 2 * experts * slots),
            transcendentals=slots * experts * pad,
        ),
        name="expert_front",
    )(*x_parts, where, dy_all, gate_up, down, slot_row, weight_row, slot_col, *kept)
    return list(results[:2]), list(results[2:])


def expert_out_kernel(experts, cap, hid, down, slot_row, weight_row, slot_col, near, far, parts):
    width = down.shape[2]
    tile = min(1024, width)
    weights = [
        slot_weights(
            select_rows(slot_row[0, q], experts, cap), weight_row[0, q], experts, cap
        )
        for q in range(QUARTET)
    ]
    for e in range(experts):

        def front(n, carry, e=e):
            cols = pl.ds(pl.multiple_of(n * tile, tile), tile)
            rows = dot_plain(hid[0, e], down[e, :, cols])
            for q in range(QUARTET):
                parts[q, e * cap : (e + 1) * cap, cols] = (
                    rows[q * cap : (q + 1) * cap] * weights[q][e * cap : (e + 1) * cap]
                ).astype(BF)
            return carry

        lax.fori_loop(0, width // tile, front, 0)
    for q in range(QUARTET):
        choose = jnp.where(select_cols(slot_col[0, q], experts, cap), 1.0, 0.0).astype(BF)
        out = (near, far)[q // 2]

        def gather(n, carry, q=q, choose=choose, out=out):
            cols = pl.ds(pl.multiple_of(n * tile, tile), tile)
            out[0, q % 2, :, cols] = dot_plain(choose, parts[q, :, cols]).astype(BF)
            return carry

        lax.fori_loop(0, width // tile, gather, 0)


def expert_out(hid_all, down, tables, cap):
    steps, experts, slots, pad = hid_all.shape
    width = down.shape[2]
    slot_row, weight_row, slot_col = tables
    return pl.pallas_call(
        functools.partial(expert_out_kernel, experts, cap),
        grid=(steps,),
        out_shape=[jax.ShapeDtypeStruct((steps, 2, HALF, width), BF)] * 2,
        in_specs=[
            pl.BlockSpec((1, experts, slots, pad), lambda i: (i, 0, 0, 0)),
            pl.BlockSpec((experts, pad, width), lambda i: (0, 0, 0)),
            pl.BlockSpec((1,) + slot_row.shape[1:], lambda i: (i, 0, 0, 0)),
            pl.BlockSpec((1,) + weight_row.shape[1:], lambda i: (i, 0, 0, 0)),
            pl.BlockSpec((1,) + slot_col.shape[1:], lambda i: (i, 0, 0, 0)),
        ],
        out_specs=[pl.BlockSpec((1, 2, HALF, width), lambda i: (i, 0, 0, 0))] * 2,
        scratch_shapes=[pltpu.VMEM((QUARTET, experts * cap, width), BF)],
        compiler_params=pltpu.CompilerParams(vmem_limit_bytes=48 * 1024 * 1024),
        cost_estimate=pl.CostEstimate(
            flops=steps * (2 * slots * experts * width * pad + 2 * QUARTET * HALF * experts * cap * width),
            bytes_accessed=2 * steps * QUARTET * HALF * width + 2 * hid_all.size + 2 * down.size,
            transcendentals=0,
        ),
        name="expert_out",
    )(hid_all, down, slot_row, weight_row, slot_col)


def expert_grads_kernel(dgu, x, hid, d, gate_grad, up_grad, down_grad):
    local = gate_grad.shape[1]
    pad = hid.shape[3]
    width = x.shape[3]
    tile = min(1024, width)

    @pl.when(pl.program_id(1) == 0)
    def _():
        gate_grad[...] = jnp.zeros_like(gate_grad)
        up_grad[...] = jnp.zeros_like(up_grad)
        down_grad[...] = jnp.zeros_like(down_grad)

    def part(n, carry):
        cols = pl.ds(pl.multiple_of(n * tile, tile), tile)
        gate_grad[0, :, cols] += dot_first(dgu[0, 0, :, :pad], x[0, 0, :, cols])[:local]
        up_grad[0, :, cols] += dot_first(dgu[0, 0, :, pad:], x[0, 0, :, cols])[:local]
        down_grad[0, :, cols] += dot_first(hid[0, 0], d[0, 0, :, cols])[:local]
        return carry

    lax.fori_loop(0, width // tile, part, 0)


def expert_grads(kept, local):
    x_all, d_all, hid_all, dgu_all = kept
    steps, experts, slots, width = x_all.shape
    pad = hid_all.shape[3]

    def block(array):
        return pl.BlockSpec((1, 1) + array.shape[2:], lambda e, i: (i, e, 0, 0))

    grad = jax.ShapeDtypeStruct((experts, local, width), F32)
    return pl.pallas_call(
        expert_grads_kernel,
        grid=(experts, steps),
        out_shape=[grad] * 3,
        in_specs=[block(dgu_all), block(x_all), block(hid_all), block(d_all)],
        out_specs=[pl.BlockSpec((1, local, width), lambda e, i: (e, 0, 0))] * 3,
        compiler_params=pltpu.CompilerParams(vmem_limit_bytes=48 * 1024 * 1024),
        cost_estimate=pl.CostEstimate(
            flops=2 * 3 * steps * experts * slots * width * pad,
            bytes_accessed=2 * (x_all.size + d_all.size + hid_all.size + dgu_all.size)
            + 12 * experts * local * width,
            transcendentals=0,
        ),
        name="expert_grads",
    )(dgu_all, x_all, hid_all, d_all)


def mesh_copy(src, dst, sends, arrivals, number, device):
    return pltpu.make_async_remote_copy(
        src_ref=src,
        dst_ref=dst,
        send_sem=sends.at[number],
        recv_sem=arrivals.at[number],
        device_id=device,
        device_id_type=pl.DeviceIdType.MESH,
    )


def plane_neighbours():
    place, column = lax.axis_index("fsdp"), lax.axis_index("tp")
    core, along, across = place % 2, (place // 2) % 2, place // 4
    return (
        (place + 1 - 2 * core, column),
        (place + 2 - 4 * along, column),
        (place + 4 - 8 * across, column),
    )


def column_neighbours(count):
    place, column = lax.axis_index("fsdp"), lax.axis_index("tp")
    return [(place, (column + s) % count) for s in range(1, count)]


def greet(devices):
    barrier = pltpu.get_barrier_semaphore()
    for device in devices:
        pl.semaphore_signal(
            barrier, inc=1, device_id=device, device_id_type=pl.DeviceIdType.MESH
        )
    pl.semaphore_wait(barrier, len(devices))


class ColumnGather:
    def __init__(self, blocks, rows_of, sends, arrivals, base, own=None):
        self.blocks, self.rows_of = blocks, rows_of
        self.own = blocks.at[rows_of(0)] if own is None else own
        self.sends, self.arrivals, self.base = sends, arrivals, base
        self.row = lax.axis_index("tp")
        self.column = column_neighbours(4)

    def direct(self, s):
        place = self.blocks.at[self.rows_of(0)]
        return mesh_copy(
            self.own, place, self.sends, self.arrivals, self.base + s - 1, self.column[s - 1]
        )

    def start(self):
        @pl.when(self.row < 3)
        def _():
            self.direct(1).start()

        @pl.when(self.row > 0)
        def _():
            self.direct(3).start()

        self.direct(2).start()

    def wait(self, b):
        self.direct(4 - b).wait_recv()
        if b == 2:

            @pl.when(self.row == 1)
            def _():
                self.relay(3).start()

            @pl.when(self.row == 2)
            def _():
                self.relay(1).start()

    def relay(self, s):
        place = self.blocks.at[self.rows_of(2)]
        return pltpu.make_async_remote_copy(
            src_ref=place,
            dst_ref=place,
            send_sem=self.sends.at[self.base + 3],
            recv_sem=self.arrivals.at[self.base + 3 - s],
            device_id=self.column[s - 1],
            device_id_type=pl.DeviceIdType.MESH,
        )

    def drain(self):
        @pl.when(self.row < 3)
        def _():
            self.direct(1).wait_send()

        @pl.when(self.row > 0)
        def _():
            self.direct(3).wait_send()

        self.direct(2).wait_send()

        @pl.when(self.row == 1)
        def _():
            self.relay(3).wait_send()

        @pl.when(self.row == 2)
        def _():
            self.relay(1).wait_send()


class ColumnSum:
    def __init__(self, parts, rows_of, landed, relayed, sends, arrivals, base):
        self.parts, self.rows_of, self.landed, self.relayed = parts, rows_of, landed, relayed
        self.sends, self.arrivals, self.base = sends, arrivals, base
        self.row = lax.axis_index("tp")
        self.column = column_neighbours(4)

    def direct(self, s):
        return mesh_copy(
            self.parts.at[self.rows_of(s)],
            self.landed.at[s - 1],
            self.sends,
            self.arrivals,
            self.base + s - 1,
            self.column[s - 1],
        )

    def first_leg(self, s):
        return mesh_copy(
            self.parts.at[self.rows_of(4 - s)],
            self.relayed.at[0],
            self.sends,
            self.arrivals,
            self.base + 3,
            self.column[s - 1],
        )

    def own_part(self, local):
        return pltpu.make_async_copy(self.parts.at[self.rows_of(2)], self.relayed.at[1], local)

    def second_leg(self):
        return mesh_copy(
            self.relayed.at[1],
            self.landed.at[1],
            self.sends,
            self.arrivals,
            self.base + 1,
            self.column[1],
        )

    def start(self, local):
        @pl.when(self.row == 0)
        def _():
            self.first_leg(1).start()

        @pl.when(self.row == 3)
        def _():
            self.first_leg(3).start()

        @pl.when((self.row == 1) | (self.row == 2))
        def _():
            self.own_part(local).start()

        @pl.when(self.row < 3)
        def _():
            self.direct(1).start()

        @pl.when(self.row > 0)
        def _():
            self.direct(3).start()

        @pl.when((self.row == 0) | (self.row == 3))
        def _():
            self.direct(2).start()

    def middle(self, local):
        @pl.when((self.row == 1) | (self.row == 2))
        def _():
            self.own_part(local).wait()
            self.first_leg(1).wait_recv()

            def some(i, carry):
                rows = pl.ds(pl.multiple_of(i * 32, 32), 32)
                self.relayed[1, rows, :] = (
                    self.relayed[0, rows, :].astype(F32) + self.relayed[1, rows, :].astype(F32)
                ).astype(BF)
                return carry

            lax.fori_loop(0, self.relayed.shape[1] // 32, some, 0)
            self.second_leg().start()

    def clear(self):
        @pl.when(self.row == 0)
        def _():
            self.landed[0] = jnp.zeros(self.landed.shape[1:], BF)

        @pl.when(self.row == 3)
        def _():
            self.landed[2] = jnp.zeros(self.landed.shape[1:], BF)

    def total(self, own):
        @pl.when(self.row > 0)
        def _():
            self.direct(1).wait_recv()

        @pl.when(self.row < 3)
        def _():
            self.direct(3).wait_recv()

        self.direct(2).wait_recv()
        total = own.astype(F32)
        for s in range(3):
            total = total + self.landed[s].astype(F32)
        return total

    def drain(self):
        @pl.when(self.row == 0)
        def _():
            self.first_leg(1).wait_send()

        @pl.when(self.row == 3)
        def _():
            self.first_leg(3).wait_send()

        @pl.when(self.row < 3)
        def _():
            self.direct(1).wait_send()

        @pl.when(self.row > 0)
        def _():
            self.direct(3).wait_send()

        self.direct(2).wait_send()


class PlaneGather:
    def __init__(self, own, others, rows_of, sends, arrivals, base):
        self.own, self.others, self.rows_of = own, others, rows_of
        self.sends, self.arrivals, self.base = sends, arrivals, base
        self.partner, self.along, self.across = plane_neighbours()

    def copies(self, b):
        half = self.own.shape[1] // 2
        rows = self.rows_of(b)
        left, right = pl.ds(0, half), pl.ds(half, half)
        other = {r: self.others.at[r - 1] for r in range(1, 8)}
        plan = [
            (self.own.at[rows], other[2].at[rows], self.along),
            (self.own.at[rows], other[4].at[rows], self.across),
            (self.own.at[rows], other[1].at[rows], self.partner),
            (other[2].at[rows, left], other[6].at[rows, left], self.across),
            (other[4].at[rows, right], other[6].at[rows, right], self.along),
            (other[2].at[rows], other[3].at[rows], self.partner),
            (other[4].at[rows], other[5].at[rows], self.partner),
            (other[6].at[rows], other[7].at[rows], self.partner),
        ]
        return [
            mesh_copy(src, dst, self.sends, self.arrivals, self.base + 8 * b + i, device)
            for i, (src, dst, device) in enumerate(plan)
        ]

    def start(self, b):
        for copy in self.copies(b)[:3]:
            copy.start()

    def forward(self, b):
        along, across, _, left, right, third, fifth, _ = self.copies(b)
        along.wait_recv()
        left.start()
        third.start()
        across.wait_recv()
        right.start()
        fifth.start()

    def last(self, b):
        copies = self.copies(b)
        copies[3].wait_recv()
        copies[4].wait_recv()
        copies[7].start()

    def arrived(self, b, numbers):
        copies = self.copies(b)
        for i in numbers:
            copies[i].wait_recv()

    def drain(self, b):
        for copy in self.copies(b):
            copy.wait_send()


def block_rows(columns, size):
    row = lax.axis_index("tp")
    return lambda s: pl.ds(pl.multiple_of((row + s) % columns * size, size), size)


def slots_of(table, experts, columns, size, b, q):
    place = pl.ds(pl.multiple_of((lax.axis_index("tp") + b) % columns * size, size), size)
    rows = []
    for e in range(experts):
        low, high = 2 * q * experts + e, (2 * q + 1) * experts + e
        rows.append(
            jnp.concatenate([table[low : low + 1, place], table[high : high + 1, place]], axis=1)
        )
    return jnp.concatenate(rows, axis=0)


def token_sums(table, experts, columns, size, wide, b, slots, keep):
    width = slots.shape[2]
    tile = min(1024, width)
    for q in range(QUARTET):
        entries = slots_of(table, experts, columns, size, b, q)
        entries = jnp.concatenate(
            [entries, jnp.full((8 - experts, HALF), NO_SLOT, F32)], axis=0
        )
        choose = jnp.where(select_cols(entries.T, experts, wide), 1.0, 0.0).astype(BF)

        def gather(n, carry, q=q, choose=choose):
            cols = pl.ds(pl.multiple_of(n * tile, tile), tile)
            keep(q, cols, dot_plain(choose, slots[q, :, cols]).astype(BF))
            return carry

        lax.fori_loop(0, width // tile, gather, 0)


def expert_kernel(cap, columns, size, *refs):
    (
        attn_in,
        tokens_in,
        cotan_in,
        gate_in,
        up_in,
        down_in,
        gain_ref,
        raw_ref,
        mixed_out,
        ffn_all,
        dx_out,
        slots_out,
        weights_out,
        x_all,
        d_all,
        hid_all,
        dgu_all,
        x_others,
        dy_others,
        theirs,
        links,
        attn_v,
        tokens_v,
        arrived_v,
        relayed_v,
        mixed_v,
        ffn_v,
        xb,
        db,
        gate_up,
        down,
        xs,
        ds,
        dxs,
        others,
        chip,
        stage,
        hid,
        dgu,
        d_hidden,
        slot_table,
        weight_table,
        sends,
        arrivals,
        local,
        loads,
        sum_local,
        spill,
    ) = refs
    count = QUARTET
    previous = {2: 0, 1: 2, 3: 1}
    experts, local_hidden = gate_in.shape[:2]
    width = xb.shape[2]
    pad = down.shape[1]
    tile = min(1024, width)
    wide = 2 * cap
    rows_of = block_rows(columns, size)
    partner, along, across = plane_neighbours()
    column = column_neighbours(columns)
    number = 0

    def reserve(amount):
        nonlocal number
        number += amount
        return number - amount

    x_gather = PlaneGather(ffn_all, x_others, rows_of, sends, arrivals, reserve(8 * columns))
    dy_gather = PlaneGather(cotan_in, dy_others, rows_of, sends, arrivals, reserve(8 * columns))
    gather = ColumnGather(ffn_all, rows_of, sends, arrivals, reserve(4))
    summed = ColumnSum(attn_in, rows_of, arrived_v, relayed_v, sends, arrivals, reserve(4))
    plane = PlaneSum(
        lambda r, h: others.at[r // 2],
        chip,
        theirs,
        links,
        stage,
        sends,
        arrivals,
        reserve(plane_sum_sizes(columns)[0]),
        sum_local,
    )

    greet([partner, along, across] + column)
    summed.start(local.at[2])
    first = [
        pltpu.make_async_copy(attn_in.at[rows_of(0)], attn_v, local.at[0]),
        pltpu.make_async_copy(tokens_in, tokens_v, local.at[1]),
    ]
    for copy in first:
        copy.start()
    for b in (0, 2, 1):
        dy_gather.start(b)
    if pad > local_hidden:
        rest = pad - local_hidden
        for e in range(experts):
            for ref, start in ((gate_up, local_hidden), (gate_up, pad + local_hidden), (down, local_hidden)):
                ref[e, start : start + rest, :] = jnp.zeros((rest, width), BF)
    weights_in = []
    for e in range(experts):
        weights_in += [
            pltpu.make_async_copy(
                gate_in.at[e], gate_up.at[e, pl.ds(0, local_hidden)], local.at[3 + 3 * e]
            ),
            pltpu.make_async_copy(
                up_in.at[e], gate_up.at[e, pl.ds(pad, local_hidden)], local.at[4 + 3 * e]
            ),
            pltpu.make_async_copy(
                down_in.at[e], down.at[e, pl.ds(0, local_hidden)], local.at[5 + 3 * e]
            ),
        ]
    for copy in weights_in:
        copy.start()

    summed.clear()
    summed.middle(local.at[2])

    earlier = lax.broadcasted_iota(jnp.int32, (size, size), 0)
    later = lax.broadcasted_iota(jnp.int32, (size, size), 1)
    before = jnp.where(earlier < later, 1.0, 0.0).astype(BF)
    own_first = (lax.axis_index("fsdp") * experts).astype(F32)
    for r in range(8):
        for e in range(experts):
            member = jnp.zeros((1, SEQ), F32)
            weight = jnp.zeros((1, SEQ), F32)
            for pick in range(TOPK):
                same = raw_ref[r, pick : pick + 1, :] == own_first + float(e)
                member = jnp.where(same, 1.0, member)
                weight = weight + jnp.where(
                    same, raw_ref[r, RAW_ROWS + pick : RAW_ROWS + pick + 1, :], 0.0
                )
            slot_table[r * experts + e : r * experts + e + 1, :] = member
            weight_table[r * experts + e : r * experts + e + 1, :] = weight
    second = lax.broadcasted_iota(jnp.int32, (8 * experts, size), 0) // experts % 2
    shift = second.astype(F32) * float(cap)
    for b in range(columns):
        cols = pl.ds(b * size, size)
        member = slot_table[:, cols]
        rank = dot_plain(member.astype(BF), before)
        slot_table[:, cols] = jnp.where(member > 0.5, rank + shift, NO_SLOT)
    slots_out[...] = slot_table[...]
    weights_out[...] = weight_table[...]

    def enter(b):
        if b > 0:
            gather.wait(b)
        x_gather.start(b)

    def ready(b):
        x_gather.last(b)
        x_gather.arrived(b, [2, 5, 6, 7])

    def source(own, gathered, r):
        return own if r == 0 else gathered.at[r - 1]

    def load(b, k):
        own, gathered, target = ((ffn_all, x_others, xb), (cotan_in, dy_others, db))[k]
        return [
            pltpu.make_async_copy(
                source(own, gathered, r).at[rows_of(b)],
                target.at[r // 2, pl.ds(r % 2 * size, size)],
                loads.at[8 * k + r],
            )
            for r in range(8)
        ]

    def combine(b, keep):
        token_sums(slot_table, experts, columns, size, wide, b, dxs, keep)

    def spills(b):
        return [
            pltpu.make_async_copy(xs, x_all.at[b], spill.at[0]),
            pltpu.make_async_copy(hid.at[b], hid_all.at[b], spill.at[1]),
            pltpu.make_async_copy(dgu, dgu_all.at[b], spill.at[2]),
        ]

    def d_spill(b):
        return pltpu.make_async_copy(ds, d_all.at[b], spill.at[3])

    def choice(b, q):
        return select_rows(
            slots_of(slot_table, experts, columns, size, b, q), experts, wide
        )

    def spread(q, source_rows, target, weights, hit):
        choose = jnp.where(hit, 1.0, 0.0).astype(BF)

        def one(n, carry):
            cols = pl.ds(pl.multiple_of(n * tile, tile), tile)
            rows = dot_plain(choose, source_rows[q, :, cols])
            if weights is not None:
                rows = rows * weights
            for e in range(experts):
                target[e, q * wide : (q + 1) * wide, cols] = rows[
                    e * wide : (e + 1) * wide
                ].astype(BF)
            return carry

        lax.fori_loop(0, width // tile, one, 0)

    def back(b):
        dy_gather.last(b)
        dy_gather.arrived(b, [2, 5, 6, 7])
        copies = load(b, 1)
        for copy in copies:
            copy.start()
        if b == 0:
            for copy in weights_in:
                copy.wait()
        else:
            d_spill(previous[b]).wait()
        for q in range(count):
            for copy in copies[2 * q : 2 * q + 2]:
                copy.wait()
            hit = choice(b, q)
            spread(
                q,
                db,
                ds,
                slot_weights(
                    hit, slots_of(weight_table, experts, columns, size, b, q), experts, wide
                ),
                hit,
            )
        d_spill(b).start()

        def one_expert(e, carry):
            d_hidden[b, e] = dot_rows(ds[e], down[e])
            return carry

        lax.fori_loop(0, experts, one_expert, 0)

    def front(b):
        copies = load(b, 0)
        for copy in copies:
            copy.start()
        if b > 0:
            for copy in spills(previous[b]):
                copy.wait()
        for q in range(count):
            for copy in copies[2 * q : 2 * q + 2]:
                copy.wait()
            spread(q, xb, xs, None, choice(b, q))
        out_copies = spills(b)
        out_copies[0].start()

        def one_expert(e, carry):
            both = dot_rows(xs[e], gate_up[e])
            gate_pre, up_pre = both[:, :pad], both[:, pad:]
            d_hid = d_hidden[b, e]
            sigmoid = jax.nn.sigmoid(gate_pre)
            silu = gate_pre * sigmoid
            hid[b, e] = (silu * up_pre).astype(BF)
            gate_grad = d_hid * up_pre * (sigmoid * (1.0 + gate_pre * (1.0 - sigmoid)))
            dgu[e] = jnp.concatenate([gate_grad, d_hid * silu], axis=1).astype(BF)

            def inward(n, inner):
                cols = pl.ds(pl.multiple_of(n * tile, tile), tile)
                part = dot_plain(dgu[e], gate_up[e, :, cols]).astype(BF)
                for q in range(count):
                    dxs[q, pl.ds(pl.multiple_of(e * wide, wide), wide), cols] = part[
                        q * wide : (q + 1) * wide
                    ]
                return inner

            lax.fori_loop(0, width // tile, inward, 0)
            return carry

        lax.fori_loop(0, experts, one_expert, 0)
        out_copies[1].start()
        out_copies[2].start()
        if b > 0:
            for i in range(4):
                plane.pair(i, previous[b]).wait_send()

        def keep(q, cols, value):
            chip[q, b, :, cols] = value[:size]
            others[q, :, cols] = value[size:]

        combine(b, keep)
        for i in range(4):
            plane.pair(i, b).start()

    dy_gather.forward(0)
    dy_gather.forward(2)
    back(0)

    for copy in first:
        copy.wait()
    total = summed.total(attn_v[...]) + tokens_v[...].astype(F32)
    mixed_v[...] = total
    inverse = lax.rsqrt(jnp.mean(total * total, axis=1, keepdims=True) + EPSILON)
    ffn_v[...] = (total * inverse * gain_ref[...]).astype(BF)
    own_copy = pltpu.make_async_copy(ffn_v, ffn_all.at[rows_of(0)], local.at[0])
    own_copy.start()
    mixed_copy = pltpu.make_async_copy(mixed_v, mixed_out, local.at[1])
    mixed_copy.start()
    own_copy.wait()

    gather.start()
    enter(0)
    back(2)
    x_gather.forward(0)
    enter(2)
    enter(1)
    x_gather.forward(2)
    dy_gather.forward(1)
    dy_gather.start(3)
    ready(0)
    front(0)
    enter(3)
    x_gather.forward(1)
    ready(2)
    front(2)
    x_gather.forward(3)
    dy_gather.forward(3)
    plane.send_first([0], False)
    back(1)
    ready(1)
    front(1)
    back(3)
    plane.send_first([2], False)
    plane.send_second([0])
    ready(3)
    front(3)
    plane.send_first([1], False)
    plane.send_second([2])
    done = {}

    def close(b):
        plane.finish([b])
        done[b] = pltpu.make_async_copy(chip.at[0, b], dx_out.at[rows_of(b)], loads.at[b])
        done[b].start()

    plane.send_first([3], False)
    close(0)
    plane.send_second([1])
    close(2)
    plane.send_second([3])
    close(1)
    close(3)
    for copy in spills(3) + [d_spill(3)]:
        copy.wait()
    for b in range(columns):
        done[b].wait()
    mixed_copy.wait()

    for b in range(columns):
        x_gather.drain(b)
        dy_gather.drain(b)
    gather.drain()
    summed.drain()
    plane.drain(3)


def expert_call(attn_part, tokens, cotan_all, gate, up, down, gain, raw, cap):
    columns = lax.axis_size("tp")
    size, width = tokens.shape
    experts, local_hidden, _ = gate.shape
    pad = -(-local_hidden // 128) * 128
    slots = 8 * cap
    anywhere = pl.BlockSpec(memory_space=pl.ANY)
    held = pl.BlockSpec(memory_space=pltpu.VMEM)

    def array(*dims, kind=BF):
        return jax.ShapeDtypeStruct(dims, kind)

    landing, scratch = plane_sum_space(columns, size, width)
    remote, near = plane_sum_sizes(columns)
    remote = remote + 16 * columns + 8
    results = pl.pallas_call(
        functools.partial(expert_kernel, cap, columns, size),
        out_shape=[
            array(size, width, kind=F32),
            array(SEQ, width),
            array(SEQ, width),
            array(8 * experts, SEQ, kind=F32),
            array(8 * experts, SEQ, kind=F32),
            array(columns, experts, slots, width),
            array(columns, experts, slots, width),
            array(columns, experts, slots, pad),
            array(columns, experts, slots, 2 * pad),
            array(7, SEQ, width),
            array(7, SEQ, width),
        ]
        + landing,
        in_specs=[anywhere] * 6 + [held] * 2,
        out_specs=[anywhere] * 3 + [held] * 2 + [anywhere] * 8,
        scratch_shapes=[
            pltpu.VMEM((size, width), BF),
            pltpu.VMEM((size, width), BF),
            pltpu.VMEM((columns - 1, size, width), BF),
            pltpu.VMEM((2, size, width), BF),
            pltpu.VMEM((size, width), F32),
            pltpu.VMEM((size, width), BF),
            pltpu.VMEM((QUARTET, HALF, width), BF),
            pltpu.VMEM((QUARTET, HALF, width), BF),
            pltpu.VMEM((experts, 2 * pad, width), BF),
            pltpu.VMEM((experts, pad, width), BF),
            pltpu.VMEM((experts, slots, width), BF),
            pltpu.VMEM((experts, slots, width), BF),
            pltpu.VMEM((QUARTET, 2 * experts * cap, width), BF),
            pltpu.VMEM((4, size, width), BF),
        ]
        + scratch
        + [
            pltpu.VMEM((columns, experts, slots, pad), BF),
            pltpu.VMEM((experts, slots, 2 * pad), BF),
            pltpu.VMEM((columns, experts, slots, pad), F32),
            pltpu.VMEM((8 * experts, SEQ), F32),
            pltpu.VMEM((8 * experts, SEQ), F32),
            pltpu.SemaphoreType.DMA((remote,)),
            pltpu.SemaphoreType.DMA((remote,)),
            pltpu.SemaphoreType.DMA((3 + 3 * experts,)),
            pltpu.SemaphoreType.DMA((16,)),
            pltpu.SemaphoreType.DMA((near,)),
            pltpu.SemaphoreType.DMA((4,)),
        ],
        compiler_params=pltpu.CompilerParams(
            collective_id=1, has_side_effects=True, vmem_limit_bytes=67_043_328
        ),
        cost_estimate=pl.CostEstimate(
            flops=16 * SEQ * experts * cap * width * 8,
            bytes_accessed=800 * SEQ * width,
            transcendentals=0,
        ),
        name="experts",
    )(attn_part, tokens, cotan_all, gate, up, down, gain, raw)
    return results[:9]


def first_kernel(columns, size, kinds, *refs):
    amount = len(kinds)
    rows_in, own_in = refs[:2], refs[2 : 2 + amount]
    rows_all, alls = refs[2 + amount : 4 + amount], refs[4 + amount : 4 + 2 * amount]
    rows_v, held = refs[4 + 2 * amount : 6 + 2 * amount], refs[6 + 2 * amount : 6 + 3 * amount]
    sends, arrivals, local = refs[6 + 3 * amount :]
    partner, along, across = plane_neighbours()
    column = column_neighbours(columns)
    rows_of = block_rows(columns, size)
    place = lax.axis_index("fsdp")
    devices = {
        0: place,
        1: partner[0],
        2: along[0],
        4: across[0],
        6: along[0] + across[0] - place,
    }
    greet([partner, along, across] + column)
    gathers = [
        ColumnGather(rows_all[n], rows_of, sends, arrivals, 8 * amount + 4 * n, rows_in[n])
        for n in range(2)
    ]
    for gather in gathers:
        gather.start()
    plans = []
    for k, kind in enumerate(kinds):
        own, everything = own_in[k], alls[k]
        rows, cols = own.shape
        top, bottom = pl.ds(0, rows // 2), pl.ds(rows // 2, rows // 2)
        whole = pl.ds(0, rows)

        def spot(r, hop, part, kind=kind, everything=everything, cols=cols):
            if kind == "relative":
                return everything.at[r ^ hop, part]
            if kind == "rows":
                return everything.at[devices[r], part]
            start = pl.multiple_of(devices[r] * cols, cols)
            return everything.at[part, pl.ds(start, cols)]

        plan = [
            (own, spot(0, 2, whole), along),
            (own, spot(0, 4, whole), across),
            (own, spot(0, 1, whole), partner),
            (spot(2, 0, top), spot(2, 4, top), across),
            (spot(4, 0, bottom), spot(4, 2, bottom), along),
            (spot(2, 0, whole), spot(2, 1, whole), partner),
            (spot(4, 0, whole), spot(4, 1, whole), partner),
            (spot(6, 0, whole), spot(6, 1, whole), partner),
        ]
        plans.append(
            [
                mesh_copy(src, dst, sends, arrivals, 8 * k + i, device)
                for i, (src, dst, device) in enumerate(plan)
            ]
        )
    for copies in plans:
        for copy in copies[:3]:
            copy.start()
    here = [pltpu.make_async_copy(rows_in[n], rows_v[n], local.at[n]) for n in range(2)]
    there = [
        pltpu.make_async_copy(rows_v[n], rows_all[n].at[rows_of(0)], local.at[n]) for n in range(2)
    ]
    for k, kind in enumerate(kinds):
        rows, cols = own_in[k].shape
        if kind == "relative":
            spot_here = alls[k].at[0]
        elif kind == "rows":
            spot_here = alls[k].at[place]
        else:
            spot_here = alls[k].at[:, pl.ds(pl.multiple_of(place * cols, cols), cols)]
        here.append(pltpu.make_async_copy(own_in[k], held[k], local.at[2 + k]))
        there.append(pltpu.make_async_copy(held[k], spot_here, local.at[2 + k]))
    for copy in here:
        copy.start()
    for copy in here:
        copy.wait()
    for copy in there:
        copy.start()
    for n, copies in enumerate(plans):
        copies[0].wait_recv()
        copies[3].start()
        copies[5].start()
        copies[1].wait_recv()
        copies[4].start()
        copies[6].start()
        if n == amount - 3:
            gathers[0].wait(2)
    for copies in plans:
        copies[3].wait_recv()
        copies[4].wait_recv()
        copies[7].start()
    for copies in plans:
        for i in (2, 5, 6, 7):
            copies[i].wait_recv()
    gathers[1].wait(2)
    for gather in gathers:
        gather.wait(1)
        gather.wait(3)
    for copy in there:
        copy.wait()
    for gather in gathers:
        gather.drain()
    for copies in plans:
        for copy in copies:
            copy.wait_send()


def first_call(tokens, cotan, owns, kinds):
    columns = lax.axis_size("tp")
    size, width = tokens.shape
    anywhere = pl.BlockSpec(memory_space=pl.ANY)
    copies = 8 * len(owns) + 8

    def gathered(own, kind):
        rows, cols = own.shape
        return (rows, 8 * cols) if kind == "columns" else (8, rows, cols)

    return pl.pallas_call(
        functools.partial(first_kernel, columns, size, kinds),
        out_shape=[jax.ShapeDtypeStruct((columns * size, width), BF)] * 2
        + [jax.ShapeDtypeStruct(gathered(own, kind), own.dtype) for own, kind in zip(owns, kinds)],
        in_specs=[anywhere] * (2 + len(owns)),
        out_specs=[anywhere] * (2 + len(owns)),
        scratch_shapes=[pltpu.VMEM((size, width), BF)] * 2
        + [pltpu.VMEM(own.shape, own.dtype) for own in owns]
        + [
            pltpu.SemaphoreType.DMA((copies,)),
            pltpu.SemaphoreType.DMA((copies,)),
            pltpu.SemaphoreType.DMA((2 + len(owns),)),
        ],
        compiler_params=pltpu.CompilerParams(collective_id=2, has_side_effects=True),
        cost_estimate=pl.CostEstimate(
            flops=0, bytes_accessed=240 * SEQ * width, transcendentals=0
        ),
        name="first_gather",
    )(tokens, cotan, *owns)


class PlaneSum:
    def __init__(self, source, chip, theirs, links, stage, sends, arrivals, base, local):
        self.source, self.chip, self.theirs, self.links = source, chip, theirs, links
        self.stage, self.sends, self.arrivals, self.base = stage, sends, arrivals, base
        self.local = local
        self.parts, self.rows = chip.shape[1], chip.shape[2]
        self.partner, self.along, self.across = plane_neighbours()

    def pair(self, i, h):
        return mesh_copy(
            self.source(2 * i + 1, h),
            self.theirs.at[i, h],
            self.sends,
            self.arrivals,
            self.base + i * self.parts + h,
            self.partner,
        )

    def mine(self, i, h):
        return pltpu.make_async_copy(
            self.source(2 * i, h), self.chip.at[i, h], self.local.at[4 + i * self.parts + h]
        )

    def begin(self):
        for i in (3, 1, 2, 0):
            for h in range(self.parts):
                self.pair(i, h).start()
                self.mine(i, h).start()

    def fetch(self, landed, slot):
        size = landed.shape[0]
        return pltpu.make_async_copy(
            landed, self.stage.at[slot, pl.ds(0, size)], self.local.at[slot]
        )

    def add(self, i, h, start, size, slot):
        some = min(32, size)

        def one(n, carry):
            rows = pl.ds(pl.multiple_of(start + n * some, some), some)
            from_rows = pl.ds(pl.multiple_of(n * some, some), some)
            self.chip[i, h, rows, :] = (
                self.chip[i, h, rows, :].astype(F32) + self.stage[slot, from_rows, :].astype(F32)
            ).astype(BF)
            return carry

        lax.fori_loop(0, size // some, one, 0)

    def send_first(self, parts=None, fetched=True):
        for h in range(self.parts) if parts is None else parts:
            for i in (3, 1, 2, 0):
                self.pair(i, h).wait_recv()
                self.fetch(self.theirs.at[i, h], i).start()
            for i in (3, 1, 2, 0):
                if fetched:
                    self.mine(i, h).wait()
                self.fetch(self.theirs.at[i, h], i).wait()
                self.add(i, h, 0, self.rows, i)
                if i == 3:
                    self.send(1, [h])
                if i == 2:
                    self.send(0, [h])

    def link(self, stage_number, side, h):
        first_hop, second_hop = (
            (self.along, self.across) if side == 0 else (self.across, self.along)
        )
        near, far = (1, 2) if side == 0 else (2, 1)
        i = (near, 3, far)[stage_number]
        place = (stage_number * 2 + side) * self.parts + h
        rows = pl.ds(side * (self.rows // 2), self.rows // 2)
        return mesh_copy(
            self.chip.at[i, h, rows],
            self.links.at[place],
            self.sends,
            self.arrivals,
            self.base + 4 * self.parts + place,
            second_hop if stage_number == 2 else first_hop,
        )

    def landed(self, stage_number, side, h):
        return self.links.at[(stage_number * 2 + side) * self.parts + h]

    def send(self, stage_number, parts=None):
        for h in range(self.parts) if parts is None else parts:
            for side in range(2):
                self.link(stage_number, side, h).start()

    def send_second(self, parts=None):
        half = self.rows // 2
        for h in range(self.parts) if parts is None else parts:
            for side in range(2):
                self.link(1, side, h).wait_recv()
                self.fetch(self.landed(1, side, h), side).start()
            for side in range(2):
                self.fetch(self.landed(1, side, h), side).wait()
                self.add((2, 1)[side], h, side * half, half, side)
                self.link(2, side, h).start()

    def finish(self, parts=None):
        half = self.rows // 2
        for h in range(self.parts) if parts is None else parts:
            for stage_number in (0, 2):
                for side in range(2):
                    self.link(stage_number, side, h).wait_recv()
                    self.fetch(self.landed(stage_number, side, h), stage_number + side).start()
            for stage_number in (0, 2):
                for side in range(2):
                    slot = stage_number + side
                    self.fetch(self.landed(stage_number, side, h), slot).wait()
                    self.add(0, h, side * half, half, slot)

    def drain(self, first_part=0):
        for h in range(self.parts):
            for i in range(4):
                if h >= first_part:
                    self.pair(i, h).wait_send()
            for stage_number in range(3):
                for side in range(2):
                    self.link(stage_number, side, h).wait_send()


def plane_sum_sizes(parts):
    return 10 * parts, 4 + 4 * parts


def plane_sum_space(parts, rows, width):
    landing = [
        jax.ShapeDtypeStruct((4, parts, rows, width), BF),
        jax.ShapeDtypeStruct((6 * parts, rows // 2, width), BF),
    ]
    scratch = [pltpu.VMEM((4, parts, rows, width), BF), pltpu.VMEM((4, rows, width), BF)]
    return landing, scratch


def middle_kernel(cap, columns, size, experts, steps, local_hidden, *refs):
    (
        d_ffn_in,
        mixed_in,
        cotan_in,
        gain_ref,
        slot_table,
        weight_table,
        down_in,
        x_all,
        d_all,
        hid_all,
        dgu_all,
        d_mixed_out,
        d_proj_all,
        gain_out,
        routed_out,
        gate_grad,
        up_grad,
        down_grad,
        theirs,
        links,
        chip,
        stage,
        own_v,
        arrived_v,
        relayed_v,
        mixed_v,
        cotan_v,
        proj_v,
        xk,
        dk,
        hk,
        gk,
        totals,
        hid,
        down,
        parts,
        others,
        sends,
        arrivals,
        local,
        sum_local,
        work,
        written,
    ) = refs
    partner, along, across = plane_neighbours()
    column = column_neighbours(columns)
    greet([partner, along, across] + column)
    plane = PlaneSum(
        lambda r, h: others.at[h % 2, r // 2],
        chip,
        theirs,
        links,
        stage,
        sends,
        arrivals,
        0,
        sum_local,
    )
    base = plane_sum_sizes(columns)[0]
    rows_of = block_rows(columns, size)
    summed = ColumnSum(d_ffn_in, rows_of, arrived_v, relayed_v, sends, arrivals, base)
    gather = ColumnGather(d_proj_all, rows_of, sends, arrivals, base + 4)
    summed.start(local.at[3])
    first = [
        pltpu.make_async_copy(d_ffn_in.at[rows_of(0)], own_v, local.at[0]),
        pltpu.make_async_copy(mixed_in, mixed_v, local.at[1]),
        pltpu.make_async_copy(cotan_in, cotan_v, local.at[2]),
    ]
    for copy in first:
        copy.start()
    width = xk.shape[2]
    pad = hk.shape[2]
    tile = min(1024, width)
    hidden_in = [pltpu.make_async_copy(hid_all.at[b], hid.at[b], local.at[4 + b]) for b in range(columns)]
    down_copies = [
        pltpu.make_async_copy(
            down_in.at[e], down.at[e, pl.ds(0, local_hidden)], local.at[4 + columns + e]
        )
        for e in range(experts)
    ]
    for copy in down_copies + hidden_in:
        copy.start()
    summed.clear()
    rest = down.shape[1] - local_hidden
    if rest > 0:
        for e in range(experts):
            down[e, local_hidden:, :] = jnp.zeros((rest, down.shape[2]), BF)
    for copy in down_copies:
        copy.wait()
    wide = 2 * cap

    def out_part(b):
        hidden_in[b].wait()
        weights = [
            slot_weights(
                select_rows(slots_of(slot_table, experts, columns, size, b, q), experts, wide),
                slots_of(weight_table, experts, columns, size, b, q),
                experts,
                wide,
            )
            for q in range(QUARTET)
        ]
        for e in range(experts):

            def one_tile(n, carry, e=e):
                cols = pl.ds(pl.multiple_of(n * tile, tile), tile)
                rows = dot_plain(hid[b, e], down[e, :, cols])
                for q in range(QUARTET):
                    parts[q, e * wide : (e + 1) * wide, cols] = (
                        rows[q * wide : (q + 1) * wide] * weights[q][e * wide : (e + 1) * wide]
                    ).astype(BF)
                return carry

            lax.fori_loop(0, width // tile, one_tile, 0)
        if b > 1:
            for i in range(4):
                plane.pair(i, b - 2).wait_send()

        def keep(q, cols, value):
            chip[q, b, :, cols] = value[:size]
            others[b % 2, q, :, cols] = value[size:]

        token_sums(slot_table, experts, columns, size, wide, b, parts, keep)
        for i in range(4):
            plane.pair(i, b).start()

    jobs = [(e, step) for e in range(experts) for step in range(steps)]

    def fetch(k):
        e, step = jobs[k]
        slot = k % 2
        return [
            pltpu.make_async_copy(x_all.at[step, e], xk.at[slot], work.at[slot, 0]),
            pltpu.make_async_copy(d_all.at[step, e], dk.at[slot], work.at[slot, 1]),
            pltpu.make_async_copy(hid_all.at[step, e], hk.at[slot], work.at[slot, 2]),
            pltpu.make_async_copy(dgu_all.at[step, e], gk.at[slot], work.at[slot, 3]),
        ]

    def write(e):
        return [
            pltpu.make_async_copy(
                totals.at[e % 2, i, pl.ds(0, local_hidden)], grad.at[e], written.at[e % 2, i]
            )
            for i, grad in enumerate((gate_grad, up_grad, down_grad))
        ]

    def job(k):
        e, step = jobs[k]
        slot, place = k % 2, e % 2
        if k + 1 < len(jobs):
            for copy in fetch(k + 1):
                copy.start()
        for copy in fetch(k):
            copy.wait()
        if step == 0 and e > 1:
            for copy in write(e - 2):
                copy.wait()

        def one(n, carry):
            cols = pl.ds(pl.multiple_of(n * tile, tile), tile)
            found = [
                dot_first(gk[slot, :, :pad], xk[slot, :, cols]),
                dot_first(gk[slot, :, pad:], xk[slot, :, cols]),
                dot_first(hk[slot], dk[slot, :, cols]),
            ]
            for i, value in enumerate(found):
                if step == 0:
                    totals[place, i, :, cols] = value
                else:
                    totals[place, i, :, cols] += value
            return carry

        lax.fori_loop(0, width // tile, one, 0)
        if step == steps - 1:
            for copy in write(e):
                copy.start()

    out_part(0)
    out_part(1)
    summed.middle(local.at[3])
    plane.send_first([0], False)
    out_part(2)
    plane.send_first([1], False)
    for copy in fetch(0):
        copy.start()
    out_part(3)
    plane.send_first([2], False)
    job(0)
    plane.send_first([3], False)

    for copy in first:
        copy.wait()
    total = summed.total(own_v[...])
    mixed = mixed_v[...]
    inverse = lax.rsqrt(jnp.mean(mixed * mixed, axis=1, keepdims=True) + EPSILON)
    unit = mixed * inverse
    scaled = total * gain_ref[...]
    gain_out[...] = jnp.sum(total * unit, axis=0, keepdims=True)
    back = inverse * (scaled - unit * jnp.mean(scaled * unit, axis=1, keepdims=True))
    d_mixed = cotan_v[...].astype(F32) + back
    mixed_v[...] = d_mixed
    proj_v[...] = d_mixed.astype(BF)
    own_copy = pltpu.make_async_copy(proj_v, d_proj_all.at[rows_of(0)], local.at[0])
    own_copy.start()
    mixed_copy = pltpu.make_async_copy(mixed_v, d_mixed_out, local.at[1])
    mixed_copy.start()
    own_copy.wait()
    gather.start()
    for b in range(columns):
        if b + 1 < len(jobs):
            job(b + 1)
        plane.send_second([b])
        if b == 1:
            gather.wait(2)
    for b in range(columns):
        if columns + 1 + b < len(jobs):
            job(columns + 1 + b)
        if b < columns - 1:
            plane.finish([b])
    for k in range(2 * columns + 1, len(jobs)):
        job(k)
    plane.finish([columns - 1])
    done = [
        pltpu.make_async_copy(chip.at[0, h], routed_out.at[rows_of(h)], sum_local.at[4 + h])
        for h in range(columns)
    ]
    for copy in done:
        copy.start()
    gather.wait(1)
    gather.wait(3)
    for copy in done + [mixed_copy]:
        copy.wait()
    for e in range(max(0, experts - 2), experts):
        for copy in write(e):
            copy.wait()
    plane.drain(2)
    gather.drain()
    summed.drain()


def middle_call(d_ffn, mixed, cotan, gain, tables, down, kept, cap):
    columns = lax.axis_size("tp")
    size, width = cotan.shape
    x_all, d_all, hid_all, dgu_all = kept
    steps, experts, slots, pad = hid_all.shape
    local_hidden = down.shape[1]
    anywhere = pl.BlockSpec(memory_space=pl.ANY)
    held = pl.BlockSpec(memory_space=pltpu.VMEM)
    landing, scratch = plane_sum_space(columns, size, width)
    remote, near = plane_sum_sizes(columns)
    remote = remote + 8
    grad = jax.ShapeDtypeStruct((experts, local_hidden, width), F32)
    results = pl.pallas_call(
        functools.partial(middle_kernel, cap, columns, size, experts, steps, local_hidden),
        out_shape=[
            jax.ShapeDtypeStruct((size, width), F32),
            jax.ShapeDtypeStruct((SEQ, width), BF),
            jax.ShapeDtypeStruct((1, width), F32),
            jax.ShapeDtypeStruct((SEQ, width), BF),
            grad,
            grad,
            grad,
        ]
        + landing,
        in_specs=[anywhere] * 3 + [held] * 3 + [anywhere] * 5,
        out_specs=[anywhere] * 2 + [held] + [anywhere] * 6,
        scratch_shapes=scratch
        + [
            pltpu.VMEM((size, width), BF),
            pltpu.VMEM((columns - 1, size, width), BF),
            pltpu.VMEM((2, size, width), BF),
            pltpu.VMEM((size, width), F32),
            pltpu.VMEM((size, width), BF),
            pltpu.VMEM((size, width), BF),
            pltpu.VMEM((2, slots, width), BF),
            pltpu.VMEM((2, slots, width), BF),
            pltpu.VMEM((2, slots, pad), BF),
            pltpu.VMEM((2, slots, 2 * pad), BF),
            pltpu.VMEM((2, 3, pad, width), F32),
            pltpu.VMEM((steps, experts, slots, pad), BF),
            pltpu.VMEM((experts, pad, width), BF),
            pltpu.VMEM((QUARTET, 2 * experts * cap, width), BF),
            pltpu.VMEM((2, 4, size, width), BF),
            pltpu.SemaphoreType.DMA((remote,)),
            pltpu.SemaphoreType.DMA((remote,)),
            pltpu.SemaphoreType.DMA((4 + columns + experts,)),
            pltpu.SemaphoreType.DMA((near,)),
            pltpu.SemaphoreType.DMA((2, 4)),
            pltpu.SemaphoreType.DMA((2, 3)),
        ],
        compiler_params=pltpu.CompilerParams(
            collective_id=3, has_side_effects=True, vmem_limit_bytes=67_043_328
        ),
        cost_estimate=pl.CostEstimate(
            flops=2 * 3 * steps * experts * slots * width * pad,
            bytes_accessed=300 * SEQ * width,
            transcendentals=0,
        ),
        name="middle",
    )(d_ffn, mixed, cotan, gain, *tables, down, x_all, d_all, hid_all, dgu_all)
    return results[:7]


def last_kernel(columns, size, latent_start, latent_width, *refs):
    (
        d_normed_in,
        tokens_in,
        d_mixed_in,
        gain_ref,
        joint_in,
        up_in,
        out_in,
        sums_in,
        grad_out,
        joint_out,
        up_out,
        out_out,
        latent_out,
        sums_out,
        joint_theirs,
        joint_links,
        up_theirs,
        up_links,
        out_theirs,
        out_links,
        joint_chip,
        joint_stage,
        up_chip,
        up_stage,
        out_chip,
        out_stage,
        own_v,
        arrived_v,
        relayed_v,
        tokens_v,
        mixed_v,
        running,
        sums_v,
        latent_v,
        sends,
        arrivals,
        local,
        joint_local,
        up_local,
        out_local,
    ) = refs
    partner, along, across = plane_neighbours()
    column = column_neighbours(columns)
    place, row = lax.axis_index("fsdp"), lax.axis_index("tp")
    core, right, above = place % 2, (place // 2) % 2, place // 4

    def absolute(r):
        return (
            (above + r // 4) % 2 * 4 + (right + r // 2 % 2) % 2 * 2 + (core + r % 2) % 2
        )

    greet([partner, along, across] + column)
    each = plane_sum_sizes(1)[0]
    joint_rows, up_rows = joint_chip.shape[2], up_chip.shape[2]
    out_cols = out_chip.shape[3]

    def by_rows(ref, count):
        return lambda r, h: ref.at[pl.ds(pl.multiple_of(absolute(r) * count, count), count)]

    joint = PlaneSum(
        by_rows(joint_in, joint_rows),
        joint_chip,
        joint_theirs,
        joint_links,
        joint_stage,
        sends,
        arrivals,
        0,
        joint_local,
    )
    up = PlaneSum(
        by_rows(up_in, up_rows),
        up_chip,
        up_theirs,
        up_links,
        up_stage,
        sends,
        arrivals,
        each,
        up_local,
    )
    out = PlaneSum(
        lambda r, h: out_in.at[
            :, pl.ds(pl.multiple_of(absolute(r) * out_cols, out_cols), out_cols)
        ],
        out_chip,
        out_theirs,
        out_links,
        out_stage,
        sends,
        arrivals,
        2 * each,
        out_local,
    )
    base = 3 * each
    rows_of = block_rows(columns, size)
    summed = ColumnSum(d_normed_in, rows_of, arrived_v, relayed_v, sends, arrivals, base)
    base = base + 4
    summed.start(local.at[4])
    first = [
        pltpu.make_async_copy(d_normed_in.at[rows_of(0)], own_v, local.at[0]),
        pltpu.make_async_copy(tokens_in, tokens_v, local.at[1]),
        pltpu.make_async_copy(d_mixed_in, mixed_v, local.at[2]),
        pltpu.make_async_copy(sums_in, running.at[0], local.at[3]),
    ]
    for copy in first:
        copy.start()
    for part in (out, joint, up):
        part.begin()
    summed.clear()
    first[3].wait()

    def small(i, device):
        return mesh_copy(running.at[i], sums_v.at[i], sends, arrivals, base + i, device)

    hops = [small(i, device) for i, device in enumerate((partner, along, across))]
    for i, copy in enumerate(hops):
        copy.start()
        copy.wait_recv()
        running[i + 1] = running[i] + sums_v[i]
    gains = [
        mesh_copy(running.at[3], sums_v.at[2 + s], sends, arrivals, base + 2 + s, column[s - 1])
        for s in range(1, columns)
    ]
    base = base + 2 + columns
    for copy in gains:
        copy.start()
    summed.middle(local.at[4])
    for part in (out, joint, up):
        part.send_first()
    for part in (out, joint, up):
        part.send_second()
    for part in (out, joint, up):
        part.finish()

    pieces = joint_rows // columns
    across_columns = [
        mesh_copy(
            joint_chip.at[
                0,
                0,
                pl.ds(pl.multiple_of((row + s) % columns * pieces, pieces), pieces),
                pl.ds(latent_start, latent_width),
            ],
            latent_v.at[s - 1],
            sends,
            arrivals,
            base + s - 1,
            column[s - 1],
        )
        for s in range(1, columns)
    ]
    for copy in across_columns:
        copy.start()
    done = [
        pltpu.make_async_copy(joint_chip.at[0, 0], joint_out, joint_local.at[4]),
        pltpu.make_async_copy(up_chip.at[0, 0], up_out, up_local.at[4]),
        pltpu.make_async_copy(out_chip.at[0, 0], out_out, out_local.at[4]),
    ]
    for copy in done:
        copy.start()

    for copy in first[:3]:
        copy.wait()
    total = summed.total(own_v[...])
    tokens = tokens_v[...].astype(F32)
    inverse = lax.rsqrt(jnp.mean(tokens * tokens, axis=1, keepdims=True) + EPSILON)
    unit = tokens * inverse
    scaled = total * gain_ref[...]
    mixed_v[...] = mixed_v[...] + inverse * (
        scaled - unit * jnp.mean(scaled * unit, axis=1, keepdims=True)
    )
    grad_copy = pltpu.make_async_copy(mixed_v, grad_out, local.at[0])
    grad_copy.start()
    gathered = running[3]
    for s in range(1, columns):
        gains[s - 1].wait_recv()
        gathered = gathered + sums_v[2 + s]
    sums_out[...] = gathered
    latent = joint_chip[
        0,
        0,
        pl.ds(pl.multiple_of(row * pieces, pieces), pieces),
        pl.ds(latent_start, latent_width),
    ].astype(F32)
    for s in range(1, columns):
        across_columns[s - 1].wait_recv()
        latent = latent + latent_v[s - 1].astype(F32)
    latent_out[...] = latent
    for copy in done + [grad_copy]:
        copy.wait()
    for part in (out, joint, up):
        part.drain()
    summed.drain()
    for copy in hops + gains + across_columns:
        copy.wait_send()


def last_call(d_normed, tokens, d_mixed, gain, joint, up, out, sums, latent_start, latent_width):
    columns = lax.axis_size("tp")
    size, width = tokens.shape
    anywhere = pl.BlockSpec(memory_space=pl.ANY)
    held = pl.BlockSpec(memory_space=pltpu.VMEM)
    shapes = [
        (joint.shape[0] // 8, joint.shape[1]),
        (up.shape[0] // 8, up.shape[1]),
        (out.shape[0], out.shape[1] // 8),
    ]
    landing, scratch = [], []
    for rows, cols in shapes:
        one = plane_sum_space(1, rows, cols)
        landing, scratch = landing + one[0], scratch + one[1]
    remote, near = plane_sum_sizes(1)
    remote = 3 * remote + 2 * (columns - 1) + 7
    pieces = shapes[0][0] // columns
    return pl.pallas_call(
        functools.partial(last_kernel, columns, size, latent_start, latent_width),
        out_shape=[jax.ShapeDtypeStruct((size, width), F32)]
        + [jax.ShapeDtypeStruct(shape, BF) for shape in shapes]
        + [
            jax.ShapeDtypeStruct((pieces, latent_width), F32),
            jax.ShapeDtypeStruct(sums.shape, F32),
        ]
        + landing,
        in_specs=[anywhere] * 3 + [held] + [anywhere] * 4,
        out_specs=[anywhere] * 4 + [held] * 2 + [anywhere] * 6,
        scratch_shapes=scratch
        + [
            pltpu.VMEM((size, width), BF),
            pltpu.VMEM((columns - 1, size, width), BF),
            pltpu.VMEM((2, size, width), BF),
            pltpu.VMEM((size, width), BF),
            pltpu.VMEM((size, width), F32),
            pltpu.VMEM((4,) + sums.shape, F32),
            pltpu.VMEM((2 + columns,) + sums.shape, F32),
            pltpu.VMEM((columns - 1, pieces, latent_width), BF),
            pltpu.SemaphoreType.DMA((remote,)),
            pltpu.SemaphoreType.DMA((remote,)),
            pltpu.SemaphoreType.DMA((5,)),
            pltpu.SemaphoreType.DMA((near,)),
            pltpu.SemaphoreType.DMA((near,)),
            pltpu.SemaphoreType.DMA((near,)),
        ],
        compiler_params=pltpu.CompilerParams(
            collective_id=4, has_side_effects=True, vmem_limit_bytes=48 * 1024 * 1024
        ),
        cost_estimate=pl.CostEstimate(
            flops=0, bytes_accessed=180 * SEQ * width, transcendentals=0
        ),
        name="last_sums",
    )(d_normed, tokens, d_mixed, gain, joint, up, out, sums)[:6]


def plane_units(count):
    return [[(2 * i + j // 2, j % 2) for j in range(4)] for i in range(count // 2)]


def plane_gather(rows, count):
    gathered = lax.all_gather(rows, "fsdp", axis=0)
    return {
        (r, h): gathered[r, h * HALF : (h + 1) * HALF] for r in range(count) for h in (0, 1)
    }


def plane_scatter_whole(pairs, units, count):
    parts = {}
    for unit, pair in zip(units, pairs):
        for q, key in enumerate(unit):
            parts[key] = pair[q // 2][q % 2]
    stacked = jnp.concatenate([parts[r, h] for r in range(count) for h in (0, 1)], axis=0)
    return lax.psum_scatter(stacked, "fsdp", scatter_dimension=0, tiled=True).astype(F32)


def sum_everywhere(values):
    for axis_name in ("fsdp", "tp"):
        count = lax.axis_size(axis_name)
        if is_power(count):
            bit = 1
            while bit < count:
                values = values + swap(values, axis_name, bit)
                bit *= 2
        else:
            values = lax.psum(values, axis_name)
    return values


def expert_tables(expert_ids, expert_wts, local_experts, units, cap):
    fsdp_count = lax.axis_size("fsdp")
    fsdp_rank = lax.axis_index("fsdp")
    expert_count = local_experts * fsdp_count
    names = jnp.arange(expert_count, dtype=jnp.int32)[:, None]
    member = jnp.zeros((expert_count, SEQ), jnp.bool_)
    weight = jnp.zeros((expert_count, SEQ), F32)
    ids_rows, wts_rows = expert_ids.T, expert_wts.T
    for pick in range(TOPK):
        same = ids_rows[pick : pick + 1] == names
        member = member | same
        weight = weight + jnp.where(same, wts_rows[pick : pick + 1], 0.0)
    position = jnp.arange(HALF)
    before = (position[:, None] < position[None, :]).astype(BF)
    rank = jnp.dot(
        member.astype(BF).reshape(expert_count * 2, HALF), before, preferred_element_type=F32
    ).reshape(expert_count, SEQ)
    slot = jnp.where(member, rank, NO_SLOT)
    table = jnp.concatenate([slot, weight], axis=0)
    table = lax.all_gather(table, "fsdp", axis=0, tiled=True)
    table = table.reshape(fsdp_count, 2, fsdp_count, local_experts, 2, HALF)
    table = lax.dynamic_index_in_dim(table, fsdp_rank, axis=2, keepdims=False)
    slot_steps, weight_steps = [], []
    for unit in units:
        slot_steps.append(jnp.stack([table[r, 0, :, h] for r, h in unit]))
        weight_steps.append(jnp.stack([table[r, 1, :, h] for r, h in unit]))
    slot_row, weight_row = jnp.stack(slot_steps), jnp.stack(weight_steps)
    return (slot_row, weight_row, jnp.swapaxes(slot_row, 2, 3))


def per_device(
    block_in,
    out_cotan,
    segment_ids,
    expert_ids,
    expert_wts,
    attn_gain,
    query_proj,
    latent_proj,
    latent_gain,
    latent_up,
    out_proj,
    ffn_gain,
    shared_gate,
    shared_up,
    shared_down,
    routed_gate,
    routed_up,
    routed_down,
):
    tp_count = lax.axis_size("tp")
    fsdp_count = lax.axis_size("fsdp")
    tp_rank = lax.axis_index("tp")
    fsdp_rank = lax.axis_index("fsdp")
    tok_rows, model_width = block_in.shape
    local_experts, local_hidden = routed_gate.shape[:2]
    expert_count = local_experts * fsdp_count
    cap_rows = tok_rows * TOPK * 4 // (3 * expert_count)
    cap = cap_rows * (HALF // tok_rows)
    paired = fsdp_count == 8 and tp_count == 4 and tok_rows * 2 == HALF
    heads_local = H // tp_count
    head_width = NOPE + ROPE
    score_scale = head_width ** (-0.5)
    shard_rows, query_cols = query_proj.shape
    latent_cols = latent_proj.shape[1]
    up_cols = latent_up.shape[1]
    out_rows = out_proj.shape[0]

    joint = query_cols + latent_cols
    spare = (-joint) % 128
    spare = spare + 128 if spare < 3 else spare
    gains = jnp.concatenate(
        [
            attn_gain[:, None],
            ffn_gain[:, None],
            jnp.pad(latent_gain, (0, shard_rows - latent_gain.shape[0]))[:, None],
            jnp.zeros((shard_rows, spare - 3), BF),
        ],
        axis=1,
    )
    packed = jnp.concatenate([query_proj, latent_proj, gains], axis=1)
    if paired:
        low, high = (0, RAW_ROWS - TOPK), (0, 0)
        raw = jnp.concatenate(
            [jnp.pad(expert_ids.T.astype(F32), (low, high)), jnp.pad(expert_wts.T, (low, high))]
        )
        (
            tokens_all,
            cotan_all,
            packed_all,
            latent_up_weight,
            out_weight,
            raw,
            shared_weight,
            shared_down_weight,
        ) = first_call(
            block_in,
            out_cotan,
            [
                packed,
                latent_up,
                out_proj,
                raw,
                jnp.concatenate([shared_gate, shared_up], axis=1),
                shared_down,
            ],
            ("rows", "rows", "columns", "relative", "rows", "columns"),
        )
        shared_weight = shared_weight.reshape(model_width, -1)
        packed_all = packed_all.reshape(-1, packed.shape[1])
        latent_up_weight = latent_up_weight.reshape(LAT, up_cols)
    else:
        packed_all = lax.all_gather(packed, "fsdp", axis=0, tiled=True)
        latent_up_weight = lax.all_gather(latent_up, "fsdp", axis=0, tiled=True)
        out_weight = lax.all_gather(out_proj, "fsdp", axis=1, tiled=True)
        tokens_all = column_gather(block_in)
        cotan_all = column_gather(out_cotan)
        shared_weight = lax.all_gather(
            jnp.concatenate([shared_gate, shared_up], axis=1), "fsdp", axis=0, tiled=True
        )
        shared_down_weight = lax.all_gather(shared_down, "fsdp", axis=1, tiled=True)
    gain_attn = packed_all[:, joint].astype(F32)
    gain_ffn = packed_all[:, joint + 1].astype(F32)
    gain_latent = (
        packed_all[:, joint + 2]
        .reshape(fsdp_count, shard_rows)[:, : latent_gain.shape[0]]
        .reshape(LAT)
        .astype(F32)
    )
    shared_cols = shared_gate.shape[1]

    def scatter(part, dimension):
        return lax.psum_scatter(part.astype(BF), "fsdp", scatter_dimension=dimension, tiled=True)

    unit_all, inverse_all = norm_parts(tokens_all.astype(F32))
    normed_all = (unit_all * gain_attn).astype(BF)
    joint_rows = jnp.dot(normed_all, packed_all, preferred_element_type=F32)
    queries = joint_rows[:, :query_cols].reshape(SEQ, heads_local, head_width)
    latent = joint_rows[:, query_cols:joint]
    unit_lat, inverse_lat = norm_parts(latent[:, :LAT])
    positions = jnp.arange(SEQ, dtype=jnp.int32)
    cosine, sine_part = rope_tables(positions, ROPE)
    compressed_all = (unit_lat * gain_latent).astype(BF)
    key_rope_all = rotate(latent[:, LAT:], cosine, sine_part).astype(BF)
    query_cat = jnp.concatenate(
        [
            queries[:, :, :NOPE],
            rotate(queries[:, :, NOPE:], cosine[:, None, :], sine_part[:, None, :]),
        ],
        axis=2,
    ).astype(BF)
    key_value = (
        jnp.dot(compressed_all, latent_up_weight, preferred_element_type=F32)
        .reshape(SEQ, heads_local, NOPE + DV)
        .astype(BF)
    )
    key_cat = jnp.concatenate(
        [
            key_value[:, :, :NOPE],
            jnp.broadcast_to(key_rope_all[:, None, :], (SEQ, heads_local, ROPE)),
        ],
        axis=2,
    )
    values = key_value[:, :, NOPE:]
    allowed = (positions[None, :] <= positions[:, None]) & (
        segment_ids[None, :] == segment_ids[:, None]
    )
    raw_scores = (
        jnp.einsum("qhd,khd->hqk", query_cat, key_cat, preferred_element_type=F32) * score_scale
    )
    masked = jnp.where(allowed[None], raw_scores, MASK_FILL)
    top_score = jnp.max(masked, axis=2, keepdims=True)
    exponent = jnp.exp(masked - top_score)
    row_total = jnp.sum(exponent, axis=2, keepdims=True)
    probabilities = exponent / row_total
    probs_low = probabilities.astype(BF)
    attended = (
        jnp.einsum("hqk,khd->qhd", probs_low, values, preferred_element_type=F32)
        .reshape(SEQ, heads_local * DV)
        .astype(BF)
    )
    attn_part = jnp.dot(attended, out_weight, preferred_element_type=F32).astype(BF)
    if paired:
        mixed_rows, normed_ffn_all, d_routed_in, *kept = expert_call(
            attn_part,
            block_in,
            cotan_all,
            routed_gate,
            routed_up,
            routed_down,
            gain_ffn[None, :],
            raw,
            cap_rows,
        )
        unit_two, inverse_two = norm_parts(mixed_rows)
        d_routed_in = d_routed_in.astype(F32)
    else:
        units = plane_units(fsdp_count)
        tables = expert_tables(expert_ids, expert_wts, local_experts, units, cap)
        hidden_pad = -(-local_hidden // 128) * 128
        lift = ((0, 0), (0, hidden_pad - local_hidden), (0, 0))
        routed_gate_up = jnp.concatenate(
            [jnp.pad(routed_gate, lift), jnp.pad(routed_up, lift)], axis=1
        )
        routed_down_pad = jnp.pad(routed_down, lift)
        mixed_rows = block_in.astype(F32) + column_scatter(attn_part)
        unit_two, inverse_two = norm_parts(mixed_rows)
        normed_ffn_all = column_gather((unit_two * gain_ffn).astype(BF))
        x_blocks = plane_gather(normed_ffn_all, fsdp_count)
        dy_all = lax.all_gather(cotan_all, "fsdp", axis=0, tiled=True)
        kept = []
        dx_pairs = []
        for step, unit in enumerate(units):
            pair, kept = expert_front(
                step,
                len(units),
                [x_blocks[key] for key in unit],
                jnp.array([2 * r + h for r, h in unit], jnp.int32),
                dy_all,
                routed_gate_up,
                routed_down_pad,
                tables,
                kept,
                cap,
            )
            dx_pairs.append(pair)
        near, far = expert_out(kept[2], routed_down_pad, tables, cap)
        d_routed_in = plane_scatter_whole(dx_pairs, units, fsdp_count)
    if not paired:
        routed_gate_grad, routed_up_grad, routed_down_grad = expert_grads(kept, local_hidden)

    shared_pre = jnp.dot(normed_ffn_all, shared_weight, preferred_element_type=F32)
    shared_gate_pre, shared_up_pre = shared_pre[:, :shared_cols], shared_pre[:, shared_cols:]
    shared_hidden = (jax.nn.silu(shared_gate_pre) * shared_up_pre).astype(BF)
    shared_rows = jnp.dot(shared_hidden, shared_down_weight, preferred_element_type=F32)
    shared_down_part = jnp.dot(shared_hidden.T, cotan_all, preferred_element_type=F32)
    d_shared_hidden = jnp.dot(cotan_all, shared_down_weight.T, preferred_element_type=F32)
    d_shared = jnp.concatenate(silu_back(d_shared_hidden, shared_gate_pre, shared_up_pre), axis=1)
    shared_part = jnp.dot(normed_ffn_all.T, d_shared, preferred_element_type=F32)
    d_shared_in = jnp.dot(d_shared, shared_weight.T, preferred_element_type=F32)

    if paired:
        d_ffn_rows, shared_part, shared_down_part = tie(
            (d_shared_in + d_routed_in).astype(BF),
            shared_part.astype(BF),
            shared_down_part.astype(BF),
        )
        (
            d_mixed,
            d_proj_all,
            ffn_gain_part,
            routed_rows,
            routed_gate_grad,
            routed_up_grad,
            routed_down_grad,
        ) = middle_call(
            d_ffn_rows,
            mixed_rows,
            out_cotan,
            gain_ffn[None, :],
            kept[:2],
            routed_down,
            kept[2:],
            cap_rows,
        )
        ffn_gain_part = ffn_gain_part[0]
        routed_rows = routed_rows.astype(F32)
    else:
        d_normed_ffn = column_scatter(d_shared_in + d_routed_in)
        out_pairs = [(near[step], far[step]) for step in range(len(units))]
        routed_rows = plane_scatter_whole(out_pairs, units, fsdp_count)
        ffn_gain_part, d_mixed_norm = norm_back(d_normed_ffn, unit_two, inverse_two, gain_ffn)
        d_mixed = out_cotan.astype(F32) + d_mixed_norm
        d_proj_all = column_gather(d_mixed.astype(BF))
    shared_grad = scatter(shared_part, 0)
    down_own, ffn_rows, shared_grad = tie(
        shared_down_part.astype(BF), (shared_rows + routed_rows).astype(BF), shared_grad
    )
    shared_down_grad = scatter(down_own, 1)
    ffn_rows = column_scatter(ffn_rows)
    block_out = (mixed_rows + ffn_rows).astype(BF)

    out_part = jnp.dot(attended.T, d_proj_all, preferred_element_type=F32)
    d_attended = (
        jnp.dot(d_proj_all, out_weight.T, preferred_element_type=F32)
        .astype(BF)
        .reshape(SEQ, heads_local, DV)
    )
    prob_grad = jnp.einsum("qhd,khd->hqk", d_attended, values, preferred_element_type=F32)
    score_grad = (
        probabilities
        * (prob_grad - jnp.sum(probabilities * prob_grad, axis=2, keepdims=True))
    ).astype(BF)
    query_grad = (
        jnp.einsum("hqk,khd->qhd", score_grad, key_cat, preferred_element_type=F32) * score_scale
    )
    key_grad = (
        jnp.einsum("hqk,qhd->khd", score_grad, query_cat, preferred_element_type=F32) * score_scale
    )
    value_grad = jnp.einsum("hqk,qhd->khd", probs_low, d_attended, preferred_element_type=F32)
    d_queries = (
        jnp.concatenate(
            [
                query_grad[:, :, :NOPE],
                unrotate(query_grad[:, :, NOPE:], cosine[:, None, :], sine_part[:, None, :]),
            ],
            axis=2,
        )
        .reshape(SEQ, heads_local * head_width)
        .astype(BF)
    )
    d_key_value = (
        jnp.concatenate([key_grad[:, :, :NOPE], value_grad], axis=2)
        .reshape(SEQ, heads_local * (NOPE + DV))
        .astype(BF)
    )
    latent_up_part = jnp.dot(compressed_all.T, d_key_value, preferred_element_type=F32)
    d_compressed = jnp.dot(d_key_value, latent_up_weight.T, preferred_element_type=F32)
    d_key_rope = jnp.sum(key_grad[:, :, NOPE:], axis=1)
    latent_gain_part, d_latent_main = norm_back(d_compressed, unit_lat, inverse_lat, gain_latent)
    d_latent = jnp.concatenate(
        [d_latent_main, unrotate(d_key_rope, cosine, sine_part)], axis=1
    ).astype(BF)
    d_joint = jnp.concatenate([d_queries, d_latent, jnp.zeros((SEQ, spare), BF)], axis=1)
    joint_part = jnp.dot(normed_all.T, d_joint, preferred_element_type=F32)
    d_normed_part = jnp.dot(d_joint, packed_all.T, preferred_element_type=F32)
    attn_gain_part = jnp.sum(d_normed_part * unit_all, axis=0)

    gain_parts = jnp.concatenate([attn_gain_part, latent_gain_part, ffn_gain_part]).reshape(
        -1, 128
    )
    joint_part = joint_part.astype(BF)
    if paired:
        latent_width = joint_part.shape[1] - query_cols
        (
            block_in_grad,
            joint_grad,
            latent_up_grad,
            out_proj_grad,
            latent_proj_grad,
            gain_sums,
        ) = last_call(
            d_normed_part.astype(BF),
            block_in,
            d_mixed,
            gain_attn[None, :],
            joint_part,
            latent_up_part.astype(BF),
            out_part.astype(BF),
            gain_parts,
            query_cols,
            latent_width,
        )
        latent_proj_grad = latent_proj_grad[:, :latent_cols]
    else:
        d_normed = column_scatter(d_normed_part)
        unit_one, inverse_one = norm_parts(block_in.astype(F32))
        _, d_tokens_norm = norm_back(d_normed, unit_one, inverse_one, gain_attn)
        block_in_grad = d_mixed + d_tokens_norm
        out_proj_grad = scatter(out_part, 1)
        latent_up_grad = scatter(latent_up_part, 0)
        joint_grad = scatter(joint_part, 0)
        latent_proj_grad = column_scatter(joint_grad[:, query_cols:joint])
        gain_sums = sum_everywhere(gain_parts)
    gain_sums = gain_sums.reshape(-1)
    query_proj_grad = joint_grad[:, :query_cols].astype(F32)
    latent_up_grad = latent_up_grad.astype(F32)
    out_proj_grad = out_proj_grad.astype(F32)
    shared_grad = shared_grad.astype(F32)
    shared_gate_grad, shared_up_grad = shared_grad[:, :shared_cols], shared_grad[:, shared_cols:]
    shared_down_grad = shared_down_grad.astype(F32)
    device = fsdp_rank * tp_count + tp_rank
    devices = tp_count * fsdp_count

    def own_gain(start, size):
        return lax.dynamic_slice(gain_sums, (start + device * (size // devices),), (size // devices,))

    attn_gain_grad = own_gain(0, model_width)
    latent_gain_grad = own_gain(model_width, LAT)
    ffn_gain_grad = own_gain(model_width + LAT, model_width)
    return (
        block_out,
        block_in_grad,
        attn_gain_grad,
        query_proj_grad,
        latent_proj_grad,
        latent_gain_grad,
        latent_up_grad,
        out_proj_grad,
        ffn_gain_grad,
        shared_gate_grad,
        shared_up_grad,
        shared_down_grad,
        routed_gate_grad,
        routed_up_grad,
        routed_down_grad,
    )


def solution(mesh):
    placed = (
        P(("fsdp", "tp"), None),
        P(("fsdp", "tp"), None),
        P("fsdp"),
        P("fsdp", None),
        P("fsdp", None),
        P("fsdp"),
        P("fsdp", "tp"),
        P("fsdp", None),
        P("fsdp"),
        P("fsdp", "tp"),
        P("tp", "fsdp"),
        P("fsdp"),
        P("fsdp", "tp"),
        P("fsdp", "tp"),
        P("tp", "fsdp"),
        P("fsdp", "tp", None),
        P("fsdp", "tp", None),
        P("fsdp", "tp", None),
    )
    return jax.shard_map(
        per_device,
        mesh=mesh,
        in_specs=placed,
        out_specs=(
            P(("fsdp", "tp"), None),
            P(("fsdp", "tp"), None),
            P(("fsdp", "tp")),
            P("fsdp", "tp"),
            P(("fsdp", "tp"), None),
            P(("fsdp", "tp")),
            P("fsdp", "tp"),
            P("tp", "fsdp"),
            P(("fsdp", "tp")),
            P("fsdp", "tp"),
            P("fsdp", "tp"),
            P("tp", "fsdp"),
            P("fsdp", "tp", None),
            P("fsdp", "tp", None),
            P("fsdp", "tp", None),
        ),
        check_vma=False,
    )
```

```python
import functools

import jax
import jax.numpy as jnp
from jax import lax
from jax.experimental import pallas as pl
from jax.experimental.pallas import tpu as pltpu
from jax.sharding import PartitionSpec as P

H = 16
NOPE = 128
ROPE = 64
DV = 128
LAT = 512
TOPK = 6
SEQ = 512
HALF = 256
QUARTET = 4
RAW_ROWS = 8


EPSILON = 1e-06
THETA_BASE = 10000.0
MASK_FILL = -1e30
NO_SLOT = -1e6

BF = jnp.bfloat16
F32 = jnp.float32


def rope_tables(positions, width_rope):
    middle = width_rope // 2
    frequency = THETA_BASE ** (-(jnp.arange(middle) * 2).astype(jnp.float32) / width_rope)
    angles = positions.astype(jnp.float32)[:, None] * frequency[None, :]
    return (jnp.cos(angles), jnp.sin(angles))


def rotate(values, cosine, sine_part):
    middle = values.shape[-1] // 2
    first_half = values[..., :middle]
    second_half = values[..., middle:]
    return jnp.concatenate(
        [
            first_half * cosine - second_half * sine_part,
            second_half * cosine + first_half * sine_part,
        ],
        axis=-1,
    )


def unrotate(values, cosine, sine_part):
    middle = values.shape[-1] // 2
    first_half = values[..., :middle]
    second_half = values[..., middle:]
    return jnp.concatenate(
        [
            first_half * cosine + second_half * sine_part,
            second_half * cosine - first_half * sine_part,
        ],
        axis=-1,
    )


def norm_parts(values):
    inverse = lax.rsqrt(jnp.mean(values * values, axis=-1, keepdims=True) + EPSILON)
    return (values * inverse, inverse)


def norm_back(upstream, unit_rows, inverse, scaling):
    scaled = upstream * scaling
    gain_grad = jnp.sum(upstream * unit_rows, axis=0)
    input_grad = inverse * (
        scaled - unit_rows * jnp.mean(scaled * unit_rows, axis=-1, keepdims=True)
    )
    return (gain_grad, input_grad)


def silu_back(grad_hidden, gate_pre, up_pre):
    sigmoid = jax.nn.sigmoid(gate_pre)
    gate_grad = grad_hidden * up_pre * (sigmoid * (1.0 + gate_pre * (1.0 - sigmoid)))
    up_grad = grad_hidden * (gate_pre * sigmoid)
    return (gate_grad.astype(jnp.bfloat16), up_grad.astype(jnp.bfloat16))


def is_power(count):
    return count & (count - 1) == 0


def swap(values, axis_name, bit):
    count = lax.axis_size(axis_name)
    return lax.ppermute(values, axis_name, [(i, i ^ bit) for i in range(count)])


def tie(*values):
    return lax.optimization_barrier(values)


def column_gather(rows):
    return lax.all_gather(rows, "tp", axis=0, tiled=True)


def column_scatter(values):
    return lax.psum_scatter(values.astype(BF), "tp", scatter_dimension=0, tiled=True).astype(F32)


def dot_rows(left, right):
    return lax.dot_general(left, right, (((1,), (1,)), ((), ())), preferred_element_type=F32)


def dot_plain(left, right):
    return lax.dot_general(left, right, (((1,), (0,)), ((), ())), preferred_element_type=F32)


def dot_first(left, right):
    return lax.dot_general(left, right, (((0,), (0,)), ((), ())), preferred_element_type=F32)


def select_rows(slot_rows, experts, cap):
    row = lax.broadcasted_iota(jnp.int32, (experts * cap, HALF), 0).astype(F32)
    hit = row == slot_rows[0:1, :]
    for e in range(1, experts):
        hit = hit | (row == slot_rows[e : e + 1, :] + float(e * cap))
    return hit


def select_cols(slot_cols, experts, cap):
    lane = lax.broadcasted_iota(jnp.int32, (HALF, experts * cap), 1).astype(F32)
    hit = lane == slot_cols[:, 0:1]
    for e in range(1, experts):
        hit = hit | (lane == slot_cols[:, e : e + 1] + float(e * cap))
    return hit


def slot_weights(hit, weight_rows, experts, cap):
    pieces = []
    for e in range(experts):
        part = hit[e * cap : (e + 1) * cap, :]
        pieces.append(
            jnp.sum(jnp.where(part, weight_rows[e : e + 1, :], 0.0), axis=1, keepdims=True)
        )
    return jnp.concatenate(pieces, axis=0)


def expert_front_kernel(step, experts, cap, aliased, *refs):
    count = QUARTET
    x_in = refs[:count]
    where_ref, dy_in, gate_up_in, down_in, slot_row_ref, weight_row_ref, slot_col_ref = refs[
        count : count + 7
    ]
    base = count + 7 + aliased
    dx_out = refs[base : base + 2]
    x_all, d_all, hid_all, dgu_all = refs[base + 2 : base + 6]
    (xb, db, gate_up, down, xs, ds, dxs, dxo, hid, dgu, sem_in, sem_w, sem_out, sem_dx) = refs[
        base + 6 :
    ]
    width = xb.shape[2]
    pad = down.shape[1]
    tile = min(1024, width)
    x_copies = [pltpu.make_async_copy(x_in[q], xb.at[q], sem_in.at[q]) for q in range(count)]
    d_copies = [
        pltpu.make_async_copy(
            dy_in.at[pl.ds(pl.multiple_of(where_ref[q] * HALF, HALF), HALF)],
            db.at[q],
            sem_in.at[count + q],
        )
        for q in range(count)
    ]
    w_copies = [
        pltpu.make_async_copy(gate_up_in, gate_up, sem_w.at[0]),
        pltpu.make_async_copy(down_in, down, sem_w.at[1]),
    ]
    for q in range(count):
        x_copies[q].start()
        d_copies[q].start()
    for copy in w_copies:
        copy.start()
    for q in range(count):
        x_copies[q].wait()
        d_copies[q].wait()

        hit = select_rows(slot_row_ref[q], experts, cap)
        weights = slot_weights(hit, weight_row_ref[q], experts, cap)
        choose = jnp.where(hit, 1.0, 0.0).astype(BF)

        def spread(n, carry, q=q, choose=choose, weights=weights):
            cols = pl.ds(pl.multiple_of(n * tile, tile), tile)
            rows = dot_plain(choose, xb[q, :, cols])
            grads = dot_plain(choose, db[q, :, cols]) * weights
            for e in range(experts):
                xs[e, q * cap : (q + 1) * cap, cols] = rows[e * cap : (e + 1) * cap].astype(BF)
                ds[e, q * cap : (q + 1) * cap, cols] = grads[e * cap : (e + 1) * cap].astype(BF)
            return carry

        lax.fori_loop(0, width // tile, spread, 0)
    out_copies = [
        pltpu.make_async_copy(xs, x_all.at[step], sem_out.at[0]),
        pltpu.make_async_copy(ds, d_all.at[step], sem_out.at[1]),
        pltpu.make_async_copy(hid, hid_all.at[step], sem_out.at[2]),
        pltpu.make_async_copy(dgu, dgu_all.at[step], sem_out.at[3]),
    ]
    out_copies[0].start()
    out_copies[1].start()
    for copy in w_copies:
        copy.wait()

    def one_expert(e, carry):
        both = dot_rows(xs[e], gate_up[e])
        gate_pre, up_pre = both[:, :pad], both[:, pad:]
        d_hidden = dot_rows(ds[e], down[e])
        sigmoid = jax.nn.sigmoid(gate_pre)
        silu = gate_pre * sigmoid
        hid[e] = (silu * up_pre).astype(BF)
        gate_grad = d_hidden * up_pre * (sigmoid * (1.0 + gate_pre * (1.0 - sigmoid)))
        grads = jnp.concatenate([gate_grad, d_hidden * silu], axis=1).astype(BF)
        dgu[e] = grads

        def back(n, inner):
            cols = pl.ds(pl.multiple_of(n * tile, tile), tile)
            part = dot_plain(dgu[e], gate_up[e, :, cols]).astype(BF)
            for q in range(count):
                dxs[q, pl.ds(pl.multiple_of(e * cap, cap), cap), cols] = part[
                    q * cap : (q + 1) * cap
                ]
            return inner

        lax.fori_loop(0, width // tile, back, 0)
        return carry

    lax.fori_loop(0, experts, one_expert, 0)
    out_copies[2].start()
    out_copies[3].start()
    dx_copies = [
        pltpu.make_async_copy(dxo.at[q], dx_out[q // 2].at[q % 2], sem_dx.at[q])
        for q in range(count)
    ]
    for q in range(count):
        choose = jnp.where(select_cols(slot_col_ref[q], experts, cap), 1.0, 0.0).astype(BF)

        def gather(n, carry, q=q, choose=choose):
            cols = pl.ds(pl.multiple_of(n * tile, tile), tile)
            dxo[q, :, cols] = dot_plain(choose, dxs[q, :, cols]).astype(BF)
            return carry

        lax.fori_loop(0, width // tile, gather, 0)
        dx_copies[q].start()
    for copy in out_copies:
        copy.wait()
    for copy in dx_copies:
        copy.wait()


def expert_front(step, steps, x_parts, where, dy_all, gate_up, down, tables, kept, cap):
    experts, wide, width = gate_up.shape
    pad = wide // 2
    slots = QUARTET * cap
    slot_row, weight_row, slot_col = (t[step] for t in tables)
    any_spec = pl.BlockSpec(memory_space=pl.ANY)
    vmem_spec = pl.BlockSpec(memory_space=pltpu.VMEM)
    pair_shape = jax.ShapeDtypeStruct((2, HALF, width), BF)
    kept_shapes = [
        jax.ShapeDtypeStruct((steps, experts, slots, columns), BF)
        for columns in (width, width, pad, wide)
    ]
    results = pl.pallas_call(
        functools.partial(expert_front_kernel, step, experts, cap, len(kept)),
        out_shape=[pair_shape] * 2 + kept_shapes,
        in_specs=[any_spec] * QUARTET
        + [pl.BlockSpec(memory_space=pltpu.SMEM)]
        + [any_spec] * 3
        + [vmem_spec] * 3
        + [any_spec] * len(kept),
        out_specs=[any_spec] * 6,
        input_output_aliases={QUARTET + 7 + i: 2 + i for i in range(len(kept))},
        scratch_shapes=[
            pltpu.VMEM((QUARTET, HALF, width), BF),
            pltpu.VMEM((QUARTET, HALF, width), BF),
            pltpu.VMEM((experts, wide, width), BF),
            pltpu.VMEM((experts, pad, width), BF),
            pltpu.VMEM((experts, slots, width), BF),
            pltpu.VMEM((experts, slots, width), BF),
            pltpu.VMEM((QUARTET, experts * cap, width), BF),
            pltpu.VMEM((QUARTET, HALF, width), BF),
            pltpu.VMEM((experts, slots, pad), BF),
            pltpu.VMEM((experts, slots, wide), BF),
            pltpu.SemaphoreType.DMA((2 * QUARTET,)),
            pltpu.SemaphoreType.DMA((2,)),
            pltpu.SemaphoreType.DMA((4,)),
            pltpu.SemaphoreType.DMA((QUARTET,)),
        ],
        compiler_params=pltpu.CompilerParams(vmem_limit_bytes=62 * 1024 * 1024),
        cost_estimate=pl.CostEstimate(
            flops=2 * slots * experts * width * pad * 5
            + 6 * QUARTET * HALF * experts * cap * width,
            bytes_accessed=2 * width * (3 * QUARTET * HALF + experts * 3 * pad + 2 * experts * slots),
            transcendentals=slots * experts * pad,
        ),
        name="expert_front",
    )(*x_parts, where, dy_all, gate_up, down, slot_row, weight_row, slot_col, *kept)
    return list(results[:2]), list(results[2:])


def expert_out_kernel(experts, cap, hid, down, slot_row, weight_row, slot_col, near, far, parts):
    width = down.shape[2]
    tile = min(1024, width)
    weights = [
        slot_weights(
            select_rows(slot_row[0, q], experts, cap), weight_row[0, q], experts, cap
        )
        for q in range(QUARTET)
    ]
    for e in range(experts):

        def front(n, carry, e=e):
            cols = pl.ds(pl.multiple_of(n * tile, tile), tile)
            rows = dot_plain(hid[0, e], down[e, :, cols])
            for q in range(QUARTET):
                parts[q, e * cap : (e + 1) * cap, cols] = (
                    rows[q * cap : (q + 1) * cap] * weights[q][e * cap : (e + 1) * cap]
                ).astype(BF)
            return carry

        lax.fori_loop(0, width // tile, front, 0)
    for q in range(QUARTET):
        choose = jnp.where(select_cols(slot_col[0, q], experts, cap), 1.0, 0.0).astype(BF)
        out = (near, far)[q // 2]

        def gather(n, carry, q=q, choose=choose, out=out):
            cols = pl.ds(pl.multiple_of(n * tile, tile), tile)
            out[0, q % 2, :, cols] = dot_plain(choose, parts[q, :, cols]).astype(BF)
            return carry

        lax.fori_loop(0, width // tile, gather, 0)


def expert_out(hid_all, down, tables, cap):
    steps, experts, slots, pad = hid_all.shape
    width = down.shape[2]
    slot_row, weight_row, slot_col = tables
    return pl.pallas_call(
        functools.partial(expert_out_kernel, experts, cap),
        grid=(steps,),
        out_shape=[jax.ShapeDtypeStruct((steps, 2, HALF, width), BF)] * 2,
        in_specs=[
            pl.BlockSpec((1, experts, slots, pad), lambda i: (i, 0, 0, 0)),
            pl.BlockSpec((experts, pad, width), lambda i: (0, 0, 0)),
            pl.BlockSpec((1,) + slot_row.shape[1:], lambda i: (i, 0, 0, 0)),
            pl.BlockSpec((1,) + weight_row.shape[1:], lambda i: (i, 0, 0, 0)),
            pl.BlockSpec((1,) + slot_col.shape[1:], lambda i: (i, 0, 0, 0)),
        ],
        out_specs=[pl.BlockSpec((1, 2, HALF, width), lambda i: (i, 0, 0, 0))] * 2,
        scratch_shapes=[pltpu.VMEM((QUARTET, experts * cap, width), BF)],
        compiler_params=pltpu.CompilerParams(vmem_limit_bytes=48 * 1024 * 1024),
        cost_estimate=pl.CostEstimate(
            flops=steps * (2 * slots * experts * width * pad + 2 * QUARTET * HALF * experts * cap * width),
            bytes_accessed=2 * steps * QUARTET * HALF * width + 2 * hid_all.size + 2 * down.size,
            transcendentals=0,
        ),
        name="expert_out",
    )(hid_all, down, slot_row, weight_row, slot_col)


def expert_grads_kernel(dgu, x, hid, d, gate_grad, up_grad, down_grad):
    local = gate_grad.shape[1]
    pad = hid.shape[3]
    width = x.shape[3]
    tile = min(1024, width)

    @pl.when(pl.program_id(1) == 0)
    def _():
        gate_grad[...] = jnp.zeros_like(gate_grad)
        up_grad[...] = jnp.zeros_like(up_grad)
        down_grad[...] = jnp.zeros_like(down_grad)

    def part(n, carry):
        cols = pl.ds(pl.multiple_of(n * tile, tile), tile)
        gate_grad[0, :, cols] += dot_first(dgu[0, 0, :, :pad], x[0, 0, :, cols])[:local]
        up_grad[0, :, cols] += dot_first(dgu[0, 0, :, pad:], x[0, 0, :, cols])[:local]
        down_grad[0, :, cols] += dot_first(hid[0, 0], d[0, 0, :, cols])[:local]
        return carry

    lax.fori_loop(0, width // tile, part, 0)


def expert_grads(kept, local):
    x_all, d_all, hid_all, dgu_all = kept
    steps, experts, slots, width = x_all.shape
    pad = hid_all.shape[3]

    def block(array):
        return pl.BlockSpec((1, 1) + array.shape[2:], lambda e, i: (i, e, 0, 0))

    grad = jax.ShapeDtypeStruct((experts, local, width), F32)
    return pl.pallas_call(
        expert_grads_kernel,
        grid=(experts, steps),
        out_shape=[grad] * 3,
        in_specs=[block(dgu_all), block(x_all), block(hid_all), block(d_all)],
        out_specs=[pl.BlockSpec((1, local, width), lambda e, i: (e, 0, 0))] * 3,
        compiler_params=pltpu.CompilerParams(vmem_limit_bytes=48 * 1024 * 1024),
        cost_estimate=pl.CostEstimate(
            flops=2 * 3 * steps * experts * slots * width * pad,
            bytes_accessed=2 * (x_all.size + d_all.size + hid_all.size + dgu_all.size)
            + 12 * experts * local * width,
            transcendentals=0,
        ),
        name="expert_grads",
    )(dgu_all, x_all, hid_all, d_all)


def mesh_copy(src, dst, sends, arrivals, number, device):
    return pltpu.make_async_remote_copy(
        src_ref=src,
        dst_ref=dst,
        send_sem=sends.at[number],
        recv_sem=arrivals.at[number],
        device_id=device,
        device_id_type=pl.DeviceIdType.MESH,
    )


def plane_neighbours():
    place, column = lax.axis_index("fsdp"), lax.axis_index("tp")
    core, along, across = place % 2, (place // 2) % 2, place // 4
    return (
        (place + 1 - 2 * core, column),
        (place + 2 - 4 * along, column),
        (place + 4 - 8 * across, column),
    )


def column_neighbours(count):
    place, column = lax.axis_index("fsdp"), lax.axis_index("tp")
    return [(place, (column + s) % count) for s in range(1, count)]


def greet(devices):
    barrier = pltpu.get_barrier_semaphore()
    for device in devices:
        pl.semaphore_signal(
            barrier, inc=1, device_id=device, device_id_type=pl.DeviceIdType.MESH
        )
    pl.semaphore_wait(barrier, len(devices))


class ColumnGather:
    def __init__(self, blocks, rows_of, sends, arrivals, base, own=None):
        self.blocks, self.rows_of = blocks, rows_of
        self.own = blocks.at[rows_of(0)] if own is None else own
        self.sends, self.arrivals, self.base = sends, arrivals, base
        self.row = lax.axis_index("tp")
        self.column = column_neighbours(4)

    def direct(self, s):
        place = self.blocks.at[self.rows_of(0)]
        return mesh_copy(
            self.own, place, self.sends, self.arrivals, self.base + s - 1, self.column[s - 1]
        )

    def start(self):
        @pl.when(self.row < 3)
        def _():
            self.direct(1).start()

        @pl.when(self.row > 0)
        def _():
            self.direct(3).start()

        self.direct(2).start()

    def wait(self, b):
        self.direct(4 - b).wait_recv()
        if b == 2:

            @pl.when(self.row == 1)
            def _():
                self.relay(3).start()

            @pl.when(self.row == 2)
            def _():
                self.relay(1).start()

    def relay(self, s):
        place = self.blocks.at[self.rows_of(2)]
        return pltpu.make_async_remote_copy(
            src_ref=place,
            dst_ref=place,
            send_sem=self.sends.at[self.base + 3],
            recv_sem=self.arrivals.at[self.base + 3 - s],
            device_id=self.column[s - 1],
            device_id_type=pl.DeviceIdType.MESH,
        )

    def drain(self):
        @pl.when(self.row < 3)
        def _():
            self.direct(1).wait_send()

        @pl.when(self.row > 0)
        def _():
            self.direct(3).wait_send()

        self.direct(2).wait_send()

        @pl.when(self.row == 1)
        def _():
            self.relay(3).wait_send()

        @pl.when(self.row == 2)
        def _():
            self.relay(1).wait_send()


class ColumnSum:
    def __init__(self, parts, rows_of, landed, relayed, sends, arrivals, base):
        self.parts, self.rows_of, self.landed, self.relayed = parts, rows_of, landed, relayed
        self.sends, self.arrivals, self.base = sends, arrivals, base
        self.row = lax.axis_index("tp")
        self.column = column_neighbours(4)

    def direct(self, s):
        return mesh_copy(
            self.parts.at[self.rows_of(s)],
            self.landed.at[s - 1],
            self.sends,
            self.arrivals,
            self.base + s - 1,
            self.column[s - 1],
        )

    def first_leg(self, s):
        return mesh_copy(
            self.parts.at[self.rows_of(4 - s)],
            self.relayed.at[0],
            self.sends,
            self.arrivals,
            self.base + 3,
            self.column[s - 1],
        )

    def own_part(self, local):
        return pltpu.make_async_copy(self.parts.at[self.rows_of(2)], self.relayed.at[1], local)

    def second_leg(self):
        return mesh_copy(
            self.relayed.at[1],
            self.landed.at[1],
            self.sends,
            self.arrivals,
            self.base + 1,
            self.column[1],
        )

    def start(self, local):
        @pl.when(self.row == 0)
        def _():
            self.first_leg(1).start()

        @pl.when(self.row == 3)
        def _():
            self.first_leg(3).start()

        @pl.when((self.row == 1) | (self.row == 2))
        def _():
            self.own_part(local).start()

        @pl.when(self.row < 3)
        def _():
            self.direct(1).start()

        @pl.when(self.row > 0)
        def _():
            self.direct(3).start()

        @pl.when((self.row == 0) | (self.row == 3))
        def _():
            self.direct(2).start()

    def middle(self, local):
        @pl.when((self.row == 1) | (self.row == 2))
        def _():
            self.own_part(local).wait()
            self.first_leg(1).wait_recv()

            def some(i, carry):
                rows = pl.ds(pl.multiple_of(i * 32, 32), 32)
                self.relayed[1, rows, :] = (
                    self.relayed[0, rows, :].astype(F32) + self.relayed[1, rows, :].astype(F32)
                ).astype(BF)
                return carry

            lax.fori_loop(0, self.relayed.shape[1] // 32, some, 0)
            self.second_leg().start()

    def clear(self):
        @pl.when(self.row == 0)
        def _():
            self.landed[0] = jnp.zeros(self.landed.shape[1:], BF)

        @pl.when(self.row == 3)
        def _():
            self.landed[2] = jnp.zeros(self.landed.shape[1:], BF)

    def total(self, own):
        @pl.when(self.row > 0)
        def _():
            self.direct(1).wait_recv()

        @pl.when(self.row < 3)
        def _():
            self.direct(3).wait_recv()

        self.direct(2).wait_recv()
        total = own.astype(F32)
        for s in range(3):
            total = total + self.landed[s].astype(F32)
        return total

    def drain(self):
        @pl.when(self.row == 0)
        def _():
            self.first_leg(1).wait_send()

        @pl.when(self.row == 3)
        def _():
            self.first_leg(3).wait_send()

        @pl.when(self.row < 3)
        def _():
            self.direct(1).wait_send()

        @pl.when(self.row > 0)
        def _():
            self.direct(3).wait_send()

        self.direct(2).wait_send()


class PlaneGather:
    def __init__(self, own, others, rows_of, sends, arrivals, base):
        self.own, self.others, self.rows_of = own, others, rows_of
        self.sends, self.arrivals, self.base = sends, arrivals, base
        self.partner, self.along, self.across = plane_neighbours()

    def copies(self, b):
        half = self.own.shape[1] // 2
        rows = self.rows_of(b)
        left, right = pl.ds(0, half), pl.ds(half, half)
        other = {r: self.others.at[r - 1] for r in range(1, 8)}
        plan = [
            (self.own.at[rows], other[2].at[rows], self.along),
            (self.own.at[rows], other[4].at[rows], self.across),
            (self.own.at[rows], other[1].at[rows], self.partner),
            (other[2].at[rows, left], other[6].at[rows, left], self.across),
            (other[4].at[rows, right], other[6].at[rows, right], self.along),
            (other[2].at[rows], other[3].at[rows], self.partner),
            (other[4].at[rows], other[5].at[rows], self.partner),
            (other[6].at[rows], other[7].at[rows], self.partner),
        ]
        return [
            mesh_copy(src, dst, self.sends, self.arrivals, self.base + 8 * b + i, device)
            for i, (src, dst, device) in enumerate(plan)
        ]

    def start(self, b):
        for copy in self.copies(b)[:3]:
            copy.start()

    def forward(self, b):
        along, across, _, left, right, third, fifth, _ = self.copies(b)
        along.wait_recv()
        left.start()
        third.start()
        across.wait_recv()
        right.start()
        fifth.start()

    def last(self, b):
        copies = self.copies(b)
        copies[3].wait_recv()
        copies[4].wait_recv()
        copies[7].start()

    def arrived(self, b, numbers):
        copies = self.copies(b)
        for i in numbers:
            copies[i].wait_recv()

    def drain(self, b):
        for copy in self.copies(b):
            copy.wait_send()


def block_rows(columns, size):
    row = lax.axis_index("tp")
    return lambda s: pl.ds(pl.multiple_of((row + s) % columns * size, size), size)


def slots_of(table, experts, columns, size, b, q):
    place = pl.ds(pl.multiple_of((lax.axis_index("tp") + b) % columns * size, size), size)
    rows = []
    for e in range(experts):
        low, high = 2 * q * experts + e, (2 * q + 1) * experts + e
        rows.append(
            jnp.concatenate([table[low : low + 1, place], table[high : high + 1, place]], axis=1)
        )
    return jnp.concatenate(rows, axis=0)


def token_sums(table, experts, columns, size, wide, b, slots, keep):
    width = slots.shape[2]
    tile = min(1024, width)
    for q in range(QUARTET):
        entries = slots_of(table, experts, columns, size, b, q)
        entries = jnp.concatenate(
            [entries, jnp.full((8 - experts, HALF), NO_SLOT, F32)], axis=0
        )
        choose = jnp.where(select_cols(entries.T, experts, wide), 1.0, 0.0).astype(BF)

        def gather(n, carry, q=q, choose=choose):
            cols = pl.ds(pl.multiple_of(n * tile, tile), tile)
            keep(q, cols, dot_plain(choose, slots[q, :, cols]).astype(BF))
            return carry

        lax.fori_loop(0, width // tile, gather, 0)


def expert_kernel(cap, columns, size, *refs):
    (
        attn_in,
        tokens_in,
        cotan_in,
        gate_in,
        up_in,
        down_in,
        gain_ref,
        raw_ref,
        mixed_out,
        ffn_all,
        dx_out,
        slots_out,
        weights_out,
        x_all,
        d_all,
        hid_all,
        dgu_all,
        x_others,
        dy_others,
        theirs,
        links,
        attn_v,
        tokens_v,
        arrived_v,
        relayed_v,
        mixed_v,
        ffn_v,
        xb,
        db,
        gate_up,
        down,
        xs,
        ds,
        dxs,
        others,
        chip,
        stage,
        hid,
        dgu,
        slot_table,
        weight_table,
        sends,
        arrivals,
        local,
        loads,
        sum_local,
        spill,
    ) = refs
    count = QUARTET
    previous = {2: 0, 1: 2, 3: 1}
    experts, local_hidden = gate_in.shape[:2]
    width = xb.shape[2]
    pad = down.shape[1]
    tile = min(1024, width)
    wide = 2 * cap
    rows_of = block_rows(columns, size)
    partner, along, across = plane_neighbours()
    column = column_neighbours(columns)
    number = 0

    def reserve(amount):
        nonlocal number
        number += amount
        return number - amount

    x_gather = PlaneGather(ffn_all, x_others, rows_of, sends, arrivals, reserve(8 * columns))
    dy_gather = PlaneGather(cotan_in, dy_others, rows_of, sends, arrivals, reserve(8 * columns))
    gather = ColumnGather(ffn_all, rows_of, sends, arrivals, reserve(4))
    summed = ColumnSum(attn_in, rows_of, arrived_v, relayed_v, sends, arrivals, reserve(4))
    plane = PlaneSum(
        lambda r, h: others.at[r // 2],
        chip,
        theirs,
        links,
        stage,
        sends,
        arrivals,
        reserve(plane_sum_sizes(columns)[0]),
        sum_local,
    )

    greet([partner, along, across] + column)
    summed.start(local.at[2])
    first = [
        pltpu.make_async_copy(attn_in.at[rows_of(0)], attn_v, local.at[0]),
        pltpu.make_async_copy(tokens_in, tokens_v, local.at[1]),
    ]
    for copy in first:
        copy.start()
    order = (0, 2, 1, 3)
    for b in order:
        dy_gather.start(b)
    if pad > local_hidden:
        rest = pad - local_hidden
        for e in range(experts):
            for ref, start in ((gate_up, local_hidden), (gate_up, pad + local_hidden), (down, local_hidden)):
                ref[e, start : start + rest, :] = jnp.zeros((rest, width), BF)
    weights_in = []
    for e in range(experts):
        weights_in += [
            pltpu.make_async_copy(
                gate_in.at[e], gate_up.at[e, pl.ds(0, local_hidden)], local.at[3 + 3 * e]
            ),
            pltpu.make_async_copy(
                up_in.at[e], gate_up.at[e, pl.ds(pad, local_hidden)], local.at[4 + 3 * e]
            ),
            pltpu.make_async_copy(
                down_in.at[e], down.at[e, pl.ds(0, local_hidden)], local.at[5 + 3 * e]
            ),
        ]
    for copy in weights_in:
        copy.start()

    summed.clear()
    summed.middle(local.at[2])

    earlier = lax.broadcasted_iota(jnp.int32, (size, size), 0)
    later = lax.broadcasted_iota(jnp.int32, (size, size), 1)
    before = jnp.where(earlier < later, 1.0, 0.0).astype(BF)
    own_first = (lax.axis_index("fsdp") * experts).astype(F32)
    for r in range(8):
        for e in range(experts):
            member = jnp.zeros((1, SEQ), F32)
            weight = jnp.zeros((1, SEQ), F32)
            for pick in range(TOPK):
                same = raw_ref[r, pick : pick + 1, :] == own_first + float(e)
                member = jnp.where(same, 1.0, member)
                weight = weight + jnp.where(
                    same, raw_ref[r, RAW_ROWS + pick : RAW_ROWS + pick + 1, :], 0.0
                )
            slot_table[r * experts + e : r * experts + e + 1, :] = member
            weight_table[r * experts + e : r * experts + e + 1, :] = weight
    second = lax.broadcasted_iota(jnp.int32, (8 * experts, size), 0) // experts % 2
    shift = second.astype(F32) * float(cap)
    for b in range(columns):
        cols = pl.ds(b * size, size)
        member = slot_table[:, cols]
        rank = dot_plain(member.astype(BF), before)
        slot_table[:, cols] = jnp.where(member > 0.5, rank + shift, NO_SLOT)
    slots_out[...] = slot_table[...]
    weights_out[...] = weight_table[...]

    for copy in first:
        copy.wait()
    total = summed.total(attn_v[...]) + tokens_v[...].astype(F32)
    mixed_v[...] = total
    inverse = lax.rsqrt(jnp.mean(total * total, axis=1, keepdims=True) + EPSILON)
    ffn_v[...] = (total * inverse * gain_ref[...]).astype(BF)
    own_copy = pltpu.make_async_copy(ffn_v, ffn_all.at[rows_of(0)], local.at[0])
    own_copy.start()
    mixed_copy = pltpu.make_async_copy(mixed_v, mixed_out, local.at[1])
    mixed_copy.start()
    own_copy.wait()

    gather.start()

    def enter(b):
        if b > 0:
            gather.wait(b)
        x_gather.start(b)

    def ready(b):
        x_gather.last(b)
        dy_gather.last(b)
        x_gather.arrived(b, [2, 5, 6, 7])
        dy_gather.arrived(b, [2, 5, 6, 7])

    def source(own, gathered, r):
        return own if r == 0 else gathered.at[r - 1]

    def load(b, k):
        own, gathered, target = ((ffn_all, x_others, xb), (cotan_in, dy_others, db))[k]
        return [
            pltpu.make_async_copy(
                source(own, gathered, r).at[rows_of(b)],
                target.at[r // 2, pl.ds(r % 2 * size, size)],
                loads.at[8 * k + r],
            )
            for r in range(8)
        ]

    def combine(b, keep):
        token_sums(slot_table, experts, columns, size, wide, b, dxs, keep)

    def spills(b):
        return [
            pltpu.make_async_copy(xs, x_all.at[b], spill.at[0]),
            pltpu.make_async_copy(ds, d_all.at[b], spill.at[1]),
            pltpu.make_async_copy(hid.at[b], hid_all.at[b], spill.at[2]),
            pltpu.make_async_copy(dgu, dgu_all.at[b], spill.at[3]),
        ]

    def front(b):
        x_load, dy_load = load(b, 0), load(b, 1)
        for copy in x_load + dy_load:
            copy.start()
        if b == 0:
            for copy in weights_in:
                copy.wait()
        if b > 0:
            for copy in spills(previous[b]):
                copy.wait()
        for q in range(count):
            for copy in x_load[2 * q : 2 * q + 2] + dy_load[2 * q : 2 * q + 2]:
                copy.wait()
            hit = select_rows(slots_of(slot_table, experts, columns, size, b, q), experts, wide)
            weights = slot_weights(hit, slots_of(weight_table, experts, columns, size, b, q), experts, wide)
            choose = jnp.where(hit, 1.0, 0.0).astype(BF)

            def spread(n, carry, q=q, choose=choose, weights=weights):
                cols = pl.ds(pl.multiple_of(n * tile, tile), tile)
                rows = dot_plain(choose, xb[q, :, cols])
                grads = dot_plain(choose, db[q, :, cols]) * weights
                for e in range(experts):
                    low, high = e * wide, (e + 1) * wide
                    xs[e, q * wide : (q + 1) * wide, cols] = rows[low:high].astype(BF)
                    ds[e, q * wide : (q + 1) * wide, cols] = grads[low:high].astype(BF)
                return carry

            lax.fori_loop(0, width // tile, spread, 0)
        out_copies = spills(b)
        out_copies[0].start()
        out_copies[1].start()

        def one_expert(e, carry):
            both = dot_rows(xs[e], gate_up[e])
            gate_pre, up_pre = both[:, :pad], both[:, pad:]
            d_hidden = dot_rows(ds[e], down[e])
            sigmoid = jax.nn.sigmoid(gate_pre)
            silu = gate_pre * sigmoid
            hid[b, e] = (silu * up_pre).astype(BF)
            gate_grad = d_hidden * up_pre * (sigmoid * (1.0 + gate_pre * (1.0 - sigmoid)))
            dgu[e] = jnp.concatenate([gate_grad, d_hidden * silu], axis=1).astype(BF)

            def back(n, inner):
                cols = pl.ds(pl.multiple_of(n * tile, tile), tile)
                part = dot_plain(dgu[e], gate_up[e, :, cols]).astype(BF)
                for q in range(count):
                    dxs[q, pl.ds(pl.multiple_of(e * wide, wide), wide), cols] = part[
                        q * wide : (q + 1) * wide
                    ]
                return inner

            lax.fori_loop(0, width // tile, back, 0)
            return carry

        lax.fori_loop(0, experts, one_expert, 0)
        out_copies[2].start()
        out_copies[3].start()
        if b > 0:
            for i in range(4):
                plane.pair(i, previous[b]).wait_send()

        def keep(q, cols, value):
            chip[q, b, :, cols] = value[:size]
            others[q, :, cols] = value[size:]

        combine(b, keep)
        for i in range(4):
            plane.pair(i, b).start()

    dy_gather.forward(0)
    enter(0)
    x_gather.forward(0)
    dy_gather.forward(2)
    enter(2)
    dy_gather.forward(1)
    enter(1)
    x_gather.forward(2)
    ready(0)
    front(0)
    dy_gather.forward(3)
    enter(3)
    x_gather.forward(1)
    ready(2)
    front(2)
    x_gather.forward(3)
    plane.send_first([0], False)
    ready(1)
    front(1)
    plane.send_first([2], False)
    plane.send_second([0])
    ready(3)
    front(3)
    plane.send_first([1], False)
    plane.send_second([2])
    done = {}

    def close(b):
        plane.finish([b])
        done[b] = pltpu.make_async_copy(chip.at[0, b], dx_out.at[rows_of(b)], loads.at[b])
        done[b].start()

    plane.send_first([3], False)
    close(0)
    plane.send_second([1])
    close(2)
    plane.send_second([3])
    close(1)
    close(3)
    for copy in spills(3):
        copy.wait()
    for b in range(columns):
        done[b].wait()
    mixed_copy.wait()

    for b in range(columns):
        x_gather.drain(b)
        dy_gather.drain(b)
    gather.drain()
    summed.drain()
    plane.drain(3)


def expert_call(attn_part, tokens, cotan_all, gate, up, down, gain, raw, cap):
    columns = lax.axis_size("tp")
    size, width = tokens.shape
    experts, local_hidden, _ = gate.shape
    pad = -(-local_hidden // 128) * 128
    slots = 8 * cap
    anywhere = pl.BlockSpec(memory_space=pl.ANY)
    held = pl.BlockSpec(memory_space=pltpu.VMEM)

    def array(*dims, kind=BF):
        return jax.ShapeDtypeStruct(dims, kind)

    landing, scratch = plane_sum_space(columns, size, width)
    remote, near = plane_sum_sizes(columns)
    remote = remote + 16 * columns + 8
    results = pl.pallas_call(
        functools.partial(expert_kernel, cap, columns, size),
        out_shape=[
            array(size, width, kind=F32),
            array(SEQ, width),
            array(SEQ, width),
            array(8 * experts, SEQ, kind=F32),
            array(8 * experts, SEQ, kind=F32),
            array(columns, experts, slots, width),
            array(columns, experts, slots, width),
            array(columns, experts, slots, pad),
            array(columns, experts, slots, 2 * pad),
            array(7, SEQ, width),
            array(7, SEQ, width),
        ]
        + landing,
        in_specs=[anywhere] * 6 + [held] * 2,
        out_specs=[anywhere] * 3 + [held] * 2 + [anywhere] * 8,
        scratch_shapes=[
            pltpu.VMEM((size, width), BF),
            pltpu.VMEM((size, width), BF),
            pltpu.VMEM((columns - 1, size, width), BF),
            pltpu.VMEM((2, size, width), BF),
            pltpu.VMEM((size, width), F32),
            pltpu.VMEM((size, width), BF),
            pltpu.VMEM((QUARTET, HALF, width), BF),
            pltpu.VMEM((QUARTET, HALF, width), BF),
            pltpu.VMEM((experts, 2 * pad, width), BF),
            pltpu.VMEM((experts, pad, width), BF),
            pltpu.VMEM((experts, slots, width), BF),
            pltpu.VMEM((experts, slots, width), BF),
            pltpu.VMEM((QUARTET, 2 * experts * cap, width), BF),
            pltpu.VMEM((4, size, width), BF),
        ]
        + scratch
        + [
            pltpu.VMEM((columns, experts, slots, pad), BF),
            pltpu.VMEM((experts, slots, 2 * pad), BF),
            pltpu.VMEM((8 * experts, SEQ), F32),
            pltpu.VMEM((8 * experts, SEQ), F32),
            pltpu.SemaphoreType.DMA((remote,)),
            pltpu.SemaphoreType.DMA((remote,)),
            pltpu.SemaphoreType.DMA((3 + 3 * experts,)),
            pltpu.SemaphoreType.DMA((16,)),
            pltpu.SemaphoreType.DMA((near,)),
            pltpu.SemaphoreType.DMA((4,)),
        ],
        compiler_params=pltpu.CompilerParams(
            collective_id=1, has_side_effects=True, vmem_limit_bytes=67_043_328
        ),
        cost_estimate=pl.CostEstimate(
            flops=16 * SEQ * experts * cap * width * 8,
            bytes_accessed=800 * SEQ * width,
            transcendentals=0,
        ),
        name="experts",
    )(attn_part, tokens, cotan_all, gate, up, down, gain, raw)
    return results[:9]


def first_kernel(columns, size, kinds, *refs):
    amount = len(kinds)
    tokens_in, own_in = refs[0], refs[1 : 1 + amount]
    tokens_all, alls = refs[1 + amount], refs[2 + amount : 2 + 2 * amount]
    tokens_v, held = refs[2 + 2 * amount], refs[3 + 2 * amount : 3 + 3 * amount]
    sends, arrivals, local = refs[3 + 3 * amount :]
    partner, along, across = plane_neighbours()
    column = column_neighbours(columns)
    rows_of = block_rows(columns, size)
    place = lax.axis_index("fsdp")
    devices = {
        0: place,
        1: partner[0],
        2: along[0],
        4: across[0],
        6: along[0] + across[0] - place,
    }
    greet([partner, along, across] + column)
    gather = ColumnGather(tokens_all, rows_of, sends, arrivals, 8 * amount, tokens_in)
    gather.start()
    plans = []
    for k, kind in enumerate(kinds):
        own, everything = own_in[k], alls[k]
        rows, cols = own.shape
        top, bottom = pl.ds(0, rows // 2), pl.ds(rows // 2, rows // 2)
        whole = pl.ds(0, rows)

        def spot(r, hop, part, kind=kind, everything=everything, cols=cols):
            if kind == "relative":
                return everything.at[r ^ hop, part]
            if kind == "rows":
                return everything.at[devices[r], part]
            start = pl.multiple_of(devices[r] * cols, cols)
            return everything.at[part, pl.ds(start, cols)]

        plan = [
            (own, spot(0, 2, whole), along),
            (own, spot(0, 4, whole), across),
            (own, spot(0, 1, whole), partner),
            (spot(2, 0, top), spot(2, 4, top), across),
            (spot(4, 0, bottom), spot(4, 2, bottom), along),
            (spot(2, 0, whole), spot(2, 1, whole), partner),
            (spot(4, 0, whole), spot(4, 1, whole), partner),
            (spot(6, 0, whole), spot(6, 1, whole), partner),
        ]
        plans.append(
            [
                mesh_copy(src, dst, sends, arrivals, 8 * k + i, device)
                for i, (src, dst, device) in enumerate(plan)
            ]
        )
    for copies in plans:
        for copy in copies[:3]:
            copy.start()
    here = [pltpu.make_async_copy(tokens_in, tokens_v, local.at[0])]
    there = [pltpu.make_async_copy(tokens_v, tokens_all.at[rows_of(0)], local.at[0])]
    for k, kind in enumerate(kinds):
        rows, cols = own_in[k].shape
        if kind == "relative":
            spot_here = alls[k].at[0]
        elif kind == "rows":
            spot_here = alls[k].at[place]
        else:
            spot_here = alls[k].at[:, pl.ds(pl.multiple_of(place * cols, cols), cols)]
        here.append(pltpu.make_async_copy(own_in[k], held[k], local.at[1 + k]))
        there.append(pltpu.make_async_copy(held[k], spot_here, local.at[1 + k]))
    for copy in here:
        copy.start()
    for copy in here:
        copy.wait()
    for copy in there:
        copy.start()
    for n, copies in enumerate(plans):
        copies[0].wait_recv()
        copies[3].start()
        copies[5].start()
        copies[1].wait_recv()
        copies[4].start()
        copies[6].start()
        if n == amount - 2:
            gather.wait(2)
    for copies in plans:
        copies[3].wait_recv()
        copies[4].wait_recv()
        copies[7].start()
    for copies in plans:
        for i in (2, 5, 6, 7):
            copies[i].wait_recv()
    gather.wait(1)
    gather.wait(3)
    for copy in there:
        copy.wait()
    gather.drain()
    for copies in plans:
        for copy in copies:
            copy.wait_send()


def first_call(tokens, owns, kinds):
    columns = lax.axis_size("tp")
    size, width = tokens.shape
    anywhere = pl.BlockSpec(memory_space=pl.ANY)
    copies = 8 * len(owns) + 4

    def gathered(own, kind):
        rows, cols = own.shape
        return (rows, 8 * cols) if kind == "columns" else (8, rows, cols)

    return pl.pallas_call(
        functools.partial(first_kernel, columns, size, kinds),
        out_shape=[jax.ShapeDtypeStruct((columns * size, width), BF)]
        + [jax.ShapeDtypeStruct(gathered(own, kind), own.dtype) for own, kind in zip(owns, kinds)],
        in_specs=[anywhere] * (1 + len(owns)),
        out_specs=[anywhere] * (1 + len(owns)),
        scratch_shapes=[pltpu.VMEM((size, width), BF)]
        + [pltpu.VMEM(own.shape, own.dtype) for own in owns]
        + [
            pltpu.SemaphoreType.DMA((copies,)),
            pltpu.SemaphoreType.DMA((copies,)),
            pltpu.SemaphoreType.DMA((1 + len(owns),)),
        ],
        compiler_params=pltpu.CompilerParams(collective_id=2, has_side_effects=True),
        cost_estimate=pl.CostEstimate(
            flops=0, bytes_accessed=240 * SEQ * width, transcendentals=0
        ),
        name="first_gather",
    )(tokens, *owns)


class PlaneSum:
    def __init__(self, source, chip, theirs, links, stage, sends, arrivals, base, local):
        self.source, self.chip, self.theirs, self.links = source, chip, theirs, links
        self.stage, self.sends, self.arrivals, self.base = stage, sends, arrivals, base
        self.local = local
        self.parts, self.rows = chip.shape[1], chip.shape[2]
        self.partner, self.along, self.across = plane_neighbours()

    def pair(self, i, h):
        return mesh_copy(
            self.source(2 * i + 1, h),
            self.theirs.at[i, h],
            self.sends,
            self.arrivals,
            self.base + i * self.parts + h,
            self.partner,
        )

    def mine(self, i, h):
        return pltpu.make_async_copy(
            self.source(2 * i, h), self.chip.at[i, h], self.local.at[4 + i * self.parts + h]
        )

    def begin(self):
        for i in (3, 1, 2, 0):
            for h in range(self.parts):
                self.pair(i, h).start()
                self.mine(i, h).start()

    def fetch(self, landed, slot):
        size = landed.shape[0]
        return pltpu.make_async_copy(
            landed, self.stage.at[slot, pl.ds(0, size)], self.local.at[slot]
        )

    def add(self, i, h, start, size, slot):
        some = min(32, size)

        def one(n, carry):
            rows = pl.ds(pl.multiple_of(start + n * some, some), some)
            from_rows = pl.ds(pl.multiple_of(n * some, some), some)
            self.chip[i, h, rows, :] = (
                self.chip[i, h, rows, :].astype(F32) + self.stage[slot, from_rows, :].astype(F32)
            ).astype(BF)
            return carry

        lax.fori_loop(0, size // some, one, 0)

    def send_first(self, parts=None, fetched=True):
        for h in range(self.parts) if parts is None else parts:
            for i in (3, 1, 2, 0):
                self.pair(i, h).wait_recv()
                self.fetch(self.theirs.at[i, h], i).start()
            for i in (3, 1, 2, 0):
                if fetched:
                    self.mine(i, h).wait()
                self.fetch(self.theirs.at[i, h], i).wait()
                self.add(i, h, 0, self.rows, i)
                if i == 3:
                    self.send(1, [h])
                if i == 2:
                    self.send(0, [h])

    def link(self, stage_number, side, h):
        first_hop, second_hop = (
            (self.along, self.across) if side == 0 else (self.across, self.along)
        )
        near, far = (1, 2) if side == 0 else (2, 1)
        i = (near, 3, far)[stage_number]
        place = (stage_number * 2 + side) * self.parts + h
        rows = pl.ds(side * (self.rows // 2), self.rows // 2)
        return mesh_copy(
            self.chip.at[i, h, rows],
            self.links.at[place],
            self.sends,
            self.arrivals,
            self.base + 4 * self.parts + place,
            second_hop if stage_number == 2 else first_hop,
        )

    def landed(self, stage_number, side, h):
        return self.links.at[(stage_number * 2 + side) * self.parts + h]

    def send(self, stage_number, parts=None):
        for h in range(self.parts) if parts is None else parts:
            for side in range(2):
                self.link(stage_number, side, h).start()

    def send_second(self, parts=None):
        half = self.rows // 2
        for h in range(self.parts) if parts is None else parts:
            for side in range(2):
                self.link(1, side, h).wait_recv()
                self.fetch(self.landed(1, side, h), side).start()
            for side in range(2):
                self.fetch(self.landed(1, side, h), side).wait()
                self.add((2, 1)[side], h, side * half, half, side)
                self.link(2, side, h).start()

    def finish(self, parts=None):
        half = self.rows // 2
        for h in range(self.parts) if parts is None else parts:
            for stage_number in (0, 2):
                for side in range(2):
                    self.link(stage_number, side, h).wait_recv()
                    self.fetch(self.landed(stage_number, side, h), stage_number + side).start()
            for stage_number in (0, 2):
                for side in range(2):
                    slot = stage_number + side
                    self.fetch(self.landed(stage_number, side, h), slot).wait()
                    self.add(0, h, side * half, half, slot)

    def drain(self, first_part=0):
        for h in range(self.parts):
            for i in range(4):
                if h >= first_part:
                    self.pair(i, h).wait_send()
            for stage_number in range(3):
                for side in range(2):
                    self.link(stage_number, side, h).wait_send()


def plane_sum_sizes(parts):
    return 10 * parts, 4 + 4 * parts


def plane_sum_space(parts, rows, width):
    landing = [
        jax.ShapeDtypeStruct((4, parts, rows, width), BF),
        jax.ShapeDtypeStruct((6 * parts, rows // 2, width), BF),
    ]
    scratch = [pltpu.VMEM((4, parts, rows, width), BF), pltpu.VMEM((4, rows, width), BF)]
    return landing, scratch


def middle_kernel(cap, columns, size, experts, steps, local_hidden, *refs):
    (
        d_ffn_in,
        mixed_in,
        cotan_in,
        gain_ref,
        slot_table,
        weight_table,
        down_in,
        x_all,
        d_all,
        hid_all,
        dgu_all,
        d_mixed_out,
        d_proj_all,
        gain_out,
        routed_out,
        gate_grad,
        up_grad,
        down_grad,
        theirs,
        links,
        chip,
        stage,
        own_v,
        arrived_v,
        relayed_v,
        mixed_v,
        cotan_v,
        proj_v,
        xk,
        dk,
        hk,
        gk,
        totals,
        hid,
        down,
        parts,
        others,
        sends,
        arrivals,
        local,
        sum_local,
        work,
        written,
    ) = refs
    partner, along, across = plane_neighbours()
    column = column_neighbours(columns)
    greet([partner, along, across] + column)
    plane = PlaneSum(
        lambda r, h: others.at[h % 2, r // 2],
        chip,
        theirs,
        links,
        stage,
        sends,
        arrivals,
        0,
        sum_local,
    )
    base = plane_sum_sizes(columns)[0]
    rows_of = block_rows(columns, size)
    summed = ColumnSum(d_ffn_in, rows_of, arrived_v, relayed_v, sends, arrivals, base)
    gather = ColumnGather(d_proj_all, rows_of, sends, arrivals, base + 4)
    summed.start(local.at[3])
    first = [
        pltpu.make_async_copy(d_ffn_in.at[rows_of(0)], own_v, local.at[0]),
        pltpu.make_async_copy(mixed_in, mixed_v, local.at[1]),
        pltpu.make_async_copy(cotan_in, cotan_v, local.at[2]),
    ]
    for copy in first:
        copy.start()
    width = xk.shape[2]
    pad = hk.shape[2]
    tile = min(1024, width)
    hidden_in = [pltpu.make_async_copy(hid_all.at[b], hid.at[b], local.at[4 + b]) for b in range(columns)]
    down_copies = [
        pltpu.make_async_copy(
            down_in.at[e], down.at[e, pl.ds(0, local_hidden)], local.at[4 + columns + e]
        )
        for e in range(experts)
    ]
    for copy in down_copies + hidden_in:
        copy.start()
    summed.clear()
    rest = down.shape[1] - local_hidden
    if rest > 0:
        for e in range(experts):
            down[e, local_hidden:, :] = jnp.zeros((rest, down.shape[2]), BF)
    for copy in down_copies:
        copy.wait()
    wide = 2 * cap

    def out_part(b):
        hidden_in[b].wait()
        weights = [
            slot_weights(
                select_rows(slots_of(slot_table, experts, columns, size, b, q), experts, wide),
                slots_of(weight_table, experts, columns, size, b, q),
                experts,
                wide,
            )
            for q in range(QUARTET)
        ]
        for e in range(experts):

            def one_tile(n, carry, e=e):
                cols = pl.ds(pl.multiple_of(n * tile, tile), tile)
                rows = dot_plain(hid[b, e], down[e, :, cols])
                for q in range(QUARTET):
                    parts[q, e * wide : (e + 1) * wide, cols] = (
                        rows[q * wide : (q + 1) * wide] * weights[q][e * wide : (e + 1) * wide]
                    ).astype(BF)
                return carry

            lax.fori_loop(0, width // tile, one_tile, 0)
        if b > 1:
            for i in range(4):
                plane.pair(i, b - 2).wait_send()

        def keep(q, cols, value):
            chip[q, b, :, cols] = value[:size]
            others[b % 2, q, :, cols] = value[size:]

        token_sums(slot_table, experts, columns, size, wide, b, parts, keep)
        for i in range(4):
            plane.pair(i, b).start()

    jobs = [(e, step) for e in range(experts) for step in range(steps)]

    def fetch(k):
        e, step = jobs[k]
        slot = k % 2
        return [
            pltpu.make_async_copy(x_all.at[step, e], xk.at[slot], work.at[slot, 0]),
            pltpu.make_async_copy(d_all.at[step, e], dk.at[slot], work.at[slot, 1]),
            pltpu.make_async_copy(hid_all.at[step, e], hk.at[slot], work.at[slot, 2]),
            pltpu.make_async_copy(dgu_all.at[step, e], gk.at[slot], work.at[slot, 3]),
        ]

    def write(e):
        return [
            pltpu.make_async_copy(
                totals.at[e % 2, i, pl.ds(0, local_hidden)], grad.at[e], written.at[e % 2, i]
            )
            for i, grad in enumerate((gate_grad, up_grad, down_grad))
        ]

    def job(k):
        e, step = jobs[k]
        slot, place = k % 2, e % 2
        if k + 1 < len(jobs):
            for copy in fetch(k + 1):
                copy.start()
        for copy in fetch(k):
            copy.wait()
        if step == 0 and e > 1:
            for copy in write(e - 2):
                copy.wait()

        def one(n, carry):
            cols = pl.ds(pl.multiple_of(n * tile, tile), tile)
            found = [
                dot_first(gk[slot, :, :pad], xk[slot, :, cols]),
                dot_first(gk[slot, :, pad:], xk[slot, :, cols]),
                dot_first(hk[slot], dk[slot, :, cols]),
            ]
            for i, value in enumerate(found):
                if step == 0:
                    totals[place, i, :, cols] = value
                else:
                    totals[place, i, :, cols] += value
            return carry

        lax.fori_loop(0, width // tile, one, 0)
        if step == steps - 1:
            for copy in write(e):
                copy.start()

    out_part(0)
    out_part(1)
    summed.middle(local.at[3])
    plane.send_first([0], False)
    out_part(2)
    plane.send_first([1], False)
    for copy in fetch(0):
        copy.start()
    out_part(3)
    plane.send_first([2], False)
    job(0)
    plane.send_first([3], False)

    for copy in first:
        copy.wait()
    total = summed.total(own_v[...])
    mixed = mixed_v[...]
    inverse = lax.rsqrt(jnp.mean(mixed * mixed, axis=1, keepdims=True) + EPSILON)
    unit = mixed * inverse
    scaled = total * gain_ref[...]
    gain_out[...] = jnp.sum(total * unit, axis=0, keepdims=True)
    back = inverse * (scaled - unit * jnp.mean(scaled * unit, axis=1, keepdims=True))
    d_mixed = cotan_v[...].astype(F32) + back
    mixed_v[...] = d_mixed
    proj_v[...] = d_mixed.astype(BF)
    own_copy = pltpu.make_async_copy(proj_v, d_proj_all.at[rows_of(0)], local.at[0])
    own_copy.start()
    mixed_copy = pltpu.make_async_copy(mixed_v, d_mixed_out, local.at[1])
    mixed_copy.start()
    own_copy.wait()
    gather.start()
    for b in range(columns):
        if b + 1 < len(jobs):
            job(b + 1)
        plane.send_second([b])
        if b == 1:
            gather.wait(2)
    for b in range(columns):
        if columns + 1 + b < len(jobs):
            job(columns + 1 + b)
        if b < columns - 1:
            plane.finish([b])
    for k in range(2 * columns + 1, len(jobs)):
        job(k)
    plane.finish([columns - 1])
    done = [
        pltpu.make_async_copy(chip.at[0, h], routed_out.at[rows_of(h)], sum_local.at[4 + h])
        for h in range(columns)
    ]
    for copy in done:
        copy.start()
    gather.wait(1)
    gather.wait(3)
    for copy in done + [mixed_copy]:
        copy.wait()
    for e in range(max(0, experts - 2), experts):
        for copy in write(e):
            copy.wait()
    plane.drain(2)
    gather.drain()
    summed.drain()


def middle_call(d_ffn, mixed, cotan, gain, tables, down, kept, cap):
    columns = lax.axis_size("tp")
    size, width = cotan.shape
    x_all, d_all, hid_all, dgu_all = kept
    steps, experts, slots, pad = hid_all.shape
    local_hidden = down.shape[1]
    anywhere = pl.BlockSpec(memory_space=pl.ANY)
    held = pl.BlockSpec(memory_space=pltpu.VMEM)
    landing, scratch = plane_sum_space(columns, size, width)
    remote, near = plane_sum_sizes(columns)
    remote = remote + 8
    grad = jax.ShapeDtypeStruct((experts, local_hidden, width), F32)
    results = pl.pallas_call(
        functools.partial(middle_kernel, cap, columns, size, experts, steps, local_hidden),
        out_shape=[
            jax.ShapeDtypeStruct((size, width), F32),
            jax.ShapeDtypeStruct((SEQ, width), BF),
            jax.ShapeDtypeStruct((1, width), F32),
            jax.ShapeDtypeStruct((SEQ, width), BF),
            grad,
            grad,
            grad,
        ]
        + landing,
        in_specs=[anywhere] * 3 + [held] * 3 + [anywhere] * 5,
        out_specs=[anywhere] * 2 + [held] + [anywhere] * 6,
        scratch_shapes=scratch
        + [
            pltpu.VMEM((size, width), BF),
            pltpu.VMEM((columns - 1, size, width), BF),
            pltpu.VMEM((2, size, width), BF),
            pltpu.VMEM((size, width), F32),
            pltpu.VMEM((size, width), BF),
            pltpu.VMEM((size, width), BF),
            pltpu.VMEM((2, slots, width), BF),
            pltpu.VMEM((2, slots, width), BF),
            pltpu.VMEM((2, slots, pad), BF),
            pltpu.VMEM((2, slots, 2 * pad), BF),
            pltpu.VMEM((2, 3, pad, width), F32),
            pltpu.VMEM((steps, experts, slots, pad), BF),
            pltpu.VMEM((experts, pad, width), BF),
            pltpu.VMEM((QUARTET, 2 * experts * cap, width), BF),
            pltpu.VMEM((2, 4, size, width), BF),
            pltpu.SemaphoreType.DMA((remote,)),
            pltpu.SemaphoreType.DMA((remote,)),
            pltpu.SemaphoreType.DMA((4 + columns + experts,)),
            pltpu.SemaphoreType.DMA((near,)),
            pltpu.SemaphoreType.DMA((2, 4)),
            pltpu.SemaphoreType.DMA((2, 3)),
        ],
        compiler_params=pltpu.CompilerParams(
            collective_id=3, has_side_effects=True, vmem_limit_bytes=67_043_328
        ),
        cost_estimate=pl.CostEstimate(
            flops=2 * 3 * steps * experts * slots * width * pad,
            bytes_accessed=300 * SEQ * width,
            transcendentals=0,
        ),
        name="middle",
    )(d_ffn, mixed, cotan, gain, *tables, down, x_all, d_all, hid_all, dgu_all)
    return results[:7]


def last_kernel(columns, size, latent_start, latent_width, *refs):
    (
        d_normed_in,
        tokens_in,
        d_mixed_in,
        gain_ref,
        joint_in,
        up_in,
        out_in,
        sums_in,
        grad_out,
        joint_out,
        up_out,
        out_out,
        latent_out,
        sums_out,
        joint_theirs,
        joint_links,
        up_theirs,
        up_links,
        out_theirs,
        out_links,
        joint_chip,
        joint_stage,
        up_chip,
        up_stage,
        out_chip,
        out_stage,
        own_v,
        arrived_v,
        relayed_v,
        tokens_v,
        mixed_v,
        running,
        sums_v,
        latent_v,
        sends,
        arrivals,
        local,
        joint_local,
        up_local,
        out_local,
    ) = refs
    partner, along, across = plane_neighbours()
    column = column_neighbours(columns)
    place, row = lax.axis_index("fsdp"), lax.axis_index("tp")
    core, right, above = place % 2, (place // 2) % 2, place // 4

    def absolute(r):
        return (
            (above + r // 4) % 2 * 4 + (right + r // 2 % 2) % 2 * 2 + (core + r % 2) % 2
        )

    greet([partner, along, across] + column)
    each = plane_sum_sizes(1)[0]
    joint_rows, up_rows = joint_chip.shape[2], up_chip.shape[2]
    out_cols = out_chip.shape[3]

    def by_rows(ref, count):
        return lambda r, h: ref.at[pl.ds(pl.multiple_of(absolute(r) * count, count), count)]

    joint = PlaneSum(
        by_rows(joint_in, joint_rows),
        joint_chip,
        joint_theirs,
        joint_links,
        joint_stage,
        sends,
        arrivals,
        0,
        joint_local,
    )
    up = PlaneSum(
        by_rows(up_in, up_rows),
        up_chip,
        up_theirs,
        up_links,
        up_stage,
        sends,
        arrivals,
        each,
        up_local,
    )
    out = PlaneSum(
        lambda r, h: out_in.at[
            :, pl.ds(pl.multiple_of(absolute(r) * out_cols, out_cols), out_cols)
        ],
        out_chip,
        out_theirs,
        out_links,
        out_stage,
        sends,
        arrivals,
        2 * each,
        out_local,
    )
    base = 3 * each
    rows_of = block_rows(columns, size)
    summed = ColumnSum(d_normed_in, rows_of, arrived_v, relayed_v, sends, arrivals, base)
    base = base + 4
    summed.start(local.at[4])
    first = [
        pltpu.make_async_copy(d_normed_in.at[rows_of(0)], own_v, local.at[0]),
        pltpu.make_async_copy(tokens_in, tokens_v, local.at[1]),
        pltpu.make_async_copy(d_mixed_in, mixed_v, local.at[2]),
        pltpu.make_async_copy(sums_in, running.at[0], local.at[3]),
    ]
    for copy in first:
        copy.start()
    for part in (out, joint, up):
        part.begin()
    summed.clear()
    first[3].wait()

    def small(i, device):
        return mesh_copy(running.at[i], sums_v.at[i], sends, arrivals, base + i, device)

    hops = [small(i, device) for i, device in enumerate((partner, along, across))]
    for i, copy in enumerate(hops):
        copy.start()
        copy.wait_recv()
        running[i + 1] = running[i] + sums_v[i]
    gains = [
        mesh_copy(running.at[3], sums_v.at[2 + s], sends, arrivals, base + 2 + s, column[s - 1])
        for s in range(1, columns)
    ]
    base = base + 2 + columns
    for copy in gains:
        copy.start()
    summed.middle(local.at[4])
    for part in (out, joint, up):
        part.send_first()
    for part in (out, joint, up):
        part.send_second()
    for part in (out, joint, up):
        part.finish()

    pieces = joint_rows // columns
    across_columns = [
        mesh_copy(
            joint_chip.at[
                0,
                0,
                pl.ds(pl.multiple_of((row + s) % columns * pieces, pieces), pieces),
                pl.ds(latent_start, latent_width),
            ],
            latent_v.at[s - 1],
            sends,
            arrivals,
            base + s - 1,
            column[s - 1],
        )
        for s in range(1, columns)
    ]
    for copy in across_columns:
        copy.start()
    done = [
        pltpu.make_async_copy(joint_chip.at[0, 0], joint_out, joint_local.at[4]),
        pltpu.make_async_copy(up_chip.at[0, 0], up_out, up_local.at[4]),
        pltpu.make_async_copy(out_chip.at[0, 0], out_out, out_local.at[4]),
    ]
    for copy in done:
        copy.start()

    for copy in first[:3]:
        copy.wait()
    total = summed.total(own_v[...])
    tokens = tokens_v[...].astype(F32)
    inverse = lax.rsqrt(jnp.mean(tokens * tokens, axis=1, keepdims=True) + EPSILON)
    unit = tokens * inverse
    scaled = total * gain_ref[...]
    mixed_v[...] = mixed_v[...] + inverse * (
        scaled - unit * jnp.mean(scaled * unit, axis=1, keepdims=True)
    )
    grad_copy = pltpu.make_async_copy(mixed_v, grad_out, local.at[0])
    grad_copy.start()
    gathered = running[3]
    for s in range(1, columns):
        gains[s - 1].wait_recv()
        gathered = gathered + sums_v[2 + s]
    sums_out[...] = gathered
    latent = joint_chip[
        0,
        0,
        pl.ds(pl.multiple_of(row * pieces, pieces), pieces),
        pl.ds(latent_start, latent_width),
    ].astype(F32)
    for s in range(1, columns):
        across_columns[s - 1].wait_recv()
        latent = latent + latent_v[s - 1].astype(F32)
    latent_out[...] = latent
    for copy in done + [grad_copy]:
        copy.wait()
    for part in (out, joint, up):
        part.drain()
    summed.drain()
    for copy in hops + gains + across_columns:
        copy.wait_send()


def last_call(d_normed, tokens, d_mixed, gain, joint, up, out, sums, latent_start, latent_width):
    columns = lax.axis_size("tp")
    size, width = tokens.shape
    anywhere = pl.BlockSpec(memory_space=pl.ANY)
    held = pl.BlockSpec(memory_space=pltpu.VMEM)
    shapes = [
        (joint.shape[0] // 8, joint.shape[1]),
        (up.shape[0] // 8, up.shape[1]),
        (out.shape[0], out.shape[1] // 8),
    ]
    landing, scratch = [], []
    for rows, cols in shapes:
        one = plane_sum_space(1, rows, cols)
        landing, scratch = landing + one[0], scratch + one[1]
    remote, near = plane_sum_sizes(1)
    remote = 3 * remote + 2 * (columns - 1) + 7
    pieces = shapes[0][0] // columns
    return pl.pallas_call(
        functools.partial(last_kernel, columns, size, latent_start, latent_width),
        out_shape=[jax.ShapeDtypeStruct((size, width), F32)]
        + [jax.ShapeDtypeStruct(shape, BF) for shape in shapes]
        + [
            jax.ShapeDtypeStruct((pieces, latent_width), F32),
            jax.ShapeDtypeStruct(sums.shape, F32),
        ]
        + landing,
        in_specs=[anywhere] * 3 + [held] + [anywhere] * 4,
        out_specs=[anywhere] * 4 + [held] * 2 + [anywhere] * 6,
        scratch_shapes=scratch
        + [
            pltpu.VMEM((size, width), BF),
            pltpu.VMEM((columns - 1, size, width), BF),
            pltpu.VMEM((2, size, width), BF),
            pltpu.VMEM((size, width), BF),
            pltpu.VMEM((size, width), F32),
            pltpu.VMEM((4,) + sums.shape, F32),
            pltpu.VMEM((2 + columns,) + sums.shape, F32),
            pltpu.VMEM((columns - 1, pieces, latent_width), BF),
            pltpu.SemaphoreType.DMA((remote,)),
            pltpu.SemaphoreType.DMA((remote,)),
            pltpu.SemaphoreType.DMA((5,)),
            pltpu.SemaphoreType.DMA((near,)),
            pltpu.SemaphoreType.DMA((near,)),
            pltpu.SemaphoreType.DMA((near,)),
        ],
        compiler_params=pltpu.CompilerParams(
            collective_id=4, has_side_effects=True, vmem_limit_bytes=48 * 1024 * 1024
        ),
        cost_estimate=pl.CostEstimate(
            flops=0, bytes_accessed=180 * SEQ * width, transcendentals=0
        ),
        name="last_sums",
    )(d_normed, tokens, d_mixed, gain, joint, up, out, sums)[:6]


def plane_units(count):
    return [[(2 * i + j // 2, j % 2) for j in range(4)] for i in range(count // 2)]


def plane_gather(rows, count):
    gathered = lax.all_gather(rows, "fsdp", axis=0)
    return {
        (r, h): gathered[r, h * HALF : (h + 1) * HALF] for r in range(count) for h in (0, 1)
    }


def plane_scatter_whole(pairs, units, count):
    parts = {}
    for unit, pair in zip(units, pairs):
        for q, key in enumerate(unit):
            parts[key] = pair[q // 2][q % 2]
    stacked = jnp.concatenate([parts[r, h] for r in range(count) for h in (0, 1)], axis=0)
    return lax.psum_scatter(stacked, "fsdp", scatter_dimension=0, tiled=True).astype(F32)


def sum_everywhere(values):
    for axis_name in ("fsdp", "tp"):
        count = lax.axis_size(axis_name)
        if is_power(count):
            bit = 1
            while bit < count:
                values = values + swap(values, axis_name, bit)
                bit *= 2
        else:
            values = lax.psum(values, axis_name)
    return values


def expert_tables(expert_ids, expert_wts, local_experts, units, cap):
    fsdp_count = lax.axis_size("fsdp")
    fsdp_rank = lax.axis_index("fsdp")
    expert_count = local_experts * fsdp_count
    names = jnp.arange(expert_count, dtype=jnp.int32)[:, None]
    member = jnp.zeros((expert_count, SEQ), jnp.bool_)
    weight = jnp.zeros((expert_count, SEQ), F32)
    ids_rows, wts_rows = expert_ids.T, expert_wts.T
    for pick in range(TOPK):
        same = ids_rows[pick : pick + 1] == names
        member = member | same
        weight = weight + jnp.where(same, wts_rows[pick : pick + 1], 0.0)
    position = jnp.arange(HALF)
    before = (position[:, None] < position[None, :]).astype(BF)
    rank = jnp.dot(
        member.astype(BF).reshape(expert_count * 2, HALF), before, preferred_element_type=F32
    ).reshape(expert_count, SEQ)
    slot = jnp.where(member, rank, NO_SLOT)
    table = jnp.concatenate([slot, weight], axis=0)
    table = lax.all_gather(table, "fsdp", axis=0, tiled=True)
    table = table.reshape(fsdp_count, 2, fsdp_count, local_experts, 2, HALF)
    table = lax.dynamic_index_in_dim(table, fsdp_rank, axis=2, keepdims=False)
    slot_steps, weight_steps = [], []
    for unit in units:
        slot_steps.append(jnp.stack([table[r, 0, :, h] for r, h in unit]))
        weight_steps.append(jnp.stack([table[r, 1, :, h] for r, h in unit]))
    slot_row, weight_row = jnp.stack(slot_steps), jnp.stack(weight_steps)
    return (slot_row, weight_row, jnp.swapaxes(slot_row, 2, 3))


def per_device(
    block_in,
    out_cotan,
    segment_ids,
    expert_ids,
    expert_wts,
    attn_gain,
    query_proj,
    latent_proj,
    latent_gain,
    latent_up,
    out_proj,
    ffn_gain,
    shared_gate,
    shared_up,
    shared_down,
    routed_gate,
    routed_up,
    routed_down,
):
    tp_count = lax.axis_size("tp")
    fsdp_count = lax.axis_size("fsdp")
    tp_rank = lax.axis_index("tp")
    fsdp_rank = lax.axis_index("fsdp")
    tok_rows, model_width = block_in.shape
    local_experts, local_hidden = routed_gate.shape[:2]
    expert_count = local_experts * fsdp_count
    cap_rows = tok_rows * TOPK * 4 // (3 * expert_count)
    cap = cap_rows * (HALF // tok_rows)
    paired = fsdp_count == 8 and tp_count == 4 and tok_rows * 2 == HALF
    heads_local = H // tp_count
    head_width = NOPE + ROPE
    score_scale = head_width ** (-0.5)
    shard_rows, query_cols = query_proj.shape
    latent_cols = latent_proj.shape[1]
    up_cols = latent_up.shape[1]
    out_rows = out_proj.shape[0]

    joint = query_cols + latent_cols
    spare = (-joint) % 128
    spare = spare + 128 if spare < 3 else spare
    gains = jnp.concatenate(
        [
            attn_gain[:, None],
            ffn_gain[:, None],
            jnp.pad(latent_gain, (0, shard_rows - latent_gain.shape[0]))[:, None],
            jnp.zeros((shard_rows, spare - 3), BF),
        ],
        axis=1,
    )
    packed = jnp.concatenate([query_proj, latent_proj, gains], axis=1)
    cotan_all = column_gather(out_cotan)
    if paired:
        low, high = (0, RAW_ROWS - TOPK), (0, 0)
        raw = jnp.concatenate(
            [jnp.pad(expert_ids.T.astype(F32), (low, high)), jnp.pad(expert_wts.T, (low, high))]
        )
        (
            tokens_all,
            packed_all,
            latent_up_weight,
            out_weight,
            raw,
            shared_weight,
            shared_down_weight,
        ) = first_call(
            block_in,
            [
                packed,
                latent_up,
                out_proj,
                raw,
                jnp.concatenate([shared_gate, shared_up], axis=1),
                shared_down,
            ],
            ("rows", "rows", "columns", "relative", "rows", "columns"),
        )
        shared_weight = shared_weight.reshape(model_width, -1)
        packed_all = packed_all.reshape(-1, packed.shape[1])
        latent_up_weight = latent_up_weight.reshape(LAT, up_cols)
    else:
        packed_all = lax.all_gather(packed, "fsdp", axis=0, tiled=True)
        latent_up_weight = lax.all_gather(latent_up, "fsdp", axis=0, tiled=True)
        out_weight = lax.all_gather(out_proj, "fsdp", axis=1, tiled=True)
        tokens_all = column_gather(block_in)
        shared_weight = lax.all_gather(
            jnp.concatenate([shared_gate, shared_up], axis=1), "fsdp", axis=0, tiled=True
        )
        shared_down_weight = lax.all_gather(shared_down, "fsdp", axis=1, tiled=True)
    gain_attn = packed_all[:, joint].astype(F32)
    gain_ffn = packed_all[:, joint + 1].astype(F32)
    gain_latent = (
        packed_all[:, joint + 2]
        .reshape(fsdp_count, shard_rows)[:, : latent_gain.shape[0]]
        .reshape(LAT)
        .astype(F32)
    )
    shared_cols = shared_gate.shape[1]

    def scatter(part, dimension):
        return lax.psum_scatter(part.astype(BF), "fsdp", scatter_dimension=dimension, tiled=True)

    unit_all, inverse_all = norm_parts(tokens_all.astype(F32))
    normed_all = (unit_all * gain_attn).astype(BF)
    joint_rows = jnp.dot(normed_all, packed_all, preferred_element_type=F32)
    queries = joint_rows[:, :query_cols].reshape(SEQ, heads_local, head_width)
    latent = joint_rows[:, query_cols:joint]
    unit_lat, inverse_lat = norm_parts(latent[:, :LAT])
    positions = jnp.arange(SEQ, dtype=jnp.int32)
    cosine, sine_part = rope_tables(positions, ROPE)
    compressed_all = (unit_lat * gain_latent).astype(BF)
    key_rope_all = rotate(latent[:, LAT:], cosine, sine_part).astype(BF)
    query_cat = jnp.concatenate(
        [
            queries[:, :, :NOPE],
            rotate(queries[:, :, NOPE:], cosine[:, None, :], sine_part[:, None, :]),
        ],
        axis=2,
    ).astype(BF)
    key_value = (
        jnp.dot(compressed_all, latent_up_weight, preferred_element_type=F32)
        .reshape(SEQ, heads_local, NOPE + DV)
        .astype(BF)
    )
    key_cat = jnp.concatenate(
        [
            key_value[:, :, :NOPE],
            jnp.broadcast_to(key_rope_all[:, None, :], (SEQ, heads_local, ROPE)),
        ],
        axis=2,
    )
    values = key_value[:, :, NOPE:]
    allowed = (positions[None, :] <= positions[:, None]) & (
        segment_ids[None, :] == segment_ids[:, None]
    )
    raw_scores = (
        jnp.einsum("qhd,khd->hqk", query_cat, key_cat, preferred_element_type=F32) * score_scale
    )
    masked = jnp.where(allowed[None], raw_scores, MASK_FILL)
    top_score = jnp.max(masked, axis=2, keepdims=True)
    exponent = jnp.exp(masked - top_score)
    row_total = jnp.sum(exponent, axis=2, keepdims=True)
    probabilities = exponent / row_total
    probs_low = probabilities.astype(BF)
    attended = (
        jnp.einsum("hqk,khd->qhd", probs_low, values, preferred_element_type=F32)
        .reshape(SEQ, heads_local * DV)
        .astype(BF)
    )
    attn_part = jnp.dot(attended, out_weight, preferred_element_type=F32).astype(BF)
    if paired:
        mixed_rows, normed_ffn_all, d_routed_in, *kept = expert_call(
            attn_part,
            block_in,
            cotan_all,
            routed_gate,
            routed_up,
            routed_down,
            gain_ffn[None, :],
            raw,
            cap_rows,
        )
        unit_two, inverse_two = norm_parts(mixed_rows)
        d_routed_in = d_routed_in.astype(F32)
    else:
        units = plane_units(fsdp_count)
        tables = expert_tables(expert_ids, expert_wts, local_experts, units, cap)
        hidden_pad = -(-local_hidden // 128) * 128
        lift = ((0, 0), (0, hidden_pad - local_hidden), (0, 0))
        routed_gate_up = jnp.concatenate(
            [jnp.pad(routed_gate, lift), jnp.pad(routed_up, lift)], axis=1
        )
        routed_down_pad = jnp.pad(routed_down, lift)
        mixed_rows = block_in.astype(F32) + column_scatter(attn_part)
        unit_two, inverse_two = norm_parts(mixed_rows)
        normed_ffn_all = column_gather((unit_two * gain_ffn).astype(BF))
        x_blocks = plane_gather(normed_ffn_all, fsdp_count)
        dy_all = lax.all_gather(cotan_all, "fsdp", axis=0, tiled=True)
        kept = []
        dx_pairs = []
        for step, unit in enumerate(units):
            pair, kept = expert_front(
                step,
                len(units),
                [x_blocks[key] for key in unit],
                jnp.array([2 * r + h for r, h in unit], jnp.int32),
                dy_all,
                routed_gate_up,
                routed_down_pad,
                tables,
                kept,
                cap,
            )
            dx_pairs.append(pair)
        near, far = expert_out(kept[2], routed_down_pad, tables, cap)
        d_routed_in = plane_scatter_whole(dx_pairs, units, fsdp_count)
    if not paired:
        routed_gate_grad, routed_up_grad, routed_down_grad = expert_grads(kept, local_hidden)

    shared_pre = jnp.dot(normed_ffn_all, shared_weight, preferred_element_type=F32)
    shared_gate_pre, shared_up_pre = shared_pre[:, :shared_cols], shared_pre[:, shared_cols:]
    shared_hidden = (jax.nn.silu(shared_gate_pre) * shared_up_pre).astype(BF)
    shared_rows = jnp.dot(shared_hidden, shared_down_weight, preferred_element_type=F32)
    shared_down_part = jnp.dot(shared_hidden.T, cotan_all, preferred_element_type=F32)
    d_shared_hidden = jnp.dot(cotan_all, shared_down_weight.T, preferred_element_type=F32)
    d_shared = jnp.concatenate(silu_back(d_shared_hidden, shared_gate_pre, shared_up_pre), axis=1)
    shared_part = jnp.dot(normed_ffn_all.T, d_shared, preferred_element_type=F32)
    d_shared_in = jnp.dot(d_shared, shared_weight.T, preferred_element_type=F32)

    if paired:
        d_ffn_rows, shared_part, shared_down_part = tie(
            (d_shared_in + d_routed_in).astype(BF),
            shared_part.astype(BF),
            shared_down_part.astype(BF),
        )
        (
            d_mixed,
            d_proj_all,
            ffn_gain_part,
            routed_rows,
            routed_gate_grad,
            routed_up_grad,
            routed_down_grad,
        ) = middle_call(
            d_ffn_rows,
            mixed_rows,
            out_cotan,
            gain_ffn[None, :],
            kept[:2],
            routed_down,
            kept[2:],
            cap_rows,
        )
        ffn_gain_part = ffn_gain_part[0]
        routed_rows = routed_rows.astype(F32)
    else:
        d_normed_ffn = column_scatter(d_shared_in + d_routed_in)
        out_pairs = [(near[step], far[step]) for step in range(len(units))]
        routed_rows = plane_scatter_whole(out_pairs, units, fsdp_count)
        ffn_gain_part, d_mixed_norm = norm_back(d_normed_ffn, unit_two, inverse_two, gain_ffn)
        d_mixed = out_cotan.astype(F32) + d_mixed_norm
        d_proj_all = column_gather(d_mixed.astype(BF))
    shared_grad = scatter(shared_part, 0)
    down_own, ffn_rows, shared_grad = tie(
        shared_down_part.astype(BF), (shared_rows + routed_rows).astype(BF), shared_grad
    )
    shared_down_grad = scatter(down_own, 1)
    ffn_rows = column_scatter(ffn_rows)
    block_out = (mixed_rows + ffn_rows).astype(BF)

    out_part = jnp.dot(attended.T, d_proj_all, preferred_element_type=F32)
    d_attended = (
        jnp.dot(d_proj_all, out_weight.T, preferred_element_type=F32)
        .astype(BF)
        .reshape(SEQ, heads_local, DV)
    )
    prob_grad = jnp.einsum("qhd,khd->hqk", d_attended, values, preferred_element_type=F32)
    score_grad = (
        probabilities
        * (prob_grad - jnp.sum(probabilities * prob_grad, axis=2, keepdims=True))
    ).astype(BF)
    query_grad = (
        jnp.einsum("hqk,khd->qhd", score_grad, key_cat, preferred_element_type=F32) * score_scale
    )
    key_grad = (
        jnp.einsum("hqk,qhd->khd", score_grad, query_cat, preferred_element_type=F32) * score_scale
    )
    value_grad = jnp.einsum("hqk,qhd->khd", probs_low, d_attended, preferred_element_type=F32)
    d_queries = (
        jnp.concatenate(
            [
                query_grad[:, :, :NOPE],
                unrotate(query_grad[:, :, NOPE:], cosine[:, None, :], sine_part[:, None, :]),
            ],
            axis=2,
        )
        .reshape(SEQ, heads_local * head_width)
        .astype(BF)
    )
    d_key_value = (
        jnp.concatenate([key_grad[:, :, :NOPE], value_grad], axis=2)
        .reshape(SEQ, heads_local * (NOPE + DV))
        .astype(BF)
    )
    latent_up_part = jnp.dot(compressed_all.T, d_key_value, preferred_element_type=F32)
    d_compressed = jnp.dot(d_key_value, latent_up_weight.T, preferred_element_type=F32)
    d_key_rope = jnp.sum(key_grad[:, :, NOPE:], axis=1)
    latent_gain_part, d_latent_main = norm_back(d_compressed, unit_lat, inverse_lat, gain_latent)
    d_latent = jnp.concatenate(
        [d_latent_main, unrotate(d_key_rope, cosine, sine_part)], axis=1
    ).astype(BF)
    d_joint = jnp.concatenate([d_queries, d_latent, jnp.zeros((SEQ, spare), BF)], axis=1)
    joint_part = jnp.dot(normed_all.T, d_joint, preferred_element_type=F32)
    d_normed_part = jnp.dot(d_joint, packed_all.T, preferred_element_type=F32)
    attn_gain_part = jnp.sum(d_normed_part * unit_all, axis=0)

    gain_parts = jnp.concatenate([attn_gain_part, latent_gain_part, ffn_gain_part]).reshape(
        -1, 128
    )
    joint_part = joint_part.astype(BF)
    if paired:
        latent_width = joint_part.shape[1] - query_cols
        (
            block_in_grad,
            joint_grad,
            latent_up_grad,
            out_proj_grad,
            latent_proj_grad,
            gain_sums,
        ) = last_call(
            d_normed_part.astype(BF),
            block_in,
            d_mixed,
            gain_attn[None, :],
            joint_part,
            latent_up_part.astype(BF),
            out_part.astype(BF),
            gain_parts,
            query_cols,
            latent_width,
        )
        latent_proj_grad = latent_proj_grad[:, :latent_cols]
    else:
        d_normed = column_scatter(d_normed_part)
        unit_one, inverse_one = norm_parts(block_in.astype(F32))
        _, d_tokens_norm = norm_back(d_normed, unit_one, inverse_one, gain_attn)
        block_in_grad = d_mixed + d_tokens_norm
        out_proj_grad = scatter(out_part, 1)
        latent_up_grad = scatter(latent_up_part, 0)
        joint_grad = scatter(joint_part, 0)
        latent_proj_grad = column_scatter(joint_grad[:, query_cols:joint])
        gain_sums = sum_everywhere(gain_parts)
    gain_sums = gain_sums.reshape(-1)
    query_proj_grad = joint_grad[:, :query_cols].astype(F32)
    latent_up_grad = latent_up_grad.astype(F32)
    out_proj_grad = out_proj_grad.astype(F32)
    shared_grad = shared_grad.astype(F32)
    shared_gate_grad, shared_up_grad = shared_grad[:, :shared_cols], shared_grad[:, shared_cols:]
    shared_down_grad = shared_down_grad.astype(F32)
    device = fsdp_rank * tp_count + tp_rank
    devices = tp_count * fsdp_count

    def own_gain(start, size):
        return lax.dynamic_slice(gain_sums, (start + device * (size // devices),), (size // devices,))

    attn_gain_grad = own_gain(0, model_width)
    latent_gain_grad = own_gain(model_width, LAT)
    ffn_gain_grad = own_gain(model_width + LAT, model_width)
    return (
        block_out,
        block_in_grad,
        attn_gain_grad,
        query_proj_grad,
        latent_proj_grad,
        latent_gain_grad,
        latent_up_grad,
        out_proj_grad,
        ffn_gain_grad,
        shared_gate_grad,
        shared_up_grad,
        shared_down_grad,
        routed_gate_grad,
        routed_up_grad,
        routed_down_grad,
    )


def solution(mesh):
    placed = (
        P(("fsdp", "tp"), None),
        P(("fsdp", "tp"), None),
        P("fsdp"),
        P("fsdp", None),
        P("fsdp", None),
        P("fsdp"),
        P("fsdp", "tp"),
        P("fsdp", None),
        P("fsdp"),
        P("fsdp", "tp"),
        P("tp", "fsdp"),
        P("fsdp"),
        P("fsdp", "tp"),
        P("fsdp", "tp"),
        P("tp", "fsdp"),
        P("fsdp", "tp", None),
        P("fsdp", "tp", None),
        P("fsdp", "tp", None),
    )
    return jax.shard_map(
        per_device,
        mesh=mesh,
        in_specs=placed,
        out_specs=(
            P(("fsdp", "tp"), None),
            P(("fsdp", "tp"), None),
            P(("fsdp", "tp")),
            P("fsdp", "tp"),
            P(("fsdp", "tp"), None),
            P(("fsdp", "tp")),
            P("fsdp", "tp"),
            P("tp", "fsdp"),
            P(("fsdp", "tp")),
            P("fsdp", "tp"),
            P("fsdp", "tp"),
            P("tp", "fsdp"),
            P("fsdp", "tp", None),
            P("fsdp", "tp", None),
            P("fsdp", "tp", None),
        ),
        check_vma=False,
    )
```

```python
import functools

import jax
import jax.numpy as jnp
from jax import lax
from jax.experimental import pallas as pl
from jax.experimental.pallas import tpu as pltpu
from jax.sharding import PartitionSpec as P

H = 16
NOPE = 128
ROPE = 64
DV = 128
LAT = 512
TOPK = 6
SEQ = 512
HALF = 256
QUARTET = 4
RAW_ROWS = 8


EPSILON = 1e-06
THETA_BASE = 10000.0
MASK_FILL = -1e30
NO_SLOT = -1e6

BF = jnp.bfloat16
F32 = jnp.float32


def rope_tables(positions, width_rope):
    middle = width_rope // 2
    frequency = THETA_BASE ** (-(jnp.arange(middle) * 2).astype(jnp.float32) / width_rope)
    angles = positions.astype(jnp.float32)[:, None] * frequency[None, :]
    return (jnp.cos(angles), jnp.sin(angles))


def rotate(values, cosine, sine_part):
    middle = values.shape[-1] // 2
    first_half = values[..., :middle]
    second_half = values[..., middle:]
    return jnp.concatenate(
        [
            first_half * cosine - second_half * sine_part,
            second_half * cosine + first_half * sine_part,
        ],
        axis=-1,
    )


def unrotate(values, cosine, sine_part):
    middle = values.shape[-1] // 2
    first_half = values[..., :middle]
    second_half = values[..., middle:]
    return jnp.concatenate(
        [
            first_half * cosine + second_half * sine_part,
            second_half * cosine - first_half * sine_part,
        ],
        axis=-1,
    )


def norm_parts(values):
    inverse = lax.rsqrt(jnp.mean(values * values, axis=-1, keepdims=True) + EPSILON)
    return (values * inverse, inverse)


def norm_back(upstream, unit_rows, inverse, scaling):
    scaled = upstream * scaling
    gain_grad = jnp.sum(upstream * unit_rows, axis=0)
    input_grad = inverse * (
        scaled - unit_rows * jnp.mean(scaled * unit_rows, axis=-1, keepdims=True)
    )
    return (gain_grad, input_grad)


def silu_back(grad_hidden, gate_pre, up_pre):
    sigmoid = jax.nn.sigmoid(gate_pre)
    gate_grad = grad_hidden * up_pre * (sigmoid * (1.0 + gate_pre * (1.0 - sigmoid)))
    up_grad = grad_hidden * (gate_pre * sigmoid)
    return (gate_grad.astype(jnp.bfloat16), up_grad.astype(jnp.bfloat16))


def is_power(count):
    return count & (count - 1) == 0


def swap(values, axis_name, bit):
    count = lax.axis_size(axis_name)
    return lax.ppermute(values, axis_name, [(i, i ^ bit) for i in range(count)])


def tie(*values):
    return lax.optimization_barrier(values)


def column_gather(rows):
    return lax.all_gather(rows, "tp", axis=0, tiled=True)


def column_scatter(values):
    return lax.psum_scatter(values.astype(BF), "tp", scatter_dimension=0, tiled=True).astype(F32)


def dot_rows(left, right):
    return lax.dot_general(left, right, (((1,), (1,)), ((), ())), preferred_element_type=F32)


def dot_plain(left, right):
    return lax.dot_general(left, right, (((1,), (0,)), ((), ())), preferred_element_type=F32)


def dot_first(left, right):
    return lax.dot_general(left, right, (((0,), (0,)), ((), ())), preferred_element_type=F32)


def select_rows(slot_rows, experts, cap):
    row = lax.broadcasted_iota(jnp.int32, (experts * cap, HALF), 0).astype(F32)
    hit = row == slot_rows[0:1, :]
    for e in range(1, experts):
        hit = hit | (row == slot_rows[e : e + 1, :] + float(e * cap))
    return hit


def select_cols(slot_cols, experts, cap):
    lane = lax.broadcasted_iota(jnp.int32, (HALF, experts * cap), 1).astype(F32)
    hit = lane == slot_cols[:, 0:1]
    for e in range(1, experts):
        hit = hit | (lane == slot_cols[:, e : e + 1] + float(e * cap))
    return hit


def slot_weights(hit, weight_rows, experts, cap):
    pieces = []
    for e in range(experts):
        part = hit[e * cap : (e + 1) * cap, :]
        pieces.append(
            jnp.sum(jnp.where(part, weight_rows[e : e + 1, :], 0.0), axis=1, keepdims=True)
        )
    return jnp.concatenate(pieces, axis=0)


def expert_front_kernel(step, experts, cap, aliased, *refs):
    count = QUARTET
    x_in = refs[:count]
    where_ref, dy_in, gate_up_in, down_in, slot_row_ref, weight_row_ref, slot_col_ref = refs[
        count : count + 7
    ]
    base = count + 7 + aliased
    dx_out = refs[base : base + 2]
    x_all, d_all, hid_all, dgu_all = refs[base + 2 : base + 6]
    (xb, db, gate_up, down, xs, ds, dxs, dxo, hid, dgu, sem_in, sem_w, sem_out, sem_dx) = refs[
        base + 6 :
    ]
    width = xb.shape[2]
    pad = down.shape[1]
    tile = min(1024, width)
    x_copies = [pltpu.make_async_copy(x_in[q], xb.at[q], sem_in.at[q]) for q in range(count)]
    d_copies = [
        pltpu.make_async_copy(
            dy_in.at[pl.ds(pl.multiple_of(where_ref[q] * HALF, HALF), HALF)],
            db.at[q],
            sem_in.at[count + q],
        )
        for q in range(count)
    ]
    w_copies = [
        pltpu.make_async_copy(gate_up_in, gate_up, sem_w.at[0]),
        pltpu.make_async_copy(down_in, down, sem_w.at[1]),
    ]
    for q in range(count):
        x_copies[q].start()
        d_copies[q].start()
    for copy in w_copies:
        copy.start()
    for q in range(count):
        x_copies[q].wait()
        d_copies[q].wait()

        hit = select_rows(slot_row_ref[q], experts, cap)
        weights = slot_weights(hit, weight_row_ref[q], experts, cap)
        choose = jnp.where(hit, 1.0, 0.0).astype(BF)

        def spread(n, carry, q=q, choose=choose, weights=weights):
            cols = pl.ds(pl.multiple_of(n * tile, tile), tile)
            rows = dot_plain(choose, xb[q, :, cols])
            grads = dot_plain(choose, db[q, :, cols]) * weights
            for e in range(experts):
                xs[e, q * cap : (q + 1) * cap, cols] = rows[e * cap : (e + 1) * cap].astype(BF)
                ds[e, q * cap : (q + 1) * cap, cols] = grads[e * cap : (e + 1) * cap].astype(BF)
            return carry

        lax.fori_loop(0, width // tile, spread, 0)
    out_copies = [
        pltpu.make_async_copy(xs, x_all.at[step], sem_out.at[0]),
        pltpu.make_async_copy(ds, d_all.at[step], sem_out.at[1]),
        pltpu.make_async_copy(hid, hid_all.at[step], sem_out.at[2]),
        pltpu.make_async_copy(dgu, dgu_all.at[step], sem_out.at[3]),
    ]
    out_copies[0].start()
    out_copies[1].start()
    for copy in w_copies:
        copy.wait()

    def one_expert(e, carry):
        both = dot_rows(xs[e], gate_up[e])
        gate_pre, up_pre = both[:, :pad], both[:, pad:]
        d_hidden = dot_rows(ds[e], down[e])
        sigmoid = jax.nn.sigmoid(gate_pre)
        silu = gate_pre * sigmoid
        hid[e] = (silu * up_pre).astype(BF)
        gate_grad = d_hidden * up_pre * (sigmoid * (1.0 + gate_pre * (1.0 - sigmoid)))
        grads = jnp.concatenate([gate_grad, d_hidden * silu], axis=1).astype(BF)
        dgu[e] = grads

        def back(n, inner):
            cols = pl.ds(pl.multiple_of(n * tile, tile), tile)
            part = dot_plain(dgu[e], gate_up[e, :, cols]).astype(BF)
            for q in range(count):
                dxs[q, pl.ds(pl.multiple_of(e * cap, cap), cap), cols] = part[
                    q * cap : (q + 1) * cap
                ]
            return inner

        lax.fori_loop(0, width // tile, back, 0)
        return carry

    lax.fori_loop(0, experts, one_expert, 0)
    out_copies[2].start()
    out_copies[3].start()
    dx_copies = [
        pltpu.make_async_copy(dxo.at[q], dx_out[q // 2].at[q % 2], sem_dx.at[q])
        for q in range(count)
    ]
    for q in range(count):
        choose = jnp.where(select_cols(slot_col_ref[q], experts, cap), 1.0, 0.0).astype(BF)

        def gather(n, carry, q=q, choose=choose):
            cols = pl.ds(pl.multiple_of(n * tile, tile), tile)
            dxo[q, :, cols] = dot_plain(choose, dxs[q, :, cols]).astype(BF)
            return carry

        lax.fori_loop(0, width // tile, gather, 0)
        dx_copies[q].start()
    for copy in out_copies:
        copy.wait()
    for copy in dx_copies:
        copy.wait()


def expert_front(step, steps, x_parts, where, dy_all, gate_up, down, tables, kept, cap):
    experts, wide, width = gate_up.shape
    pad = wide // 2
    slots = QUARTET * cap
    slot_row, weight_row, slot_col = (t[step] for t in tables)
    any_spec = pl.BlockSpec(memory_space=pl.ANY)
    vmem_spec = pl.BlockSpec(memory_space=pltpu.VMEM)
    pair_shape = jax.ShapeDtypeStruct((2, HALF, width), BF)
    kept_shapes = [
        jax.ShapeDtypeStruct((steps, experts, slots, columns), BF)
        for columns in (width, width, pad, wide)
    ]
    results = pl.pallas_call(
        functools.partial(expert_front_kernel, step, experts, cap, len(kept)),
        out_shape=[pair_shape] * 2 + kept_shapes,
        in_specs=[any_spec] * QUARTET
        + [pl.BlockSpec(memory_space=pltpu.SMEM)]
        + [any_spec] * 3
        + [vmem_spec] * 3
        + [any_spec] * len(kept),
        out_specs=[any_spec] * 6,
        input_output_aliases={QUARTET + 7 + i: 2 + i for i in range(len(kept))},
        scratch_shapes=[
            pltpu.VMEM((QUARTET, HALF, width), BF),
            pltpu.VMEM((QUARTET, HALF, width), BF),
            pltpu.VMEM((experts, wide, width), BF),
            pltpu.VMEM((experts, pad, width), BF),
            pltpu.VMEM((experts, slots, width), BF),
            pltpu.VMEM((experts, slots, width), BF),
            pltpu.VMEM((QUARTET, experts * cap, width), BF),
            pltpu.VMEM((QUARTET, HALF, width), BF),
            pltpu.VMEM((experts, slots, pad), BF),
            pltpu.VMEM((experts, slots, wide), BF),
            pltpu.SemaphoreType.DMA((2 * QUARTET,)),
            pltpu.SemaphoreType.DMA((2,)),
            pltpu.SemaphoreType.DMA((4,)),
            pltpu.SemaphoreType.DMA((QUARTET,)),
        ],
        compiler_params=pltpu.CompilerParams(vmem_limit_bytes=62 * 1024 * 1024),
        cost_estimate=pl.CostEstimate(
            flops=2 * slots * experts * width * pad * 5
            + 6 * QUARTET * HALF * experts * cap * width,
            bytes_accessed=2 * width * (3 * QUARTET * HALF + experts * 3 * pad + 2 * experts * slots),
            transcendentals=slots * experts * pad,
        ),
        name="expert_front",
    )(*x_parts, where, dy_all, gate_up, down, slot_row, weight_row, slot_col, *kept)
    return list(results[:2]), list(results[2:])


def expert_out_kernel(experts, cap, hid, down, slot_row, weight_row, slot_col, near, far, parts):
    width = down.shape[2]
    tile = min(1024, width)
    weights = [
        slot_weights(
            select_rows(slot_row[0, q], experts, cap), weight_row[0, q], experts, cap
        )
        for q in range(QUARTET)
    ]
    for e in range(experts):

        def front(n, carry, e=e):
            cols = pl.ds(pl.multiple_of(n * tile, tile), tile)
            rows = dot_plain(hid[0, e], down[e, :, cols])
            for q in range(QUARTET):
                parts[q, e * cap : (e + 1) * cap, cols] = (
                    rows[q * cap : (q + 1) * cap] * weights[q][e * cap : (e + 1) * cap]
                ).astype(BF)
            return carry

        lax.fori_loop(0, width // tile, front, 0)
    for q in range(QUARTET):
        choose = jnp.where(select_cols(slot_col[0, q], experts, cap), 1.0, 0.0).astype(BF)
        out = (near, far)[q // 2]

        def gather(n, carry, q=q, choose=choose, out=out):
            cols = pl.ds(pl.multiple_of(n * tile, tile), tile)
            out[0, q % 2, :, cols] = dot_plain(choose, parts[q, :, cols]).astype(BF)
            return carry

        lax.fori_loop(0, width // tile, gather, 0)


def expert_out(hid_all, down, tables, cap):
    steps, experts, slots, pad = hid_all.shape
    width = down.shape[2]
    slot_row, weight_row, slot_col = tables
    return pl.pallas_call(
        functools.partial(expert_out_kernel, experts, cap),
        grid=(steps,),
        out_shape=[jax.ShapeDtypeStruct((steps, 2, HALF, width), BF)] * 2,
        in_specs=[
            pl.BlockSpec((1, experts, slots, pad), lambda i: (i, 0, 0, 0)),
            pl.BlockSpec((experts, pad, width), lambda i: (0, 0, 0)),
            pl.BlockSpec((1,) + slot_row.shape[1:], lambda i: (i, 0, 0, 0)),
            pl.BlockSpec((1,) + weight_row.shape[1:], lambda i: (i, 0, 0, 0)),
            pl.BlockSpec((1,) + slot_col.shape[1:], lambda i: (i, 0, 0, 0)),
        ],
        out_specs=[pl.BlockSpec((1, 2, HALF, width), lambda i: (i, 0, 0, 0))] * 2,
        scratch_shapes=[pltpu.VMEM((QUARTET, experts * cap, width), BF)],
        compiler_params=pltpu.CompilerParams(vmem_limit_bytes=48 * 1024 * 1024),
        cost_estimate=pl.CostEstimate(
            flops=steps * (2 * slots * experts * width * pad + 2 * QUARTET * HALF * experts * cap * width),
            bytes_accessed=2 * steps * QUARTET * HALF * width + 2 * hid_all.size + 2 * down.size,
            transcendentals=0,
        ),
        name="expert_out",
    )(hid_all, down, slot_row, weight_row, slot_col)


def expert_grads_kernel(dgu, x, hid, d, gate_grad, up_grad, down_grad):
    local = gate_grad.shape[1]
    pad = hid.shape[3]
    width = x.shape[3]
    tile = min(1024, width)

    @pl.when(pl.program_id(1) == 0)
    def _():
        gate_grad[...] = jnp.zeros_like(gate_grad)
        up_grad[...] = jnp.zeros_like(up_grad)
        down_grad[...] = jnp.zeros_like(down_grad)

    def part(n, carry):
        cols = pl.ds(pl.multiple_of(n * tile, tile), tile)
        gate_grad[0, :, cols] += dot_first(dgu[0, 0, :, :pad], x[0, 0, :, cols])[:local]
        up_grad[0, :, cols] += dot_first(dgu[0, 0, :, pad:], x[0, 0, :, cols])[:local]
        down_grad[0, :, cols] += dot_first(hid[0, 0], d[0, 0, :, cols])[:local]
        return carry

    lax.fori_loop(0, width // tile, part, 0)


def expert_grads(kept, local):
    x_all, d_all, hid_all, dgu_all = kept
    steps, experts, slots, width = x_all.shape
    pad = hid_all.shape[3]

    def block(array):
        return pl.BlockSpec((1, 1) + array.shape[2:], lambda e, i: (i, e, 0, 0))

    grad = jax.ShapeDtypeStruct((experts, local, width), F32)
    return pl.pallas_call(
        expert_grads_kernel,
        grid=(experts, steps),
        out_shape=[grad] * 3,
        in_specs=[block(dgu_all), block(x_all), block(hid_all), block(d_all)],
        out_specs=[pl.BlockSpec((1, local, width), lambda e, i: (e, 0, 0))] * 3,
        compiler_params=pltpu.CompilerParams(vmem_limit_bytes=48 * 1024 * 1024),
        cost_estimate=pl.CostEstimate(
            flops=2 * 3 * steps * experts * slots * width * pad,
            bytes_accessed=2 * (x_all.size + d_all.size + hid_all.size + dgu_all.size)
            + 12 * experts * local * width,
            transcendentals=0,
        ),
        name="expert_grads",
    )(dgu_all, x_all, hid_all, d_all)


def mesh_copy(src, dst, sends, arrivals, number, device):
    return pltpu.make_async_remote_copy(
        src_ref=src,
        dst_ref=dst,
        send_sem=sends.at[number],
        recv_sem=arrivals.at[number],
        device_id=device,
        device_id_type=pl.DeviceIdType.MESH,
    )


def plane_neighbours():
    place, column = lax.axis_index("fsdp"), lax.axis_index("tp")
    core, along, across = place % 2, (place // 2) % 2, place // 4
    return (
        (place + 1 - 2 * core, column),
        (place + 2 - 4 * along, column),
        (place + 4 - 8 * across, column),
    )


def column_neighbours(count):
    place, column = lax.axis_index("fsdp"), lax.axis_index("tp")
    return [(place, (column + s) % count) for s in range(1, count)]


def greet(devices):
    barrier = pltpu.get_barrier_semaphore()
    for device in devices:
        pl.semaphore_signal(
            barrier, inc=1, device_id=device, device_id_type=pl.DeviceIdType.MESH
        )
    pl.semaphore_wait(barrier, len(devices))


class ColumnGather:
    def __init__(self, blocks, rows_of, sends, arrivals, base, own=None):
        self.blocks, self.rows_of = blocks, rows_of
        self.own = blocks.at[rows_of(0)] if own is None else own
        self.sends, self.arrivals, self.base = sends, arrivals, base
        self.row = lax.axis_index("tp")
        self.column = column_neighbours(4)

    def direct(self, s):
        place = self.blocks.at[self.rows_of(0)]
        return mesh_copy(
            self.own, place, self.sends, self.arrivals, self.base + s - 1, self.column[s - 1]
        )

    def start(self):
        @pl.when(self.row < 3)
        def _():
            self.direct(1).start()

        @pl.when(self.row > 0)
        def _():
            self.direct(3).start()

        self.direct(2).start()

    def wait(self, b):
        self.direct(4 - b).wait_recv()
        if b == 2:

            @pl.when(self.row == 1)
            def _():
                self.relay(3).start()

            @pl.when(self.row == 2)
            def _():
                self.relay(1).start()

    def relay(self, s):
        place = self.blocks.at[self.rows_of(2)]
        return pltpu.make_async_remote_copy(
            src_ref=place,
            dst_ref=place,
            send_sem=self.sends.at[self.base + 3],
            recv_sem=self.arrivals.at[self.base + 3 - s],
            device_id=self.column[s - 1],
            device_id_type=pl.DeviceIdType.MESH,
        )

    def drain(self):
        @pl.when(self.row < 3)
        def _():
            self.direct(1).wait_send()

        @pl.when(self.row > 0)
        def _():
            self.direct(3).wait_send()

        self.direct(2).wait_send()

        @pl.when(self.row == 1)
        def _():
            self.relay(3).wait_send()

        @pl.when(self.row == 2)
        def _():
            self.relay(1).wait_send()


class ColumnSum:
    def __init__(self, parts, rows_of, landed, relayed, sends, arrivals, base):
        self.parts, self.rows_of, self.landed, self.relayed = parts, rows_of, landed, relayed
        self.sends, self.arrivals, self.base = sends, arrivals, base
        self.row = lax.axis_index("tp")
        self.column = column_neighbours(4)

    def direct(self, s):
        return mesh_copy(
            self.parts.at[self.rows_of(s)],
            self.landed.at[s - 1],
            self.sends,
            self.arrivals,
            self.base + s - 1,
            self.column[s - 1],
        )

    def first_leg(self, s):
        return mesh_copy(
            self.parts.at[self.rows_of(4 - s)],
            self.relayed.at[0],
            self.sends,
            self.arrivals,
            self.base + 3,
            self.column[s - 1],
        )

    def own_part(self, local):
        return pltpu.make_async_copy(self.parts.at[self.rows_of(2)], self.relayed.at[1], local)

    def second_leg(self):
        return mesh_copy(
            self.relayed.at[1],
            self.landed.at[1],
            self.sends,
            self.arrivals,
            self.base + 1,
            self.column[1],
        )

    def start(self, local):
        @pl.when(self.row == 0)
        def _():
            self.first_leg(1).start()

        @pl.when(self.row == 3)
        def _():
            self.first_leg(3).start()

        @pl.when((self.row == 1) | (self.row == 2))
        def _():
            self.own_part(local).start()

        @pl.when(self.row < 3)
        def _():
            self.direct(1).start()

        @pl.when(self.row > 0)
        def _():
            self.direct(3).start()

        @pl.when((self.row == 0) | (self.row == 3))
        def _():
            self.direct(2).start()

    def middle(self, local):
        @pl.when((self.row == 1) | (self.row == 2))
        def _():
            self.own_part(local).wait()
            self.first_leg(1).wait_recv()

            def some(i, carry):
                rows = pl.ds(pl.multiple_of(i * 32, 32), 32)
                self.relayed[1, rows, :] = (
                    self.relayed[0, rows, :].astype(F32) + self.relayed[1, rows, :].astype(F32)
                ).astype(BF)
                return carry

            lax.fori_loop(0, self.relayed.shape[1] // 32, some, 0)
            self.second_leg().start()

    def clear(self):
        @pl.when(self.row == 0)
        def _():
            self.landed[0] = jnp.zeros(self.landed.shape[1:], BF)

        @pl.when(self.row == 3)
        def _():
            self.landed[2] = jnp.zeros(self.landed.shape[1:], BF)

    def total(self, own):
        @pl.when(self.row > 0)
        def _():
            self.direct(1).wait_recv()

        @pl.when(self.row < 3)
        def _():
            self.direct(3).wait_recv()

        self.direct(2).wait_recv()
        total = own.astype(F32)
        for s in range(3):
            total = total + self.landed[s].astype(F32)
        return total

    def drain(self):
        @pl.when(self.row == 0)
        def _():
            self.first_leg(1).wait_send()

        @pl.when(self.row == 3)
        def _():
            self.first_leg(3).wait_send()

        @pl.when(self.row < 3)
        def _():
            self.direct(1).wait_send()

        @pl.when(self.row > 0)
        def _():
            self.direct(3).wait_send()

        self.direct(2).wait_send()


class PlaneGather:
    def __init__(self, own, others, rows_of, sends, arrivals, base):
        self.own, self.others, self.rows_of = own, others, rows_of
        self.sends, self.arrivals, self.base = sends, arrivals, base
        self.partner, self.along, self.across = plane_neighbours()

    def copies(self, b):
        half = self.own.shape[1] // 2
        rows = self.rows_of(b)
        left, right = pl.ds(0, half), pl.ds(half, half)
        other = {r: self.others.at[r - 1] for r in range(1, 8)}
        plan = [
            (self.own.at[rows], other[2].at[rows], self.along),
            (self.own.at[rows], other[4].at[rows], self.across),
            (self.own.at[rows], other[1].at[rows], self.partner),
            (other[2].at[rows, left], other[6].at[rows, left], self.across),
            (other[4].at[rows, right], other[6].at[rows, right], self.along),
            (other[2].at[rows], other[3].at[rows], self.partner),
            (other[4].at[rows], other[5].at[rows], self.partner),
            (other[6].at[rows], other[7].at[rows], self.partner),
        ]
        return [
            mesh_copy(src, dst, self.sends, self.arrivals, self.base + 8 * b + i, device)
            for i, (src, dst, device) in enumerate(plan)
        ]

    def start(self, b):
        for copy in self.copies(b)[:3]:
            copy.start()

    def forward(self, b):
        along, across, _, left, right, third, fifth, _ = self.copies(b)
        along.wait_recv()
        left.start()
        third.start()
        across.wait_recv()
        right.start()
        fifth.start()

    def last(self, b):
        copies = self.copies(b)
        copies[3].wait_recv()
        copies[4].wait_recv()
        copies[7].start()

    def arrived(self, b, numbers):
        copies = self.copies(b)
        for i in numbers:
            copies[i].wait_recv()

    def drain(self, b):
        for copy in self.copies(b):
            copy.wait_send()


def block_rows(columns, size):
    row = lax.axis_index("tp")
    return lambda s: pl.ds(pl.multiple_of((row + s) % columns * size, size), size)


def slots_of(table, experts, columns, size, b, q):
    place = pl.ds(pl.multiple_of((lax.axis_index("tp") + b) % columns * size, size), size)
    rows = []
    for e in range(experts):
        low, high = 2 * q * experts + e, (2 * q + 1) * experts + e
        rows.append(
            jnp.concatenate([table[low : low + 1, place], table[high : high + 1, place]], axis=1)
        )
    return jnp.concatenate(rows, axis=0)


def token_sums(table, experts, columns, size, wide, b, slots, keep):
    width = slots.shape[2]
    tile = min(1024, width)
    for q in range(QUARTET):
        entries = slots_of(table, experts, columns, size, b, q)
        entries = jnp.concatenate(
            [entries, jnp.full((8 - experts, HALF), NO_SLOT, F32)], axis=0
        )
        choose = jnp.where(select_cols(entries.T, experts, wide), 1.0, 0.0).astype(BF)

        def gather(n, carry, q=q, choose=choose):
            cols = pl.ds(pl.multiple_of(n * tile, tile), tile)
            keep(q, cols, dot_plain(choose, slots[q, :, cols]).astype(BF))
            return carry

        lax.fori_loop(0, width // tile, gather, 0)


def expert_kernel(cap, columns, size, *refs):
    (
        attn_in,
        tokens_in,
        cotan_in,
        gate_in,
        up_in,
        down_in,
        gain_ref,
        raw_ref,
        mixed_out,
        ffn_all,
        dx_out,
        slots_out,
        weights_out,
        x_all,
        d_all,
        hid_all,
        dgu_all,
        x_others,
        dy_others,
        theirs,
        links,
        attn_v,
        tokens_v,
        arrived_v,
        relayed_v,
        mixed_v,
        ffn_v,
        xb,
        db,
        gate_up,
        down,
        xs,
        ds,
        dxs,
        others,
        chip,
        stage,
        hid,
        dgu,
        slot_table,
        weight_table,
        sends,
        arrivals,
        local,
        loads,
        sum_local,
        spill,
    ) = refs
    count = QUARTET
    previous = {2: 0, 1: 2, 3: 1}
    experts, local_hidden = gate_in.shape[:2]
    width = xb.shape[2]
    pad = down.shape[1]
    tile = min(1024, width)
    wide = 2 * cap
    rows_of = block_rows(columns, size)
    partner, along, across = plane_neighbours()
    column = column_neighbours(columns)
    number = 0

    def reserve(amount):
        nonlocal number
        number += amount
        return number - amount

    x_gather = PlaneGather(ffn_all, x_others, rows_of, sends, arrivals, reserve(8 * columns))
    dy_gather = PlaneGather(cotan_in, dy_others, rows_of, sends, arrivals, reserve(8 * columns))
    gather = ColumnGather(ffn_all, rows_of, sends, arrivals, reserve(4))
    summed = ColumnSum(attn_in, rows_of, arrived_v, relayed_v, sends, arrivals, reserve(4))
    plane = PlaneSum(
        lambda r, h: others.at[r // 2],
        chip,
        theirs,
        links,
        stage,
        sends,
        arrivals,
        reserve(plane_sum_sizes(columns)[0]),
        sum_local,
    )

    greet([partner, along, across] + column)
    summed.start(local.at[2])
    first = [
        pltpu.make_async_copy(attn_in.at[rows_of(0)], attn_v, local.at[0]),
        pltpu.make_async_copy(tokens_in, tokens_v, local.at[1]),
    ]
    for copy in first:
        copy.start()
    order = (0, 2, 1, 3)
    for b in order:
        dy_gather.start(b)
    if pad > local_hidden:
        rest = pad - local_hidden
        for e in range(experts):
            for ref, start in ((gate_up, local_hidden), (gate_up, pad + local_hidden), (down, local_hidden)):
                ref[e, start : start + rest, :] = jnp.zeros((rest, width), BF)
    weights_in = []
    for e in range(experts):
        weights_in += [
            pltpu.make_async_copy(
                gate_in.at[e], gate_up.at[e, pl.ds(0, local_hidden)], local.at[3 + 3 * e]
            ),
            pltpu.make_async_copy(
                up_in.at[e], gate_up.at[e, pl.ds(pad, local_hidden)], local.at[4 + 3 * e]
            ),
            pltpu.make_async_copy(
                down_in.at[e], down.at[e, pl.ds(0, local_hidden)], local.at[5 + 3 * e]
            ),
        ]
    for copy in weights_in:
        copy.start()

    summed.clear()
    summed.middle(local.at[2])

    earlier = lax.broadcasted_iota(jnp.int32, (size, size), 0)
    later = lax.broadcasted_iota(jnp.int32, (size, size), 1)
    before = jnp.where(earlier < later, 1.0, 0.0).astype(BF)
    own_first = (lax.axis_index("fsdp") * experts).astype(F32)
    for r in range(8):
        for e in range(experts):
            member = jnp.zeros((1, SEQ), F32)
            weight = jnp.zeros((1, SEQ), F32)
            for pick in range(TOPK):
                same = raw_ref[r, pick : pick + 1, :] == own_first + float(e)
                member = jnp.where(same, 1.0, member)
                weight = weight + jnp.where(
                    same, raw_ref[r, RAW_ROWS + pick : RAW_ROWS + pick + 1, :], 0.0
                )
            slot_table[r * experts + e : r * experts + e + 1, :] = member
            weight_table[r * experts + e : r * experts + e + 1, :] = weight
    second = lax.broadcasted_iota(jnp.int32, (8 * experts, size), 0) // experts % 2
    shift = second.astype(F32) * float(cap)
    for b in range(columns):
        cols = pl.ds(b * size, size)
        member = slot_table[:, cols]
        rank = dot_plain(member.astype(BF), before)
        slot_table[:, cols] = jnp.where(member > 0.5, rank + shift, NO_SLOT)
    slots_out[...] = slot_table[...]
    weights_out[...] = weight_table[...]

    for copy in first:
        copy.wait()
    total = summed.total(attn_v[...]) + tokens_v[...].astype(F32)
    mixed_v[...] = total
    inverse = lax.rsqrt(jnp.mean(total * total, axis=1, keepdims=True) + EPSILON)
    ffn_v[...] = (total * inverse * gain_ref[...]).astype(BF)
    own_copy = pltpu.make_async_copy(ffn_v, ffn_all.at[rows_of(0)], local.at[0])
    own_copy.start()
    mixed_copy = pltpu.make_async_copy(mixed_v, mixed_out, local.at[1])
    mixed_copy.start()
    own_copy.wait()

    gather.start()

    def enter(b):
        if b > 0:
            gather.wait(b)
        x_gather.start(b)

    def ready(b):
        x_gather.last(b)
        dy_gather.last(b)
        x_gather.arrived(b, [2, 5, 6, 7])
        dy_gather.arrived(b, [2, 5, 6, 7])

    def source(own, gathered, r):
        return own if r == 0 else gathered.at[r - 1]

    def load(b, k):
        own, gathered, target = ((ffn_all, x_others, xb), (cotan_in, dy_others, db))[k]
        return [
            pltpu.make_async_copy(
                source(own, gathered, r).at[rows_of(b)],
                target.at[r // 2, pl.ds(r % 2 * size, size)],
                loads.at[8 * k + r],
            )
            for r in range(8)
        ]

    def combine(b, keep):
        token_sums(slot_table, experts, columns, size, wide, b, dxs, keep)

    def spills(b):
        return [
            pltpu.make_async_copy(xs, x_all.at[b], spill.at[0]),
            pltpu.make_async_copy(ds, d_all.at[b], spill.at[1]),
            pltpu.make_async_copy(hid.at[b], hid_all.at[b], spill.at[2]),
            pltpu.make_async_copy(dgu, dgu_all.at[b], spill.at[3]),
        ]

    def front(b):
        x_load, dy_load = load(b, 0), load(b, 1)
        for copy in x_load + dy_load:
            copy.start()
        if b == 0:
            for copy in weights_in:
                copy.wait()
        if b > 0:
            for copy in spills(previous[b]):
                copy.wait()
        for q in range(count):
            for copy in x_load[2 * q : 2 * q + 2] + dy_load[2 * q : 2 * q + 2]:
                copy.wait()
            hit = select_rows(slots_of(slot_table, experts, columns, size, b, q), experts, wide)
            weights = slot_weights(hit, slots_of(weight_table, experts, columns, size, b, q), experts, wide)
            choose = jnp.where(hit, 1.0, 0.0).astype(BF)

            def spread(n, carry, q=q, choose=choose, weights=weights):
                cols = pl.ds(pl.multiple_of(n * tile, tile), tile)
                rows = dot_plain(choose, xb[q, :, cols])
                grads = dot_plain(choose, db[q, :, cols]) * weights
                for e in range(experts):
                    low, high = e * wide, (e + 1) * wide
                    xs[e, q * wide : (q + 1) * wide, cols] = rows[low:high].astype(BF)
                    ds[e, q * wide : (q + 1) * wide, cols] = grads[low:high].astype(BF)
                return carry

            lax.fori_loop(0, width // tile, spread, 0)
        out_copies = spills(b)
        out_copies[0].start()
        out_copies[1].start()

        def one_expert(e, carry):
            both = dot_rows(xs[e], gate_up[e])
            gate_pre, up_pre = both[:, :pad], both[:, pad:]
            d_hidden = dot_rows(ds[e], down[e])
            sigmoid = jax.nn.sigmoid(gate_pre)
            silu = gate_pre * sigmoid
            hid[b, e] = (silu * up_pre).astype(BF)
            gate_grad = d_hidden * up_pre * (sigmoid * (1.0 + gate_pre * (1.0 - sigmoid)))
            dgu[e] = jnp.concatenate([gate_grad, d_hidden * silu], axis=1).astype(BF)

            def back(n, inner):
                cols = pl.ds(pl.multiple_of(n * tile, tile), tile)
                part = dot_plain(dgu[e], gate_up[e, :, cols]).astype(BF)
                for q in range(count):
                    dxs[q, pl.ds(pl.multiple_of(e * wide, wide), wide), cols] = part[
                        q * wide : (q + 1) * wide
                    ]
                return inner

            lax.fori_loop(0, width // tile, back, 0)
            return carry

        lax.fori_loop(0, experts, one_expert, 0)
        out_copies[2].start()
        out_copies[3].start()
        if b > 0:
            for i in range(4):
                plane.pair(i, previous[b]).wait_send()

        def keep(q, cols, value):
            chip[q, b, :, cols] = value[:size]
            others[q, :, cols] = value[size:]

        combine(b, keep)
        for i in range(4):
            plane.pair(i, b).start()

    dy_gather.forward(0)
    enter(0)
    x_gather.forward(0)
    dy_gather.forward(2)
    enter(2)
    dy_gather.forward(1)
    enter(1)
    x_gather.forward(2)
    ready(0)
    front(0)
    dy_gather.forward(3)
    enter(3)
    x_gather.forward(1)
    ready(2)
    front(2)
    x_gather.forward(3)
    plane.send_first([0], False)
    ready(1)
    front(1)
    plane.send_first([2], False)
    plane.send_second([0])
    ready(3)
    front(3)
    plane.send_first([1], False)
    plane.send_second([2])
    done = {}

    def close(b):
        plane.finish([b])
        done[b] = pltpu.make_async_copy(chip.at[0, b], dx_out.at[rows_of(b)], loads.at[b])
        done[b].start()

    plane.send_first([3], False)
    close(0)
    plane.send_second([1])
    close(2)
    plane.send_second([3])
    close(1)
    close(3)
    for copy in spills(3):
        copy.wait()
    for b in range(columns):
        done[b].wait()
    mixed_copy.wait()

    for b in range(columns):
        x_gather.drain(b)
        dy_gather.drain(b)
    gather.drain()
    summed.drain()
    plane.drain(3)


def expert_call(attn_part, tokens, cotan_all, gate, up, down, gain, raw, cap):
    columns = lax.axis_size("tp")
    size, width = tokens.shape
    experts, local_hidden, _ = gate.shape
    pad = -(-local_hidden // 128) * 128
    slots = 8 * cap
    anywhere = pl.BlockSpec(memory_space=pl.ANY)
    held = pl.BlockSpec(memory_space=pltpu.VMEM)

    def array(*dims, kind=BF):
        return jax.ShapeDtypeStruct(dims, kind)

    landing, scratch = plane_sum_space(columns, size, width)
    remote, near = plane_sum_sizes(columns)
    remote = remote + 16 * columns + 8
    results = pl.pallas_call(
        functools.partial(expert_kernel, cap, columns, size),
        out_shape=[
            array(size, width, kind=F32),
            array(SEQ, width),
            array(SEQ, width),
            array(8 * experts, SEQ, kind=F32),
            array(8 * experts, SEQ, kind=F32),
            array(columns, experts, slots, width),
            array(columns, experts, slots, width),
            array(columns, experts, slots, pad),
            array(columns, experts, slots, 2 * pad),
            array(7, SEQ, width),
            array(7, SEQ, width),
        ]
        + landing,
        in_specs=[anywhere] * 6 + [held] * 2,
        out_specs=[anywhere] * 3 + [held] * 2 + [anywhere] * 8,
        scratch_shapes=[
            pltpu.VMEM((size, width), BF),
            pltpu.VMEM((size, width), BF),
            pltpu.VMEM((columns - 1, size, width), BF),
            pltpu.VMEM((2, size, width), BF),
            pltpu.VMEM((size, width), F32),
            pltpu.VMEM((size, width), BF),
            pltpu.VMEM((QUARTET, HALF, width), BF),
            pltpu.VMEM((QUARTET, HALF, width), BF),
            pltpu.VMEM((experts, 2 * pad, width), BF),
            pltpu.VMEM((experts, pad, width), BF),
            pltpu.VMEM((experts, slots, width), BF),
            pltpu.VMEM((experts, slots, width), BF),
            pltpu.VMEM((QUARTET, 2 * experts * cap, width), BF),
            pltpu.VMEM((4, size, width), BF),
        ]
        + scratch
        + [
            pltpu.VMEM((columns, experts, slots, pad), BF),
            pltpu.VMEM((experts, slots, 2 * pad), BF),
            pltpu.VMEM((8 * experts, SEQ), F32),
            pltpu.VMEM((8 * experts, SEQ), F32),
            pltpu.SemaphoreType.DMA((remote,)),
            pltpu.SemaphoreType.DMA((remote,)),
            pltpu.SemaphoreType.DMA((3 + 3 * experts,)),
            pltpu.SemaphoreType.DMA((16,)),
            pltpu.SemaphoreType.DMA((near,)),
            pltpu.SemaphoreType.DMA((4,)),
        ],
        compiler_params=pltpu.CompilerParams(
            collective_id=1, has_side_effects=True, vmem_limit_bytes=67_043_328
        ),
        cost_estimate=pl.CostEstimate(
            flops=16 * SEQ * experts * cap * width * 8,
            bytes_accessed=800 * SEQ * width,
            transcendentals=0,
        ),
        name="experts",
    )(attn_part, tokens, cotan_all, gate, up, down, gain, raw)
    return results[:9]


def first_kernel(columns, size, kinds, *refs):
    amount = len(kinds)
    tokens_in, own_in = refs[0], refs[1 : 1 + amount]
    tokens_all, alls = refs[1 + amount], refs[2 + amount : 2 + 2 * amount]
    tokens_v, held = refs[2 + 2 * amount], refs[3 + 2 * amount : 3 + 3 * amount]
    sends, arrivals, local = refs[3 + 3 * amount :]
    partner, along, across = plane_neighbours()
    column = column_neighbours(columns)
    rows_of = block_rows(columns, size)
    place = lax.axis_index("fsdp")
    devices = {
        0: place,
        1: partner[0],
        2: along[0],
        4: across[0],
        6: along[0] + across[0] - place,
    }
    greet([partner, along, across] + column)
    gather = ColumnGather(tokens_all, rows_of, sends, arrivals, 8 * amount, tokens_in)
    gather.start()
    plans = []
    for k, kind in enumerate(kinds):
        own, everything = own_in[k], alls[k]
        rows, cols = own.shape
        top, bottom = pl.ds(0, rows // 2), pl.ds(rows // 2, rows // 2)
        whole = pl.ds(0, rows)

        def spot(r, hop, part, kind=kind, everything=everything, cols=cols):
            if kind == "relative":
                return everything.at[r ^ hop, part]
            if kind == "rows":
                return everything.at[devices[r], part]
            start = pl.multiple_of(devices[r] * cols, cols)
            return everything.at[part, pl.ds(start, cols)]

        plan = [
            (own, spot(0, 2, whole), along),
            (own, spot(0, 4, whole), across),
            (own, spot(0, 1, whole), partner),
            (spot(2, 0, top), spot(2, 4, top), across),
            (spot(4, 0, bottom), spot(4, 2, bottom), along),
            (spot(2, 0, whole), spot(2, 1, whole), partner),
            (spot(4, 0, whole), spot(4, 1, whole), partner),
            (spot(6, 0, whole), spot(6, 1, whole), partner),
        ]
        plans.append(
            [
                mesh_copy(src, dst, sends, arrivals, 8 * k + i, device)
                for i, (src, dst, device) in enumerate(plan)
            ]
        )
    for copies in plans:
        for copy in copies[:3]:
            copy.start()
    here = [pltpu.make_async_copy(tokens_in, tokens_v, local.at[0])]
    there = [pltpu.make_async_copy(tokens_v, tokens_all.at[rows_of(0)], local.at[0])]
    for k, kind in enumerate(kinds):
        rows, cols = own_in[k].shape
        if kind == "relative":
            spot_here = alls[k].at[0]
        elif kind == "rows":
            spot_here = alls[k].at[place]
        else:
            spot_here = alls[k].at[:, pl.ds(pl.multiple_of(place * cols, cols), cols)]
        here.append(pltpu.make_async_copy(own_in[k], held[k], local.at[1 + k]))
        there.append(pltpu.make_async_copy(held[k], spot_here, local.at[1 + k]))
    for copy in here:
        copy.start()
    for copy in here:
        copy.wait()
    for copy in there:
        copy.start()
    for n, copies in enumerate(plans):
        copies[0].wait_recv()
        copies[3].start()
        copies[5].start()
        copies[1].wait_recv()
        copies[4].start()
        copies[6].start()
        if n == amount - 2:
            gather.wait(2)
    for copies in plans:
        copies[3].wait_recv()
        copies[4].wait_recv()
        copies[7].start()
    for copies in plans:
        for i in (2, 5, 6, 7):
            copies[i].wait_recv()
    gather.wait(1)
    gather.wait(3)
    for copy in there:
        copy.wait()
    gather.drain()
    for copies in plans:
        for copy in copies:
            copy.wait_send()


def first_call(tokens, owns, kinds):
    columns = lax.axis_size("tp")
    size, width = tokens.shape
    anywhere = pl.BlockSpec(memory_space=pl.ANY)
    copies = 8 * len(owns) + 4

    def gathered(own, kind):
        rows, cols = own.shape
        return (rows, 8 * cols) if kind == "columns" else (8, rows, cols)

    return pl.pallas_call(
        functools.partial(first_kernel, columns, size, kinds),
        out_shape=[jax.ShapeDtypeStruct((columns * size, width), BF)]
        + [jax.ShapeDtypeStruct(gathered(own, kind), own.dtype) for own, kind in zip(owns, kinds)],
        in_specs=[anywhere] * (1 + len(owns)),
        out_specs=[anywhere] * (1 + len(owns)),
        scratch_shapes=[pltpu.VMEM((size, width), BF)]
        + [pltpu.VMEM(own.shape, own.dtype) for own in owns]
        + [
            pltpu.SemaphoreType.DMA((copies,)),
            pltpu.SemaphoreType.DMA((copies,)),
            pltpu.SemaphoreType.DMA((1 + len(owns),)),
        ],
        compiler_params=pltpu.CompilerParams(collective_id=2, has_side_effects=True),
        cost_estimate=pl.CostEstimate(
            flops=0, bytes_accessed=240 * SEQ * width, transcendentals=0
        ),
        name="first_gather",
    )(tokens, *owns)


class PlaneSum:
    def __init__(self, source, chip, theirs, links, stage, sends, arrivals, base, local):
        self.source, self.chip, self.theirs, self.links = source, chip, theirs, links
        self.stage, self.sends, self.arrivals, self.base = stage, sends, arrivals, base
        self.local = local
        self.parts, self.rows = chip.shape[1], chip.shape[2]
        self.partner, self.along, self.across = plane_neighbours()

    def pair(self, i, h):
        return mesh_copy(
            self.source(2 * i + 1, h),
            self.theirs.at[i, h],
            self.sends,
            self.arrivals,
            self.base + i * self.parts + h,
            self.partner,
        )

    def mine(self, i, h):
        return pltpu.make_async_copy(
            self.source(2 * i, h), self.chip.at[i, h], self.local.at[4 + i * self.parts + h]
        )

    def begin(self):
        for i in (3, 1, 2, 0):
            for h in range(self.parts):
                self.pair(i, h).start()
                self.mine(i, h).start()

    def fetch(self, landed, slot):
        size = landed.shape[0]
        return pltpu.make_async_copy(
            landed, self.stage.at[slot, pl.ds(0, size)], self.local.at[slot]
        )

    def add(self, i, h, start, size, slot):
        some = min(32, size)

        def one(n, carry):
            rows = pl.ds(pl.multiple_of(start + n * some, some), some)
            from_rows = pl.ds(pl.multiple_of(n * some, some), some)
            self.chip[i, h, rows, :] = (
                self.chip[i, h, rows, :].astype(F32) + self.stage[slot, from_rows, :].astype(F32)
            ).astype(BF)
            return carry

        lax.fori_loop(0, size // some, one, 0)

    def send_first(self, parts=None, fetched=True):
        for h in range(self.parts) if parts is None else parts:
            for i in (3, 1, 2, 0):
                self.pair(i, h).wait_recv()
                self.fetch(self.theirs.at[i, h], i).start()
            for i in (3, 1, 2, 0):
                if fetched:
                    self.mine(i, h).wait()
                self.fetch(self.theirs.at[i, h], i).wait()
                self.add(i, h, 0, self.rows, i)
                if i == 3:
                    self.send(1, [h])
                if i == 2:
                    self.send(0, [h])

    def link(self, stage_number, side, h):
        first_hop, second_hop = (
            (self.along, self.across) if side == 0 else (self.across, self.along)
        )
        near, far = (1, 2) if side == 0 else (2, 1)
        i = (near, 3, far)[stage_number]
        place = (stage_number * 2 + side) * self.parts + h
        rows = pl.ds(side * (self.rows // 2), self.rows // 2)
        return mesh_copy(
            self.chip.at[i, h, rows],
            self.links.at[place],
            self.sends,
            self.arrivals,
            self.base + 4 * self.parts + place,
            second_hop if stage_number == 2 else first_hop,
        )

    def landed(self, stage_number, side, h):
        return self.links.at[(stage_number * 2 + side) * self.parts + h]

    def send(self, stage_number, parts=None):
        for h in range(self.parts) if parts is None else parts:
            for side in range(2):
                self.link(stage_number, side, h).start()

    def send_second(self, parts=None):
        half = self.rows // 2
        for h in range(self.parts) if parts is None else parts:
            for side in range(2):
                self.link(1, side, h).wait_recv()
                self.fetch(self.landed(1, side, h), side).start()
            for side in range(2):
                self.fetch(self.landed(1, side, h), side).wait()
                self.add((2, 1)[side], h, side * half, half, side)
                self.link(2, side, h).start()

    def finish(self, parts=None):
        half = self.rows // 2
        for h in range(self.parts) if parts is None else parts:
            for stage_number in (0, 2):
                for side in range(2):
                    self.link(stage_number, side, h).wait_recv()
                    self.fetch(self.landed(stage_number, side, h), stage_number + side).start()
            for stage_number in (0, 2):
                for side in range(2):
                    slot = stage_number + side
                    self.fetch(self.landed(stage_number, side, h), slot).wait()
                    self.add(0, h, side * half, half, slot)

    def drain(self, first_part=0):
        for h in range(self.parts):
            for i in range(4):
                if h >= first_part:
                    self.pair(i, h).wait_send()
            for stage_number in range(3):
                for side in range(2):
                    self.link(stage_number, side, h).wait_send()


def plane_sum_sizes(parts):
    return 10 * parts, 4 + 4 * parts


def plane_sum_space(parts, rows, width):
    landing = [
        jax.ShapeDtypeStruct((4, parts, rows, width), BF),
        jax.ShapeDtypeStruct((6 * parts, rows // 2, width), BF),
    ]
    scratch = [pltpu.VMEM((4, parts, rows, width), BF), pltpu.VMEM((4, rows, width), BF)]
    return landing, scratch


def middle_kernel(cap, columns, size, experts, steps, local_hidden, *refs):
    (
        d_ffn_in,
        mixed_in,
        cotan_in,
        gain_ref,
        slot_table,
        weight_table,
        down_in,
        x_all,
        d_all,
        hid_all,
        dgu_all,
        d_mixed_out,
        d_proj_all,
        gain_out,
        routed_out,
        gate_grad,
        up_grad,
        down_grad,
        theirs,
        links,
        chip,
        stage,
        own_v,
        arrived_v,
        relayed_v,
        mixed_v,
        cotan_v,
        proj_v,
        xk,
        dk,
        hk,
        gk,
        totals,
        hid,
        down,
        parts,
        others,
        sends,
        arrivals,
        local,
        sum_local,
        work,
        written,
    ) = refs
    partner, along, across = plane_neighbours()
    column = column_neighbours(columns)
    greet([partner, along, across] + column)
    plane = PlaneSum(
        lambda r, h: others.at[h % 2, r // 2],
        chip,
        theirs,
        links,
        stage,
        sends,
        arrivals,
        0,
        sum_local,
    )
    base = plane_sum_sizes(columns)[0]
    rows_of = block_rows(columns, size)
    summed = ColumnSum(d_ffn_in, rows_of, arrived_v, relayed_v, sends, arrivals, base)
    gather = ColumnGather(d_proj_all, rows_of, sends, arrivals, base + 4)
    summed.start(local.at[3])
    first = [
        pltpu.make_async_copy(d_ffn_in.at[rows_of(0)], own_v, local.at[0]),
        pltpu.make_async_copy(mixed_in, mixed_v, local.at[1]),
        pltpu.make_async_copy(cotan_in, cotan_v, local.at[2]),
    ]
    for copy in first:
        copy.start()
    width = xk.shape[2]
    pad = hk.shape[2]
    tile = min(1024, width)
    hidden_in = [pltpu.make_async_copy(hid_all.at[b], hid.at[b], local.at[4 + b]) for b in range(columns)]
    down_copies = [
        pltpu.make_async_copy(
            down_in.at[e], down.at[e, pl.ds(0, local_hidden)], local.at[4 + columns + e]
        )
        for e in range(experts)
    ]
    for copy in down_copies + hidden_in:
        copy.start()
    summed.clear()
    rest = down.shape[1] - local_hidden
    if rest > 0:
        for e in range(experts):
            down[e, local_hidden:, :] = jnp.zeros((rest, down.shape[2]), BF)
    for copy in down_copies:
        copy.wait()
    wide = 2 * cap

    def out_part(b):
        hidden_in[b].wait()
        weights = [
            slot_weights(
                select_rows(slots_of(slot_table, experts, columns, size, b, q), experts, wide),
                slots_of(weight_table, experts, columns, size, b, q),
                experts,
                wide,
            )
            for q in range(QUARTET)
        ]
        for e in range(experts):

            def one_tile(n, carry, e=e):
                cols = pl.ds(pl.multiple_of(n * tile, tile), tile)
                rows = dot_plain(hid[b, e], down[e, :, cols])
                for q in range(QUARTET):
                    parts[q, e * wide : (e + 1) * wide, cols] = (
                        rows[q * wide : (q + 1) * wide] * weights[q][e * wide : (e + 1) * wide]
                    ).astype(BF)
                return carry

            lax.fori_loop(0, width // tile, one_tile, 0)
        if b > 1:
            for i in range(4):
                plane.pair(i, b - 2).wait_send()

        def keep(q, cols, value):
            chip[q, b, :, cols] = value[:size]
            others[b % 2, q, :, cols] = value[size:]

        token_sums(slot_table, experts, columns, size, wide, b, parts, keep)
        for i in range(4):
            plane.pair(i, b).start()

    jobs = [(e, step) for e in range(experts) for step in range(steps)]

    def fetch(k):
        e, step = jobs[k]
        slot = k % 2
        return [
            pltpu.make_async_copy(x_all.at[step, e], xk.at[slot], work.at[slot, 0]),
            pltpu.make_async_copy(d_all.at[step, e], dk.at[slot], work.at[slot, 1]),
            pltpu.make_async_copy(hid_all.at[step, e], hk.at[slot], work.at[slot, 2]),
            pltpu.make_async_copy(dgu_all.at[step, e], gk.at[slot], work.at[slot, 3]),
        ]

    def write(e):
        return [
            pltpu.make_async_copy(
                totals.at[e % 2, i, pl.ds(0, local_hidden)], grad.at[e], written.at[e % 2, i]
            )
            for i, grad in enumerate((gate_grad, up_grad, down_grad))
        ]

    def job(k):
        e, step = jobs[k]
        slot, place = k % 2, e % 2
        if k + 1 < len(jobs):
            for copy in fetch(k + 1):
                copy.start()
        for copy in fetch(k):
            copy.wait()
        if step == 0 and e > 1:
            for copy in write(e - 2):
                copy.wait()

        def one(n, carry):
            cols = pl.ds(pl.multiple_of(n * tile, tile), tile)
            found = [
                dot_first(gk[slot, :, :pad], xk[slot, :, cols]),
                dot_first(gk[slot, :, pad:], xk[slot, :, cols]),
                dot_first(hk[slot], dk[slot, :, cols]),
            ]
            for i, value in enumerate(found):
                if step == 0:
                    totals[place, i, :, cols] = value
                else:
                    totals[place, i, :, cols] += value
            return carry

        lax.fori_loop(0, width // tile, one, 0)
        if step == steps - 1:
            for copy in write(e):
                copy.start()

    out_part(0)
    out_part(1)
    summed.middle(local.at[3])
    plane.send_first([0], False)
    out_part(2)
    plane.send_first([1], False)
    for copy in fetch(0):
        copy.start()
    out_part(3)
    plane.send_first([2], False)
    plane.send_first([3], False)

    for copy in first:
        copy.wait()
    total = summed.total(own_v[...])
    mixed = mixed_v[...]
    inverse = lax.rsqrt(jnp.mean(mixed * mixed, axis=1, keepdims=True) + EPSILON)
    unit = mixed * inverse
    scaled = total * gain_ref[...]
    gain_out[...] = jnp.sum(total * unit, axis=0, keepdims=True)
    back = inverse * (scaled - unit * jnp.mean(scaled * unit, axis=1, keepdims=True))
    d_mixed = cotan_v[...].astype(F32) + back
    mixed_v[...] = d_mixed
    proj_v[...] = d_mixed.astype(BF)
    own_copy = pltpu.make_async_copy(proj_v, d_proj_all.at[rows_of(0)], local.at[0])
    own_copy.start()
    mixed_copy = pltpu.make_async_copy(mixed_v, d_mixed_out, local.at[1])
    mixed_copy.start()
    own_copy.wait()
    gather.start()
    job(0)
    for b in range(columns):
        if b + 1 < len(jobs):
            job(b + 1)
        plane.send_second([b])
        if b == 1:
            gather.wait(2)
    for b in range(columns):
        if columns + 1 + b < len(jobs):
            job(columns + 1 + b)
        if b < columns - 1:
            plane.finish([b])
    for k in range(2 * columns + 1, len(jobs)):
        job(k)
    plane.finish([columns - 1])
    done = [
        pltpu.make_async_copy(chip.at[0, h], routed_out.at[rows_of(h)], sum_local.at[4 + h])
        for h in range(columns)
    ]
    for copy in done:
        copy.start()
    gather.wait(1)
    gather.wait(3)
    for copy in done + [mixed_copy]:
        copy.wait()
    for e in range(max(0, experts - 2), experts):
        for copy in write(e):
            copy.wait()
    plane.drain(2)
    gather.drain()
    summed.drain()


def middle_call(d_ffn, mixed, cotan, gain, tables, down, kept, cap):
    columns = lax.axis_size("tp")
    size, width = cotan.shape
    x_all, d_all, hid_all, dgu_all = kept
    steps, experts, slots, pad = hid_all.shape
    local_hidden = down.shape[1]
    anywhere = pl.BlockSpec(memory_space=pl.ANY)
    held = pl.BlockSpec(memory_space=pltpu.VMEM)
    landing, scratch = plane_sum_space(columns, size, width)
    remote, near = plane_sum_sizes(columns)
    remote = remote + 8
    grad = jax.ShapeDtypeStruct((experts, local_hidden, width), F32)
    results = pl.pallas_call(
        functools.partial(middle_kernel, cap, columns, size, experts, steps, local_hidden),
        out_shape=[
            jax.ShapeDtypeStruct((size, width), F32),
            jax.ShapeDtypeStruct((SEQ, width), BF),
            jax.ShapeDtypeStruct((1, width), F32),
            jax.ShapeDtypeStruct((SEQ, width), BF),
            grad,
            grad,
            grad,
        ]
        + landing,
        in_specs=[anywhere] * 3 + [held] * 3 + [anywhere] * 5,
        out_specs=[anywhere] * 2 + [held] + [anywhere] * 6,
        scratch_shapes=scratch
        + [
            pltpu.VMEM((size, width), BF),
            pltpu.VMEM((columns - 1, size, width), BF),
            pltpu.VMEM((2, size, width), BF),
            pltpu.VMEM((size, width), F32),
            pltpu.VMEM((size, width), BF),
            pltpu.VMEM((size, width), BF),
            pltpu.VMEM((2, slots, width), BF),
            pltpu.VMEM((2, slots, width), BF),
            pltpu.VMEM((2, slots, pad), BF),
            pltpu.VMEM((2, slots, 2 * pad), BF),
            pltpu.VMEM((2, 3, pad, width), F32),
            pltpu.VMEM((steps, experts, slots, pad), BF),
            pltpu.VMEM((experts, pad, width), BF),
            pltpu.VMEM((QUARTET, 2 * experts * cap, width), BF),
            pltpu.VMEM((2, 4, size, width), BF),
            pltpu.SemaphoreType.DMA((remote,)),
            pltpu.SemaphoreType.DMA((remote,)),
            pltpu.SemaphoreType.DMA((4 + columns + experts,)),
            pltpu.SemaphoreType.DMA((near,)),
            pltpu.SemaphoreType.DMA((2, 4)),
            pltpu.SemaphoreType.DMA((2, 3)),
        ],
        compiler_params=pltpu.CompilerParams(
            collective_id=3, has_side_effects=True, vmem_limit_bytes=67_043_328
        ),
        cost_estimate=pl.CostEstimate(
            flops=2 * 3 * steps * experts * slots * width * pad,
            bytes_accessed=300 * SEQ * width,
            transcendentals=0,
        ),
        name="middle",
    )(d_ffn, mixed, cotan, gain, *tables, down, x_all, d_all, hid_all, dgu_all)
    return results[:7]


def last_kernel(columns, size, latent_start, latent_width, *refs):
    (
        d_normed_in,
        tokens_in,
        d_mixed_in,
        gain_ref,
        joint_in,
        up_in,
        out_in,
        sums_in,
        grad_out,
        joint_out,
        up_out,
        out_out,
        latent_out,
        sums_out,
        joint_theirs,
        joint_links,
        up_theirs,
        up_links,
        out_theirs,
        out_links,
        joint_chip,
        joint_stage,
        up_chip,
        up_stage,
        out_chip,
        out_stage,
        own_v,
        arrived_v,
        relayed_v,
        tokens_v,
        mixed_v,
        running,
        sums_v,
        latent_v,
        sends,
        arrivals,
        local,
        joint_local,
        up_local,
        out_local,
    ) = refs
    partner, along, across = plane_neighbours()
    column = column_neighbours(columns)
    place, row = lax.axis_index("fsdp"), lax.axis_index("tp")
    core, right, above = place % 2, (place // 2) % 2, place // 4

    def absolute(r):
        return (
            (above + r // 4) % 2 * 4 + (right + r // 2 % 2) % 2 * 2 + (core + r % 2) % 2
        )

    greet([partner, along, across] + column)
    each = plane_sum_sizes(1)[0]
    joint_rows, up_rows = joint_chip.shape[2], up_chip.shape[2]
    out_cols = out_chip.shape[3]

    def by_rows(ref, count):
        return lambda r, h: ref.at[pl.ds(pl.multiple_of(absolute(r) * count, count), count)]

    joint = PlaneSum(
        by_rows(joint_in, joint_rows),
        joint_chip,
        joint_theirs,
        joint_links,
        joint_stage,
        sends,
        arrivals,
        0,
        joint_local,
    )
    up = PlaneSum(
        by_rows(up_in, up_rows),
        up_chip,
        up_theirs,
        up_links,
        up_stage,
        sends,
        arrivals,
        each,
        up_local,
    )
    out = PlaneSum(
        lambda r, h: out_in.at[
            :, pl.ds(pl.multiple_of(absolute(r) * out_cols, out_cols), out_cols)
        ],
        out_chip,
        out_theirs,
        out_links,
        out_stage,
        sends,
        arrivals,
        2 * each,
        out_local,
    )
    base = 3 * each
    rows_of = block_rows(columns, size)
    summed = ColumnSum(d_normed_in, rows_of, arrived_v, relayed_v, sends, arrivals, base)
    base = base + 4
    summed.start(local.at[4])
    first = [
        pltpu.make_async_copy(d_normed_in.at[rows_of(0)], own_v, local.at[0]),
        pltpu.make_async_copy(tokens_in, tokens_v, local.at[1]),
        pltpu.make_async_copy(d_mixed_in, mixed_v, local.at[2]),
        pltpu.make_async_copy(sums_in, running.at[0], local.at[3]),
    ]
    for copy in first:
        copy.start()
    summed.clear()
    first[3].wait()

    def small(i, device):
        return mesh_copy(running.at[i], sums_v.at[i], sends, arrivals, base + i, device)

    hops = [small(i, device) for i, device in enumerate((partner, along, across))]
    hops[0].start()
    for part in (out, joint, up):
        part.begin()
    for i, copy in enumerate(hops):
        if i > 0:
            copy.start()
        copy.wait_recv()
        running[i + 1] = running[i] + sums_v[i]
    gains = [
        mesh_copy(running.at[3], sums_v.at[2 + s], sends, arrivals, base + 2 + s, column[s - 1])
        for s in range(1, columns)
    ]
    base = base + 2 + columns
    for copy in gains:
        copy.start()
    summed.middle(local.at[4])
    for part in (out, joint, up):
        part.send_first()
    for part in (out, joint, up):
        part.send_second()
    for part in (out, joint, up):
        part.finish()

    pieces = joint_rows // columns
    across_columns = [
        mesh_copy(
            joint_chip.at[
                0,
                0,
                pl.ds(pl.multiple_of((row + s) % columns * pieces, pieces), pieces),
                pl.ds(latent_start, latent_width),
            ],
            latent_v.at[s - 1],
            sends,
            arrivals,
            base + s - 1,
            column[s - 1],
        )
        for s in range(1, columns)
    ]
    for copy in across_columns:
        copy.start()
    done = [
        pltpu.make_async_copy(joint_chip.at[0, 0], joint_out, joint_local.at[4]),
        pltpu.make_async_copy(up_chip.at[0, 0], up_out, up_local.at[4]),
        pltpu.make_async_copy(out_chip.at[0, 0], out_out, out_local.at[4]),
    ]
    for copy in done:
        copy.start()

    for copy in first[:3]:
        copy.wait()
    total = summed.total(own_v[...])
    tokens = tokens_v[...].astype(F32)
    inverse = lax.rsqrt(jnp.mean(tokens * tokens, axis=1, keepdims=True) + EPSILON)
    unit = tokens * inverse
    scaled = total * gain_ref[...]
    mixed_v[...] = mixed_v[...] + inverse * (
        scaled - unit * jnp.mean(scaled * unit, axis=1, keepdims=True)
    )
    grad_copy = pltpu.make_async_copy(mixed_v, grad_out, local.at[0])
    grad_copy.start()
    gathered = running[3]
    for s in range(1, columns):
        gains[s - 1].wait_recv()
        gathered = gathered + sums_v[2 + s]
    sums_out[...] = gathered
    latent = joint_chip[
        0,
        0,
        pl.ds(pl.multiple_of(row * pieces, pieces), pieces),
        pl.ds(latent_start, latent_width),
    ].astype(F32)
    for s in range(1, columns):
        across_columns[s - 1].wait_recv()
        latent = latent + latent_v[s - 1].astype(F32)
    latent_out[...] = latent
    for copy in done + [grad_copy]:
        copy.wait()
    for part in (out, joint, up):
        part.drain()
    summed.drain()
    for copy in hops + gains + across_columns:
        copy.wait_send()


def last_call(d_normed, tokens, d_mixed, gain, joint, up, out, sums, latent_start, latent_width):
    columns = lax.axis_size("tp")
    size, width = tokens.shape
    anywhere = pl.BlockSpec(memory_space=pl.ANY)
    held = pl.BlockSpec(memory_space=pltpu.VMEM)
    shapes = [
        (joint.shape[0] // 8, joint.shape[1]),
        (up.shape[0] // 8, up.shape[1]),
        (out.shape[0], out.shape[1] // 8),
    ]
    landing, scratch = [], []
    for rows, cols in shapes:
        one = plane_sum_space(1, rows, cols)
        landing, scratch = landing + one[0], scratch + one[1]
    remote, near = plane_sum_sizes(1)
    remote = 3 * remote + 2 * (columns - 1) + 7
    pieces = shapes[0][0] // columns
    return pl.pallas_call(
        functools.partial(last_kernel, columns, size, latent_start, latent_width),
        out_shape=[jax.ShapeDtypeStruct((size, width), F32)]
        + [jax.ShapeDtypeStruct(shape, BF) for shape in shapes]
        + [
            jax.ShapeDtypeStruct((pieces, latent_width), F32),
            jax.ShapeDtypeStruct(sums.shape, F32),
        ]
        + landing,
        in_specs=[anywhere] * 3 + [held] + [anywhere] * 4,
        out_specs=[anywhere] * 4 + [held] * 2 + [anywhere] * 6,
        scratch_shapes=scratch
        + [
            pltpu.VMEM((size, width), BF),
            pltpu.VMEM((columns - 1, size, width), BF),
            pltpu.VMEM((2, size, width), BF),
            pltpu.VMEM((size, width), BF),
            pltpu.VMEM((size, width), F32),
            pltpu.VMEM((4,) + sums.shape, F32),
            pltpu.VMEM((2 + columns,) + sums.shape, F32),
            pltpu.VMEM((columns - 1, pieces, latent_width), BF),
            pltpu.SemaphoreType.DMA((remote,)),
            pltpu.SemaphoreType.DMA((remote,)),
            pltpu.SemaphoreType.DMA((5,)),
            pltpu.SemaphoreType.DMA((near,)),
            pltpu.SemaphoreType.DMA((near,)),
            pltpu.SemaphoreType.DMA((near,)),
        ],
        compiler_params=pltpu.CompilerParams(
            collective_id=4, has_side_effects=True, vmem_limit_bytes=48 * 1024 * 1024
        ),
        cost_estimate=pl.CostEstimate(
            flops=0, bytes_accessed=180 * SEQ * width, transcendentals=0
        ),
        name="last_sums",
    )(d_normed, tokens, d_mixed, gain, joint, up, out, sums)[:6]


def plane_units(count):
    return [[(2 * i + j // 2, j % 2) for j in range(4)] for i in range(count // 2)]


def plane_gather(rows, count):
    gathered = lax.all_gather(rows, "fsdp", axis=0)
    return {
        (r, h): gathered[r, h * HALF : (h + 1) * HALF] for r in range(count) for h in (0, 1)
    }


def plane_scatter_whole(pairs, units, count):
    parts = {}
    for unit, pair in zip(units, pairs):
        for q, key in enumerate(unit):
            parts[key] = pair[q // 2][q % 2]
    stacked = jnp.concatenate([parts[r, h] for r in range(count) for h in (0, 1)], axis=0)
    return lax.psum_scatter(stacked, "fsdp", scatter_dimension=0, tiled=True).astype(F32)


def sum_everywhere(values):
    for axis_name in ("fsdp", "tp"):
        count = lax.axis_size(axis_name)
        if is_power(count):
            bit = 1
            while bit < count:
                values = values + swap(values, axis_name, bit)
                bit *= 2
        else:
            values = lax.psum(values, axis_name)
    return values


def expert_tables(expert_ids, expert_wts, local_experts, units, cap):
    fsdp_count = lax.axis_size("fsdp")
    fsdp_rank = lax.axis_index("fsdp")
    expert_count = local_experts * fsdp_count
    names = jnp.arange(expert_count, dtype=jnp.int32)[:, None]
    member = jnp.zeros((expert_count, SEQ), jnp.bool_)
    weight = jnp.zeros((expert_count, SEQ), F32)
    ids_rows, wts_rows = expert_ids.T, expert_wts.T
    for pick in range(TOPK):
        same = ids_rows[pick : pick + 1] == names
        member = member | same
        weight = weight + jnp.where(same, wts_rows[pick : pick + 1], 0.0)
    position = jnp.arange(HALF)
    before = (position[:, None] < position[None, :]).astype(BF)
    rank = jnp.dot(
        member.astype(BF).reshape(expert_count * 2, HALF), before, preferred_element_type=F32
    ).reshape(expert_count, SEQ)
    slot = jnp.where(member, rank, NO_SLOT)
    table = jnp.concatenate([slot, weight], axis=0)
    table = lax.all_gather(table, "fsdp", axis=0, tiled=True)
    table = table.reshape(fsdp_count, 2, fsdp_count, local_experts, 2, HALF)
    table = lax.dynamic_index_in_dim(table, fsdp_rank, axis=2, keepdims=False)
    slot_steps, weight_steps = [], []
    for unit in units:
        slot_steps.append(jnp.stack([table[r, 0, :, h] for r, h in unit]))
        weight_steps.append(jnp.stack([table[r, 1, :, h] for r, h in unit]))
    slot_row, weight_row = jnp.stack(slot_steps), jnp.stack(weight_steps)
    return (slot_row, weight_row, jnp.swapaxes(slot_row, 2, 3))


def per_device(
    block_in,
    out_cotan,
    segment_ids,
    expert_ids,
    expert_wts,
    attn_gain,
    query_proj,
    latent_proj,
    latent_gain,
    latent_up,
    out_proj,
    ffn_gain,
    shared_gate,
    shared_up,
    shared_down,
    routed_gate,
    routed_up,
    routed_down,
):
    tp_count = lax.axis_size("tp")
    fsdp_count = lax.axis_size("fsdp")
    tp_rank = lax.axis_index("tp")
    fsdp_rank = lax.axis_index("fsdp")
    tok_rows, model_width = block_in.shape
    local_experts, local_hidden = routed_gate.shape[:2]
    expert_count = local_experts * fsdp_count
    cap_rows = tok_rows * TOPK * 4 // (3 * expert_count)
    cap = cap_rows * (HALF // tok_rows)
    paired = fsdp_count == 8 and tp_count == 4 and tok_rows * 2 == HALF
    heads_local = H // tp_count
    head_width = NOPE + ROPE
    score_scale = head_width ** (-0.5)
    shard_rows, query_cols = query_proj.shape
    latent_cols = latent_proj.shape[1]
    up_cols = latent_up.shape[1]
    out_rows = out_proj.shape[0]

    joint = query_cols + latent_cols
    spare = (-joint) % 128
    spare = spare + 128 if spare < 3 else spare
    gains = jnp.concatenate(
        [
            attn_gain[:, None],
            ffn_gain[:, None],
            jnp.pad(latent_gain, (0, shard_rows - latent_gain.shape[0]))[:, None],
            jnp.zeros((shard_rows, spare - 3), BF),
        ],
        axis=1,
    )
    packed = jnp.concatenate([query_proj, latent_proj, gains], axis=1)
    cotan_all = column_gather(out_cotan)
    if paired:
        low, high = (0, RAW_ROWS - TOPK), (0, 0)
        raw = jnp.concatenate(
            [jnp.pad(expert_ids.T.astype(F32), (low, high)), jnp.pad(expert_wts.T, (low, high))]
        )
        (
            tokens_all,
            packed_all,
            latent_up_weight,
            out_weight,
            raw,
            shared_weight,
            shared_down_weight,
        ) = first_call(
            block_in,
            [
                packed,
                latent_up,
                out_proj,
                raw,
                jnp.concatenate([shared_gate, shared_up], axis=1),
                shared_down,
            ],
            ("rows", "rows", "columns", "relative", "rows", "columns"),
        )
        shared_weight = shared_weight.reshape(model_width, -1)
        packed_all = packed_all.reshape(-1, packed.shape[1])
        latent_up_weight = latent_up_weight.reshape(LAT, up_cols)
    else:
        packed_all = lax.all_gather(packed, "fsdp", axis=0, tiled=True)
        latent_up_weight = lax.all_gather(latent_up, "fsdp", axis=0, tiled=True)
        out_weight = lax.all_gather(out_proj, "fsdp", axis=1, tiled=True)
        tokens_all = column_gather(block_in)
        shared_weight = lax.all_gather(
            jnp.concatenate([shared_gate, shared_up], axis=1), "fsdp", axis=0, tiled=True
        )
        shared_down_weight = lax.all_gather(shared_down, "fsdp", axis=1, tiled=True)
    gain_attn = packed_all[:, joint].astype(F32)
    gain_ffn = packed_all[:, joint + 1].astype(F32)
    gain_latent = (
        packed_all[:, joint + 2]
        .reshape(fsdp_count, shard_rows)[:, : latent_gain.shape[0]]
        .reshape(LAT)
        .astype(F32)
    )
    shared_cols = shared_gate.shape[1]

    def scatter(part, dimension):
        return lax.psum_scatter(part.astype(BF), "fsdp", scatter_dimension=dimension, tiled=True)

    unit_all, inverse_all = norm_parts(tokens_all.astype(F32))
    normed_all = (unit_all * gain_attn).astype(BF)
    joint_rows = jnp.dot(normed_all, packed_all, preferred_element_type=F32)
    queries = joint_rows[:, :query_cols].reshape(SEQ, heads_local, head_width)
    latent = joint_rows[:, query_cols:joint]
    unit_lat, inverse_lat = norm_parts(latent[:, :LAT])
    positions = jnp.arange(SEQ, dtype=jnp.int32)
    cosine, sine_part = rope_tables(positions, ROPE)
    compressed_all = (unit_lat * gain_latent).astype(BF)
    key_rope_all = rotate(latent[:, LAT:], cosine, sine_part).astype(BF)
    query_cat = jnp.concatenate(
        [
            queries[:, :, :NOPE],
            rotate(queries[:, :, NOPE:], cosine[:, None, :], sine_part[:, None, :]),
        ],
        axis=2,
    ).astype(BF)
    key_value = (
        jnp.dot(compressed_all, latent_up_weight, preferred_element_type=F32)
        .reshape(SEQ, heads_local, NOPE + DV)
        .astype(BF)
    )
    key_cat = jnp.concatenate(
        [
            key_value[:, :, :NOPE],
            jnp.broadcast_to(key_rope_all[:, None, :], (SEQ, heads_local, ROPE)),
        ],
        axis=2,
    )
    values = key_value[:, :, NOPE:]
    allowed = (positions[None, :] <= positions[:, None]) & (
        segment_ids[None, :] == segment_ids[:, None]
    )
    raw_scores = (
        jnp.einsum("qhd,khd->hqk", query_cat, key_cat, preferred_element_type=F32) * score_scale
    )
    masked = jnp.where(allowed[None], raw_scores, MASK_FILL)
    top_score = jnp.max(masked, axis=2, keepdims=True)
    exponent = jnp.exp(masked - top_score)
    row_total = jnp.sum(exponent, axis=2, keepdims=True)
    probabilities = exponent / row_total
    probs_low = probabilities.astype(BF)
    attended = (
        jnp.einsum("hqk,khd->qhd", probs_low, values, preferred_element_type=F32)
        .reshape(SEQ, heads_local * DV)
        .astype(BF)
    )
    attn_part = jnp.dot(attended, out_weight, preferred_element_type=F32).astype(BF)
    if paired:
        mixed_rows, normed_ffn_all, d_routed_in, *kept = expert_call(
            attn_part,
            block_in,
            cotan_all,
            routed_gate,
            routed_up,
            routed_down,
            gain_ffn[None, :],
            raw,
            cap_rows,
        )
        unit_two, inverse_two = norm_parts(mixed_rows)
        d_routed_in = d_routed_in.astype(F32)
    else:
        units = plane_units(fsdp_count)
        tables = expert_tables(expert_ids, expert_wts, local_experts, units, cap)
        hidden_pad = -(-local_hidden // 128) * 128
        lift = ((0, 0), (0, hidden_pad - local_hidden), (0, 0))
        routed_gate_up = jnp.concatenate(
            [jnp.pad(routed_gate, lift), jnp.pad(routed_up, lift)], axis=1
        )
        routed_down_pad = jnp.pad(routed_down, lift)
        mixed_rows = block_in.astype(F32) + column_scatter(attn_part)
        unit_two, inverse_two = norm_parts(mixed_rows)
        normed_ffn_all = column_gather((unit_two * gain_ffn).astype(BF))
        x_blocks = plane_gather(normed_ffn_all, fsdp_count)
        dy_all = lax.all_gather(cotan_all, "fsdp", axis=0, tiled=True)
        kept = []
        dx_pairs = []
        for step, unit in enumerate(units):
            pair, kept = expert_front(
                step,
                len(units),
                [x_blocks[key] for key in unit],
                jnp.array([2 * r + h for r, h in unit], jnp.int32),
                dy_all,
                routed_gate_up,
                routed_down_pad,
                tables,
                kept,
                cap,
            )
            dx_pairs.append(pair)
        near, far = expert_out(kept[2], routed_down_pad, tables, cap)
        d_routed_in = plane_scatter_whole(dx_pairs, units, fsdp_count)
    if not paired:
        routed_gate_grad, routed_up_grad, routed_down_grad = expert_grads(kept, local_hidden)

    shared_pre = jnp.dot(normed_ffn_all, shared_weight, preferred_element_type=F32)
    shared_gate_pre, shared_up_pre = shared_pre[:, :shared_cols], shared_pre[:, shared_cols:]
    shared_hidden = (jax.nn.silu(shared_gate_pre) * shared_up_pre).astype(BF)
    shared_rows = jnp.dot(shared_hidden, shared_down_weight, preferred_element_type=F32)
    shared_down_part = jnp.dot(shared_hidden.T, cotan_all, preferred_element_type=F32)
    d_shared_hidden = jnp.dot(cotan_all, shared_down_weight.T, preferred_element_type=F32)
    d_shared = jnp.concatenate(silu_back(d_shared_hidden, shared_gate_pre, shared_up_pre), axis=1)
    shared_part = jnp.dot(normed_ffn_all.T, d_shared, preferred_element_type=F32)
    d_shared_in = jnp.dot(d_shared, shared_weight.T, preferred_element_type=F32)

    if paired:
        d_ffn_rows, shared_part, shared_down_part = tie(
            (d_shared_in + d_routed_in).astype(BF),
            shared_part.astype(BF),
            shared_down_part.astype(BF),
        )
        (
            d_mixed,
            d_proj_all,
            ffn_gain_part,
            routed_rows,
            routed_gate_grad,
            routed_up_grad,
            routed_down_grad,
        ) = middle_call(
            d_ffn_rows,
            mixed_rows,
            out_cotan,
            gain_ffn[None, :],
            kept[:2],
            routed_down,
            kept[2:],
            cap_rows,
        )
        ffn_gain_part = ffn_gain_part[0]
        routed_rows = routed_rows.astype(F32)
    else:
        d_normed_ffn = column_scatter(d_shared_in + d_routed_in)
        out_pairs = [(near[step], far[step]) for step in range(len(units))]
        routed_rows = plane_scatter_whole(out_pairs, units, fsdp_count)
        ffn_gain_part, d_mixed_norm = norm_back(d_normed_ffn, unit_two, inverse_two, gain_ffn)
        d_mixed = out_cotan.astype(F32) + d_mixed_norm
        d_proj_all = column_gather(d_mixed.astype(BF))
    shared_grad = scatter(shared_part, 0)
    down_own, ffn_rows, shared_grad = tie(
        shared_down_part.astype(BF), (shared_rows + routed_rows).astype(BF), shared_grad
    )
    shared_down_grad = scatter(down_own, 1)
    ffn_rows = column_scatter(ffn_rows)
    block_out = (mixed_rows + ffn_rows).astype(BF)

    out_part = jnp.dot(attended.T, d_proj_all, preferred_element_type=F32)
    d_attended = (
        jnp.dot(d_proj_all, out_weight.T, preferred_element_type=F32)
        .astype(BF)
        .reshape(SEQ, heads_local, DV)
    )
    prob_grad = jnp.einsum("qhd,khd->hqk", d_attended, values, preferred_element_type=F32)
    score_grad = (
        probabilities
        * (prob_grad - jnp.sum(probabilities * prob_grad, axis=2, keepdims=True))
    ).astype(BF)
    query_grad = (
        jnp.einsum("hqk,khd->qhd", score_grad, key_cat, preferred_element_type=F32) * score_scale
    )
    key_grad = (
        jnp.einsum("hqk,qhd->khd", score_grad, query_cat, preferred_element_type=F32) * score_scale
    )
    value_grad = jnp.einsum("hqk,qhd->khd", probs_low, d_attended, preferred_element_type=F32)
    d_queries = (
        jnp.concatenate(
            [
                query_grad[:, :, :NOPE],
                unrotate(query_grad[:, :, NOPE:], cosine[:, None, :], sine_part[:, None, :]),
            ],
            axis=2,
        )
        .reshape(SEQ, heads_local * head_width)
        .astype(BF)
    )
    d_key_value = (
        jnp.concatenate([key_grad[:, :, :NOPE], value_grad], axis=2)
        .reshape(SEQ, heads_local * (NOPE + DV))
        .astype(BF)
    )
    latent_up_part = jnp.dot(compressed_all.T, d_key_value, preferred_element_type=F32)
    d_compressed = jnp.dot(d_key_value, latent_up_weight.T, preferred_element_type=F32)
    d_key_rope = jnp.sum(key_grad[:, :, NOPE:], axis=1)
    latent_gain_part, d_latent_main = norm_back(d_compressed, unit_lat, inverse_lat, gain_latent)
    d_latent = jnp.concatenate(
        [d_latent_main, unrotate(d_key_rope, cosine, sine_part)], axis=1
    ).astype(BF)
    d_joint = jnp.concatenate([d_queries, d_latent, jnp.zeros((SEQ, spare), BF)], axis=1)
    joint_part = jnp.dot(normed_all.T, d_joint, preferred_element_type=F32)
    d_normed_part = jnp.dot(d_joint, packed_all.T, preferred_element_type=F32)
    attn_gain_part = jnp.sum(d_normed_part * unit_all, axis=0)

    gain_parts = jnp.concatenate([attn_gain_part, latent_gain_part, ffn_gain_part]).reshape(
        -1, 128
    )
    joint_part = joint_part.astype(BF)
    if paired:
        latent_width = joint_part.shape[1] - query_cols
        (
            block_in_grad,
            joint_grad,
            latent_up_grad,
            out_proj_grad,
            latent_proj_grad,
            gain_sums,
        ) = last_call(
            d_normed_part.astype(BF),
            block_in,
            d_mixed,
            gain_attn[None, :],
            joint_part,
            latent_up_part.astype(BF),
            out_part.astype(BF),
            gain_parts,
            query_cols,
            latent_width,
        )
        latent_proj_grad = latent_proj_grad[:, :latent_cols]
    else:
        d_normed = column_scatter(d_normed_part)
        unit_one, inverse_one = norm_parts(block_in.astype(F32))
        _, d_tokens_norm = norm_back(d_normed, unit_one, inverse_one, gain_attn)
        block_in_grad = d_mixed + d_tokens_norm
        out_proj_grad = scatter(out_part, 1)
        latent_up_grad = scatter(latent_up_part, 0)
        joint_grad = scatter(joint_part, 0)
        latent_proj_grad = column_scatter(joint_grad[:, query_cols:joint])
        gain_sums = sum_everywhere(gain_parts)
    gain_sums = gain_sums.reshape(-1)
    query_proj_grad = joint_grad[:, :query_cols].astype(F32)
    latent_up_grad = latent_up_grad.astype(F32)
    out_proj_grad = out_proj_grad.astype(F32)
    shared_grad = shared_grad.astype(F32)
    shared_gate_grad, shared_up_grad = shared_grad[:, :shared_cols], shared_grad[:, shared_cols:]
    shared_down_grad = shared_down_grad.astype(F32)
    device = fsdp_rank * tp_count + tp_rank
    devices = tp_count * fsdp_count

    def own_gain(start, size):
        return lax.dynamic_slice(gain_sums, (start + device * (size // devices),), (size // devices,))

    attn_gain_grad = own_gain(0, model_width)
    latent_gain_grad = own_gain(model_width, LAT)
    ffn_gain_grad = own_gain(model_width + LAT, model_width)
    return (
        block_out,
        block_in_grad,
        attn_gain_grad,
        query_proj_grad,
        latent_proj_grad,
        latent_gain_grad,
        latent_up_grad,
        out_proj_grad,
        ffn_gain_grad,
        shared_gate_grad,
        shared_up_grad,
        shared_down_grad,
        routed_gate_grad,
        routed_up_grad,
        routed_down_grad,
    )


def solution(mesh):
    placed = (
        P(("fsdp", "tp"), None),
        P(("fsdp", "tp"), None),
        P("fsdp"),
        P("fsdp", None),
        P("fsdp", None),
        P("fsdp"),
        P("fsdp", "tp"),
        P("fsdp", None),
        P("fsdp"),
        P("fsdp", "tp"),
        P("tp", "fsdp"),
        P("fsdp"),
        P("fsdp", "tp"),
        P("fsdp", "tp"),
        P("tp", "fsdp"),
        P("fsdp", "tp", None),
        P("fsdp", "tp", None),
        P("fsdp", "tp", None),
    )
    return jax.shard_map(
        per_device,
        mesh=mesh,
        in_specs=placed,
        out_specs=(
            P(("fsdp", "tp"), None),
            P(("fsdp", "tp"), None),
            P(("fsdp", "tp")),
            P("fsdp", "tp"),
            P(("fsdp", "tp"), None),
            P(("fsdp", "tp")),
            P("fsdp", "tp"),
            P("tp", "fsdp"),
            P(("fsdp", "tp")),
            P("fsdp", "tp"),
            P("fsdp", "tp"),
            P("tp", "fsdp"),
            P("fsdp", "tp", None),
            P("fsdp", "tp", None),
            P("fsdp", "tp", None),
        ),
        check_vma=False,
    )
```
